32 devices in a mesh: seq: 4 (over y, x), chan: 8 (over z, core).
Axes of the slice: x: 2, y: 2, z: 4, core: 2. Of those that a mesh axis runs over, the one named last changes fastest.
Arguments:
- tokens: bfloat16 [16, 2048, 1024], P(None, 'seq', 'chan'), may hold values from -6 to 6
- cotangent: bfloat16 [16, 2048, 1024], P(None, 'seq', 'chan'), may hold values from -6 to 6
- doc_starts: int32 [16, 8], P('chan'), may hold values from 0 to 2048, as said below
- lengths: int32 [16], P('chan'), may hold values from 1024 to 2048, as said below
- norm1_gain: float32 [1024], replicated, may hold values from 0.5 to 1.5
- recur_input: bfloat16 [1024, 1536], replicated, may hold values from -0.1875 to 0.1875
- recur_gate: bfloat16 [1024, 1536], replicated, may hold values from -0.1875 to 0.1875
- conv_kernel: float32 [4, 1536], replicated, may hold values from -3 to 3
- conv_bias: float32 [1536], replicated, may hold values from -3 to 3
- lru_gates: bfloat16 [1536, 192], replicated, may hold values from -0.625 to 0.625
- lru_bias: float32 [2, 1536], replicated, may hold values from -4 to 4
- lru_decay: float32 [1536], replicated, may hold values from 3 to 9
- recur_out: bfloat16 [1536, 1024], replicated, may hold values from -0.21875 to 0.21875
- norm2_gain: float32 [1024], replicated, may hold values from 0.5 to 1.5
- mlp_gate: bfloat16 [1024, 3072], replicated, may hold values from -0.1875 to 0.1875
- mlp_up: bfloat16 [1024, 3072], replicated, may hold values from -0.1875 to 0.1875
- mlp_down: bfloat16 [3072, 1024], replicated, may hold values from -0.15625 to 0.15625
Outputs:
- output: bfloat16 [16, 2048, 1024], P(None, 'seq', 'chan')
- grad_tokens: bfloat16 [16, 2048, 1024], P(None, 'seq', 'chan')
- grad_norm1_gain: float32 [1024], P(('seq', 'chan'))
- grad_recur_input: float32 [1024, 1536], P(('seq', 'chan'))
- grad_recur_gate: float32 [1024, 1536], P(('seq', 'chan'))
- grad_conv_kernel: float32 [4, 1536], P(None, ('seq', 'chan'))
- grad_conv_bias: float32 [1536], P(('seq', 'chan'))
- grad_lru_gates: float32 [1536, 192], P(('seq', 'chan'))
- grad_lru_bias: float32 [2, 1536], P(None, ('seq', 'chan'))
- grad_lru_decay: float32 [1536], P(('seq', 'chan'))
- grad_recur_out: float32 [1536, 1024], P(('seq', 'chan'))
- grad_norm2_gain: float32 [1024], P(('seq', 'chan'))
- grad_mlp_gate: float32 [1024, 3072], P(('seq', 'chan'))
- grad_mlp_up: float32 [1024, 3072], P(('seq', 'chan'))
- grad_mlp_down: float32 [3072, 1024], P(('seq', 'chan'))
The draws below stay inside these ranges and needn't reach their ends.
Inputs may be any that keep to these rules, and one draw needn't show every extreme that they name: `doc_starts`: each row's list ascends from 0; unused slots hold 2048. `lengths`: some row has length 2048.
All inputs are finite; a program needn't handle non-finite values.
Results may differ from the reference program's by a relative error of at most 0.0095.
Values may be sent and summed in bfloat16 or wider, within the bound.
A program may use at most 320 MiB of HBM per device.

```python
import jax
import jax.numpy as jnp
from jax import lax

D = 1024
R = 1536
F = 3072
H = 16
BW = 96
KW = 4
LEN = 2048
MAXDOCS = 8
ROWS = 16


def draw_doc_starts(key, part):
    key_count = jax.random.fold_in(key, 11)
    key_values = jax.random.fold_in(key, 12)
    doc_count = jax.random.randint(key_count, (ROWS, 1), 1, MAXDOCS + 1)
    row_index = jnp.arange(ROWS, dtype=jnp.int32)[:, None]
    doc_count = jnp.where(row_index == 0, 1, doc_count)
    picks = jax.random.randint(key_values, (ROWS, MAXDOCS - 1), 1, LEN)
    picks = jnp.sort(picks, axis=1)
    slots = jnp.arange(1, MAXDOCS, dtype=jnp.int32)[None, :]
    later = jnp.where(slots < doc_count, picks, LEN)
    return jnp.concatenate([jnp.zeros((ROWS, 1), jnp.int32), later.astype(jnp.int32)], axis=1)


def draw_lengths(key, part):
    key_length = jax.random.fold_in(key, 21)
    key_row = jax.random.fold_in(key, 22)
    drawn = jax.random.randint(key_length, (ROWS,), LEN // 2, LEN + 1)
    chosen = jax.random.randint(key_row, (), 0, ROWS)
    return jnp.where(jnp.arange(ROWS, dtype=jnp.int32) == chosen, LEN, drawn).astype(jnp.int32)


def shard_levels(rng, extent, shards, low, largest):
    gain, own = 1.0, jax.random.fold_in(rng, 6)
    for dim, parts in shards:
        draws = jnp.exp(jax.random.uniform(jax.random.fold_in(own, dim), (parts,), jnp.float32, low / len(shards), largest / len(shards)))
        gain = gain * jnp.repeat(draws, extent[dim] // parts).reshape([-1 if axis == dim else 1 for axis in range(len(extent))])
    return gain


def noise(key, extent, deviation, bound, shards=(), kind=jnp.bfloat16):
    factor_of = shard_levels(key, extent, shards, -0.22, 0.18) if shards else 1.0
    values = jax.random.normal(key, extent, jnp.float32) * deviation * factor_of
    return jnp.minimum(jnp.maximum(values, -bound), bound).astype(kind)


def setup_inputs(seed: int = 0) -> dict:
    splits = jax.random.split(jax.random.key(seed), 18)
    tokens = noise(splits[0], (ROWS, LEN, D), 1.0, 6.0, ((1, 4), (2, 8)))
    cotangent = noise(splits[1], (ROWS, LEN, D), 1.0, 6.0, ((1, 4), (2, 8)))
    doc_starts = draw_doc_starts(jax.random.fold_in(splits[17], 71), 0)
    lengths = draw_lengths(jax.random.fold_in(splits[17], 71), 0)
    norm1_gain = jnp.clip(1.0 + 0.1 * jax.random.normal(splits[4], (D,), jnp.float32), 0.5, 1.5)
    recur_input = noise(splits[5], (D, R), D ** -0.5, 0.1875)
    recur_gate = noise(splits[6], (D, R), D ** -0.5, 0.1875)
    conv_kernel = noise(splits[7], (KW, R), 0.5, 3.0, (), jnp.float32)
    conv_bias = noise(splits[8], (R,), 0.5, 3.0, (), jnp.float32)
    lru_gates = noise(splits[9], (R, 2 * BW), BW ** -0.5, 0.625)
    lru_bias = noise(splits[10], (2, R), 0.7, 4.0, (), jnp.float32)
    lru_decay = jnp.clip(jax.random.uniform(splits[11], (R,), jnp.float32, 3.0, 9.0), 3.0, 9.0)
    recur_out = noise(splits[12], (R, D), (R // 2) ** -0.5, 0.21875)
    norm2_gain = jnp.clip(1.0 + 0.1 * jax.random.normal(splits[13], (D,), jnp.float32), 0.5, 1.5)
    mlp_gate = noise(splits[14], (D, F), D ** -0.5, 0.1875)
    mlp_up = noise(splits[15], (D, F), D ** -0.5, 0.1875)
    mlp_down = noise(splits[16], (F, D), (F // 2) ** -0.5, 0.15625)
    return dict(tokens=tokens, cotangent=cotangent, doc_starts=doc_starts, lengths=lengths, norm1_gain=norm1_gain, recur_input=recur_input, recur_gate=recur_gate, conv_kernel=conv_kernel, conv_bias=conv_bias, lru_gates=lru_gates, lru_bias=lru_bias, lru_decay=lru_decay, recur_out=recur_out, norm2_gain=norm2_gain, mlp_gate=mlp_gate, mlp_up=mlp_up, mlp_down=mlp_down)


EPS = 1e-06
ROOT_FLOOR = 1e-06
HIGH = lax.Precision.HIGHEST

@jax.custom_vjp
def low(v):
    return lax.optimization_barrier(v.astype(jnp.bfloat16)).astype(jnp.float32)

@jax.custom_vjp
def low_back(v):
    return v

def low_keep(v):
    return (low(v), None)

def low_pass(kept, grad):
    return (grad,)

def back_keep(v):
    return (v, None)

def back_low(kept, grad):
    return (low(grad),)
low.defvjp(low_keep, low_pass)
low_back.defvjp(back_keep, back_low)

def gelu_fn(value):
    return jax.nn.gelu(value, approximate=True)

def matmul(left, right):
    return jnp.einsum('btd,df->btf', left, right, precision=HIGH)

def rms_normed(value):
    return value * lax.rsqrt(lax.optimization_barrier(jnp.mean(value * value, axis=-1, keepdims=True)) + EPS)

def block_forward(params, tokens, seg_start, position):
    norm1_gain, recur_input, recur_gate, conv_kernel, conv_bias, lru_gates, lru_bias, lru_decay, recur_out, norm2_gain, mlp_gate, mlp_up, mlp_down = params
    group_rows = tokens.shape[0]
    seq_len = tokens.shape[1]
    rec_width = recur_input.shape[1]
    head_size = rec_width // H
    normed_low = low(rms_normed(tokens) * norm1_gain)
    branch_pre = low_back(matmul(normed_low, recur_input))
    gate_pre = low_back(matmul(normed_low, recur_gate))
    gate_act = gelu_fn(gate_pre)
    conv_sum = jnp.zeros_like(branch_pre) + conv_bias
    for offset in range(KW):
        shifted = jnp.pad(branch_pre, ((0, 0), (offset, 0), (0, 0)))[:, :seq_len, :]
        tap_keep = (position[None, :] - offset >= seg_start)[:, :, None]
        conv_sum = conv_sum + conv_kernel[offset] * jnp.where(tap_keep, shifted, 0.0)
    lru_in = low(conv_sum)
    gate_blocks = lru_gates.reshape(H, head_size, 2 * head_size)
    gate_both = jnp.einsum('bthi,hij->bthj', lru_in.reshape(group_rows, seq_len, H, head_size), gate_blocks, precision=HIGH)
    rate_pre = low_back(gate_both[..., :head_size].reshape(group_rows, seq_len, rec_width) + lru_bias[0])
    input_pre = low_back(gate_both[..., head_size:].reshape(group_rows, seq_len, rec_width) + lru_bias[1])
    rate_gate = jax.nn.sigmoid(rate_pre)
    input_gate = jax.nn.sigmoid(input_pre)
    log_decay = -8.0 * rate_gate * jax.nn.softplus(-lru_decay)
    decay_rate = jnp.exp(log_decay)
    root_term = jnp.sqrt(jnp.maximum(-jnp.expm1(2.0 * log_decay), ROOT_FLOOR))
    at_start = (seg_start == position[None, :])[:, :, None]
    decay_coef = jnp.where(at_start, 0.0, decay_rate)
    scale_in = jnp.where(at_start, 1.0, root_term)
    lru_drive = scale_in * input_gate * lru_in

    def step_fn(running, element):
        updated = element[0] * running + element[1]
        return (updated, updated)
    start_state = jnp.zeros((group_rows, rec_width), tokens.dtype)
    _, states = lax.scan(step_fn, start_state, (jnp.swapaxes(decay_coef, 0, 1), jnp.swapaxes(lru_drive, 0, 1)))
    lru_state = jnp.swapaxes(states, 0, 1)
    mixed_low = low(lru_state * gate_act)
    branch_out = low_back(matmul(mixed_low, recur_out))
    resid_one = tokens + branch_out
    normed_two = low(rms_normed(resid_one) * norm2_gain)
    mlp_gate_pre = low_back(matmul(normed_two, mlp_gate))
    mlp_up_pre = low_back(matmul(normed_two, mlp_up))
    hidden_low = low(gelu_fn(mlp_gate_pre) * mlp_up_pre)
    return resid_one + low_back(matmul(hidden_low, mlp_down))

def reference(tokens, cotangent, doc_starts, lengths, norm1_gain, recur_input, recur_gate, conv_kernel, conv_bias, lru_gates, lru_bias, lru_decay, recur_out, norm2_gain, mlp_gate, mlp_up, mlp_down):
    weights = tuple((weight.astype(jnp.float32) for weight in (norm1_gain, recur_input, recur_gate, conv_kernel, conv_bias, lru_gates, lru_bias, lru_decay, recur_out, norm2_gain, mlp_gate, mlp_up, mlp_down)))
    group_rows = 2
    group_count = ROWS // group_rows
    position = jnp.arange(LEN, dtype=jnp.int32)

    def group_fn(totals, element):
        group_x, group_g, group_starts, group_lengths = element
        bounds = jnp.concatenate([group_starts, group_lengths[:, None]], axis=1).astype(jnp.int32)
        is_before = bounds[:, None, :] <= position[None, :, None]
        seg_start = lax.optimization_barrier(jnp.max(jnp.where(is_before, bounds[:, None, :], 0), axis=2)).astype(jnp.int32)
        is_valid = (position[None, :] < group_lengths[:, None])[:, :, None]

        def closed(params, inputs):
            return block_forward(params, inputs, seg_start, position)
        result, pull = jax.vjp(closed, weights, group_x.astype(jnp.float32))
        grad_in = jnp.where(is_valid, group_g.astype(jnp.float32), 0.0)
        grad_params, grad_x = pull(grad_in)
        totals = jax.tree.map(jnp.add, totals, grad_params)
        return (totals, (result.astype(jnp.bfloat16), grad_x.astype(jnp.bfloat16)))
    start_totals = jax.tree.map(jnp.zeros_like, weights)
    inputs = (tokens.reshape(group_count, group_rows, LEN, D), cotangent.reshape(group_count, group_rows, LEN, D), doc_starts.reshape(group_count, group_rows, MAXDOCS), lengths.reshape(group_count, group_rows))
    totals, (output, grad_tokens) = lax.scan(group_fn, start_totals, inputs)
    output = output.reshape(ROWS, LEN, D)
    grad_tokens = grad_tokens.reshape(ROWS, LEN, D)
    return (output, grad_tokens, totals[0], totals[1], totals[2], totals[3], totals[4], totals[5], totals[6], totals[7], totals[8], totals[9], totals[10], totals[11], totals[12])
```

```python
import functools
import math

import jax
import jax.numpy as jnp
from jax import lax
from jax.experimental import pallas as pl
from jax.experimental.pallas import tpu as pltpu
from jax.sharding import PartitionSpec as P

H = 16


EPS = 1e-06
ROOT_FLOOR = 1e-06
LANES = 128
SUBLANES = 8
STEP = 16
VMEM_BYTES = 56 * 1024 * 1024


def sigmoid(value):
    return 0.5 * jnp.tanh(0.5 * value) + 0.5


GELU_C = 0.7978845608
GELU_A = 0.044715


def gelu_pair(value):
    square = value * value
    inner = jnp.tanh(value * (GELU_C + (GELU_C * GELU_A) * square))
    half = 0.5 + 0.5 * inner
    slope = GELU_C + (3.0 * GELU_C * GELU_A) * square
    return (value * half, half + 0.5 * value * (1.0 - inner * inner) * slope)


def root_argument(log_decay, decay):
    y = 2.0 * log_decay
    series = 1.0 + y * (1.0 / 7.0)
    for divisor in (6.0, 5.0, 4.0, 3.0, 2.0):
        series = 1.0 + (y * (1.0 / divisor)) * series
    return jnp.where(y > -0.25, -y * series, 1.0 - decay * decay)


def across(column, width):
    return jnp.concatenate([column] * (width // LANES), axis=1)


def forward_kernel(
    branch_ref,
    rim_ref,
    dist_ref,
    par_ref,
    gates_ref,
    lru_ref,
    rate_ref,
    igate_ref,
    state_ref,
    cum_ref,
    both_ref,
):
    rows, length, width = branch_ref.shape
    taps = [par_ref[k : k + 1, :] for k in range(4)]
    conv_bias, rate_bias, input_bias, soft = (par_ref[k : k + 1, :] for k in range(4, 8))
    place = lax.broadcasted_iota(jnp.int32, (SUBLANES, width), 0)

    for row in range(rows):

        def conv_step(index, before, row=row):
            base = pl.multiple_of(index * STEP, STEP)
            pieces = []
            for half in range(STEP // SUBLANES):
                at = pl.ds(base + half * SUBLANES, SUBLANES)
                here = branch_ref[row, at, :]
                dist = across(dist_ref[row, at, :], width)
                total = conv_bias + taps[0] * here
                for k in range(1, 4):
                    shifted = pltpu.roll(jnp.where(place < SUBLANES - k, here, before), k, 0)
                    total = total + taps[k] * jnp.where(dist >= k, shifted, 0.0)
                pieces.append(total)
                before = here
            lru_ref[row, pl.ds(base, STEP), :] = jnp.concatenate(pieces, axis=0).astype(jnp.bfloat16)
            return before

        lax.fori_loop(0, length // STEP, conv_step, rim_ref[row])

        piece = min(length, 256)

        def dot_step(index, carry, row=row):
            at = pl.ds(pl.multiple_of(index * piece, piece), piece)
            both_ref[row, at, :] = jnp.dot(
                lru_ref[row, at, :], gates_ref[...], preferred_element_type=jnp.float32
            )
            return carry

        lax.fori_loop(0, length // piece, dot_step, 0)

    def scan_step(index, carry):
        base = pl.multiple_of(index * STEP, STEP)
        later = []
        for row in range(rows):
            run_cum, run_state = carry[row]
            lru_both = lru_ref[row, pl.ds(base, STEP), :].astype(jnp.float32)
            for half in range(STEP // SUBLANES):
                at = pl.ds(base + half * SUBLANES, SUBLANES)
                lru = lru_both[half * SUBLANES : (half + 1) * SUBLANES]
                start = across(dist_ref[row, at, :], width) == 0
                rate = sigmoid(both_ref[row, at, :width] + rate_bias)
                igate = sigmoid(both_ref[row, at, width:] + input_bias)
                log_decay = rate * soft
                decay = jnp.exp(log_decay)
                arg = jnp.maximum(root_argument(log_decay, decay), ROOT_FLOOR)
                root = arg * lax.rsqrt(arg)
                cum = jnp.where(start, 0.0, decay)
                value = jnp.where(start, 1.0, root) * igate * lru
                rate_ref[row, at, :] = rate
                igate_ref[row, at, :] = igate
                for shift in (1, 2, 4):
                    live = place >= shift
                    value = value + cum * jnp.where(live, pltpu.roll(value, shift, 0), 0.0)
                    cum = cum * jnp.where(live, pltpu.roll(cum, shift, 0), 1.0)
                value = value + cum * run_state
                cum = cum * run_cum
                state_ref[row, at, :] = value
                cum_ref[row, at, :] = cum
                run_state = value[SUBLANES - 1 :, :]
                run_cum = cum[SUBLANES - 1 :, :]
            later.append((run_cum, run_state))
        return tuple(later)

    one, zero = (jnp.ones((1, width), jnp.float32), jnp.zeros((1, width), jnp.float32))
    lax.fori_loop(0, length // STEP, scan_step, tuple((one, zero) for _ in range(rows)))


def adjoint_kernel(
    dmix_ref,
    pre_ref,
    state_ref,
    cum_ref,
    carry_ref,
    rate_ref,
    dist_ref,
    par_ref,
    dgate_ref,
    local_ref,
    back_ref,
    first_ref,
):
    rows, length, width = dmix_ref.shape
    soft = par_ref[7:8, :]
    place = lax.broadcasted_iota(jnp.int32, (SUBLANES, width), 0)
    last = length // STEP - 1

    def step(index, carry):
        base = pl.multiple_of((last - index) * STEP, STEP)
        later = []
        for row in range(rows):
            run_cum, run_back = carry[row]
            entering = carry_ref[row]
            pieces = []
            for half in reversed(range(STEP // SUBLANES)):
                at = pl.ds(base + half * SUBLANES, SUBLANES)
                start = across(dist_ref[row, at, :], width) == 0
                state = state_ref[row, at, :] + cum_ref[row, at, :] * entering
                act, slope = gelu_pair(pre_ref[row, at, :])
                dmix = dmix_ref[row, at, :]
                pieces.append(dmix * state * slope)
                dstate = dmix * act
                coef = jnp.where(start, 0.0, jnp.exp(rate_ref[row, at, :] * soft))
                value = coef * dstate
                for shift in (1, 2, 4):
                    live = place < SUBLANES - shift
                    turn = SUBLANES - shift
                    value = value + coef * jnp.where(live, pltpu.roll(value, turn, 0), 0.0)
                    coef = coef * jnp.where(live, pltpu.roll(coef, turn, 0), 1.0)
                value = value + coef * run_back
                coef = coef * run_cum
                inside = place < SUBLANES - 1
                local_ref[row, at, :] = dstate + jnp.where(
                    inside, pltpu.roll(value, SUBLANES - 1, 0), run_back
                )
                back_ref[row, at, :] = jnp.where(inside, pltpu.roll(coef, SUBLANES - 1, 0), run_cum)
                run_back = value[:1, :]
                run_cum = coef[:1, :]
            dgate_ref[row, pl.ds(base, STEP), :] = jnp.concatenate(pieces[::-1], axis=0).astype(
                jnp.bfloat16
            )
            later.append((run_cum, run_back))
        return tuple(later)

    one, zero = (jnp.ones((1, width), jnp.float32), jnp.zeros((1, width), jnp.float32))
    done = lax.fori_loop(0, last + 1, step, tuple((one, zero) for _ in range(rows)))
    for row in range(rows):
        first_ref[row] = done[row][1]


def backward_kernel(
    head_size,
    local_ref,
    back_ref,
    out_ref,
    state_ref,
    cum_ref,
    in_ref,
    rate_ref,
    igate_ref,
    lru_ref,
    dist_ref,
    branch_ref,
    rim_ref,
    par_ref,
    gates_ref,
    dbranch_ref,
    tail_ref,
    head_ref,
    sums_ref,
    dgates_ref,
    both_ref,
    dconv_ref,
):
    rows, length, width = local_ref.shape
    taps = [par_ref[k : k + 1, :] for k in range(4)]
    soft = par_ref[7:8, :]
    place = lax.broadcasted_iota(jnp.int32, (SUBLANES, width), 0)
    zeros = jnp.zeros((SUBLANES, width), jnp.float32)

    def gate_step(index, carry):
        sums, earlier = carry
        decay_sum, rate_sum, input_sum = sums
        base = pl.multiple_of(index * STEP, STEP)
        later = []
        for row in range(rows):
            before = earlier[row]
            entering = in_ref[row]
            leaving = out_ref[row]
            lru_both = lru_ref[row, pl.ds(base, STEP), :].astype(jnp.float32)
            drates, dinputs = ([], [])
            for half in range(STEP // SUBLANES):
                at = pl.ds(base + half * SUBLANES, SUBLANES)
                lru = lru_both[half * SUBLANES : (half + 1) * SUBLANES]
                start = across(dist_ref[row, at, :], width) == 0
                adjoint = local_ref[row, at, :] + back_ref[row, at, :] * leaving
                state = state_ref[row, at, :] + cum_ref[row, at, :] * entering
                previous = jnp.where(place < 1, before, pltpu.roll(state, 1, 0))
                before = state[SUBLANES - 1 :, :]
                rate = rate_ref[row, at, :]
                igate = igate_ref[row, at, :]
                log_decay = rate * soft
                decay = jnp.exp(log_decay)
                arg = root_argument(log_decay, decay)
                above = arg > ROOT_FLOOR
                arg = jnp.maximum(arg, ROOT_FLOOR)
                inverse = lax.rsqrt(arg)
                scale = jnp.where(start, 1.0, arg * inverse)
                gated = adjoint * igate
                dscale = gated * lru
                pull = jnp.where(above, dscale * decay * decay * inverse, 0.0)
                dlog = jnp.where(start, 0.0, adjoint * previous * decay - pull)
                dig = adjoint * scale * lru
                weighted = dlog * rate
                decay_sum = decay_sum + weighted
                drates.append(weighted * soft * (1.0 - rate))
                dinputs.append(dig * igate * (1.0 - igate))
                dconv_ref[row, at, :] = gated * scale
            drate = jnp.concatenate(drates, axis=0).astype(jnp.bfloat16)
            dinput = jnp.concatenate(dinputs, axis=0).astype(jnp.bfloat16)
            both_ref[row, pl.ds(base, STEP), :width] = drate
            both_ref[row, pl.ds(base, STEP), width:] = dinput
            drate = drate.astype(jnp.float32)
            dinput = dinput.astype(jnp.float32)
            rate_sum = rate_sum + (drate[:SUBLANES] + drate[SUBLANES:])
            input_sum = input_sum + (dinput[:SUBLANES] + dinput[SUBLANES:])
            later.append(before)
        return ((decay_sum, rate_sum, input_sum), tuple(later))

    sums, _ = lax.fori_loop(
        0,
        length // STEP,
        gate_step,
        ((zeros, zeros, zeros), tuple(in_ref[row] for row in range(rows))),
    )
    for slot, total in zip((5, 6, 7), (sums[1], sums[2], sums[0])):
        sums_ref[slot : slot + 1, :] = jnp.sum(total, axis=0, keepdims=True)

    piece = min(length, 256)
    wide = None
    for row in range(rows):

        def dot_step(index, carry, row=row):
            at = pl.ds(pl.multiple_of(index * piece, piece), piece)
            dconv_ref[row, at, :] += lax.dot_general(
                both_ref[row, at, :],
                gates_ref[...],
                (((1,), (1,)), ((), ())),
                preferred_element_type=jnp.float32,
            )
            return carry

        lax.fori_loop(0, length // piece, dot_step, 0)
        part = lax.dot_general(
            lru_ref[row], both_ref[row], (((0,), (0,)), ((), ())), preferred_element_type=jnp.float32
        )
        wide = part if wide is None else wide + part
    row_head = lax.broadcasted_iota(jnp.int32, (width, width), 0) // head_size
    col_head = lax.broadcasted_iota(jnp.int32, (width, width), 1) // head_size
    own = row_head == col_head
    for part in range(2):
        kept = jnp.where(own, wide[:, part * width : (part + 1) * width], 0.0)
        folded = kept
        for other in range(1, width // head_size):
            folded = folded + pltpu.roll(kept, width - other * head_size, 1)
        dgates_ref[:, part * LANES : (part + 1) * LANES] = folded[:, :LANES]

    def conv_step(index, carry):
        sums, following = carry
        sums = list(sums)
        base = pl.multiple_of((length // STEP - 1 - index) * STEP, STEP)
        later = []
        for row in range(rows):
            after = following[row]
            pieces = []
            for half in reversed(range(STEP // SUBLANES)):
                at = pl.ds(base + half * SUBLANES, SUBLANES)
                dist = across(dist_ref[row, at, :], width)
                branch = branch_ref[row, at, :]
                here = dconv_ref[row, at, :]
                total = taps[0] * here
                sums[0] = sums[0] + here * branch
                sums[4] = sums[4] + here
                masked = tuple(jnp.where(dist >= k, here, 0.0) for k in range(1, 4))
                for k in range(1, 4):
                    moved = pltpu.roll(
                        jnp.where(place >= k, masked[k - 1], after[k - 1]), SUBLANES - k, 0
                    )
                    total = total + taps[k] * moved
                    sums[k] = sums[k] + branch * moved
                after = masked
                pieces.append(total)
            whole = jnp.concatenate(pieces[::-1], axis=0)
            dbranch_ref[row, pl.ds(base, STEP), :] = whole.astype(jnp.bfloat16)
            later.append(after)

            @pl.when(index == 0)
            def _(row=row, whole=whole):
                tail_ref[row] = whole[STEP - SUBLANES :]

        return (tuple(sums), tuple(later))

    sums, firsts = lax.fori_loop(
        0,
        length // STEP,
        conv_step,
        ((zeros,) * 5, tuple((zeros,) * 3 for _ in range(rows))),
    )
    sums = list(sums)
    for row in range(rows):
        total = zeros
        rim = rim_ref[row]
        for k in range(1, 4):
            moved = pltpu.roll(jnp.where(place >= k, 0.0, firsts[row][k - 1]), SUBLANES - k, 0)
            total = total + taps[k] * moved
            sums[k] = sums[k] + rim * moved
        head_ref[row] = total
    for slot in range(5):
        sums_ref[slot : slot + 1, :] = jnp.sum(sums[slot], axis=0, keepdims=True)


def channel_call(kernel, name, arrays, specs, outs, out_specs, scratch, blocks, flops):
    moved = sum(math.prod(a.shape) * a.dtype.itemsize for a in (*arrays, *outs))
    return pl.pallas_call(
        kernel,
        name=name,
        grid=(blocks,),
        in_specs=specs,
        out_specs=out_specs,
        out_shape=outs,
        scratch_shapes=scratch,
        compiler_params=pltpu.CompilerParams(vmem_limit_bytes=VMEM_BYTES),
        cost_estimate=pl.CostEstimate(flops=flops, bytes_accessed=moved, transcendentals=0),
    )(*arrays)


class Recurrence:
    def __init__(self, rows, length, channels, head_size):
        self.rows, self.length, self.channels = (rows, length, channels)
        self.head_size = head_size
        self.width = head_size * LANES // math.gcd(head_size, LANES)
        self.blocks = channels // self.width
        self.flops = 2 * rows * length * channels * 2 * self.width

    def tall(self):
        return pl.BlockSpec((self.rows, self.length, self.width), lambda j: (0, 0, j))

    def short(self, size):
        return pl.BlockSpec((self.rows, size, self.width), lambda j: (0, 0, j))

    def flat(self, size):
        return pl.BlockSpec((size, self.width), lambda j: (0, j))

    def dist(self):
        return pl.BlockSpec((self.rows, self.length, LANES), lambda j: (0, 0, 0))

    def gates(self, columns):
        return pl.BlockSpec((self.width, columns), lambda j: (j, 0))

    def shape(self, size, dtype):
        return jax.ShapeDtypeStruct((self.rows, size, self.channels), dtype)

    def widen(self, lru_gates):
        size, width = (self.head_size, self.width)
        heads = width // size
        column = jnp.arange(2 * width)
        source = (column // width) * size + column % size
        spread = (jnp.arange(2 * size)[:, None] == source[None, :]).astype(jnp.bfloat16)
        owner = (column % width) // size
        mine = (jnp.arange(self.channels) // size) % heads
        wide = jnp.dot(lru_gates, spread, preferred_element_type=jnp.float32)
        return jnp.where(mine[:, None] == owner[None, :], wide, 0.0).astype(jnp.bfloat16)

    def forward(self, branch, rim, dist, params, gates):
        f32 = jnp.float32
        outs = [self.shape(self.length, d) for d in (jnp.bfloat16, f32, f32, f32, f32)]
        return channel_call(
            forward_kernel,
            "recurrence_forward",
            (branch, rim, dist, params, gates),
            [self.tall(), self.short(SUBLANES), self.dist(), self.flat(16), self.gates(2 * self.width)],
            outs,
            [self.tall()] * 5,
            [pltpu.VMEM((self.rows, self.length, 2 * self.width), f32)],
            self.blocks,
            self.flops,
        )

    def adjoint(self, dmix, pre, state, cum, entering, rate, dist, params):
        f32 = jnp.float32
        outs = [self.shape(self.length, d) for d in (jnp.bfloat16, f32, f32)] + [self.shape(1, f32)]
        tall = self.tall()
        return channel_call(
            adjoint_kernel,
            "recurrence_adjoint",
            (dmix, pre, state, cum, entering, rate, dist, params),
            [tall, tall, tall, tall, self.short(1), tall, self.dist(), self.flat(16)],
            outs,
            [tall, tall, tall, self.short(1)],
            [],
            self.blocks,
            0,
        )

    def backward(
        self, local, back, leaving, state, cum, entering, rate, igate, lru, dist, branch, rim, params, gates
    ):
        f32 = jnp.float32
        outs = [
            self.shape(self.length, jnp.bfloat16),
            self.shape(SUBLANES, f32),
            self.shape(SUBLANES, f32),
            jax.ShapeDtypeStruct((SUBLANES, self.channels), f32),
            jax.ShapeDtypeStruct((self.channels, 2 * LANES), f32),
        ]
        tall, one = (self.tall(), self.short(1))
        return channel_call(
            functools.partial(backward_kernel, self.head_size),
            "recurrence_backward",
            (local, back, leaving, state, cum, entering, rate, igate, lru, dist, branch, rim, params, gates),
            [tall, tall, one, tall, tall, one, tall, tall, tall, self.dist(), tall]
            + [self.short(SUBLANES), self.flat(16), self.gates(2 * self.width)],
            outs,
            [tall, self.short(SUBLANES), self.short(SUBLANES), self.flat(SUBLANES), self.gates(2 * LANES)],
            [
                pltpu.VMEM((self.rows, self.length, 2 * self.width), jnp.bfloat16),
                pltpu.VMEM((self.rows, self.length, self.width), f32),
            ],
            self.blocks,
            2 * self.flops,
        )


def prefix(value, axis, join, neutral, backward):
    count, mine = (lax.axis_size(axis), lax.axis_index(axis))
    pieces = jax.tree.map(lambda part: lax.all_gather(part, axis), value)
    if backward:
        pieces = jax.tree.map(lambda part: part[::-1], pieces)
        mine = count - 1 - mine
    subtotal = jax.tree.map(
        lambda part, zero: jnp.full_like(part, 0) + jnp.asarray(zero, part.dtype), value, neutral
    )

    def hop(position, subtotal):
        longer = join(subtotal, jax.tree.map(lambda part: part[position], pieces))
        return jax.tree.map(lambda new, old: jnp.where(position < mine, new, old), longer, subtotal)

    return lax.fori_loop(0, count - 1, hop, subtotal)


def passed_along(value, axis, steps):
    count = lax.axis_size(axis)
    leading, last = (max(0, -steps), min(count, count - steps))
    return lax.ppermute(value, axis, [(source, source + steps) for source in range(leading, last)])


def as_sent(x):
    return jax.tree.map(lambda a: a.astype(jnp.bfloat16) if a.dtype == jnp.float32 else a, x)


def trans_dot(left, right):
    return lax.dot_general(
        left, right, (((0,), (0,)), ((), ())), preferred_element_type=jnp.float32
    )


def back_dot(left, right):
    return lax.dot_general(
        left, right, (((1,), (1,)), ((), ())), preferred_element_type=jnp.float32
    )


def fwd_dot(left, right):
    return jnp.dot(left, right, preferred_element_type=jnp.float32)


def gelu_fn(value):
    return jax.nn.gelu(value, approximate=True)


def pair_join(earlier, later):
    return (earlier[0] * later[0], later[0] * earlier[1] + later[1])


def norm_back(grad_norm, normed, inverse, gain):
    scaled = grad_norm * gain
    mean_term = jnp.mean(scaled * normed, axis=1, keepdims=True)
    return (inverse * (scaled - normed * mean_term), jnp.sum(grad_norm * normed, axis=0))


def lane_rows(matrix):
    return matrix.reshape(-1, LANES)


def carry_forward(summary):
    identity = (jnp.ones_like(summary[0]), jnp.zeros_like(summary[1]))
    return prefix(summary, "seq", pair_join, identity, False)[1]


def carry_backward(summary):
    identity = (jnp.ones_like(summary[0]), jnp.zeros_like(summary[1]))
    return prefix(summary, "seq", pair_join, identity, True)[1]


def body(
    tokens,
    cotangent,
    doc_starts,
    lengths,
    norm1_gain,
    recur_input,
    recur_gate,
    conv_kernel,
    conv_bias,
    lru_gates,
    lru_bias,
    lru_decay,
    recur_out,
    norm2_gain,
    mlp_gate,
    mlp_up,
    mlp_down,
):
    seq_x, seq_g = (
        lax.all_to_all(tokens, "chan", split_axis=0, concat_axis=2, tiled=True),
        lax.all_to_all(cotangent, "chan", split_axis=0, concat_axis=2, tiled=True),
    )
    row_count, block_len, model_dim = seq_x.shape
    tok_count = row_count * block_len
    rec_width = recur_input.shape[1]
    ffn_width = mlp_gate.shape[1]
    head_count = H
    head_size = rec_width // head_count
    tap_count = conv_kernel.shape[0]
    rim_size = tap_count - 1
    seq_index = lax.axis_index("seq")
    position = seq_index * block_len + jnp.arange(block_len, dtype=jnp.int32)
    bounds = jnp.concatenate([doc_starts, lengths[:, None]], axis=1)
    is_before = bounds[:, None, :] <= position[None, :, None]
    seg_start = jnp.max(jnp.where(is_before, bounds[:, None, :], 0), axis=2)
    is_valid = (position[None, :] < lengths[:, None]).reshape(tok_count, 1)
    flat_x = seq_x.reshape(tok_count, model_dim).astype(jnp.float32)
    inv_one = lax.rsqrt(jnp.mean(flat_x * flat_x, axis=1, keepdims=True) + EPS)
    normed_one = flat_x * inv_one
    normed_low = (normed_one * norm1_gain).astype(jnp.bfloat16)
    branch_pre = fwd_dot(normed_low, recur_input)
    gate_pre = fwd_dot(normed_low, recur_gate)
    gate_act = gelu_fn(gate_pre)
    branch_rows = branch_pre.reshape(row_count, block_len, rec_width)
    core = Recurrence(row_count, block_len, rec_width, head_size)
    prev_rim = passed_along(
        branch_rows[:, block_len - rim_size :, :].astype(jnp.bfloat16), "seq", 1
    ).astype(jnp.float32)
    rim = jnp.pad(prev_rim, ((0, 0), (SUBLANES - rim_size, 0), (0, 0)))
    dist = jnp.broadcast_to(
        (position[None, :] - seg_start)[:, :, None], (row_count, block_len, LANES)
    )
    soft_decay = jax.nn.softplus(-lru_decay)
    params = jnp.concatenate(
        [
            conv_kernel,
            conv_bias[None],
            lru_bias,
            (-8.0 * soft_decay)[None],
            jnp.zeros((SUBLANES, rec_width), jnp.float32),
        ],
        axis=0,
    )
    wide_gates = core.widen(lru_gates)
    lru_in, rate_gate, input_gate, local_state, cum_coef = core.forward(
        branch_rows, rim, dist, params, wide_gates
    )
    carry_in = carry_forward((cum_coef[:, -1, :], local_state[:, -1, :]))
    entering = carry_in[:, None, :]
    state_rows = local_state + cum_coef * entering
    state_flat = state_rows.reshape(tok_count, rec_width)
    mixed_low = (state_flat * gate_act).astype(jnp.bfloat16)
    resid_one = flat_x + fwd_dot(mixed_low, recur_out)
    inv_two = lax.rsqrt(jnp.mean(resid_one * resid_one, axis=1, keepdims=True) + EPS)
    normed_two = resid_one * inv_two
    normed_low2 = (normed_two * norm2_gain).astype(jnp.bfloat16)
    mlp_gate_pre = fwd_dot(normed_low2, mlp_gate)
    mlp_up_pre = fwd_dot(normed_low2, mlp_up)
    gelu_gate = gelu_fn(mlp_gate_pre)
    hidden_low = (gelu_gate * mlp_up_pre).astype(jnp.bfloat16)
    result = (resid_one + fwd_dot(hidden_low, mlp_down)).astype(jnp.bfloat16)
    output = lax.all_to_all(
        result.reshape(row_count, block_len, model_dim),
        "chan",
        split_axis=2,
        concat_axis=0,
        tiled=True,
    )
    grad_out = jnp.where(is_valid, seq_g.reshape(tok_count, model_dim).astype(jnp.float32), 0.0)
    grad_low = grad_out.astype(jnp.bfloat16)
    grad_down = trans_dot(hidden_low, grad_low)
    grad_hidden = back_dot(grad_low, mlp_down)
    _, gelu_pull = jax.vjp(gelu_fn, mlp_gate_pre)
    mgate_low = gelu_pull(grad_hidden * mlp_up_pre)[0].astype(jnp.bfloat16)
    mup_low = (grad_hidden * gelu_gate).astype(jnp.bfloat16)
    grad_mgate = trans_dot(normed_low2, mgate_low)
    grad_mup = trans_dot(normed_low2, mup_low)
    grad_norm2 = back_dot(mgate_low, mlp_gate) + back_dot(mup_low, mlp_up)
    resid_part, grad_gain2 = norm_back(grad_norm2, normed_two, inv_two, norm2_gain)
    grad_resid = grad_out + resid_part
    resid_low = grad_resid.astype(jnp.bfloat16)
    grad_rout = trans_dot(mixed_low, resid_low)
    grad_mixed = back_dot(resid_low, recur_out)
    gate_low, back_local, back_cum, first_term = core.adjoint(
        grad_mixed.reshape(row_count, block_len, rec_width),
        gate_pre.reshape(row_count, block_len, rec_width),
        local_state,
        cum_coef,
        entering,
        rate_gate,
        dist,
        params,
    )
    gate_low = gate_low.reshape(tok_count, rec_width)
    carry_out = carry_backward((cum_coef[:, -1, :], first_term[:, 0, :]))
    branch_local, tail, lead, channel_sums, gate_sums = core.backward(
        back_local,
        back_cum,
        carry_out[:, None, :],
        local_state,
        cum_coef,
        entering,
        rate_gate,
        input_gate,
        lru_in,
        dist,
        branch_rows,
        rim,
        params,
        wide_gates,
    )
    grad_ckernel = channel_sums[:4]
    grad_cbias = channel_sums[4]
    grad_lbias = channel_sums[5:7]
    grad_decay = 8.0 * jax.nn.sigmoid(-lru_decay) * channel_sums[7]
    grad_lgates = jnp.concatenate(
        [gate_sums[:, :head_size], gate_sums[:, LANES : LANES + head_size]], axis=1
    )
    from_next = passed_along(as_sent(lead[:, SUBLANES - rim_size :, :]), "seq", -1)
    ending = tail + jnp.pad(from_next.astype(jnp.float32), ((0, 0), (SUBLANES - rim_size, 0), (0, 0)))
    branch_low = lax.dynamic_update_slice(
        branch_local, ending.astype(jnp.bfloat16), (0, block_len - SUBLANES, 0)
    ).reshape(tok_count, rec_width)
    grad_rin = trans_dot(normed_low, branch_low)
    grad_rgate = trans_dot(normed_low, gate_low)
    grad_norm1 = back_dot(branch_low, recur_input) + back_dot(gate_low, recur_gate)
    input_part, grad_gain1 = norm_back(grad_norm1, normed_one, inv_one, norm1_gain)
    grad_x = (grad_resid + input_part).astype(jnp.bfloat16).reshape(row_count, block_len, model_dim)
    grad_tokens = lax.all_to_all(grad_x, "chan", split_axis=2, concat_axis=0, tiled=True)
    terms = (
        grad_gain1,
        lane_rows(grad_rin),
        lane_rows(grad_rgate),
        grad_ckernel,
        grad_cbias,
        grad_lgates,
        grad_lbias,
        grad_decay,
        lane_rows(grad_rout),
        grad_gain2,
        lane_rows(grad_mgate),
        lane_rows(grad_mup),
        lane_rows(grad_down),
    )
    summed = (
        lax.psum_scatter(terms[0], ("seq", "chan"), scatter_dimension=0, tiled=True),
        lax.psum_scatter(terms[1], ("seq", "chan"), scatter_dimension=0, tiled=True),
        lax.psum_scatter(terms[2], ("seq", "chan"), scatter_dimension=0, tiled=True),
        lax.psum_scatter(terms[3], ("seq", "chan"), scatter_dimension=1, tiled=True),
        lax.psum_scatter(terms[4], ("seq", "chan"), scatter_dimension=0, tiled=True),
        lax.psum_scatter(terms[5], ("seq", "chan"), scatter_dimension=0, tiled=True),
        lax.psum_scatter(terms[6], ("seq", "chan"), scatter_dimension=1, tiled=True),
        lax.psum_scatter(terms[7], ("seq", "chan"), scatter_dimension=0, tiled=True),
        lax.psum_scatter(terms[8], ("seq", "chan"), scatter_dimension=0, tiled=True),
        lax.psum_scatter(terms[9], ("seq", "chan"), scatter_dimension=0, tiled=True),
        lax.psum_scatter(terms[10], ("seq", "chan"), scatter_dimension=0, tiled=True),
        lax.psum_scatter(terms[11], ("seq", "chan"), scatter_dimension=0, tiled=True),
        lax.psum_scatter(terms[12], ("seq", "chan"), scatter_dimension=0, tiled=True),
    )
    (
        sum_gain1,
        sum_rin,
        sum_rgate,
        sum_ckernel,
        sum_cbias,
        sum_lgates,
        sum_lbias,
        sum_decay,
        sum_rout,
        sum_gain2,
        sum_mgate,
        sum_mup,
        sum_down,
    ) = summed
    return (
        output,
        grad_tokens,
        sum_gain1,
        sum_rin.reshape(-1, rec_width),
        sum_rgate.reshape(-1, rec_width),
        sum_ckernel,
        sum_cbias,
        sum_lgates,
        sum_lbias,
        sum_decay,
        sum_rout.reshape(-1, model_dim),
        sum_gain2,
        sum_mgate.reshape(-1, ffn_width),
        sum_mup.reshape(-1, ffn_width),
        sum_down.reshape(-1, model_dim),
    )


def solution(mesh):
    return jax.shard_map(
        body,
        mesh=mesh,
        in_specs=(
            P(None, "seq", "chan"),
            P(None, "seq", "chan"),
            P("chan", None),
            P("chan"),
            P(),
            P(),
            P(),
            P(),
            P(),
            P(),
            P(),
            P(),
            P(),
            P(),
            P(),
            P(),
            P(),
        ),
        out_specs=(
            P(None, "seq", "chan"),
            P(None, "seq", "chan"),
            P(("seq", "chan")),
            P(("seq", "chan"), None),
            P(("seq", "chan"), None),
            P(None, ("seq", "chan")),
            P(("seq", "chan")),
            P(("seq", "chan"), None),
            P(None, ("seq", "chan")),
            P(("seq", "chan")),
            P(("seq", "chan"), None),
            P(("seq", "chan")),
            P(("seq", "chan"), None),
            P(("seq", "chan"), None),
            P(("seq", "chan"), None),
        ),
        check_vma=False,
    )
```

```python
import functools
import math

import jax
import jax.numpy as jnp
from jax import lax
from jax.experimental import pallas as pl
from jax.experimental.pallas import tpu as pltpu
from jax.sharding import PartitionSpec as P

H = 16


EPS = 1e-06
ROOT_FLOOR = 1e-06
LANES = 128
SUBLANES = 8
STEP = 16
VMEM_BYTES = 56 * 1024 * 1024


def sigmoid(value):
    return 0.5 * jnp.tanh(0.5 * value) + 0.5


GELU_C = 0.7978845608
GELU_A = 0.044715


def gelu_pair(value):
    square = value * value
    inner = jnp.tanh(value * (GELU_C + (GELU_C * GELU_A) * square))
    half = 0.5 + 0.5 * inner
    slope = GELU_C + (3.0 * GELU_C * GELU_A) * square
    return (value * half, half + 0.5 * value * (1.0 - inner * inner) * slope)


def root_argument(log_decay, decay):
    y = 2.0 * log_decay
    series = 1.0 + y * (1.0 / 7.0)
    for divisor in (6.0, 5.0, 4.0, 3.0, 2.0):
        series = 1.0 + (y * (1.0 / divisor)) * series
    return jnp.where(y > -0.25, -y * series, 1.0 - decay * decay)


def across(column, width):
    return jnp.concatenate([column] * (width // LANES), axis=1)


def forward_kernel(
    branch_ref,
    rim_ref,
    dist_ref,
    par_ref,
    gates_ref,
    lru_ref,
    rate_ref,
    igate_ref,
    state_ref,
    cum_ref,
    both_ref,
):
    rows, length, width = branch_ref.shape
    taps = [par_ref[k : k + 1, :] for k in range(4)]
    conv_bias, rate_bias, input_bias, soft = (par_ref[k : k + 1, :] for k in range(4, 8))
    place = lax.broadcasted_iota(jnp.int32, (SUBLANES, width), 0)

    for row in range(rows):

        def conv_step(index, before, row=row):
            base = pl.multiple_of(index * STEP, STEP)
            pieces = []
            for half in range(STEP // SUBLANES):
                at = pl.ds(base + half * SUBLANES, SUBLANES)
                here = branch_ref[row, at, :]
                dist = across(dist_ref[row, at, :], width)
                total = conv_bias + taps[0] * here
                for k in range(1, 4):
                    shifted = pltpu.roll(jnp.where(place < SUBLANES - k, here, before), k, 0)
                    total = total + taps[k] * jnp.where(dist >= k, shifted, 0.0)
                pieces.append(total)
                before = here
            lru_ref[row, pl.ds(base, STEP), :] = jnp.concatenate(pieces, axis=0).astype(jnp.bfloat16)
            return before

        lax.fori_loop(0, length // STEP, conv_step, rim_ref[row])

        piece = min(length, 256)

        def dot_step(index, carry, row=row):
            at = pl.ds(pl.multiple_of(index * piece, piece), piece)
            both_ref[row, at, :] = jnp.dot(
                lru_ref[row, at, :], gates_ref[...], preferred_element_type=jnp.float32
            )
            return carry

        lax.fori_loop(0, length // piece, dot_step, 0)

    def scan_step(index, carry):
        base = pl.multiple_of(index * STEP, STEP)
        later = []
        for row in range(rows):
            run_cum, run_state = carry[row]
            lru_both = lru_ref[row, pl.ds(base, STEP), :].astype(jnp.float32)
            for half in range(STEP // SUBLANES):
                at = pl.ds(base + half * SUBLANES, SUBLANES)
                lru = lru_both[half * SUBLANES : (half + 1) * SUBLANES]
                start = across(dist_ref[row, at, :], width) == 0
                rate = sigmoid(both_ref[row, at, :width] + rate_bias)
                igate = sigmoid(both_ref[row, at, width:] + input_bias)
                log_decay = rate * soft
                decay = jnp.exp(log_decay)
                arg = jnp.maximum(root_argument(log_decay, decay), ROOT_FLOOR)
                root = arg * lax.rsqrt(arg)
                cum = jnp.where(start, 0.0, decay)
                value = jnp.where(start, 1.0, root) * igate * lru
                rate_ref[row, at, :] = rate
                igate_ref[row, at, :] = igate
                for shift in (1, 2, 4):
                    live = place >= shift
                    value = value + cum * jnp.where(live, pltpu.roll(value, shift, 0), 0.0)
                    cum = cum * jnp.where(live, pltpu.roll(cum, shift, 0), 1.0)
                value = value + cum * run_state
                cum = cum * run_cum
                state_ref[row, at, :] = value
                cum_ref[row, at, :] = cum
                run_state = value[SUBLANES - 1 :, :]
                run_cum = cum[SUBLANES - 1 :, :]
            later.append((run_cum, run_state))
        return tuple(later)

    one, zero = (jnp.ones((1, width), jnp.float32), jnp.zeros((1, width), jnp.float32))
    lax.fori_loop(0, length // STEP, scan_step, tuple((one, zero) for _ in range(rows)))


def adjoint_kernel(
    dmix_ref,
    pre_ref,
    state_ref,
    cum_ref,
    carry_ref,
    rate_ref,
    dist_ref,
    par_ref,
    dgate_ref,
    local_ref,
    back_ref,
    first_ref,
):
    rows, length, width = dmix_ref.shape
    soft = par_ref[7:8, :]
    place = lax.broadcasted_iota(jnp.int32, (SUBLANES, width), 0)
    last = length // STEP - 1

    def step(index, carry):
        base = pl.multiple_of((last - index) * STEP, STEP)
        later = []
        for row in range(rows):
            run_cum, run_back = carry[row]
            entering = carry_ref[row]
            pieces = []
            for half in reversed(range(STEP // SUBLANES)):
                at = pl.ds(base + half * SUBLANES, SUBLANES)
                start = across(dist_ref[row, at, :], width) == 0
                state = state_ref[row, at, :] + cum_ref[row, at, :] * entering
                act, slope = gelu_pair(pre_ref[row, at, :])
                dmix = dmix_ref[row, at, :]
                pieces.append(dmix * state * slope)
                dstate = dmix * act
                coef = jnp.where(start, 0.0, jnp.exp(rate_ref[row, at, :] * soft))
                value = coef * dstate
                for shift in (1, 2, 4):
                    live = place < SUBLANES - shift
                    turn = SUBLANES - shift
                    value = value + coef * jnp.where(live, pltpu.roll(value, turn, 0), 0.0)
                    coef = coef * jnp.where(live, pltpu.roll(coef, turn, 0), 1.0)
                value = value + coef * run_back
                coef = coef * run_cum
                inside = place < SUBLANES - 1
                local_ref[row, at, :] = dstate + jnp.where(
                    inside, pltpu.roll(value, SUBLANES - 1, 0), run_back
                )
                back_ref[row, at, :] = jnp.where(inside, pltpu.roll(coef, SUBLANES - 1, 0), run_cum)
                run_back = value[:1, :]
                run_cum = coef[:1, :]
            dgate_ref[row, pl.ds(base, STEP), :] = jnp.concatenate(pieces[::-1], axis=0).astype(
                jnp.bfloat16
            )
            later.append((run_cum, run_back))
        return tuple(later)

    one, zero = (jnp.ones((1, width), jnp.float32), jnp.zeros((1, width), jnp.float32))
    done = lax.fori_loop(0, last + 1, step, tuple((one, zero) for _ in range(rows)))
    for row in range(rows):
        first_ref[row] = done[row][1]


def backward_kernel(
    head_size,
    local_ref,
    back_ref,
    out_ref,
    state_ref,
    cum_ref,
    in_ref,
    rate_ref,
    igate_ref,
    lru_ref,
    dist_ref,
    branch_ref,
    rim_ref,
    par_ref,
    gates_ref,
    dbranch_ref,
    tail_ref,
    head_ref,
    sums_ref,
    dgates_ref,
    both_ref,
    dconv_ref,
):
    rows, length, width = local_ref.shape
    taps = [par_ref[k : k + 1, :] for k in range(4)]
    soft = par_ref[7:8, :]
    place = lax.broadcasted_iota(jnp.int32, (SUBLANES, width), 0)
    zeros = jnp.zeros((SUBLANES, width), jnp.float32)

    def gate_step(index, carry):
        sums, earlier = carry
        decay_sum, rate_sum, input_sum = sums
        base = pl.multiple_of(index * STEP, STEP)
        later = []
        for row in range(rows):
            before = earlier[row]
            entering = in_ref[row]
            leaving = out_ref[row]
            lru_both = lru_ref[row, pl.ds(base, STEP), :].astype(jnp.float32)
            drates, dinputs = ([], [])
            for half in range(STEP // SUBLANES):
                at = pl.ds(base + half * SUBLANES, SUBLANES)
                lru = lru_both[half * SUBLANES : (half + 1) * SUBLANES]
                start = across(dist_ref[row, at, :], width) == 0
                adjoint = local_ref[row, at, :] + back_ref[row, at, :] * leaving
                state = state_ref[row, at, :] + cum_ref[row, at, :] * entering
                previous = jnp.where(place < 1, before, pltpu.roll(state, 1, 0))
                before = state[SUBLANES - 1 :, :]
                rate = rate_ref[row, at, :]
                igate = igate_ref[row, at, :]
                log_decay = rate * soft
                decay = jnp.exp(log_decay)
                arg = root_argument(log_decay, decay)
                above = arg > ROOT_FLOOR
                arg = jnp.maximum(arg, ROOT_FLOOR)
                inverse = lax.rsqrt(arg)
                scale = jnp.where(start, 1.0, arg * inverse)
                gated = adjoint * igate
                dscale = gated * lru
                pull = jnp.where(above, dscale * decay * decay * inverse, 0.0)
                dlog = jnp.where(start, 0.0, adjoint * previous * decay - pull)
                dig = adjoint * scale * lru
                weighted = dlog * rate
                decay_sum = decay_sum + weighted
                drates.append(weighted * soft * (1.0 - rate))
                dinputs.append(dig * igate * (1.0 - igate))
                dconv_ref[row, at, :] = gated * scale
            drate = jnp.concatenate(drates, axis=0).astype(jnp.bfloat16)
            dinput = jnp.concatenate(dinputs, axis=0).astype(jnp.bfloat16)
            both_ref[row, pl.ds(base, STEP), :width] = drate
            both_ref[row, pl.ds(base, STEP), width:] = dinput
            drate = drate.astype(jnp.float32)
            dinput = dinput.astype(jnp.float32)
            rate_sum = rate_sum + (drate[:SUBLANES] + drate[SUBLANES:])
            input_sum = input_sum + (dinput[:SUBLANES] + dinput[SUBLANES:])
            later.append(before)
        return ((decay_sum, rate_sum, input_sum), tuple(later))

    sums, _ = lax.fori_loop(
        0,
        length // STEP,
        gate_step,
        ((zeros, zeros, zeros), tuple(in_ref[row] for row in range(rows))),
    )
    for slot, total in zip((5, 6, 7), (sums[1], sums[2], sums[0])):
        sums_ref[slot : slot + 1, :] = jnp.sum(total, axis=0, keepdims=True)

    piece = min(length, 256)
    wide = None
    for row in range(rows):

        def dot_step(index, carry, row=row):
            at = pl.ds(pl.multiple_of(index * piece, piece), piece)
            dconv_ref[row, at, :] += lax.dot_general(
                both_ref[row, at, :],
                gates_ref[...],
                (((1,), (1,)), ((), ())),
                preferred_element_type=jnp.float32,
            )
            return carry

        lax.fori_loop(0, length // piece, dot_step, 0)
        part = lax.dot_general(
            lru_ref[row], both_ref[row], (((0,), (0,)), ((), ())), preferred_element_type=jnp.float32
        )
        wide = part if wide is None else wide + part
    row_head = lax.broadcasted_iota(jnp.int32, (width, width), 0) // head_size
    col_head = lax.broadcasted_iota(jnp.int32, (width, width), 1) // head_size
    own = row_head == col_head
    for part in range(2):
        kept = jnp.where(own, wide[:, part * width : (part + 1) * width], 0.0)
        folded = kept
        for other in range(1, width // head_size):
            folded = folded + pltpu.roll(kept, width - other * head_size, 1)
        dgates_ref[:, part * LANES : (part + 1) * LANES] = folded[:, :LANES]

    def conv_step(index, carry):
        sums, following = carry
        sums = list(sums)
        base = pl.multiple_of((length // STEP - 1 - index) * STEP, STEP)
        later = []
        for row in range(rows):
            after = following[row]
            pieces = []
            for half in reversed(range(STEP // SUBLANES)):
                at = pl.ds(base + half * SUBLANES, SUBLANES)
                dist = across(dist_ref[row, at, :], width)
                branch = branch_ref[row, at, :]
                here = dconv_ref[row, at, :]
                total = taps[0] * here
                sums[0] = sums[0] + here * branch
                sums[4] = sums[4] + here
                masked = tuple(jnp.where(dist >= k, here, 0.0) for k in range(1, 4))
                for k in range(1, 4):
                    moved = pltpu.roll(
                        jnp.where(place >= k, masked[k - 1], after[k - 1]), SUBLANES - k, 0
                    )
                    total = total + taps[k] * moved
                    sums[k] = sums[k] + branch * moved
                after = masked
                pieces.append(total)
            whole = jnp.concatenate(pieces[::-1], axis=0)
            dbranch_ref[row, pl.ds(base, STEP), :] = whole.astype(jnp.bfloat16)
            later.append(after)

            @pl.when(index == 0)
            def _(row=row, whole=whole):
                tail_ref[row] = whole[STEP - SUBLANES :]

        return (tuple(sums), tuple(later))

    sums, firsts = lax.fori_loop(
        0,
        length // STEP,
        conv_step,
        ((zeros,) * 5, tuple((zeros,) * 3 for _ in range(rows))),
    )
    sums = list(sums)
    for row in range(rows):
        total = zeros
        rim = rim_ref[row]
        for k in range(1, 4):
            moved = pltpu.roll(jnp.where(place >= k, 0.0, firsts[row][k - 1]), SUBLANES - k, 0)
            total = total + taps[k] * moved
            sums[k] = sums[k] + rim * moved
        head_ref[row] = total
    for slot in range(5):
        sums_ref[slot : slot + 1, :] = jnp.sum(sums[slot], axis=0, keepdims=True)


def channel_call(kernel, name, arrays, specs, outs, out_specs, scratch, blocks, flops):
    moved = sum(math.prod(a.shape) * a.dtype.itemsize for a in (*arrays, *outs))
    return pl.pallas_call(
        kernel,
        name=name,
        grid=(blocks,),
        in_specs=specs,
        out_specs=out_specs,
        out_shape=outs,
        scratch_shapes=scratch,
        compiler_params=pltpu.CompilerParams(vmem_limit_bytes=VMEM_BYTES),
        cost_estimate=pl.CostEstimate(flops=flops, bytes_accessed=moved, transcendentals=0),
    )(*arrays)


class Recurrence:
    def __init__(self, rows, length, channels, head_size):
        self.rows, self.length, self.channels = (rows, length, channels)
        self.head_size = head_size
        self.width = head_size * LANES // math.gcd(head_size, LANES)
        self.blocks = channels // self.width
        self.flops = 2 * rows * length * channels * 2 * self.width

    def tall(self):
        return pl.BlockSpec((self.rows, self.length, self.width), lambda j: (0, 0, j))

    def short(self, size):
        return pl.BlockSpec((self.rows, size, self.width), lambda j: (0, 0, j))

    def flat(self, size):
        return pl.BlockSpec((size, self.width), lambda j: (0, j))

    def dist(self):
        return pl.BlockSpec((self.rows, self.length, LANES), lambda j: (0, 0, 0))

    def gates(self, columns):
        return pl.BlockSpec((self.width, columns), lambda j: (j, 0))

    def shape(self, size, dtype):
        return jax.ShapeDtypeStruct((self.rows, size, self.channels), dtype)

    def widen(self, lru_gates):
        size, width = (self.head_size, self.width)
        heads = width // size
        column = jnp.arange(2 * width)
        source = (column // width) * size + column % size
        spread = (jnp.arange(2 * size)[:, None] == source[None, :]).astype(jnp.bfloat16)
        owner = (column % width) // size
        mine = (jnp.arange(self.channels) // size) % heads
        wide = jnp.dot(lru_gates, spread, preferred_element_type=jnp.float32)
        return jnp.where(mine[:, None] == owner[None, :], wide, 0.0).astype(jnp.bfloat16)

    def forward(self, branch, rim, dist, params, gates):
        f32 = jnp.float32
        outs = [self.shape(self.length, d) for d in (jnp.bfloat16, f32, f32, f32, f32)]
        return channel_call(
            forward_kernel,
            "recurrence_forward",
            (branch, rim, dist, params, gates),
            [self.tall(), self.short(SUBLANES), self.dist(), self.flat(16), self.gates(2 * self.width)],
            outs,
            [self.tall()] * 5,
            [pltpu.VMEM((self.rows, self.length, 2 * self.width), f32)],
            self.blocks,
            self.flops,
        )

    def adjoint(self, dmix, pre, state, cum, entering, rate, dist, params):
        f32 = jnp.float32
        outs = [self.shape(self.length, d) for d in (jnp.bfloat16, f32, f32)] + [self.shape(1, f32)]
        tall = self.tall()
        return channel_call(
            adjoint_kernel,
            "recurrence_adjoint",
            (dmix, pre, state, cum, entering, rate, dist, params),
            [tall, tall, tall, tall, self.short(1), tall, self.dist(), self.flat(16)],
            outs,
            [tall, tall, tall, self.short(1)],
            [],
            self.blocks,
            0,
        )

    def backward(
        self, local, back, leaving, state, cum, entering, rate, igate, lru, dist, branch, rim, params, gates
    ):
        f32 = jnp.float32
        outs = [
            self.shape(self.length, jnp.bfloat16),
            self.shape(SUBLANES, f32),
            self.shape(SUBLANES, f32),
            jax.ShapeDtypeStruct((SUBLANES, self.channels), f32),
            jax.ShapeDtypeStruct((self.channels, 2 * LANES), f32),
        ]
        tall, one = (self.tall(), self.short(1))
        return channel_call(
            functools.partial(backward_kernel, self.head_size),
            "recurrence_backward",
            (local, back, leaving, state, cum, entering, rate, igate, lru, dist, branch, rim, params, gates),
            [tall, tall, one, tall, tall, one, tall, tall, tall, self.dist(), tall]
            + [self.short(SUBLANES), self.flat(16), self.gates(2 * self.width)],
            outs,
            [tall, self.short(SUBLANES), self.short(SUBLANES), self.flat(SUBLANES), self.gates(2 * LANES)],
            [
                pltpu.VMEM((self.rows, self.length, 2 * self.width), jnp.bfloat16),
                pltpu.VMEM((self.rows, self.length, self.width), f32),
            ],
            self.blocks,
            2 * self.flops,
        )


def carried(factor, value, axis, backward):
    count, mine = (lax.axis_size(axis), lax.axis_index(axis))
    pieces = lax.all_gather(jnp.stack([factor, value]), axis)
    order = range(count - 1, 0, -1) if backward else range(count - 1)
    total = jnp.zeros_like(value)
    for place in order:
        longer = pieces[place, 0] * total + pieces[place, 1]
        total = jnp.where(place > mine if backward else place < mine, longer, total)
    return total


def passed_along(value, axis, steps):
    count = lax.axis_size(axis)
    leading, last = (max(0, -steps), min(count, count - steps))
    return lax.ppermute(value, axis, [(source, source + steps) for source in range(leading, last)])


def weight_grad(left, right):
    return lax.dot_general(
        left, right, (((0,), (0,)), ((), ())), preferred_element_type=jnp.float32
    ).astype(jnp.bfloat16)


def back_dot(left, right):
    return lax.dot_general(
        left, right, (((1,), (1,)), ((), ())), preferred_element_type=jnp.float32
    )


def fwd_dot(left, right):
    return jnp.dot(left, right, preferred_element_type=jnp.float32)


def gelu_fn(value):
    return jax.nn.gelu(value, approximate=True)


def norm_back(grad_norm, normed, inverse, gain):
    scaled = grad_norm * gain
    mean_term = jnp.mean(scaled * normed, axis=1, keepdims=True)
    return inverse * (scaled - normed * mean_term)


def halved(blocks, axis, bit, high, dtype):
    count = lax.axis_size(axis)
    mine = (lax.axis_index(axis) >> bit) & 1
    half = blocks.shape[0] // 2
    place = 0 if high else 1
    pairs = blocks.reshape(((2, half) if high else (half, 2)) + blocks.shape[1:])
    sent = lax.dynamic_index_in_dim(pairs, 1 - mine, place, keepdims=False)
    kept = lax.dynamic_index_in_dim(pairs, mine, place, keepdims=False)
    got = lax.ppermute(sent, axis, [(source, source ^ (1 << bit)) for source in range(count)])
    return (kept.astype(jnp.float32) + got.astype(jnp.float32)).astype(dtype)


def bits(axis):
    return range(lax.axis_size(axis).bit_length() - 1)


def core_summed(gradient):
    devices = lax.axis_size(("seq", "zed", "core"))
    blocks = gradient.reshape(devices, gradient.shape[0] // devices, gradient.shape[1])
    return halved(blocks, "core", 0, False, gradient.dtype)


def chips_summed(blocks, high):
    seq, zed = (lax.axis_size("seq"), lax.axis_size("zed"))
    low = blocks.dtype
    seq_bits = reversed(bits("seq")) if high else bits("seq")
    for bit in seq_bits:
        outer = blocks.shape[0] // zed
        blocks = blocks.reshape((outer, zed) + blocks.shape[1:])
        blocks = halved(blocks, "seq", bit, high, low)
        blocks = blocks.reshape((outer // 2 * zed,) + blocks.shape[2:])
    for bit in bits("zed"):
        blocks = halved(blocks, "zed", bit, False, jnp.float32 if bit == bits("zed")[-1] else low)
    return blocks[0]


def body(
    tokens,
    cotangent,
    doc_starts,
    lengths,
    norm1_gain,
    recur_input,
    recur_gate,
    conv_kernel,
    conv_bias,
    lru_gates,
    lru_bias,
    lru_decay,
    recur_out,
    norm2_gain,
    mlp_gate,
    mlp_up,
    mlp_down,
):
    seq_x, seq_g = (
        lax.all_to_all(tokens, ("zed", "core"), split_axis=0, concat_axis=2, tiled=True),
        lax.all_to_all(cotangent, ("zed", "core"), split_axis=0, concat_axis=2, tiled=True),
    )
    row_count, block_len, model_dim = seq_x.shape
    tok_count = row_count * block_len
    rec_width = recur_input.shape[1]
    ffn_width = mlp_gate.shape[1]
    head_count = H
    head_size = rec_width // head_count
    tap_count = conv_kernel.shape[0]
    rim_size = tap_count - 1
    seq_index = lax.axis_index("seq")
    position = seq_index * block_len + jnp.arange(block_len, dtype=jnp.int32)
    bounds = jnp.concatenate([doc_starts, lengths[:, None]], axis=1)
    is_before = bounds[:, None, :] <= position[None, :, None]
    seg_start = jnp.max(jnp.where(is_before, bounds[:, None, :], 0), axis=2)
    is_valid = (position[None, :] < lengths[:, None]).reshape(tok_count, 1)
    flat_x = seq_x.reshape(tok_count, model_dim).astype(jnp.float32)
    inv_one = lax.rsqrt(jnp.mean(flat_x * flat_x, axis=1, keepdims=True) + EPS)
    normed_one = flat_x * inv_one
    normed_low = (normed_one * norm1_gain).astype(jnp.bfloat16)
    branch_pre = fwd_dot(normed_low, recur_input)
    gate_pre = fwd_dot(normed_low, recur_gate)
    gate_act = gelu_fn(gate_pre)
    branch_rows = branch_pre.reshape(row_count, block_len, rec_width)
    core = Recurrence(row_count, block_len, rec_width, head_size)
    prev_rim = passed_along(
        branch_rows[:, block_len - rim_size :, :].astype(jnp.bfloat16), "seq", 1
    ).astype(jnp.float32)
    rim = jnp.pad(prev_rim, ((0, 0), (SUBLANES - rim_size, 0), (0, 0)))
    dist = jnp.broadcast_to(
        (position[None, :] - seg_start)[:, :, None], (row_count, block_len, LANES)
    )
    soft_decay = jax.nn.softplus(-lru_decay)
    params = jnp.concatenate(
        [
            conv_kernel,
            conv_bias[None],
            lru_bias,
            (-8.0 * soft_decay)[None],
            jnp.zeros((SUBLANES, rec_width), jnp.float32),
        ],
        axis=0,
    )
    wide_gates = core.widen(lru_gates)
    lru_in, rate_gate, input_gate, local_state, cum_coef = core.forward(
        branch_rows, rim, dist, params, wide_gates
    )
    carry_in = carried(cum_coef[:, -1, :], local_state[:, -1, :], "seq", False)
    entering = carry_in[:, None, :]
    state_rows = local_state + cum_coef * entering
    state_flat = state_rows.reshape(tok_count, rec_width)
    mixed_low = (state_flat * gate_act).astype(jnp.bfloat16)
    resid_one = flat_x + fwd_dot(mixed_low, recur_out)
    inv_two = lax.rsqrt(jnp.mean(resid_one * resid_one, axis=1, keepdims=True) + EPS)
    normed_two = resid_one * inv_two
    normed_low2 = (normed_two * norm2_gain).astype(jnp.bfloat16)
    mlp_gate_pre = fwd_dot(normed_low2, mlp_gate)
    mlp_up_pre = fwd_dot(normed_low2, mlp_up)
    gelu_gate = gelu_fn(mlp_gate_pre)
    hidden_low = (gelu_gate * mlp_up_pre).astype(jnp.bfloat16)
    result = (resid_one + fwd_dot(hidden_low, mlp_down)).astype(jnp.bfloat16)
    output = lax.all_to_all(
        result.reshape(row_count, block_len, model_dim),
        ("zed", "core"),
        split_axis=2,
        concat_axis=0,
        tiled=True,
    )
    grad_out = jnp.where(is_valid, seq_g.reshape(tok_count, model_dim).astype(jnp.float32), 0.0)
    grad_low = grad_out.astype(jnp.bfloat16)
    grad_down = core_summed(weight_grad(hidden_low, grad_low))
    grad_hidden = back_dot(grad_low, mlp_down)
    _, gelu_pull = jax.vjp(gelu_fn, mlp_gate_pre)
    mgate_low = gelu_pull(grad_hidden * mlp_up_pre)[0].astype(jnp.bfloat16)
    mup_low = (grad_hidden * gelu_gate).astype(jnp.bfloat16)
    grad_mgate = core_summed(weight_grad(normed_low2, mgate_low))
    grad_mup = core_summed(weight_grad(normed_low2, mup_low))
    chips = grad_down.shape[0]
    parts = [
        jnp.swapaxes(part.reshape(chips, part.shape[1], -1, model_dim), 1, 2).reshape(
            chips, -1, model_dim
        )
        for part in (grad_mgate, grad_mup)
    ]
    merged = jnp.concatenate([*parts, grad_down], axis=1)
    own = lax.psum_scatter(merged, ("seq", "zed"), scatter_dimension=0, tiled=True)[0]
    own = own.astype(jnp.float32)
    own_rows = model_dim // (2 * chips)
    count = parts[0].shape[1]

    def unfolded(part):
        return jnp.swapaxes(part.reshape(-1, own_rows, model_dim), 0, 1).reshape(own_rows, -1)

    sum_mgate, sum_mup = (unfolded(own[:count]), unfolded(own[count : 2 * count]))
    sum_down = own[2 * count :]
    grad_norm2 = back_dot(mgate_low, mlp_gate) + back_dot(mup_low, mlp_up)
    resid_part = norm_back(grad_norm2, normed_two, inv_two, norm2_gain)
    grad_resid = grad_out + resid_part
    resid_low = grad_resid.astype(jnp.bfloat16)
    sum_rout = chips_summed(core_summed(weight_grad(mixed_low, resid_low)), True)
    grad_mixed = back_dot(resid_low, recur_out)
    gate_low, back_local, back_cum, first_term = core.adjoint(
        grad_mixed.reshape(row_count, block_len, rec_width),
        gate_pre.reshape(row_count, block_len, rec_width),
        local_state,
        cum_coef,
        entering,
        rate_gate,
        dist,
        params,
    )
    gate_low = gate_low.reshape(tok_count, rec_width)
    carry_out = carried(cum_coef[:, -1, :], first_term[:, 0, :], "seq", True)
    branch_local, tail, lead, channel_sums, gate_sums = core.backward(
        back_local,
        back_cum,
        carry_out[:, None, :],
        local_state,
        cum_coef,
        entering,
        rate_gate,
        input_gate,
        lru_in,
        dist,
        branch_rows,
        rim,
        params,
        wide_gates,
    )
    spare = jnp.swapaxes(channel_sums, 0, 1)
    small = jnp.concatenate(
        [gate_sums[:, :head_size], spare, gate_sums[:, head_size + SUBLANES :]], axis=1
    )
    own_small = chips_summed(core_summed(small), True)
    sum_lgates = jnp.concatenate(
        [own_small[:, :head_size], own_small[:, LANES : LANES + head_size]], axis=1
    )
    own_sums = jnp.swapaxes(own_small[:, head_size : head_size + SUBLANES], 0, 1)
    from_next = passed_along(
        lead[:, SUBLANES - rim_size :, :].astype(jnp.bfloat16), "seq", -1
    )
    ending = tail + jnp.pad(from_next.astype(jnp.float32), ((0, 0), (SUBLANES - rim_size, 0), (0, 0)))
    branch_low = lax.dynamic_update_slice(
        branch_local, ending.astype(jnp.bfloat16), (0, block_len - SUBLANES, 0)
    ).reshape(tok_count, rec_width)
    sum_rin = chips_summed(core_summed(weight_grad(normed_low, branch_low)), False)
    sum_rgate = chips_summed(core_summed(weight_grad(normed_low, gate_low)), False)
    grad_norm1 = back_dot(branch_low, recur_input) + back_dot(gate_low, recur_gate)
    input_part = norm_back(grad_norm1, normed_one, inv_one, norm1_gain)
    grad_x = (grad_resid + input_part).astype(jnp.bfloat16).reshape(row_count, block_len, model_dim)
    grad_tokens = lax.all_to_all(grad_x, ("zed", "core"), split_axis=2, concat_axis=0, tiled=True)
    device = lax.axis_index(("seq", "zed", "core"))

    def mine(array, size, axis=0):
        return lax.dynamic_slice_in_dim(array, device * size, size, axis)

    def weighed(weight, gradient):
        return jnp.sum(mine(weight, own_rows).astype(jnp.float32) * gradient, axis=1)

    sum_gain1 = (weighed(recur_input, sum_rin) + weighed(recur_gate, sum_rgate)) / mine(
        norm1_gain, own_rows
    )
    sum_gain2 = (weighed(mlp_gate, sum_mgate) + weighed(mlp_up, sum_mup)) / mine(
        norm2_gain, own_rows
    )
    own_channels = own_sums.shape[1]
    sum_decay = 8.0 * jax.nn.sigmoid(-mine(lru_decay, own_channels)) * own_sums[7]
    return (
        output,
        grad_tokens,
        sum_gain1,
        sum_rin,
        sum_rgate,
        own_sums[:4],
        own_sums[4],
        sum_lgates,
        own_sums[5:7],
        sum_decay,
        sum_rout,
        sum_gain2,
        sum_mgate,
        sum_mup,
        sum_down,
    )


def solution(mesh):
    seq, chan = (mesh.shape["seq"], mesh.shape["chan"])
    chips = jax.sharding.Mesh(mesh.devices.reshape(seq, chan // 2, 2), ("seq", "zed", "core"))
    chan = ("zed", "core")
    every = ("seq", "zed", "core")
    activations = P(None, "seq", chan)
    rows, columns, vector = (P(every, None), P(None, every), P(every))
    return jax.shard_map(
        body,
        mesh=chips,
        in_specs=(activations, activations, P(chan, None), P(chan)) + (P(),) * 13,
        out_specs=(
            activations,
            activations,
            vector,
            rows,
            rows,
            columns,
            vector,
            rows,
            columns,
            vector,
            rows,
            vector,
            rows,
            rows,
            rows,
        ),
        check_vma=False,
    )
```

```python
import functools
import math

import jax
import jax.numpy as jnp
from jax import lax
from jax.experimental import pallas as pl
from jax.experimental.pallas import tpu as pltpu
from jax.sharding import PartitionSpec as P

H = 16


EPS = 1e-06
ROOT_FLOOR = 1e-06
LANES = 128
SUBLANES = 8
STEP = 16
VMEM_BYTES = 56 * 1024 * 1024


def sigmoid(value):
    return 0.5 * jnp.tanh(0.5 * value) + 0.5


GELU_C = 0.7978845608
GELU_A = 0.044715


def gelu_pair(value):
    square = value * value
    inner = jnp.tanh(value * (GELU_C + (GELU_C * GELU_A) * square))
    half = 0.5 + 0.5 * inner
    slope = GELU_C + (3.0 * GELU_C * GELU_A) * square
    return (value * half, half + 0.5 * value * (1.0 - inner * inner) * slope)


def root_argument(log_decay, decay):
    y = 2.0 * log_decay
    series = 1.0 + y * (1.0 / 7.0)
    for divisor in (6.0, 5.0, 4.0, 3.0, 2.0):
        series = 1.0 + (y * (1.0 / divisor)) * series
    return jnp.where(y > -0.25, -y * series, 1.0 - decay * decay)


def across(column, width):
    return jnp.concatenate([column] * (width // LANES), axis=1)


def forward_kernel(
    branch_ref,
    rim_ref,
    dist_ref,
    par_ref,
    gates_ref,
    lru_ref,
    rate_ref,
    igate_ref,
    state_ref,
    cum_ref,
    both_ref,
):
    rows, length, width = branch_ref.shape
    taps = [par_ref[k : k + 1, :] for k in range(4)]
    conv_bias, rate_bias, input_bias, soft = (par_ref[k : k + 1, :] for k in range(4, 8))
    place = lax.broadcasted_iota(jnp.int32, (SUBLANES, width), 0)

    for row in range(rows):

        def conv_step(index, before, row=row):
            base = pl.multiple_of(index * STEP, STEP)
            pieces = []
            for half in range(STEP // SUBLANES):
                at = pl.ds(base + half * SUBLANES, SUBLANES)
                here = branch_ref[row, at, :]
                dist = across(dist_ref[row, at, :], width)
                total = conv_bias + taps[0] * here
                for k in range(1, 4):
                    shifted = pltpu.roll(jnp.where(place < SUBLANES - k, here, before), k, 0)
                    total = total + taps[k] * jnp.where(dist >= k, shifted, 0.0)
                pieces.append(total)
                before = here
            lru_ref[row, pl.ds(base, STEP), :] = jnp.concatenate(pieces, axis=0).astype(jnp.bfloat16)
            return before

        lax.fori_loop(0, length // STEP, conv_step, rim_ref[row])

        piece = min(length, 256)

        def dot_step(index, carry, row=row):
            at = pl.ds(pl.multiple_of(index * piece, piece), piece)
            both_ref[row, at, :] = jnp.dot(
                lru_ref[row, at, :], gates_ref[...], preferred_element_type=jnp.float32
            )
            return carry

        lax.fori_loop(0, length // piece, dot_step, 0)

    def scan_step(index, carry):
        base = pl.multiple_of(index * STEP, STEP)
        later = []
        for row in range(rows):
            run_cum, run_state = carry[row]
            lru_both = lru_ref[row, pl.ds(base, STEP), :].astype(jnp.float32)
            for half in range(STEP // SUBLANES):
                at = pl.ds(base + half * SUBLANES, SUBLANES)
                lru = lru_both[half * SUBLANES : (half + 1) * SUBLANES]
                start = across(dist_ref[row, at, :], width) == 0
                rate = sigmoid(both_ref[row, at, :width] + rate_bias)
                igate = sigmoid(both_ref[row, at, width:] + input_bias)
                log_decay = rate * soft
                decay = jnp.exp(log_decay)
                arg = jnp.maximum(root_argument(log_decay, decay), ROOT_FLOOR)
                root = arg * lax.rsqrt(arg)
                cum = jnp.where(start, 0.0, decay)
                value = jnp.where(start, 1.0, root) * igate * lru
                rate_ref[row, at, :] = rate
                igate_ref[row, at, :] = igate
                for shift in (1, 2, 4):
                    live = place >= shift
                    value = value + cum * jnp.where(live, pltpu.roll(value, shift, 0), 0.0)
                    cum = cum * jnp.where(live, pltpu.roll(cum, shift, 0), 1.0)
                value = value + cum * run_state
                cum = cum * run_cum
                state_ref[row, at, :] = value
                cum_ref[row, at, :] = cum
                run_state = value[SUBLANES - 1 :, :]
                run_cum = cum[SUBLANES - 1 :, :]
            later.append((run_cum, run_state))
        return tuple(later)

    one, zero = (jnp.ones((1, width), jnp.float32), jnp.zeros((1, width), jnp.float32))
    lax.fori_loop(0, length // STEP, scan_step, tuple((one, zero) for _ in range(rows)))


def adjoint_kernel(
    dmix_ref,
    pre_ref,
    state_ref,
    cum_ref,
    carry_ref,
    rate_ref,
    dist_ref,
    par_ref,
    dgate_ref,
    local_ref,
    back_ref,
    first_ref,
):
    rows, length, width = dmix_ref.shape
    soft = par_ref[7:8, :]
    place = lax.broadcasted_iota(jnp.int32, (SUBLANES, width), 0)
    last = length // STEP - 1

    def step(index, carry):
        base = pl.multiple_of((last - index) * STEP, STEP)
        later = []
        for row in range(rows):
            run_cum, run_back = carry[row]
            entering = carry_ref[row]
            pieces = []
            for half in reversed(range(STEP // SUBLANES)):
                at = pl.ds(base + half * SUBLANES, SUBLANES)
                start = across(dist_ref[row, at, :], width) == 0
                state = state_ref[row, at, :] + cum_ref[row, at, :] * entering
                act, slope = gelu_pair(pre_ref[row, at, :])
                dmix = dmix_ref[row, at, :]
                pieces.append(dmix * state * slope)
                dstate = dmix * act
                coef = jnp.where(start, 0.0, jnp.exp(rate_ref[row, at, :] * soft))
                value = coef * dstate
                for shift in (1, 2, 4):
                    live = place < SUBLANES - shift
                    turn = SUBLANES - shift
                    value = value + coef * jnp.where(live, pltpu.roll(value, turn, 0), 0.0)
                    coef = coef * jnp.where(live, pltpu.roll(coef, turn, 0), 1.0)
                value = value + coef * run_back
                coef = coef * run_cum
                inside = place < SUBLANES - 1
                local_ref[row, at, :] = dstate + jnp.where(
                    inside, pltpu.roll(value, SUBLANES - 1, 0), run_back
                )
                back_ref[row, at, :] = jnp.where(inside, pltpu.roll(coef, SUBLANES - 1, 0), run_cum)
                run_back = value[:1, :]
                run_cum = coef[:1, :]
            dgate_ref[row, pl.ds(base, STEP), :] = jnp.concatenate(pieces[::-1], axis=0).astype(
                jnp.bfloat16
            )
            later.append((run_cum, run_back))
        return tuple(later)

    one, zero = (jnp.ones((1, width), jnp.float32), jnp.zeros((1, width), jnp.float32))
    done = lax.fori_loop(0, last + 1, step, tuple((one, zero) for _ in range(rows)))
    for row in range(rows):
        first_ref[row] = done[row][1]


def backward_kernel(
    head_size,
    local_ref,
    back_ref,
    out_ref,
    state_ref,
    cum_ref,
    in_ref,
    rate_ref,
    igate_ref,
    lru_ref,
    dist_ref,
    branch_ref,
    rim_ref,
    par_ref,
    gates_ref,
    dbranch_ref,
    tail_ref,
    head_ref,
    sums_ref,
    dgates_ref,
    both_ref,
    dconv_ref,
):
    rows, length, width = local_ref.shape
    taps = [par_ref[k : k + 1, :] for k in range(4)]
    soft = par_ref[7:8, :]
    place = lax.broadcasted_iota(jnp.int32, (SUBLANES, width), 0)
    zeros = jnp.zeros((SUBLANES, width), jnp.float32)

    def gate_step(index, carry):
        sums, earlier = carry
        decay_sum, rate_sum, input_sum = sums
        base = pl.multiple_of(index * STEP, STEP)
        later = []
        for row in range(rows):
            before = earlier[row]
            entering = in_ref[row]
            leaving = out_ref[row]
            lru_both = lru_ref[row, pl.ds(base, STEP), :].astype(jnp.float32)
            drates, dinputs = ([], [])
            for half in range(STEP // SUBLANES):
                at = pl.ds(base + half * SUBLANES, SUBLANES)
                lru = lru_both[half * SUBLANES : (half + 1) * SUBLANES]
                start = across(dist_ref[row, at, :], width) == 0
                adjoint = local_ref[row, at, :] + back_ref[row, at, :] * leaving
                state = state_ref[row, at, :] + cum_ref[row, at, :] * entering
                previous = jnp.where(place < 1, before, pltpu.roll(state, 1, 0))
                before = state[SUBLANES - 1 :, :]
                rate = rate_ref[row, at, :]
                igate = igate_ref[row, at, :]
                log_decay = rate * soft
                decay = jnp.exp(log_decay)
                arg = root_argument(log_decay, decay)
                above = arg > ROOT_FLOOR
                arg = jnp.maximum(arg, ROOT_FLOOR)
                inverse = lax.rsqrt(arg)
                scale = jnp.where(start, 1.0, arg * inverse)
                gated = adjoint * igate
                dscale = gated * lru
                pull = jnp.where(above, dscale * decay * decay * inverse, 0.0)
                dlog = jnp.where(start, 0.0, adjoint * previous * decay - pull)
                dig = adjoint * scale * lru
                weighted = dlog * rate
                decay_sum = decay_sum + weighted
                drates.append(weighted * soft * (1.0 - rate))
                dinputs.append(dig * igate * (1.0 - igate))
                dconv_ref[row, at, :] = gated * scale
            drate = jnp.concatenate(drates, axis=0).astype(jnp.bfloat16)
            dinput = jnp.concatenate(dinputs, axis=0).astype(jnp.bfloat16)
            both_ref[row, pl.ds(base, STEP), :width] = drate
            both_ref[row, pl.ds(base, STEP), width:] = dinput
            drate = drate.astype(jnp.float32)
            dinput = dinput.astype(jnp.float32)
            rate_sum = rate_sum + (drate[:SUBLANES] + drate[SUBLANES:])
            input_sum = input_sum + (dinput[:SUBLANES] + dinput[SUBLANES:])
            later.append(before)
        return ((decay_sum, rate_sum, input_sum), tuple(later))

    sums, _ = lax.fori_loop(
        0,
        length // STEP,
        gate_step,
        ((zeros, zeros, zeros), tuple(in_ref[row] for row in range(rows))),
    )
    for slot, total in zip((5, 6, 7), (sums[1], sums[2], sums[0])):
        sums_ref[slot : slot + 1, :] = jnp.sum(total, axis=0, keepdims=True)

    piece = min(length, 256)
    wide = None
    for row in range(rows):

        def dot_step(index, carry, row=row):
            at = pl.ds(pl.multiple_of(index * piece, piece), piece)
            dconv_ref[row, at, :] += lax.dot_general(
                both_ref[row, at, :],
                gates_ref[...],
                (((1,), (1,)), ((), ())),
                preferred_element_type=jnp.float32,
            )
            return carry

        lax.fori_loop(0, length // piece, dot_step, 0)
        part = lax.dot_general(
            lru_ref[row], both_ref[row], (((0,), (0,)), ((), ())), preferred_element_type=jnp.float32
        )
        wide = part if wide is None else wide + part
    row_head = lax.broadcasted_iota(jnp.int32, (width, width), 0) // head_size
    col_head = lax.broadcasted_iota(jnp.int32, (width, width), 1) // head_size
    own = row_head == col_head
    for part in range(2):
        kept = jnp.where(own, wide[:, part * width : (part + 1) * width], 0.0)
        folded = kept
        for other in range(1, width // head_size):
            folded = folded + pltpu.roll(kept, width - other * head_size, 1)
        dgates_ref[:, part * LANES : (part + 1) * LANES] = folded[:, :LANES]

    def conv_step(index, carry):
        sums, following = carry
        sums = list(sums)
        base = pl.multiple_of((length // STEP - 1 - index) * STEP, STEP)
        later = []
        for row in range(rows):
            after = following[row]
            pieces = []
            for half in reversed(range(STEP // SUBLANES)):
                at = pl.ds(base + half * SUBLANES, SUBLANES)
                dist = across(dist_ref[row, at, :], width)
                branch = branch_ref[row, at, :]
                here = dconv_ref[row, at, :]
                total = taps[0] * here
                sums[0] = sums[0] + here * branch
                sums[4] = sums[4] + here
                masked = tuple(jnp.where(dist >= k, here, 0.0) for k in range(1, 4))
                for k in range(1, 4):
                    moved = pltpu.roll(
                        jnp.where(place >= k, masked[k - 1], after[k - 1]), SUBLANES - k, 0
                    )
                    total = total + taps[k] * moved
                    sums[k] = sums[k] + branch * moved
                after = masked
                pieces.append(total)
            whole = jnp.concatenate(pieces[::-1], axis=0)
            dbranch_ref[row, pl.ds(base, STEP), :] = whole.astype(jnp.bfloat16)
            later.append(after)

            @pl.when(index == 0)
            def _(row=row, whole=whole):
                tail_ref[row] = whole[STEP - SUBLANES :]

        return (tuple(sums), tuple(later))

    sums, firsts = lax.fori_loop(
        0,
        length // STEP,
        conv_step,
        ((zeros,) * 5, tuple((zeros,) * 3 for _ in range(rows))),
    )
    sums = list(sums)
    for row in range(rows):
        total = zeros
        rim = rim_ref[row]
        for k in range(1, 4):
            moved = pltpu.roll(jnp.where(place >= k, 0.0, firsts[row][k - 1]), SUBLANES - k, 0)
            total = total + taps[k] * moved
            sums[k] = sums[k] + rim * moved
        head_ref[row] = total
    for slot in range(5):
        sums_ref[slot : slot + 1, :] = jnp.sum(sums[slot], axis=0, keepdims=True)


def channel_call(kernel, name, arrays, specs, outs, out_specs, scratch, blocks, flops):
    moved = sum(math.prod(a.shape) * a.dtype.itemsize for a in (*arrays, *outs))
    return pl.pallas_call(
        kernel,
        name=name,
        grid=(blocks,),
        in_specs=specs,
        out_specs=out_specs,
        out_shape=outs,
        scratch_shapes=scratch,
        compiler_params=pltpu.CompilerParams(vmem_limit_bytes=VMEM_BYTES),
        cost_estimate=pl.CostEstimate(flops=flops, bytes_accessed=moved, transcendentals=0),
    )(*arrays)


class Recurrence:
    def __init__(self, rows, length, channels, head_size):
        self.rows, self.length, self.channels = (rows, length, channels)
        self.head_size = head_size
        self.width = head_size * LANES // math.gcd(head_size, LANES)
        self.blocks = channels // self.width
        self.flops = 2 * rows * length * channels * 2 * self.width

    def tall(self):
        return pl.BlockSpec((self.rows, self.length, self.width), lambda j: (0, 0, j))

    def short(self, size):
        return pl.BlockSpec((self.rows, size, self.width), lambda j: (0, 0, j))

    def flat(self, size):
        return pl.BlockSpec((size, self.width), lambda j: (0, j))

    def dist(self):
        return pl.BlockSpec((self.rows, self.length, LANES), lambda j: (0, 0, 0))

    def gates(self, columns):
        return pl.BlockSpec((self.width, columns), lambda j: (j, 0))

    def shape(self, size, dtype):
        return jax.ShapeDtypeStruct((self.rows, size, self.channels), dtype)

    def widen(self, lru_gates):
        size, width = (self.head_size, self.width)
        heads = width // size
        column = jnp.arange(2 * width)
        source = (column // width) * size + column % size
        spread = (jnp.arange(2 * size)[:, None] == source[None, :]).astype(jnp.bfloat16)
        owner = (column % width) // size
        mine = (jnp.arange(self.channels) // size) % heads
        wide = jnp.dot(lru_gates, spread, preferred_element_type=jnp.float32)
        return jnp.where(mine[:, None] == owner[None, :], wide, 0.0).astype(jnp.bfloat16)

    def forward(self, branch, rim, dist, params, gates):
        f32 = jnp.float32
        outs = [self.shape(self.length, d) for d in (jnp.bfloat16, f32, f32, f32, f32)]
        return channel_call(
            forward_kernel,
            "recurrence_forward",
            (branch, rim, dist, params, gates),
            [self.tall(), self.short(SUBLANES), self.dist(), self.flat(16), self.gates(2 * self.width)],
            outs,
            [self.tall()] * 5,
            [pltpu.VMEM((self.rows, self.length, 2 * self.width), f32)],
            self.blocks,
            self.flops,
        )

    def adjoint(self, dmix, pre, state, cum, entering, rate, dist, params):
        f32 = jnp.float32
        outs = [self.shape(self.length, d) for d in (jnp.bfloat16, f32, f32)] + [self.shape(1, f32)]
        tall = self.tall()
        return channel_call(
            adjoint_kernel,
            "recurrence_adjoint",
            (dmix, pre, state, cum, entering, rate, dist, params),
            [tall, tall, tall, tall, self.short(1), tall, self.dist(), self.flat(16)],
            outs,
            [tall, tall, tall, self.short(1)],
            [],
            self.blocks,
            0,
        )

    def backward(
        self, local, back, leaving, state, cum, entering, rate, igate, lru, dist, branch, rim, params, gates
    ):
        f32 = jnp.float32
        outs = [
            self.shape(self.length, jnp.bfloat16),
            self.shape(SUBLANES, f32),
            self.shape(SUBLANES, f32),
            jax.ShapeDtypeStruct((SUBLANES, self.channels), f32),
            jax.ShapeDtypeStruct((self.channels, 2 * LANES), f32),
        ]
        tall, one = (self.tall(), self.short(1))
        return channel_call(
            functools.partial(backward_kernel, self.head_size),
            "recurrence_backward",
            (local, back, leaving, state, cum, entering, rate, igate, lru, dist, branch, rim, params, gates),
            [tall, tall, one, tall, tall, one, tall, tall, tall, self.dist(), tall]
            + [self.short(SUBLANES), self.flat(16), self.gates(2 * self.width)],
            outs,
            [tall, self.short(SUBLANES), self.short(SUBLANES), self.flat(SUBLANES), self.gates(2 * LANES)],
            [
                pltpu.VMEM((self.rows, self.length, 2 * self.width), jnp.bfloat16),
                pltpu.VMEM((self.rows, self.length, self.width), f32),
            ],
            self.blocks,
            2 * self.flops,
        )


MESH = pl.DeviceIdType.MESH


class Corners:
    def __init__(self, seq, zed):
        self.seq_bits, self.zed_bits = (seq.bit_length() - 1, zed.bit_length() - 1)
        self.count = self.seq_bits + self.zed_bits
        self.dims = (2,) * self.count
        self.low = tuple(range(self.seq_bits))[::-1] + tuple(range(self.seq_bits, self.count))[::-1]
        self.high = tuple(range(self.seq_bits)) + tuple(range(self.seq_bits, self.count))[::-1]

    def place(self, dim):
        if dim < self.seq_bits:
            return ("seq", 2 ** (self.seq_bits - 1 - dim))
        return ("zed", 2 ** (self.count - 1 - dim))

    def bit(self, dim):
        axis, weight = self.place(dim)
        return lax.rem(lax.div(lax.axis_index(axis), weight), 2)

    def partner(self, dim):
        axis, weight = self.place(dim)
        return {axis: lax.axis_index(axis) + weight * (1 - 2 * self.bit(dim))}


def reduce_kernel(corners, orders, *refs):
    streams = len(orders)
    stages = corners.count + 1
    given, outs, rest = (refs[:streams], refs[streams : 2 * streams], refs[2 * streams :])
    owns, rest = (rest[:streams], rest[streams:])
    slots, (send_sem, recv_sem, load_sem) = (rest[:-3], rest[-3:])
    core = lax.axis_index("core")
    partners = [{"core": 1 - core}] + [corners.partner(dim) for dim in range(corners.count)]
    barrier = pltpu.get_barrier_semaphore()
    for partner in partners:
        pl.semaphore_signal(barrier, inc=1, device_id=partner, device_id_type=MESH)
    pl.semaphore_wait(barrier, len(partners))

    def indices(order, stage, last):
        fixed = {dim: corners.bit(dim) for dim in order[: stage - 1]}
        if last is not None:
            fixed[order[stage - 1]] = last
        return tuple(fixed.get(dim, slice(None)) for dim in range(corners.count))

    def copy(stream, stage):
        order = orders[stream]
        if stage == 0:
            source = given[stream].at[(slice(None),) * corners.count + (1 - core,)]
            target = {"core": 1 - core}
        else:
            dim = order[stage - 1]
            source = owns[stream].at[indices(order, stage, 1 - corners.bit(dim))]
            target = corners.partner(dim)
        return pltpu.make_async_remote_copy(
            src_ref=source,
            dst_ref=slots[stream * stages + stage],
            send_sem=send_sem.at[stream, stage],
            recv_sem=recv_sem.at[stream, stage],
            device_id=target,
            device_id_type=MESH,
        )

    def load(stream):
        return pltpu.make_async_copy(
            given[stream].at[(slice(None),) * corners.count + (core,)],
            owns[stream],
            load_sem.at[stream],
        )

    for stream in range(streams):
        copy(stream, 0).start()
        load(stream).start()
    for stage in range(stages):
        for stream in range(streams):
            order = orders[stream]
            own, slot = (owns[stream], slots[stream * stages + stage])
            if stage == 0:
                load(stream).wait()
            copy(stream, stage).wait_recv()
            left = [dim for dim in range(corners.count) if dim not in order[:stage]]
            fixed = {dim: corners.bit(dim) for dim in order[:stage]}
            if left:

                def add(index, carry, own=own, slot=slot, left=left, fixed=fixed):
                    part = {
                        dim: lax.rem(lax.div(index, 2 ** (len(left) - 1 - place)), 2)
                        for place, dim in enumerate(left)
                    }
                    mine = tuple({**fixed, **part}[dim] for dim in range(corners.count))
                    come = tuple(part[dim] for dim in left)
                    total = own[mine].astype(jnp.float32) + slot[come].astype(jnp.float32)
                    own[mine] = total.astype(own.dtype)
                    return carry

                lax.fori_loop(0, 2 ** len(left), add, 0)
                copy(stream, stage + 1).start()
            else:
                mine = tuple(fixed[dim] for dim in range(corners.count))
                outs[stream][...] = own[mine].astype(jnp.float32) + slot[...].astype(jnp.float32)
    for stage in range(stages):
        for stream in range(streams):
            copy(stream, stage).wait_send()


def reduce_streams(gradients, highs):
    corners = Corners(lax.axis_size("seq"), lax.axis_size("zed"))
    devices = 2 ** (corners.count + 1)
    orders = [corners.high if high else corners.low for high in highs]
    blocks = [
        g.reshape(corners.dims + (2, g.shape[0] // devices, g.shape[1])) for g in gradients
    ]
    outs = [jax.ShapeDtypeStruct(b.shape[-2:], jnp.float32) for b in blocks]
    owns = [pltpu.VMEM(corners.dims + b.shape[-2:], b.dtype) for b in blocks]
    slots = [
        pltpu.VMEM((2,) * min(corners.count, corners.count - stage) + b.shape[-2:], b.dtype)
        for b in blocks
        for stage in range(corners.count + 1)
    ]
    grid = (len(blocks), corners.count + 1)
    moved = sum(math.prod(g.shape) * g.dtype.itemsize for g in gradients)
    return pl.pallas_call(
        functools.partial(reduce_kernel, corners, orders),
        name="reduce_streams",
        in_specs=[pl.BlockSpec(memory_space=pl.ANY)] * len(blocks),
        out_specs=[pl.BlockSpec(memory_space=pltpu.VMEM)] * len(blocks),
        out_shape=outs,
        scratch_shapes=owns
        + slots
        + [
            pltpu.SemaphoreType.DMA(grid),
            pltpu.SemaphoreType.DMA(grid),
            pltpu.SemaphoreType.DMA((len(blocks),)),
        ],
        compiler_params=pltpu.CompilerParams(
            collective_id=1, has_side_effects=True, vmem_limit_bytes=VMEM_BYTES
        ),
        cost_estimate=pl.CostEstimate(flops=0, bytes_accessed=20 * moved, transcendentals=0),
    )(*blocks)


def grads_kernel(
    normed_ref,
    dgate_ref,
    dup_ref,
    hidden_ref,
    gout_ref,
    mixed_ref,
    dres_ref,
    out_ref,
    turned_ref,
    made_wide,
    made_down,
    made_out,
    come_wide,
    come_down,
    come_out,
    send_sem,
    recv_sem,
    store_sem,
):
    step = pl.program_id(0)
    core = lax.axis_index("core")
    other = {"core": 1 - core}
    wide_rows, down_rows, out_rows = (made_wide.shape[3], made_down.shape[3], made_out.shape[3])
    wides, downs, lasts = (come_wide.shape[0], come_down.shape[0], come_out.shape[0])
    total = wides + downs + lasts
    down_at, out_at = (wides * wide_rows, wides * wide_rows + down_rows)

    def exchange(made, come, index, slot):
        return pltpu.make_async_remote_copy(
            src_ref=made.at[lax.rem(index, 2), 1 - core],
            dst_ref=come.at[index],
            send_sem=send_sem.at[slot],
            recv_sem=recv_sem.at[slot],
            device_id=other,
            device_id_type=MESH,
        )

    def store_wide(index):
        return pltpu.make_async_copy(
            come_wide.at[index],
            out_ref.at[:, pl.ds(pl.multiple_of(index * wide_rows, wide_rows), wide_rows)],
            store_sem.at[index],
        )

    def store_down(index):
        chips = come_down.shape[1]
        return pltpu.make_async_copy(
            come_down.at[index],
            out_ref.at[pl.ds(index * chips, chips), pl.ds(down_at, down_rows)],
            store_sem.at[index + wides],
        )

    def store_out(index):
        chips = come_out.shape[1]
        return pltpu.make_async_copy(
            come_out.at[index],
            out_ref.at[pl.ds(index * chips, chips), pl.ds(out_at, out_rows)],
            store_sem.at[index + wides + downs],
        )

    @pl.when(step == 0)
    def _():
        barrier = pltpu.get_barrier_semaphore()
        pl.semaphore_signal(barrier, inc=1, device_id=other, device_id_type=MESH)
        pl.semaphore_wait(barrier, 1)
        turned_ref[...] = normed_ref[...].T

    def product_wide(source, index):
        made = made_wide.at[lax.rem(index, 2)]
        chips, rows = (made.shape[1], made.shape[2])
        tile = 256

        def column(place, carry):
            at = pl.ds(pl.multiple_of(place * tile, tile), tile)
            part = jnp.dot(turned_ref[...], source[:, at], preferred_element_type=jnp.float32)
            part = part.astype(jnp.bfloat16).reshape(chips, 2, rows, tile)
            made[0, :, :, at] = part[:, 0]
            made[1, :, :, at] = part[:, 1]
            return carry

        lax.fori_loop(0, source.shape[1] // tile, column, 0)

    def product_tall(left, right, made_all, index):
        made = made_all.at[lax.rem(index, 2)]
        chips, rows = (made.shape[1], made.shape[2])
        tile = 256

        def column(place, carry):
            at = pl.ds(pl.multiple_of(place * tile, tile), tile)
            part = lax.dot_general(
                left[...], right[:, at], (((0,), (0,)), ((), ())), preferred_element_type=jnp.float32
            )
            part = part.astype(jnp.bfloat16).reshape(chips, 2, rows, tile)
            made[0, :, :, at] = part[:, 0]
            made[1, :, :, at] = part[:, 1]
            return carry

        lax.fori_loop(0, right.shape[1] // tile, column, 0)

    half = wides // 2

    @pl.when(step < half)
    def _():
        product_wide(dgate_ref, step)

    @pl.when((step >= half) & (step < wides))
    def _():
        product_wide(dup_ref, step)

    @pl.when(step < wides)
    def _():
        exchange(made_wide, come_wide, step, step).start()

    @pl.when((step >= wides) & (step < wides + downs))
    def _():
        product_tall(hidden_ref, gout_ref, made_down, step - wides)
        exchange(made_down, come_down, step - wides, step).start()

    @pl.when((step >= wides + downs) & (step < total))
    def _():
        product_tall(mixed_ref, dres_ref, made_out, step - wides - downs)
        exchange(made_out, come_out, step - wides - downs, step).start()

    def finish(made, come, index, slot, store):
        exchange(made, come, index, slot).wait()
        mine = made.at[lax.rem(index, 2), core]
        arrived = come.at[index]

        def add(chip, carry):
            both = mine[chip].astype(jnp.float32) + arrived[chip].astype(jnp.float32)
            arrived[chip] = both.astype(jnp.bfloat16)
            return carry

        lax.fori_loop(0, come.shape[1], add, 0)
        store(index).start()

    before = step - 1

    @pl.when((before >= 0) & (before < wides))
    def _():
        finish(made_wide, come_wide, before, before, store_wide)

    @pl.when((before >= wides) & (before < wides + downs))
    def _():
        finish(made_down, come_down, before - wides, before, store_down)

    @pl.when(before >= wides + downs)
    def _():
        finish(made_out, come_out, before - wides - downs, before, store_out)

    @pl.when(step == total)
    def _():
        for index in range(wides):
            store_wide(index).wait()
        for index in range(downs):
            store_down(index).wait()
        for index in range(lasts):
            store_out(index).wait()


def block_gradients(normed, dgate, dup, hidden, gout, mixed, dres):
    tokens, model = normed.shape
    ffn, rec = (hidden.shape[1], mixed.shape[1])
    chips = lax.axis_size("seq") * lax.axis_size("zed")
    devices = 2 * chips
    wide_rows, down_rows, out_rows = (model // devices, ffn // devices, rec // devices)
    chunk = 768
    wides, downs, lasts = (2 * ffn // model, ffn // chunk, rec // chunk)
    half = wides // 2
    down_chips, out_chips = (chunk // (2 * down_rows), chunk // (2 * out_rows))
    rows = wides * wide_rows + down_rows + out_rows
    low = jnp.bfloat16

    def whole(array):
        return pl.BlockSpec(array.shape, lambda s: (0, 0), pipeline_mode=pl.Buffered(1))

    def part(columns, first, count):
        return pl.BlockSpec((tokens, columns), lambda s: (0, jnp.clip(s - first, 0, count - 1)))

    total = wides + downs + lasts
    flops = 2 * tokens * model * (3 * ffn + rec)
    arrays = (normed, dgate, dup, hidden, gout, mixed, dres)
    moved = sum(math.prod(a.shape) * 2 for a in arrays) + chips * rows * model * 2
    return pl.pallas_call(
        grads_kernel,
        name="block_gradients",
        grid=(total + 1,),
        in_specs=[
            whole(normed),
            part(model, 0, half),
            part(model, half, half),
            part(chunk, wides, downs),
            whole(gout),
            part(chunk, wides + downs, lasts),
            whole(dres),
        ],
        out_specs=pl.BlockSpec(memory_space=pl.ANY),
        out_shape=jax.ShapeDtypeStruct((chips, rows, model), low),
        scratch_shapes=[
            pltpu.VMEM((model, tokens), low),
            pltpu.VMEM((2, 2, chips, wide_rows, model), low),
            pltpu.VMEM((2, 2, down_chips, down_rows, model), low),
            pltpu.VMEM((2, 2, out_chips, out_rows, model), low),
            pltpu.VMEM((wides, chips, wide_rows, model), low),
            pltpu.VMEM((downs, down_chips, down_rows, model), low),
            pltpu.VMEM((lasts, out_chips, out_rows, model), low),
            pltpu.SemaphoreType.DMA((total,)),
            pltpu.SemaphoreType.DMA((total,)),
            pltpu.SemaphoreType.DMA((total,)),
        ],
        compiler_params=pltpu.CompilerParams(
            collective_id=2, has_side_effects=True, vmem_limit_bytes=VMEM_BYTES
        ),
        cost_estimate=pl.CostEstimate(flops=flops, bytes_accessed=moved, transcendentals=0),
    )(*arrays)


def carried(factor, value, axis, backward):
    count, mine = (lax.axis_size(axis), lax.axis_index(axis))
    pieces = lax.all_gather(jnp.stack([factor, value]), axis)
    order = range(count - 1, 0, -1) if backward else range(count - 1)
    total = jnp.zeros_like(value)
    for place in order:
        longer = pieces[place, 0] * total + pieces[place, 1]
        total = jnp.where(place > mine if backward else place < mine, longer, total)
    return total


def passed_along(value, axis, steps):
    count = lax.axis_size(axis)
    leading, last = (max(0, -steps), min(count, count - steps))
    return lax.ppermute(value, axis, [(source, source + steps) for source in range(leading, last)])


def weight_grad(left, right):
    return lax.dot_general(
        left, right, (((0,), (0,)), ((), ())), preferred_element_type=jnp.float32
    ).astype(jnp.bfloat16)


def back_dot(left, right):
    return lax.dot_general(
        left, right, (((1,), (1,)), ((), ())), preferred_element_type=jnp.float32
    )


def fwd_dot(left, right):
    return jnp.dot(left, right, preferred_element_type=jnp.float32)


def gelu_fn(value):
    return jax.nn.gelu(value, approximate=True)


def norm_back(grad_norm, normed, inverse, gain):
    scaled = grad_norm * gain
    mean_term = jnp.mean(scaled * normed, axis=1, keepdims=True)
    return inverse * (scaled - normed * mean_term)


def scattered(gradient):
    return lax.psum_scatter(
        gradient, ("seq", "zed", "core"), scatter_dimension=0, tiled=True
    ).astype(jnp.float32)


def body(
    tokens,
    cotangent,
    doc_starts,
    lengths,
    norm1_gain,
    recur_input,
    recur_gate,
    conv_kernel,
    conv_bias,
    lru_gates,
    lru_bias,
    lru_decay,
    recur_out,
    norm2_gain,
    mlp_gate,
    mlp_up,
    mlp_down,
):
    seq_x, seq_g = (
        lax.all_to_all(tokens, ("zed", "core"), split_axis=0, concat_axis=2, tiled=True),
        lax.all_to_all(cotangent, ("zed", "core"), split_axis=0, concat_axis=2, tiled=True),
    )
    row_count, block_len, model_dim = seq_x.shape
    tok_count = row_count * block_len
    rec_width = recur_input.shape[1]
    ffn_width = mlp_gate.shape[1]
    head_count = H
    head_size = rec_width // head_count
    tap_count = conv_kernel.shape[0]
    rim_size = tap_count - 1
    seq_index = lax.axis_index("seq")
    position = seq_index * block_len + jnp.arange(block_len, dtype=jnp.int32)
    bounds = jnp.concatenate([doc_starts, lengths[:, None]], axis=1)
    is_before = bounds[:, None, :] <= position[None, :, None]
    seg_start = jnp.max(jnp.where(is_before, bounds[:, None, :], 0), axis=2)
    is_valid = (position[None, :] < lengths[:, None]).reshape(tok_count, 1)
    flat_x = seq_x.reshape(tok_count, model_dim).astype(jnp.float32)
    inv_one = lax.rsqrt(jnp.mean(flat_x * flat_x, axis=1, keepdims=True) + EPS)
    normed_one = flat_x * inv_one
    normed_low = (normed_one * norm1_gain).astype(jnp.bfloat16)
    branch_pre = fwd_dot(normed_low, recur_input)
    gate_pre = fwd_dot(normed_low, recur_gate)
    gate_act = gelu_fn(gate_pre)
    branch_rows = branch_pre.reshape(row_count, block_len, rec_width)
    core = Recurrence(row_count, block_len, rec_width, head_size)
    prev_rim = passed_along(
        branch_rows[:, block_len - rim_size :, :].astype(jnp.bfloat16), "seq", 1
    ).astype(jnp.float32)
    rim = jnp.pad(prev_rim, ((0, 0), (SUBLANES - rim_size, 0), (0, 0)))
    dist = jnp.broadcast_to(
        (position[None, :] - seg_start)[:, :, None], (row_count, block_len, LANES)
    )
    soft_decay = jax.nn.softplus(-lru_decay)
    params = jnp.concatenate(
        [
            conv_kernel,
            conv_bias[None],
            lru_bias,
            (-8.0 * soft_decay)[None],
            jnp.zeros((SUBLANES, rec_width), jnp.float32),
        ],
        axis=0,
    )
    wide_gates = core.widen(lru_gates)
    lru_in, rate_gate, input_gate, local_state, cum_coef = core.forward(
        branch_rows, rim, dist, params, wide_gates
    )
    carry_in = carried(cum_coef[:, -1, :], local_state[:, -1, :], "seq", False)
    entering = carry_in[:, None, :]
    state_rows = local_state + cum_coef * entering
    state_flat = state_rows.reshape(tok_count, rec_width)
    mixed_low = (state_flat * gate_act).astype(jnp.bfloat16)
    resid_one = flat_x + fwd_dot(mixed_low, recur_out)
    inv_two = lax.rsqrt(jnp.mean(resid_one * resid_one, axis=1, keepdims=True) + EPS)
    normed_two = resid_one * inv_two
    normed_low2 = (normed_two * norm2_gain).astype(jnp.bfloat16)
    mlp_gate_pre = fwd_dot(normed_low2, mlp_gate)
    mlp_up_pre = fwd_dot(normed_low2, mlp_up)
    gelu_gate = gelu_fn(mlp_gate_pre)
    hidden_low = (gelu_gate * mlp_up_pre).astype(jnp.bfloat16)
    result = (resid_one + fwd_dot(hidden_low, mlp_down)).astype(jnp.bfloat16)
    output = lax.all_to_all(
        result.reshape(row_count, block_len, model_dim),
        ("zed", "core"),
        split_axis=2,
        concat_axis=0,
        tiled=True,
    )
    grad_out = jnp.where(is_valid, seq_g.reshape(tok_count, model_dim).astype(jnp.float32), 0.0)
    grad_low = grad_out.astype(jnp.bfloat16)
    grad_hidden = back_dot(grad_low, mlp_down)
    _, gelu_pull = jax.vjp(gelu_fn, mlp_gate_pre)
    mgate_low = gelu_pull(grad_hidden * mlp_up_pre)[0].astype(jnp.bfloat16)
    mup_low = (grad_hidden * gelu_gate).astype(jnp.bfloat16)
    grad_norm2 = back_dot(mgate_low, mlp_gate) + back_dot(mup_low, mlp_up)
    resid_part = norm_back(grad_norm2, normed_two, inv_two, norm2_gain)
    grad_resid = grad_out + resid_part
    resid_low = grad_resid.astype(jnp.bfloat16)
    devices = lax.axis_size(("seq", "zed", "core"))
    own_rows = model_dim // devices
    tiled = own_rows % (2 * SUBLANES) == 0 and ffn_width % model_dim == 0
    if tiled:
        merged = block_gradients(
            normed_low2, mgate_low, mup_low, hidden_low, grad_low, mixed_low, resid_low
        )
        merged, resid_low = lax.optimization_barrier((merged, resid_low))
        merged = lax.psum_scatter(merged, "seq", scatter_dimension=0, tiled=True)
    grad_mixed = back_dot(resid_low, recur_out)
    gate_low, back_local, back_cum, first_term = core.adjoint(
        grad_mixed.reshape(row_count, block_len, rec_width),
        gate_pre.reshape(row_count, block_len, rec_width),
        local_state,
        cum_coef,
        entering,
        rate_gate,
        dist,
        params,
    )
    gate_low = gate_low.reshape(tok_count, rec_width)
    carry_out = carried(cum_coef[:, -1, :], first_term[:, 0, :], "seq", True)
    branch_local, tail, lead, channel_sums, gate_sums = core.backward(
        back_local,
        back_cum,
        carry_out[:, None, :],
        local_state,
        cum_coef,
        entering,
        rate_gate,
        input_gate,
        lru_in,
        dist,
        branch_rows,
        rim,
        params,
        wide_gates,
    )
    spare = jnp.swapaxes(channel_sums, 0, 1)
    small = jnp.concatenate(
        [gate_sums[:, :head_size], spare, gate_sums[:, head_size + SUBLANES :]], axis=1
    )
    from_next = passed_along(
        lead[:, SUBLANES - rim_size :, :].astype(jnp.bfloat16), "seq", -1
    )
    ending = tail + jnp.pad(from_next.astype(jnp.float32), ((0, 0), (SUBLANES - rim_size, 0), (0, 0)))
    branch_low = lax.dynamic_update_slice(
        branch_local, ending.astype(jnp.bfloat16), (0, block_len - SUBLANES, 0)
    ).reshape(tok_count, rec_width)
    grad_rin = weight_grad(normed_low, branch_low)
    grad_rgate = weight_grad(normed_low, gate_low)
    grad_norm1 = back_dot(branch_low, recur_input) + back_dot(gate_low, recur_gate)
    input_part = norm_back(grad_norm1, normed_one, inv_one, norm1_gain)
    grad_x = (grad_resid + input_part).astype(jnp.bfloat16).reshape(row_count, block_len, model_dim)
    if tiled:
        merged, grad_x = lax.optimization_barrier((merged, grad_x))
        merged = lax.psum_scatter(merged, "zed", scatter_dimension=0, tiled=True)
    grad_tokens = lax.all_to_all(grad_x, ("zed", "core"), split_axis=2, concat_axis=0, tiled=True)
    if tiled:
        sum_rgate, sum_rin, own_small = reduce_streams(
            (grad_rgate, grad_rin, small.astype(jnp.bfloat16)), (False, True, False)
        )
        own = merged[0].astype(jnp.float32)
        count = ffn_width // model_dim * own_rows

        def unfolded(part):
            return jnp.swapaxes(part.reshape(-1, own_rows, model_dim), 0, 1).reshape(own_rows, -1)

        sum_mgate, sum_mup = (unfolded(own[:count]), unfolded(own[count : 2 * count]))
        sum_down = own[2 * count : 2 * count + ffn_width // devices]
        sum_rout = own[2 * count + ffn_width // devices :]
    else:
        sum_mgate, sum_mup, sum_down, sum_rout, sum_rgate, sum_rin = (
            scattered(weight_grad(left, right))
            for left, right in (
                (normed_low2, mgate_low),
                (normed_low2, mup_low),
                (hidden_low, grad_low),
                (mixed_low, resid_low),
                (normed_low, gate_low),
                (normed_low, branch_low),
            )
        )
        own_small = scattered(small)
    sum_lgates = jnp.concatenate(
        [own_small[:, :head_size], own_small[:, LANES : LANES + head_size]], axis=1
    )
    own_sums = jnp.swapaxes(own_small[:, head_size : head_size + SUBLANES], 0, 1)
    device = lax.axis_index(("seq", "zed", "core"))

    def mine(array, size, axis=0):
        return lax.dynamic_slice_in_dim(array, device * size, size, axis)

    def weighed(weight, gradient):
        return jnp.sum(mine(weight, own_rows).astype(jnp.float32) * gradient, axis=1)

    sum_gain1 = (weighed(recur_input, sum_rin) + weighed(recur_gate, sum_rgate)) / mine(
        norm1_gain, own_rows
    )
    sum_gain2 = (weighed(mlp_gate, sum_mgate) + weighed(mlp_up, sum_mup)) / mine(
        norm2_gain, own_rows
    )
    own_channels = own_sums.shape[1]
    sum_decay = 8.0 * jax.nn.sigmoid(-mine(lru_decay, own_channels)) * own_sums[7]
    return (
        output,
        grad_tokens,
        sum_gain1,
        sum_rin,
        sum_rgate,
        own_sums[:4],
        own_sums[4],
        sum_lgates,
        own_sums[5:7],
        sum_decay,
        sum_rout,
        sum_gain2,
        sum_mgate,
        sum_mup,
        sum_down,
    )


def solution(mesh):
    seq, chan = (mesh.shape["seq"], mesh.shape["chan"])
    chips = jax.sharding.Mesh(mesh.devices.reshape(seq, chan // 2, 2), ("seq", "zed", "core"))
    chan = ("zed", "core")
    every = ("seq", "zed", "core")
    activations = P(None, "seq", chan)
    rows, columns, vector = (P(every, None), P(None, every), P(every))
    return jax.shard_map(
        body,
        mesh=chips,
        in_specs=(activations, activations, P(chan, None), P(chan)) + (P(),) * 13,
        out_specs=(
            activations,
            activations,
            vector,
            rows,
            rows,
            columns,
            vector,
            rows,
            columns,
            vector,
            rows,
            vector,
            rows,
            rows,
            rows,
        ),
        check_vma=False,
    )
```

```python
import functools
import math

import jax
import jax.numpy as jnp
from jax import lax
from jax.experimental import pallas as pl
from jax.experimental.pallas import tpu as pltpu
from jax.sharding import PartitionSpec as P

H = 16


EPS = 1e-06
ROOT_FLOOR = 1e-06
LANES = 128
SUBLANES = 8
STEP = 16
VMEM_BYTES = 56 * 1024 * 1024


def sigmoid(value):
    return 0.5 * jnp.tanh(0.5 * value) + 0.5


GELU_C = 0.7978845608
GELU_A = 0.044715


def gelu_pair(value):
    square = value * value
    inner = jnp.tanh(value * (GELU_C + (GELU_C * GELU_A) * square))
    half = 0.5 + 0.5 * inner
    slope = GELU_C + (3.0 * GELU_C * GELU_A) * square
    return (value * half, half + 0.5 * value * (1.0 - inner * inner) * slope)


def root_argument(log_decay, decay):
    y = 2.0 * log_decay
    series = 1.0 + y * (1.0 / 7.0)
    for divisor in (6.0, 5.0, 4.0, 3.0, 2.0):
        series = 1.0 + (y * (1.0 / divisor)) * series
    return jnp.where(y > -0.25, -y * series, 1.0 - decay * decay)


def across(column, width):
    return jnp.concatenate([column] * (width // LANES), axis=1)


def forward_kernel(
    branch_ref,
    rim_ref,
    dist_ref,
    par_ref,
    gates_ref,
    lru_ref,
    rate_ref,
    igate_ref,
    state_ref,
    cum_ref,
    both_ref,
):
    rows, length, width = branch_ref.shape
    taps = [par_ref[k : k + 1, :] for k in range(4)]
    conv_bias, rate_bias, input_bias, soft = (par_ref[k : k + 1, :] for k in range(4, 8))
    place = lax.broadcasted_iota(jnp.int32, (SUBLANES, width), 0)

    for row in range(rows):

        def conv_step(index, before, row=row):
            base = pl.multiple_of(index * STEP, STEP)
            pieces = []
            for half in range(STEP // SUBLANES):
                at = pl.ds(base + half * SUBLANES, SUBLANES)
                here = branch_ref[row, at, :]
                dist = across(dist_ref[row, at, :], width)
                total = conv_bias + taps[0] * here
                for k in range(1, 4):
                    shifted = pltpu.roll(jnp.where(place < SUBLANES - k, here, before), k, 0)
                    total = total + taps[k] * jnp.where(dist >= k, shifted, 0.0)
                pieces.append(total)
                before = here
            lru_ref[row, pl.ds(base, STEP), :] = jnp.concatenate(pieces, axis=0).astype(jnp.bfloat16)
            return before

        lax.fori_loop(0, length // STEP, conv_step, rim_ref[row])

        piece = min(length, 256)

        def dot_step(index, carry, row=row):
            at = pl.ds(pl.multiple_of(index * piece, piece), piece)
            both_ref[row, at, :] = jnp.dot(
                lru_ref[row, at, :], gates_ref[...], preferred_element_type=jnp.float32
            )
            return carry

        lax.fori_loop(0, length // piece, dot_step, 0)

    def scan_step(index, carry):
        base = pl.multiple_of(index * STEP, STEP)
        later = []
        for row in range(rows):
            run_cum, run_state = carry[row]
            lru_both = lru_ref[row, pl.ds(base, STEP), :].astype(jnp.float32)
            for half in range(STEP // SUBLANES):
                at = pl.ds(base + half * SUBLANES, SUBLANES)
                lru = lru_both[half * SUBLANES : (half + 1) * SUBLANES]
                start = across(dist_ref[row, at, :], width) == 0
                rate = sigmoid(both_ref[row, at, :width] + rate_bias)
                igate = sigmoid(both_ref[row, at, width:] + input_bias)
                log_decay = rate * soft
                decay = jnp.exp(log_decay)
                arg = jnp.maximum(root_argument(log_decay, decay), ROOT_FLOOR)
                root = arg * lax.rsqrt(arg)
                cum = jnp.where(start, 0.0, decay)
                value = jnp.where(start, 1.0, root) * igate * lru
                rate_ref[row, at, :] = rate
                igate_ref[row, at, :] = igate
                for shift in (1, 2, 4):
                    live = place >= shift
                    value = value + cum * jnp.where(live, pltpu.roll(value, shift, 0), 0.0)
                    cum = cum * jnp.where(live, pltpu.roll(cum, shift, 0), 1.0)
                value = value + cum * run_state
                cum = cum * run_cum
                state_ref[row, at, :] = value
                cum_ref[row, at, :] = cum
                run_state = value[SUBLANES - 1 :, :]
                run_cum = cum[SUBLANES - 1 :, :]
            later.append((run_cum, run_state))
        return tuple(later)

    one, zero = (jnp.ones((1, width), jnp.float32), jnp.zeros((1, width), jnp.float32))
    lax.fori_loop(0, length // STEP, scan_step, tuple((one, zero) for _ in range(rows)))


def adjoint_kernel(
    dmix_ref,
    pre_ref,
    state_ref,
    cum_ref,
    carry_ref,
    rate_ref,
    dist_ref,
    par_ref,
    dgate_ref,
    local_ref,
    back_ref,
    first_ref,
):
    rows, length, width = dmix_ref.shape
    soft = par_ref[7:8, :]
    place = lax.broadcasted_iota(jnp.int32, (SUBLANES, width), 0)
    last = length // STEP - 1

    def step(index, carry):
        base = pl.multiple_of((last - index) * STEP, STEP)
        later = []
        for row in range(rows):
            run_cum, run_back = carry[row]
            entering = carry_ref[row]
            pieces = []
            for half in reversed(range(STEP // SUBLANES)):
                at = pl.ds(base + half * SUBLANES, SUBLANES)
                start = across(dist_ref[row, at, :], width) == 0
                state = state_ref[row, at, :] + cum_ref[row, at, :] * entering
                act, slope = gelu_pair(pre_ref[row, at, :])
                dmix = dmix_ref[row, at, :]
                pieces.append(dmix * state * slope)
                dstate = dmix * act
                coef = jnp.where(start, 0.0, jnp.exp(rate_ref[row, at, :] * soft))
                value = coef * dstate
                for shift in (1, 2, 4):
                    live = place < SUBLANES - shift
                    turn = SUBLANES - shift
                    value = value + coef * jnp.where(live, pltpu.roll(value, turn, 0), 0.0)
                    coef = coef * jnp.where(live, pltpu.roll(coef, turn, 0), 1.0)
                value = value + coef * run_back
                coef = coef * run_cum
                inside = place < SUBLANES - 1
                local_ref[row, at, :] = dstate + jnp.where(
                    inside, pltpu.roll(value, SUBLANES - 1, 0), run_back
                )
                back_ref[row, at, :] = jnp.where(inside, pltpu.roll(coef, SUBLANES - 1, 0), run_cum)
                run_back = value[:1, :]
                run_cum = coef[:1, :]
            dgate_ref[row, pl.ds(base, STEP), :] = jnp.concatenate(pieces[::-1], axis=0).astype(
                jnp.bfloat16
            )
            later.append((run_cum, run_back))
        return tuple(later)

    one, zero = (jnp.ones((1, width), jnp.float32), jnp.zeros((1, width), jnp.float32))
    done = lax.fori_loop(0, last + 1, step, tuple((one, zero) for _ in range(rows)))
    for row in range(rows):
        first_ref[row] = done[row][1]


def backward_kernel(
    head_size,
    local_ref,
    back_ref,
    out_ref,
    state_ref,
    cum_ref,
    in_ref,
    rate_ref,
    igate_ref,
    lru_ref,
    dist_ref,
    branch_ref,
    rim_ref,
    par_ref,
    gates_ref,
    dbranch_ref,
    tail_ref,
    head_ref,
    sums_ref,
    dgates_ref,
    both_ref,
    dconv_ref,
):
    rows, length, width = local_ref.shape
    taps = [par_ref[k : k + 1, :] for k in range(4)]
    soft = par_ref[7:8, :]
    place = lax.broadcasted_iota(jnp.int32, (SUBLANES, width), 0)
    zeros = jnp.zeros((SUBLANES, width), jnp.float32)

    def gate_step(index, carry):
        sums, earlier = carry
        decay_sum, rate_sum, input_sum = sums
        base = pl.multiple_of(index * STEP, STEP)
        later = []
        for row in range(rows):
            before = earlier[row]
            entering = in_ref[row]
            leaving = out_ref[row]
            lru_both = lru_ref[row, pl.ds(base, STEP), :].astype(jnp.float32)
            drates, dinputs = ([], [])
            for half in range(STEP // SUBLANES):
                at = pl.ds(base + half * SUBLANES, SUBLANES)
                lru = lru_both[half * SUBLANES : (half + 1) * SUBLANES]
                start = across(dist_ref[row, at, :], width) == 0
                adjoint = local_ref[row, at, :] + back_ref[row, at, :] * leaving
                state = state_ref[row, at, :] + cum_ref[row, at, :] * entering
                previous = jnp.where(place < 1, before, pltpu.roll(state, 1, 0))
                before = state[SUBLANES - 1 :, :]
                rate = rate_ref[row, at, :]
                igate = igate_ref[row, at, :]
                log_decay = rate * soft
                decay = jnp.exp(log_decay)
                arg = root_argument(log_decay, decay)
                above = arg > ROOT_FLOOR
                arg = jnp.maximum(arg, ROOT_FLOOR)
                inverse = lax.rsqrt(arg)
                scale = jnp.where(start, 1.0, arg * inverse)
                gated = adjoint * igate
                dscale = gated * lru
                pull = jnp.where(above, dscale * decay * decay * inverse, 0.0)
                dlog = jnp.where(start, 0.0, adjoint * previous * decay - pull)
                dig = adjoint * scale * lru
                weighted = dlog * rate
                decay_sum = decay_sum + weighted
                drates.append(weighted * soft * (1.0 - rate))
                dinputs.append(dig * igate * (1.0 - igate))
                dconv_ref[row, at, :] = gated * scale
            drate = jnp.concatenate(drates, axis=0).astype(jnp.bfloat16)
            dinput = jnp.concatenate(dinputs, axis=0).astype(jnp.bfloat16)
            both_ref[row, pl.ds(base, STEP), :width] = drate
            both_ref[row, pl.ds(base, STEP), width:] = dinput
            drate = drate.astype(jnp.float32)
            dinput = dinput.astype(jnp.float32)
            rate_sum = rate_sum + (drate[:SUBLANES] + drate[SUBLANES:])
            input_sum = input_sum + (dinput[:SUBLANES] + dinput[SUBLANES:])
            later.append(before)
        return ((decay_sum, rate_sum, input_sum), tuple(later))

    sums, _ = lax.fori_loop(
        0,
        length // STEP,
        gate_step,
        ((zeros, zeros, zeros), tuple(in_ref[row] for row in range(rows))),
    )
    for slot, total in zip((5, 6, 7), (sums[1], sums[2], sums[0])):
        sums_ref[slot : slot + 1, :] = jnp.sum(total, axis=0, keepdims=True)

    piece = min(length, 256)
    wide = None
    for row in range(rows):

        def dot_step(index, carry, row=row):
            at = pl.ds(pl.multiple_of(index * piece, piece), piece)
            dconv_ref[row, at, :] += lax.dot_general(
                both_ref[row, at, :],
                gates_ref[...],
                (((1,), (1,)), ((), ())),
                preferred_element_type=jnp.float32,
            )
            return carry

        lax.fori_loop(0, length // piece, dot_step, 0)
        part = lax.dot_general(
            lru_ref[row], both_ref[row], (((0,), (0,)), ((), ())), preferred_element_type=jnp.float32
        )
        wide = part if wide is None else wide + part
    row_head = lax.broadcasted_iota(jnp.int32, (width, width), 0) // head_size
    col_head = lax.broadcasted_iota(jnp.int32, (width, width), 1) // head_size
    own = row_head == col_head
    for part in range(2):
        kept = jnp.where(own, wide[:, part * width : (part + 1) * width], 0.0)
        folded = kept
        for other in range(1, width // head_size):
            folded = folded + pltpu.roll(kept, width - other * head_size, 1)
        dgates_ref[:, part * LANES : (part + 1) * LANES] = folded[:, :LANES]

    def conv_step(index, carry):
        sums, following = carry
        sums = list(sums)
        base = pl.multiple_of((length // STEP - 1 - index) * STEP, STEP)
        later = []
        for row in range(rows):
            after = following[row]
            pieces = []
            for half in reversed(range(STEP // SUBLANES)):
                at = pl.ds(base + half * SUBLANES, SUBLANES)
                dist = across(dist_ref[row, at, :], width)
                branch = branch_ref[row, at, :]
                here = dconv_ref[row, at, :]
                total = taps[0] * here
                sums[0] = sums[0] + here * branch
                sums[4] = sums[4] + here
                masked = tuple(jnp.where(dist >= k, here, 0.0) for k in range(1, 4))
                for k in range(1, 4):
                    moved = pltpu.roll(
                        jnp.where(place >= k, masked[k - 1], after[k - 1]), SUBLANES - k, 0
                    )
                    total = total + taps[k] * moved
                    sums[k] = sums[k] + branch * moved
                after = masked
                pieces.append(total)
            whole = jnp.concatenate(pieces[::-1], axis=0)
            dbranch_ref[row, pl.ds(base, STEP), :] = whole.astype(jnp.bfloat16)
            later.append(after)

            @pl.when(index == 0)
            def _(row=row, whole=whole):
                tail_ref[row] = whole[STEP - SUBLANES :]

        return (tuple(sums), tuple(later))

    sums, firsts = lax.fori_loop(
        0,
        length // STEP,
        conv_step,
        ((zeros,) * 5, tuple((zeros,) * 3 for _ in range(rows))),
    )
    sums = list(sums)
    for row in range(rows):
        total = zeros
        rim = rim_ref[row]
        for k in range(1, 4):
            moved = pltpu.roll(jnp.where(place >= k, 0.0, firsts[row][k - 1]), SUBLANES - k, 0)
            total = total + taps[k] * moved
            sums[k] = sums[k] + rim * moved
        head_ref[row] = total
    for slot in range(5):
        sums_ref[slot : slot + 1, :] = jnp.sum(sums[slot], axis=0, keepdims=True)


def channel_call(kernel, name, arrays, specs, outs, out_specs, scratch, blocks, flops):
    moved = sum(math.prod(a.shape) * a.dtype.itemsize for a in (*arrays, *outs))
    return pl.pallas_call(
        kernel,
        name=name,
        grid=(blocks,),
        in_specs=specs,
        out_specs=out_specs,
        out_shape=outs,
        scratch_shapes=scratch,
        compiler_params=pltpu.CompilerParams(vmem_limit_bytes=VMEM_BYTES),
        cost_estimate=pl.CostEstimate(flops=flops, bytes_accessed=moved, transcendentals=0),
    )(*arrays)


class Recurrence:
    def __init__(self, rows, length, channels, head_size):
        self.rows, self.length, self.channels = (rows, length, channels)
        self.head_size = head_size
        self.width = head_size * LANES // math.gcd(head_size, LANES)
        self.blocks = channels // self.width
        self.flops = 2 * rows * length * channels * 2 * self.width

    def tall(self):
        return pl.BlockSpec((self.rows, self.length, self.width), lambda j: (0, 0, j))

    def short(self, size):
        return pl.BlockSpec((self.rows, size, self.width), lambda j: (0, 0, j))

    def flat(self, size):
        return pl.BlockSpec((size, self.width), lambda j: (0, j))

    def dist(self):
        return pl.BlockSpec((self.rows, self.length, LANES), lambda j: (0, 0, 0))

    def gates(self, columns):
        return pl.BlockSpec((self.width, columns), lambda j: (j, 0))

    def shape(self, size, dtype):
        return jax.ShapeDtypeStruct((self.rows, size, self.channels), dtype)

    def widen(self, lru_gates):
        size, width = (self.head_size, self.width)
        heads = width // size
        column = jnp.arange(2 * width)
        source = (column // width) * size + column % size
        spread = (jnp.arange(2 * size)[:, None] == source[None, :]).astype(jnp.bfloat16)
        owner = (column % width) // size
        mine = (jnp.arange(self.channels) // size) % heads
        wide = jnp.dot(lru_gates, spread, preferred_element_type=jnp.float32)
        return jnp.where(mine[:, None] == owner[None, :], wide, 0.0).astype(jnp.bfloat16)

    def forward(self, branch, rim, dist, params, gates):
        f32 = jnp.float32
        outs = [self.shape(self.length, d) for d in (jnp.bfloat16, f32, f32, f32, f32)]
        return channel_call(
            forward_kernel,
            "recurrence_forward",
            (branch, rim, dist, params, gates),
            [self.tall(), self.short(SUBLANES), self.dist(), self.flat(16), self.gates(2 * self.width)],
            outs,
            [self.tall()] * 5,
            [pltpu.VMEM((self.rows, self.length, 2 * self.width), f32)],
            self.blocks,
            self.flops,
        )

    def adjoint(self, dmix, pre, state, cum, entering, rate, dist, params):
        f32 = jnp.float32
        outs = [self.shape(self.length, d) for d in (jnp.bfloat16, f32, f32)] + [self.shape(1, f32)]
        tall = self.tall()
        return channel_call(
            adjoint_kernel,
            "recurrence_adjoint",
            (dmix, pre, state, cum, entering, rate, dist, params),
            [tall, tall, tall, tall, self.short(1), tall, self.dist(), self.flat(16)],
            outs,
            [tall, tall, tall, self.short(1)],
            [],
            self.blocks,
            0,
        )

    def backward(
        self, local, back, leaving, state, cum, entering, rate, igate, lru, dist, branch, rim, params, gates
    ):
        f32 = jnp.float32
        outs = [
            self.shape(self.length, jnp.bfloat16),
            self.shape(SUBLANES, f32),
            self.shape(SUBLANES, f32),
            jax.ShapeDtypeStruct((SUBLANES, self.channels), f32),
            jax.ShapeDtypeStruct((self.channels, 2 * LANES), f32),
        ]
        tall, one = (self.tall(), self.short(1))
        return channel_call(
            functools.partial(backward_kernel, self.head_size),
            "recurrence_backward",
            (local, back, leaving, state, cum, entering, rate, igate, lru, dist, branch, rim, params, gates),
            [tall, tall, one, tall, tall, one, tall, tall, tall, self.dist(), tall]
            + [self.short(SUBLANES), self.flat(16), self.gates(2 * self.width)],
            outs,
            [tall, self.short(SUBLANES), self.short(SUBLANES), self.flat(SUBLANES), self.gates(2 * LANES)],
            [
                pltpu.VMEM((self.rows, self.length, 2 * self.width), jnp.bfloat16),
                pltpu.VMEM((self.rows, self.length, self.width), f32),
            ],
            self.blocks,
            2 * self.flops,
        )


def gathered(parts_ref, at):
    return jnp.concatenate([parts_ref[k, at, :] for k in range(parts_ref.shape[0])], axis=1)


def front_kernel(
    parts_ref, gain_ref, input_ref, gate_ref, x_ref, inverse_ref, normed_ref, branch_ref, pre_ref
):
    tokens = x_ref.shape[0]
    piece = 64

    @pl.when(pl.program_id(0) == 0)
    def _():
        def norm(index, carry):
            at = pl.ds(pl.multiple_of(index * piece, piece), piece)
            low = gathered(parts_ref, at)
            x_ref[at, :] = low
            value = low.astype(jnp.float32)
            inverse = lax.rsqrt(jnp.mean(value * value, axis=1, keepdims=True) + EPS)
            inverse_ref[at, :] = jnp.broadcast_to(inverse, (piece, LANES))
            normed_ref[at, :] = (value * inverse * gain_ref[...]).astype(jnp.bfloat16)
            return carry

        lax.fori_loop(0, tokens // piece, norm, 0)

    def multiply(index, carry):
        at = pl.ds(pl.multiple_of(index * 256, 256), 256)
        normed = normed_ref[at, :]
        branch_ref[at, :] = jnp.dot(normed, input_ref[...], preferred_element_type=jnp.float32)
        pre_ref[at, :] = jnp.dot(normed, gate_ref[...], preferred_element_type=jnp.float32)
        return carry

    lax.fori_loop(0, tokens // 256, multiply, 0)


def front(parts, gain, recur_input, recur_gate):
    count, tokens, width = parts.shape
    model, rec = recur_input.shape
    columns = 3 * LANES
    low, f32 = (jnp.bfloat16, jnp.float32)
    tall = pl.BlockSpec((model, columns), lambda j: (0, j))
    wide = pl.BlockSpec((tokens, columns), lambda j: (0, j))

    def whole(shape):
        return pl.BlockSpec(shape, lambda j: (0,) * len(shape))

    return pl.pallas_call(
        front_kernel,
        name="norm_and_project",
        grid=(rec // columns,),
        in_specs=[whole(parts.shape), whole((1, model)), tall, tall],
        out_specs=[whole((tokens, model)), whole((tokens, LANES)), whole((tokens, model)), wide, wide],
        out_shape=[
            jax.ShapeDtypeStruct((tokens, model), low),
            jax.ShapeDtypeStruct((tokens, LANES), f32),
            jax.ShapeDtypeStruct((tokens, model), low),
            jax.ShapeDtypeStruct((tokens, rec), f32),
            jax.ShapeDtypeStruct((tokens, rec), f32),
        ],
        compiler_params=pltpu.CompilerParams(vmem_limit_bytes=VMEM_BYTES),
        cost_estimate=pl.CostEstimate(
            flops=4 * tokens * model * rec, bytes_accessed=20 * tokens * model, transcendentals=0
        ),
    )(parts, gain[None], recur_input, recur_gate)


def collect_kernel(left_ref, parts_ref, out_ref):
    rows, length = (left_ref.shape[0], out_ref.shape[0] // left_ref.shape[0])
    piece = 64
    for row in range(rows):

        def step(index, carry, row=row):
            base = pl.multiple_of(index * piece, piece)
            at = pl.ds(row * length + base, piece)
            low = gathered(parts_ref, at)
            place = base + lax.broadcasted_iota(jnp.int32, low.shape, 0)
            value = jnp.where(place < left_ref[row], low.astype(jnp.float32), 0.0)
            out_ref[at, :] = value.astype(jnp.bfloat16)
            return carry

        lax.fori_loop(0, length // piece, step, 0)


def collect(parts, left):
    count, tokens, width = parts.shape
    return pl.pallas_call(
        collect_kernel,
        name="collect_cotangent",
        in_specs=[
            pl.BlockSpec(memory_space=pltpu.SMEM),
            pl.BlockSpec(memory_space=pltpu.VMEM),
        ],
        out_specs=pl.BlockSpec(memory_space=pltpu.VMEM),
        out_shape=jax.ShapeDtypeStruct((tokens, count * width), parts.dtype),
        compiler_params=pltpu.CompilerParams(vmem_limit_bytes=VMEM_BYTES),
        cost_estimate=pl.CostEstimate(
            flops=0, bytes_accessed=4 * count * tokens * width, transcendentals=0
        ),
    )(left, parts)


def spread_kernel(whole_ref, out_ref):
    out_ref[0] = whole_ref[...]


def spread(whole, count):
    tokens, width = (whole.shape[0], whole.shape[1] // count)
    return pl.pallas_call(
        spread_kernel,
        name="spread_features",
        grid=(count,),
        in_specs=[pl.BlockSpec((tokens, width), lambda j: (0, j))],
        out_specs=pl.BlockSpec((1, tokens, width), lambda j: (j, 0, 0)),
        out_shape=jax.ShapeDtypeStruct((count, tokens, width), whole.dtype),
        cost_estimate=pl.CostEstimate(
            flops=0, bytes_accessed=4 * tokens * whole.shape[1], transcendentals=0
        ),
    )(whole)


CHAN = ("zed", "core")


def features_in(local):
    count = lax.axis_size(CHAN)
    rows, length, width = local.shape
    if width % LANES == 0:
        moved = lax.all_to_all(
            local.reshape(count, rows // count, length, width), CHAN, 0, 0, tiled=True
        )
        return moved.reshape(count, -1, width)
    moved = lax.all_to_all(local, CHAN, split_axis=0, concat_axis=2, tiled=True)
    return moved.reshape(1, -1, count * width)


def features_apart(whole, length):
    count = lax.axis_size(CHAN)
    width = whole.shape[1] // count
    if width % LANES == 0:
        return spread(whole, count).reshape(count, -1, length, width)
    return whole.reshape(1, -1, length, count * width)


def features_out(parts):
    if parts.shape[0] > 1:
        moved = lax.all_to_all(parts, CHAN, 0, 0, tiled=True)
        return moved.reshape(-1, *parts.shape[2:])
    return lax.all_to_all(parts[0], CHAN, split_axis=2, concat_axis=0, tiled=True)


MESH = pl.DeviceIdType.MESH


class Corners:
    def __init__(self, seq, zed):
        self.seq_bits, self.zed_bits = (seq.bit_length() - 1, zed.bit_length() - 1)
        self.count = self.seq_bits + self.zed_bits
        self.dims = (2,) * self.count
        self.low = tuple(range(self.seq_bits))[::-1] + tuple(range(self.seq_bits, self.count))[::-1]
        self.high = tuple(range(self.seq_bits)) + tuple(range(self.seq_bits, self.count))[::-1]

    def place(self, dim):
        if dim < self.seq_bits:
            return ("seq", 2 ** (self.seq_bits - 1 - dim))
        return ("zed", 2 ** (self.count - 1 - dim))

    def bit(self, dim):
        axis, weight = self.place(dim)
        return lax.rem(lax.div(lax.axis_index(axis), weight), 2)

    def partner(self, dim):
        axis, weight = self.place(dim)
        return {axis: lax.axis_index(axis) + weight * (1 - 2 * self.bit(dim))}


def reduce_kernel(corners, orders, *refs):
    streams = len(orders)
    stages = corners.count + 1
    given, outs, rest = (refs[:streams], refs[streams : 2 * streams], refs[2 * streams :])
    owns, rest = (rest[:streams], rest[streams:])
    slots, (send_sem, recv_sem, load_sem) = (rest[:-3], rest[-3:])
    core = lax.axis_index("core")
    partners = [{"core": 1 - core}] + [corners.partner(dim) for dim in range(corners.count)]
    barrier = pltpu.get_barrier_semaphore()
    for partner in partners:
        pl.semaphore_signal(barrier, inc=1, device_id=partner, device_id_type=MESH)
    pl.semaphore_wait(barrier, len(partners))

    def indices(order, stage, last):
        fixed = {dim: corners.bit(dim) for dim in order[: stage - 1]}
        if last is not None:
            fixed[order[stage - 1]] = last
        return tuple(fixed.get(dim, slice(None)) for dim in range(corners.count))

    def copy(stream, stage):
        order = orders[stream]
        if stage == 0:
            source = given[stream].at[(slice(None),) * corners.count + (1 - core,)]
            target = {"core": 1 - core}
        else:
            dim = order[stage - 1]
            source = owns[stream].at[indices(order, stage, 1 - corners.bit(dim))]
            target = corners.partner(dim)
        return pltpu.make_async_remote_copy(
            src_ref=source,
            dst_ref=slots[stream * stages + stage],
            send_sem=send_sem.at[stream, stage],
            recv_sem=recv_sem.at[stream, stage],
            device_id=target,
            device_id_type=MESH,
        )

    def load(stream):
        return pltpu.make_async_copy(
            given[stream].at[(slice(None),) * corners.count + (core,)],
            owns[stream],
            load_sem.at[stream],
        )

    for stream in range(streams):
        copy(stream, 0).start()
        load(stream).start()
    for stage in range(stages):
        for stream in range(streams):
            order = orders[stream]
            own, slot = (owns[stream], slots[stream * stages + stage])
            if stage == 0:
                load(stream).wait()
            copy(stream, stage).wait_recv()
            left = [dim for dim in range(corners.count) if dim not in order[:stage]]
            fixed = {dim: corners.bit(dim) for dim in order[:stage]}
            if left:

                def add(index, carry, own=own, slot=slot, left=left, fixed=fixed):
                    part = {
                        dim: lax.rem(lax.div(index, 2 ** (len(left) - 1 - place)), 2)
                        for place, dim in enumerate(left)
                    }
                    mine = tuple({**fixed, **part}[dim] for dim in range(corners.count))
                    come = tuple(part[dim] for dim in left)
                    total = own[mine].astype(jnp.float32) + slot[come].astype(jnp.float32)
                    own[mine] = total.astype(own.dtype)
                    return carry

                lax.fori_loop(0, 2 ** len(left), add, 0)
                copy(stream, stage + 1).start()
            else:
                mine = tuple(fixed[dim] for dim in range(corners.count))
                outs[stream][...] = own[mine].astype(jnp.float32) + slot[...].astype(jnp.float32)
    for stage in range(stages):
        for stream in range(streams):
            copy(stream, stage).wait_send()


def reduce_streams(gradients, highs):
    corners = Corners(lax.axis_size("seq"), lax.axis_size("zed"))
    devices = 2 ** (corners.count + 1)
    orders = [corners.high if high else corners.low for high in highs]
    blocks = [
        g.reshape(corners.dims + (2, g.shape[0] // devices, g.shape[1])) for g in gradients
    ]
    outs = [jax.ShapeDtypeStruct(b.shape[-2:], jnp.float32) for b in blocks]
    owns = [pltpu.VMEM(corners.dims + b.shape[-2:], b.dtype) for b in blocks]
    slots = [
        pltpu.VMEM((2,) * min(corners.count, corners.count - stage) + b.shape[-2:], b.dtype)
        for b in blocks
        for stage in range(corners.count + 1)
    ]
    grid = (len(blocks), corners.count + 1)
    moved = sum(math.prod(g.shape) * g.dtype.itemsize for g in gradients)
    return pl.pallas_call(
        functools.partial(reduce_kernel, corners, orders),
        name="reduce_streams",
        in_specs=[pl.BlockSpec(memory_space=pl.ANY)] * len(blocks),
        out_specs=[pl.BlockSpec(memory_space=pltpu.VMEM)] * len(blocks),
        out_shape=outs,
        scratch_shapes=owns
        + slots
        + [
            pltpu.SemaphoreType.DMA(grid),
            pltpu.SemaphoreType.DMA(grid),
            pltpu.SemaphoreType.DMA((len(blocks),)),
        ],
        compiler_params=pltpu.CompilerParams(
            collective_id=1, has_side_effects=True, vmem_limit_bytes=VMEM_BYTES
        ),
        cost_estimate=pl.CostEstimate(flops=0, bytes_accessed=20 * moved, transcendentals=0),
    )(*blocks)


def grads_kernel(
    normed_ref,
    dgate_ref,
    dup_ref,
    hidden_ref,
    gout_ref,
    mixed_ref,
    dres_ref,
    out_ref,
    turned_ref,
    made_wide,
    made_down,
    made_out,
    come_wide,
    come_down,
    come_out,
    send_sem,
    recv_sem,
    store_sem,
):
    step = pl.program_id(0)
    core = lax.axis_index("core")
    other = {"core": 1 - core}
    wide_rows, down_rows, out_rows = (made_wide.shape[3], made_down.shape[3], made_out.shape[3])
    wides, downs, lasts = (come_wide.shape[0], come_down.shape[0], come_out.shape[0])
    total = wides + downs + lasts
    down_at, out_at = (wides * wide_rows, wides * wide_rows + down_rows)

    def exchange(made, come, index, slot):
        return pltpu.make_async_remote_copy(
            src_ref=made.at[lax.rem(index, 2), 1 - core],
            dst_ref=come.at[index],
            send_sem=send_sem.at[slot],
            recv_sem=recv_sem.at[slot],
            device_id=other,
            device_id_type=MESH,
        )

    def store_wide(index):
        return pltpu.make_async_copy(
            come_wide.at[index],
            out_ref.at[:, pl.ds(pl.multiple_of(index * wide_rows, wide_rows), wide_rows)],
            store_sem.at[index],
        )

    def store_down(index):
        chips = come_down.shape[1]
        return pltpu.make_async_copy(
            come_down.at[index],
            out_ref.at[pl.ds(index * chips, chips), pl.ds(down_at, down_rows)],
            store_sem.at[index + wides],
        )

    def store_out(index):
        chips = come_out.shape[1]
        return pltpu.make_async_copy(
            come_out.at[index],
            out_ref.at[pl.ds(index * chips, chips), pl.ds(out_at, out_rows)],
            store_sem.at[index + wides + downs],
        )

    @pl.when(step == 0)
    def _():
        barrier = pltpu.get_barrier_semaphore()
        pl.semaphore_signal(barrier, inc=1, device_id=other, device_id_type=MESH)
        pl.semaphore_wait(barrier, 1)
        turned_ref[...] = normed_ref[...].T

    def product_wide(source, index):
        made = made_wide.at[lax.rem(index, 2)]
        chips, rows = (made.shape[1], made.shape[2])
        tile = 256

        def column(place, carry):
            at = pl.ds(pl.multiple_of(place * tile, tile), tile)
            part = jnp.dot(turned_ref[...], source[:, at], preferred_element_type=jnp.float32)
            part = part.astype(jnp.bfloat16).reshape(chips, 2, rows, tile)
            made[0, :, :, at] = part[:, 0]
            made[1, :, :, at] = part[:, 1]
            return carry

        lax.fori_loop(0, source.shape[1] // tile, column, 0)

    def product_tall(left, right, made_all, index):
        made = made_all.at[lax.rem(index, 2)]
        chips, rows = (made.shape[1], made.shape[2])
        tile = 256

        def column(place, carry):
            at = pl.ds(pl.multiple_of(place * tile, tile), tile)
            part = lax.dot_general(
                left[...], right[:, at], (((0,), (0,)), ((), ())), preferred_element_type=jnp.float32
            )
            part = part.astype(jnp.bfloat16).reshape(chips, 2, rows, tile)
            made[0, :, :, at] = part[:, 0]
            made[1, :, :, at] = part[:, 1]
            return carry

        lax.fori_loop(0, right.shape[1] // tile, column, 0)

    half = wides // 2

    @pl.when(step < half)
    def _():
        product_wide(dgate_ref, step)

    @pl.when((step >= half) & (step < wides))
    def _():
        product_wide(dup_ref, step)

    @pl.when(step < wides)
    def _():
        exchange(made_wide, come_wide, step, step).start()

    @pl.when((step >= wides) & (step < wides + downs))
    def _():
        product_tall(hidden_ref, gout_ref, made_down, step - wides)
        exchange(made_down, come_down, step - wides, step).start()

    @pl.when((step >= wides + downs) & (step < total))
    def _():
        product_tall(mixed_ref, dres_ref, made_out, step - wides - downs)
        exchange(made_out, come_out, step - wides - downs, step).start()

    def finish(made, come, index, slot, store):
        exchange(made, come, index, slot).wait()
        mine = made.at[lax.rem(index, 2), core]
        arrived = come.at[index]

        def add(chip, carry):
            both = mine[chip].astype(jnp.float32) + arrived[chip].astype(jnp.float32)
            arrived[chip] = both.astype(jnp.bfloat16)
            return carry

        lax.fori_loop(0, come.shape[1], add, 0)
        store(index).start()

    before = step - 1

    @pl.when((before >= 0) & (before < wides))
    def _():
        finish(made_wide, come_wide, before, before, store_wide)

    @pl.when((before >= wides) & (before < wides + downs))
    def _():
        finish(made_down, come_down, before - wides, before, store_down)

    @pl.when(before >= wides + downs)
    def _():
        finish(made_out, come_out, before - wides - downs, before, store_out)

    @pl.when(step == total)
    def _():
        for index in range(wides):
            store_wide(index).wait()
        for index in range(downs):
            store_down(index).wait()
        for index in range(lasts):
            store_out(index).wait()


def block_gradients(normed, dgate, dup, hidden, gout, mixed, dres):
    tokens, model = normed.shape
    ffn, rec = (hidden.shape[1], mixed.shape[1])
    chips = lax.axis_size("seq") * lax.axis_size("zed")
    devices = 2 * chips
    wide_rows, down_rows, out_rows = (model // devices, ffn // devices, rec // devices)
    chunk = 768
    wides, downs, lasts = (2 * ffn // model, ffn // chunk, rec // chunk)
    half = wides // 2
    down_chips, out_chips = (chunk // (2 * down_rows), chunk // (2 * out_rows))
    rows = wides * wide_rows + down_rows + out_rows
    low = jnp.bfloat16

    def whole(array):
        return pl.BlockSpec(array.shape, lambda s: (0, 0), pipeline_mode=pl.Buffered(1))

    def part(columns, first, count):
        return pl.BlockSpec((tokens, columns), lambda s: (0, jnp.clip(s - first, 0, count - 1)))

    total = wides + downs + lasts
    flops = 2 * tokens * model * (3 * ffn + rec)
    arrays = (normed, dgate, dup, hidden, gout, mixed, dres)
    moved = sum(math.prod(a.shape) * 2 for a in arrays) + chips * rows * model * 2
    return pl.pallas_call(
        grads_kernel,
        name="block_gradients",
        grid=(total + 1,),
        in_specs=[
            whole(normed),
            part(model, 0, half),
            part(model, half, half),
            part(chunk, wides, downs),
            whole(gout),
            part(chunk, wides + downs, lasts),
            whole(dres),
        ],
        out_specs=pl.BlockSpec(memory_space=pl.ANY),
        out_shape=jax.ShapeDtypeStruct((chips, rows, model), low),
        scratch_shapes=[
            pltpu.VMEM((model, tokens), low),
            pltpu.VMEM((2, 2, chips, wide_rows, model), low),
            pltpu.VMEM((2, 2, down_chips, down_rows, model), low),
            pltpu.VMEM((2, 2, out_chips, out_rows, model), low),
            pltpu.VMEM((wides, chips, wide_rows, model), low),
            pltpu.VMEM((downs, down_chips, down_rows, model), low),
            pltpu.VMEM((lasts, out_chips, out_rows, model), low),
            pltpu.SemaphoreType.DMA((total,)),
            pltpu.SemaphoreType.DMA((total,)),
            pltpu.SemaphoreType.DMA((total,)),
        ],
        compiler_params=pltpu.CompilerParams(
            collective_id=2, has_side_effects=True, vmem_limit_bytes=VMEM_BYTES
        ),
        cost_estimate=pl.CostEstimate(flops=flops, bytes_accessed=moved, transcendentals=0),
    )(*arrays)


def carried(factor, value, axis, backward):
    count, mine = (lax.axis_size(axis), lax.axis_index(axis))
    pieces = lax.all_gather(jnp.stack([factor, value]), axis)
    order = range(count - 1, 0, -1) if backward else range(count - 1)
    total = jnp.zeros_like(value)
    for place in order:
        longer = pieces[place, 0] * total + pieces[place, 1]
        total = jnp.where(place > mine if backward else place < mine, longer, total)
    return total


def passed_along(value, axis, steps):
    count = lax.axis_size(axis)
    leading, last = (max(0, -steps), min(count, count - steps))
    return lax.ppermute(value, axis, [(source, source + steps) for source in range(leading, last)])


def weight_grad(left, right):
    return lax.dot_general(
        left, right, (((0,), (0,)), ((), ())), preferred_element_type=jnp.float32
    ).astype(jnp.bfloat16)


def back_dot(left, right):
    return lax.dot_general(
        left, right, (((1,), (1,)), ((), ())), preferred_element_type=jnp.float32
    )


def fwd_dot(left, right):
    return jnp.dot(left, right, preferred_element_type=jnp.float32)


def gelu_fn(value):
    return jax.nn.gelu(value, approximate=True)


def norm_back(grad_norm, normed, inverse, gain):
    scaled = grad_norm * gain
    mean_term = jnp.mean(scaled * normed, axis=1, keepdims=True)
    return inverse * (scaled - normed * mean_term)


def scattered(gradient):
    return lax.psum_scatter(
        gradient, ("seq", "zed", "core"), scatter_dimension=0, tiled=True
    ).astype(jnp.float32)


def body(
    tokens,
    cotangent,
    doc_starts,
    lengths,
    norm1_gain,
    recur_input,
    recur_gate,
    conv_kernel,
    conv_bias,
    lru_gates,
    lru_bias,
    lru_decay,
    recur_out,
    norm2_gain,
    mlp_gate,
    mlp_up,
    mlp_down,
):
    count = lax.axis_size(CHAN)
    row_count, block_len = (tokens.shape[0] // count, tokens.shape[1])
    model_dim = tokens.shape[2] * count
    tok_count = row_count * block_len
    rec_width = recur_input.shape[1]
    ffn_width = mlp_gate.shape[1]
    head_count = H
    head_size = rec_width // head_count
    tap_count = conv_kernel.shape[0]
    rim_size = tap_count - 1
    seq_index = lax.axis_index("seq")
    position = seq_index * block_len + jnp.arange(block_len, dtype=jnp.int32)
    bounds = jnp.concatenate([doc_starts, lengths[:, None]], axis=1)
    is_before = bounds[:, None, :] <= position[None, :, None]
    seg_start = jnp.max(jnp.where(is_before, bounds[:, None, :], 0), axis=2)
    low_x, inverse_lanes, normed_low, branch_pre, gate_pre = front(
        features_in(tokens), norm1_gain, recur_input, recur_gate
    )
    gate_act = gelu_fn(gate_pre)
    branch_rows = branch_pre.reshape(row_count, block_len, rec_width)
    core = Recurrence(row_count, block_len, rec_width, head_size)
    prev_rim = passed_along(
        branch_rows[:, block_len - rim_size :, :].astype(jnp.bfloat16), "seq", 1
    ).astype(jnp.float32)
    rim = jnp.pad(prev_rim, ((0, 0), (SUBLANES - rim_size, 0), (0, 0)))
    dist = jnp.broadcast_to(
        (position[None, :] - seg_start)[:, :, None], (row_count, block_len, LANES)
    )
    soft_decay = jax.nn.softplus(-lru_decay)
    params = jnp.concatenate(
        [
            conv_kernel,
            conv_bias[None],
            lru_bias,
            (-8.0 * soft_decay)[None],
            jnp.zeros((SUBLANES, rec_width), jnp.float32),
        ],
        axis=0,
    )
    wide_gates = core.widen(lru_gates)
    lru_in, rate_gate, input_gate, local_state, cum_coef = core.forward(
        branch_rows, rim, dist, params, wide_gates
    )
    cotangent, local_state = lax.optimization_barrier((features_in(cotangent), local_state))
    carry_in = carried(cum_coef[:, -1, :], local_state[:, -1, :], "seq", False)
    entering = carry_in[:, None, :]
    state_rows = local_state + cum_coef * entering
    state_flat = state_rows.reshape(tok_count, rec_width)
    mixed_low = (state_flat * gate_act).astype(jnp.bfloat16)
    resid_one = low_x.astype(jnp.float32) + fwd_dot(mixed_low, recur_out)
    inv_two = lax.rsqrt(jnp.mean(resid_one * resid_one, axis=1, keepdims=True) + EPS)
    normed_two = resid_one * inv_two
    normed_low2 = (normed_two * norm2_gain).astype(jnp.bfloat16)
    mlp_gate_pre = fwd_dot(normed_low2, mlp_gate)
    mlp_up_pre = fwd_dot(normed_low2, mlp_up)
    gelu_gate = gelu_fn(mlp_gate_pre)
    hidden_low = (gelu_gate * mlp_up_pre).astype(jnp.bfloat16)
    result = (resid_one + fwd_dot(hidden_low, mlp_down)).astype(jnp.bfloat16)
    grad_low = collect(cotangent, lengths - seq_index * block_len)
    grad_hidden = back_dot(grad_low, mlp_down)
    _, gelu_pull = jax.vjp(gelu_fn, mlp_gate_pre)
    mgate_low = gelu_pull(grad_hidden * mlp_up_pre)[0].astype(jnp.bfloat16)
    mup_low = (grad_hidden * gelu_gate).astype(jnp.bfloat16)
    result_parts, mgate_low, mup_low = lax.optimization_barrier(
        (features_apart(result, block_len), mgate_low, mup_low)
    )
    output = features_out(result_parts)
    grad_norm2 = back_dot(mgate_low, mlp_gate) + back_dot(mup_low, mlp_up)
    resid_part = norm_back(grad_norm2, normed_two, inv_two, norm2_gain)
    grad_resid = grad_low.astype(jnp.float32) + resid_part
    resid_low = grad_resid.astype(jnp.bfloat16)
    devices = lax.axis_size(("seq", "zed", "core"))
    own_rows = model_dim // devices
    tiled = own_rows % (2 * SUBLANES) == 0 and ffn_width % model_dim == 0
    if tiled:
        merged = block_gradients(
            normed_low2, mgate_low, mup_low, hidden_low, grad_low, mixed_low, resid_low
        )
        merged, resid_low = lax.optimization_barrier((merged, resid_low))
        merged = lax.psum_scatter(merged, "seq", scatter_dimension=0, tiled=True)
    grad_mixed = back_dot(resid_low, recur_out)
    gate_low, back_local, back_cum, first_term = core.adjoint(
        grad_mixed.reshape(row_count, block_len, rec_width),
        gate_pre.reshape(row_count, block_len, rec_width),
        local_state,
        cum_coef,
        entering,
        rate_gate,
        dist,
        params,
    )
    gate_low = gate_low.reshape(tok_count, rec_width)
    output, back_local = lax.optimization_barrier((output, back_local))
    carry_out = carried(cum_coef[:, -1, :], first_term[:, 0, :], "seq", True)
    branch_local, tail, lead, channel_sums, gate_sums = core.backward(
        back_local,
        back_cum,
        carry_out[:, None, :],
        local_state,
        cum_coef,
        entering,
        rate_gate,
        input_gate,
        lru_in,
        dist,
        branch_rows,
        rim,
        params,
        wide_gates,
    )
    spare = jnp.swapaxes(channel_sums, 0, 1)
    small = jnp.concatenate(
        [gate_sums[:, :head_size], spare, gate_sums[:, head_size + SUBLANES :]], axis=1
    )
    from_next = passed_along(
        lead[:, SUBLANES - rim_size :, :].astype(jnp.bfloat16), "seq", -1
    )
    ending = tail + jnp.pad(from_next.astype(jnp.float32), ((0, 0), (SUBLANES - rim_size, 0), (0, 0)))
    branch_low = lax.dynamic_update_slice(
        branch_local, ending.astype(jnp.bfloat16), (0, block_len - SUBLANES, 0)
    ).reshape(tok_count, rec_width)
    grad_rin = weight_grad(normed_low, branch_low)
    grad_rgate = weight_grad(normed_low, gate_low)
    grad_norm1 = back_dot(branch_low, recur_input) + back_dot(gate_low, recur_gate)
    inv_one = inverse_lanes[:, :1]
    normed_one = low_x.astype(jnp.float32) * inv_one
    input_part = norm_back(grad_norm1, normed_one, inv_one, norm1_gain)
    grad_x = (grad_resid + input_part).astype(jnp.bfloat16)
    if tiled:
        merged, grad_x = lax.optimization_barrier((merged, grad_x))
        merged = lax.psum_scatter(merged, "zed", scatter_dimension=0, tiled=True)
    grad_tokens = features_out(features_apart(grad_x, block_len))
    if tiled:
        sum_rgate, sum_rin, own_small = reduce_streams(
            (grad_rgate, grad_rin, small.astype(jnp.bfloat16)), (False, True, False)
        )
        own = merged[0].astype(jnp.float32)
        span = ffn_width // model_dim * own_rows

        def unfolded(part):
            return jnp.swapaxes(part.reshape(-1, own_rows, model_dim), 0, 1).reshape(own_rows, -1)

        sum_mgate, sum_mup = (unfolded(own[:span]), unfolded(own[span : 2 * span]))
        sum_down = own[2 * span : 2 * span + ffn_width // devices]
        sum_rout = own[2 * span + ffn_width // devices :]
    else:
        sum_mgate, sum_mup, sum_down, sum_rout, sum_rgate, sum_rin = (
            scattered(weight_grad(left, right))
            for left, right in (
                (normed_low2, mgate_low),
                (normed_low2, mup_low),
                (hidden_low, grad_low),
                (mixed_low, resid_low),
                (normed_low, gate_low),
                (normed_low, branch_low),
            )
        )
        own_small = scattered(small)
    sum_lgates = jnp.concatenate(
        [own_small[:, :head_size], own_small[:, LANES : LANES + head_size]], axis=1
    )
    own_sums = jnp.swapaxes(own_small[:, head_size : head_size + SUBLANES], 0, 1)
    device = lax.axis_index(("seq", "zed", "core"))

    def mine(array, size, axis=0):
        return lax.dynamic_slice_in_dim(array, device * size, size, axis)

    def weighed(weight, gradient):
        return jnp.sum(mine(weight, own_rows).astype(jnp.float32) * gradient, axis=1)

    sum_gain1 = (weighed(recur_input, sum_rin) + weighed(recur_gate, sum_rgate)) / mine(
        norm1_gain, own_rows
    )
    sum_gain2 = (weighed(mlp_gate, sum_mgate) + weighed(mlp_up, sum_mup)) / mine(
        norm2_gain, own_rows
    )
    own_channels = own_sums.shape[1]
    sum_decay = 8.0 * jax.nn.sigmoid(-mine(lru_decay, own_channels)) * own_sums[7]
    return (
        output,
        grad_tokens,
        sum_gain1,
        sum_rin,
        sum_rgate,
        own_sums[:4],
        own_sums[4],
        sum_lgates,
        own_sums[5:7],
        sum_decay,
        sum_rout,
        sum_gain2,
        sum_mgate,
        sum_mup,
        sum_down,
    )


def solution(mesh):
    seq, chan = (mesh.shape["seq"], mesh.shape["chan"])
    chips = jax.sharding.Mesh(mesh.devices.reshape(seq, chan // 2, 2), ("seq", "zed", "core"))
    chan = ("zed", "core")
    every = ("seq", "zed", "core")
    activations = P(None, "seq", chan)
    rows, columns, vector = (P(every, None), P(None, every), P(every))
    return jax.shard_map(
        body,
        mesh=chips,
        in_specs=(activations, activations, P(chan, None), P(chan)) + (P(),) * 13,
        out_specs=(
            activations,
            activations,
            vector,
            rows,
            rows,
            columns,
            vector,
            rows,
            columns,
            vector,
            rows,
            vector,
            rows,
            rows,
            rows,
        ),
        check_vma=False,
    )
```

```python
import functools
import math

import jax
import jax.numpy as jnp
from jax import lax
from jax.experimental import pallas as pl
from jax.experimental.pallas import tpu as pltpu
from jax.sharding import PartitionSpec as P

H = 16


EPS = 1e-06
ROOT_FLOOR = 1e-06
LANES = 128
SUBLANES = 8
STEP = 16
VMEM_BYTES = 56 * 1024 * 1024


def sigmoid(value):
    return 0.5 * jnp.tanh(0.5 * value) + 0.5


GELU_C = 0.7978845608
GELU_A = 0.044715


def gelu_pair(value):
    square = value * value
    inner = jnp.tanh(value * (GELU_C + (GELU_C * GELU_A) * square))
    half = 0.5 + 0.5 * inner
    slope = GELU_C + (3.0 * GELU_C * GELU_A) * square
    return (value * half, half + 0.5 * value * (1.0 - inner * inner) * slope)


def root_argument(log_decay, decay):
    y = 2.0 * log_decay
    series = 1.0 + y * (1.0 / 7.0)
    for divisor in (6.0, 5.0, 4.0, 3.0, 2.0):
        series = 1.0 + (y * (1.0 / divisor)) * series
    return jnp.where(y > -0.25, -y * series, 1.0 - decay * decay)


def across(column, width):
    return jnp.concatenate([column] * (width // LANES), axis=1)


def forward_kernel(
    branch_ref,
    rim_ref,
    dist_ref,
    par_ref,
    gates_ref,
    lru_ref,
    rate_ref,
    igate_ref,
    state_ref,
    cum_ref,
    both_ref,
):
    rows, length, width = branch_ref.shape
    taps = [par_ref[k : k + 1, :] for k in range(4)]
    conv_bias, rate_bias, input_bias, soft = (par_ref[k : k + 1, :] for k in range(4, 8))
    place = lax.broadcasted_iota(jnp.int32, (SUBLANES, width), 0)

    for row in range(rows):

        def conv_step(index, before, row=row):
            base = pl.multiple_of(index * STEP, STEP)
            pieces = []
            for half in range(STEP // SUBLANES):
                at = pl.ds(base + half * SUBLANES, SUBLANES)
                here = branch_ref[row, at, :]
                dist = across(dist_ref[row, at, :], width)
                total = conv_bias + taps[0] * here
                for k in range(1, 4):
                    shifted = pltpu.roll(jnp.where(place < SUBLANES - k, here, before), k, 0)
                    total = total + taps[k] * jnp.where(dist >= k, shifted, 0.0)
                pieces.append(total)
                before = here
            lru_ref[row, pl.ds(base, STEP), :] = jnp.concatenate(pieces, axis=0).astype(jnp.bfloat16)
            return before

        lax.fori_loop(0, length // STEP, conv_step, rim_ref[row])

        piece = min(length, 256)

        def dot_step(index, carry, row=row):
            at = pl.ds(pl.multiple_of(index * piece, piece), piece)
            both_ref[row, at, :] = jnp.dot(
                lru_ref[row, at, :], gates_ref[...], preferred_element_type=jnp.float32
            )
            return carry

        lax.fori_loop(0, length // piece, dot_step, 0)

    def scan_step(index, carry):
        base = pl.multiple_of(index * STEP, STEP)
        later = []
        for row in range(rows):
            run_cum, run_state = carry[row]
            lru_both = lru_ref[row, pl.ds(base, STEP), :].astype(jnp.float32)
            for half in range(STEP // SUBLANES):
                at = pl.ds(base + half * SUBLANES, SUBLANES)
                lru = lru_both[half * SUBLANES : (half + 1) * SUBLANES]
                start = across(dist_ref[row, at, :], width) == 0
                rate = sigmoid(both_ref[row, at, :width] + rate_bias)
                igate = sigmoid(both_ref[row, at, width:] + input_bias)
                log_decay = rate * soft
                decay = jnp.exp(log_decay)
                arg = jnp.maximum(root_argument(log_decay, decay), ROOT_FLOOR)
                root = arg * lax.rsqrt(arg)
                cum = jnp.where(start, 0.0, decay)
                value = jnp.where(start, 1.0, root) * igate * lru
                rate_ref[row, at, :] = rate
                igate_ref[row, at, :] = igate
                for shift in (1, 2, 4):
                    live = place >= shift
                    value = value + cum * jnp.where(live, pltpu.roll(value, shift, 0), 0.0)
                    cum = cum * jnp.where(live, pltpu.roll(cum, shift, 0), 1.0)
                value = value + cum * run_state
                cum = cum * run_cum
                state_ref[row, at, :] = value
                cum_ref[row, at, :] = cum
                run_state = value[SUBLANES - 1 :, :]
                run_cum = cum[SUBLANES - 1 :, :]
            later.append((run_cum, run_state))
        return tuple(later)

    one, zero = (jnp.ones((1, width), jnp.float32), jnp.zeros((1, width), jnp.float32))
    lax.fori_loop(0, length // STEP, scan_step, tuple((one, zero) for _ in range(rows)))


def adjoint_kernel(
    dmix_ref,
    pre_ref,
    state_ref,
    cum_ref,
    carry_ref,
    rate_ref,
    dist_ref,
    par_ref,
    dgate_ref,
    local_ref,
    back_ref,
    first_ref,
):
    rows, length, width = dmix_ref.shape
    soft = par_ref[7:8, :]
    place = lax.broadcasted_iota(jnp.int32, (SUBLANES, width), 0)
    last = length // STEP - 1

    def step(index, carry):
        base = pl.multiple_of((last - index) * STEP, STEP)
        later = []
        for row in range(rows):
            run_cum, run_back = carry[row]
            entering = carry_ref[row]
            pieces = []
            for half in reversed(range(STEP // SUBLANES)):
                at = pl.ds(base + half * SUBLANES, SUBLANES)
                start = across(dist_ref[row, at, :], width) == 0
                state = state_ref[row, at, :] + cum_ref[row, at, :] * entering
                act, slope = gelu_pair(pre_ref[row, at, :])
                dmix = dmix_ref[row, at, :]
                pieces.append(dmix * state * slope)
                dstate = dmix * act
                coef = jnp.where(start, 0.0, jnp.exp(rate_ref[row, at, :] * soft))
                value = coef * dstate
                for shift in (1, 2, 4):
                    live = place < SUBLANES - shift
                    turn = SUBLANES - shift
                    value = value + coef * jnp.where(live, pltpu.roll(value, turn, 0), 0.0)
                    coef = coef * jnp.where(live, pltpu.roll(coef, turn, 0), 1.0)
                value = value + coef * run_back
                coef = coef * run_cum
                inside = place < SUBLANES - 1
                local_ref[row, at, :] = dstate + jnp.where(
                    inside, pltpu.roll(value, SUBLANES - 1, 0), run_back
                )
                back_ref[row, at, :] = jnp.where(inside, pltpu.roll(coef, SUBLANES - 1, 0), run_cum)
                run_back = value[:1, :]
                run_cum = coef[:1, :]
            dgate_ref[row, pl.ds(base, STEP), :] = jnp.concatenate(pieces[::-1], axis=0).astype(
                jnp.bfloat16
            )
            later.append((run_cum, run_back))
        return tuple(later)

    one, zero = (jnp.ones((1, width), jnp.float32), jnp.zeros((1, width), jnp.float32))
    done = lax.fori_loop(0, last + 1, step, tuple((one, zero) for _ in range(rows)))
    for row in range(rows):
        first_ref[row] = done[row][1]


def backward_kernel(
    head_size,
    local_ref,
    back_ref,
    out_ref,
    state_ref,
    cum_ref,
    in_ref,
    rate_ref,
    igate_ref,
    lru_ref,
    dist_ref,
    branch_ref,
    rim_ref,
    par_ref,
    gates_ref,
    dbranch_ref,
    tail_ref,
    head_ref,
    sums_ref,
    dgates_ref,
    both_ref,
    dconv_ref,
):
    rows, length, width = local_ref.shape
    taps = [par_ref[k : k + 1, :] for k in range(4)]
    soft = par_ref[7:8, :]
    place = lax.broadcasted_iota(jnp.int32, (SUBLANES, width), 0)
    zeros = jnp.zeros((SUBLANES, width), jnp.float32)

    def gate_step(index, carry):
        sums, earlier = carry
        decay_sum, rate_sum, input_sum = sums
        base = pl.multiple_of(index * STEP, STEP)
        later = []
        for row in range(rows):
            before = earlier[row]
            entering = in_ref[row]
            leaving = out_ref[row]
            lru_both = lru_ref[row, pl.ds(base, STEP), :].astype(jnp.float32)
            drates, dinputs = ([], [])
            for half in range(STEP // SUBLANES):
                at = pl.ds(base + half * SUBLANES, SUBLANES)
                lru = lru_both[half * SUBLANES : (half + 1) * SUBLANES]
                start = across(dist_ref[row, at, :], width) == 0
                adjoint = local_ref[row, at, :] + back_ref[row, at, :] * leaving
                state = state_ref[row, at, :] + cum_ref[row, at, :] * entering
                previous = jnp.where(place < 1, before, pltpu.roll(state, 1, 0))
                before = state[SUBLANES - 1 :, :]
                rate = rate_ref[row, at, :]
                igate = igate_ref[row, at, :]
                log_decay = rate * soft
                decay = jnp.exp(log_decay)
                arg = root_argument(log_decay, decay)
                above = arg > ROOT_FLOOR
                arg = jnp.maximum(arg, ROOT_FLOOR)
                inverse = lax.rsqrt(arg)
                scale = jnp.where(start, 1.0, arg * inverse)
                gated = adjoint * igate
                dscale = gated * lru
                pull = jnp.where(above, dscale * decay * decay * inverse, 0.0)
                dlog = jnp.where(start, 0.0, adjoint * previous * decay - pull)
                dig = adjoint * scale * lru
                weighted = dlog * rate
                decay_sum = decay_sum + weighted
                drates.append(weighted * soft * (1.0 - rate))
                dinputs.append(dig * igate * (1.0 - igate))
                dconv_ref[row, at, :] = gated * scale
            drate = jnp.concatenate(drates, axis=0).astype(jnp.bfloat16)
            dinput = jnp.concatenate(dinputs, axis=0).astype(jnp.bfloat16)
            both_ref[row, pl.ds(base, STEP), :width] = drate
            both_ref[row, pl.ds(base, STEP), width:] = dinput
            drate = drate.astype(jnp.float32)
            dinput = dinput.astype(jnp.float32)
            rate_sum = rate_sum + (drate[:SUBLANES] + drate[SUBLANES:])
            input_sum = input_sum + (dinput[:SUBLANES] + dinput[SUBLANES:])
            later.append(before)
        return ((decay_sum, rate_sum, input_sum), tuple(later))

    sums, _ = lax.fori_loop(
        0,
        length // STEP,
        gate_step,
        ((zeros, zeros, zeros), tuple(in_ref[row] for row in range(rows))),
    )
    for slot, total in zip((5, 6, 7), (sums[1], sums[2], sums[0])):
        sums_ref[slot : slot + 1, :] = jnp.sum(total, axis=0, keepdims=True)

    piece = min(length, 256)
    wide = None
    for row in range(rows):

        def dot_step(index, carry, row=row):
            at = pl.ds(pl.multiple_of(index * piece, piece), piece)
            dconv_ref[row, at, :] += lax.dot_general(
                both_ref[row, at, :],
                gates_ref[...],
                (((1,), (1,)), ((), ())),
                preferred_element_type=jnp.float32,
            )
            return carry

        lax.fori_loop(0, length // piece, dot_step, 0)
        part = lax.dot_general(
            lru_ref[row], both_ref[row], (((0,), (0,)), ((), ())), preferred_element_type=jnp.float32
        )
        wide = part if wide is None else wide + part
    row_head = lax.broadcasted_iota(jnp.int32, (width, width), 0) // head_size
    col_head = lax.broadcasted_iota(jnp.int32, (width, width), 1) // head_size
    own = row_head == col_head
    for part in range(2):
        kept = jnp.where(own, wide[:, part * width : (part + 1) * width], 0.0)
        folded = kept
        for other in range(1, width // head_size):
            folded = folded + pltpu.roll(kept, width - other * head_size, 1)
        dgates_ref[:, part * LANES : (part + 1) * LANES] = folded[:, :LANES]

    def conv_step(index, carry):
        sums, following = carry
        sums = list(sums)
        base = pl.multiple_of((length // STEP - 1 - index) * STEP, STEP)
        later = []
        for row in range(rows):
            after = following[row]
            pieces = []
            for half in reversed(range(STEP // SUBLANES)):
                at = pl.ds(base + half * SUBLANES, SUBLANES)
                dist = across(dist_ref[row, at, :], width)
                branch = branch_ref[row, at, :]
                here = dconv_ref[row, at, :]
                total = taps[0] * here
                sums[0] = sums[0] + here * branch
                sums[4] = sums[4] + here
                masked = tuple(jnp.where(dist >= k, here, 0.0) for k in range(1, 4))
                for k in range(1, 4):
                    moved = pltpu.roll(
                        jnp.where(place >= k, masked[k - 1], after[k - 1]), SUBLANES - k, 0
                    )
                    total = total + taps[k] * moved
                    sums[k] = sums[k] + branch * moved
                after = masked
                pieces.append(total)
            whole = jnp.concatenate(pieces[::-1], axis=0)
            dbranch_ref[row, pl.ds(base, STEP), :] = whole.astype(jnp.bfloat16)
            later.append(after)

            @pl.when(index == 0)
            def _(row=row, whole=whole):
                tail_ref[row] = whole[STEP - SUBLANES :]

        return (tuple(sums), tuple(later))

    sums, firsts = lax.fori_loop(
        0,
        length // STEP,
        conv_step,
        ((zeros,) * 5, tuple((zeros,) * 3 for _ in range(rows))),
    )
    sums = list(sums)
    for row in range(rows):
        total = zeros
        rim = rim_ref[row]
        for k in range(1, 4):
            moved = pltpu.roll(jnp.where(place >= k, 0.0, firsts[row][k - 1]), SUBLANES - k, 0)
            total = total + taps[k] * moved
            sums[k] = sums[k] + rim * moved
        head_ref[row] = total
    for slot in range(5):
        sums_ref[slot : slot + 1, :] = jnp.sum(sums[slot], axis=0, keepdims=True)


def channel_call(kernel, name, arrays, specs, outs, out_specs, scratch, blocks, flops):
    moved = sum(math.prod(a.shape) * a.dtype.itemsize for a in (*arrays, *outs))
    return pl.pallas_call(
        kernel,
        name=name,
        grid=(blocks,),
        in_specs=specs,
        out_specs=out_specs,
        out_shape=outs,
        scratch_shapes=scratch,
        compiler_params=pltpu.CompilerParams(vmem_limit_bytes=VMEM_BYTES),
        cost_estimate=pl.CostEstimate(flops=flops, bytes_accessed=moved, transcendentals=0),
    )(*arrays)


class Recurrence:
    def __init__(self, rows, length, channels, head_size):
        self.rows, self.length, self.channels = (rows, length, channels)
        self.head_size = head_size
        self.width = head_size * LANES // math.gcd(head_size, LANES)
        self.blocks = channels // self.width
        self.flops = 2 * rows * length * channels * 2 * self.width

    def tall(self):
        return pl.BlockSpec((self.rows, self.length, self.width), lambda j: (0, 0, j))

    def short(self, size):
        return pl.BlockSpec((self.rows, size, self.width), lambda j: (0, 0, j))

    def flat(self, size):
        return pl.BlockSpec((size, self.width), lambda j: (0, j))

    def dist(self):
        return pl.BlockSpec((self.rows, self.length, LANES), lambda j: (0, 0, 0))

    def gates(self, columns):
        return pl.BlockSpec((self.width, columns), lambda j: (j, 0))

    def shape(self, size, dtype):
        return jax.ShapeDtypeStruct((self.rows, size, self.channels), dtype)

    def widen(self, lru_gates):
        size, width = (self.head_size, self.width)
        heads = width // size
        column = jnp.arange(2 * width)
        source = (column // width) * size + column % size
        spread = (jnp.arange(2 * size)[:, None] == source[None, :]).astype(jnp.bfloat16)
        owner = (column % width) // size
        mine = (jnp.arange(self.channels) // size) % heads
        wide = jnp.dot(lru_gates, spread, preferred_element_type=jnp.float32)
        return jnp.where(mine[:, None] == owner[None, :], wide, 0.0).astype(jnp.bfloat16)

    def forward(self, branch, rim, dist, params, gates):
        f32 = jnp.float32
        outs = [self.shape(self.length, d) for d in (jnp.bfloat16, f32, f32, f32, f32)]
        return channel_call(
            forward_kernel,
            "recurrence_forward",
            (branch, rim, dist, params, gates),
            [self.tall(), self.short(SUBLANES), self.dist(), self.flat(16), self.gates(2 * self.width)],
            outs,
            [self.tall()] * 5,
            [pltpu.VMEM((self.rows, self.length, 2 * self.width), f32)],
            self.blocks,
            self.flops,
        )

    def adjoint(self, dmix, pre, state, cum, entering, rate, dist, params):
        f32 = jnp.float32
        outs = [self.shape(self.length, d) for d in (jnp.bfloat16, f32, f32)] + [self.shape(1, f32)]
        tall = self.tall()
        return channel_call(
            adjoint_kernel,
            "recurrence_adjoint",
            (dmix, pre, state, cum, entering, rate, dist, params),
            [tall, tall, tall, tall, self.short(1), tall, self.dist(), self.flat(16)],
            outs,
            [tall, tall, tall, self.short(1)],
            [],
            self.blocks,
            0,
        )

    def backward(
        self, local, back, leaving, state, cum, entering, rate, igate, lru, dist, branch, rim, params, gates
    ):
        f32 = jnp.float32
        outs = [
            self.shape(self.length, jnp.bfloat16),
            self.shape(SUBLANES, f32),
            self.shape(SUBLANES, f32),
            jax.ShapeDtypeStruct((SUBLANES, self.channels), f32),
            jax.ShapeDtypeStruct((self.channels, 2 * LANES), f32),
        ]
        tall, one = (self.tall(), self.short(1))
        return channel_call(
            functools.partial(backward_kernel, self.head_size),
            "recurrence_backward",
            (local, back, leaving, state, cum, entering, rate, igate, lru, dist, branch, rim, params, gates),
            [tall, tall, one, tall, tall, one, tall, tall, tall, self.dist(), tall]
            + [self.short(SUBLANES), self.flat(16), self.gates(2 * self.width)],
            outs,
            [tall, self.short(SUBLANES), self.short(SUBLANES), self.flat(SUBLANES), self.gates(2 * LANES)],
            [
                pltpu.VMEM((self.rows, self.length, 2 * self.width), jnp.bfloat16),
                pltpu.VMEM((self.rows, self.length, self.width), f32),
            ],
            self.blocks,
            2 * self.flops,
        )


def gathered(parts_ref, at):
    return jnp.concatenate([parts_ref[k, at, :] for k in range(parts_ref.shape[0])], axis=1)


def front_kernel(
    parts_ref, gain_ref, input_ref, gate_ref, x_ref, inverse_ref, normed_ref, branch_ref, pre_ref
):
    tokens = x_ref.shape[0]
    piece, tall = (64, min(tokens, 512))

    @pl.when(pl.program_id(0) == 0)
    def _():
        def norm(index, carry):
            at = pl.ds(pl.multiple_of(index * piece, piece), piece)
            low = gathered(parts_ref, at)
            x_ref[at, :] = low
            value = low.astype(jnp.float32)
            inverse = lax.rsqrt(jnp.mean(value * value, axis=1, keepdims=True) + EPS)
            inverse_ref[at, :] = jnp.broadcast_to(inverse, (piece, LANES))
            normed_ref[at, :] = (value * inverse * gain_ref[...]).astype(jnp.bfloat16)
            return carry

        lax.fori_loop(0, tokens // piece, norm, 0)

    def multiply(index, carry):
        at = pl.ds(pl.multiple_of(index * tall, tall), tall)
        normed = normed_ref[at, :]
        branch_ref[at, :] = jnp.dot(normed, input_ref[...], preferred_element_type=jnp.float32)
        pre_ref[at, :] = jnp.dot(normed, gate_ref[...], preferred_element_type=jnp.float32)
        return carry

    lax.fori_loop(0, tokens // tall, multiply, 0)


def front(parts, gain, recur_input, recur_gate):
    count, tokens, width = parts.shape
    model, rec = recur_input.shape
    columns = 4 * LANES
    low, f32 = (jnp.bfloat16, jnp.float32)
    tall = pl.BlockSpec((model, columns), lambda j: (0, j))
    wide = pl.BlockSpec((tokens, columns), lambda j: (0, j))

    def whole(shape):
        return pl.BlockSpec(shape, lambda j: (0,) * len(shape))

    return pl.pallas_call(
        front_kernel,
        name="norm_and_project",
        grid=(rec // columns,),
        in_specs=[whole(parts.shape), whole((1, model)), tall, tall],
        out_specs=[whole((tokens, model)), whole((tokens, LANES)), whole((tokens, model)), wide, wide],
        out_shape=[
            jax.ShapeDtypeStruct((tokens, model), low),
            jax.ShapeDtypeStruct((tokens, LANES), f32),
            jax.ShapeDtypeStruct((tokens, model), low),
            jax.ShapeDtypeStruct((tokens, rec), f32),
            jax.ShapeDtypeStruct((tokens, rec), f32),
        ],
        compiler_params=pltpu.CompilerParams(vmem_limit_bytes=VMEM_BYTES),
        cost_estimate=pl.CostEstimate(
            flops=4 * tokens * model * rec, bytes_accessed=20 * tokens * model, transcendentals=0
        ),
    )(parts, gain[None], recur_input, recur_gate)


def mlp_kernel(
    left_ref,
    parts_ref,
    normed_ref,
    resid_ref,
    gain_ref,
    gate_ref,
    up_ref,
    down_ref,
    gout_ref,
    hidden_ref,
    dgate_ref,
    dup_ref,
    result_ref,
    dres_ref,
    total_ref,
    back_ref,
):
    tokens, model = normed_ref.shape
    chunk = down_ref.shape[0]
    rows = left_ref.shape[0]
    length = tokens // rows
    step = pl.program_id(0)
    slab = 32

    @pl.when(step == 0)
    def _():
        for row in range(rows):

            def collect(index, carry, row=row):
                base = pl.multiple_of(index * slab, slab)
                at = pl.ds(row * length + base, slab)
                low = gathered(parts_ref, at)
                place = base + lax.broadcasted_iota(jnp.int32, low.shape, 0)
                value = jnp.where(place < left_ref[row], low.astype(jnp.float32), 0.0)
                gout_ref[at, :] = value.astype(jnp.bfloat16)
                total_ref[at, :] = resid_ref[at, :]
                back_ref[at, :] = jnp.zeros((slab, model), jnp.float32)
                return carry

            lax.fori_loop(0, length // slab, collect, 0)

    tall = min(tokens, 512)
    wide = 256

    def tile(index, carry):
        at = pl.ds(pl.multiple_of(index * tall, tall), tall)
        for column in range(chunk // wide):
            own = slice(column * wide, (column + 1) * wide)
            gate = jnp.dot(normed_ref[at, :], gate_ref[:, own], preferred_element_type=jnp.float32)
            up = jnp.dot(normed_ref[at, :], up_ref[:, own], preferred_element_type=jnp.float32)
            dhid = lax.dot_general(
                gout_ref[at, :],
                down_ref[own, :],
                (((1,), (1,)), ((), ())),
                preferred_element_type=jnp.float32,
            )
            act, slope = gelu_pair(gate)
            hidden_ref[at, own] = (act * up).astype(jnp.bfloat16)
            dgate_ref[at, own] = (dhid * up * slope).astype(jnp.bfloat16)
            dup_ref[at, own] = (dhid * act).astype(jnp.bfloat16)
        for column in range(model // (2 * wide)):
            own = slice(column * 2 * wide, (column + 1) * 2 * wide)
            total_ref[at, own] += jnp.dot(
                hidden_ref[at, :], down_ref[:, own], preferred_element_type=jnp.float32
            )
            back_ref[at, own] += lax.dot_general(
                dgate_ref[at, :],
                gate_ref[own, :],
                (((1,), (1,)), ((), ())),
                preferred_element_type=jnp.float32,
            ) + lax.dot_general(
                dup_ref[at, :],
                up_ref[own, :],
                (((1,), (1,)), ((), ())),
                preferred_element_type=jnp.float32,
            )
        return carry

    lax.fori_loop(0, tokens // tall, tile, 0)

    @pl.when(step == pl.num_programs(0) - 1)
    def _():
        parts, width = (result_ref.shape[0], result_ref.shape[2])
        small = 16

        def finish(index, carry):
            at = pl.ds(pl.multiple_of(index * small, small), small)
            result = total_ref[at, :].astype(jnp.bfloat16)
            for part in range(parts):
                result_ref[part, at, :] = result[:, part * width : (part + 1) * width]
            resid = resid_ref[at, :]
            inverse = lax.rsqrt(jnp.mean(resid * resid, axis=1, keepdims=True) + EPS)
            normed = resid * inverse
            scaled = back_ref[at, :] * gain_ref[...]
            mean = jnp.mean(scaled * normed, axis=1, keepdims=True)
            dres = gout_ref[at, :].astype(jnp.float32) + inverse * (scaled - normed * mean)
            dres_ref[at, :] = dres.astype(jnp.bfloat16)
            return carry

        lax.fori_loop(0, tokens // small, finish, 0)


def mlp(left, parts, normed, resid, gain, mlp_gate, mlp_up, mlp_down):
    tokens, model = normed.shape
    ffn = mlp_gate.shape[1]
    chunk = 768
    low, f32 = (jnp.bfloat16, jnp.float32)

    def whole(shape):
        return pl.BlockSpec(shape, lambda s: (0,) * len(shape), pipeline_mode=pl.Buffered(1))

    columns = pl.BlockSpec((model, chunk), lambda s: (0, s))
    made = pl.BlockSpec((tokens, chunk), lambda s: (0, s))
    tall = jax.ShapeDtypeStruct((tokens, ffn), low)
    square = jax.ShapeDtypeStruct((tokens, model), low)
    return pl.pallas_call(
        mlp_kernel,
        name="mlp_forward_backward",
        grid=(ffn // chunk,),
        in_specs=[
            pl.BlockSpec(memory_space=pltpu.SMEM),
            whole(parts.shape),
            whole(normed.shape),
            whole(resid.shape),
            whole((1, model)),
            columns,
            columns,
            pl.BlockSpec((chunk, model), lambda s: (s, 0)),
        ],
        out_specs=[
            whole((tokens, model)),
            made,
            made,
            made,
            whole(parts.shape),
            whole((tokens, model)),
        ],
        out_shape=[square, tall, tall, tall, jax.ShapeDtypeStruct(parts.shape, low), square],
        scratch_shapes=[pltpu.VMEM((tokens, model), f32), pltpu.VMEM((tokens, model), f32)],
        compiler_params=pltpu.CompilerParams(vmem_limit_bytes=VMEM_BYTES),
        cost_estimate=pl.CostEstimate(
            flops=12 * tokens * model * ffn,
            bytes_accessed=6 * (model + tokens) * ffn + 14 * tokens * model,
            transcendentals=0,
        ),
    )(left, parts, normed, resid, gain[None], mlp_gate, mlp_up, mlp_down)


def spread_kernel(whole_ref, out_ref):
    out_ref[0] = whole_ref[...]


def spread(whole, count):
    tokens, width = (whole.shape[0], whole.shape[1] // count)
    return pl.pallas_call(
        spread_kernel,
        name="spread_features",
        grid=(count,),
        in_specs=[pl.BlockSpec((tokens, width), lambda j: (0, j))],
        out_specs=pl.BlockSpec((1, tokens, width), lambda j: (j, 0, 0)),
        out_shape=jax.ShapeDtypeStruct((count, tokens, width), whole.dtype),
        cost_estimate=pl.CostEstimate(
            flops=0, bytes_accessed=4 * tokens * whole.shape[1], transcendentals=0
        ),
    )(whole)


CHAN = ("zed", "core")


def features_in(local):
    count = lax.axis_size(CHAN)
    rows, length, width = local.shape
    if width % LANES == 0:
        moved = lax.all_to_all(
            local.reshape(count, rows // count, length, width), CHAN, 0, 0, tiled=True
        )
        return moved.reshape(count, -1, width)
    moved = lax.all_to_all(local, CHAN, split_axis=0, concat_axis=2, tiled=True)
    return moved.reshape(1, -1, count * width)


def features_apart(whole):
    count = lax.axis_size(CHAN)
    if (whole.shape[1] // count) % LANES == 0:
        return spread(whole, count)
    return whole[None]


def features_out(parts, rows):
    blocks, tokens, width = parts.shape
    parts = parts.reshape(blocks, rows, tokens // rows, width)
    if blocks > 1:
        moved = lax.all_to_all(parts, CHAN, 0, 0, tiled=True)
        return moved.reshape(-1, *parts.shape[2:])
    return lax.all_to_all(parts[0], CHAN, split_axis=2, concat_axis=0, tiled=True)


MESH = pl.DeviceIdType.MESH


class Corners:
    def __init__(self, seq, zed):
        self.seq_bits, self.zed_bits = (seq.bit_length() - 1, zed.bit_length() - 1)
        self.count = self.seq_bits + self.zed_bits
        self.dims = (2,) * self.count
        self.low = tuple(range(self.seq_bits))[::-1] + tuple(range(self.seq_bits, self.count))[::-1]
        self.high = tuple(range(self.seq_bits)) + tuple(range(self.seq_bits, self.count))[::-1]

    def place(self, dim):
        if dim < self.seq_bits:
            return ("seq", 2 ** (self.seq_bits - 1 - dim))
        return ("zed", 2 ** (self.count - 1 - dim))

    def bit(self, dim):
        axis, weight = self.place(dim)
        return lax.rem(lax.div(lax.axis_index(axis), weight), 2)

    def partner(self, dim):
        axis, weight = self.place(dim)
        return {axis: lax.axis_index(axis) + weight * (1 - 2 * self.bit(dim))}


def reduce_kernel(corners, orders, *refs):
    streams = len(orders)
    stages = corners.count + 1
    given, outs, rest = (refs[:streams], refs[streams : 2 * streams], refs[2 * streams :])
    owns, rest = (rest[:streams], rest[streams:])
    slots, (send_sem, recv_sem, load_sem) = (rest[:-3], rest[-3:])
    core = lax.axis_index("core")
    partners = [{"core": 1 - core}] + [corners.partner(dim) for dim in range(corners.count)]
    barrier = pltpu.get_barrier_semaphore()
    for partner in partners:
        pl.semaphore_signal(barrier, inc=1, device_id=partner, device_id_type=MESH)
    pl.semaphore_wait(barrier, len(partners))

    def indices(order, stage, last):
        fixed = {dim: corners.bit(dim) for dim in order[: stage - 1]}
        if last is not None:
            fixed[order[stage - 1]] = last
        return tuple(fixed.get(dim, slice(None)) for dim in range(corners.count))

    def copy(stream, stage):
        order = orders[stream]
        if stage == 0:
            source = given[stream].at[(slice(None),) * corners.count + (1 - core,)]
            target = {"core": 1 - core}
        else:
            dim = order[stage - 1]
            source = owns[stream].at[indices(order, stage, 1 - corners.bit(dim))]
            target = corners.partner(dim)
        return pltpu.make_async_remote_copy(
            src_ref=source,
            dst_ref=slots[stream * stages + stage],
            send_sem=send_sem.at[stream, stage],
            recv_sem=recv_sem.at[stream, stage],
            device_id=target,
            device_id_type=MESH,
        )

    def load(stream):
        return pltpu.make_async_copy(
            given[stream].at[(slice(None),) * corners.count + (core,)],
            owns[stream],
            load_sem.at[stream],
        )

    for stream in range(streams):
        copy(stream, 0).start()
        load(stream).start()
    for stage in range(stages):
        for stream in range(streams):
            order = orders[stream]
            own, slot = (owns[stream], slots[stream * stages + stage])
            if stage == 0:
                load(stream).wait()
            copy(stream, stage).wait_recv()
            left = [dim for dim in range(corners.count) if dim not in order[:stage]]
            fixed = {dim: corners.bit(dim) for dim in order[:stage]}
            if left:

                def add(index, carry, own=own, slot=slot, left=left, fixed=fixed):
                    part = {
                        dim: lax.rem(lax.div(index, 2 ** (len(left) - 1 - place)), 2)
                        for place, dim in enumerate(left)
                    }
                    mine = tuple({**fixed, **part}[dim] for dim in range(corners.count))
                    come = tuple(part[dim] for dim in left)
                    total = own[mine].astype(jnp.float32) + slot[come].astype(jnp.float32)
                    own[mine] = total.astype(own.dtype)
                    return carry

                lax.fori_loop(0, 2 ** len(left), add, 0)
                copy(stream, stage + 1).start()
            else:
                mine = tuple(fixed[dim] for dim in range(corners.count))
                outs[stream][...] = own[mine].astype(jnp.float32) + slot[...].astype(jnp.float32)
    for stage in range(stages):
        for stream in range(streams):
            copy(stream, stage).wait_send()


def reduce_streams(gradients, highs):
    corners = Corners(lax.axis_size("seq"), lax.axis_size("zed"))
    devices = 2 ** (corners.count + 1)
    orders = [corners.high if high else corners.low for high in highs]
    blocks = [
        g.reshape(corners.dims + (2, g.shape[0] // devices, g.shape[1])) for g in gradients
    ]
    outs = [jax.ShapeDtypeStruct(b.shape[-2:], jnp.float32) for b in blocks]
    owns = [pltpu.VMEM(corners.dims + b.shape[-2:], b.dtype) for b in blocks]
    slots = [
        pltpu.VMEM((2,) * min(corners.count, corners.count - stage) + b.shape[-2:], b.dtype)
        for b in blocks
        for stage in range(corners.count + 1)
    ]
    grid = (len(blocks), corners.count + 1)
    moved = sum(math.prod(g.shape) * g.dtype.itemsize for g in gradients)
    return pl.pallas_call(
        functools.partial(reduce_kernel, corners, orders),
        name="reduce_streams",
        in_specs=[pl.BlockSpec(memory_space=pl.ANY)] * len(blocks),
        out_specs=[pl.BlockSpec(memory_space=pltpu.VMEM)] * len(blocks),
        out_shape=outs,
        scratch_shapes=owns
        + slots
        + [
            pltpu.SemaphoreType.DMA(grid),
            pltpu.SemaphoreType.DMA(grid),
            pltpu.SemaphoreType.DMA((len(blocks),)),
        ],
        compiler_params=pltpu.CompilerParams(
            collective_id=1, has_side_effects=True, vmem_limit_bytes=VMEM_BYTES
        ),
        cost_estimate=pl.CostEstimate(flops=0, bytes_accessed=20 * moved, transcendentals=0),
    )(*blocks)


def grads_kernel(
    normed_ref,
    dgate_ref,
    dup_ref,
    hidden_ref,
    gout_ref,
    mixed_ref,
    dres_ref,
    out_ref,
    turned_ref,
    made_wide,
    made_down,
    made_out,
    come_wide,
    come_down,
    come_out,
    send_sem,
    recv_sem,
    store_sem,
):
    step = pl.program_id(0)
    core = lax.axis_index("core")
    other = {"core": 1 - core}
    wide_rows, down_rows, out_rows = (made_wide.shape[3], made_down.shape[3], made_out.shape[3])
    wides, downs, lasts = (come_wide.shape[0], come_down.shape[0], come_out.shape[0])
    total = wides + downs + lasts
    down_at, out_at = (wides * wide_rows, wides * wide_rows + down_rows)

    def exchange(made, come, index, slot):
        return pltpu.make_async_remote_copy(
            src_ref=made.at[lax.rem(index, 2), 1 - core],
            dst_ref=come.at[index],
            send_sem=send_sem.at[slot],
            recv_sem=recv_sem.at[slot],
            device_id=other,
            device_id_type=MESH,
        )

    def store_wide(index):
        return pltpu.make_async_copy(
            come_wide.at[index],
            out_ref.at[:, pl.ds(pl.multiple_of(index * wide_rows, wide_rows), wide_rows)],
            store_sem.at[index],
        )

    def store_down(index):
        chips = come_down.shape[1]
        return pltpu.make_async_copy(
            come_down.at[index],
            out_ref.at[pl.ds(index * chips, chips), pl.ds(down_at, down_rows)],
            store_sem.at[index + wides],
        )

    def store_out(index):
        chips = come_out.shape[1]
        return pltpu.make_async_copy(
            come_out.at[index],
            out_ref.at[pl.ds(index * chips, chips), pl.ds(out_at, out_rows)],
            store_sem.at[index + wides + downs],
        )

    @pl.when(step == 0)
    def _():
        barrier = pltpu.get_barrier_semaphore()
        pl.semaphore_signal(barrier, inc=1, device_id=other, device_id_type=MESH)
        pl.semaphore_wait(barrier, 1)
        turned_ref[...] = normed_ref[...].T

    def product_wide(source, index):
        made = made_wide.at[lax.rem(index, 2)]
        chips, rows = (made.shape[1], made.shape[2])
        tile = 256

        def column(place, carry):
            at = pl.ds(pl.multiple_of(place * tile, tile), tile)
            part = jnp.dot(turned_ref[...], source[:, at], preferred_element_type=jnp.float32)
            part = part.astype(jnp.bfloat16).reshape(chips, 2, rows, tile)
            made[0, :, :, at] = part[:, 0]
            made[1, :, :, at] = part[:, 1]
            return carry

        lax.fori_loop(0, source.shape[1] // tile, column, 0)

    def product_tall(left, right, made_all, index):
        made = made_all.at[lax.rem(index, 2)]
        chips, rows = (made.shape[1], made.shape[2])
        tile = 256

        def column(place, carry):
            at = pl.ds(pl.multiple_of(place * tile, tile), tile)
            part = lax.dot_general(
                left[...], right[:, at], (((0,), (0,)), ((), ())), preferred_element_type=jnp.float32
            )
            part = part.astype(jnp.bfloat16).reshape(chips, 2, rows, tile)
            made[0, :, :, at] = part[:, 0]
            made[1, :, :, at] = part[:, 1]
            return carry

        lax.fori_loop(0, right.shape[1] // tile, column, 0)

    half = wides // 2

    @pl.when(step < half)
    def _():
        product_wide(dgate_ref, step)

    @pl.when((step >= half) & (step < wides))
    def _():
        product_wide(dup_ref, step)

    @pl.when(step < wides)
    def _():
        exchange(made_wide, come_wide, step, step).start()

    @pl.when((step >= wides) & (step < wides + downs))
    def _():
        product_tall(hidden_ref, gout_ref, made_down, step - wides)
        exchange(made_down, come_down, step - wides, step).start()

    @pl.when((step >= wides + downs) & (step < total))
    def _():
        product_tall(mixed_ref, dres_ref, made_out, step - wides - downs)
        exchange(made_out, come_out, step - wides - downs, step).start()

    def finish(made, come, index, slot, store):
        exchange(made, come, index, slot).wait()
        mine = made.at[lax.rem(index, 2), core]
        arrived = come.at[index]

        def add(chip, carry):
            both = mine[chip].astype(jnp.float32) + arrived[chip].astype(jnp.float32)
            arrived[chip] = both.astype(jnp.bfloat16)
            return carry

        lax.fori_loop(0, come.shape[1], add, 0)
        store(index).start()

    before = step - 1

    @pl.when((before >= 0) & (before < wides))
    def _():
        finish(made_wide, come_wide, before, before, store_wide)

    @pl.when((before >= wides) & (before < wides + downs))
    def _():
        finish(made_down, come_down, before - wides, before, store_down)

    @pl.when(before >= wides + downs)
    def _():
        finish(made_out, come_out, before - wides - downs, before, store_out)

    @pl.when(step == total)
    def _():
        for index in range(wides):
            store_wide(index).wait()
        for index in range(downs):
            store_down(index).wait()
        for index in range(lasts):
            store_out(index).wait()


def block_gradients(normed, dgate, dup, hidden, gout, mixed, dres):
    tokens, model = normed.shape
    ffn, rec = (hidden.shape[1], mixed.shape[1])
    chips = lax.axis_size("seq") * lax.axis_size("zed")
    devices = 2 * chips
    wide_rows, down_rows, out_rows = (model // devices, ffn // devices, rec // devices)
    chunk = 768
    wides, downs, lasts = (2 * ffn // model, ffn // chunk, rec // chunk)
    half = wides // 2
    down_chips, out_chips = (chunk // (2 * down_rows), chunk // (2 * out_rows))
    rows = wides * wide_rows + down_rows + out_rows
    low = jnp.bfloat16

    def whole(array):
        return pl.BlockSpec(array.shape, lambda s: (0, 0), pipeline_mode=pl.Buffered(1))

    def part(columns, first, count):
        return pl.BlockSpec((tokens, columns), lambda s: (0, jnp.clip(s - first, 0, count - 1)))

    total = wides + downs + lasts
    flops = 2 * tokens * model * (3 * ffn + rec)
    arrays = (normed, dgate, dup, hidden, gout, mixed, dres)
    moved = sum(math.prod(a.shape) * 2 for a in arrays) + chips * rows * model * 2
    return pl.pallas_call(
        grads_kernel,
        name="block_gradients",
        grid=(total + 1,),
        in_specs=[
            whole(normed),
            part(model, 0, half),
            part(model, half, half),
            part(chunk, wides, downs),
            whole(gout),
            part(chunk, wides + downs, lasts),
            whole(dres),
        ],
        out_specs=pl.BlockSpec(memory_space=pl.ANY),
        out_shape=jax.ShapeDtypeStruct((chips, rows, model), low),
        scratch_shapes=[
            pltpu.VMEM((model, tokens), low),
            pltpu.VMEM((2, 2, chips, wide_rows, model), low),
            pltpu.VMEM((2, 2, down_chips, down_rows, model), low),
            pltpu.VMEM((2, 2, out_chips, out_rows, model), low),
            pltpu.VMEM((wides, chips, wide_rows, model), low),
            pltpu.VMEM((downs, down_chips, down_rows, model), low),
            pltpu.VMEM((lasts, out_chips, out_rows, model), low),
            pltpu.SemaphoreType.DMA((total,)),
            pltpu.SemaphoreType.DMA((total,)),
            pltpu.SemaphoreType.DMA((total,)),
        ],
        compiler_params=pltpu.CompilerParams(
            collective_id=2, has_side_effects=True, vmem_limit_bytes=VMEM_BYTES
        ),
        cost_estimate=pl.CostEstimate(flops=flops, bytes_accessed=moved, transcendentals=0),
    )(*arrays)


def carried(factor, value, axis, backward):
    count, mine = (lax.axis_size(axis), lax.axis_index(axis))
    pieces = lax.all_gather(jnp.stack([factor, value]), axis)
    order = range(count - 1, 0, -1) if backward else range(count - 1)
    total = jnp.zeros_like(value)
    for place in order:
        longer = pieces[place, 0] * total + pieces[place, 1]
        total = jnp.where(place > mine if backward else place < mine, longer, total)
    return total


def passed_along(value, axis, steps):
    count = lax.axis_size(axis)
    leading, last = (max(0, -steps), min(count, count - steps))
    return lax.ppermute(value, axis, [(source, source + steps) for source in range(leading, last)])


def weight_grad(left, right):
    return lax.dot_general(
        left, right, (((0,), (0,)), ((), ())), preferred_element_type=jnp.float32
    ).astype(jnp.bfloat16)


def back_dot(left, right):
    return lax.dot_general(
        left, right, (((1,), (1,)), ((), ())), preferred_element_type=jnp.float32
    )


def fwd_dot(left, right):
    return jnp.dot(left, right, preferred_element_type=jnp.float32)


def gelu_fn(value):
    return jax.nn.gelu(value, approximate=True)


def norm_back(grad_norm, normed, inverse, gain):
    scaled = grad_norm * gain
    mean_term = jnp.mean(scaled * normed, axis=1, keepdims=True)
    return inverse * (scaled - normed * mean_term)


def scattered(gradient):
    return lax.psum_scatter(
        gradient, ("seq", "zed", "core"), scatter_dimension=0, tiled=True
    ).astype(jnp.float32)


def body(
    tokens,
    cotangent,
    doc_starts,
    lengths,
    norm1_gain,
    recur_input,
    recur_gate,
    conv_kernel,
    conv_bias,
    lru_gates,
    lru_bias,
    lru_decay,
    recur_out,
    norm2_gain,
    mlp_gate,
    mlp_up,
    mlp_down,
):
    count = lax.axis_size(CHAN)
    row_count, block_len = (tokens.shape[0] // count, tokens.shape[1])
    model_dim = tokens.shape[2] * count
    tok_count = row_count * block_len
    rec_width = recur_input.shape[1]
    ffn_width = mlp_gate.shape[1]
    head_count = H
    head_size = rec_width // head_count
    tap_count = conv_kernel.shape[0]
    rim_size = tap_count - 1
    seq_index = lax.axis_index("seq")
    position = seq_index * block_len + jnp.arange(block_len, dtype=jnp.int32)
    bounds = jnp.concatenate([doc_starts, lengths[:, None]], axis=1)
    is_before = bounds[:, None, :] <= position[None, :, None]
    seg_start = jnp.max(jnp.where(is_before, bounds[:, None, :], 0), axis=2)
    low_x, inverse_lanes, normed_low, branch_pre, gate_pre = front(
        features_in(tokens), norm1_gain, recur_input, recur_gate
    )
    gate_act = gelu_fn(gate_pre)
    branch_rows = branch_pre.reshape(row_count, block_len, rec_width)
    core = Recurrence(row_count, block_len, rec_width, head_size)
    prev_rim = passed_along(
        branch_rows[:, block_len - rim_size :, :].astype(jnp.bfloat16), "seq", 1
    ).astype(jnp.float32)
    rim = jnp.pad(prev_rim, ((0, 0), (SUBLANES - rim_size, 0), (0, 0)))
    dist = jnp.broadcast_to(
        (position[None, :] - seg_start)[:, :, None], (row_count, block_len, LANES)
    )
    soft_decay = jax.nn.softplus(-lru_decay)
    params = jnp.concatenate(
        [
            conv_kernel,
            conv_bias[None],
            lru_bias,
            (-8.0 * soft_decay)[None],
            jnp.zeros((SUBLANES, rec_width), jnp.float32),
        ],
        axis=0,
    )
    wide_gates = core.widen(lru_gates)
    lru_in, rate_gate, input_gate, local_state, cum_coef = core.forward(
        branch_rows, rim, dist, params, wide_gates
    )
    cotangent, local_state = lax.optimization_barrier((features_in(cotangent), local_state))
    carry_in = carried(cum_coef[:, -1, :], local_state[:, -1, :], "seq", False)
    entering = carry_in[:, None, :]
    state_rows = local_state + cum_coef * entering
    state_flat = state_rows.reshape(tok_count, rec_width)
    mixed_low = (state_flat * gate_act).astype(jnp.bfloat16)
    resid_one = low_x.astype(jnp.float32) + fwd_dot(mixed_low, recur_out)
    inv_two = lax.rsqrt(jnp.mean(resid_one * resid_one, axis=1, keepdims=True) + EPS)
    normed_two = resid_one * inv_two
    normed_low2 = (normed_two * norm2_gain).astype(jnp.bfloat16)
    grad_low, hidden_low, mgate_low, mup_low, result_parts, resid_low = mlp(
        lengths - seq_index * block_len,
        cotangent,
        normed_low2,
        resid_one,
        norm2_gain,
        mlp_gate,
        mlp_up,
        mlp_down,
    )
    output = features_out(result_parts, row_count)
    devices = lax.axis_size(("seq", "zed", "core"))
    own_rows = model_dim // devices
    tiled = own_rows % (2 * SUBLANES) == 0 and ffn_width % model_dim == 0
    if tiled:
        merged = block_gradients(
            normed_low2, mgate_low, mup_low, hidden_low, grad_low, mixed_low, resid_low
        )
        merged, resid_low = lax.optimization_barrier((merged, resid_low))
        merged = lax.psum_scatter(merged, "seq", scatter_dimension=0, tiled=True)
    grad_mixed = back_dot(resid_low, recur_out)
    gate_low, back_local, back_cum, first_term = core.adjoint(
        grad_mixed.reshape(row_count, block_len, rec_width),
        gate_pre.reshape(row_count, block_len, rec_width),
        local_state,
        cum_coef,
        entering,
        rate_gate,
        dist,
        params,
    )
    gate_low = gate_low.reshape(tok_count, rec_width)
    output, back_local = lax.optimization_barrier((output, back_local))
    carry_out = carried(cum_coef[:, -1, :], first_term[:, 0, :], "seq", True)
    branch_local, tail, lead, channel_sums, gate_sums = core.backward(
        back_local,
        back_cum,
        carry_out[:, None, :],
        local_state,
        cum_coef,
        entering,
        rate_gate,
        input_gate,
        lru_in,
        dist,
        branch_rows,
        rim,
        params,
        wide_gates,
    )
    spare = jnp.swapaxes(channel_sums, 0, 1)
    small = jnp.concatenate(
        [gate_sums[:, :head_size], spare, gate_sums[:, head_size + SUBLANES :]], axis=1
    )
    from_next = passed_along(
        lead[:, SUBLANES - rim_size :, :].astype(jnp.bfloat16), "seq", -1
    )
    ending = tail + jnp.pad(from_next.astype(jnp.float32), ((0, 0), (SUBLANES - rim_size, 0), (0, 0)))
    branch_low = lax.dynamic_update_slice(
        branch_local, ending.astype(jnp.bfloat16), (0, block_len - SUBLANES, 0)
    ).reshape(tok_count, rec_width)
    grad_rin = weight_grad(normed_low, branch_low)
    grad_rgate = weight_grad(normed_low, gate_low)
    grad_norm1 = back_dot(branch_low, recur_input) + back_dot(gate_low, recur_gate)
    inv_one = inverse_lanes[:, :1]
    normed_one = low_x.astype(jnp.float32) * inv_one
    input_part = norm_back(grad_norm1, normed_one, inv_one, norm1_gain)
    grad_x = (resid_low.astype(jnp.float32) + input_part).astype(jnp.bfloat16)
    if tiled:
        merged, grad_x = lax.optimization_barrier((merged, grad_x))
        merged = lax.psum_scatter(merged, "zed", scatter_dimension=0, tiled=True)
    grad_tokens = features_out(features_apart(grad_x), row_count)
    if tiled:
        sum_rgate, sum_rin, own_small = reduce_streams(
            (grad_rgate, grad_rin, small.astype(jnp.bfloat16)), (False, True, False)
        )
        own = merged[0].astype(jnp.float32)
        span = ffn_width // model_dim * own_rows

        def unfolded(part):
            return jnp.swapaxes(part.reshape(-1, own_rows, model_dim), 0, 1).reshape(own_rows, -1)

        sum_mgate, sum_mup = (unfolded(own[:span]), unfolded(own[span : 2 * span]))
        sum_down = own[2 * span : 2 * span + ffn_width // devices]
        sum_rout = own[2 * span + ffn_width // devices :]
    else:
        sum_mgate, sum_mup, sum_down, sum_rout, sum_rgate, sum_rin = (
            scattered(weight_grad(left, right))
            for left, right in (
                (normed_low2, mgate_low),
                (normed_low2, mup_low),
                (hidden_low, grad_low),
                (mixed_low, resid_low),
                (normed_low, gate_low),
                (normed_low, branch_low),
            )
        )
        own_small = scattered(small)
    sum_lgates = jnp.concatenate(
        [own_small[:, :head_size], own_small[:, LANES : LANES + head_size]], axis=1
    )
    own_sums = jnp.swapaxes(own_small[:, head_size : head_size + SUBLANES], 0, 1)
    device = lax.axis_index(("seq", "zed", "core"))

    def mine(array, size, axis=0):
        return lax.dynamic_slice_in_dim(array, device * size, size, axis)

    def weighed(weight, gradient):
        return jnp.sum(mine(weight, own_rows).astype(jnp.float32) * gradient, axis=1)

    sum_gain1 = (weighed(recur_input, sum_rin) + weighed(recur_gate, sum_rgate)) / mine(
        norm1_gain, own_rows
    )
    sum_gain2 = (weighed(mlp_gate, sum_mgate) + weighed(mlp_up, sum_mup)) / mine(
        norm2_gain, own_rows
    )
    own_channels = own_sums.shape[1]
    sum_decay = 8.0 * jax.nn.sigmoid(-mine(lru_decay, own_channels)) * own_sums[7]
    return (
        output,
        grad_tokens,
        sum_gain1,
        sum_rin,
        sum_rgate,
        own_sums[:4],
        own_sums[4],
        sum_lgates,
        own_sums[5:7],
        sum_decay,
        sum_rout,
        sum_gain2,
        sum_mgate,
        sum_mup,
        sum_down,
    )


def solution(mesh):
    seq, chan = (mesh.shape["seq"], mesh.shape["chan"])
    chips = jax.sharding.Mesh(mesh.devices.reshape(seq, chan // 2, 2), ("seq", "zed", "core"))
    chan = ("zed", "core")
    every = ("seq", "zed", "core")
    activations = P(None, "seq", chan)
    rows, columns, vector = (P(every, None), P(None, every), P(every))
    return jax.shard_map(
        body,
        mesh=chips,
        in_specs=(activations, activations, P(chan, None), P(chan)) + (P(),) * 13,
        out_specs=(
            activations,
            activations,
            vector,
            rows,
            rows,
            columns,
            vector,
            rows,
            columns,
            vector,
            rows,
            vector,
            rows,
            rows,
            rows,
        ),
        check_vma=False,
    )
```

```python
import functools
import math

import jax
import jax.numpy as jnp
from jax import lax
from jax.experimental import pallas as pl
from jax.experimental.pallas import tpu as pltpu
from jax.sharding import PartitionSpec as P

H = 16


EPS = 1e-06
ROOT_FLOOR = 1e-06
LANES = 128
SUBLANES = 8
STEP = 16
VMEM_BYTES = 56 * 1024 * 1024


def sigmoid(value):
    return 0.5 * jnp.tanh(0.5 * value) + 0.5


GELU_C = 0.7978845608
GELU_A = 0.044715


def gelu_pair(value):
    square = value * value
    inner = jnp.tanh(value * (GELU_C + (GELU_C * GELU_A) * square))
    half = 0.5 + 0.5 * inner
    slope = GELU_C + (3.0 * GELU_C * GELU_A) * square
    return (value * half, half + 0.5 * value * (1.0 - inner * inner) * slope)


def root_argument(log_decay, decay):
    y = 2.0 * log_decay
    series = 1.0 + y * (1.0 / 7.0)
    for divisor in (6.0, 5.0, 4.0, 3.0, 2.0):
        series = 1.0 + (y * (1.0 / divisor)) * series
    return jnp.where(y > -0.25, -y * series, 1.0 - decay * decay)


def across(column, width):
    return jnp.concatenate([column] * (width // LANES), axis=1)


def forward_kernel(
    branch_ref,
    rim_ref,
    dist_ref,
    par_ref,
    gates_ref,
    lru_ref,
    rate_ref,
    igate_ref,
    state_ref,
    cum_ref,
    both_ref,
):
    rows, length, width = branch_ref.shape
    taps = [par_ref[k : k + 1, :] for k in range(4)]
    conv_bias, rate_bias, input_bias, soft = (par_ref[k : k + 1, :] for k in range(4, 8))
    place = lax.broadcasted_iota(jnp.int32, (SUBLANES, width), 0)

    for row in range(rows):

        def conv_step(index, before, row=row):
            base = pl.multiple_of(index * STEP, STEP)
            pieces = []
            for half in range(STEP // SUBLANES):
                at = pl.ds(base + half * SUBLANES, SUBLANES)
                here = branch_ref[row, at, :]
                dist = across(dist_ref[row, at, :], width)
                total = conv_bias + taps[0] * here
                for k in range(1, 4):
                    shifted = pltpu.roll(jnp.where(place < SUBLANES - k, here, before), k, 0)
                    total = total + taps[k] * jnp.where(dist >= k, shifted, 0.0)
                pieces.append(total)
                before = here
            lru_ref[row, pl.ds(base, STEP), :] = jnp.concatenate(pieces, axis=0).astype(jnp.bfloat16)
            return before

        lax.fori_loop(0, length // STEP, conv_step, rim_ref[row])

        piece = min(length, 256)

        def dot_step(index, carry, row=row):
            at = pl.ds(pl.multiple_of(index * piece, piece), piece)
            both_ref[row, at, :] = jnp.dot(
                lru_ref[row, at, :], gates_ref[...], preferred_element_type=jnp.float32
            )
            return carry

        lax.fori_loop(0, length // piece, dot_step, 0)

    def scan_step(index, carry):
        base = pl.multiple_of(index * STEP, STEP)
        later = []
        for row in range(rows):
            run_cum, run_state = carry[row]
            lru_both = lru_ref[row, pl.ds(base, STEP), :].astype(jnp.float32)
            for half in range(STEP // SUBLANES):
                at = pl.ds(base + half * SUBLANES, SUBLANES)
                lru = lru_both[half * SUBLANES : (half + 1) * SUBLANES]
                start = across(dist_ref[row, at, :], width) == 0
                rate = sigmoid(both_ref[row, at, :width] + rate_bias)
                igate = sigmoid(both_ref[row, at, width:] + input_bias)
                log_decay = rate * soft
                decay = jnp.exp(log_decay)
                arg = jnp.maximum(root_argument(log_decay, decay), ROOT_FLOOR)
                root = arg * lax.rsqrt(arg)
                cum = jnp.where(start, 0.0, decay)
                value = jnp.where(start, 1.0, root) * igate * lru
                rate_ref[row, at, :] = rate
                igate_ref[row, at, :] = igate
                for shift in (1, 2, 4):
                    live = place >= shift
                    value = value + cum * jnp.where(live, pltpu.roll(value, shift, 0), 0.0)
                    cum = cum * jnp.where(live, pltpu.roll(cum, shift, 0), 1.0)
                value = value + cum * run_state
                cum = cum * run_cum
                state_ref[row, at, :] = value
                cum_ref[row, at, :] = cum
                run_state = value[SUBLANES - 1 :, :]
                run_cum = cum[SUBLANES - 1 :, :]
            later.append((run_cum, run_state))
        return tuple(later)

    one, zero = (jnp.ones((1, width), jnp.float32), jnp.zeros((1, width), jnp.float32))
    lax.fori_loop(0, length // STEP, scan_step, tuple((one, zero) for _ in range(rows)))


def adjoint_kernel(
    dmix_ref,
    pre_ref,
    state_ref,
    cum_ref,
    carry_ref,
    rate_ref,
    dist_ref,
    par_ref,
    dgate_ref,
    local_ref,
    back_ref,
    first_ref,
):
    rows, length, width = dmix_ref.shape
    soft = par_ref[7:8, :]
    place = lax.broadcasted_iota(jnp.int32, (SUBLANES, width), 0)
    last = length // STEP - 1

    def step(index, carry):
        base = pl.multiple_of((last - index) * STEP, STEP)
        later = []
        for row in range(rows):
            run_cum, run_back = carry[row]
            entering = carry_ref[row]
            pieces = []
            for half in reversed(range(STEP // SUBLANES)):
                at = pl.ds(base + half * SUBLANES, SUBLANES)
                start = across(dist_ref[row, at, :], width) == 0
                state = state_ref[row, at, :] + cum_ref[row, at, :] * entering
                act, slope = gelu_pair(pre_ref[row, at, :])
                dmix = dmix_ref[row, at, :]
                pieces.append(dmix * state * slope)
                dstate = dmix * act
                coef = jnp.where(start, 0.0, jnp.exp(rate_ref[row, at, :] * soft))
                value = coef * dstate
                for shift in (1, 2, 4):
                    live = place < SUBLANES - shift
                    turn = SUBLANES - shift
                    value = value + coef * jnp.where(live, pltpu.roll(value, turn, 0), 0.0)
                    coef = coef * jnp.where(live, pltpu.roll(coef, turn, 0), 1.0)
                value = value + coef * run_back
                coef = coef * run_cum
                inside = place < SUBLANES - 1
                local_ref[row, at, :] = dstate + jnp.where(
                    inside, pltpu.roll(value, SUBLANES - 1, 0), run_back
                )
                back_ref[row, at, :] = jnp.where(inside, pltpu.roll(coef, SUBLANES - 1, 0), run_cum)
                run_back = value[:1, :]
                run_cum = coef[:1, :]
            dgate_ref[row, pl.ds(base, STEP), :] = jnp.concatenate(pieces[::-1], axis=0).astype(
                jnp.bfloat16
            )
            later.append((run_cum, run_back))
        return tuple(later)

    one, zero = (jnp.ones((1, width), jnp.float32), jnp.zeros((1, width), jnp.float32))
    done = lax.fori_loop(0, last + 1, step, tuple((one, zero) for _ in range(rows)))
    for row in range(rows):
        first_ref[row] = done[row][1]


def backward_kernel(
    head_size,
    local_ref,
    back_ref,
    out_ref,
    state_ref,
    cum_ref,
    in_ref,
    rate_ref,
    igate_ref,
    lru_ref,
    dist_ref,
    branch_ref,
    rim_ref,
    par_ref,
    gates_ref,
    dbranch_ref,
    tail_ref,
    head_ref,
    dgates_ref,
    both_ref,
    dconv_ref,
    sums_ref,
):
    rows, length, width = local_ref.shape
    taps = [par_ref[k : k + 1, :] for k in range(4)]
    soft = par_ref[7:8, :]
    place = lax.broadcasted_iota(jnp.int32, (SUBLANES, width), 0)
    zeros = jnp.zeros((SUBLANES, width), jnp.float32)

    def gate_step(index, carry):
        sums, earlier = carry
        decay_sum, rate_sum, input_sum = sums
        base = pl.multiple_of(index * STEP, STEP)
        later = []
        for row in range(rows):
            before = earlier[row]
            entering = in_ref[row]
            leaving = out_ref[row]
            lru_both = lru_ref[row, pl.ds(base, STEP), :].astype(jnp.float32)
            drates, dinputs = ([], [])
            for half in range(STEP // SUBLANES):
                at = pl.ds(base + half * SUBLANES, SUBLANES)
                lru = lru_both[half * SUBLANES : (half + 1) * SUBLANES]
                start = across(dist_ref[row, at, :], width) == 0
                adjoint = local_ref[row, at, :] + back_ref[row, at, :] * leaving
                state = state_ref[row, at, :] + cum_ref[row, at, :] * entering
                previous = jnp.where(place < 1, before, pltpu.roll(state, 1, 0))
                before = state[SUBLANES - 1 :, :]
                rate = rate_ref[row, at, :]
                igate = igate_ref[row, at, :]
                log_decay = rate * soft
                decay = jnp.exp(log_decay)
                arg = root_argument(log_decay, decay)
                above = arg > ROOT_FLOOR
                arg = jnp.maximum(arg, ROOT_FLOOR)
                inverse = lax.rsqrt(arg)
                scale = jnp.where(start, 1.0, arg * inverse)
                gated = adjoint * igate
                dscale = gated * lru
                pull = jnp.where(above, dscale * decay * decay * inverse, 0.0)
                dlog = jnp.where(start, 0.0, adjoint * previous * decay - pull)
                dig = adjoint * scale * lru
                weighted = dlog * rate
                decay_sum = decay_sum + weighted
                drates.append(weighted * soft * (1.0 - rate))
                dinputs.append(dig * igate * (1.0 - igate))
                dconv_ref[row, at, :] = gated * scale
            drate = jnp.concatenate(drates, axis=0).astype(jnp.bfloat16)
            dinput = jnp.concatenate(dinputs, axis=0).astype(jnp.bfloat16)
            both_ref[row, pl.ds(base, STEP), :width] = drate
            both_ref[row, pl.ds(base, STEP), width:] = dinput
            drate = drate.astype(jnp.float32)
            dinput = dinput.astype(jnp.float32)
            rate_sum = rate_sum + (drate[:SUBLANES] + drate[SUBLANES:])
            input_sum = input_sum + (dinput[:SUBLANES] + dinput[SUBLANES:])
            later.append(before)
        return ((decay_sum, rate_sum, input_sum), tuple(later))

    sums, _ = lax.fori_loop(
        0,
        length // STEP,
        gate_step,
        ((zeros, zeros, zeros), tuple(in_ref[row] for row in range(rows))),
    )
    for slot, total in zip((5, 6, 7), (sums[1], sums[2], sums[0])):
        sums_ref[slot : slot + 1, :] = jnp.sum(total, axis=0, keepdims=True)

    piece = min(length, 256)
    wide = None
    for row in range(rows):

        def dot_step(index, carry, row=row):
            at = pl.ds(pl.multiple_of(index * piece, piece), piece)
            dconv_ref[row, at, :] += lax.dot_general(
                both_ref[row, at, :],
                gates_ref[...],
                (((1,), (1,)), ((), ())),
                preferred_element_type=jnp.float32,
            )
            return carry

        lax.fori_loop(0, length // piece, dot_step, 0)
        part = lax.dot_general(
            lru_ref[row], both_ref[row], (((0,), (0,)), ((), ())), preferred_element_type=jnp.float32
        )
        wide = part if wide is None else wide + part
    row_head = lax.broadcasted_iota(jnp.int32, (width, width), 0) // head_size
    col_head = lax.broadcasted_iota(jnp.int32, (width, width), 1) // head_size
    own = row_head == col_head
    folds = []
    for part in range(2):
        kept = jnp.where(own, wide[:, part * width : (part + 1) * width], 0.0)
        folded = kept
        for other in range(1, width // head_size):
            folded = folded + pltpu.roll(kept, width - other * head_size, 1)
        folds.append(folded[:, :LANES])

    def conv_step(index, carry):
        sums, following = carry
        sums = list(sums)
        base = pl.multiple_of((length // STEP - 1 - index) * STEP, STEP)
        later = []
        for row in range(rows):
            after = following[row]
            pieces = []
            for half in reversed(range(STEP // SUBLANES)):
                at = pl.ds(base + half * SUBLANES, SUBLANES)
                dist = across(dist_ref[row, at, :], width)
                branch = branch_ref[row, at, :]
                here = dconv_ref[row, at, :]
                total = taps[0] * here
                sums[0] = sums[0] + here * branch
                sums[4] = sums[4] + here
                masked = tuple(jnp.where(dist >= k, here, 0.0) for k in range(1, 4))
                for k in range(1, 4):
                    moved = pltpu.roll(
                        jnp.where(place >= k, masked[k - 1], after[k - 1]), SUBLANES - k, 0
                    )
                    total = total + taps[k] * moved
                    sums[k] = sums[k] + branch * moved
                after = masked
                pieces.append(total)
            whole = jnp.concatenate(pieces[::-1], axis=0)
            dbranch_ref[row, pl.ds(base, STEP), :] = whole.astype(jnp.bfloat16)
            later.append(after)

            @pl.when(index == 0)
            def _(row=row, whole=whole):
                tail_ref[row] = whole[STEP - SUBLANES :]

        return (tuple(sums), tuple(later))

    sums, firsts = lax.fori_loop(
        0,
        length // STEP,
        conv_step,
        ((zeros,) * 5, tuple((zeros,) * 3 for _ in range(rows))),
    )
    sums = list(sums)
    for row in range(rows):
        total = zeros
        rim = rim_ref[row]
        for k in range(1, 4):
            moved = pltpu.roll(jnp.where(place >= k, 0.0, firsts[row][k - 1]), SUBLANES - k, 0)
            total = total + taps[k] * moved
            sums[k] = sums[k] + rim * moved
        head_ref[row] = total
    for slot in range(5):
        sums_ref[slot : slot + 1, :] = jnp.sum(sums[slot], axis=0, keepdims=True)
    above = jnp.zeros((head_size, width), jnp.float32)
    below = jnp.zeros((LANES - head_size - SUBLANES, width), jnp.float32)
    turned = jnp.concatenate([above, sums_ref[...], below], axis=0).T
    lane = lax.broadcasted_iota(jnp.int32, (width, LANES), 1)
    dgates_ref[:, :LANES] = jnp.where(lane < head_size, folds[0], turned).astype(dgates_ref.dtype)
    dgates_ref[:, LANES:] = folds[1].astype(dgates_ref.dtype)


def channel_call(kernel, name, arrays, specs, outs, out_specs, scratch, blocks, flops):
    moved = sum(math.prod(a.shape) * a.dtype.itemsize for a in (*arrays, *outs))
    return pl.pallas_call(
        kernel,
        name=name,
        grid=(blocks,),
        in_specs=specs,
        out_specs=out_specs,
        out_shape=outs,
        scratch_shapes=scratch,
        compiler_params=pltpu.CompilerParams(vmem_limit_bytes=VMEM_BYTES),
        cost_estimate=pl.CostEstimate(flops=flops, bytes_accessed=moved, transcendentals=0),
    )(*arrays)


class Recurrence:
    def __init__(self, rows, length, channels, head_size):
        self.rows, self.length, self.channels = (rows, length, channels)
        self.head_size = head_size
        self.width = head_size * LANES // math.gcd(head_size, LANES)
        self.blocks = channels // self.width
        self.flops = 2 * rows * length * channels * 2 * self.width

    def tall(self):
        return pl.BlockSpec((self.rows, self.length, self.width), lambda j: (0, 0, j))

    def short(self, size):
        return pl.BlockSpec((self.rows, size, self.width), lambda j: (0, 0, j))

    def flat(self, size):
        return pl.BlockSpec((size, self.width), lambda j: (0, j))

    def dist(self):
        return pl.BlockSpec((self.rows, self.length, LANES), lambda j: (0, 0, 0))

    def gates(self, columns):
        return pl.BlockSpec((self.width, columns), lambda j: (j, 0))

    def shape(self, size, dtype):
        return jax.ShapeDtypeStruct((self.rows, size, self.channels), dtype)

    def widen(self, lru_gates):
        size, width = (self.head_size, self.width)
        heads = width // size
        column = jnp.arange(2 * width)
        source = (column // width) * size + column % size
        spread = (jnp.arange(2 * size)[:, None] == source[None, :]).astype(jnp.bfloat16)
        owner = (column % width) // size
        mine = (jnp.arange(self.channels) // size) % heads
        wide = jnp.dot(lru_gates, spread, preferred_element_type=jnp.float32)
        return jnp.where(mine[:, None] == owner[None, :], wide, 0.0).astype(jnp.bfloat16)

    def forward(self, branch, rim, dist, params, gates):
        f32 = jnp.float32
        outs = [self.shape(self.length, d) for d in (jnp.bfloat16, f32, f32, f32, f32)]
        return channel_call(
            forward_kernel,
            "recurrence_forward",
            (branch, rim, dist, params, gates),
            [self.tall(), self.short(SUBLANES), self.dist(), self.flat(16), self.gates(2 * self.width)],
            outs,
            [self.tall()] * 5,
            [pltpu.VMEM((self.rows, self.length, 2 * self.width), f32)],
            self.blocks,
            self.flops,
        )

    def adjoint(self, dmix, pre, state, cum, entering, rate, dist, params):
        f32 = jnp.float32
        outs = [self.shape(self.length, d) for d in (jnp.bfloat16, f32, f32)] + [self.shape(1, f32)]
        tall = self.tall()
        return channel_call(
            adjoint_kernel,
            "recurrence_adjoint",
            (dmix, pre, state, cum, entering, rate, dist, params),
            [tall, tall, tall, tall, self.short(1), tall, self.dist(), self.flat(16)],
            outs,
            [tall, tall, tall, self.short(1)],
            [],
            self.blocks,
            0,
        )

    def backward(
        self, local, back, leaving, state, cum, entering, rate, igate, lru, dist, branch, rim, params, gates
    ):
        f32 = jnp.float32
        outs = [
            self.shape(self.length, jnp.bfloat16),
            self.shape(SUBLANES, f32),
            self.shape(SUBLANES, f32),
            jax.ShapeDtypeStruct((self.channels, 2 * LANES), jnp.bfloat16),
        ]
        tall, one = (self.tall(), self.short(1))
        return channel_call(
            functools.partial(backward_kernel, self.head_size),
            "recurrence_backward",
            (local, back, leaving, state, cum, entering, rate, igate, lru, dist, branch, rim, params, gates),
            [tall, tall, one, tall, tall, one, tall, tall, tall, self.dist(), tall]
            + [self.short(SUBLANES), self.flat(16), self.gates(2 * self.width)],
            outs,
            [tall, self.short(SUBLANES), self.short(SUBLANES), self.gates(2 * LANES)],
            [
                pltpu.VMEM((self.rows, self.length, 2 * self.width), jnp.bfloat16),
                pltpu.VMEM((self.rows, self.length, self.width), f32),
                pltpu.VMEM((SUBLANES, self.width), f32),
            ],
            self.blocks,
            2 * self.flops,
        )


def gathered(parts_ref, at):
    return jnp.concatenate([parts_ref[k, at, :] for k in range(parts_ref.shape[0])], axis=1)


def front_kernel(
    parts_ref, gain_ref, input_ref, gate_ref, x_ref, inverse_ref, normed_ref, branch_ref, pre_ref
):
    tokens = x_ref.shape[0]
    piece, tall = (64, min(tokens, 512))

    @pl.when(pl.program_id(0) == 0)
    def _():
        def norm(index, carry):
            at = pl.ds(pl.multiple_of(index * piece, piece), piece)
            low = gathered(parts_ref, at)
            x_ref[at, :] = low
            value = low.astype(jnp.float32)
            inverse = lax.rsqrt(jnp.mean(value * value, axis=1, keepdims=True) + EPS)
            inverse_ref[at, :] = jnp.broadcast_to(inverse, (piece, LANES))
            normed_ref[at, :] = (value * inverse * gain_ref[...]).astype(jnp.bfloat16)
            return carry

        lax.fori_loop(0, tokens // piece, norm, 0)

    def multiply(index, carry):
        at = pl.ds(pl.multiple_of(index * tall, tall), tall)
        normed = normed_ref[at, :]
        branch_ref[at, :] = jnp.dot(normed, input_ref[...], preferred_element_type=jnp.float32)
        pre_ref[at, :] = jnp.dot(normed, gate_ref[...], preferred_element_type=jnp.float32)
        return carry

    lax.fori_loop(0, tokens // tall, multiply, 0)


def front(parts, gain, recur_input, recur_gate):
    count, tokens, width = parts.shape
    model, rec = recur_input.shape
    columns = 4 * LANES
    low, f32 = (jnp.bfloat16, jnp.float32)
    tall = pl.BlockSpec((model, columns), lambda j: (0, j))
    wide = pl.BlockSpec((tokens, columns), lambda j: (0, j))

    def whole(shape):
        return pl.BlockSpec(shape, lambda j: (0,) * len(shape))

    return pl.pallas_call(
        front_kernel,
        name="norm_and_project",
        grid=(rec // columns,),
        in_specs=[whole(parts.shape), whole((1, model)), tall, tall],
        out_specs=[whole((tokens, model)), whole((tokens, LANES)), whole((tokens, model)), wide, wide],
        out_shape=[
            jax.ShapeDtypeStruct((tokens, model), low),
            jax.ShapeDtypeStruct((tokens, LANES), f32),
            jax.ShapeDtypeStruct((tokens, model), low),
            jax.ShapeDtypeStruct((tokens, rec), f32),
            jax.ShapeDtypeStruct((tokens, rec), f32),
        ],
        compiler_params=pltpu.CompilerParams(vmem_limit_bytes=VMEM_BYTES),
        cost_estimate=pl.CostEstimate(
            flops=4 * tokens * model * rec, bytes_accessed=20 * tokens * model, transcendentals=0
        ),
    )(parts, gain[None], recur_input, recur_gate)


def mlp_kernel(
    left_ref,
    parts_ref,
    normed_ref,
    resid_ref,
    gain_ref,
    gate_ref,
    up_ref,
    down_ref,
    gout_ref,
    hidden_ref,
    dgate_ref,
    dup_ref,
    result_ref,
    dres_ref,
    total_ref,
    back_ref,
):
    tokens, model = normed_ref.shape
    chunk = down_ref.shape[0]
    rows = left_ref.shape[0]
    length = tokens // rows
    step = pl.program_id(0)
    slab = 32

    @pl.when(step == 0)
    def _():
        for row in range(rows):

            def collect(index, carry, row=row):
                base = pl.multiple_of(index * slab, slab)
                at = pl.ds(row * length + base, slab)
                low = gathered(parts_ref, at)
                place = base + lax.broadcasted_iota(jnp.int32, low.shape, 0)
                value = jnp.where(place < left_ref[row], low.astype(jnp.float32), 0.0)
                gout_ref[at, :] = value.astype(jnp.bfloat16)
                total_ref[at, :] = resid_ref[at, :]
                back_ref[at, :] = jnp.zeros((slab, model), jnp.float32)
                return carry

            lax.fori_loop(0, length // slab, collect, 0)

    tall = min(tokens, 512)
    wide = 256

    def tile(index, carry):
        at = pl.ds(pl.multiple_of(index * tall, tall), tall)
        for column in range(chunk // wide):
            own = slice(column * wide, (column + 1) * wide)
            gate = jnp.dot(normed_ref[at, :], gate_ref[:, own], preferred_element_type=jnp.float32)
            up = jnp.dot(normed_ref[at, :], up_ref[:, own], preferred_element_type=jnp.float32)
            dhid = lax.dot_general(
                gout_ref[at, :],
                down_ref[own, :],
                (((1,), (1,)), ((), ())),
                preferred_element_type=jnp.float32,
            )
            act, slope = gelu_pair(gate)
            hidden_ref[at, own] = (act * up).astype(jnp.bfloat16)
            dgate_ref[at, own] = (dhid * up * slope).astype(jnp.bfloat16)
            dup_ref[at, own] = (dhid * act).astype(jnp.bfloat16)
        for column in range(model // (2 * wide)):
            own = slice(column * 2 * wide, (column + 1) * 2 * wide)
            total_ref[at, own] += jnp.dot(
                hidden_ref[at, :], down_ref[:, own], preferred_element_type=jnp.float32
            )
            back_ref[at, own] += lax.dot_general(
                dgate_ref[at, :],
                gate_ref[own, :],
                (((1,), (1,)), ((), ())),
                preferred_element_type=jnp.float32,
            ) + lax.dot_general(
                dup_ref[at, :],
                up_ref[own, :],
                (((1,), (1,)), ((), ())),
                preferred_element_type=jnp.float32,
            )
        return carry

    lax.fori_loop(0, tokens // tall, tile, 0)

    @pl.when(step == pl.num_programs(0) - 1)
    def _():
        parts, width = (result_ref.shape[0], result_ref.shape[2])
        small = 16

        def finish(index, carry):
            at = pl.ds(pl.multiple_of(index * small, small), small)
            result = total_ref[at, :].astype(jnp.bfloat16)
            for part in range(parts):
                result_ref[part, at, :] = result[:, part * width : (part + 1) * width]
            resid = resid_ref[at, :]
            inverse = lax.rsqrt(jnp.mean(resid * resid, axis=1, keepdims=True) + EPS)
            normed = resid * inverse
            scaled = back_ref[at, :] * gain_ref[...]
            mean = jnp.mean(scaled * normed, axis=1, keepdims=True)
            dres = gout_ref[at, :].astype(jnp.float32) + inverse * (scaled - normed * mean)
            dres_ref[at, :] = dres.astype(jnp.bfloat16)
            return carry

        lax.fori_loop(0, tokens // small, finish, 0)


def mlp(left, parts, normed, resid, gain, mlp_gate, mlp_up, mlp_down):
    tokens, model = normed.shape
    ffn = mlp_gate.shape[1]
    chunk = 768
    low, f32 = (jnp.bfloat16, jnp.float32)

    def whole(shape):
        return pl.BlockSpec(shape, lambda s: (0,) * len(shape), pipeline_mode=pl.Buffered(1))

    columns = pl.BlockSpec((model, chunk), lambda s: (0, s))
    made = pl.BlockSpec((tokens, chunk), lambda s: (0, s))
    tall = jax.ShapeDtypeStruct((tokens, ffn), low)
    square = jax.ShapeDtypeStruct((tokens, model), low)
    return pl.pallas_call(
        mlp_kernel,
        name="mlp_forward_backward",
        grid=(ffn // chunk,),
        in_specs=[
            pl.BlockSpec(memory_space=pltpu.SMEM),
            whole(parts.shape),
            whole(normed.shape),
            whole(resid.shape),
            whole((1, model)),
            columns,
            columns,
            pl.BlockSpec((chunk, model), lambda s: (s, 0)),
        ],
        out_specs=[
            whole((tokens, model)),
            made,
            made,
            made,
            whole(parts.shape),
            whole((tokens, model)),
        ],
        out_shape=[square, tall, tall, tall, jax.ShapeDtypeStruct(parts.shape, low), square],
        scratch_shapes=[pltpu.VMEM((tokens, model), f32), pltpu.VMEM((tokens, model), f32)],
        compiler_params=pltpu.CompilerParams(vmem_limit_bytes=VMEM_BYTES),
        cost_estimate=pl.CostEstimate(
            flops=12 * tokens * model * ffn,
            bytes_accessed=6 * (model + tokens) * ffn + 14 * tokens * model,
            transcendentals=0,
        ),
    )(left, parts, normed, resid, gain[None], mlp_gate, mlp_up, mlp_down)


def spread_kernel(whole_ref, out_ref):
    out_ref[0] = whole_ref[...]


def spread(whole, count):
    tokens, width = (whole.shape[0], whole.shape[1] // count)
    return pl.pallas_call(
        spread_kernel,
        name="spread_features",
        grid=(count,),
        in_specs=[pl.BlockSpec((tokens, width), lambda j: (0, j))],
        out_specs=pl.BlockSpec((1, tokens, width), lambda j: (j, 0, 0)),
        out_shape=jax.ShapeDtypeStruct((count, tokens, width), whole.dtype),
        cost_estimate=pl.CostEstimate(
            flops=0, bytes_accessed=4 * tokens * whole.shape[1], transcendentals=0
        ),
    )(whole)


CHAN = ("zed", "core")


def features_in(local):
    count = lax.axis_size(CHAN)
    rows, length, width = local.shape
    if width % LANES == 0:
        moved = lax.all_to_all(
            local.reshape(count, rows // count, length, width), CHAN, 0, 0, tiled=True
        )
        return moved.reshape(count, -1, width)
    moved = lax.all_to_all(local, CHAN, split_axis=0, concat_axis=2, tiled=True)
    return moved.reshape(1, -1, count * width)


def features_apart(whole):
    count = lax.axis_size(CHAN)
    if (whole.shape[1] // count) % LANES == 0:
        return spread(whole, count)
    return whole[None]


def features_out(parts, rows):
    blocks, tokens, width = parts.shape
    parts = parts.reshape(blocks, rows, tokens // rows, width)
    if blocks > 1:
        moved = lax.all_to_all(parts, CHAN, 0, 0, tiled=True)
        return moved.reshape(-1, *parts.shape[2:])
    return lax.all_to_all(parts[0], CHAN, split_axis=2, concat_axis=0, tiled=True)


MESH = pl.DeviceIdType.MESH


class Corners:
    def __init__(self, seq, zed):
        self.seq_bits, self.zed_bits = (seq.bit_length() - 1, zed.bit_length() - 1)
        self.count = self.seq_bits + self.zed_bits
        self.dims = (2,) * self.count
        self.low = tuple(range(self.seq_bits))[::-1] + tuple(range(self.seq_bits, self.count))[::-1]
        self.high = tuple(range(self.seq_bits)) + tuple(range(self.seq_bits, self.count))[::-1]

    def place(self, dim):
        if dim < self.seq_bits:
            return ("seq", 2 ** (self.seq_bits - 1 - dim))
        return ("zed", 2 ** (self.count - 1 - dim))

    def bit(self, dim):
        axis, weight = self.place(dim)
        return lax.rem(lax.div(lax.axis_index(axis), weight), 2)

    def partner(self, dim):
        axis, weight = self.place(dim)
        return {axis: lax.axis_index(axis) + weight * (1 - 2 * self.bit(dim))}


def tail_kernel(
    corners,
    orders,
    dgate_hbm,
    dbranch_hbm,
    ending_ref,
    leading_ref,
    mixed_hbm,
    dres_hbm,
    normed_hbm,
    x_hbm,
    inverse_hbm,
    gain_ref,
    input_hbm,
    gate_hbm,
    small_hbm,
    tokens_ref,
    sum_gate,
    sum_out,
    sum_in,
    sum_small,
    *refs,
):
    stages = corners.count + 1
    dgate, dbranch, mixed, dres, normed, x, inverse, weight_in, weight_gate = refs[:9]
    made_in, made_out, own_small, back, parts, rim = refs[9:15]
    slots_in, slots_out, slots_small = (
        refs[15 + k * stages : 15 + (k + 1) * stages] for k in range(3)
    )
    (
        send_sem,
        recv_sem,
        load_sem,
        move_send,
        move_recv,
        keep_sem,
        rim_send,
        rim_recv,
    ) = refs[15 + 3 * stages :]
    seq, zed, core = (lax.axis_index(axis) for axis in ("seq", "zed", "core"))
    seqs, group = (lax.axis_size("seq"), 2 * lax.axis_size("zed"))
    mine = zed * 2 + core
    rows, length = (rim.shape[0], tokens_ref.shape[1])
    model = x.shape[1]

    def member(index):
        return {"zed": lax.div(index, 2), "core": lax.rem(index, 2)}

    loads = [
        pltpu.make_async_copy(source, target, load_sem.at[place])
        for place, (source, target) in enumerate(
            (
                (dbranch_hbm, dbranch),
                (input_hbm, weight_in),
                (dgate_hbm, dgate),
                (gate_hbm, weight_gate),
                (x_hbm, x),
                (inverse_hbm, inverse),
                (dres_hbm, dres),
                (normed_hbm, normed),
                (mixed_hbm, mixed),
                (small_hbm.at[(slice(None),) * corners.count + (core,)], own_small),
            )
        )
    ]
    for load in loads:
        load.start()

    barrier = pltpu.get_barrier_semaphore()
    for other in range(1, group):
        pl.semaphore_signal(
            barrier, inc=1, device_id=member(lax.rem(mine + other, group)), device_id_type=MESH
        )
    for other in range(1, seqs):
        pl.semaphore_signal(
            barrier, inc=1, device_id={"seq": lax.rem(seq + other, seqs)}, device_id_type=MESH
        )
    pl.semaphore_wait(barrier, group - 1 + seqs - 1)

    rim_copy = pltpu.make_async_remote_copy(
        src_ref=leading_ref,
        dst_ref=rim,
        send_sem=rim_send,
        recv_sem=rim_recv,
        device_id={"seq": lax.rem(seq + seqs - 1, seqs)},
        device_id_type=MESH,
    )
    rim_copy.start()

    def own(stream, index):
        if stream < 4:
            return made_in.at[(stream,) + index + (core,)]
        if stream < 6:
            return made_out.at[(stream - 4,) + index + (core,)]
        return own_small.at[index]

    def slot(stream, stage):
        if stream < 4:
            return slots_in[stage].at[stream]
        if stream < 6:
            return slots_out[stage].at[stream - 4]
        return slots_small[stage]

    def copy(stream, stage):
        order = orders[stream]
        every = (slice(None),) * corners.count
        if stage == 0:
            if stream < 4:
                source = made_in.at[(stream,) + every + (1 - core,)]
            elif stream < 6:
                source = made_out.at[(stream - 4,) + every + (1 - core,)]
            else:
                source = small_hbm.at[every + (1 - core,)]
            target = {"core": 1 - core}
        else:
            dim = order[stage - 1]
            fixed = {before: corners.bit(before) for before in order[: stage - 1]}
            fixed[dim] = 1 - corners.bit(dim)
            source = own(stream, tuple(fixed.get(d, slice(None)) for d in range(corners.count)))
            target = corners.partner(dim)
        return pltpu.make_async_remote_copy(
            src_ref=source,
            dst_ref=slot(stream, stage),
            send_sem=send_sem.at[stream, stage],
            recv_sem=recv_sem.at[stream, stage],
            device_id=target,
            device_id_type=MESH,
        )

    sums = [
        sum_gate.at[:, : sum_gate.shape[1] // 2],
        sum_gate.at[:, sum_gate.shape[1] // 2 :],
        sum_in.at[:, : sum_in.shape[1] // 2],
        sum_in.at[:, sum_in.shape[1] // 2 :],
        sum_out.at[:, : sum_out.shape[1] // 2],
        sum_out.at[:, sum_out.shape[1] // 2 :],
        sum_small,
    ]

    def advance(stream, stage):
        order = orders[stream]
        copy(stream, stage).wait_recv()
        left = [dim for dim in range(corners.count) if dim not in order[:stage]]
        fixed = {dim: corners.bit(dim) for dim in order[:stage]}
        arrived = slot(stream, stage)
        if not left:
            index = tuple(fixed[dim] for dim in range(corners.count))
            sums[stream][...] = own(stream, index)[...].astype(jnp.float32) + arrived[...].astype(
                jnp.float32
            )
            return

        def add(index, carry):
            part = {
                dim: lax.rem(lax.div(index, 2 ** (len(left) - 1 - place)), 2)
                for place, dim in enumerate(left)
            }
            kept = own(stream, tuple({**fixed, **part}[dim] for dim in range(corners.count)))
            total = kept[...].astype(jnp.float32) + arrived[
                tuple(part[dim] for dim in left)
            ].astype(jnp.float32)
            kept[...] = total.astype(jnp.bfloat16)
            return carry

        lax.fori_loop(0, 2 ** len(left), add, 0)
        copy(stream, stage + 1).start()

    def move(other, row):
        to = lax.rem(mine + other, group)
        return pltpu.make_async_remote_copy(
            src_ref=parts.at[to, pl.ds(row * length, length)],
            dst_ref=tokens_ref.at[mine * rows + row],
            send_sem=move_send.at[other - 1, row],
            recv_sem=move_recv.at[other - 1, row],
            device_id=member(to),
            device_id_type=MESH,
        )

    def keep(row):
        return pltpu.make_async_copy(
            parts.at[mine, pl.ds(row * length, length)],
            tokens_ref.at[mine * rows + row],
            keep_sem.at[row],
        )

    tile = 256
    width = parts.shape[2]

    def back_row(row):
        at_row = slice(row * length, (row + 1) * length)

        def product(index, carry):
            at = pl.ds(pl.multiple_of(index * tile, tile), tile)
            contract = (((1,), (1,)), ((), ()))
            back[:, at] = lax.dot_general(
                dbranch[at_row, :], weight_in[at, :], contract, preferred_element_type=jnp.float32
            ) + lax.dot_general(
                dgate[at_row, :], weight_gate[at, :], contract, preferred_element_type=jnp.float32
            )
            return carry

        lax.fori_loop(0, model // tile, product, 0)
        slab = 16

        def norm(index, carry):
            base = pl.multiple_of(index * slab, slab)
            at = pl.ds(row * length + base, slab)
            inv = inverse[at, :1]
            value = x[at, :].astype(jnp.float32) * inv
            scaled = back[pl.ds(base, slab), :] * gain_ref[...]
            mean = jnp.mean(scaled * value, axis=1, keepdims=True)
            grad = dres[at, :].astype(jnp.float32) + inv * (scaled - value * mean)
            grad = grad.astype(jnp.bfloat16)
            for part in range(parts.shape[0]):
                parts[part, at, :] = grad[:, part * width : (part + 1) * width]
            return carry

        lax.fori_loop(0, length // slab, norm, 0)
        for other in range(1, group):
            move(other, row).start()
        keep(row).start()

    def weight_product(left, right, made, stream, first):
        columns = made.shape[-1]
        shape = made.shape[1:-1]

        def product(index, carry):
            at = pl.ds(pl.multiple_of(index * tile, tile), tile)
            source = pl.ds(pl.multiple_of(first + index * tile, tile), tile)
            part = lax.dot_general(
                left[...],
                right[:, source],
                (((0,), (0,)), ((), ())),
                preferred_element_type=jnp.float32,
            )
            made[(stream,) + (slice(None),) * len(shape) + (at,)] = part.astype(
                jnp.bfloat16
            ).reshape(shape + (tile,))
            return carry

        lax.fori_loop(0, columns // tile, product, 0)

    for load in loads[:2]:
        load.wait()
    rim_copy.wait()
    live = jnp.where(seq < seqs - 1, 1.0, 0.0)
    for row in range(rows):
        at = slice((row + 1) * length - STEP, (row + 1) * length)
        inside = dbranch[at, :].astype(jnp.float32)
        last = ending_ref[row] + live * rim[row]
        dbranch[at, :] = jnp.concatenate([inside[: STEP - SUBLANES], last], axis=0).astype(
            jnp.bfloat16
        )
    for load in loads[2:7]:
        load.wait()
    copy(6, 0).start()
    for row in range(rows):
        back_row(row)
    for load in loads[7:]:
        load.wait()
    half = made_in.shape[-1]
    for stream in (0, 1):
        weight_product(normed, dgate, made_in, stream, stream * half)
        copy(stream, 0).start()
    half_out = made_out.shape[-1]
    for stream in (4, 5):
        weight_product(mixed, dres, made_out, stream - 4, (stream - 4) * half_out)
        copy(stream, 0).start()
    for stream in (0, 1, 6):
        advance(stream, 0)
    for stream in (2, 3):
        weight_product(normed, dbranch, made_in, stream, (stream - 2) * half)
        copy(stream, 0).start()
    for stream in (4, 5, 2, 3):
        advance(stream, 0)
    for stage in range(1, stages):
        for stream in (0, 1, 6, 4, 5, 2, 3):
            advance(stream, stage)
    for stage in range(stages):
        for stream in range(7):
            copy(stream, stage).wait_send()
    for row in range(rows):
        for other in range(1, group):
            move(other, row).wait()
        keep(row).wait()


def tail(dgate, dbranch, ending, leading, mixed, dres, normed, x, inverse, gain, w_in, w_gate, small):
    corners = Corners(lax.axis_size("seq"), lax.axis_size("zed"))
    group, devices = (lax.axis_size(CHAN), 2 ** (corners.count + 1))
    tokens, model = x.shape
    rec = dgate.shape[1]
    rows = ending.shape[0]
    length, width = (tokens // rows, model // group)
    low, f32 = (jnp.bfloat16, jnp.float32)
    stages = corners.count + 1
    in_rows, out_rows = (model // devices, rec // devices)
    small = small.reshape(corners.dims + (2, out_rows, small.shape[1]))
    orders = [corners.low, corners.high] * 3 + [corners.low]

    def slots(lead, shape):
        return [pltpu.VMEM(lead + (2,) * (corners.count - k) + shape, low) for k in range(stages)]

    in_shape, out_shape = ((in_rows, rec // 2), (out_rows, model // 2))
    loaded = (dgate, dbranch, mixed, dres, normed, x, inverse, w_in, w_gate)
    anyplace = pl.BlockSpec(memory_space=pl.ANY)
    vmem = pl.BlockSpec(memory_space=pltpu.VMEM)
    dma = pltpu.SemaphoreType.DMA
    moved = sum(math.prod(a.shape) * a.dtype.itemsize for a in loaded)
    return pl.pallas_call(
        functools.partial(tail_kernel, corners, orders),
        name="tail",
        in_specs=[anyplace, anyplace, vmem, vmem] + [anyplace] * 5 + [vmem] + [anyplace] * 3,
        out_specs=[anyplace] + [vmem] * 4,
        out_shape=[
            jax.ShapeDtypeStruct((group * rows, length, width), low),
            jax.ShapeDtypeStruct((in_rows, rec), f32),
            jax.ShapeDtypeStruct((out_rows, model), f32),
            jax.ShapeDtypeStruct((in_rows, rec), f32),
            jax.ShapeDtypeStruct(small.shape[-2:], f32),
        ],
        scratch_shapes=[pltpu.VMEM(a.shape, a.dtype) for a in loaded]
        + [
            pltpu.VMEM((4,) + corners.dims + (2,) + in_shape, low),
            pltpu.VMEM((2,) + corners.dims + (2,) + out_shape, low),
            pltpu.VMEM(corners.dims + small.shape[-2:], low),
            pltpu.VMEM((length, model), f32),
            pltpu.VMEM((group, tokens, width), low),
            pltpu.VMEM(leading.shape, leading.dtype),
        ]
        + slots((4,), in_shape)
        + slots((2,), out_shape)
        + slots((), small.shape[-2:])
        + [
            dma((7, stages)),
            dma((7, stages)),
            dma((10,)),
            dma((group - 1, rows)),
            dma((group - 1, rows)),
            dma((rows,)),
            dma,
            dma,
        ],
        compiler_params=pltpu.CompilerParams(
            collective_id=1, has_side_effects=True, vmem_limit_bytes=60 * 1024 * 1024
        ),
        cost_estimate=pl.CostEstimate(
            flops=10 * tokens * model * rec, bytes_accessed=2 * moved, transcendentals=0
        ),
    )(dgate, dbranch, ending, leading, mixed, dres, normed, x, inverse, gain[None], w_in, w_gate, small)


def grads_kernel(
    normed_ref,
    dgate_ref,
    dup_ref,
    hidden_ref,
    gout_ref,
    out_ref,
    turned_ref,
    made_wide,
    made_down,
    come_wide,
    come_down,
    send_sem,
    recv_sem,
    store_sem,
):
    step = pl.program_id(0)
    core = lax.axis_index("core")
    other = {"core": 1 - core}
    wide_rows, down_rows = (made_wide.shape[3], made_down.shape[3])
    wides, downs = (come_wide.shape[0], come_down.shape[0])
    total = wides + downs
    down_at = wides * wide_rows

    def exchange(made, come, index, slot):
        return pltpu.make_async_remote_copy(
            src_ref=made.at[lax.rem(index, 2), 1 - core],
            dst_ref=come.at[index],
            send_sem=send_sem.at[slot],
            recv_sem=recv_sem.at[slot],
            device_id=other,
            device_id_type=MESH,
        )

    def store_wide(index):
        return pltpu.make_async_copy(
            come_wide.at[index],
            out_ref.at[:, pl.ds(pl.multiple_of(index * wide_rows, wide_rows), wide_rows)],
            store_sem.at[index],
        )

    def store_down(index):
        chips = come_down.shape[1]
        return pltpu.make_async_copy(
            come_down.at[index],
            out_ref.at[pl.ds(index * chips, chips), pl.ds(down_at, down_rows)],
            store_sem.at[index + wides],
        )

    @pl.when(step == 0)
    def _():
        barrier = pltpu.get_barrier_semaphore()
        pl.semaphore_signal(barrier, inc=1, device_id=other, device_id_type=MESH)
        pl.semaphore_wait(barrier, 1)
        turned_ref[...] = normed_ref[...].T

    def product_wide(source, index):
        made = made_wide.at[lax.rem(index, 2)]
        chips, rows = (made.shape[1], made.shape[2])
        tile = 256

        def column(place, carry):
            at = pl.ds(pl.multiple_of(place * tile, tile), tile)
            part = jnp.dot(turned_ref[...], source[:, at], preferred_element_type=jnp.float32)
            part = part.astype(jnp.bfloat16).reshape(chips, 2, rows, tile)
            made[0, :, :, at] = part[:, 0]
            made[1, :, :, at] = part[:, 1]
            return carry

        lax.fori_loop(0, source.shape[1] // tile, column, 0)

    def product_tall(left, right, made_all, index):
        made = made_all.at[lax.rem(index, 2)]
        chips, rows = (made.shape[1], made.shape[2])
        tile = 256

        def column(place, carry):
            at = pl.ds(pl.multiple_of(place * tile, tile), tile)
            part = lax.dot_general(
                left[...], right[:, at], (((0,), (0,)), ((), ())), preferred_element_type=jnp.float32
            )
            part = part.astype(jnp.bfloat16).reshape(chips, 2, rows, tile)
            made[0, :, :, at] = part[:, 0]
            made[1, :, :, at] = part[:, 1]
            return carry

        lax.fori_loop(0, right.shape[1] // tile, column, 0)

    half = wides // 2

    @pl.when(step < half)
    def _():
        product_wide(dgate_ref, step)

    @pl.when((step >= half) & (step < wides))
    def _():
        product_wide(dup_ref, step)

    @pl.when(step < wides)
    def _():
        exchange(made_wide, come_wide, step, step).start()

    @pl.when((step >= wides) & (step < total))
    def _():
        product_tall(hidden_ref, gout_ref, made_down, step - wides)
        exchange(made_down, come_down, step - wides, step).start()

    def finish(made, come, index, slot, store):
        exchange(made, come, index, slot).wait()
        mine = made.at[lax.rem(index, 2), core]
        arrived = come.at[index]

        def add(chip, carry):
            both = mine[chip].astype(jnp.float32) + arrived[chip].astype(jnp.float32)
            arrived[chip] = both.astype(jnp.bfloat16)
            return carry

        lax.fori_loop(0, come.shape[1], add, 0)
        store(index).start()

    before = step - 1

    @pl.when((before >= 0) & (before < wides))
    def _():
        finish(made_wide, come_wide, before, before, store_wide)

    @pl.when(before >= wides)
    def _():
        finish(made_down, come_down, before - wides, before, store_down)

    @pl.when(step == total)
    def _():
        for index in range(wides):
            store_wide(index).wait()
        for index in range(downs):
            store_down(index).wait()


def block_gradients(normed, dgate, dup, hidden, gout):
    tokens, model = normed.shape
    ffn = hidden.shape[1]
    chips = lax.axis_size("seq") * lax.axis_size("zed")
    devices = 2 * chips
    wide_rows, down_rows = (model // devices, ffn // devices)
    chunk = 768
    wides, downs = (2 * ffn // model, ffn // chunk)
    half = wides // 2
    down_chips = chunk // (2 * down_rows)
    rows = wides * wide_rows + down_rows
    low = jnp.bfloat16

    def whole(array):
        return pl.BlockSpec(array.shape, lambda s: (0, 0), pipeline_mode=pl.Buffered(1))

    def part(columns, first, count):
        return pl.BlockSpec((tokens, columns), lambda s: (0, jnp.clip(s - first, 0, count - 1)))

    total = wides + downs
    flops = 6 * tokens * model * ffn
    arrays = (normed, dgate, dup, hidden, gout)
    moved = sum(math.prod(a.shape) * 2 for a in arrays) + chips * rows * model * 2
    return pl.pallas_call(
        grads_kernel,
        name="block_gradients",
        grid=(total + 1,),
        in_specs=[
            whole(normed),
            part(model, 0, half),
            part(model, half, half),
            part(chunk, wides, downs),
            whole(gout),
        ],
        out_specs=pl.BlockSpec(memory_space=pl.ANY),
        out_shape=jax.ShapeDtypeStruct((chips, rows, model), low),
        scratch_shapes=[
            pltpu.VMEM((model, tokens), low),
            pltpu.VMEM((2, 2, chips, wide_rows, model), low),
            pltpu.VMEM((2, 2, down_chips, down_rows, model), low),
            pltpu.VMEM((wides, chips, wide_rows, model), low),
            pltpu.VMEM((downs, down_chips, down_rows, model), low),
            pltpu.SemaphoreType.DMA((total,)),
            pltpu.SemaphoreType.DMA((total,)),
            pltpu.SemaphoreType.DMA((total,)),
        ],
        compiler_params=pltpu.CompilerParams(
            collective_id=2, has_side_effects=True, vmem_limit_bytes=VMEM_BYTES
        ),
        cost_estimate=pl.CostEstimate(flops=flops, bytes_accessed=moved, transcendentals=0),
    )(*arrays)


def carried(factor, value, axis, backward):
    count, mine = (lax.axis_size(axis), lax.axis_index(axis))
    pieces = lax.all_gather(jnp.stack([factor, value]), axis)
    order = range(count - 1, 0, -1) if backward else range(count - 1)
    total = jnp.zeros_like(value)
    for place in order:
        longer = pieces[place, 0] * total + pieces[place, 1]
        total = jnp.where(place > mine if backward else place < mine, longer, total)
    return total


def passed_along(value, axis, steps):
    count = lax.axis_size(axis)
    leading, last = (max(0, -steps), min(count, count - steps))
    return lax.ppermute(value, axis, [(source, source + steps) for source in range(leading, last)])


def weight_grad(left, right):
    return lax.dot_general(
        left, right, (((0,), (0,)), ((), ())), preferred_element_type=jnp.float32
    ).astype(jnp.bfloat16)


def back_dot(left, right):
    return lax.dot_general(
        left, right, (((1,), (1,)), ((), ())), preferred_element_type=jnp.float32
    )


def fwd_dot(left, right):
    return jnp.dot(left, right, preferred_element_type=jnp.float32)


def gelu_fn(value):
    return jax.nn.gelu(value, approximate=True)


def norm_back(grad_norm, normed, inverse, gain):
    scaled = grad_norm * gain
    mean_term = jnp.mean(scaled * normed, axis=1, keepdims=True)
    return inverse * (scaled - normed * mean_term)


def scattered(gradient):
    return lax.psum_scatter(
        gradient, ("seq", "zed", "core"), scatter_dimension=0, tiled=True
    ).astype(jnp.float32)


def body(
    tokens,
    cotangent,
    doc_starts,
    lengths,
    norm1_gain,
    recur_input,
    recur_gate,
    conv_kernel,
    conv_bias,
    lru_gates,
    lru_bias,
    lru_decay,
    recur_out,
    norm2_gain,
    mlp_gate,
    mlp_up,
    mlp_down,
):
    count = lax.axis_size(CHAN)
    row_count, block_len = (tokens.shape[0] // count, tokens.shape[1])
    model_dim = tokens.shape[2] * count
    tok_count = row_count * block_len
    rec_width = recur_input.shape[1]
    ffn_width = mlp_gate.shape[1]
    head_count = H
    head_size = rec_width // head_count
    tap_count = conv_kernel.shape[0]
    rim_size = tap_count - 1
    seq_index = lax.axis_index("seq")
    position = seq_index * block_len + jnp.arange(block_len, dtype=jnp.int32)
    bounds = jnp.concatenate([doc_starts, lengths[:, None]], axis=1)
    is_before = bounds[:, None, :] <= position[None, :, None]
    seg_start = jnp.max(jnp.where(is_before, bounds[:, None, :], 0), axis=2)
    low_x, inverse_lanes, normed_low, branch_pre, gate_pre = front(
        features_in(tokens), norm1_gain, recur_input, recur_gate
    )
    gate_act = gelu_fn(gate_pre)
    branch_rows = branch_pre.reshape(row_count, block_len, rec_width)
    core = Recurrence(row_count, block_len, rec_width, head_size)
    prev_rim = passed_along(
        branch_rows[:, block_len - rim_size :, :].astype(jnp.bfloat16), "seq", 1
    ).astype(jnp.float32)
    rim = jnp.pad(prev_rim, ((0, 0), (SUBLANES - rim_size, 0), (0, 0)))
    dist = jnp.broadcast_to(
        (position[None, :] - seg_start)[:, :, None], (row_count, block_len, LANES)
    )
    soft_decay = jax.nn.softplus(-lru_decay)
    params = jnp.concatenate(
        [
            conv_kernel,
            conv_bias[None],
            lru_bias,
            (-8.0 * soft_decay)[None],
            jnp.zeros((SUBLANES, rec_width), jnp.float32),
        ],
        axis=0,
    )
    wide_gates = core.widen(lru_gates)
    lru_in, rate_gate, input_gate, local_state, cum_coef = core.forward(
        branch_rows, rim, dist, params, wide_gates
    )
    cotangent, local_state = lax.optimization_barrier((features_in(cotangent), local_state))
    carry_in = carried(cum_coef[:, -1, :], local_state[:, -1, :], "seq", False)
    entering = carry_in[:, None, :]
    state_rows = local_state + cum_coef * entering
    state_flat = state_rows.reshape(tok_count, rec_width)
    mixed_low = (state_flat * gate_act).astype(jnp.bfloat16)
    resid_one = low_x.astype(jnp.float32) + fwd_dot(mixed_low, recur_out)
    inv_two = lax.rsqrt(jnp.mean(resid_one * resid_one, axis=1, keepdims=True) + EPS)
    normed_two = resid_one * inv_two
    normed_low2 = (normed_two * norm2_gain).astype(jnp.bfloat16)
    grad_low, hidden_low, mgate_low, mup_low, result_parts, resid_low = mlp(
        lengths - seq_index * block_len,
        cotangent,
        normed_low2,
        resid_one,
        norm2_gain,
        mlp_gate,
        mlp_up,
        mlp_down,
    )
    output = features_out(result_parts, row_count)
    devices = lax.axis_size(("seq", "zed", "core"))
    own_rows = model_dim // devices
    tiled = own_rows % (2 * SUBLANES) == 0 and tokens.shape[2] % LANES == 0
    if tiled:
        merged = block_gradients(
            normed_low2, mgate_low, mup_low, hidden_low, grad_low
        )
        merged, resid_low = lax.optimization_barrier((merged, resid_low))
        merged = lax.psum_scatter(merged, "seq", scatter_dimension=0, tiled=True)
    grad_mixed = back_dot(resid_low, recur_out)
    gate_low, back_local, back_cum, first_term = core.adjoint(
        grad_mixed.reshape(row_count, block_len, rec_width),
        gate_pre.reshape(row_count, block_len, rec_width),
        local_state,
        cum_coef,
        entering,
        rate_gate,
        dist,
        params,
    )
    gate_low = gate_low.reshape(tok_count, rec_width)
    output, back_local = lax.optimization_barrier((output, back_local))
    carry_out = carried(cum_coef[:, -1, :], first_term[:, 0, :], "seq", True)
    branch_local, ending, leading, small = core.backward(
        back_local,
        back_cum,
        carry_out[:, None, :],
        local_state,
        cum_coef,
        entering,
        rate_gate,
        input_gate,
        lru_in,
        dist,
        branch_rows,
        rim,
        params,
        wide_gates,
    )
    branch_low = branch_local.reshape(tok_count, rec_width)
    if tiled:
        merged, branch_low = lax.optimization_barrier((merged, branch_low))
        merged = lax.psum_scatter(merged, "zed", scatter_dimension=0, tiled=True)
        grad_tokens, sum_rgate, sum_rout, sum_rin, own_small = tail(
            gate_low,
            branch_low,
            ending,
            leading,
            mixed_low,
            resid_low,
            normed_low,
            low_x,
            inverse_lanes,
            norm1_gain,
            recur_input,
            recur_gate,
            small,
        )
        own = merged[0].astype(jnp.float32)
        span = ffn_width // model_dim * own_rows

        def unfolded(part):
            return jnp.swapaxes(part.reshape(-1, own_rows, model_dim), 0, 1).reshape(own_rows, -1)

        sum_mgate, sum_mup = (unfolded(own[:span]), unfolded(own[span : 2 * span]))
        sum_down = own[2 * span :]
    else:
        from_next = passed_along(
            leading[:, SUBLANES - rim_size :, :].astype(jnp.bfloat16), "seq", -1
        )
        ending = ending + jnp.pad(
            from_next.astype(jnp.float32), ((0, 0), (SUBLANES - rim_size, 0), (0, 0))
        )
        branch_low = lax.dynamic_update_slice(
            branch_local, ending.astype(jnp.bfloat16), (0, block_len - SUBLANES, 0)
        ).reshape(tok_count, rec_width)
        grad_norm1 = back_dot(branch_low, recur_input) + back_dot(gate_low, recur_gate)
        inv_one = inverse_lanes[:, :1]
        normed_one = low_x.astype(jnp.float32) * inv_one
        input_part = norm_back(grad_norm1, normed_one, inv_one, norm1_gain)
        grad_x = (resid_low.astype(jnp.float32) + input_part).astype(jnp.bfloat16)
        grad_tokens = features_out(features_apart(grad_x), row_count)
        sum_mgate, sum_mup, sum_down, sum_rout, sum_rgate, sum_rin = (
            scattered(weight_grad(left, right))
            for left, right in (
                (normed_low2, mgate_low),
                (normed_low2, mup_low),
                (hidden_low, grad_low),
                (mixed_low, resid_low),
                (normed_low, gate_low),
                (normed_low, branch_low),
            )
        )
        own_small = scattered(small)
    sum_lgates = jnp.concatenate(
        [own_small[:, :head_size], own_small[:, LANES : LANES + head_size]], axis=1
    )
    own_sums = jnp.swapaxes(own_small[:, head_size : head_size + SUBLANES], 0, 1)
    device = lax.axis_index(("seq", "zed", "core"))

    def mine(array, size, axis=0):
        return lax.dynamic_slice_in_dim(array, device * size, size, axis)

    def weighed(weight, gradient):
        return jnp.sum(mine(weight, own_rows).astype(jnp.float32) * gradient, axis=1)

    sum_gain1 = (weighed(recur_input, sum_rin) + weighed(recur_gate, sum_rgate)) / mine(
        norm1_gain, own_rows
    )
    sum_gain2 = (weighed(mlp_gate, sum_mgate) + weighed(mlp_up, sum_mup)) / mine(
        norm2_gain, own_rows
    )
    own_channels = own_sums.shape[1]
    sum_decay = 8.0 * jax.nn.sigmoid(-mine(lru_decay, own_channels)) * own_sums[7]
    return (
        output,
        grad_tokens,
        sum_gain1,
        sum_rin,
        sum_rgate,
        own_sums[:4],
        own_sums[4],
        sum_lgates,
        own_sums[5:7],
        sum_decay,
        sum_rout,
        sum_gain2,
        sum_mgate,
        sum_mup,
        sum_down,
    )


def solution(mesh):
    seq, chan = (mesh.shape["seq"], mesh.shape["chan"])
    chips = jax.sharding.Mesh(mesh.devices.reshape(seq, chan // 2, 2), ("seq", "zed", "core"))
    chan = ("zed", "core")
    every = ("seq", "zed", "core")
    activations = P(None, "seq", chan)
    rows, columns, vector = (P(every, None), P(None, every), P(every))
    return jax.shard_map(
        body,
        mesh=chips,
        in_specs=(activations, activations, P(chan, None), P(chan)) + (P(),) * 13,
        out_specs=(
            activations,
            activations,
            vector,
            rows,
            rows,
            columns,
            vector,
            rows,
            columns,
            vector,
            rows,
            vector,
            rows,
            rows,
            rows,
        ),
        check_vma=False,
    )
```

```python
import functools
import math

import jax
import jax.numpy as jnp
from jax import lax
from jax.experimental import pallas as pl
from jax.experimental.pallas import tpu as pltpu
from jax.sharding import PartitionSpec as P

H = 16


EPS = 1e-06
ROOT_FLOOR = 1e-06
LANES = 128
SUBLANES = 8
STEP = 16
VMEM_BYTES = 56 * 1024 * 1024
MESH = pl.DeviceIdType.MESH


def sigmoid(value):
    return 0.5 * jnp.tanh(0.5 * value) + 0.5


GELU_C = 0.7978845608
GELU_A = 0.044715


def gelu_pair(value):
    square = value * value
    inner = jnp.tanh(value * (GELU_C + (GELU_C * GELU_A) * square))
    half = 0.5 + 0.5 * inner
    slope = GELU_C + (3.0 * GELU_C * GELU_A) * square
    return (value * half, half + 0.5 * value * (1.0 - inner * inner) * slope)


def root_argument(log_decay, decay):
    y = 2.0 * log_decay
    series = 1.0 + y * (0.5 + y * (1.0 / 6.0 + y * (1.0 / 24.0)))
    return jnp.where(y > -0.05, -y * series, 1.0 - decay * decay)


def across(column, width):
    return jnp.concatenate([column] * (width // LANES), axis=1)


class Rows:
    def __init__(self, refs):
        self.refs = refs

    def __getitem__(self, index):
        if not isinstance(index, tuple):
            return self.refs[index][0]
        return self.refs[index[0]][(0,) + index[1:]]


def by_rows(refs, rows, apart):
    found = []
    for split in apart:
        count = rows if split else 1
        found.append(Rows(refs[:count]) if split else refs[0])
        refs = refs[count:]
    return found, refs


def forward_kernel(
    branch_ref,
    rim_ref,
    dist_ref,
    par_ref,
    gates_ref,
    lru_ref,
    rate_ref,
    igate_ref,
    state_ref,
    cum_ref,
    last_ref,
    both_ref,
):
    rows, length, width = branch_ref.shape
    span = 2 * STEP if rows == 1 else STEP
    taps = [par_ref[k : k + 1, :] for k in range(4)]
    conv_bias, rate_bias, input_bias, soft = (par_ref[k : k + 1, :] for k in range(4, 8))
    place = lax.broadcasted_iota(jnp.int32, (SUBLANES, width), 0)

    for row in range(rows):

        def conv_step(index, before, row=row):
            base = pl.multiple_of(index * STEP, STEP)
            pieces = []
            for half in range(STEP // SUBLANES):
                at = pl.ds(base + half * SUBLANES, SUBLANES)
                here = branch_ref[row, at, :]
                dist = across(dist_ref[row, at, :], width)
                total = conv_bias + taps[0] * here
                for k in range(1, 4):
                    shifted = pltpu.roll(jnp.where(place < SUBLANES - k, here, before), k, 0)
                    total = total + taps[k] * jnp.where(dist >= k, shifted, 0.0)
                pieces.append(total)
                before = here
            lru_ref[row, pl.ds(base, STEP), :] = jnp.concatenate(pieces, axis=0).astype(jnp.bfloat16)
            return before

        lax.fori_loop(0, length // STEP, conv_step, rim_ref[row])

        piece = min(length, 256)

        def dot_step(index, carry, row=row):
            at = pl.ds(pl.multiple_of(index * piece, piece), piece)
            both_ref[row, at, :] = jnp.dot(
                lru_ref[row, at, :], gates_ref[...], preferred_element_type=jnp.float32
            )
            return carry

        lax.fori_loop(0, length // piece, dot_step, 0)

    def scan_step(index, carry):
        base = pl.multiple_of(index * span, span)
        later = []
        for row in range(rows):
            run_cum, run_state = carry[row]
            lru_both = lru_ref[row, pl.ds(base, span), :].astype(jnp.float32)
            for half in range(span // SUBLANES):
                at = pl.ds(base + half * SUBLANES, SUBLANES)
                lru = lru_both[half * SUBLANES : (half + 1) * SUBLANES]
                start = across(dist_ref[row, at, :], width) == 0
                rate = sigmoid(both_ref[row, at, :width] + rate_bias)
                igate = sigmoid(both_ref[row, at, width:] + input_bias)
                log_decay = rate * soft
                decay = jnp.exp(log_decay)
                arg = jnp.maximum(root_argument(log_decay, decay), ROOT_FLOOR)
                root = arg * lax.rsqrt(arg)
                cum = jnp.where(start, 0.0, decay)
                value = jnp.where(start, 1.0, root) * igate * lru
                rate_ref[row, at, :] = rate
                igate_ref[row, at, :] = igate
                for shift in (1, 2, 4):
                    live = place >= shift
                    value = value + cum * jnp.where(live, pltpu.roll(value, shift, 0), 0.0)
                    cum = cum * jnp.where(live, pltpu.roll(cum, shift, 0), 1.0)
                value = value + cum * run_state
                cum = cum * run_cum
                state_ref[row, at, :] = value
                cum_ref[row, at, :] = cum
                run_state = value[SUBLANES - 1 :, :]
                run_cum = cum[SUBLANES - 1 :, :]
            later.append((run_cum, run_state))
        return tuple(later)

    one, zero = (jnp.ones((1, width), jnp.float32), jnp.zeros((1, width), jnp.float32))
    done = lax.fori_loop(0, length // span, scan_step, tuple((one, zero) for _ in range(rows)))
    for row in range(rows):
        for place in range(2):
            last_ref[row, place : place + 1, :] = done[row][place]


def carried(sent_ref, got_ref, out_ref, send_sem, recv_sem, backward):
    seq, count = (lax.axis_index("seq"), lax.axis_size("seq"))

    def other(step):
        return {"seq": lax.rem(seq + step, count)}

    barrier = pltpu.get_barrier_semaphore()
    for step in range(1, count):
        pl.semaphore_signal(barrier, inc=1, device_id=other(step), device_id_type=MESH)
    pl.semaphore_wait(barrier, count - 1)
    copies = [
        pltpu.make_async_remote_copy(
            src_ref=sent_ref,
            dst_ref=got_ref.at[seq],
            send_sem=send_sem.at[step - 1],
            recv_sem=recv_sem.at[step - 1],
            device_id=other(step),
            device_id_type=MESH,
        )
        for step in range(1, count)
    ]
    for copy in copies:
        copy.start()
    got_ref[seq] = sent_ref[...]
    for copy in copies:
        copy.wait()
    for row in range(sent_ref.shape[0]):
        total = jnp.zeros(out_ref.shape[1:], jnp.float32)
        for place in range(count - 1, 0, -1) if backward else range(count - 1):
            longer = got_ref[place, row, 0:1, :] * total + got_ref[place, row, 1:2, :]
            total = jnp.where(place > seq if backward else place < seq, longer, total)
        out_ref[row] = total


def adjoint_kernel(rows, *refs):
    (dmix_ref, pre_ref, state_ref, cum_ref, carry_ref, rate_ref, dist_ref, par_ref), outs = by_rows(
        refs, rows, (False, True, True, True, False, True, False, False)
    )
    dgate_ref, local_ref, back_ref, first_ref = outs
    _, length, width = dmix_ref.shape
    soft = par_ref[7:8, :]
    place = lax.broadcasted_iota(jnp.int32, (SUBLANES, width), 0)
    last = length // STEP - 1

    def step(index, carry):
        base = pl.multiple_of((last - index) * STEP, STEP)
        later = []
        for row in range(rows):
            run_cum, run_back = carry[row]
            entering = carry_ref[row]
            pieces = []
            for half in reversed(range(STEP // SUBLANES)):
                at = pl.ds(base + half * SUBLANES, SUBLANES)
                start = across(dist_ref[row, at, :], width) == 0
                state = state_ref[row, at, :] + cum_ref[row, at, :] * entering
                act, slope = gelu_pair(pre_ref[row, at, :])
                dmix = dmix_ref[row, at, :]
                pieces.append(dmix * state * slope)
                dstate = dmix * act
                coef = jnp.where(start, 0.0, jnp.exp(rate_ref[row, at, :] * soft))
                value = coef * dstate
                for shift in (1, 2, 4):
                    live = place < SUBLANES - shift
                    turn = SUBLANES - shift
                    value = value + coef * jnp.where(live, pltpu.roll(value, turn, 0), 0.0)
                    coef = coef * jnp.where(live, pltpu.roll(coef, turn, 0), 1.0)
                value = value + coef * run_back
                coef = coef * run_cum
                inside = place < SUBLANES - 1
                local_ref[row, at, :] = dstate + jnp.where(
                    inside, pltpu.roll(value, SUBLANES - 1, 0), run_back
                )
                back_ref[row, at, :] = jnp.where(inside, pltpu.roll(coef, SUBLANES - 1, 0), run_cum)
                run_back = value[:1, :]
                run_cum = coef[:1, :]
            dgate_ref[row, pl.ds(base, STEP), :] = jnp.concatenate(pieces[::-1], axis=0).astype(
                jnp.bfloat16
            )
            later.append((run_cum, run_back))
        return tuple(later)

    one, zero = (jnp.ones((1, width), jnp.float32), jnp.zeros((1, width), jnp.float32))
    done = lax.fori_loop(0, last + 1, step, tuple((one, zero) for _ in range(rows)))
    for row in range(rows):
        first_ref[row] = done[row][1]


def backward_kernel(head_size, rows, *refs):
    (
        local_ref,
        back_ref,
        first_ref,
        last_ref,
        state_ref,
        cum_ref,
        in_ref,
        rate_ref,
        igate_ref,
        lru_ref,
        dist_ref,
        branch_ref,
        rim_ref,
        par_ref,
        gates_ref,
    ), others = by_rows(
        refs, rows, (False,) * 3 + (True,) * 3 + (False,) + (True,) * 3 + (False,) + (True,) * 2 + (False,) * 2
    )
    dbranch_ref, tail_ref, head_ref, dgates_ref, both_ref, dconv_ref, sums_ref = others[:7]
    leaving_ref, sent_ref, got_ref, send_sem, recv_sem = others[7:]
    _, length, width = local_ref.shape

    @pl.when(pl.program_id(0) == 0)
    def _():
        for row in range(rows):
            sent_ref[row, 0:1, :] = last_ref[row, 0:1, :]
            sent_ref[row, 1:2, :] = first_ref[row]
        carried(sent_ref, got_ref, leaving_ref, send_sem, recv_sem, True)

    block = pl.ds(pl.multiple_of(pl.program_id(0) * width, width), width)
    taps = [par_ref[k : k + 1, :] for k in range(4)]
    soft = par_ref[7:8, :]
    place = lax.broadcasted_iota(jnp.int32, (SUBLANES, width), 0)
    zeros = jnp.zeros((SUBLANES, width), jnp.float32)

    def gate_step(index, carry):
        sums, earlier = carry
        decay_sum, rate_sum, input_sum = sums
        base = pl.multiple_of(index * STEP, STEP)
        later = []
        for row in range(rows):
            before = earlier[row]
            entering = in_ref[row]
            leaving = leaving_ref[row, :, block]
            lru_both = lru_ref[row, pl.ds(base, STEP), :].astype(jnp.float32)
            drates, dinputs = ([], [])
            for half in range(STEP // SUBLANES):
                at = pl.ds(base + half * SUBLANES, SUBLANES)
                lru = lru_both[half * SUBLANES : (half + 1) * SUBLANES]
                start = across(dist_ref[row, at, :], width) == 0
                adjoint = local_ref[row, at, :] + back_ref[row, at, :] * leaving
                state = state_ref[row, at, :] + cum_ref[row, at, :] * entering
                previous = jnp.where(place < 1, before, pltpu.roll(state, 1, 0))
                before = state[SUBLANES - 1 :, :]
                rate = rate_ref[row, at, :]
                igate = igate_ref[row, at, :]
                log_decay = rate * soft
                decay = jnp.exp(log_decay)
                arg = root_argument(log_decay, decay)
                above = arg > ROOT_FLOOR
                arg = jnp.maximum(arg, ROOT_FLOOR)
                inverse = lax.rsqrt(arg)
                scale = jnp.where(start, 1.0, arg * inverse)
                gated = adjoint * igate
                dscale = gated * lru
                pull = jnp.where(above, dscale * decay * decay * inverse, 0.0)
                dlog = jnp.where(start, 0.0, adjoint * previous * decay - pull)
                dig = adjoint * scale * lru
                weighted = dlog * rate
                decay_sum = decay_sum + weighted
                drates.append(weighted * soft * (1.0 - rate))
                dinputs.append(dig * igate * (1.0 - igate))
                dconv_ref[row, at, :] = gated * scale
            drate = jnp.concatenate(drates, axis=0).astype(jnp.bfloat16)
            dinput = jnp.concatenate(dinputs, axis=0).astype(jnp.bfloat16)
            both_ref[row, pl.ds(base, STEP), :width] = drate
            both_ref[row, pl.ds(base, STEP), width:] = dinput
            drate = drate.astype(jnp.float32)
            dinput = dinput.astype(jnp.float32)
            rate_sum = rate_sum + (drate[:SUBLANES] + drate[SUBLANES:])
            input_sum = input_sum + (dinput[:SUBLANES] + dinput[SUBLANES:])
            later.append(before)
        return ((decay_sum, rate_sum, input_sum), tuple(later))

    sums, _ = lax.fori_loop(
        0,
        length // STEP,
        gate_step,
        ((zeros, zeros, zeros), tuple(in_ref[row] for row in range(rows))),
    )
    for slot, total in zip((5, 6, 7), (sums[1], sums[2], sums[0])):
        sums_ref[slot : slot + 1, :] = jnp.sum(total, axis=0, keepdims=True)

    piece = min(length, 256)
    wide = None
    for row in range(rows):

        def dot_step(index, carry, row=row):
            at = pl.ds(pl.multiple_of(index * piece, piece), piece)
            dconv_ref[row, at, :] += lax.dot_general(
                both_ref[row, at, :],
                gates_ref[...],
                (((1,), (1,)), ((), ())),
                preferred_element_type=jnp.float32,
            )
            return carry

        lax.fori_loop(0, length // piece, dot_step, 0)
        part = lax.dot_general(
            lru_ref[row], both_ref[row], (((0,), (0,)), ((), ())), preferred_element_type=jnp.float32
        )
        wide = part if wide is None else wide + part
    row_head = lax.broadcasted_iota(jnp.int32, (width, width), 0) // head_size
    col_head = lax.broadcasted_iota(jnp.int32, (width, width), 1) // head_size
    own = row_head == col_head
    folds = []
    for part in range(2):
        kept = jnp.where(own, wide[:, part * width : (part + 1) * width], 0.0)
        folded = kept
        for other in range(1, width // head_size):
            folded = folded + pltpu.roll(kept, width - other * head_size, 1)
        folds.append(folded[:, :LANES])

    def conv_step(index, carry):
        sums, following = carry
        sums = list(sums)
        base = pl.multiple_of((length // STEP - 1 - index) * STEP, STEP)
        later = []
        for row in range(rows):
            after = following[row]
            pieces = []
            for half in reversed(range(STEP // SUBLANES)):
                at = pl.ds(base + half * SUBLANES, SUBLANES)
                dist = across(dist_ref[row, at, :], width)
                branch = branch_ref[row, at, :]
                here = dconv_ref[row, at, :]
                total = taps[0] * here
                sums[0] = sums[0] + here * branch
                sums[4] = sums[4] + here
                masked = tuple(jnp.where(dist >= k, here, 0.0) for k in range(1, 4))
                for k in range(1, 4):
                    moved = pltpu.roll(
                        jnp.where(place >= k, masked[k - 1], after[k - 1]), SUBLANES - k, 0
                    )
                    total = total + taps[k] * moved
                    sums[k] = sums[k] + branch * moved
                after = masked
                pieces.append(total)
            whole = jnp.concatenate(pieces[::-1], axis=0)
            dbranch_ref[row, pl.ds(base, STEP), :] = whole.astype(jnp.bfloat16)
            later.append(after)

            @pl.when(index == 0)
            def _(row=row, whole=whole):
                tail_ref[row] = whole[STEP - SUBLANES :]

        return (tuple(sums), tuple(later))

    sums, firsts = lax.fori_loop(
        0,
        length // STEP,
        conv_step,
        ((zeros,) * 5, tuple((zeros,) * 3 for _ in range(rows))),
    )
    sums = list(sums)
    for row in range(rows):
        total = zeros
        rim = rim_ref[row]
        for k in range(1, 4):
            moved = pltpu.roll(jnp.where(place >= k, 0.0, firsts[row][k - 1]), SUBLANES - k, 0)
            total = total + taps[k] * moved
            sums[k] = sums[k] + rim * moved
        head_ref[row] = total
    for slot in range(5):
        sums_ref[slot : slot + 1, :] = jnp.sum(sums[slot], axis=0, keepdims=True)
    above = jnp.zeros((head_size, width), jnp.float32)
    below = jnp.zeros((LANES - head_size - SUBLANES, width), jnp.float32)
    turned = jnp.concatenate([above, sums_ref[...], below], axis=0).T
    lane = lax.broadcasted_iota(jnp.int32, (width, LANES), 1)
    dgates_ref[:, :LANES] = jnp.where(lane < head_size, folds[0], turned).astype(dgates_ref.dtype)
    dgates_ref[:, LANES:] = folds[1].astype(dgates_ref.dtype)


def channel_call(
    kernel, name, arrays, specs, outs, out_specs, scratch, blocks, flops, params=()
):
    moved = sum(math.prod(a.shape) * a.dtype.itemsize for a in (*arrays, *outs))
    return pl.pallas_call(
        kernel,
        name=name,
        grid=(blocks,),
        in_specs=specs,
        out_specs=out_specs,
        out_shape=outs,
        scratch_shapes=scratch,
        compiler_params=pltpu.CompilerParams(vmem_limit_bytes=VMEM_BYTES, **dict(params)),
        cost_estimate=pl.CostEstimate(flops=flops, bytes_accessed=moved, transcendentals=0),
    )(*arrays)


class Recurrence:
    def __init__(self, rows, length, channels, head_size):
        self.rows, self.length, self.channels = (rows, length, channels)
        self.head_size = head_size
        self.width = head_size * LANES // math.gcd(head_size, LANES)
        self.blocks = channels // self.width
        self.flops = 2 * rows * length * channels * 2 * self.width

    def tall(self):
        return pl.BlockSpec((self.rows, self.length, self.width), lambda j: (0, 0, j))

    def short(self, size):
        return pl.BlockSpec((self.rows, size, self.width), lambda j: (0, 0, j))

    def apart(self, size):
        return [pl.BlockSpec((1, size, self.width), lambda j: (0, 0, j))] * self.rows

    def whole(self, rows, size):
        return pl.BlockSpec((rows, size, self.channels), lambda j: (0, 0, 0))

    def flat(self, size):
        return pl.BlockSpec((size, self.width), lambda j: (0, j))

    def dist(self):
        return pl.BlockSpec((self.rows, self.length, LANES), lambda j: (0, 0, 0))

    def gates(self, columns):
        return pl.BlockSpec((self.width, columns), lambda j: (j, 0))

    def shape(self, size, dtype):
        return jax.ShapeDtypeStruct((self.rows, size, self.channels), dtype)

    def widen(self, lru_gates):
        size, width = (self.head_size, self.width)
        heads = width // size
        column = jnp.arange(2 * width)
        source = (column // width) * size + column % size
        spread = (jnp.arange(2 * size)[:, None] == source[None, :]).astype(jnp.bfloat16)
        owner = (column % width) // size
        mine = (jnp.arange(self.channels) // size) % heads
        wide = jnp.dot(lru_gates, spread, preferred_element_type=jnp.float32)
        return jnp.where(mine[:, None] == owner[None, :], wide, 0.0).astype(jnp.bfloat16)

    def forward(self, branch, rim, dist, params, gates):
        f32 = jnp.float32
        outs = [self.shape(self.length, d) for d in (jnp.bfloat16, f32, f32, f32, f32)]
        return channel_call(
            forward_kernel,
            "recurrence_forward",
            (branch, rim, dist, params, gates),
            [self.tall(), self.short(SUBLANES), self.dist(), self.flat(16), self.gates(2 * self.width)],
            outs + [self.shape(2, f32)],
            [self.tall()] * 5 + [self.short(2)],
            [pltpu.VMEM((self.rows, self.length, 2 * self.width), f32)],
            self.blocks,
            self.flops,
        )

    def adjoint(self, dmix, pre, state, cum, entering, rate, dist, params):
        f32 = jnp.float32
        outs = [self.shape(self.length, d) for d in (jnp.bfloat16, f32, f32)] + [self.shape(1, f32)]
        tall, apart = (self.tall(), self.apart(self.length))
        return channel_call(
            functools.partial(adjoint_kernel, self.rows),
            "recurrence_adjoint",
            (dmix, *pre, *state, *cum, entering, *rate, dist, params),
            [tall, *apart * 3, self.short(1), *apart, self.dist(), self.flat(16)],
            outs,
            [tall, tall, tall, self.short(1)],
            [],
            self.blocks,
            0,
        )

    def backward(
        self, local, back, first, last, state, cum, entering, rate, igate, lru, dist, branch, rim, params, gates
    ):
        f32 = jnp.float32
        outs = [
            self.shape(self.length, jnp.bfloat16),
            self.shape(SUBLANES, f32),
            self.shape(SUBLANES, f32),
            jax.ShapeDtypeStruct((self.channels, 2 * LANES), jnp.bfloat16),
        ]
        tall, apart = (self.tall(), self.apart(self.length))
        seqs = lax.axis_size("seq")
        summary = (self.rows, 2, self.channels)
        return channel_call(
            functools.partial(backward_kernel, self.head_size, self.rows),
            "recurrence_backward",
            (local, back, first, *last, *state, *cum, entering, *rate, *igate, *lru, dist, *branch, *rim)
            + (params, gates),
            [tall, tall, self.whole(self.rows, 1), *[self.whole(1, 2)] * self.rows, *apart * 2]
            + [self.short(1), *apart * 3, self.dist(), *apart, *self.apart(SUBLANES)]
            + [self.flat(16), self.gates(2 * self.width)],
            outs,
            [tall, self.short(SUBLANES), self.short(SUBLANES), self.gates(2 * LANES)],
            [
                pltpu.VMEM((self.rows, self.length, 2 * self.width), jnp.bfloat16),
                pltpu.VMEM((self.rows, self.length, self.width), f32),
                pltpu.VMEM((SUBLANES, self.width), f32),
                pltpu.VMEM((self.rows, 1, self.channels), f32),
                pltpu.VMEM(summary, f32),
                pltpu.VMEM((seqs,) + summary, f32),
                pltpu.SemaphoreType.DMA((seqs - 1,)),
                pltpu.SemaphoreType.DMA((seqs - 1,)),
            ],
            self.blocks,
            2 * self.flops,
            {"collective_id": 5, "has_side_effects": True},
        )


def gathered(parts_ref, at):
    return jnp.concatenate([parts_ref[k, at, :] for k in range(parts_ref.shape[0])], axis=1)


def front_kernel(
    parts_ref,
    gain_ref,
    input_ref,
    gate_ref,
    x_ref,
    inverse_ref,
    normed_ref,
    branch_ref,
    pre_ref,
    rim_ref,
    edge_ref,
    landed_ref,
    send_sem,
    recv_sem,
):
    tokens = x_ref.shape[0]
    piece, tall = (64, min(tokens, 512))
    step, steps = (pl.program_id(0), edge_ref.shape[0])
    seq, seqs = (lax.axis_index("seq"), lax.axis_size("seq"))
    barrier = pltpu.get_barrier_semaphore()

    @pl.when(step == 0)
    def _():
        before = {"seq": lax.rem(seq + seqs - 1, seqs)}
        pl.semaphore_signal(barrier, inc=1, device_id=before, device_id_type=MESH)

        def norm(index, carry):
            at = pl.ds(pl.multiple_of(index * piece, piece), piece)
            low = gathered(parts_ref, at)
            x_ref[at, :] = low
            value = low.astype(jnp.float32)
            inverse = lax.rsqrt(jnp.mean(value * value, axis=1, keepdims=True) + EPS)
            inverse_ref[at, :] = jnp.broadcast_to(inverse, (piece, LANES))
            normed_ref[at, :] = (value * inverse * gain_ref[...]).astype(jnp.bfloat16)
            return carry

        lax.fori_loop(0, tokens // piece, norm, 0)

    def multiply(index, carry):
        at = pl.ds(pl.multiple_of(index * tall, tall), tall)
        normed = normed_ref[at, :]
        branch_ref[at, :] = jnp.dot(normed, input_ref[...], preferred_element_type=jnp.float32)
        pre_ref[at, :] = jnp.dot(normed, gate_ref[...], preferred_element_type=jnp.float32)
        return carry

    lax.fori_loop(0, tokens // tall, multiply, 0)
    edge_ref[step] = branch_ref[tokens - SUBLANES :, :]

    def rim_copy(place):
        return pltpu.make_async_remote_copy(
            src_ref=edge_ref.at[place],
            dst_ref=landed_ref.at[place],
            send_sem=send_sem.at[place],
            recv_sem=recv_sem.at[place],
            device_id={"seq": lax.rem(seq + 1, seqs)},
            device_id_type=MESH,
        )

    @pl.when(step == 0)
    def _():
        pl.semaphore_wait(barrier, 1)

    rim_copy(step).start()

    @pl.when(step == steps - 1)
    def _():
        columns = edge_ref.shape[2]
        live = jnp.where(seq > 0, 1.0, 0.0)
        for place in range(steps):
            rim_copy(place).wait()
            rim_ref[:, place * columns : (place + 1) * columns] = live * landed_ref[place]


def front(parts, gain, recur_input, recur_gate):
    count, tokens, width = parts.shape
    model, rec = recur_input.shape
    columns = 4 * LANES
    steps = rec // columns
    low, f32 = (jnp.bfloat16, jnp.float32)
    tall = pl.BlockSpec((model, columns), lambda j: (0, j))
    wide = pl.BlockSpec((tokens, columns), lambda j: (0, j))

    def whole(shape):
        return pl.BlockSpec(shape, lambda j: (0,) * len(shape))

    return pl.pallas_call(
        front_kernel,
        name="norm_and_project",
        grid=(steps,),
        in_specs=[whole(parts.shape), whole((1, model)), tall, tall],
        out_specs=[whole((tokens, model)), whole((tokens, LANES)), whole((tokens, model)), wide, wide]
        + [whole((SUBLANES, rec))],
        out_shape=[
            jax.ShapeDtypeStruct((tokens, model), low),
            jax.ShapeDtypeStruct((tokens, LANES), f32),
            jax.ShapeDtypeStruct((tokens, model), low),
            jax.ShapeDtypeStruct((tokens, rec), f32),
            jax.ShapeDtypeStruct((tokens, rec), f32),
            jax.ShapeDtypeStruct((SUBLANES, rec), f32),
        ],
        scratch_shapes=[
            pltpu.VMEM((steps, SUBLANES, columns), f32),
            pltpu.VMEM((steps, SUBLANES, columns), f32),
            pltpu.SemaphoreType.DMA((steps,)),
            pltpu.SemaphoreType.DMA((steps,)),
        ],
        compiler_params=pltpu.CompilerParams(
            collective_id=3, has_side_effects=True, vmem_limit_bytes=VMEM_BYTES
        ),
        cost_estimate=pl.CostEstimate(
            flops=4 * tokens * model * rec, bytes_accessed=20 * tokens * model, transcendentals=0
        ),
    )(parts, gain[None], recur_input, recur_gate)


def middle_kernel(rows, *refs):
    (last_ref, state_ref, cum_ref, pre_ref, x_ref, out_ref, gain_ref), others = by_rows(
        refs, rows, (True,) * 5 + (False,) * 2
    )
    entering_ref, mixed_ref, resid_ref, normed_ref = others[:4]
    sent_ref, got_ref, send_sem, recv_sem = others[4:]
    tall, model = resid_ref.shape
    step = pl.program_id(0)
    tiles = pl.num_programs(0) // rows
    slab = 16

    @pl.when(step == 0)
    def _():
        for row in range(rows):
            sent_ref[row] = last_ref[row]
        carried(sent_ref, got_ref, entering_ref, send_sem, recv_sem, False)

    for row in range(rows):

        @pl.when(lax.div(step, tiles) == row)
        def _(row=row):
            def mix(index, carry):
                at = pl.ds(pl.multiple_of(index * slab, slab), slab)
                state = state_ref[row, at, :] + cum_ref[row, at, :] * entering_ref[row]
                pre = pre_ref[row, at, :]
                inner = jnp.tanh(pre * (GELU_C + (GELU_C * GELU_A) * (pre * pre)))
                mixed_ref[at, :] = (state * (pre * (0.5 + 0.5 * inner))).astype(jnp.bfloat16)
                return carry

            lax.fori_loop(0, tall // slab, mix, 0)
            tile = 512
            for first in range(0, model, tile):
                at = slice(first, first + tile)
                resid_ref[:, at] = x_ref.refs[row][:, at].astype(jnp.float32) + jnp.dot(
                    mixed_ref[...], out_ref[:, at], preferred_element_type=jnp.float32
                )

    def norm(index, carry):
        at = pl.ds(pl.multiple_of(index * slab, slab), slab)
        resid = resid_ref[at, :]
        inverse = lax.rsqrt(jnp.mean(resid * resid, axis=1, keepdims=True) + EPS)
        normed_ref[at, :] = (resid * inverse * gain_ref[...]).astype(jnp.bfloat16)
        return carry

    lax.fori_loop(0, tall // slab, norm, 0)


def middle(last, state, cum, pre, x, recur_out, gain):
    rows = len(state)
    _, length, rec = state[0].shape
    model = recur_out.shape[1]
    tall = min(length, 256)
    tiles = length // tall
    tokens = rows * length
    seqs = lax.axis_size("seq")
    low, f32 = (jnp.bfloat16, jnp.float32)

    def whole(shape):
        return pl.BlockSpec(shape, lambda s: (0,) * len(shape), pipeline_mode=pl.Buffered(1))

    def part(row):
        return lambda s: (0, jnp.clip(s - row * tiles, 0, tiles - 1), 0)

    def flat(row):
        return lambda s: (jnp.clip(s - row * tiles, 0, tiles - 1), 0)

    apart = [pl.BlockSpec((1, tall, rec), part(row)) for row in range(rows)]
    summary = (rows, 2, rec)
    return pl.pallas_call(
        functools.partial(middle_kernel, rows),
        name="mix_and_norm",
        grid=(rows * tiles,),
        in_specs=[whole((1, 2, rec))] * rows
        + apart * 3
        + [pl.BlockSpec((tall, model), flat(row)) for row in range(rows)]
        + [whole(recur_out.shape), whole((1, model))],
        out_specs=[
            pl.BlockSpec((rows, 1, rec), lambda s: (0, 0, 0)),
            pl.BlockSpec((tall, rec), lambda s: (s, 0)),
            pl.BlockSpec((tall, model), lambda s: (s, 0)),
            pl.BlockSpec((tall, model), lambda s: (s, 0)),
        ],
        out_shape=[
            jax.ShapeDtypeStruct((rows, 1, rec), f32),
            jax.ShapeDtypeStruct((tokens, rec), low),
            jax.ShapeDtypeStruct((tokens, model), f32),
            jax.ShapeDtypeStruct((tokens, model), low),
        ],
        scratch_shapes=[
            pltpu.VMEM(summary, f32),
            pltpu.VMEM((seqs,) + summary, f32),
            pltpu.SemaphoreType.DMA((seqs - 1,)),
            pltpu.SemaphoreType.DMA((seqs - 1,)),
        ],
        compiler_params=pltpu.CompilerParams(
            collective_id=4, has_side_effects=True, vmem_limit_bytes=VMEM_BYTES
        ),
        cost_estimate=pl.CostEstimate(
            flops=2 * tokens * rec * model, bytes_accessed=14 * tokens * rec, transcendentals=0
        ),
    )(*last, *state, *cum, *pre, *x, recur_out, gain[None])


def mlp_kernel(
    left_ref,
    parts_ref,
    normed_ref,
    resid_ref,
    gain_ref,
    gate_ref,
    up_ref,
    down_ref,
    gout_ref,
    hidden_ref,
    dgate_ref,
    dup_ref,
    result_ref,
    dres_ref,
    total_ref,
    back_ref,
):
    tokens, model = normed_ref.shape
    chunk = down_ref.shape[0]
    rows = left_ref.shape[0]
    length = tokens // rows
    step = pl.program_id(0)
    slab = 32

    @pl.when(step == 0)
    def _():
        for row in range(rows):

            def collect(index, carry, row=row):
                base = pl.multiple_of(index * slab, slab)
                at = pl.ds(row * length + base, slab)
                low = gathered(parts_ref, at)
                place = base + lax.broadcasted_iota(jnp.int32, low.shape, 0)
                value = jnp.where(place < left_ref[row], low.astype(jnp.float32), 0.0)
                gout_ref[at, :] = value.astype(jnp.bfloat16)
                total_ref[at, :] = resid_ref[at, :]
                back_ref[at, :] = jnp.zeros((slab, model), jnp.float32)
                return carry

            lax.fori_loop(0, length // slab, collect, 0)

    tall = min(tokens, 512)
    wide = 256

    def tile(index, carry):
        at = pl.ds(pl.multiple_of(index * tall, tall), tall)
        for column in range(chunk // wide):
            own = slice(column * wide, (column + 1) * wide)
            gate = jnp.dot(normed_ref[at, :], gate_ref[:, own], preferred_element_type=jnp.float32)
            up = jnp.dot(normed_ref[at, :], up_ref[:, own], preferred_element_type=jnp.float32)
            dhid = lax.dot_general(
                gout_ref[at, :],
                down_ref[own, :],
                (((1,), (1,)), ((), ())),
                preferred_element_type=jnp.float32,
            )
            act, slope = gelu_pair(gate)
            hidden_ref[at, own] = (act * up).astype(jnp.bfloat16)
            dgate_ref[at, own] = (dhid * up * slope).astype(jnp.bfloat16)
            dup_ref[at, own] = (dhid * act).astype(jnp.bfloat16)
        for column in range(model // (2 * wide)):
            own = slice(column * 2 * wide, (column + 1) * 2 * wide)
            total_ref[at, own] += jnp.dot(
                hidden_ref[at, :], down_ref[:, own], preferred_element_type=jnp.float32
            )
            back_ref[at, own] += lax.dot_general(
                dgate_ref[at, :],
                gate_ref[own, :],
                (((1,), (1,)), ((), ())),
                preferred_element_type=jnp.float32,
            ) + lax.dot_general(
                dup_ref[at, :],
                up_ref[own, :],
                (((1,), (1,)), ((), ())),
                preferred_element_type=jnp.float32,
            )
        return carry

    lax.fori_loop(0, tokens // tall, tile, 0)

    @pl.when(step == pl.num_programs(0) - 1)
    def _():
        parts, width = (result_ref.shape[0], result_ref.shape[2])
        small = 16

        def finish(index, carry):
            at = pl.ds(pl.multiple_of(index * small, small), small)
            result = total_ref[at, :].astype(jnp.bfloat16)
            for part in range(parts):
                result_ref[part, at, :] = result[:, part * width : (part + 1) * width]
            resid = resid_ref[at, :]
            inverse = lax.rsqrt(jnp.mean(resid * resid, axis=1, keepdims=True) + EPS)
            normed = resid * inverse
            scaled = back_ref[at, :] * gain_ref[...]
            mean = jnp.mean(scaled * normed, axis=1, keepdims=True)
            dres = gout_ref[at, :].astype(jnp.float32) + inverse * (scaled - normed * mean)
            dres_ref[at, :] = dres.astype(jnp.bfloat16)
            return carry

        lax.fori_loop(0, tokens // small, finish, 0)


def mlp(left, parts, normed, resid, gain, mlp_gate, mlp_up, mlp_down):
    tokens, model = normed.shape
    ffn = mlp_gate.shape[1]
    chunk = 768
    low, f32 = (jnp.bfloat16, jnp.float32)

    def whole(shape):
        return pl.BlockSpec(shape, lambda s: (0,) * len(shape), pipeline_mode=pl.Buffered(1))

    columns = pl.BlockSpec((model, chunk), lambda s: (0, s))
    made = pl.BlockSpec((tokens, chunk), lambda s: (0, s))
    tall = jax.ShapeDtypeStruct((tokens, ffn), low)
    square = jax.ShapeDtypeStruct((tokens, model), low)
    return pl.pallas_call(
        mlp_kernel,
        name="mlp_forward_backward",
        grid=(ffn // chunk,),
        in_specs=[
            pl.BlockSpec(memory_space=pltpu.SMEM),
            whole(parts.shape),
            whole(normed.shape),
            whole(resid.shape),
            whole((1, model)),
            columns,
            columns,
            pl.BlockSpec((chunk, model), lambda s: (s, 0)),
        ],
        out_specs=[
            whole((tokens, model)),
            made,
            made,
            made,
            whole(parts.shape),
            whole((tokens, model)),
        ],
        out_shape=[square, tall, tall, tall, jax.ShapeDtypeStruct(parts.shape, low), square],
        scratch_shapes=[pltpu.VMEM((tokens, model), f32), pltpu.VMEM((tokens, model), f32)],
        compiler_params=pltpu.CompilerParams(vmem_limit_bytes=VMEM_BYTES),
        cost_estimate=pl.CostEstimate(
            flops=12 * tokens * model * ffn,
            bytes_accessed=6 * (model + tokens) * ffn + 14 * tokens * model,
            transcendentals=0,
        ),
    )(left, parts, normed, resid, gain[None], mlp_gate, mlp_up, mlp_down)


def spread_kernel(whole_ref, out_ref):
    out_ref[0] = whole_ref[...]


def spread(whole, count):
    tokens, width = (whole.shape[0], whole.shape[1] // count)
    return pl.pallas_call(
        spread_kernel,
        name="spread_features",
        grid=(count,),
        in_specs=[pl.BlockSpec((tokens, width), lambda j: (0, j))],
        out_specs=pl.BlockSpec((1, tokens, width), lambda j: (j, 0, 0)),
        out_shape=jax.ShapeDtypeStruct((count, tokens, width), whole.dtype),
        cost_estimate=pl.CostEstimate(
            flops=0, bytes_accessed=4 * tokens * whole.shape[1], transcendentals=0
        ),
    )(whole)


CHAN = ("zed", "core")


def features_in(local, pick=slice(None)):
    count = lax.axis_size(CHAN)
    rows, length, width = local.shape
    local = local.reshape(count, rows // count, length, width)[:, pick]
    if width % LANES == 0:
        return lax.all_to_all(local, CHAN, 0, 0, tiled=True).reshape(count, -1, width)
    moved = lax.all_to_all(
        local.reshape(-1, length, width), CHAN, split_axis=0, concat_axis=2, tiled=True
    )
    return moved.reshape(1, -1, count * width)


def features_apart(whole):
    count = lax.axis_size(CHAN)
    if (whole.shape[1] // count) % LANES == 0:
        return spread(whole, count)
    return whole[None]


def features_out(parts, rows):
    blocks, tokens, width = parts.shape
    parts = parts.reshape(blocks, rows, tokens // rows, width)
    if blocks > 1:
        moved = lax.all_to_all(parts, CHAN, 0, 0, tiled=True)
        return moved.reshape(-1, *parts.shape[2:])
    return lax.all_to_all(parts[0], CHAN, split_axis=2, concat_axis=0, tiled=True)


class Corners:
    def __init__(self, seq, zed):
        self.seq_bits, self.zed_bits = (seq.bit_length() - 1, zed.bit_length() - 1)
        self.count = self.seq_bits + self.zed_bits
        self.dims = (2,) * self.count
        self.low = tuple(range(self.seq_bits))[::-1] + tuple(range(self.seq_bits, self.count))[::-1]
        self.high = tuple(range(self.seq_bits)) + tuple(range(self.seq_bits, self.count))[::-1]

    def place(self, dim):
        if dim < self.seq_bits:
            return ("seq", 2 ** (self.seq_bits - 1 - dim))
        return ("zed", 2 ** (self.count - 1 - dim))

    def bit(self, dim):
        axis, weight = self.place(dim)
        return lax.rem(lax.div(lax.axis_index(axis), weight), 2)

    def partner(self, dim):
        axis, weight = self.place(dim)
        return {axis: lax.axis_index(axis) + weight * (1 - 2 * self.bit(dim))}


def tail_kernel(
    corners,
    orders,
    dgate_hbm,
    dbranch_hbm,
    ending_ref,
    leading_ref,
    mixed_hbm,
    dres_hbm,
    gain_ref,
    input_hbm,
    gate_hbm,
    small_hbm,
    *refs,
):
    rows = ending_ref.shape[0]
    normed_hbms, x_hbms, inverse_hbms = (refs[k * rows : (k + 1) * rows] for k in range(3))
    tokens_ref, sum_gate, sum_out, sum_in, sum_small = refs[3 * rows : 3 * rows + 5]
    refs = refs[3 * rows + 5 :]
    stages = corners.count + 1
    dgate, dbranch, mixed, dres, normed, x, inverse, weight_in, weight_gate = refs[:9]
    made_in, made_out, own_small, back, parts, rim = refs[9:15]
    slots_in, slots_out, slots_small = (
        refs[15 + k * stages : 15 + (k + 1) * stages] for k in range(3)
    )
    (
        send_sem,
        recv_sem,
        load_sem,
        move_send,
        move_recv,
        keep_sem,
        rim_send,
        rim_recv,
    ) = refs[15 + 3 * stages :]
    seq, zed, core = (lax.axis_index(axis) for axis in ("seq", "zed", "core"))
    seqs, group = (lax.axis_size("seq"), 2 * lax.axis_size("zed"))
    mine = zed * 2 + core
    length = tokens_ref.shape[1]
    model = x.shape[1]

    def member(index):
        return {"zed": lax.div(index, 2), "core": lax.rem(index, 2)}

    def by_row(sources, target):
        return [
            (source, target.at[pl.ds(row * length, length)]) for row, source in enumerate(sources)
        ]

    early = [
        (dbranch_hbm, dbranch),
        (input_hbm, weight_in),
        (dgate_hbm, dgate),
        (gate_hbm, weight_gate),
        (dres_hbm, dres),
        *by_row(x_hbms, x),
        *by_row(inverse_hbms, inverse),
    ]
    late = [
        *by_row(normed_hbms, normed),
        (mixed_hbm, mixed),
        (small_hbm.at[(slice(None),) * corners.count + (core,)], own_small),
    ]
    loads = [
        pltpu.make_async_copy(source, target, load_sem.at[place])
        for place, (source, target) in enumerate(early + late)
    ]
    for load in loads:
        load.start()

    barrier = pltpu.get_barrier_semaphore()
    for other in range(1, group):
        pl.semaphore_signal(
            barrier, inc=1, device_id=member(lax.rem(mine + other, group)), device_id_type=MESH
        )
    for other in range(1, seqs):
        pl.semaphore_signal(
            barrier, inc=1, device_id={"seq": lax.rem(seq + other, seqs)}, device_id_type=MESH
        )
    pl.semaphore_wait(barrier, group - 1 + seqs - 1)

    rim_copy = pltpu.make_async_remote_copy(
        src_ref=leading_ref,
        dst_ref=rim,
        send_sem=rim_send,
        recv_sem=rim_recv,
        device_id={"seq": lax.rem(seq + seqs - 1, seqs)},
        device_id_type=MESH,
    )
    rim_copy.start()

    def own(stream, index):
        if stream < 4:
            return made_in.at[(stream,) + index + (core,)]
        if stream < 6:
            return made_out.at[(stream - 4,) + index + (core,)]
        return own_small.at[index]

    def slot(stream, stage):
        if stream < 4:
            return slots_in[stage].at[stream]
        if stream < 6:
            return slots_out[stage].at[stream - 4]
        return slots_small[stage]

    def copy(stream, stage):
        order = orders[stream]
        every = (slice(None),) * corners.count
        if stage == 0:
            if stream < 4:
                source = made_in.at[(stream,) + every + (1 - core,)]
            elif stream < 6:
                source = made_out.at[(stream - 4,) + every + (1 - core,)]
            else:
                source = small_hbm.at[every + (1 - core,)]
            target = {"core": 1 - core}
        else:
            dim = order[stage - 1]
            fixed = {before: corners.bit(before) for before in order[: stage - 1]}
            fixed[dim] = 1 - corners.bit(dim)
            source = own(stream, tuple(fixed.get(d, slice(None)) for d in range(corners.count)))
            target = corners.partner(dim)
        return pltpu.make_async_remote_copy(
            src_ref=source,
            dst_ref=slot(stream, stage),
            send_sem=send_sem.at[stream, stage],
            recv_sem=recv_sem.at[stream, stage],
            device_id=target,
            device_id_type=MESH,
        )

    sums = [
        sum_gate.at[:, : sum_gate.shape[1] // 2],
        sum_gate.at[:, sum_gate.shape[1] // 2 :],
        sum_in.at[:, : sum_in.shape[1] // 2],
        sum_in.at[:, sum_in.shape[1] // 2 :],
        sum_out.at[:, : sum_out.shape[1] // 2],
        sum_out.at[:, sum_out.shape[1] // 2 :],
        sum_small,
    ]

    def advance(stream, stage):
        order = orders[stream]
        copy(stream, stage).wait_recv()
        left = [dim for dim in range(corners.count) if dim not in order[:stage]]
        fixed = {dim: corners.bit(dim) for dim in order[:stage]}
        arrived = slot(stream, stage)
        if not left:
            index = tuple(fixed[dim] for dim in range(corners.count))
            sums[stream][...] = own(stream, index)[...].astype(jnp.float32) + arrived[...].astype(
                jnp.float32
            )
            return

        def add(index, carry):
            part = {
                dim: lax.rem(lax.div(index, 2 ** (len(left) - 1 - place)), 2)
                for place, dim in enumerate(left)
            }
            kept = own(stream, tuple({**fixed, **part}[dim] for dim in range(corners.count)))
            total = kept[...].astype(jnp.float32) + arrived[
                tuple(part[dim] for dim in left)
            ].astype(jnp.float32)
            kept[...] = total.astype(jnp.bfloat16)
            return carry

        lax.fori_loop(0, 2 ** len(left), add, 0)
        copy(stream, stage + 1).start()

    def move(other, row):
        to = lax.rem(mine + other, group)
        return pltpu.make_async_remote_copy(
            src_ref=parts.at[to, pl.ds(row * length, length)],
            dst_ref=tokens_ref.at[mine * rows + row],
            send_sem=move_send.at[other - 1, row],
            recv_sem=move_recv.at[other - 1, row],
            device_id=member(to),
            device_id_type=MESH,
        )

    def keep(row):
        return pltpu.make_async_copy(
            parts.at[mine, pl.ds(row * length, length)],
            tokens_ref.at[mine * rows + row],
            keep_sem.at[row],
        )

    tile = 256
    width = parts.shape[2]

    def back_row(row):
        at_row = slice(row * length, (row + 1) * length)

        def product(index, carry):
            at = pl.ds(pl.multiple_of(index * tile, tile), tile)
            contract = (((1,), (1,)), ((), ()))
            back[:, at] = lax.dot_general(
                dbranch[at_row, :], weight_in[at, :], contract, preferred_element_type=jnp.float32
            ) + lax.dot_general(
                dgate[at_row, :], weight_gate[at, :], contract, preferred_element_type=jnp.float32
            )
            return carry

        lax.fori_loop(0, model // tile, product, 0)
        slab = 16

        def norm(index, carry):
            base = pl.multiple_of(index * slab, slab)
            at = pl.ds(row * length + base, slab)
            inv = inverse[at, :1]
            value = x[at, :].astype(jnp.float32) * inv
            scaled = back[pl.ds(base, slab), :] * gain_ref[...]
            mean = jnp.mean(scaled * value, axis=1, keepdims=True)
            grad = dres[at, :].astype(jnp.float32) + inv * (scaled - value * mean)
            grad = grad.astype(jnp.bfloat16)
            for part in range(parts.shape[0]):
                parts[part, at, :] = grad[:, part * width : (part + 1) * width]
            return carry

        lax.fori_loop(0, length // slab, norm, 0)
        for other in range(1, group):
            move(other, row).start()
        keep(row).start()

    def weight_product(left, right, made, stream, first):
        columns = made.shape[-1]
        shape = made.shape[1:-1]

        def product(index, carry):
            at = pl.ds(pl.multiple_of(index * tile, tile), tile)
            source = pl.ds(pl.multiple_of(first + index * tile, tile), tile)
            part = lax.dot_general(
                left[...],
                right[:, source],
                (((0,), (0,)), ((), ())),
                preferred_element_type=jnp.float32,
            )
            made[(stream,) + (slice(None),) * len(shape) + (at,)] = part.astype(
                jnp.bfloat16
            ).reshape(shape + (tile,))
            return carry

        lax.fori_loop(0, columns // tile, product, 0)

    for load in loads[:2]:
        load.wait()
    rim_copy.wait()
    live = jnp.where(seq < seqs - 1, 1.0, 0.0)
    for row in range(rows):
        at = slice((row + 1) * length - STEP, (row + 1) * length)
        inside = dbranch[at, :].astype(jnp.float32)
        last = ending_ref[row] + live * rim[row]
        dbranch[at, :] = jnp.concatenate([inside[: STEP - SUBLANES], last], axis=0).astype(
            jnp.bfloat16
        )
    for load in loads[2 : len(early)]:
        load.wait()
    copy(6, 0).start()
    for row in range(rows):
        back_row(row)
    for load in loads[len(early) :]:
        load.wait()
    half = made_in.shape[-1]
    for stream in (0, 1):
        weight_product(normed, dgate, made_in, stream, stream * half)
        copy(stream, 0).start()
    half_out = made_out.shape[-1]
    for stream in (4, 5):
        weight_product(mixed, dres, made_out, stream - 4, (stream - 4) * half_out)
        copy(stream, 0).start()
    for stream in (0, 1, 6):
        advance(stream, 0)
    for stream in (2, 3):
        weight_product(normed, dbranch, made_in, stream, (stream - 2) * half)
        copy(stream, 0).start()
    for stream in (4, 5, 2, 3):
        advance(stream, 0)
    for stage in range(1, stages):
        for stream in (0, 1, 6, 4, 5, 2, 3):
            advance(stream, stage)
    for stage in range(stages):
        for stream in range(7):
            copy(stream, stage).wait_send()
    for row in range(rows):
        for other in range(1, group):
            move(other, row).wait()
        keep(row).wait()


def tail(dgate, dbranch, ending, leading, mixed, dres, gain, w_in, w_gate, small, normed, x, inverse):
    corners = Corners(lax.axis_size("seq"), lax.axis_size("zed"))
    group, devices = (lax.axis_size(CHAN), 2 ** (corners.count + 1))
    tokens, model = dres.shape
    rec = dgate.shape[1]
    rows = ending.shape[0]
    length, width = (tokens // rows, model // group)
    low, f32 = (jnp.bfloat16, jnp.float32)
    stages = corners.count + 1
    in_rows, out_rows = (model // devices, rec // devices)
    small = small.reshape(corners.dims + (2, out_rows, small.shape[1]))
    orders = [corners.low, corners.high] * 3 + [corners.low]

    def slots(lead, shape):
        return [pltpu.VMEM(lead + (2,) * (corners.count - k) + shape, low) for k in range(stages)]

    in_shape, out_shape = ((in_rows, rec // 2), (out_rows, model // 2))
    loaded = (dgate, dbranch, mixed, dres, dres, dres)
    loaded += (jax.ShapeDtypeStruct((tokens, LANES), f32), w_in, w_gate)
    anyplace = pl.BlockSpec(memory_space=pl.ANY)
    vmem = pl.BlockSpec(memory_space=pltpu.VMEM)
    dma = pltpu.SemaphoreType.DMA
    moved = sum(math.prod(a.shape) * a.dtype.itemsize for a in loaded)
    return pl.pallas_call(
        functools.partial(tail_kernel, corners, orders),
        name="tail",
        in_specs=[anyplace, anyplace, vmem, vmem, anyplace, anyplace, vmem]
        + [anyplace] * (3 + 3 * rows),
        out_specs=[anyplace] + [vmem] * 4,
        out_shape=[
            jax.ShapeDtypeStruct((group * rows, length, width), low),
            jax.ShapeDtypeStruct((in_rows, rec), f32),
            jax.ShapeDtypeStruct((out_rows, model), f32),
            jax.ShapeDtypeStruct((in_rows, rec), f32),
            jax.ShapeDtypeStruct(small.shape[-2:], f32),
        ],
        scratch_shapes=[pltpu.VMEM(a.shape, a.dtype) for a in loaded]
        + [
            pltpu.VMEM((4,) + corners.dims + (2,) + in_shape, low),
            pltpu.VMEM((2,) + corners.dims + (2,) + out_shape, low),
            pltpu.VMEM(corners.dims + small.shape[-2:], low),
            pltpu.VMEM((length, model), f32),
            pltpu.VMEM((group, tokens, width), low),
            pltpu.VMEM(leading.shape, leading.dtype),
        ]
        + slots((4,), in_shape)
        + slots((2,), out_shape)
        + slots((), small.shape[-2:])
        + [
            dma((7, stages)),
            dma((7, stages)),
            dma((7 + 3 * rows,)),
            dma((group - 1, rows)),
            dma((group - 1, rows)),
            dma((rows,)),
            dma,
            dma,
        ],
        compiler_params=pltpu.CompilerParams(
            collective_id=1, has_side_effects=True, vmem_limit_bytes=60 * 1024 * 1024
        ),
        cost_estimate=pl.CostEstimate(
            flops=10 * tokens * model * rec, bytes_accessed=2 * moved, transcendentals=0
        ),
    )(dgate, dbranch, ending, leading, mixed, dres, gain[None], w_in, w_gate, small, *normed, *x, *inverse)


def grads_kernel(
    normed_ref,
    dgate_ref,
    dup_ref,
    hidden_ref,
    gout_ref,
    out_ref,
    turned_ref,
    made_wide,
    made_down,
    come_wide,
    come_down,
    send_sem,
    recv_sem,
    store_sem,
):
    step = pl.program_id(0)
    core = lax.axis_index("core")
    other = {"core": 1 - core}
    wide_rows, down_rows = (made_wide.shape[3], made_down.shape[3])
    wides, downs = (come_wide.shape[0], come_down.shape[0])
    total = wides + downs
    down_at = wides * wide_rows

    def exchange(made, come, index, slot):
        return pltpu.make_async_remote_copy(
            src_ref=made.at[lax.rem(index, 2), 1 - core],
            dst_ref=come.at[index],
            send_sem=send_sem.at[slot],
            recv_sem=recv_sem.at[slot],
            device_id=other,
            device_id_type=MESH,
        )

    def store_wide(index):
        return pltpu.make_async_copy(
            come_wide.at[index],
            out_ref.at[:, pl.ds(pl.multiple_of(index * wide_rows, wide_rows), wide_rows)],
            store_sem.at[index],
        )

    def store_down(index):
        chips = come_down.shape[1]
        return pltpu.make_async_copy(
            come_down.at[index],
            out_ref.at[pl.ds(index * chips, chips), pl.ds(down_at, down_rows)],
            store_sem.at[index + wides],
        )

    @pl.when(step == 0)
    def _():
        barrier = pltpu.get_barrier_semaphore()
        pl.semaphore_signal(barrier, inc=1, device_id=other, device_id_type=MESH)
        pl.semaphore_wait(barrier, 1)
        turned_ref[...] = normed_ref[...].T

    def product_wide(source, index):
        made = made_wide.at[lax.rem(index, 2)]
        chips, rows = (made.shape[1], made.shape[2])
        tile = 512

        def column(place, carry):
            at = pl.ds(pl.multiple_of(place * tile, tile), tile)
            part = jnp.dot(turned_ref[...], source[:, at], preferred_element_type=jnp.float32)
            part = part.astype(jnp.bfloat16).reshape(chips, 2, rows, tile)
            made[0, :, :, at] = part[:, 0]
            made[1, :, :, at] = part[:, 1]
            return carry

        lax.fori_loop(0, source.shape[1] // tile, column, 0)

    def product_tall(left, right, made_all, index):
        made = made_all.at[lax.rem(index, 2)]
        chips, rows = (made.shape[1], made.shape[2])
        tile = 512

        def column(place, carry):
            at = pl.ds(pl.multiple_of(place * tile, tile), tile)
            part = lax.dot_general(
                left[...], right[:, at], (((0,), (0,)), ((), ())), preferred_element_type=jnp.float32
            )
            part = part.astype(jnp.bfloat16).reshape(chips, 2, rows, tile)
            made[0, :, :, at] = part[:, 0]
            made[1, :, :, at] = part[:, 1]
            return carry

        lax.fori_loop(0, right.shape[1] // tile, column, 0)

    half = wides // 2

    @pl.when(step < half)
    def _():
        product_wide(dgate_ref, step)

    @pl.when((step >= half) & (step < wides))
    def _():
        product_wide(dup_ref, step)

    @pl.when(step < wides)
    def _():
        exchange(made_wide, come_wide, step, step).start()

    @pl.when((step >= wides) & (step < total))
    def _():
        product_tall(hidden_ref, gout_ref, made_down, step - wides)
        exchange(made_down, come_down, step - wides, step).start()

    def finish(made, come, index, slot, store):
        exchange(made, come, index, slot).wait()
        mine = made.at[lax.rem(index, 2), core]
        arrived = come.at[index]

        def add(chip, carry):
            both = mine[chip].astype(jnp.float32) + arrived[chip].astype(jnp.float32)
            arrived[chip] = both.astype(jnp.bfloat16)
            return carry

        lax.fori_loop(0, come.shape[1], add, 0)
        store(index).start()

    before = step - 1

    @pl.when((before >= 0) & (before < wides))
    def _():
        finish(made_wide, come_wide, before, before, store_wide)

    @pl.when(before >= wides)
    def _():
        finish(made_down, come_down, before - wides, before, store_down)

    @pl.when(step == total)
    def _():
        for index in range(wides):
            store_wide(index).wait()
        for index in range(downs):
            store_down(index).wait()


def block_gradients(normed, dgate, dup, hidden, gout):
    tokens, model = normed.shape
    ffn = hidden.shape[1]
    chips = lax.axis_size("seq") * lax.axis_size("zed")
    devices = 2 * chips
    wide_rows, down_rows = (model // devices, ffn // devices)
    chunk = 768
    wides, downs = (2 * ffn // model, ffn // chunk)
    half = wides // 2
    down_chips = chunk // (2 * down_rows)
    rows = wides * wide_rows + down_rows
    low = jnp.bfloat16

    def whole(array):
        return pl.BlockSpec(array.shape, lambda s: (0, 0), pipeline_mode=pl.Buffered(1))

    def part(columns, first, count):
        return pl.BlockSpec((tokens, columns), lambda s: (0, jnp.clip(s - first, 0, count - 1)))

    total = wides + downs
    flops = 6 * tokens * model * ffn
    arrays = (normed, dgate, dup, hidden, gout)
    moved = sum(math.prod(a.shape) * 2 for a in arrays) + chips * rows * model * 2
    return pl.pallas_call(
        grads_kernel,
        name="block_gradients",
        grid=(total + 1,),
        in_specs=[
            whole(normed),
            part(model, 0, half),
            part(model, half, half),
            part(chunk, wides, downs),
            whole(gout),
        ],
        out_specs=pl.BlockSpec(memory_space=pl.ANY),
        out_shape=jax.ShapeDtypeStruct((chips, rows, model), low),
        scratch_shapes=[
            pltpu.VMEM((model, tokens), low),
            pltpu.VMEM((2, 2, chips, wide_rows, model), low),
            pltpu.VMEM((2, 2, down_chips, down_rows, model), low),
            pltpu.VMEM((wides, chips, wide_rows, model), low),
            pltpu.VMEM((downs, down_chips, down_rows, model), low),
            pltpu.SemaphoreType.DMA((total,)),
            pltpu.SemaphoreType.DMA((total,)),
            pltpu.SemaphoreType.DMA((total,)),
        ],
        compiler_params=pltpu.CompilerParams(
            collective_id=2, has_side_effects=True, vmem_limit_bytes=VMEM_BYTES
        ),
        cost_estimate=pl.CostEstimate(flops=flops, bytes_accessed=moved, transcendentals=0),
    )(*arrays)


def passed_along(value, axis, steps):
    count = lax.axis_size(axis)
    leading, last = (max(0, -steps), min(count, count - steps))
    return lax.ppermute(value, axis, [(source, source + steps) for source in range(leading, last)])


def weight_grad(left, right):
    return lax.dot_general(
        left, right, (((0,), (0,)), ((), ())), preferred_element_type=jnp.float32
    ).astype(jnp.bfloat16)


def back_dot(left, right):
    return lax.dot_general(
        left, right, (((1,), (1,)), ((), ())), preferred_element_type=jnp.float32
    )


def fwd_dot(left, right):
    return jnp.dot(left, right, preferred_element_type=jnp.float32)


def gelu_fn(value):
    return jax.nn.gelu(value, approximate=True)


def norm_back(grad_norm, normed, inverse, gain):
    scaled = grad_norm * gain
    mean_term = jnp.mean(scaled * normed, axis=1, keepdims=True)
    return inverse * (scaled - normed * mean_term)


def scattered(gradient):
    return lax.psum_scatter(
        gradient, ("seq", "zed", "core"), scatter_dimension=0, tiled=True
    ).astype(jnp.float32)


def body(
    tokens,
    cotangent,
    doc_starts,
    lengths,
    norm1_gain,
    recur_input,
    recur_gate,
    conv_kernel,
    conv_bias,
    lru_gates,
    lru_bias,
    lru_decay,
    recur_out,
    norm2_gain,
    mlp_gate,
    mlp_up,
    mlp_down,
):
    count = lax.axis_size(CHAN)
    row_count, block_len = (tokens.shape[0] // count, tokens.shape[1])
    model_dim = tokens.shape[2] * count
    tok_count = row_count * block_len
    rec_width = recur_input.shape[1]
    ffn_width = mlp_gate.shape[1]
    head_count = H
    head_size = rec_width // head_count
    tap_count = conv_kernel.shape[0]
    rim_size = tap_count - 1
    seq_index = lax.axis_index("seq")
    position = seq_index * block_len + jnp.arange(block_len, dtype=jnp.int32)
    bounds = jnp.concatenate([doc_starts, lengths[:, None]], axis=1)
    is_before = bounds[:, None, :] <= position[None, :, None]
    seg_start = jnp.max(jnp.where(is_before, bounds[:, None, :], 0), axis=2)
    dist = jnp.broadcast_to(
        (position[None, :] - seg_start)[:, :, None], (row_count, block_len, LANES)
    )
    soft_decay = jax.nn.softplus(-lru_decay)
    params = jnp.concatenate(
        [
            conv_kernel,
            conv_bias[None],
            lru_bias,
            (-8.0 * soft_decay)[None],
            jnp.zeros((SUBLANES, rec_width), jnp.float32),
        ],
        axis=0,
    )
    core = Recurrence(row_count, block_len, rec_width, head_size)
    wide_gates = core.widen(lru_gates)
    if tokens.shape[2] % LANES == 0:
        blocks = [features_in(tokens, slice(row, row + 1)) for row in range(row_count)]
    else:
        side = features_in(tokens)
        blocks = [side[:, row * block_len : (row + 1) * block_len] for row in range(row_count)]
    single = Recurrence(1, block_len, rec_width, head_size)
    per_row = []
    for row in range(row_count):
        block = blocks[row]
        if row:
            block, _ = lax.optimization_barrier((block, per_row[-1][-1]))
        else:
            block, wide_gates, params, dist = lax.optimization_barrier(
                (block, wide_gates, params, dist)
            )
        low_x, inverse, normed, branch, pre, rim = front(block, norm1_gain, recur_input, recur_gate)
        branch, rim = (branch[None], rim[None])
        scanned = single.forward(branch, rim, dist[row : row + 1], params, wide_gates)
        per_row.append((low_x, inverse, normed, branch, pre[None], rim, *scanned))
    low_x, inverse, normed_low, branch, gate_pre, rim, lru_in, rate, igate, state, cum, last = zip(
        *per_row
    )
    entering, mixed_low, resid_one, normed_low2 = middle(
        last, state, cum, gate_pre, low_x, recur_out, norm2_gain
    )
    cotangent, _ = lax.optimization_barrier((cotangent, low_x[-1]))
    cotangent, resid_one = lax.optimization_barrier((features_in(cotangent), resid_one))
    grad_low, hidden_low, mgate_low, mup_low, result_parts, resid_low = mlp(
        lengths - seq_index * block_len,
        cotangent,
        normed_low2,
        resid_one,
        norm2_gain,
        mlp_gate,
        mlp_up,
        mlp_down,
    )
    output = features_out(result_parts, row_count)
    devices = lax.axis_size(("seq", "zed", "core"))
    own_rows = model_dim // devices
    tiled = own_rows % (2 * SUBLANES) == 0 and tokens.shape[2] % LANES == 0
    if tiled:
        merged = block_gradients(
            normed_low2, mgate_low, mup_low, hidden_low, grad_low
        )
        merged, resid_low = lax.optimization_barrier((merged, resid_low))
        merged = lax.psum_scatter(merged, "seq", scatter_dimension=0, tiled=True)
    grad_mixed = back_dot(resid_low, recur_out)
    gate_low, back_local, back_cum, first_term = core.adjoint(
        grad_mixed.reshape(row_count, block_len, rec_width),
        gate_pre,
        state,
        cum,
        entering,
        rate,
        dist,
        params,
    )
    gate_low = gate_low.reshape(tok_count, rec_width)
    output, back_local = lax.optimization_barrier((output, back_local))
    branch_local, ending, leading, small = core.backward(
        back_local,
        back_cum,
        first_term,
        last,
        state,
        cum,
        entering,
        rate,
        igate,
        lru_in,
        dist,
        branch,
        rim,
        params,
        wide_gates,
    )
    branch_low = branch_local.reshape(tok_count, rec_width)
    if tiled:
        merged, branch_low = lax.optimization_barrier((merged, branch_low))
        merged = lax.psum_scatter(merged, "zed", scatter_dimension=0, tiled=True)
        grad_tokens, sum_rgate, sum_rout, sum_rin, own_small = tail(
            gate_low,
            branch_low,
            ending,
            leading,
            mixed_low,
            resid_low,
            norm1_gain,
            recur_input,
            recur_gate,
            small,
            normed_low,
            low_x,
            inverse,
        )
        own = merged[0].astype(jnp.float32)
        span = ffn_width // model_dim * own_rows

        def unfolded(part):
            return jnp.swapaxes(part.reshape(-1, own_rows, model_dim), 0, 1).reshape(own_rows, -1)

        sum_mgate, sum_mup = (unfolded(own[:span]), unfolded(own[span : 2 * span]))
        sum_down = own[2 * span :]
    else:
        from_next = passed_along(
            leading[:, SUBLANES - rim_size :, :].astype(jnp.bfloat16), "seq", -1
        )
        ending = ending + jnp.pad(
            from_next.astype(jnp.float32), ((0, 0), (SUBLANES - rim_size, 0), (0, 0))
        )
        branch_low = lax.dynamic_update_slice(
            branch_local, ending.astype(jnp.bfloat16), (0, block_len - SUBLANES, 0)
        ).reshape(tok_count, rec_width)
        grad_norm1 = back_dot(branch_low, recur_input) + back_dot(gate_low, recur_gate)
        inv_one = jnp.concatenate(inverse)[:, :1]
        normed_one = jnp.concatenate(low_x).astype(jnp.float32) * inv_one
        normed_low = jnp.concatenate(normed_low)
        input_part = norm_back(grad_norm1, normed_one, inv_one, norm1_gain)
        grad_x = (resid_low.astype(jnp.float32) + input_part).astype(jnp.bfloat16)
        grad_tokens = features_out(features_apart(grad_x), row_count)
        sum_mgate, sum_mup, sum_down, sum_rout, sum_rgate, sum_rin = (
            scattered(weight_grad(left, right))
            for left, right in (
                (normed_low2, mgate_low),
                (normed_low2, mup_low),
                (hidden_low, grad_low),
                (mixed_low, resid_low),
                (normed_low, gate_low),
                (normed_low, branch_low),
            )
        )
        own_small = scattered(small)
    sum_lgates = jnp.concatenate(
        [own_small[:, :head_size], own_small[:, LANES : LANES + head_size]], axis=1
    )
    own_sums = jnp.swapaxes(own_small[:, head_size : head_size + SUBLANES], 0, 1)
    device = lax.axis_index(("seq", "zed", "core"))

    def mine(array, size, axis=0):
        return lax.dynamic_slice_in_dim(array, device * size, size, axis)

    def weighed(weight, gradient):
        return jnp.sum(mine(weight, own_rows).astype(jnp.float32) * gradient, axis=1)

    sum_gain1 = (weighed(recur_input, sum_rin) + weighed(recur_gate, sum_rgate)) / mine(
        norm1_gain, own_rows
    )
    sum_gain2 = (weighed(mlp_gate, sum_mgate) + weighed(mlp_up, sum_mup)) / mine(
        norm2_gain, own_rows
    )
    own_channels = own_sums.shape[1]
    sum_decay = 8.0 * jax.nn.sigmoid(-mine(lru_decay, own_channels)) * own_sums[7]
    return (
        output,
        grad_tokens,
        sum_gain1,
        sum_rin,
        sum_rgate,
        own_sums[:4],
        own_sums[4],
        sum_lgates,
        own_sums[5:7],
        sum_decay,
        sum_rout,
        sum_gain2,
        sum_mgate,
        sum_mup,
        sum_down,
    )


def solution(mesh):
    seq, chan = (mesh.shape["seq"], mesh.shape["chan"])
    chips = jax.sharding.Mesh(mesh.devices.reshape(seq, chan // 2, 2), ("seq", "zed", "core"))
    chan = ("zed", "core")
    every = ("seq", "zed", "core")
    activations = P(None, "seq", chan)
    rows, columns, vector = (P(every, None), P(None, every), P(every))
    return jax.shard_map(
        body,
        mesh=chips,
        in_specs=(activations, activations, P(chan, None), P(chan)) + (P(),) * 13,
        out_specs=(
            activations,
            activations,
            vector,
            rows,
            rows,
            columns,
            vector,
            rows,
            columns,
            vector,
            rows,
            vector,
            rows,
            rows,
            rows,
        ),
        check_vma=False,
    )
```

```python
import functools
import math

import jax
import jax.numpy as jnp
from jax import lax
from jax.experimental import pallas as pl
from jax.experimental.pallas import tpu as pltpu
from jax.sharding import PartitionSpec as P

H = 16


EPS = 1e-06
ROOT_FLOOR = 1e-06
LANES = 128
SUBLANES = 8
STEP = 16
VMEM_BYTES = 56 * 1024 * 1024
MESH = pl.DeviceIdType.MESH


def sigmoid(value):
    return 0.5 * jnp.tanh(0.5 * value) + 0.5


GELU_C = 0.7978845608
GELU_A = 0.044715


def gelu_pair(value):
    square = value * value
    inner = jnp.tanh(value * (GELU_C + (GELU_C * GELU_A) * square))
    half = 0.5 + 0.5 * inner
    slope = GELU_C + (3.0 * GELU_C * GELU_A) * square
    return (value * half, half + 0.5 * value * (1.0 - inner * inner) * slope)


def root_argument(log_decay, decay):
    y = 2.0 * log_decay
    series = 1.0 + y * (0.5 + y * (1.0 / 6.0 + y * (1.0 / 24.0)))
    return jnp.where(y > -0.05, -y * series, 1.0 - decay * decay)


def across(column, width):
    return jnp.concatenate([column] * (width // LANES), axis=1)


class Rows:
    def __init__(self, refs):
        self.refs = refs

    def __getitem__(self, index):
        if not isinstance(index, tuple):
            return self.refs[index][0]
        return self.refs[index[0]][(0,) + index[1:]]


def by_rows(refs, rows, apart):
    found = []
    for split in apart:
        count = rows if split else 1
        found.append(Rows(refs[:count]) if split else refs[0])
        refs = refs[count:]
    return found, refs


def forward_kernel(
    branch_ref,
    rim_ref,
    dist_ref,
    par_ref,
    gates_ref,
    lru_ref,
    rate_ref,
    igate_ref,
    state_ref,
    cum_ref,
    last_ref,
    both_ref,
):
    rows, length, width = branch_ref.shape
    span = 2 * STEP if rows == 1 else STEP
    taps = [par_ref[k : k + 1, :] for k in range(4)]
    conv_bias, rate_bias, input_bias, soft = (par_ref[k : k + 1, :] for k in range(4, 8))
    place = lax.broadcasted_iota(jnp.int32, (SUBLANES, width), 0)

    for row in range(rows):

        def conv_step(index, before, row=row):
            base = pl.multiple_of(index * STEP, STEP)
            pieces = []
            for half in range(STEP // SUBLANES):
                at = pl.ds(base + half * SUBLANES, SUBLANES)
                here = branch_ref[row, at, :]
                dist = across(dist_ref[row, at, :], width)
                total = conv_bias + taps[0] * here
                for k in range(1, 4):
                    shifted = pltpu.roll(jnp.where(place < SUBLANES - k, here, before), k, 0)
                    total = total + taps[k] * jnp.where(dist >= k, shifted, 0.0)
                pieces.append(total)
                before = here
            lru_ref[row, pl.ds(base, STEP), :] = jnp.concatenate(pieces, axis=0).astype(jnp.bfloat16)
            return before

        lax.fori_loop(0, length // STEP, conv_step, rim_ref[row])

        piece = min(length, 256)

        def dot_step(index, carry, row=row):
            at = pl.ds(pl.multiple_of(index * piece, piece), piece)
            both_ref[row, at, :] = jnp.dot(
                lru_ref[row, at, :], gates_ref[...], preferred_element_type=jnp.float32
            )
            return carry

        lax.fori_loop(0, length // piece, dot_step, 0)

    def scan_step(index, carry):
        base = pl.multiple_of(index * span, span)
        later = []
        for row in range(rows):
            run_cum, run_state = carry[row]
            lru_both = lru_ref[row, pl.ds(base, span), :].astype(jnp.float32)
            for half in range(span // SUBLANES):
                at = pl.ds(base + half * SUBLANES, SUBLANES)
                lru = lru_both[half * SUBLANES : (half + 1) * SUBLANES]
                start = across(dist_ref[row, at, :], width) == 0
                rate = sigmoid(both_ref[row, at, :width] + rate_bias)
                igate = sigmoid(both_ref[row, at, width:] + input_bias)
                log_decay = rate * soft
                decay = jnp.exp(log_decay)
                arg = jnp.maximum(root_argument(log_decay, decay), ROOT_FLOOR)
                root = arg * lax.rsqrt(arg)
                cum = jnp.where(start, 0.0, decay)
                value = jnp.where(start, 1.0, root) * igate * lru
                rate_ref[row, at, :] = rate
                igate_ref[row, at, :] = igate
                for shift in (1, 2, 4):
                    live = place >= shift
                    value = value + cum * jnp.where(live, pltpu.roll(value, shift, 0), 0.0)
                    cum = cum * jnp.where(live, pltpu.roll(cum, shift, 0), 1.0)
                value = value + cum * run_state
                cum = cum * run_cum
                state_ref[row, at, :] = value
                cum_ref[row, at, :] = cum
                run_state = value[SUBLANES - 1 :, :]
                run_cum = cum[SUBLANES - 1 :, :]
            later.append((run_cum, run_state))
        return tuple(later)

    one, zero = (jnp.ones((1, width), jnp.float32), jnp.zeros((1, width), jnp.float32))
    done = lax.fori_loop(0, length // span, scan_step, tuple((one, zero) for _ in range(rows)))
    for row in range(rows):
        for place in range(2):
            last_ref[row, place : place + 1, :] = done[row][place]


def carried(sent_ref, got_ref, out_ref, send_sem, recv_sem, backward):
    seq, count = (lax.axis_index("seq"), lax.axis_size("seq"))

    def other(step):
        return {"seq": lax.rem(seq + step, count)}

    barrier = pltpu.get_barrier_semaphore()
    for step in range(1, count):
        pl.semaphore_signal(barrier, inc=1, device_id=other(step), device_id_type=MESH)
    pl.semaphore_wait(barrier, count - 1)
    copies = [
        pltpu.make_async_remote_copy(
            src_ref=sent_ref,
            dst_ref=got_ref.at[seq],
            send_sem=send_sem.at[step - 1],
            recv_sem=recv_sem.at[step - 1],
            device_id=other(step),
            device_id_type=MESH,
        )
        for step in range(1, count)
    ]
    for copy in copies:
        copy.start()
    got_ref[seq] = sent_ref[...]
    for copy in copies:
        copy.wait()
    for row in range(sent_ref.shape[0]):
        total = jnp.zeros(out_ref.shape[1:], jnp.float32)
        for place in range(count - 1, 0, -1) if backward else range(count - 1):
            longer = got_ref[place, row, 0:1, :] * total + got_ref[place, row, 1:2, :]
            total = jnp.where(place > seq if backward else place < seq, longer, total)
        out_ref[row] = total


def adjoint_kernel(rows, *refs):
    (
        dres_ref,
        weight_ref,
        pre_ref,
        state_ref,
        cum_ref,
        carry_ref,
        rate_ref,
        dist_ref,
        par_ref,
    ), outs = by_rows(refs, rows, (False, False, True, True, True, False, True, False, False))
    dgate_ref, local_ref, back_ref, first_ref, dmix_ref = outs
    _, length, width = dmix_ref.shape
    for row in range(rows):
        dmix_ref[row] = lax.dot_general(
            dres_ref[row * length : (row + 1) * length, :],
            weight_ref[...],
            (((1,), (1,)), ((), ())),
            preferred_element_type=jnp.float32,
        )
    soft = par_ref[7:8, :]
    place = lax.broadcasted_iota(jnp.int32, (SUBLANES, width), 0)
    last = length // STEP - 1

    def step(index, carry):
        base = pl.multiple_of((last - index) * STEP, STEP)
        later = []
        for row in range(rows):
            run_cum, run_back = carry[row]
            entering = carry_ref[row]
            pieces = []
            for half in reversed(range(STEP // SUBLANES)):
                at = pl.ds(base + half * SUBLANES, SUBLANES)
                start = across(dist_ref[row, at, :], width) == 0
                state = state_ref[row, at, :] + cum_ref[row, at, :] * entering
                act, slope = gelu_pair(pre_ref[row, at, :])
                dmix = dmix_ref[row, at, :]
                pieces.append(dmix * state * slope)
                dstate = dmix * act
                coef = jnp.where(start, 0.0, jnp.exp(rate_ref[row, at, :] * soft))
                value = coef * dstate
                for shift in (1, 2, 4):
                    live = place < SUBLANES - shift
                    turn = SUBLANES - shift
                    value = value + coef * jnp.where(live, pltpu.roll(value, turn, 0), 0.0)
                    coef = coef * jnp.where(live, pltpu.roll(coef, turn, 0), 1.0)
                value = value + coef * run_back
                coef = coef * run_cum
                inside = place < SUBLANES - 1
                local_ref[row, at, :] = dstate + jnp.where(
                    inside, pltpu.roll(value, SUBLANES - 1, 0), run_back
                )
                back_ref[row, at, :] = jnp.where(inside, pltpu.roll(coef, SUBLANES - 1, 0), run_cum)
                run_back = value[:1, :]
                run_cum = coef[:1, :]
            dgate_ref[row, pl.ds(base, STEP), :] = jnp.concatenate(pieces[::-1], axis=0).astype(
                jnp.bfloat16
            )
            later.append((run_cum, run_back))
        return tuple(later)

    one, zero = (jnp.ones((1, width), jnp.float32), jnp.zeros((1, width), jnp.float32))
    done = lax.fori_loop(0, last + 1, step, tuple((one, zero) for _ in range(rows)))
    for row in range(rows):
        first_ref[row] = done[row][1]


def backward_kernel(head_size, rows, *refs):
    (
        local_ref,
        back_ref,
        first_ref,
        last_ref,
        state_ref,
        cum_ref,
        in_ref,
        rate_ref,
        igate_ref,
        lru_ref,
        dist_ref,
        branch_ref,
        rim_ref,
        par_ref,
        gates_ref,
    ), others = by_rows(
        refs, rows, (False,) * 3 + (True,) * 3 + (False,) + (True,) * 3 + (False,) + (True,) * 2 + (False,) * 2
    )
    dbranch_ref, tail_ref, head_ref, dgates_ref, both_ref, dconv_ref, sums_ref = others[:7]
    leaving_ref, sent_ref, got_ref, send_sem, recv_sem = others[7:]
    _, length, width = local_ref.shape

    @pl.when(pl.program_id(0) == 0)
    def _():
        for row in range(rows):
            sent_ref[row, 0:1, :] = last_ref[row, 0:1, :]
            sent_ref[row, 1:2, :] = first_ref[row]
        carried(sent_ref, got_ref, leaving_ref, send_sem, recv_sem, True)

    block = pl.ds(pl.multiple_of(pl.program_id(0) * width, width), width)
    taps = [par_ref[k : k + 1, :] for k in range(4)]
    soft = par_ref[7:8, :]
    place = lax.broadcasted_iota(jnp.int32, (SUBLANES, width), 0)
    zeros = jnp.zeros((SUBLANES, width), jnp.float32)

    def gate_step(index, carry):
        sums, earlier = carry
        decay_sum, rate_sum, input_sum = sums
        base = pl.multiple_of(index * STEP, STEP)
        later = []
        for row in range(rows):
            before = earlier[row]
            entering = in_ref[row]
            leaving = leaving_ref[row, :, block]
            lru_both = lru_ref[row, pl.ds(base, STEP), :].astype(jnp.float32)
            drates, dinputs = ([], [])
            for half in range(STEP // SUBLANES):
                at = pl.ds(base + half * SUBLANES, SUBLANES)
                lru = lru_both[half * SUBLANES : (half + 1) * SUBLANES]
                start = across(dist_ref[row, at, :], width) == 0
                adjoint = local_ref[row, at, :] + back_ref[row, at, :] * leaving
                state = state_ref[row, at, :] + cum_ref[row, at, :] * entering
                previous = jnp.where(place < 1, before, pltpu.roll(state, 1, 0))
                before = state[SUBLANES - 1 :, :]
                rate = rate_ref[row, at, :]
                igate = igate_ref[row, at, :]
                log_decay = rate * soft
                decay = jnp.exp(log_decay)
                arg = root_argument(log_decay, decay)
                above = arg > ROOT_FLOOR
                arg = jnp.maximum(arg, ROOT_FLOOR)
                inverse = lax.rsqrt(arg)
                scale = jnp.where(start, 1.0, arg * inverse)
                gated = adjoint * igate
                dscale = gated * lru
                pull = jnp.where(above, dscale * decay * decay * inverse, 0.0)
                dlog = jnp.where(start, 0.0, adjoint * previous * decay - pull)
                dig = adjoint * scale * lru
                weighted = dlog * rate
                decay_sum = decay_sum + weighted
                drates.append(weighted * soft * (1.0 - rate))
                dinputs.append(dig * igate * (1.0 - igate))
                dconv_ref[row, at, :] = gated * scale
            drate = jnp.concatenate(drates, axis=0).astype(jnp.bfloat16)
            dinput = jnp.concatenate(dinputs, axis=0).astype(jnp.bfloat16)
            both_ref[row, pl.ds(base, STEP), :width] = drate
            both_ref[row, pl.ds(base, STEP), width:] = dinput
            drate = drate.astype(jnp.float32)
            dinput = dinput.astype(jnp.float32)
            rate_sum = rate_sum + (drate[:SUBLANES] + drate[SUBLANES:])
            input_sum = input_sum + (dinput[:SUBLANES] + dinput[SUBLANES:])
            later.append(before)
        return ((decay_sum, rate_sum, input_sum), tuple(later))

    sums, _ = lax.fori_loop(
        0,
        length // STEP,
        gate_step,
        ((zeros, zeros, zeros), tuple(in_ref[row] for row in range(rows))),
    )
    for slot, total in zip((5, 6, 7), (sums[1], sums[2], sums[0])):
        sums_ref[slot : slot + 1, :] = jnp.sum(total, axis=0, keepdims=True)

    piece = min(length, 256)
    wide = None
    for row in range(rows):

        def dot_step(index, carry, row=row):
            at = pl.ds(pl.multiple_of(index * piece, piece), piece)
            dconv_ref[row, at, :] += lax.dot_general(
                both_ref[row, at, :],
                gates_ref[...],
                (((1,), (1,)), ((), ())),
                preferred_element_type=jnp.float32,
            )
            return carry

        lax.fori_loop(0, length // piece, dot_step, 0)
        part = lax.dot_general(
            lru_ref[row], both_ref[row], (((0,), (0,)), ((), ())), preferred_element_type=jnp.float32
        )
        wide = part if wide is None else wide + part
    row_head = lax.broadcasted_iota(jnp.int32, (width, width), 0) // head_size
    col_head = lax.broadcasted_iota(jnp.int32, (width, width), 1) // head_size
    own = row_head == col_head
    folds = []
    for part in range(2):
        kept = jnp.where(own, wide[:, part * width : (part + 1) * width], 0.0)
        folded = kept
        for other in range(1, width // head_size):
            folded = folded + pltpu.roll(kept, width - other * head_size, 1)
        folds.append(folded[:, :LANES])

    def conv_step(index, carry):
        sums, following = carry
        sums = list(sums)
        base = pl.multiple_of((length // STEP - 1 - index) * STEP, STEP)
        later = []
        for row in range(rows):
            after = following[row]
            pieces = []
            for half in reversed(range(STEP // SUBLANES)):
                at = pl.ds(base + half * SUBLANES, SUBLANES)
                dist = across(dist_ref[row, at, :], width)
                branch = branch_ref[row, at, :]
                here = dconv_ref[row, at, :]
                total = taps[0] * here
                sums[0] = sums[0] + here * branch
                sums[4] = sums[4] + here
                masked = tuple(jnp.where(dist >= k, here, 0.0) for k in range(1, 4))
                for k in range(1, 4):
                    moved = pltpu.roll(
                        jnp.where(place >= k, masked[k - 1], after[k - 1]), SUBLANES - k, 0
                    )
                    total = total + taps[k] * moved
                    sums[k] = sums[k] + branch * moved
                after = masked
                pieces.append(total)
            whole = jnp.concatenate(pieces[::-1], axis=0)
            dbranch_ref[row, pl.ds(base, STEP), :] = whole.astype(jnp.bfloat16)
            later.append(after)

            @pl.when(index == 0)
            def _(row=row, whole=whole):
                tail_ref[row] = whole[STEP - SUBLANES :]

        return (tuple(sums), tuple(later))

    sums, firsts = lax.fori_loop(
        0,
        length // STEP,
        conv_step,
        ((zeros,) * 5, tuple((zeros,) * 3 for _ in range(rows))),
    )
    sums = list(sums)
    for row in range(rows):
        total = zeros
        rim = rim_ref[row]
        for k in range(1, 4):
            moved = pltpu.roll(jnp.where(place >= k, 0.0, firsts[row][k - 1]), SUBLANES - k, 0)
            total = total + taps[k] * moved
            sums[k] = sums[k] + rim * moved
        head_ref[row] = total
    for slot in range(5):
        sums_ref[slot : slot + 1, :] = jnp.sum(sums[slot], axis=0, keepdims=True)
    above = jnp.zeros((head_size, width), jnp.float32)
    below = jnp.zeros((LANES - head_size - SUBLANES, width), jnp.float32)
    turned = jnp.concatenate([above, sums_ref[...], below], axis=0).T
    lane = lax.broadcasted_iota(jnp.int32, (width, LANES), 1)
    dgates_ref[:, :LANES] = jnp.where(lane < head_size, folds[0], turned).astype(dgates_ref.dtype)
    dgates_ref[:, LANES:] = folds[1].astype(dgates_ref.dtype)


def channel_call(
    kernel, name, arrays, specs, outs, out_specs, scratch, blocks, flops, params=()
):
    moved = sum(math.prod(a.shape) * a.dtype.itemsize for a in (*arrays, *outs))
    return pl.pallas_call(
        kernel,
        name=name,
        grid=(blocks,),
        in_specs=specs,
        out_specs=out_specs,
        out_shape=outs,
        scratch_shapes=scratch,
        compiler_params=pltpu.CompilerParams(vmem_limit_bytes=VMEM_BYTES, **dict(params)),
        cost_estimate=pl.CostEstimate(flops=flops, bytes_accessed=moved, transcendentals=0),
    )(*arrays)


class Recurrence:
    def __init__(self, rows, length, channels, head_size):
        self.rows, self.length, self.channels = (rows, length, channels)
        self.head_size = head_size
        self.width = head_size * LANES // math.gcd(head_size, LANES)
        self.blocks = channels // self.width
        self.flops = 2 * rows * length * channels * 2 * self.width

    def tall(self):
        return pl.BlockSpec((self.rows, self.length, self.width), lambda j: (0, 0, j))

    def short(self, size):
        return pl.BlockSpec((self.rows, size, self.width), lambda j: (0, 0, j))

    def apart(self, size):
        return [pl.BlockSpec((1, size, self.width), lambda j: (0, 0, j))] * self.rows

    def whole(self, rows, size):
        return pl.BlockSpec((rows, size, self.channels), lambda j: (0, 0, 0))

    def flat(self, size):
        return pl.BlockSpec((size, self.width), lambda j: (0, j))

    def dist(self):
        return pl.BlockSpec((self.rows, self.length, LANES), lambda j: (0, 0, 0))

    def gates(self, columns):
        return pl.BlockSpec((self.width, columns), lambda j: (j, 0))

    def shape(self, size, dtype):
        return jax.ShapeDtypeStruct((self.rows, size, self.channels), dtype)

    def widen(self, lru_gates):
        size, width = (self.head_size, self.width)
        heads = width // size
        column = jnp.arange(2 * width)
        source = (column // width) * size + column % size
        spread = (jnp.arange(2 * size)[:, None] == source[None, :]).astype(jnp.bfloat16)
        owner = (column % width) // size
        mine = (jnp.arange(self.channels) // size) % heads
        wide = jnp.dot(lru_gates, spread, preferred_element_type=jnp.float32)
        return jnp.where(mine[:, None] == owner[None, :], wide, 0.0).astype(jnp.bfloat16)

    def forward(self, branch, rim, dist, params, gates):
        f32 = jnp.float32
        outs = [self.shape(self.length, d) for d in (jnp.bfloat16, f32, f32, f32, f32)]
        return channel_call(
            forward_kernel,
            "recurrence_forward",
            (branch, rim, dist, params, gates),
            [self.tall(), self.short(SUBLANES), self.dist(), self.flat(16), self.gates(2 * self.width)],
            outs + [self.shape(2, f32)],
            [self.tall()] * 5 + [self.short(2)],
            [pltpu.VMEM((self.rows, self.length, 2 * self.width), f32)],
            self.blocks,
            self.flops,
        )

    def adjoint(self, dres, weight, pre, state, cum, entering, rate, dist, params):
        f32 = jnp.float32
        outs = [self.shape(self.length, d) for d in (jnp.bfloat16, f32, f32)] + [self.shape(1, f32)]
        tall, apart = (self.tall(), self.apart(self.length))
        return channel_call(
            functools.partial(adjoint_kernel, self.rows),
            "recurrence_adjoint",
            (dres, weight, *pre, *state, *cum, entering, *rate, dist, params),
            [
                pl.BlockSpec(dres.shape, lambda j: (0, 0)),
                self.gates(weight.shape[1]),
                *apart * 3,
                self.short(1),
                *apart,
                self.dist(),
                self.flat(16),
            ],
            outs,
            [tall, tall, tall, self.short(1)],
            [pltpu.VMEM((self.rows, self.length, self.width), f32)],
            self.blocks,
            2 * self.rows * self.length * weight.size,
        )

    def backward(
        self, local, back, first, last, state, cum, entering, rate, igate, lru, dist, branch, rim, params, gates
    ):
        f32 = jnp.float32
        outs = [
            self.shape(self.length, jnp.bfloat16),
            self.shape(SUBLANES, f32),
            self.shape(SUBLANES, f32),
            jax.ShapeDtypeStruct((self.channels, 2 * LANES), jnp.bfloat16),
        ]
        tall, apart = (self.tall(), self.apart(self.length))
        seqs = lax.axis_size("seq")
        summary = (self.rows, 2, self.channels)
        return channel_call(
            functools.partial(backward_kernel, self.head_size, self.rows),
            "recurrence_backward",
            (local, back, first, *last, *state, *cum, entering, *rate, *igate, *lru, dist, *branch, *rim)
            + (params, gates),
            [tall, tall, self.whole(self.rows, 1), *[self.whole(1, 2)] * self.rows, *apart * 2]
            + [self.short(1), *apart * 3, self.dist(), *apart, *self.apart(SUBLANES)]
            + [self.flat(16), self.gates(2 * self.width)],
            outs,
            [tall, self.short(SUBLANES), self.short(SUBLANES), self.gates(2 * LANES)],
            [
                pltpu.VMEM((self.rows, self.length, 2 * self.width), jnp.bfloat16),
                pltpu.VMEM((self.rows, self.length, self.width), f32),
                pltpu.VMEM((SUBLANES, self.width), f32),
                pltpu.VMEM((self.rows, 1, self.channels), f32),
                pltpu.VMEM(summary, f32),
                pltpu.VMEM((seqs,) + summary, f32),
                pltpu.SemaphoreType.DMA((seqs - 1,)),
                pltpu.SemaphoreType.DMA((seqs - 1,)),
            ],
            self.blocks,
            2 * self.flops,
            {"collective_id": 5, "has_side_effects": True},
        )


def gathered(parts_ref, at):
    return jnp.concatenate([parts_ref[k, at, :] for k in range(parts_ref.shape[0])], axis=1)


def front_kernel(
    parts_ref,
    gain_ref,
    input_ref,
    gate_ref,
    x_ref,
    inverse_ref,
    normed_ref,
    branch_ref,
    pre_ref,
    rim_ref,
    edge_ref,
    landed_ref,
    send_sem,
    recv_sem,
):
    tokens = x_ref.shape[0]
    piece, tall = (64, min(tokens, 512))
    step, steps = (pl.program_id(0), edge_ref.shape[0])
    seq, seqs = (lax.axis_index("seq"), lax.axis_size("seq"))
    barrier = pltpu.get_barrier_semaphore()

    @pl.when(step == 0)
    def _():
        before = {"seq": lax.rem(seq + seqs - 1, seqs)}
        pl.semaphore_signal(barrier, inc=1, device_id=before, device_id_type=MESH)

        def norm(index, carry):
            at = pl.ds(pl.multiple_of(index * piece, piece), piece)
            low = gathered(parts_ref, at)
            x_ref[at, :] = low
            value = low.astype(jnp.float32)
            inverse = lax.rsqrt(jnp.mean(value * value, axis=1, keepdims=True) + EPS)
            inverse_ref[at, :] = jnp.broadcast_to(inverse, (piece, LANES))
            normed_ref[at, :] = (value * inverse * gain_ref[...]).astype(jnp.bfloat16)
            return carry

        lax.fori_loop(0, tokens // piece, norm, 0, unroll=2)

    def multiply(index, carry):
        at = pl.ds(pl.multiple_of(index * tall, tall), tall)
        normed = normed_ref[at, :]
        branch_ref[at, :] = jnp.dot(normed, input_ref[...], preferred_element_type=jnp.float32)
        pre_ref[at, :] = jnp.dot(normed, gate_ref[...], preferred_element_type=jnp.float32)
        return carry

    lax.fori_loop(0, tokens // tall, multiply, 0)
    edge_ref[step] = branch_ref[tokens - SUBLANES :, :]

    def rim_copy(place):
        return pltpu.make_async_remote_copy(
            src_ref=edge_ref.at[place],
            dst_ref=landed_ref.at[place],
            send_sem=send_sem.at[place],
            recv_sem=recv_sem.at[place],
            device_id={"seq": lax.rem(seq + 1, seqs)},
            device_id_type=MESH,
        )

    @pl.when(step == 0)
    def _():
        pl.semaphore_wait(barrier, 1)

    rim_copy(step).start()

    @pl.when(step == steps - 1)
    def _():
        columns = edge_ref.shape[2]
        live = jnp.where(seq > 0, 1.0, 0.0)
        for place in range(steps):
            rim_copy(place).wait()
            rim_ref[:, place * columns : (place + 1) * columns] = live * landed_ref[place]


def front(parts, gain, recur_input, recur_gate):
    count, tokens, width = parts.shape
    model, rec = recur_input.shape
    columns = 4 * LANES
    steps = rec // columns
    low, f32 = (jnp.bfloat16, jnp.float32)
    tall = pl.BlockSpec((model, columns), lambda j: (0, j))
    wide = pl.BlockSpec((tokens, columns), lambda j: (0, j))

    def whole(shape):
        return pl.BlockSpec(shape, lambda j: (0,) * len(shape))

    return pl.pallas_call(
        front_kernel,
        name="norm_and_project",
        grid=(steps,),
        in_specs=[whole(parts.shape), whole((1, model)), tall, tall],
        out_specs=[whole((tokens, model)), whole((tokens, LANES)), whole((tokens, model)), wide, wide]
        + [whole((SUBLANES, rec))],
        out_shape=[
            jax.ShapeDtypeStruct((tokens, model), low),
            jax.ShapeDtypeStruct((tokens, LANES), f32),
            jax.ShapeDtypeStruct((tokens, model), low),
            jax.ShapeDtypeStruct((tokens, rec), f32),
            jax.ShapeDtypeStruct((tokens, rec), f32),
            jax.ShapeDtypeStruct((SUBLANES, rec), f32),
        ],
        scratch_shapes=[
            pltpu.VMEM((steps, SUBLANES, columns), f32),
            pltpu.VMEM((steps, SUBLANES, columns), f32),
            pltpu.SemaphoreType.DMA((steps,)),
            pltpu.SemaphoreType.DMA((steps,)),
        ],
        compiler_params=pltpu.CompilerParams(
            collective_id=3, has_side_effects=True, vmem_limit_bytes=VMEM_BYTES
        ),
        cost_estimate=pl.CostEstimate(
            flops=4 * tokens * model * rec, bytes_accessed=20 * tokens * model, transcendentals=0
        ),
    )(parts, gain[None], recur_input, recur_gate)


def middle_kernel(rows, *refs):
    (last_ref, state_ref, cum_ref, pre_ref, x_ref, out_ref, gain_ref), others = by_rows(
        refs, rows, (True,) * 5 + (False,) * 2
    )
    entering_ref, mixed_ref, resid_ref, normed_ref = others[:4]
    sent_ref, got_ref, send_sem, recv_sem = others[4:]
    tall, model = resid_ref.shape
    step = pl.program_id(0)
    tiles = pl.num_programs(0) // rows
    slab = 16

    @pl.when(step == 0)
    def _():
        for row in range(rows):
            sent_ref[row] = last_ref[row]
        carried(sent_ref, got_ref, entering_ref, send_sem, recv_sem, False)

    for row in range(rows):

        @pl.when(lax.div(step, tiles) == row)
        def _(row=row):
            def mix(index, carry):
                at = pl.ds(pl.multiple_of(index * slab, slab), slab)
                state = state_ref[row, at, :] + cum_ref[row, at, :] * entering_ref[row]
                pre = pre_ref[row, at, :]
                inner = jnp.tanh(pre * (GELU_C + (GELU_C * GELU_A) * (pre * pre)))
                mixed_ref[at, :] = (state * (pre * (0.5 + 0.5 * inner))).astype(jnp.bfloat16)
                return carry

            lax.fori_loop(0, tall // slab, mix, 0, unroll=2)
            tile = 512
            for first in range(0, model, tile):
                at = slice(first, first + tile)
                resid_ref[:, at] = x_ref.refs[row][:, at].astype(jnp.float32) + jnp.dot(
                    mixed_ref[...], out_ref[:, at], preferred_element_type=jnp.float32
                )

    def norm(index, carry):
        at = pl.ds(pl.multiple_of(index * slab, slab), slab)
        resid = resid_ref[at, :]
        inverse = lax.rsqrt(jnp.mean(resid * resid, axis=1, keepdims=True) + EPS)
        normed_ref[at, :] = (resid * inverse * gain_ref[...]).astype(jnp.bfloat16)
        return carry

    lax.fori_loop(0, tall // slab, norm, 0, unroll=4)


def middle(last, state, cum, pre, x, recur_out, gain):
    rows = len(state)
    _, length, rec = state[0].shape
    model = recur_out.shape[1]
    tall = min(length, 256)
    tiles = length // tall
    tokens = rows * length
    seqs = lax.axis_size("seq")
    low, f32 = (jnp.bfloat16, jnp.float32)

    def whole(shape):
        return pl.BlockSpec(shape, lambda s: (0,) * len(shape), pipeline_mode=pl.Buffered(1))

    def part(row):
        return lambda s: (0, jnp.clip(s - row * tiles, 0, tiles - 1), 0)

    def flat(row):
        return lambda s: (jnp.clip(s - row * tiles, 0, tiles - 1), 0)

    apart = [pl.BlockSpec((1, tall, rec), part(row)) for row in range(rows)]
    summary = (rows, 2, rec)
    return pl.pallas_call(
        functools.partial(middle_kernel, rows),
        name="mix_and_norm",
        grid=(rows * tiles,),
        in_specs=[whole((1, 2, rec))] * rows
        + apart * 3
        + [pl.BlockSpec((tall, model), flat(row)) for row in range(rows)]
        + [whole(recur_out.shape), whole((1, model))],
        out_specs=[
            pl.BlockSpec((rows, 1, rec), lambda s: (0, 0, 0)),
            pl.BlockSpec((tall, rec), lambda s: (s, 0)),
            pl.BlockSpec((tall, model), lambda s: (s, 0)),
            pl.BlockSpec((tall, model), lambda s: (s, 0)),
        ],
        out_shape=[
            jax.ShapeDtypeStruct((rows, 1, rec), f32),
            jax.ShapeDtypeStruct((tokens, rec), low),
            jax.ShapeDtypeStruct((tokens, model), f32),
            jax.ShapeDtypeStruct((tokens, model), low),
        ],
        scratch_shapes=[
            pltpu.VMEM(summary, f32),
            pltpu.VMEM((seqs,) + summary, f32),
            pltpu.SemaphoreType.DMA((seqs - 1,)),
            pltpu.SemaphoreType.DMA((seqs - 1,)),
        ],
        compiler_params=pltpu.CompilerParams(
            collective_id=4, has_side_effects=True, vmem_limit_bytes=VMEM_BYTES
        ),
        cost_estimate=pl.CostEstimate(
            flops=2 * tokens * rec * model, bytes_accessed=14 * tokens * rec, transcendentals=0
        ),
    )(*last, *state, *cum, *pre, *x, recur_out, gain[None])


def mlp_kernel(
    left_ref,
    parts_ref,
    normed_ref,
    resid_ref,
    gain_ref,
    gate_ref,
    up_ref,
    down_ref,
    gout_ref,
    hidden_ref,
    dgate_ref,
    dup_ref,
    result_ref,
    dres_ref,
    total_ref,
    back_ref,
):
    tokens, model = normed_ref.shape
    chunk = down_ref.shape[0]
    rows = left_ref.shape[0]
    length = tokens // rows
    step = pl.program_id(0)
    slab = 32

    @pl.when(step == 0)
    def _():
        for row in range(rows):

            def collect(index, carry, row=row):
                base = pl.multiple_of(index * slab, slab)
                at = pl.ds(row * length + base, slab)
                low = gathered(parts_ref, at)
                place = base + lax.broadcasted_iota(jnp.int32, low.shape, 0)
                value = jnp.where(place < left_ref[row], low.astype(jnp.float32), 0.0)
                gout_ref[at, :] = value.astype(jnp.bfloat16)
                total_ref[at, :] = resid_ref[at, :]
                back_ref[at, :] = jnp.zeros((slab, model), jnp.float32)
                return carry

            lax.fori_loop(0, length // slab, collect, 0)

    tall = min(tokens, 512)
    wide = 256

    def tile(index, carry):
        at = pl.ds(pl.multiple_of(index * tall, tall), tall)
        for column in range(chunk // wide):
            own = slice(column * wide, (column + 1) * wide)
            gate = jnp.dot(normed_ref[at, :], gate_ref[:, own], preferred_element_type=jnp.float32)
            up = jnp.dot(normed_ref[at, :], up_ref[:, own], preferred_element_type=jnp.float32)
            dhid = lax.dot_general(
                gout_ref[at, :],
                down_ref[own, :],
                (((1,), (1,)), ((), ())),
                preferred_element_type=jnp.float32,
            )
            act, slope = gelu_pair(gate)
            hidden_ref[at, own] = (act * up).astype(jnp.bfloat16)
            dgate_ref[at, own] = (dhid * up * slope).astype(jnp.bfloat16)
            dup_ref[at, own] = (dhid * act).astype(jnp.bfloat16)
        for column in range(model // (2 * wide)):
            own = slice(column * 2 * wide, (column + 1) * 2 * wide)
            total_ref[at, own] += jnp.dot(
                hidden_ref[at, :], down_ref[:, own], preferred_element_type=jnp.float32
            )
            back_ref[at, own] += lax.dot_general(
                dgate_ref[at, :],
                gate_ref[own, :],
                (((1,), (1,)), ((), ())),
                preferred_element_type=jnp.float32,
            ) + lax.dot_general(
                dup_ref[at, :],
                up_ref[own, :],
                (((1,), (1,)), ((), ())),
                preferred_element_type=jnp.float32,
            )
        return carry

    lax.fori_loop(0, tokens // tall, tile, 0)

    @pl.when(step == pl.num_programs(0) - 1)
    def _():
        parts, width = (result_ref.shape[0], result_ref.shape[2])
        small = 16

        def finish(index, carry):
            at = pl.ds(pl.multiple_of(index * small, small), small)
            result = total_ref[at, :].astype(jnp.bfloat16)
            for part in range(parts):
                result_ref[part, at, :] = result[:, part * width : (part + 1) * width]
            resid = resid_ref[at, :]
            inverse = lax.rsqrt(jnp.mean(resid * resid, axis=1, keepdims=True) + EPS)
            normed = resid * inverse
            scaled = back_ref[at, :] * gain_ref[...]
            mean = jnp.mean(scaled * normed, axis=1, keepdims=True)
            dres = gout_ref[at, :].astype(jnp.float32) + inverse * (scaled - normed * mean)
            dres_ref[at, :] = dres.astype(jnp.bfloat16)
            return carry

        lax.fori_loop(0, tokens // small, finish, 0, unroll=4)


def mlp(left, parts, normed, resid, gain, mlp_gate, mlp_up, mlp_down):
    tokens, model = normed.shape
    ffn = mlp_gate.shape[1]
    chunk = 768
    low, f32 = (jnp.bfloat16, jnp.float32)

    def whole(shape):
        return pl.BlockSpec(shape, lambda s: (0,) * len(shape), pipeline_mode=pl.Buffered(1))

    columns = pl.BlockSpec((model, chunk), lambda s: (0, s))
    made = pl.BlockSpec((tokens, chunk), lambda s: (0, s))
    tall = jax.ShapeDtypeStruct((tokens, ffn), low)
    square = jax.ShapeDtypeStruct((tokens, model), low)
    return pl.pallas_call(
        mlp_kernel,
        name="mlp_forward_backward",
        grid=(ffn // chunk,),
        in_specs=[
            pl.BlockSpec(memory_space=pltpu.SMEM),
            whole(parts.shape),
            whole(normed.shape),
            whole(resid.shape),
            whole((1, model)),
            columns,
            columns,
            pl.BlockSpec((chunk, model), lambda s: (s, 0)),
        ],
        out_specs=[
            whole((tokens, model)),
            made,
            made,
            made,
            whole(parts.shape),
            whole((tokens, model)),
        ],
        out_shape=[square, tall, tall, tall, jax.ShapeDtypeStruct(parts.shape, low), square],
        scratch_shapes=[pltpu.VMEM((tokens, model), f32), pltpu.VMEM((tokens, model), f32)],
        compiler_params=pltpu.CompilerParams(vmem_limit_bytes=VMEM_BYTES),
        cost_estimate=pl.CostEstimate(
            flops=12 * tokens * model * ffn,
            bytes_accessed=6 * (model + tokens) * ffn + 14 * tokens * model,
            transcendentals=0,
        ),
    )(left, parts, normed, resid, gain[None], mlp_gate, mlp_up, mlp_down)


def spread_kernel(whole_ref, out_ref):
    out_ref[0] = whole_ref[...]


def spread(whole, count):
    tokens, width = (whole.shape[0], whole.shape[1] // count)
    return pl.pallas_call(
        spread_kernel,
        name="spread_features",
        grid=(count,),
        in_specs=[pl.BlockSpec((tokens, width), lambda j: (0, j))],
        out_specs=pl.BlockSpec((1, tokens, width), lambda j: (j, 0, 0)),
        out_shape=jax.ShapeDtypeStruct((count, tokens, width), whole.dtype),
        cost_estimate=pl.CostEstimate(
            flops=0, bytes_accessed=4 * tokens * whole.shape[1], transcendentals=0
        ),
    )(whole)


CHAN = ("zed", "core")


def features_in(local, pick=slice(None)):
    count = lax.axis_size(CHAN)
    rows, length, width = local.shape
    local = local.reshape(count, rows // count, length, width)[:, pick]
    if width % LANES == 0:
        return lax.all_to_all(local, CHAN, 0, 0, tiled=True).reshape(count, -1, width)
    moved = lax.all_to_all(
        local.reshape(-1, length, width), CHAN, split_axis=0, concat_axis=2, tiled=True
    )
    return moved.reshape(1, -1, count * width)


def features_apart(whole):
    count = lax.axis_size(CHAN)
    if (whole.shape[1] // count) % LANES == 0:
        return spread(whole, count)
    return whole[None]


def features_out(parts, rows):
    blocks, tokens, width = parts.shape
    parts = parts.reshape(blocks, rows, tokens // rows, width)
    if blocks > 1:
        moved = lax.all_to_all(parts, CHAN, 0, 0, tiled=True)
        return moved.reshape(-1, *parts.shape[2:])
    return lax.all_to_all(parts[0], CHAN, split_axis=2, concat_axis=0, tiled=True)


class Corners:
    def __init__(self, seq, zed):
        self.seq_bits, self.zed_bits = (seq.bit_length() - 1, zed.bit_length() - 1)
        self.count = self.seq_bits + self.zed_bits
        self.dims = (2,) * self.count
        self.low = tuple(range(self.seq_bits))[::-1] + tuple(range(self.seq_bits, self.count))[::-1]
        self.high = tuple(range(self.seq_bits)) + tuple(range(self.seq_bits, self.count))[::-1]

    def place(self, dim):
        if dim < self.seq_bits:
            return ("seq", 2 ** (self.seq_bits - 1 - dim))
        return ("zed", 2 ** (self.count - 1 - dim))

    def bit(self, dim):
        axis, weight = self.place(dim)
        return lax.rem(lax.div(lax.axis_index(axis), weight), 2)

    def partner(self, dim):
        axis, weight = self.place(dim)
        return {axis: lax.axis_index(axis) + weight * (1 - 2 * self.bit(dim))}


def tail_kernel(
    corners,
    orders,
    dgate_hbm,
    dbranch_hbm,
    ending_ref,
    leading_ref,
    mixed_hbm,
    dres_hbm,
    gain_ref,
    input_hbm,
    gate_hbm,
    small_hbm,
    *refs,
):
    rows = ending_ref.shape[0]
    normed_hbms, x_hbms, inverse_hbms = (refs[k * rows : (k + 1) * rows] for k in range(3))
    tokens_ref, sum_gate, sum_out, sum_in, sum_small = refs[3 * rows : 3 * rows + 5]
    refs = refs[3 * rows + 5 :]
    stages = corners.count + 1
    dgate, dbranch, mixed, dres, normed, x, inverse, weight_in, weight_gate = refs[:9]
    made_in, made_out, own_small, back, parts, rim = refs[9:15]
    slots_in, slots_out, slots_small = (
        refs[15 + k * stages : 15 + (k + 1) * stages] for k in range(3)
    )
    (
        send_sem,
        recv_sem,
        load_sem,
        move_send,
        move_recv,
        keep_sem,
        rim_send,
        rim_recv,
    ) = refs[15 + 3 * stages :]
    seq, zed, core = (lax.axis_index(axis) for axis in ("seq", "zed", "core"))
    seqs, group = (lax.axis_size("seq"), 2 * lax.axis_size("zed"))
    mine = zed * 2 + core
    length = tokens_ref.shape[1]
    model = x.shape[1]

    def member(index):
        return {"zed": lax.div(index, 2), "core": lax.rem(index, 2)}

    def by_row(sources, target):
        return [
            (source, target.at[pl.ds(row * length, length)]) for row, source in enumerate(sources)
        ]

    pairs = [
        (dbranch_hbm, dbranch),
        (input_hbm, weight_in),
        (dgate_hbm, dgate),
        (gate_hbm, weight_gate),
        *by_row(x_hbms, x),
        *by_row(inverse_hbms, inverse),
        (dres_hbm, dres),
        *by_row(normed_hbms, normed),
        (mixed_hbm, mixed),
        (small_hbm.at[(slice(None),) * corners.count + (core,)], own_small),
    ]
    kinds = []
    for name in ('dbranch', 'win', 'dgate', 'wgate', 'x', 'inverse', 'dres', 'normed', 'mixed', 'small'):
        kinds += [name] * (rows if name in ("normed", "x", "inverse") else 1)
    loads = [
        pltpu.make_async_copy(source, target, load_sem.at[place])
        for place, (source, target) in enumerate(pairs)
    ]
    for load in loads:
        load.start()

    barrier = pltpu.get_barrier_semaphore()
    for other in range(1, group):
        pl.semaphore_signal(
            barrier, inc=1, device_id=member(lax.rem(mine + other, group)), device_id_type=MESH
        )
    for other in range(1, seqs):
        pl.semaphore_signal(
            barrier, inc=1, device_id={"seq": lax.rem(seq + other, seqs)}, device_id_type=MESH
        )
    pl.semaphore_wait(barrier, group - 1 + seqs - 1)

    rim_copy = pltpu.make_async_remote_copy(
        src_ref=leading_ref,
        dst_ref=rim,
        send_sem=rim_send,
        recv_sem=rim_recv,
        device_id={"seq": lax.rem(seq + seqs - 1, seqs)},
        device_id_type=MESH,
    )
    rim_copy.start()

    def own(stream, index):
        if stream < 4:
            return made_in.at[(stream,) + index + (core,)]
        if stream < 6:
            return made_out.at[(stream - 4,) + index + (core,)]
        return own_small.at[index]

    def slot(stream, stage):
        if stream < 4:
            return slots_in[stage].at[stream]
        if stream < 6:
            return slots_out[stage].at[stream - 4]
        return slots_small[stage]

    def copy(stream, stage):
        order = orders[stream]
        every = (slice(None),) * corners.count
        if stage == 0:
            if stream < 4:
                source = made_in.at[(stream,) + every + (1 - core,)]
            elif stream < 6:
                source = made_out.at[(stream - 4,) + every + (1 - core,)]
            else:
                source = small_hbm.at[every + (1 - core,)]
            target = {"core": 1 - core}
        else:
            dim = order[stage - 1]
            fixed = {before: corners.bit(before) for before in order[: stage - 1]}
            fixed[dim] = 1 - corners.bit(dim)
            source = own(stream, tuple(fixed.get(d, slice(None)) for d in range(corners.count)))
            target = corners.partner(dim)
        return pltpu.make_async_remote_copy(
            src_ref=source,
            dst_ref=slot(stream, stage),
            send_sem=send_sem.at[stream, stage],
            recv_sem=recv_sem.at[stream, stage],
            device_id=target,
            device_id_type=MESH,
        )

    sums = [
        sum_gate.at[:, : sum_gate.shape[1] // 2],
        sum_gate.at[:, sum_gate.shape[1] // 2 :],
        sum_in.at[:, : sum_in.shape[1] // 2],
        sum_in.at[:, sum_in.shape[1] // 2 :],
        sum_out.at[:, : sum_out.shape[1] // 2],
        sum_out.at[:, sum_out.shape[1] // 2 :],
        sum_small,
    ]

    def advance(stream, stage):
        order = orders[stream]
        copy(stream, stage).wait_recv()
        left = [dim for dim in range(corners.count) if dim not in order[:stage]]
        fixed = {dim: corners.bit(dim) for dim in order[:stage]}
        arrived = slot(stream, stage)
        if not left:
            index = tuple(fixed[dim] for dim in range(corners.count))
            sums[stream][...] = own(stream, index)[...].astype(jnp.float32) + arrived[...].astype(
                jnp.float32
            )
            return

        def add(index, carry):
            part = {
                dim: lax.rem(lax.div(index, 2 ** (len(left) - 1 - place)), 2)
                for place, dim in enumerate(left)
            }
            kept = own(stream, tuple({**fixed, **part}[dim] for dim in range(corners.count)))
            total = kept[...].astype(jnp.float32) + arrived[
                tuple(part[dim] for dim in left)
            ].astype(jnp.float32)
            kept[...] = total.astype(jnp.bfloat16)
            return carry

        lax.fori_loop(0, 2 ** len(left), add, 0)
        copy(stream, stage + 1).start()

    def move(other, row):
        to = lax.rem(mine + other, group)
        return pltpu.make_async_remote_copy(
            src_ref=parts.at[to, pl.ds(row * length, length)],
            dst_ref=tokens_ref.at[mine * rows + row],
            send_sem=move_send.at[other - 1, row],
            recv_sem=move_recv.at[other - 1, row],
            device_id=member(to),
            device_id_type=MESH,
        )

    def keep(row):
        return pltpu.make_async_copy(
            parts.at[mine, pl.ds(row * length, length)],
            tokens_ref.at[mine * rows + row],
            keep_sem.at[row],
        )

    tile = 256
    width = parts.shape[2]

    def back_row(row):
        at_row = slice(row * length, (row + 1) * length)

        def product(index, carry):
            at = pl.ds(pl.multiple_of(index * tile, tile), tile)
            contract = (((1,), (1,)), ((), ()))
            back[:, at] = lax.dot_general(
                dbranch[at_row, :], weight_in[at, :], contract, preferred_element_type=jnp.float32
            ) + lax.dot_general(
                dgate[at_row, :], weight_gate[at, :], contract, preferred_element_type=jnp.float32
            )
            return carry

        lax.fori_loop(0, model // tile, product, 0)
        slab = 16

        def norm(index, carry):
            base = pl.multiple_of(index * slab, slab)
            at = pl.ds(row * length + base, slab)
            inv = inverse[at, :1]
            value = x[at, :].astype(jnp.float32) * inv
            scaled = back[pl.ds(base, slab), :] * gain_ref[...]
            mean = jnp.mean(scaled * value, axis=1, keepdims=True)
            grad = dres[at, :].astype(jnp.float32) + inv * (scaled - value * mean)
            grad = grad.astype(jnp.bfloat16)
            for part in range(parts.shape[0]):
                parts[part, at, :] = grad[:, part * width : (part + 1) * width]
            return carry

        lax.fori_loop(0, length // slab, norm, 0, unroll=4)
        for other in range(1, group):
            move(other, row).start()
        keep(row).start()

    def weight_product(left, right, made, stream, first):
        columns = made.shape[-1]
        shape = made.shape[1:-1]

        def product(index, carry):
            at = pl.ds(pl.multiple_of(index * tile, tile), tile)
            source = pl.ds(pl.multiple_of(first + index * tile, tile), tile)
            part = lax.dot_general(
                left[...],
                right[:, source],
                (((0,), (0,)), ((), ())),
                preferred_element_type=jnp.float32,
            )
            made[(stream,) + (slice(None),) * len(shape) + (at,)] = part.astype(
                jnp.bfloat16
            ).reshape(shape + (tile,))
            return carry

        lax.fori_loop(0, columns // tile, product, 0)

    half, half_out = (made_in.shape[-1], made_out.shape[-1])
    waited, reached = (set(), {})

    def need(*names):
        for place, name in enumerate(kinds):
            if name in names and place not in waited:
                waited.add(place)
                loads[place].wait()

    def fix_rim():
        need("dbranch")
        rim_copy.wait()
        live = jnp.where(seq < seqs - 1, 1.0, 0.0)
        for row in range(rows):
            at = slice((row + 1) * length - STEP, (row + 1) * length)
            inside = dbranch[at, :].astype(jnp.float32)
            last = ending_ref[row] + live * rim[row]
            dbranch[at, :] = jnp.concatenate([inside[: STEP - SUBLANES], last], axis=0).astype(
                jnp.bfloat16
            )

    def begin(stream):
        copy(stream, 0).start()
        reached[stream] = 0

    def progress(streams):
        for stream in streams:
            if stream in reached and reached[stream] < stages:
                if stream == 6:
                    need("small")
                advance(stream, reached[stream])
                reached[stream] += 1

    def compute(item):
        if item == "gate":
            need("normed", "dgate")
            for stream in (0, 1):
                weight_product(normed, dgate, made_in, stream, stream * half)
                begin(stream)
        elif item == "out":
            need("mixed", "dres")
            for stream in (4, 5):
                weight_product(mixed, dres, made_out, stream - 4, (stream - 4) * half_out)
                begin(stream)
        elif item == "in":
            need("normed", "dbranch")
            for stream in (2, 3):
                weight_product(normed, dbranch, made_in, stream, (stream - 2) * half)
                begin(stream)
        else:
            need("dbranch", "dgate", "win", "wgate", "x", "inverse", "dres")
            back_row(item)

    begin(6)
    fix_rim()
    compute(0)
    compute(1)
    compute('gate')
    progress((6,))
    compute('out')
    progress((0, 1))
    compute('in')
    progress((0, 1))
    progress((4, 5))
    progress((6,))
    while any(reached[stream] < stages for stream in range(7)):
        progress((0, 1, 4, 5, 2, 3, 6))
    for stage in range(stages):
        for stream in range(7):
            copy(stream, stage).wait_send()
    for row in range(rows):
        for other in range(1, group):
            move(other, row).wait()
        keep(row).wait()


def tail(dgate, dbranch, ending, leading, mixed, dres, gain, w_in, w_gate, small, normed, x, inverse):
    corners = Corners(lax.axis_size("seq"), lax.axis_size("zed"))
    group, devices = (lax.axis_size(CHAN), 2 ** (corners.count + 1))
    tokens, model = dres.shape
    rec = dgate.shape[1]
    rows = ending.shape[0]
    length, width = (tokens // rows, model // group)
    low, f32 = (jnp.bfloat16, jnp.float32)
    stages = corners.count + 1
    in_rows, out_rows = (model // devices, rec // devices)
    small = small.reshape(corners.dims + (2, out_rows, small.shape[1]))
    orders = [corners.low, corners.high] * 3 + [corners.low]

    def slots(lead, shape):
        return [pltpu.VMEM(lead + (2,) * (corners.count - k) + shape, low) for k in range(stages)]

    in_shape, out_shape = ((in_rows, rec // 2), (out_rows, model // 2))
    loaded = (dgate, dbranch, mixed, dres, dres, dres)
    loaded += (jax.ShapeDtypeStruct((tokens, LANES), f32), w_in, w_gate)
    anyplace = pl.BlockSpec(memory_space=pl.ANY)
    vmem = pl.BlockSpec(memory_space=pltpu.VMEM)
    dma = pltpu.SemaphoreType.DMA
    moved = sum(math.prod(a.shape) * a.dtype.itemsize for a in loaded)
    return pl.pallas_call(
        functools.partial(tail_kernel, corners, orders),
        name="tail",
        in_specs=[anyplace, anyplace, vmem, vmem, anyplace, anyplace, vmem]
        + [anyplace] * (3 + 3 * rows),
        out_specs=[anyplace] + [vmem] * 4,
        out_shape=[
            jax.ShapeDtypeStruct((group * rows, length, width), low),
            jax.ShapeDtypeStruct((in_rows, rec), f32),
            jax.ShapeDtypeStruct((out_rows, model), f32),
            jax.ShapeDtypeStruct((in_rows, rec), f32),
            jax.ShapeDtypeStruct(small.shape[-2:], f32),
        ],
        scratch_shapes=[pltpu.VMEM(a.shape, a.dtype) for a in loaded]
        + [
            pltpu.VMEM((4,) + corners.dims + (2,) + in_shape, low),
            pltpu.VMEM((2,) + corners.dims + (2,) + out_shape, low),
            pltpu.VMEM(corners.dims + small.shape[-2:], low),
            pltpu.VMEM((length, model), f32),
            pltpu.VMEM((group, tokens, width), low),
            pltpu.VMEM(leading.shape, leading.dtype),
        ]
        + slots((4,), in_shape)
        + slots((2,), out_shape)
        + slots((), small.shape[-2:])
        + [
            dma((7, stages)),
            dma((7, stages)),
            dma((7 + 3 * rows,)),
            dma((group - 1, rows)),
            dma((group - 1, rows)),
            dma((rows,)),
            dma,
            dma,
        ],
        compiler_params=pltpu.CompilerParams(
            collective_id=1, has_side_effects=True, vmem_limit_bytes=60 * 1024 * 1024
        ),
        cost_estimate=pl.CostEstimate(
            flops=10 * tokens * model * rec, bytes_accessed=2 * moved, transcendentals=0
        ),
    )(dgate, dbranch, ending, leading, mixed, dres, gain[None], w_in, w_gate, small, *normed, *x, *inverse)


def grads_kernel(
    normed_ref,
    dgate_ref,
    dup_ref,
    hidden_ref,
    gout_ref,
    out_ref,
    turned_ref,
    made_wide,
    made_down,
    come_wide,
    come_down,
    send_sem,
    recv_sem,
    store_sem,
):
    step = pl.program_id(0)
    core = lax.axis_index("core")
    other = {"core": 1 - core}
    wide_rows, down_rows = (made_wide.shape[3], made_down.shape[3])
    wides, downs = (come_wide.shape[0], come_down.shape[0])
    total = wides + downs
    down_at = wides * wide_rows

    def exchange(made, come, index, slot):
        return pltpu.make_async_remote_copy(
            src_ref=made.at[lax.rem(index, 2), 1 - core],
            dst_ref=come.at[index],
            send_sem=send_sem.at[slot],
            recv_sem=recv_sem.at[slot],
            device_id=other,
            device_id_type=MESH,
        )

    def store_wide(index):
        return pltpu.make_async_copy(
            come_wide.at[index],
            out_ref.at[:, pl.ds(pl.multiple_of(index * wide_rows, wide_rows), wide_rows)],
            store_sem.at[index],
        )

    def store_down(index):
        chips = come_down.shape[1]
        return pltpu.make_async_copy(
            come_down.at[index],
            out_ref.at[pl.ds(index * chips, chips), pl.ds(down_at, down_rows)],
            store_sem.at[index + wides],
        )

    @pl.when(step == 0)
    def _():
        barrier = pltpu.get_barrier_semaphore()
        pl.semaphore_signal(barrier, inc=1, device_id=other, device_id_type=MESH)
        pl.semaphore_wait(barrier, 1)
        turned_ref[...] = normed_ref[...].T

    def product_wide(source, index):
        made = made_wide.at[lax.rem(index, 2)]
        chips, rows = (made.shape[1], made.shape[2])
        tile = 512

        def column(place, carry):
            at = pl.ds(pl.multiple_of(place * tile, tile), tile)
            part = jnp.dot(turned_ref[...], source[:, at], preferred_element_type=jnp.float32)
            part = part.astype(jnp.bfloat16).reshape(chips, 2, rows, tile)
            made[0, :, :, at] = part[:, 0]
            made[1, :, :, at] = part[:, 1]
            return carry

        lax.fori_loop(0, source.shape[1] // tile, column, 0)

    def product_tall(left, right, made_all, index):
        made = made_all.at[lax.rem(index, 2)]
        chips, rows = (made.shape[1], made.shape[2])
        tile = 512

        def column(place, carry):
            at = pl.ds(pl.multiple_of(place * tile, tile), tile)
            part = lax.dot_general(
                left[...], right[:, at], (((0,), (0,)), ((), ())), preferred_element_type=jnp.float32
            )
            part = part.astype(jnp.bfloat16).reshape(chips, 2, rows, tile)
            made[0, :, :, at] = part[:, 0]
            made[1, :, :, at] = part[:, 1]
            return carry

        lax.fori_loop(0, right.shape[1] // tile, column, 0)

    half = wides // 2

    @pl.when(step < half)
    def _():
        product_wide(dgate_ref, step)

    @pl.when((step >= half) & (step < wides))
    def _():
        product_wide(dup_ref, step)

    @pl.when(step < wides)
    def _():
        exchange(made_wide, come_wide, step, step).start()

    @pl.when((step >= wides) & (step < total))
    def _():
        product_tall(hidden_ref, gout_ref, made_down, step - wides)
        exchange(made_down, come_down, step - wides, step).start()

    def finish(made, come, index, slot, store):
        exchange(made, come, index, slot).wait()
        mine = made.at[lax.rem(index, 2), core]
        arrived = come.at[index]

        def add(chip, carry):
            both = mine[chip].astype(jnp.float32) + arrived[chip].astype(jnp.float32)
            arrived[chip] = both.astype(jnp.bfloat16)
            return carry

        lax.fori_loop(0, come.shape[1], add, 0)
        store(index).start()

    before = step - 1

    @pl.when((before >= 0) & (before < wides))
    def _():
        finish(made_wide, come_wide, before, before, store_wide)

    @pl.when(before >= wides)
    def _():
        finish(made_down, come_down, before - wides, before, store_down)

    @pl.when(step == total)
    def _():
        for index in range(wides):
            store_wide(index).wait()
        for index in range(downs):
            store_down(index).wait()


def block_gradients(normed, dgate, dup, hidden, gout):
    tokens, model = normed.shape
    ffn = hidden.shape[1]
    chips = lax.axis_size("seq") * lax.axis_size("zed")
    devices = 2 * chips
    wide_rows, down_rows = (model // devices, ffn // devices)
    chunk = 768
    wides, downs = (2 * ffn // model, ffn // chunk)
    half = wides // 2
    down_chips = chunk // (2 * down_rows)
    rows = wides * wide_rows + down_rows
    low = jnp.bfloat16

    def whole(array):
        return pl.BlockSpec(array.shape, lambda s: (0, 0), pipeline_mode=pl.Buffered(1))

    def part(columns, first, count):
        return pl.BlockSpec((tokens, columns), lambda s: (0, jnp.clip(s - first, 0, count - 1)))

    total = wides + downs
    flops = 6 * tokens * model * ffn
    arrays = (normed, dgate, dup, hidden, gout)
    moved = sum(math.prod(a.shape) * 2 for a in arrays) + chips * rows * model * 2
    return pl.pallas_call(
        grads_kernel,
        name="block_gradients",
        grid=(total + 1,),
        in_specs=[
            whole(normed),
            part(model, 0, half),
            part(model, half, half),
            part(chunk, wides, downs),
            whole(gout),
        ],
        out_specs=pl.BlockSpec(memory_space=pl.ANY),
        out_shape=jax.ShapeDtypeStruct((chips, rows, model), low),
        scratch_shapes=[
            pltpu.VMEM((model, tokens), low),
            pltpu.VMEM((2, 2, chips, wide_rows, model), low),
            pltpu.VMEM((2, 2, down_chips, down_rows, model), low),
            pltpu.VMEM((wides, chips, wide_rows, model), low),
            pltpu.VMEM((downs, down_chips, down_rows, model), low),
            pltpu.SemaphoreType.DMA((total,)),
            pltpu.SemaphoreType.DMA((total,)),
            pltpu.SemaphoreType.DMA((total,)),
        ],
        compiler_params=pltpu.CompilerParams(
            collective_id=2, has_side_effects=True, vmem_limit_bytes=VMEM_BYTES
        ),
        cost_estimate=pl.CostEstimate(flops=flops, bytes_accessed=moved, transcendentals=0),
    )(*arrays)


def passed_along(value, axis, steps):
    count = lax.axis_size(axis)
    leading, last = (max(0, -steps), min(count, count - steps))
    return lax.ppermute(value, axis, [(source, source + steps) for source in range(leading, last)])


def weight_grad(left, right):
    return lax.dot_general(
        left, right, (((0,), (0,)), ((), ())), preferred_element_type=jnp.float32
    ).astype(jnp.bfloat16)


def back_dot(left, right):
    return lax.dot_general(
        left, right, (((1,), (1,)), ((), ())), preferred_element_type=jnp.float32
    )


def fwd_dot(left, right):
    return jnp.dot(left, right, preferred_element_type=jnp.float32)


def gelu_fn(value):
    return jax.nn.gelu(value, approximate=True)


def norm_back(grad_norm, normed, inverse, gain):
    scaled = grad_norm * gain
    mean_term = jnp.mean(scaled * normed, axis=1, keepdims=True)
    return inverse * (scaled - normed * mean_term)


def scattered(gradient):
    return lax.psum_scatter(
        gradient, ("seq", "zed", "core"), scatter_dimension=0, tiled=True
    ).astype(jnp.float32)


def body(
    tokens,
    cotangent,
    doc_starts,
    lengths,
    norm1_gain,
    recur_input,
    recur_gate,
    conv_kernel,
    conv_bias,
    lru_gates,
    lru_bias,
    lru_decay,
    recur_out,
    norm2_gain,
    mlp_gate,
    mlp_up,
    mlp_down,
):
    count = lax.axis_size(CHAN)
    row_count, block_len = (tokens.shape[0] // count, tokens.shape[1])
    model_dim = tokens.shape[2] * count
    tok_count = row_count * block_len
    rec_width = recur_input.shape[1]
    ffn_width = mlp_gate.shape[1]
    head_count = H
    head_size = rec_width // head_count
    tap_count = conv_kernel.shape[0]
    rim_size = tap_count - 1
    seq_index = lax.axis_index("seq")
    position = seq_index * block_len + jnp.arange(block_len, dtype=jnp.int32)
    bounds = jnp.concatenate([doc_starts, lengths[:, None]], axis=1)
    is_before = bounds[:, None, :] <= position[None, :, None]
    seg_start = jnp.max(jnp.where(is_before, bounds[:, None, :], 0), axis=2)
    dist = jnp.broadcast_to(
        (position[None, :] - seg_start)[:, :, None], (row_count, block_len, LANES)
    )
    soft_decay = jax.nn.softplus(-lru_decay)
    params = jnp.concatenate(
        [
            conv_kernel,
            conv_bias[None],
            lru_bias,
            (-8.0 * soft_decay)[None],
            jnp.zeros((SUBLANES, rec_width), jnp.float32),
        ],
        axis=0,
    )
    core = Recurrence(row_count, block_len, rec_width, head_size)
    wide_gates = core.widen(lru_gates)
    if tokens.shape[2] % LANES == 0:
        blocks = [features_in(tokens, slice(row, row + 1)) for row in range(row_count)]
    else:
        side = features_in(tokens)
        blocks = [side[:, row * block_len : (row + 1) * block_len] for row in range(row_count)]
    single = Recurrence(1, block_len, rec_width, head_size)
    per_row = []
    for row in range(row_count):
        block = blocks[row]
        if row:
            block, _ = lax.optimization_barrier((block, per_row[-1][-1]))
        else:
            block, wide_gates, params, dist = lax.optimization_barrier(
                (block, wide_gates, params, dist)
            )
        low_x, inverse, normed, branch, pre, rim = front(block, norm1_gain, recur_input, recur_gate)
        branch, rim = (branch[None], rim[None])
        scanned = single.forward(branch, rim, dist[row : row + 1], params, wide_gates)
        per_row.append((low_x, inverse, normed, branch, pre[None], rim, *scanned))
    low_x, inverse, normed_low, branch, gate_pre, rim, lru_in, rate, igate, state, cum, last = zip(
        *per_row
    )
    entering, mixed_low, resid_one, normed_low2 = middle(
        last, state, cum, gate_pre, low_x, recur_out, norm2_gain
    )
    cotangent, _ = lax.optimization_barrier((cotangent, low_x[-1]))
    cotangent, resid_one = lax.optimization_barrier((features_in(cotangent), resid_one))
    grad_low, hidden_low, mgate_low, mup_low, result_parts, resid_low = mlp(
        lengths - seq_index * block_len,
        cotangent,
        normed_low2,
        resid_one,
        norm2_gain,
        mlp_gate,
        mlp_up,
        mlp_down,
    )
    output = features_out(result_parts, row_count)
    devices = lax.axis_size(("seq", "zed", "core"))
    own_rows = model_dim // devices
    tiled = own_rows % (2 * SUBLANES) == 0 and tokens.shape[2] % LANES == 0
    if tiled:
        merged = block_gradients(
            normed_low2, mgate_low, mup_low, hidden_low, grad_low
        )
        merged, resid_low = lax.optimization_barrier((merged, resid_low))
        merged = lax.psum_scatter(merged, "seq", scatter_dimension=0, tiled=True)
    gate_low, back_local, back_cum, first_term = core.adjoint(
        resid_low,
        recur_out,
        gate_pre,
        state,
        cum,
        entering,
        rate,
        dist,
        params,
    )
    gate_low = gate_low.reshape(tok_count, rec_width)
    branch_local, ending, leading, small = core.backward(
        back_local,
        back_cum,
        first_term,
        last,
        state,
        cum,
        entering,
        rate,
        igate,
        lru_in,
        dist,
        branch,
        rim,
        params,
        wide_gates,
    )
    branch_low = branch_local.reshape(tok_count, rec_width)
    if tiled:
        output, merged, branch_low = lax.optimization_barrier((output, merged, branch_low))
        merged = lax.psum_scatter(merged, "zed", scatter_dimension=0, tiled=True)
        grad_tokens, sum_rgate, sum_rout, sum_rin, own_small = tail(
            gate_low,
            branch_low,
            ending,
            leading,
            mixed_low,
            resid_low,
            norm1_gain,
            recur_input,
            recur_gate,
            small,
            normed_low,
            low_x,
            inverse,
        )
        own = merged[0].astype(jnp.float32)
        span = ffn_width // model_dim * own_rows

        def unfolded(part):
            return jnp.swapaxes(part.reshape(-1, own_rows, model_dim), 0, 1).reshape(own_rows, -1)

        sum_mgate, sum_mup = (unfolded(own[:span]), unfolded(own[span : 2 * span]))
        sum_down = own[2 * span :]
    else:
        from_next = passed_along(
            leading[:, SUBLANES - rim_size :, :].astype(jnp.bfloat16), "seq", -1
        )
        ending = ending + jnp.pad(
            from_next.astype(jnp.float32), ((0, 0), (SUBLANES - rim_size, 0), (0, 0))
        )
        branch_low = lax.dynamic_update_slice(
            branch_local, ending.astype(jnp.bfloat16), (0, block_len - SUBLANES, 0)
        ).reshape(tok_count, rec_width)
        grad_norm1 = back_dot(branch_low, recur_input) + back_dot(gate_low, recur_gate)
        inv_one = jnp.concatenate(inverse)[:, :1]
        normed_one = jnp.concatenate(low_x).astype(jnp.float32) * inv_one
        normed_low = jnp.concatenate(normed_low)
        input_part = norm_back(grad_norm1, normed_one, inv_one, norm1_gain)
        grad_x = (resid_low.astype(jnp.float32) + input_part).astype(jnp.bfloat16)
        grad_tokens = features_out(features_apart(grad_x), row_count)
        sum_mgate, sum_mup, sum_down, sum_rout, sum_rgate, sum_rin = (
            scattered(weight_grad(left, right))
            for left, right in (
                (normed_low2, mgate_low),
                (normed_low2, mup_low),
                (hidden_low, grad_low),
                (mixed_low, resid_low),
                (normed_low, gate_low),
                (normed_low, branch_low),
            )
        )
        own_small = scattered(small)
    sum_lgates = jnp.concatenate(
        [own_small[:, :head_size], own_small[:, LANES : LANES + head_size]], axis=1
    )
    own_sums = jnp.swapaxes(own_small[:, head_size : head_size + SUBLANES], 0, 1)
    device = lax.axis_index(("seq", "zed", "core"))

    def mine(array, size, axis=0):
        return lax.dynamic_slice_in_dim(array, device * size, size, axis)

    def weighed(weight, gradient):
        return jnp.sum(mine(weight, own_rows).astype(jnp.float32) * gradient, axis=1)

    sum_gain1 = (weighed(recur_input, sum_rin) + weighed(recur_gate, sum_rgate)) / mine(
        norm1_gain, own_rows
    )
    sum_gain2 = (weighed(mlp_gate, sum_mgate) + weighed(mlp_up, sum_mup)) / mine(
        norm2_gain, own_rows
    )
    own_channels = own_sums.shape[1]
    sum_decay = 8.0 * jax.nn.sigmoid(-mine(lru_decay, own_channels)) * own_sums[7]
    return (
        output,
        grad_tokens,
        sum_gain1,
        sum_rin,
        sum_rgate,
        own_sums[:4],
        own_sums[4],
        sum_lgates,
        own_sums[5:7],
        sum_decay,
        sum_rout,
        sum_gain2,
        sum_mgate,
        sum_mup,
        sum_down,
    )


def solution(mesh):
    seq, chan = (mesh.shape["seq"], mesh.shape["chan"])
    chips = jax.sharding.Mesh(mesh.devices.reshape(seq, chan // 2, 2), ("seq", "zed", "core"))
    chan = ("zed", "core")
    every = ("seq", "zed", "core")
    activations = P(None, "seq", chan)
    rows, columns, vector = (P(every, None), P(None, every), P(every))
    return jax.shard_map(
        body,
        mesh=chips,
        in_specs=(activations, activations, P(chan, None), P(chan)) + (P(),) * 13,
        out_specs=(
            activations,
            activations,
            vector,
            rows,
            rows,
            columns,
            vector,
            rows,
            columns,
            vector,
            rows,
            vector,
            rows,
            rows,
            rows,
        ),
        check_vma=False,
    )
```

```python
import functools
import math

import jax
import jax.numpy as jnp
from jax import lax
from jax.experimental import pallas as pl
from jax.experimental.pallas import tpu as pltpu
from jax.sharding import PartitionSpec as P

H = 16


EPS = 1e-06
ROOT_FLOOR = 1e-06
LANES = 128
SUBLANES = 8
STEP = 16
VMEM_BYTES = 56 * 1024 * 1024
MESH = pl.DeviceIdType.MESH


def sigmoid(value):
    return 0.5 * jnp.tanh(0.5 * value) + 0.5


GELU_C = 0.7978845608
GELU_A = 0.044715


def gelu_pair(value):
    square = value * value
    inner = jnp.tanh(value * (GELU_C + (GELU_C * GELU_A) * square))
    half = 0.5 + 0.5 * inner
    slope = GELU_C + (3.0 * GELU_C * GELU_A) * square
    return (value * half, half + 0.5 * value * (1.0 - inner * inner) * slope)


def root_argument(log_decay, decay):
    y = 2.0 * log_decay
    series = 1.0 + y * (0.5 + y * (1.0 / 6.0 + y * (1.0 / 24.0)))
    return jnp.where(y > -0.05, -y * series, 1.0 - decay * decay)


def across(column, width):
    return jnp.concatenate([column] * (width // LANES), axis=1)


class Rows:
    def __init__(self, refs):
        self.refs = refs

    def __getitem__(self, index):
        if not isinstance(index, tuple):
            return self.refs[index][0]
        return self.refs[index[0]][(0,) + index[1:]]


def by_rows(refs, rows, apart):
    found = []
    for split in apart:
        count = rows if split else 1
        found.append(Rows(refs[:count]) if split else refs[0])
        refs = refs[count:]
    return found, refs


def forward_kernel(
    branch_ref,
    rim_ref,
    dist_ref,
    par_ref,
    gates_ref,
    lru_ref,
    rate_ref,
    igate_ref,
    state_ref,
    cum_ref,
    last_ref,
    both_ref,
):
    rows, length, width = branch_ref.shape
    span = 2 * STEP if rows == 1 else STEP
    taps = [par_ref[k : k + 1, :] for k in range(4)]
    conv_bias, rate_bias, input_bias, soft = (par_ref[k : k + 1, :] for k in range(4, 8))
    place = lax.broadcasted_iota(jnp.int32, (SUBLANES, width), 0)

    for row in range(rows):

        def conv_step(index, before, row=row):
            base = pl.multiple_of(index * STEP, STEP)
            pieces = []
            for half in range(STEP // SUBLANES):
                at = pl.ds(base + half * SUBLANES, SUBLANES)
                here = branch_ref[row, at, :]
                dist = across(dist_ref[row, at, :], width)
                total = conv_bias + taps[0] * here
                for k in range(1, 4):
                    shifted = pltpu.roll(jnp.where(place < SUBLANES - k, here, before), k, 0)
                    total = total + taps[k] * jnp.where(dist >= k, shifted, 0.0)
                pieces.append(total)
                before = here
            lru_ref[row, pl.ds(base, STEP), :] = jnp.concatenate(pieces, axis=0).astype(jnp.bfloat16)
            return before

        lax.fori_loop(0, length // STEP, conv_step, rim_ref[row])

        piece = min(length, 256)

        def dot_step(index, carry, row=row):
            at = pl.ds(pl.multiple_of(index * piece, piece), piece)
            both_ref[row, at, :] = jnp.dot(
                lru_ref[row, at, :], gates_ref[...], preferred_element_type=jnp.float32
            )
            return carry

        lax.fori_loop(0, length // piece, dot_step, 0)

    def scan_step(index, carry):
        base = pl.multiple_of(index * span, span)
        later = []
        for row in range(rows):
            run_cum, run_state = carry[row]
            lru_both = lru_ref[row, pl.ds(base, span), :].astype(jnp.float32)
            for half in range(span // SUBLANES):
                at = pl.ds(base + half * SUBLANES, SUBLANES)
                lru = lru_both[half * SUBLANES : (half + 1) * SUBLANES]
                start = across(dist_ref[row, at, :], width) == 0
                rate = sigmoid(both_ref[row, at, :width] + rate_bias)
                igate = sigmoid(both_ref[row, at, width:] + input_bias)
                log_decay = rate * soft
                decay = jnp.exp(log_decay)
                arg = jnp.maximum(root_argument(log_decay, decay), ROOT_FLOOR)
                root = arg * lax.rsqrt(arg)
                cum = jnp.where(start, 0.0, decay)
                value = jnp.where(start, 1.0, root) * igate * lru
                rate_ref[row, at, :] = rate
                igate_ref[row, at, :] = igate
                for shift in (1, 2, 4):
                    live = place >= shift
                    value = value + cum * jnp.where(live, pltpu.roll(value, shift, 0), 0.0)
                    cum = cum * jnp.where(live, pltpu.roll(cum, shift, 0), 1.0)
                value = value + cum * run_state
                cum = cum * run_cum
                state_ref[row, at, :] = value
                cum_ref[row, at, :] = cum
                run_state = value[SUBLANES - 1 :, :]
                run_cum = cum[SUBLANES - 1 :, :]
            later.append((run_cum, run_state))
        return tuple(later)

    one, zero = (jnp.ones((1, width), jnp.float32), jnp.zeros((1, width), jnp.float32))
    done = lax.fori_loop(0, length // span, scan_step, tuple((one, zero) for _ in range(rows)))
    for row in range(rows):
        for place in range(2):
            last_ref[row, place : place + 1, :] = done[row][place]


def carried(sent_ref, got_ref, out_ref, send_sem, recv_sem, backward):
    seq, count = (lax.axis_index("seq"), lax.axis_size("seq"))

    def other(step):
        return {"seq": lax.rem(seq + step, count)}

    barrier = pltpu.get_barrier_semaphore()
    for step in range(1, count):
        pl.semaphore_signal(barrier, inc=1, device_id=other(step), device_id_type=MESH)
    pl.semaphore_wait(barrier, count - 1)
    copies = [
        pltpu.make_async_remote_copy(
            src_ref=sent_ref,
            dst_ref=got_ref.at[seq],
            send_sem=send_sem.at[step - 1],
            recv_sem=recv_sem.at[step - 1],
            device_id=other(step),
            device_id_type=MESH,
        )
        for step in range(1, count)
    ]
    for copy in copies:
        copy.start()
    got_ref[seq] = sent_ref[...]
    for copy in copies:
        copy.wait()
    for row in range(sent_ref.shape[0]):
        total = jnp.zeros(out_ref.shape[1:], jnp.float32)
        for place in range(count - 1, 0, -1) if backward else range(count - 1):
            longer = got_ref[place, row, 0:1, :] * total + got_ref[place, row, 1:2, :]
            total = jnp.where(place > seq if backward else place < seq, longer, total)
        out_ref[row] = total


def adjoint_kernel(rows, *refs):
    (
        dres_ref,
        weight_ref,
        pre_ref,
        state_ref,
        cum_ref,
        carry_ref,
        rate_ref,
        dist_ref,
        par_ref,
    ), outs = by_rows(refs, rows, (False, False, True, True, True, False, True, False, False))
    dgate_ref, local_ref, back_ref, first_ref, dmix_ref = outs
    _, length, width = dmix_ref.shape
    for row in range(rows):
        dmix_ref[row] = lax.dot_general(
            dres_ref[row * length : (row + 1) * length, :],
            weight_ref[...],
            (((1,), (1,)), ((), ())),
            preferred_element_type=jnp.float32,
        )
    soft = par_ref[7:8, :]
    place = lax.broadcasted_iota(jnp.int32, (SUBLANES, width), 0)
    last = length // STEP - 1

    def step(index, carry):
        base = pl.multiple_of((last - index) * STEP, STEP)
        later = []
        for row in range(rows):
            run_cum, run_back = carry[row]
            entering = carry_ref[row]
            pieces = []
            for half in reversed(range(STEP // SUBLANES)):
                at = pl.ds(base + half * SUBLANES, SUBLANES)
                start = across(dist_ref[row, at, :], width) == 0
                state = state_ref[row, at, :] + cum_ref[row, at, :] * entering
                act, slope = gelu_pair(pre_ref[row, at, :])
                dmix = dmix_ref[row, at, :]
                pieces.append(dmix * state * slope)
                dstate = dmix * act
                coef = jnp.where(start, 0.0, jnp.exp(rate_ref[row, at, :] * soft))
                value = coef * dstate
                for shift in (1, 2, 4):
                    live = place < SUBLANES - shift
                    turn = SUBLANES - shift
                    value = value + coef * jnp.where(live, pltpu.roll(value, turn, 0), 0.0)
                    coef = coef * jnp.where(live, pltpu.roll(coef, turn, 0), 1.0)
                value = value + coef * run_back
                coef = coef * run_cum
                inside = place < SUBLANES - 1
                local_ref[row, at, :] = dstate + jnp.where(
                    inside, pltpu.roll(value, SUBLANES - 1, 0), run_back
                )
                back_ref[row, at, :] = jnp.where(inside, pltpu.roll(coef, SUBLANES - 1, 0), run_cum)
                run_back = value[:1, :]
                run_cum = coef[:1, :]
            dgate_ref[row, pl.ds(base, STEP), :] = jnp.concatenate(pieces[::-1], axis=0).astype(
                jnp.bfloat16
            )
            later.append((run_cum, run_back))
        return tuple(later)

    one, zero = (jnp.ones((1, width), jnp.float32), jnp.zeros((1, width), jnp.float32))
    done = lax.fori_loop(0, last + 1, step, tuple((one, zero) for _ in range(rows)))
    for row in range(rows):
        first_ref[row] = done[row][1]


def backward_kernel(head_size, rows, *refs):
    (
        local_ref,
        back_ref,
        first_ref,
        last_ref,
        state_ref,
        cum_ref,
        in_ref,
        rate_ref,
        igate_ref,
        lru_ref,
        dist_ref,
        branch_ref,
        rim_ref,
        par_ref,
        gates_ref,
    ), others = by_rows(
        refs, rows, (False,) * 3 + (True,) * 3 + (False,) + (True,) * 3 + (False,) + (True,) * 2 + (False,) * 2
    )
    dbranch_ref, tail_ref, head_ref, dgates_ref, both_ref, dconv_ref, sums_ref = others[:7]
    leaving_ref, sent_ref, got_ref, send_sem, recv_sem = others[7:]
    _, length, width = local_ref.shape

    @pl.when(pl.program_id(0) == 0)
    def _():
        for row in range(rows):
            sent_ref[row, 0:1, :] = last_ref[row, 0:1, :]
            sent_ref[row, 1:2, :] = first_ref[row]
        carried(sent_ref, got_ref, leaving_ref, send_sem, recv_sem, True)

    block = pl.ds(pl.multiple_of(pl.program_id(0) * width, width), width)
    taps = [par_ref[k : k + 1, :] for k in range(4)]
    soft = par_ref[7:8, :]
    place = lax.broadcasted_iota(jnp.int32, (SUBLANES, width), 0)
    zeros = jnp.zeros((SUBLANES, width), jnp.float32)

    def gate_step(index, carry):
        sums, earlier = carry
        decay_sum, rate_sum, input_sum = sums
        base = pl.multiple_of(index * STEP, STEP)
        later = []
        for row in range(rows):
            before = earlier[row]
            entering = in_ref[row]
            leaving = leaving_ref[row, :, block]
            lru_both = lru_ref[row, pl.ds(base, STEP), :].astype(jnp.float32)
            drates, dinputs = ([], [])
            for half in range(STEP // SUBLANES):
                at = pl.ds(base + half * SUBLANES, SUBLANES)
                lru = lru_both[half * SUBLANES : (half + 1) * SUBLANES]
                start = across(dist_ref[row, at, :], width) == 0
                adjoint = local_ref[row, at, :] + back_ref[row, at, :] * leaving
                state = state_ref[row, at, :] + cum_ref[row, at, :] * entering
                previous = jnp.where(place < 1, before, pltpu.roll(state, 1, 0))
                before = state[SUBLANES - 1 :, :]
                rate = rate_ref[row, at, :]
                igate = igate_ref[row, at, :]
                log_decay = rate * soft
                decay = jnp.exp(log_decay)
                arg = root_argument(log_decay, decay)
                above = arg > ROOT_FLOOR
                arg = jnp.maximum(arg, ROOT_FLOOR)
                inverse = lax.rsqrt(arg)
                scale = jnp.where(start, 1.0, arg * inverse)
                gated = adjoint * igate
                dscale = gated * lru
                pull = jnp.where(above, dscale * decay * decay * inverse, 0.0)
                dlog = jnp.where(start, 0.0, adjoint * previous * decay - pull)
                dig = adjoint * scale * lru
                weighted = dlog * rate
                decay_sum = decay_sum + weighted
                drates.append(weighted * soft * (1.0 - rate))
                dinputs.append(dig * igate * (1.0 - igate))
                dconv_ref[row, at, :] = gated * scale
            drate = jnp.concatenate(drates, axis=0).astype(jnp.bfloat16)
            dinput = jnp.concatenate(dinputs, axis=0).astype(jnp.bfloat16)
            both_ref[row, pl.ds(base, STEP), :width] = drate
            both_ref[row, pl.ds(base, STEP), width:] = dinput
            drate = drate.astype(jnp.float32)
            dinput = dinput.astype(jnp.float32)
            rate_sum = rate_sum + (drate[:SUBLANES] + drate[SUBLANES:])
            input_sum = input_sum + (dinput[:SUBLANES] + dinput[SUBLANES:])
            later.append(before)
        return ((decay_sum, rate_sum, input_sum), tuple(later))

    sums, _ = lax.fori_loop(
        0,
        length // STEP,
        gate_step,
        ((zeros, zeros, zeros), tuple(in_ref[row] for row in range(rows))),
    )
    for slot, total in zip((5, 6, 7), (sums[1], sums[2], sums[0] * par_ref[8:9, :])):
        sums_ref[slot : slot + 1, :] = jnp.sum(total, axis=0, keepdims=True)

    piece = min(length, 256)
    wide = None
    for row in range(rows):

        def dot_step(index, carry, row=row):
            at = pl.ds(pl.multiple_of(index * piece, piece), piece)
            dconv_ref[row, at, :] += lax.dot_general(
                both_ref[row, at, :],
                gates_ref[...],
                (((1,), (1,)), ((), ())),
                preferred_element_type=jnp.float32,
            )
            return carry

        lax.fori_loop(0, length // piece, dot_step, 0)
        part = lax.dot_general(
            lru_ref[row], both_ref[row], (((0,), (0,)), ((), ())), preferred_element_type=jnp.float32
        )
        wide = part if wide is None else wide + part
    row_head = lax.broadcasted_iota(jnp.int32, (width, width), 0) // head_size
    col_head = lax.broadcasted_iota(jnp.int32, (width, width), 1) // head_size
    own = row_head == col_head
    folds = []
    for part in range(2):
        kept = jnp.where(own, wide[:, part * width : (part + 1) * width], 0.0)
        folded = kept
        for other in range(1, width // head_size):
            folded = folded + pltpu.roll(kept, width - other * head_size, 1)
        folds.append(folded[:, :LANES])

    def conv_step(index, carry):
        sums, following = carry
        sums = list(sums)
        base = pl.multiple_of((length // STEP - 1 - index) * STEP, STEP)
        later = []
        for row in range(rows):
            after = following[row]
            pieces = []
            for half in reversed(range(STEP // SUBLANES)):
                at = pl.ds(base + half * SUBLANES, SUBLANES)
                dist = across(dist_ref[row, at, :], width)
                branch = branch_ref[row, at, :]
                here = dconv_ref[row, at, :]
                total = taps[0] * here
                sums[0] = sums[0] + here * branch
                sums[4] = sums[4] + here
                masked = tuple(jnp.where(dist >= k, here, 0.0) for k in range(1, 4))
                for k in range(1, 4):
                    moved = pltpu.roll(
                        jnp.where(place >= k, masked[k - 1], after[k - 1]), SUBLANES - k, 0
                    )
                    total = total + taps[k] * moved
                    sums[k] = sums[k] + branch * moved
                after = masked
                pieces.append(total)
            whole = jnp.concatenate(pieces[::-1], axis=0)
            dbranch_ref[row, pl.ds(base, STEP), :] = whole.astype(jnp.bfloat16)
            later.append(after)

            @pl.when(index == 0)
            def _(row=row, whole=whole):
                tail_ref[row] = whole[STEP - SUBLANES :]

        return (tuple(sums), tuple(later))

    sums, firsts = lax.fori_loop(
        0,
        length // STEP,
        conv_step,
        ((zeros,) * 5, tuple((zeros,) * 3 for _ in range(rows))),
    )
    sums = list(sums)
    for row in range(rows):
        total = zeros
        rim = rim_ref[row]
        for k in range(1, 4):
            moved = pltpu.roll(jnp.where(place >= k, 0.0, firsts[row][k - 1]), SUBLANES - k, 0)
            total = total + taps[k] * moved
            sums[k] = sums[k] + rim * moved
        head_ref[row] = total
    for slot in range(5):
        sums_ref[slot : slot + 1, :] = jnp.sum(sums[slot], axis=0, keepdims=True)
    above = jnp.zeros((head_size, width), jnp.float32)
    below = jnp.zeros((LANES - head_size - SUBLANES, width), jnp.float32)
    turned = jnp.concatenate([above, sums_ref[...], below], axis=0).T
    lane = lax.broadcasted_iota(jnp.int32, (width, LANES), 1)
    dgates_ref[:, :LANES] = jnp.where(lane < head_size, folds[0], turned).astype(dgates_ref.dtype)
    dgates_ref[:, LANES:] = folds[1].astype(dgates_ref.dtype)


def channel_call(
    kernel, name, arrays, specs, outs, out_specs, scratch, blocks, flops, params=()
):
    moved = sum(math.prod(a.shape) * a.dtype.itemsize for a in (*arrays, *outs))
    return pl.pallas_call(
        kernel,
        name=name,
        grid=(blocks,),
        in_specs=specs,
        out_specs=out_specs,
        out_shape=outs,
        scratch_shapes=scratch,
        compiler_params=pltpu.CompilerParams(vmem_limit_bytes=VMEM_BYTES, **dict(params)),
        cost_estimate=pl.CostEstimate(flops=flops, bytes_accessed=moved, transcendentals=0),
    )(*arrays)


class Recurrence:
    def __init__(self, rows, length, channels, head_size):
        self.rows, self.length, self.channels = (rows, length, channels)
        self.head_size = head_size
        self.width = head_size * LANES // math.gcd(head_size, LANES)
        self.blocks = channels // self.width
        self.flops = 2 * rows * length * channels * 2 * self.width

    def tall(self):
        return pl.BlockSpec((self.rows, self.length, self.width), lambda j: (0, 0, j))

    def short(self, size):
        return pl.BlockSpec((self.rows, size, self.width), lambda j: (0, 0, j))

    def apart(self, size):
        return [pl.BlockSpec((1, size, self.width), lambda j: (0, 0, j))] * self.rows

    def whole(self, rows, size):
        return pl.BlockSpec((rows, size, self.channels), lambda j: (0, 0, 0))

    def flat(self, size):
        return pl.BlockSpec((size, self.width), lambda j: (0, j))

    def dist(self):
        return pl.BlockSpec((self.rows, self.length, LANES), lambda j: (0, 0, 0))

    def gates(self, columns):
        return pl.BlockSpec((self.width, columns), lambda j: (j, 0))

    def shape(self, size, dtype):
        return jax.ShapeDtypeStruct((self.rows, size, self.channels), dtype)

    def widen(self, lru_gates):
        size, width = (self.head_size, self.width)
        heads = width // size
        column = jnp.arange(2 * width)
        source = (column // width) * size + column % size
        spread = (jnp.arange(2 * size)[:, None] == source[None, :]).astype(jnp.bfloat16)
        owner = (column % width) // size
        mine = (jnp.arange(self.channels) // size) % heads
        wide = jnp.dot(lru_gates, spread, preferred_element_type=jnp.float32)
        return jnp.where(mine[:, None] == owner[None, :], wide, 0.0).astype(jnp.bfloat16)

    def forward(self, branch, rim, dist, params, gates):
        f32 = jnp.float32
        outs = [self.shape(self.length, d) for d in (jnp.bfloat16, f32, f32, f32, f32)]
        return channel_call(
            forward_kernel,
            "recurrence_forward",
            (branch, rim, dist, params, gates),
            [self.tall(), self.short(SUBLANES), self.dist(), self.flat(16), self.gates(2 * self.width)],
            outs + [self.shape(2, f32)],
            [self.tall()] * 5 + [self.short(2)],
            [pltpu.VMEM((self.rows, self.length, 2 * self.width), f32)],
            self.blocks,
            self.flops,
        )

    def adjoint(self, dres, weight, pre, state, cum, entering, rate, dist, params):
        f32 = jnp.float32
        outs = [self.shape(self.length, d) for d in (jnp.bfloat16, f32, f32)] + [self.shape(1, f32)]
        tall, apart = (self.tall(), self.apart(self.length))
        return channel_call(
            functools.partial(adjoint_kernel, self.rows),
            "recurrence_adjoint",
            (dres, weight, *pre, *state, *cum, entering, *rate, dist, params),
            [
                pl.BlockSpec(dres.shape, lambda j: (0, 0)),
                self.gates(weight.shape[1]),
                *apart * 3,
                self.short(1),
                *apart,
                self.dist(),
                self.flat(16),
            ],
            outs,
            [tall, tall, tall, self.short(1)],
            [pltpu.VMEM((self.rows, self.length, self.width), f32)],
            self.blocks,
            2 * self.rows * self.length * weight.size,
        )

    def backward(
        self, local, back, first, last, state, cum, entering, rate, igate, lru, dist, branch, rim, params, gates
    ):
        f32 = jnp.float32
        outs = [
            self.shape(self.length, jnp.bfloat16),
            self.shape(SUBLANES, f32),
            self.shape(SUBLANES, f32),
            jax.ShapeDtypeStruct((self.channels, 2 * LANES), jnp.bfloat16),
        ]
        tall, apart = (self.tall(), self.apart(self.length))
        seqs = lax.axis_size("seq")
        summary = (self.rows, 2, self.channels)
        return channel_call(
            functools.partial(backward_kernel, self.head_size, self.rows),
            "recurrence_backward",
            (local, back, first, *last, *state, *cum, entering, *rate, *igate, *lru, dist, *branch, *rim)
            + (params, gates),
            [tall, tall, self.whole(self.rows, 1), *[self.whole(1, 2)] * self.rows, *apart * 2]
            + [self.short(1), *apart * 3, self.dist(), *apart, *self.apart(SUBLANES)]
            + [self.flat(16), self.gates(2 * self.width)],
            outs,
            [tall, self.short(SUBLANES), self.short(SUBLANES), self.gates(2 * LANES)],
            [
                pltpu.VMEM((self.rows, self.length, 2 * self.width), jnp.bfloat16),
                pltpu.VMEM((self.rows, self.length, self.width), f32),
                pltpu.VMEM((SUBLANES, self.width), f32),
                pltpu.VMEM((self.rows, 1, self.channels), f32),
                pltpu.VMEM(summary, f32),
                pltpu.VMEM((seqs,) + summary, f32),
                pltpu.SemaphoreType.DMA((seqs - 1,)),
                pltpu.SemaphoreType.DMA((seqs - 1,)),
            ],
            self.blocks,
            2 * self.flops,
            {"collective_id": 5, "has_side_effects": True},
        )


def gathered(parts_ref, at):
    return jnp.concatenate([parts_ref[k, at, :] for k in range(parts_ref.shape[0])], axis=1)


def front_kernel(
    parts_ref,
    gain_ref,
    input_ref,
    gate_ref,
    x_ref,
    inverse_ref,
    normed_ref,
    branch_ref,
    pre_ref,
    rim_ref,
    edge_ref,
    landed_ref,
    send_sem,
    recv_sem,
):
    tokens = x_ref.shape[0]
    piece, tall = (64, min(tokens, 512))
    step, steps = (pl.program_id(0), edge_ref.shape[0])
    seq, seqs = (lax.axis_index("seq"), lax.axis_size("seq"))
    barrier = pltpu.get_barrier_semaphore()

    @pl.when(step == 0)
    def _():
        before = {"seq": lax.rem(seq + seqs - 1, seqs)}
        pl.semaphore_signal(barrier, inc=1, device_id=before, device_id_type=MESH)

        def norm(index, carry):
            at = pl.ds(pl.multiple_of(index * piece, piece), piece)
            low = gathered(parts_ref, at)
            x_ref[at, :] = low
            value = low.astype(jnp.float32)
            inverse = lax.rsqrt(jnp.mean(value * value, axis=1, keepdims=True) + EPS)
            inverse_ref[at, :] = jnp.broadcast_to(inverse, (piece, LANES))
            normed_ref[at, :] = (value * inverse * gain_ref[...]).astype(jnp.bfloat16)
            return carry

        lax.fori_loop(0, tokens // piece, norm, 0, unroll=2)

    def multiply(index, carry):
        at = pl.ds(pl.multiple_of(index * tall, tall), tall)
        normed = normed_ref[at, :]
        branch_ref[at, :] = jnp.dot(normed, input_ref[...], preferred_element_type=jnp.float32)
        pre_ref[at, :] = jnp.dot(normed, gate_ref[...], preferred_element_type=jnp.float32)
        return carry

    lax.fori_loop(0, tokens // tall, multiply, 0)
    edge_ref[step] = branch_ref[tokens - SUBLANES :, :]

    def rim_copy(place):
        return pltpu.make_async_remote_copy(
            src_ref=edge_ref.at[place],
            dst_ref=landed_ref.at[place],
            send_sem=send_sem.at[place],
            recv_sem=recv_sem.at[place],
            device_id={"seq": lax.rem(seq + 1, seqs)},
            device_id_type=MESH,
        )

    @pl.when(step == 0)
    def _():
        pl.semaphore_wait(barrier, 1)

    rim_copy(step).start()

    @pl.when(step == steps - 1)
    def _():
        columns = edge_ref.shape[2]
        live = jnp.where(seq > 0, 1.0, 0.0)
        for place in range(steps):
            rim_copy(place).wait()
            rim_ref[:, place * columns : (place + 1) * columns] = live * landed_ref[place]


def front(parts, gain, recur_input, recur_gate):
    count, tokens, width = parts.shape
    model, rec = recur_input.shape
    columns = 4 * LANES
    steps = rec // columns
    low, f32 = (jnp.bfloat16, jnp.float32)
    tall = pl.BlockSpec((model, columns), lambda j: (0, j))
    wide = pl.BlockSpec((tokens, columns), lambda j: (0, j))

    def whole(shape):
        return pl.BlockSpec(shape, lambda j: (0,) * len(shape))

    return pl.pallas_call(
        front_kernel,
        name="norm_and_project",
        grid=(steps,),
        in_specs=[whole(parts.shape), whole((1, model)), tall, tall],
        out_specs=[whole((tokens, model)), whole((tokens, LANES)), whole((tokens, model)), wide, wide]
        + [whole((SUBLANES, rec))],
        out_shape=[
            jax.ShapeDtypeStruct((tokens, model), low),
            jax.ShapeDtypeStruct((tokens, LANES), f32),
            jax.ShapeDtypeStruct((tokens, model), low),
            jax.ShapeDtypeStruct((tokens, rec), f32),
            jax.ShapeDtypeStruct((tokens, rec), f32),
            jax.ShapeDtypeStruct((SUBLANES, rec), f32),
        ],
        scratch_shapes=[
            pltpu.VMEM((steps, SUBLANES, columns), f32),
            pltpu.VMEM((steps, SUBLANES, columns), f32),
            pltpu.SemaphoreType.DMA((steps,)),
            pltpu.SemaphoreType.DMA((steps,)),
        ],
        compiler_params=pltpu.CompilerParams(
            collective_id=3, has_side_effects=True, vmem_limit_bytes=VMEM_BYTES
        ),
        cost_estimate=pl.CostEstimate(
            flops=4 * tokens * model * rec, bytes_accessed=20 * tokens * model, transcendentals=0
        ),
    )(parts, gain[None], recur_input, recur_gate)


def middle_kernel(rows, *refs):
    (last_ref, state_ref, cum_ref, pre_ref, x_ref, out_ref, gain_ref), others = by_rows(
        refs, rows, (True,) * 5 + (False,) * 2
    )
    entering_ref, mixed_ref, resid_ref, normed_ref = others[:4]
    sent_ref, got_ref, send_sem, recv_sem = others[4:]
    tall, model = resid_ref.shape
    step = pl.program_id(0)
    tiles = pl.num_programs(0) // rows
    slab = 16

    @pl.when(step == 0)
    def _():
        for row in range(rows):
            sent_ref[row] = last_ref[row]
        carried(sent_ref, got_ref, entering_ref, send_sem, recv_sem, False)

    for row in range(rows):

        @pl.when(lax.div(step, tiles) == row)
        def _(row=row):
            def mix(index, carry):
                at = pl.ds(pl.multiple_of(index * slab, slab), slab)
                state = state_ref[row, at, :] + cum_ref[row, at, :] * entering_ref[row]
                pre = pre_ref[row, at, :]
                inner = jnp.tanh(pre * (GELU_C + (GELU_C * GELU_A) * (pre * pre)))
                mixed_ref[at, :] = (state * (pre * (0.5 + 0.5 * inner))).astype(jnp.bfloat16)
                return carry

            lax.fori_loop(0, tall // slab, mix, 0, unroll=2)
            tile = 512
            for first in range(0, model, tile):
                at = slice(first, first + tile)
                resid_ref[:, at] = x_ref.refs[row][:, at].astype(jnp.float32) + jnp.dot(
                    mixed_ref[...], out_ref[:, at], preferred_element_type=jnp.float32
                )

    def norm(index, carry):
        at = pl.ds(pl.multiple_of(index * slab, slab), slab)
        resid = resid_ref[at, :]
        inverse = lax.rsqrt(jnp.mean(resid * resid, axis=1, keepdims=True) + EPS)
        normed_ref[at, :] = (resid * inverse * gain_ref[...]).astype(jnp.bfloat16)
        return carry

    lax.fori_loop(0, tall // slab, norm, 0, unroll=4)


def middle(last, state, cum, pre, x, recur_out, gain):
    rows = len(state)
    _, length, rec = state[0].shape
    model = recur_out.shape[1]
    tall = min(length, 256)
    tiles = length // tall
    tokens = rows * length
    seqs = lax.axis_size("seq")
    low, f32 = (jnp.bfloat16, jnp.float32)

    def whole(shape):
        return pl.BlockSpec(shape, lambda s: (0,) * len(shape), pipeline_mode=pl.Buffered(1))

    def part(row):
        return lambda s: (0, jnp.clip(s - row * tiles, 0, tiles - 1), 0)

    def flat(row):
        return lambda s: (jnp.clip(s - row * tiles, 0, tiles - 1), 0)

    apart = [pl.BlockSpec((1, tall, rec), part(row)) for row in range(rows)]
    summary = (rows, 2, rec)
    return pl.pallas_call(
        functools.partial(middle_kernel, rows),
        name="mix_and_norm",
        grid=(rows * tiles,),
        in_specs=[whole((1, 2, rec))] * rows
        + apart * 3
        + [pl.BlockSpec((tall, model), flat(row)) for row in range(rows)]
        + [whole(recur_out.shape), whole((1, model))],
        out_specs=[
            pl.BlockSpec((rows, 1, rec), lambda s: (0, 0, 0)),
            pl.BlockSpec((tall, rec), lambda s: (s, 0)),
            pl.BlockSpec((tall, model), lambda s: (s, 0)),
            pl.BlockSpec((tall, model), lambda s: (s, 0)),
        ],
        out_shape=[
            jax.ShapeDtypeStruct((rows, 1, rec), f32),
            jax.ShapeDtypeStruct((tokens, rec), low),
            jax.ShapeDtypeStruct((tokens, model), f32),
            jax.ShapeDtypeStruct((tokens, model), low),
        ],
        scratch_shapes=[
            pltpu.VMEM(summary, f32),
            pltpu.VMEM((seqs,) + summary, f32),
            pltpu.SemaphoreType.DMA((seqs - 1,)),
            pltpu.SemaphoreType.DMA((seqs - 1,)),
        ],
        compiler_params=pltpu.CompilerParams(
            collective_id=4, has_side_effects=True, vmem_limit_bytes=VMEM_BYTES
        ),
        cost_estimate=pl.CostEstimate(
            flops=2 * tokens * rec * model, bytes_accessed=14 * tokens * rec, transcendentals=0
        ),
    )(*last, *state, *cum, *pre, *x, recur_out, gain[None])


def hidden_kernel(
    left_ref,
    parts_ref,
    normed_ref,
    gate_ref,
    up_ref,
    down_ref,
    gout_ref,
    hidden_ref,
    dgate_ref,
    dup_ref,
):
    tokens, model = normed_ref.shape
    chunk = down_ref.shape[0]
    rows = left_ref.shape[0]
    length = tokens // rows
    slab = 32

    @pl.when(pl.program_id(0) == 0)
    def _():
        for row in range(rows):

            def collect(index, carry, row=row):
                base = pl.multiple_of(index * slab, slab)
                at = pl.ds(row * length + base, slab)
                low = gathered(parts_ref, at)
                place = base + lax.broadcasted_iota(jnp.int32, low.shape, 0)
                value = jnp.where(place < left_ref[row], low.astype(jnp.float32), 0.0)
                gout_ref[at, :] = value.astype(jnp.bfloat16)
                return carry

            lax.fori_loop(0, length // slab, collect, 0)

    tall = min(tokens, 512)
    wide = 256

    def tile(index, carry):
        at = pl.ds(pl.multiple_of(index * tall, tall), tall)
        for column in range(chunk // wide):
            own = slice(column * wide, (column + 1) * wide)
            gate = jnp.dot(normed_ref[at, :], gate_ref[:, own], preferred_element_type=jnp.float32)
            up = jnp.dot(normed_ref[at, :], up_ref[:, own], preferred_element_type=jnp.float32)
            dhid = lax.dot_general(
                gout_ref[at, :],
                down_ref[own, :],
                (((1,), (1,)), ((), ())),
                preferred_element_type=jnp.float32,
            )
            act, slope = gelu_pair(gate)
            hidden_ref[at, own] = (act * up).astype(jnp.bfloat16)
            dgate_ref[at, own] = (dhid * up * slope).astype(jnp.bfloat16)
            dup_ref[at, own] = (dhid * act).astype(jnp.bfloat16)
        return carry

    lax.fori_loop(0, tokens // tall, tile, 0)


def back_kernel(
    hidden_ref,
    dgate_ref,
    dup_ref,
    gout_ref,
    resid_ref,
    gain_ref,
    gate_ref,
    up_ref,
    down_ref,
    result_ref,
    dres_ref,
    total_ref,
    back_ref,
):
    tokens, model = resid_ref.shape
    step = pl.program_id(0)

    @pl.when(step == 0)
    def _():
        total_ref[...] = resid_ref[...]
        back_ref[...] = jnp.zeros_like(back_ref)

    tall = min(tokens, 512)
    wide = 512

    def tile(index, carry):
        at = pl.ds(pl.multiple_of(index * tall, tall), tall)
        contract = (((1,), (1,)), ((), ()))
        for column in range(model // wide):
            own = slice(column * wide, (column + 1) * wide)
            total_ref[at, own] += jnp.dot(
                hidden_ref[at, :], down_ref[:, own], preferred_element_type=jnp.float32
            )
            back_ref[at, own] += lax.dot_general(
                dgate_ref[at, :], gate_ref[own, :], contract, preferred_element_type=jnp.float32
            ) + lax.dot_general(
                dup_ref[at, :], up_ref[own, :], contract, preferred_element_type=jnp.float32
            )
        return carry

    lax.fori_loop(0, tokens // tall, tile, 0)

    @pl.when(step == pl.num_programs(0) - 1)
    def _():
        parts, width = (result_ref.shape[0], result_ref.shape[2])
        small = 16

        def finish(index, carry):
            at = pl.ds(pl.multiple_of(index * small, small), small)
            result = total_ref[at, :].astype(jnp.bfloat16)
            for part in range(parts):
                result_ref[part, at, :] = result[:, part * width : (part + 1) * width]
            resid = resid_ref[at, :]
            inverse = lax.rsqrt(jnp.mean(resid * resid, axis=1, keepdims=True) + EPS)
            normed = resid * inverse
            scaled = back_ref[at, :] * gain_ref[...]
            mean = jnp.mean(scaled * normed, axis=1, keepdims=True)
            dres = gout_ref[at, :].astype(jnp.float32) + inverse * (scaled - normed * mean)
            dres_ref[at, :] = dres.astype(jnp.bfloat16)
            return carry

        lax.fori_loop(0, tokens // small, finish, 0, unroll=4)


MLP_CHUNK = 768


def resident(shape):
    return pl.BlockSpec(shape, lambda s: (0,) * len(shape), pipeline_mode=pl.Buffered(1))


def mlp_specs(tokens, model):
    columns = pl.BlockSpec((model, MLP_CHUNK), lambda s: (0, s))
    down = pl.BlockSpec((MLP_CHUNK, model), lambda s: (s, 0))
    made = pl.BlockSpec((tokens, MLP_CHUNK), lambda s: (0, s))
    return ([columns, columns, down], [made] * 3)


def mlp_hidden(left, parts, normed, mlp_gate, mlp_up, mlp_down):
    tokens, model = normed.shape
    ffn = mlp_gate.shape[1]
    low = jnp.bfloat16
    weights, made = mlp_specs(tokens, model)
    tall = jax.ShapeDtypeStruct((tokens, ffn), low)
    return pl.pallas_call(
        hidden_kernel,
        name="mlp_hidden",
        grid=(ffn // MLP_CHUNK,),
        in_specs=[
            pl.BlockSpec(memory_space=pltpu.SMEM),
            resident(parts.shape),
            resident(normed.shape),
            *weights,
        ],
        out_specs=[resident((tokens, model)), *made],
        out_shape=[jax.ShapeDtypeStruct((tokens, model), low), tall, tall, tall],
        compiler_params=pltpu.CompilerParams(vmem_limit_bytes=VMEM_BYTES),
        cost_estimate=pl.CostEstimate(
            flops=6 * tokens * model * ffn,
            bytes_accessed=6 * (model + tokens) * ffn + 6 * tokens * model,
            transcendentals=0,
        ),
    )(left, parts, normed, mlp_gate, mlp_up, mlp_down)


def mlp_back(hidden, dgate, dup, gout, resid, gain, mlp_gate, mlp_up, mlp_down, parts_shape):
    tokens, model = resid.shape
    ffn = mlp_gate.shape[1]
    low, f32 = (jnp.bfloat16, jnp.float32)
    weights, made = mlp_specs(tokens, model)
    return pl.pallas_call(
        back_kernel,
        name="mlp_back",
        grid=(ffn // MLP_CHUNK,),
        in_specs=[
            *made,
            resident((tokens, model)),
            resident((tokens, model)),
            resident((1, model)),
            *weights,
        ],
        out_specs=[resident(parts_shape), resident((tokens, model))],
        out_shape=[
            jax.ShapeDtypeStruct(parts_shape, low),
            jax.ShapeDtypeStruct((tokens, model), low),
        ],
        scratch_shapes=[pltpu.VMEM((tokens, model), f32), pltpu.VMEM((tokens, model), f32)],
        compiler_params=pltpu.CompilerParams(vmem_limit_bytes=VMEM_BYTES),
        cost_estimate=pl.CostEstimate(
            flops=6 * tokens * model * ffn,
            bytes_accessed=6 * (model + tokens) * ffn + 10 * tokens * model,
            transcendentals=0,
        ),
    )(hidden, dgate, dup, gout, resid, gain[None], mlp_gate, mlp_up, mlp_down)


def outputs_kernel(
    device_ref,
    own_ref,
    gate_sum,
    in_sum,
    out_sum,
    small_ref,
    input_ref,
    gate_ref,
    mlp_gate_ref,
    mlp_up_ref,
    gain1_ref,
    gain2_ref,
    sum_gain1,
    sum_in,
    sum_gate,
    sum_taps,
    sum_bias,
    sum_lgates,
    sum_lbias,
    sum_decay,
    sum_out,
    sum_gain2,
    sum_mgate,
    sum_mup,
    sum_down,
):
    rows = sum_mgate.shape[0]
    model = own_ref.shape[1]
    parts = sum_mgate.shape[1] // model
    for part in range(parts):
        at = slice(part * model, (part + 1) * model)
        sum_mgate[:, at] = own_ref[part * rows : (part + 1) * rows, :].astype(jnp.float32)
        sum_mup[:, at] = own_ref[(parts + part) * rows : (parts + part + 1) * rows, :].astype(
            jnp.float32
        )
    sum_down[...] = own_ref[2 * parts * rows :, :].astype(jnp.float32)

    def weighed(*pairs):
        return sum(
            jnp.sum(weight[...].astype(jnp.float32) * gradient[...], axis=1, keepdims=True)
            for weight, gradient in pairs
        )

    sum_gain1[...] = weighed((input_ref, in_sum), (gate_ref, gate_sum)) / gain1_ref[...]
    sum_gain2[...] = weighed((mlp_gate_ref, sum_mgate), (mlp_up_ref, sum_mup)) / gain2_ref[...]
    sum_in[...] = in_sum[...]
    sum_gate[...] = gate_sum[...]
    sum_out[...] = out_sum[...]
    channels = small_ref.shape[0]
    size = sum_lgates.shape[1] // 2
    first, second = (small_ref[:, :LANES], small_ref[:, LANES:])
    lane = lax.broadcasted_iota(jnp.int32, (channels, LANES), 1)
    moved = pltpu.roll(second, size, 1)
    sum_lgates[:, :LANES] = jnp.where(lane < size, first, moved)
    sum_lgates[:, LANES:] = moved[:, : 2 * size - LANES]
    filled = jnp.concatenate([first, jnp.zeros((LANES - channels, LANES), jnp.float32)], axis=0)
    turned = filled.T
    sum_taps[...] = turned[size : size + 4, :channels]
    sum_bias[...] = turned[size + 4 : size + 5, :channels]
    sum_lbias[...] = turned[size + 5 : size + 7, :channels]
    sum_decay[...] = turned[size + 7 : size + 8, :channels]


def outputs(
    device, own, gate_sum, in_sum, out_sum, small, recur_input, recur_gate, mlp_gate, mlp_up, gain1, gain2, size
):
    rows, rec = in_sum.shape
    model, ffn = mlp_gate.shape
    channels = small.shape[0]
    f32 = jnp.float32

    def whole(shape):
        return pl.BlockSpec(shape, lambda s, device: (0,) * len(shape))

    def mine(shape):
        return pl.BlockSpec(shape, lambda s, device: (device[0], 0))

    given = (own, gate_sum, in_sum, out_sum, small)
    shapes = [(rows, 1), (rows, rec), (rows, rec), (4, channels), (1, channels)]
    shapes += [(channels, 2 * size), (2, channels), (1, channels), out_sum.shape, (rows, 1)]
    shapes += [(rows, ffn), (rows, ffn), (own.shape[0] - 2 * ffn // model * rows, model)]
    return pl.pallas_call(
        outputs_kernel,
        name="outputs",
        grid_spec=pltpu.PrefetchScalarGridSpec(
            num_scalar_prefetch=1,
            grid=(1,),
            in_specs=[whole(a.shape) for a in given]
            + [mine((rows, rec))] * 2
            + [mine((rows, ffn))] * 2
            + [mine((rows, 1))] * 2,
            out_specs=[whole(shape) for shape in shapes],
        ),
        out_shape=[jax.ShapeDtypeStruct(shape, f32) for shape in shapes],
        compiler_params=pltpu.CompilerParams(vmem_limit_bytes=VMEM_BYTES),
    )(
        device[None],
        *given,
        recur_input,
        recur_gate,
        mlp_gate,
        mlp_up,
        gain1[:, None],
        gain2[:, None],
    )


def spread_kernel(whole_ref, out_ref):
    out_ref[0] = whole_ref[...]


def spread(whole, count):
    tokens, width = (whole.shape[0], whole.shape[1] // count)
    return pl.pallas_call(
        spread_kernel,
        name="spread_features",
        grid=(count,),
        in_specs=[pl.BlockSpec((tokens, width), lambda j: (0, j))],
        out_specs=pl.BlockSpec((1, tokens, width), lambda j: (j, 0, 0)),
        out_shape=jax.ShapeDtypeStruct((count, tokens, width), whole.dtype),
        cost_estimate=pl.CostEstimate(
            flops=0, bytes_accessed=4 * tokens * whole.shape[1], transcendentals=0
        ),
    )(whole)


CHAN = ("zed", "core")


def features_in(local, pick=slice(None)):
    count = lax.axis_size(CHAN)
    rows, length, width = local.shape
    local = local.reshape(count, rows // count, length, width)[:, pick]
    if width % LANES == 0:
        return lax.all_to_all(local, CHAN, 0, 0, tiled=True).reshape(count, -1, width)
    moved = lax.all_to_all(
        local.reshape(-1, length, width), CHAN, split_axis=0, concat_axis=2, tiled=True
    )
    return moved.reshape(1, -1, count * width)


def features_apart(whole):
    count = lax.axis_size(CHAN)
    if (whole.shape[1] // count) % LANES == 0:
        return spread(whole, count)
    return whole[None]


def features_out(parts, rows):
    blocks, tokens, width = parts.shape
    parts = parts.reshape(blocks, rows, tokens // rows, width)
    if blocks > 1:
        moved = lax.all_to_all(parts, CHAN, 0, 0, tiled=True)
        return moved.reshape(-1, *parts.shape[2:])
    return lax.all_to_all(parts[0], CHAN, split_axis=2, concat_axis=0, tiled=True)


class Corners:
    def __init__(self, seq, zed):
        self.seq_bits, self.zed_bits = (seq.bit_length() - 1, zed.bit_length() - 1)
        self.count = self.seq_bits + self.zed_bits
        self.dims = (2,) * self.count
        self.low = tuple(range(self.seq_bits))[::-1] + tuple(range(self.seq_bits, self.count))[::-1]
        self.high = tuple(range(self.seq_bits)) + tuple(range(self.seq_bits, self.count))[::-1]

    def place(self, dim):
        if dim < self.seq_bits:
            return ("seq", 2 ** (self.seq_bits - 1 - dim))
        return ("zed", 2 ** (self.count - 1 - dim))

    def bit(self, dim):
        axis, weight = self.place(dim)
        return lax.rem(lax.div(lax.axis_index(axis), weight), 2)

    def partner(self, dim):
        axis, weight = self.place(dim)
        return {axis: lax.axis_index(axis) + weight * (1 - 2 * self.bit(dim))}


def tail_kernel(
    corners,
    orders,
    dgate_hbm,
    dbranch_hbm,
    ending_ref,
    leading_ref,
    mixed_hbm,
    dres_hbm,
    gain_ref,
    input_hbm,
    gate_hbm,
    small_hbm,
    *refs,
):
    rows = ending_ref.shape[0]
    normed_hbms, x_hbms, inverse_hbms = (refs[k * rows : (k + 1) * rows] for k in range(3))
    tokens_ref, sum_gate, sum_out, sum_in, sum_small = refs[3 * rows : 3 * rows + 5]
    refs = refs[3 * rows + 5 :]
    stages = corners.count + 1
    dgate, dbranch, mixed, dres, normed, x, inverse, weight_in, weight_gate = refs[:9]
    made_in, made_out, own_small, back, parts, rim = refs[9:15]
    slots_in, slots_out, slots_small = (
        refs[15 + k * stages : 15 + (k + 1) * stages] for k in range(3)
    )
    (
        send_sem,
        recv_sem,
        load_sem,
        move_send,
        move_recv,
        keep_sem,
        rim_send,
        rim_recv,
    ) = refs[15 + 3 * stages :]
    seq, zed, core = (lax.axis_index(axis) for axis in ("seq", "zed", "core"))
    seqs, group = (lax.axis_size("seq"), 2 * lax.axis_size("zed"))
    mine = zed * 2 + core
    length = tokens_ref.shape[1]
    model = x.shape[1]

    def member(index):
        return {"zed": lax.div(index, 2), "core": lax.rem(index, 2)}

    def by_row(sources, target):
        return [
            (source, target.at[pl.ds(row * length, length)]) for row, source in enumerate(sources)
        ]

    pairs = [
        (dbranch_hbm, dbranch),
        (input_hbm, weight_in),
        (dgate_hbm, dgate),
        (gate_hbm, weight_gate),
        *by_row(x_hbms, x),
        *by_row(inverse_hbms, inverse),
        (dres_hbm, dres),
        *by_row(normed_hbms, normed),
        (mixed_hbm, mixed),
        (small_hbm.at[(slice(None),) * corners.count + (core,)], own_small),
    ]
    kinds = []
    for name in ('dbranch', 'win', 'dgate', 'wgate', 'x', 'inverse', 'dres', 'normed', 'mixed', 'small'):
        kinds += [name] * (rows if name in ("normed", "x", "inverse") else 1)
    loads = [
        pltpu.make_async_copy(source, target, load_sem.at[place])
        for place, (source, target) in enumerate(pairs)
    ]
    for load in loads:
        load.start()

    barrier = pltpu.get_barrier_semaphore()
    for other in range(1, group):
        pl.semaphore_signal(
            barrier, inc=1, device_id=member(lax.rem(mine + other, group)), device_id_type=MESH
        )
    for other in range(1, seqs):
        pl.semaphore_signal(
            barrier, inc=1, device_id={"seq": lax.rem(seq + other, seqs)}, device_id_type=MESH
        )
    pl.semaphore_wait(barrier, group - 1 + seqs - 1)

    rim_copy = pltpu.make_async_remote_copy(
        src_ref=leading_ref,
        dst_ref=rim,
        send_sem=rim_send,
        recv_sem=rim_recv,
        device_id={"seq": lax.rem(seq + seqs - 1, seqs)},
        device_id_type=MESH,
    )
    rim_copy.start()

    def own(stream, index):
        if stream < 4:
            return made_in.at[(stream,) + index + (core,)]
        if stream < 6:
            return made_out.at[(stream - 4,) + index + (core,)]
        return own_small.at[index]

    def slot(stream, stage):
        if stream < 4:
            return slots_in[stage].at[stream]
        if stream < 6:
            return slots_out[stage].at[stream - 4]
        return slots_small[stage]

    def copy(stream, stage):
        order = orders[stream]
        every = (slice(None),) * corners.count
        if stage == 0:
            if stream < 4:
                source = made_in.at[(stream,) + every + (1 - core,)]
            elif stream < 6:
                source = made_out.at[(stream - 4,) + every + (1 - core,)]
            else:
                source = small_hbm.at[every + (1 - core,)]
            target = {"core": 1 - core}
        else:
            dim = order[stage - 1]
            fixed = {before: corners.bit(before) for before in order[: stage - 1]}
            fixed[dim] = 1 - corners.bit(dim)
            source = own(stream, tuple(fixed.get(d, slice(None)) for d in range(corners.count)))
            target = corners.partner(dim)
        return pltpu.make_async_remote_copy(
            src_ref=source,
            dst_ref=slot(stream, stage),
            send_sem=send_sem.at[stream, stage],
            recv_sem=recv_sem.at[stream, stage],
            device_id=target,
            device_id_type=MESH,
        )

    sums = [
        sum_gate.at[:, : sum_gate.shape[1] // 2],
        sum_gate.at[:, sum_gate.shape[1] // 2 :],
        sum_in.at[:, : sum_in.shape[1] // 2],
        sum_in.at[:, sum_in.shape[1] // 2 :],
        sum_out.at[:, : sum_out.shape[1] // 2],
        sum_out.at[:, sum_out.shape[1] // 2 :],
        sum_small,
    ]

    def advance(stream, stage):
        order = orders[stream]
        copy(stream, stage).wait_recv()
        left = [dim for dim in range(corners.count) if dim not in order[:stage]]
        fixed = {dim: corners.bit(dim) for dim in order[:stage]}
        arrived = slot(stream, stage)
        if not left:
            index = tuple(fixed[dim] for dim in range(corners.count))
            sums[stream][...] = own(stream, index)[...].astype(jnp.float32) + arrived[...].astype(
                jnp.float32
            )
            return

        def add(index, carry):
            part = {
                dim: lax.rem(lax.div(index, 2 ** (len(left) - 1 - place)), 2)
                for place, dim in enumerate(left)
            }
            kept = own(stream, tuple({**fixed, **part}[dim] for dim in range(corners.count)))
            total = kept[...].astype(jnp.float32) + arrived[
                tuple(part[dim] for dim in left)
            ].astype(jnp.float32)
            kept[...] = total.astype(jnp.bfloat16)
            return carry

        lax.fori_loop(0, 2 ** len(left), add, 0)
        copy(stream, stage + 1).start()

    def move(other, row):
        to = lax.rem(mine + other, group)
        return pltpu.make_async_remote_copy(
            src_ref=parts.at[to, pl.ds(row * length, length)],
            dst_ref=tokens_ref.at[mine * rows + row],
            send_sem=move_send.at[other - 1, row],
            recv_sem=move_recv.at[other - 1, row],
            device_id=member(to),
            device_id_type=MESH,
        )

    def keep(row):
        return pltpu.make_async_copy(
            parts.at[mine, pl.ds(row * length, length)],
            tokens_ref.at[mine * rows + row],
            keep_sem.at[row],
        )

    tile = 256
    width = parts.shape[2]

    def back_row(row):
        at_row = slice(row * length, (row + 1) * length)

        def product(index, carry):
            at = pl.ds(pl.multiple_of(index * tile, tile), tile)
            contract = (((1,), (1,)), ((), ()))
            back[:, at] = lax.dot_general(
                dbranch[at_row, :], weight_in[at, :], contract, preferred_element_type=jnp.float32
            ) + lax.dot_general(
                dgate[at_row, :], weight_gate[at, :], contract, preferred_element_type=jnp.float32
            )
            return carry

        lax.fori_loop(0, model // tile, product, 0)
        slab = 16

        def norm(index, carry):
            base = pl.multiple_of(index * slab, slab)
            at = pl.ds(row * length + base, slab)
            inv = inverse[at, :1]
            value = x[at, :].astype(jnp.float32) * inv
            scaled = back[pl.ds(base, slab), :] * gain_ref[...]
            mean = jnp.mean(scaled * value, axis=1, keepdims=True)
            grad = dres[at, :].astype(jnp.float32) + inv * (scaled - value * mean)
            grad = grad.astype(jnp.bfloat16)
            for part in range(parts.shape[0]):
                parts[part, at, :] = grad[:, part * width : (part + 1) * width]
            return carry

        lax.fori_loop(0, length // slab, norm, 0, unroll=4)
        for other in range(1, group):
            move(other, row).start()
        keep(row).start()

    def weight_product(left, right, made, stream, first):
        columns = made.shape[-1]
        shape = made.shape[1:-1]

        def product(index, carry):
            at = pl.ds(pl.multiple_of(index * tile, tile), tile)
            source = pl.ds(pl.multiple_of(first + index * tile, tile), tile)
            part = lax.dot_general(
                left[...],
                right[:, source],
                (((0,), (0,)), ((), ())),
                preferred_element_type=jnp.float32,
            )
            made[(stream,) + (slice(None),) * len(shape) + (at,)] = part.astype(
                jnp.bfloat16
            ).reshape(shape + (tile,))
            return carry

        lax.fori_loop(0, columns // tile, product, 0)

    half, half_out = (made_in.shape[-1], made_out.shape[-1])
    waited, reached = (set(), {})

    def need(*names):
        for place, name in enumerate(kinds):
            if name in names and place not in waited:
                waited.add(place)
                loads[place].wait()

    def fix_rim():
        need("dbranch")
        rim_copy.wait()
        live = jnp.where(seq < seqs - 1, 1.0, 0.0)
        for row in range(rows):
            at = slice((row + 1) * length - STEP, (row + 1) * length)
            inside = dbranch[at, :].astype(jnp.float32)
            last = ending_ref[row] + live * rim[row]
            dbranch[at, :] = jnp.concatenate([inside[: STEP - SUBLANES], last], axis=0).astype(
                jnp.bfloat16
            )

    def begin(stream):
        copy(stream, 0).start()
        reached[stream] = 0

    def progress(streams):
        for stream in streams:
            if stream in reached and reached[stream] < stages:
                if stream == 6:
                    need("small")
                advance(stream, reached[stream])
                reached[stream] += 1

    def compute(item):
        if item == "gate":
            need("normed", "dgate")
            for stream in (0, 1):
                weight_product(normed, dgate, made_in, stream, stream * half)
                begin(stream)
        elif item == "out":
            need("mixed", "dres")
            for stream in (4, 5):
                weight_product(mixed, dres, made_out, stream - 4, (stream - 4) * half_out)
                begin(stream)
        elif item == "in":
            need("normed", "dbranch")
            for stream in (2, 3):
                weight_product(normed, dbranch, made_in, stream, (stream - 2) * half)
                begin(stream)
        else:
            need("dbranch", "dgate", "win", "wgate", "x", "inverse", "dres")
            back_row(item)

    begin(6)
    fix_rim()
    compute(0)
    compute(1)
    compute('gate')
    progress((6,))
    compute('out')
    progress((0, 1))
    compute('in')
    progress((0, 1))
    progress((4, 5))
    progress((6,))
    while any(reached[stream] < stages for stream in range(7)):
        progress((0, 1, 4, 5, 2, 3, 6))
    for stage in range(stages):
        for stream in range(7):
            copy(stream, stage).wait_send()
    for row in range(rows):
        for other in range(1, group):
            move(other, row).wait()
        keep(row).wait()


def tail(dgate, dbranch, ending, leading, mixed, dres, gain, w_in, w_gate, small, normed, x, inverse):
    corners = Corners(lax.axis_size("seq"), lax.axis_size("zed"))
    group, devices = (lax.axis_size(CHAN), 2 ** (corners.count + 1))
    tokens, model = dres.shape
    rec = dgate.shape[1]
    rows = ending.shape[0]
    length, width = (tokens // rows, model // group)
    low, f32 = (jnp.bfloat16, jnp.float32)
    stages = corners.count + 1
    in_rows, out_rows = (model // devices, rec // devices)
    small = small.reshape(corners.dims + (2, out_rows, small.shape[1]))
    orders = [corners.low, corners.high] * 3 + [corners.low]

    def slots(lead, shape):
        return [pltpu.VMEM(lead + (2,) * (corners.count - k) + shape, low) for k in range(stages)]

    in_shape, out_shape = ((in_rows, rec // 2), (out_rows, model // 2))
    loaded = (dgate, dbranch, mixed, dres, dres, dres)
    loaded += (jax.ShapeDtypeStruct((tokens, LANES), f32), w_in, w_gate)
    anyplace = pl.BlockSpec(memory_space=pl.ANY)
    vmem = pl.BlockSpec(memory_space=pltpu.VMEM)
    dma = pltpu.SemaphoreType.DMA
    moved = sum(math.prod(a.shape) * a.dtype.itemsize for a in loaded)
    return pl.pallas_call(
        functools.partial(tail_kernel, corners, orders),
        name="tail",
        in_specs=[anyplace, anyplace, vmem, vmem, anyplace, anyplace, vmem]
        + [anyplace] * (3 + 3 * rows),
        out_specs=[anyplace] + [vmem] * 4,
        out_shape=[
            jax.ShapeDtypeStruct((group * rows, length, width), low),
            jax.ShapeDtypeStruct((in_rows, rec), f32),
            jax.ShapeDtypeStruct((out_rows, model), f32),
            jax.ShapeDtypeStruct((in_rows, rec), f32),
            jax.ShapeDtypeStruct(small.shape[-2:], f32),
        ],
        scratch_shapes=[pltpu.VMEM(a.shape, a.dtype) for a in loaded]
        + [
            pltpu.VMEM((4,) + corners.dims + (2,) + in_shape, low),
            pltpu.VMEM((2,) + corners.dims + (2,) + out_shape, low),
            pltpu.VMEM(corners.dims + small.shape[-2:], low),
            pltpu.VMEM((length, model), f32),
            pltpu.VMEM((group, tokens, width), low),
            pltpu.VMEM(leading.shape, leading.dtype),
        ]
        + slots((4,), in_shape)
        + slots((2,), out_shape)
        + slots((), small.shape[-2:])
        + [
            dma((7, stages)),
            dma((7, stages)),
            dma((7 + 3 * rows,)),
            dma((group - 1, rows)),
            dma((group - 1, rows)),
            dma((rows,)),
            dma,
            dma,
        ],
        compiler_params=pltpu.CompilerParams(
            collective_id=1, has_side_effects=True, vmem_limit_bytes=60 * 1024 * 1024
        ),
        cost_estimate=pl.CostEstimate(
            flops=10 * tokens * model * rec, bytes_accessed=2 * moved, transcendentals=0
        ),
    )(dgate, dbranch, ending, leading, mixed, dres, gain[None], w_in, w_gate, small, *normed, *x, *inverse)


def grads_kernel(
    normed_ref,
    dgate_ref,
    dup_ref,
    hidden_ref,
    gout_ref,
    out_ref,
    turned_ref,
    made_wide,
    made_down,
    come_wide,
    come_down,
    send_sem,
    recv_sem,
    store_sem,
):
    step = pl.program_id(0)
    core = lax.axis_index("core")
    other = {"core": 1 - core}
    wide_rows, down_rows = (made_wide.shape[3], made_down.shape[3])
    wides, downs = (come_wide.shape[0], come_down.shape[0])
    total = wides + downs
    down_at = wides * wide_rows

    def exchange(made, come, index, slot):
        return pltpu.make_async_remote_copy(
            src_ref=made.at[lax.rem(index, 2), 1 - core],
            dst_ref=come.at[index],
            send_sem=send_sem.at[slot],
            recv_sem=recv_sem.at[slot],
            device_id=other,
            device_id_type=MESH,
        )

    def store_wide(index):
        return pltpu.make_async_copy(
            come_wide.at[index],
            out_ref.at[:, pl.ds(pl.multiple_of(index * wide_rows, wide_rows), wide_rows)],
            store_sem.at[index],
        )

    def store_down(index):
        chips = come_down.shape[1]
        return pltpu.make_async_copy(
            come_down.at[index],
            out_ref.at[pl.ds(index * chips, chips), pl.ds(down_at, down_rows)],
            store_sem.at[index + wides],
        )

    @pl.when(step == 0)
    def _():
        barrier = pltpu.get_barrier_semaphore()
        pl.semaphore_signal(barrier, inc=1, device_id=other, device_id_type=MESH)
        pl.semaphore_wait(barrier, 1)
        turned_ref[...] = normed_ref[...].T

    def product_wide(source, index):
        made = made_wide.at[lax.rem(index, 2)]
        chips, rows = (made.shape[1], made.shape[2])
        tile = 512

        def column(place, carry):
            at = pl.ds(pl.multiple_of(place * tile, tile), tile)
            part = jnp.dot(turned_ref[...], source[:, at], preferred_element_type=jnp.float32)
            part = part.astype(jnp.bfloat16).reshape(chips, 2, rows, tile)
            made[0, :, :, at] = part[:, 0]
            made[1, :, :, at] = part[:, 1]
            return carry

        lax.fori_loop(0, source.shape[1] // tile, column, 0)

    def product_tall(left, right, made_all, index):
        made = made_all.at[lax.rem(index, 2)]
        chips, rows = (made.shape[1], made.shape[2])
        tile = 512

        def column(place, carry):
            at = pl.ds(pl.multiple_of(place * tile, tile), tile)
            part = lax.dot_general(
                left[...], right[:, at], (((0,), (0,)), ((), ())), preferred_element_type=jnp.float32
            )
            part = part.astype(jnp.bfloat16).reshape(chips, 2, rows, tile)
            made[0, :, :, at] = part[:, 0]
            made[1, :, :, at] = part[:, 1]
            return carry

        lax.fori_loop(0, right.shape[1] // tile, column, 0)

    half = wides // 2

    @pl.when(step < half)
    def _():
        product_wide(dgate_ref, step)

    @pl.when((step >= half) & (step < wides))
    def _():
        product_wide(dup_ref, step)

    @pl.when(step < wides)
    def _():
        exchange(made_wide, come_wide, step, step).start()

    @pl.when((step >= wides) & (step < total))
    def _():
        product_tall(hidden_ref, gout_ref, made_down, step - wides)
        exchange(made_down, come_down, step - wides, step).start()

    def finish(made, come, index, slot, store):
        exchange(made, come, index, slot).wait()
        mine = made.at[lax.rem(index, 2), core]
        arrived = come.at[index]

        def add(chip, carry):
            both = mine[chip].astype(jnp.float32) + arrived[chip].astype(jnp.float32)
            arrived[chip] = both.astype(jnp.bfloat16)
            return carry

        lax.fori_loop(0, come.shape[1], add, 0)
        store(index).start()

    before = step - 1

    @pl.when((before >= 0) & (before < wides))
    def _():
        finish(made_wide, come_wide, before, before, store_wide)

    @pl.when(before >= wides)
    def _():
        finish(made_down, come_down, before - wides, before, store_down)

    @pl.when(step == total)
    def _():
        for index in range(wides):
            store_wide(index).wait()
        for index in range(downs):
            store_down(index).wait()


def block_gradients(normed, dgate, dup, hidden, gout):
    tokens, model = normed.shape
    ffn = hidden.shape[1]
    chips = lax.axis_size("seq") * lax.axis_size("zed")
    devices = 2 * chips
    wide_rows, down_rows = (model // devices, ffn // devices)
    chunk = 768
    wides, downs = (2 * ffn // model, ffn // chunk)
    half = wides // 2
    down_chips = chunk // (2 * down_rows)
    rows = wides * wide_rows + down_rows
    low = jnp.bfloat16

    def whole(array):
        return pl.BlockSpec(array.shape, lambda s: (0, 0), pipeline_mode=pl.Buffered(1))

    def part(columns, first, count):
        return pl.BlockSpec((tokens, columns), lambda s: (0, jnp.clip(s - first, 0, count - 1)))

    total = wides + downs
    flops = 6 * tokens * model * ffn
    arrays = (normed, dgate, dup, hidden, gout)
    moved = sum(math.prod(a.shape) * 2 for a in arrays) + chips * rows * model * 2
    return pl.pallas_call(
        grads_kernel,
        name="block_gradients",
        grid=(total + 1,),
        in_specs=[
            whole(normed),
            part(model, 0, half),
            part(model, half, half),
            part(chunk, wides, downs),
            whole(gout),
        ],
        out_specs=pl.BlockSpec(memory_space=pl.ANY),
        out_shape=jax.ShapeDtypeStruct((chips, rows, model), low),
        scratch_shapes=[
            pltpu.VMEM((model, tokens), low),
            pltpu.VMEM((2, 2, chips, wide_rows, model), low),
            pltpu.VMEM((2, 2, down_chips, down_rows, model), low),
            pltpu.VMEM((wides, chips, wide_rows, model), low),
            pltpu.VMEM((downs, down_chips, down_rows, model), low),
            pltpu.SemaphoreType.DMA((total,)),
            pltpu.SemaphoreType.DMA((total,)),
            pltpu.SemaphoreType.DMA((total,)),
        ],
        compiler_params=pltpu.CompilerParams(
            collective_id=2, has_side_effects=True, vmem_limit_bytes=VMEM_BYTES
        ),
        cost_estimate=pl.CostEstimate(flops=flops, bytes_accessed=moved, transcendentals=0),
    )(*arrays)


def passed_along(value, axis, steps):
    count = lax.axis_size(axis)
    leading, last = (max(0, -steps), min(count, count - steps))
    return lax.ppermute(value, axis, [(source, source + steps) for source in range(leading, last)])


def weight_grad(left, right):
    return lax.dot_general(
        left, right, (((0,), (0,)), ((), ())), preferred_element_type=jnp.float32
    ).astype(jnp.bfloat16)


def back_dot(left, right):
    return lax.dot_general(
        left, right, (((1,), (1,)), ((), ())), preferred_element_type=jnp.float32
    )


def fwd_dot(left, right):
    return jnp.dot(left, right, preferred_element_type=jnp.float32)


def gelu_fn(value):
    return jax.nn.gelu(value, approximate=True)


def norm_back(grad_norm, normed, inverse, gain):
    scaled = grad_norm * gain
    mean_term = jnp.mean(scaled * normed, axis=1, keepdims=True)
    return inverse * (scaled - normed * mean_term)


def scattered(gradient):
    return lax.psum_scatter(
        gradient, ("seq", "zed", "core"), scatter_dimension=0, tiled=True
    ).astype(jnp.float32)


def body(
    tokens,
    cotangent,
    doc_starts,
    lengths,
    norm1_gain,
    recur_input,
    recur_gate,
    conv_kernel,
    conv_bias,
    lru_gates,
    lru_bias,
    lru_decay,
    recur_out,
    norm2_gain,
    mlp_gate,
    mlp_up,
    mlp_down,
):
    count = lax.axis_size(CHAN)
    row_count, block_len = (tokens.shape[0] // count, tokens.shape[1])
    model_dim = tokens.shape[2] * count
    tok_count = row_count * block_len
    rec_width = recur_input.shape[1]
    ffn_width = mlp_gate.shape[1]
    head_count = H
    head_size = rec_width // head_count
    tap_count = conv_kernel.shape[0]
    rim_size = tap_count - 1
    seq_index = lax.axis_index("seq")
    position = seq_index * block_len + jnp.arange(block_len, dtype=jnp.int32)
    bounds = jnp.concatenate([doc_starts, lengths[:, None]], axis=1)
    is_before = bounds[:, None, :] <= position[None, :, None]
    seg_start = jnp.max(jnp.where(is_before, bounds[:, None, :], 0), axis=2)
    dist = jnp.broadcast_to(
        (position[None, :] - seg_start)[:, :, None], (row_count, block_len, LANES)
    )
    soft_decay = jax.nn.softplus(-lru_decay)
    params = jnp.concatenate(
        [
            conv_kernel,
            conv_bias[None],
            lru_bias,
            (-8.0 * soft_decay)[None],
            (8.0 * jax.nn.sigmoid(-lru_decay))[None],
            jnp.zeros((SUBLANES - 1, rec_width), jnp.float32),
        ],
        axis=0,
    )
    core = Recurrence(row_count, block_len, rec_width, head_size)
    wide_gates = core.widen(lru_gates)
    if tokens.shape[2] % LANES == 0:
        blocks = [features_in(tokens, slice(row, row + 1)) for row in range(row_count)]
    else:
        side = features_in(tokens)
        blocks = [side[:, row * block_len : (row + 1) * block_len] for row in range(row_count)]
    single = Recurrence(1, block_len, rec_width, head_size)
    per_row = []
    for row in range(row_count):
        block = blocks[row]
        if row:
            block, _ = lax.optimization_barrier((block, per_row[-1][-1]))
        else:
            block, wide_gates, params, dist = lax.optimization_barrier(
                (block, wide_gates, params, dist)
            )
        low_x, inverse, normed, branch, pre, rim = front(block, norm1_gain, recur_input, recur_gate)
        branch, rim = (branch[None], rim[None])
        scanned = single.forward(branch, rim, dist[row : row + 1], params, wide_gates)
        per_row.append((low_x, inverse, normed, branch, pre[None], rim, *scanned))
    low_x, inverse, normed_low, branch, gate_pre, rim, lru_in, rate, igate, state, cum, last = zip(
        *per_row
    )
    entering, mixed_low, resid_one, normed_low2 = middle(
        last, state, cum, gate_pre, low_x, recur_out, norm2_gain
    )
    cotangent, _ = lax.optimization_barrier((cotangent, block))
    cotangent, resid_one = lax.optimization_barrier((features_in(cotangent), resid_one))
    grad_low, hidden_low, mgate_low, mup_low = mlp_hidden(
        lengths - seq_index * block_len, cotangent, normed_low2, mlp_gate, mlp_up, mlp_down
    )
    devices = lax.axis_size(("seq", "zed", "core"))
    own_rows = model_dim // devices
    tiled = own_rows % (2 * SUBLANES) == 0 and tokens.shape[2] % LANES == 0
    if tiled:
        merged = block_gradients(normed_low2, mgate_low, mup_low, hidden_low, grad_low)
        merged, hidden_low = lax.optimization_barrier((merged, hidden_low))
        merged = lax.psum_scatter(merged, "seq", scatter_dimension=0, tiled=True)
    result_parts, resid_low = mlp_back(
        hidden_low,
        mgate_low,
        mup_low,
        grad_low,
        resid_one,
        norm2_gain,
        mlp_gate,
        mlp_up,
        mlp_down,
        cotangent.shape,
    )
    output = features_out(result_parts, row_count)
    gate_low, back_local, back_cum, first_term = core.adjoint(
        resid_low,
        recur_out,
        gate_pre,
        state,
        cum,
        entering,
        rate,
        dist,
        params,
    )
    gate_low = gate_low.reshape(tok_count, rec_width)
    branch_local, ending, leading, small = core.backward(
        back_local,
        back_cum,
        first_term,
        last,
        state,
        cum,
        entering,
        rate,
        igate,
        lru_in,
        dist,
        branch,
        rim,
        params,
        wide_gates,
    )
    branch_low = branch_local.reshape(tok_count, rec_width)
    if tiled:
        output, merged, branch_low = lax.optimization_barrier((output, merged, branch_low))
        merged = lax.psum_scatter(merged, "zed", scatter_dimension=0, tiled=True)
        grad_tokens, sum_rgate, sum_rout, sum_rin, own_small = tail(
            gate_low,
            branch_low,
            ending,
            leading,
            mixed_low,
            resid_low,
            norm1_gain,
            recur_input,
            recur_gate,
            small,
            normed_low,
            low_x,
            inverse,
        )
        device = lax.axis_index(("seq", "zed", "core"))
        sums = outputs(
            device,
            merged[0],
            sum_rgate,
            sum_rin,
            sum_rout,
            own_small,
            recur_input,
            recur_gate,
            mlp_gate,
            mlp_up,
            norm1_gain,
            norm2_gain,
            head_size,
        )
        flat = (0, 4, 7, 9)
        sums = [part.reshape(-1) if place in flat else part for place, part in enumerate(sums)]
        return (output, grad_tokens, *sums)
    else:
        from_next = passed_along(
            leading[:, SUBLANES - rim_size :, :].astype(jnp.bfloat16), "seq", -1
        )
        ending = ending + jnp.pad(
            from_next.astype(jnp.float32), ((0, 0), (SUBLANES - rim_size, 0), (0, 0))
        )
        branch_low = lax.dynamic_update_slice(
            branch_local, ending.astype(jnp.bfloat16), (0, block_len - SUBLANES, 0)
        ).reshape(tok_count, rec_width)
        grad_norm1 = back_dot(branch_low, recur_input) + back_dot(gate_low, recur_gate)
        inv_one = jnp.concatenate(inverse)[:, :1]
        normed_one = jnp.concatenate(low_x).astype(jnp.float32) * inv_one
        normed_low = jnp.concatenate(normed_low)
        input_part = norm_back(grad_norm1, normed_one, inv_one, norm1_gain)
        grad_x = (resid_low.astype(jnp.float32) + input_part).astype(jnp.bfloat16)
        grad_tokens = features_out(features_apart(grad_x), row_count)
        sum_mgate, sum_mup, sum_down, sum_rout, sum_rgate, sum_rin = (
            scattered(weight_grad(left, right))
            for left, right in (
                (normed_low2, mgate_low),
                (normed_low2, mup_low),
                (hidden_low, grad_low),
                (mixed_low, resid_low),
                (normed_low, gate_low),
                (normed_low, branch_low),
            )
        )
        own_small = scattered(small)
    sum_lgates = jnp.concatenate(
        [own_small[:, :head_size], own_small[:, LANES : LANES + head_size]], axis=1
    )
    own_sums = jnp.swapaxes(own_small[:, head_size : head_size + SUBLANES], 0, 1)
    device = lax.axis_index(("seq", "zed", "core"))

    def mine(array, size, axis=0):
        return lax.dynamic_slice_in_dim(array, device * size, size, axis)

    def weighed(weight, gradient):
        return jnp.sum(mine(weight, own_rows).astype(jnp.float32) * gradient, axis=1)

    sum_gain1 = (weighed(recur_input, sum_rin) + weighed(recur_gate, sum_rgate)) / mine(
        norm1_gain, own_rows
    )
    sum_gain2 = (weighed(mlp_gate, sum_mgate) + weighed(mlp_up, sum_mup)) / mine(
        norm2_gain, own_rows
    )
    sum_decay = own_sums[7]
    return (
        output,
        grad_tokens,
        sum_gain1,
        sum_rin,
        sum_rgate,
        own_sums[:4],
        own_sums[4],
        sum_lgates,
        own_sums[5:7],
        sum_decay,
        sum_rout,
        sum_gain2,
        sum_mgate,
        sum_mup,
        sum_down,
    )


def solution(mesh):
    seq, chan = (mesh.shape["seq"], mesh.shape["chan"])
    chips = jax.sharding.Mesh(mesh.devices.reshape(seq, chan // 2, 2), ("seq", "zed", "core"))
    chan = ("zed", "core")
    every = ("seq", "zed", "core")
    activations = P(None, "seq", chan)
    rows, columns, vector = (P(every, None), P(None, every), P(every))
    return jax.shard_map(
        body,
        mesh=chips,
        in_specs=(activations, activations, P(chan, None), P(chan)) + (P(),) * 13,
        out_specs=(
            activations,
            activations,
            vector,
            rows,
            rows,
            columns,
            vector,
            rows,
            columns,
            vector,
            rows,
            vector,
            rows,
            rows,
            rows,
        ),
        check_vma=False,
    )
```

```python
import functools
import math

import jax
import jax.numpy as jnp
from jax import lax
from jax.experimental import pallas as pl
from jax.experimental.pallas import tpu as pltpu
from jax.sharding import PartitionSpec as P

H = 16


EPS = 1e-06
ROOT_FLOOR = 1e-06
LANES = 128
SUBLANES = 8
STEP = 16
VMEM_BYTES = 56 * 1024 * 1024
MESH = pl.DeviceIdType.MESH


def sigmoid(value):
    return 0.5 * jnp.tanh(0.5 * value) + 0.5


GELU_C = 0.7978845608
GELU_A = 0.044715


def gelu_pair(value):
    square = value * value
    inner = jnp.tanh(value * (GELU_C + (GELU_C * GELU_A) * square))
    half = 0.5 + 0.5 * inner
    slope = GELU_C + (3.0 * GELU_C * GELU_A) * square
    return (value * half, half + 0.5 * value * (1.0 - inner * inner) * slope)


def root_argument(log_decay, decay):
    y = 2.0 * log_decay
    series = 1.0 + y * (0.5 + y * (1.0 / 6.0 + y * (1.0 / 24.0)))
    return jnp.where(y > -0.05, -y * series, 1.0 - decay * decay)


def across(column, width):
    return jnp.concatenate([column] * (width // LANES), axis=1)


class Rows:
    def __init__(self, refs):
        self.refs = refs

    def __getitem__(self, index):
        if not isinstance(index, tuple):
            return self.refs[index][0]
        return self.refs[index[0]][(0,) + index[1:]]


def by_rows(refs, rows, apart):
    found = []
    for split in apart:
        count = rows if split else 1
        found.append(Rows(refs[:count]) if split else refs[0])
        refs = refs[count:]
    return found, refs


def forward_kernel(
    branch_ref,
    rim_ref,
    dist_ref,
    par_ref,
    gates_ref,
    lru_ref,
    rate_ref,
    igate_ref,
    state_ref,
    cum_ref,
    last_ref,
    both_ref,
):
    rows, length, width = branch_ref.shape
    span = 2 * STEP if rows == 1 else STEP
    taps = [par_ref[k : k + 1, :] for k in range(4)]
    conv_bias, rate_bias, input_bias, soft = (par_ref[k : k + 1, :] for k in range(4, 8))
    place = lax.broadcasted_iota(jnp.int32, (SUBLANES, width), 0)

    for row in range(rows):

        def conv_step(index, before, row=row):
            base = pl.multiple_of(index * STEP, STEP)
            pieces = []
            for half in range(STEP // SUBLANES):
                at = pl.ds(base + half * SUBLANES, SUBLANES)
                here = branch_ref[row, at, :]
                dist = across(dist_ref[row, at, :], width)
                total = conv_bias + taps[0] * here
                for k in range(1, 4):
                    shifted = pltpu.roll(jnp.where(place < SUBLANES - k, here, before), k, 0)
                    total = total + taps[k] * jnp.where(dist >= k, shifted, 0.0)
                pieces.append(total)
                before = here
            lru_ref[row, pl.ds(base, STEP), :] = jnp.concatenate(pieces, axis=0).astype(jnp.bfloat16)
            return before

        lax.fori_loop(0, length // STEP, conv_step, rim_ref[row])

        piece = min(length, 256)

        def dot_step(index, carry, row=row):
            at = pl.ds(pl.multiple_of(index * piece, piece), piece)
            both_ref[row, at, :] = jnp.dot(
                lru_ref[row, at, :], gates_ref[...], preferred_element_type=jnp.float32
            )
            return carry

        lax.fori_loop(0, length // piece, dot_step, 0)

    def scan_step(index, carry):
        base = pl.multiple_of(index * span, span)
        later = []
        for row in range(rows):
            run_cum, run_state = carry[row]
            lru_both = lru_ref[row, pl.ds(base, span), :].astype(jnp.float32)
            for half in range(span // SUBLANES):
                at = pl.ds(base + half * SUBLANES, SUBLANES)
                lru = lru_both[half * SUBLANES : (half + 1) * SUBLANES]
                start = across(dist_ref[row, at, :], width) == 0
                rate = sigmoid(both_ref[row, at, :width] + rate_bias)
                igate = sigmoid(both_ref[row, at, width:] + input_bias)
                log_decay = rate * soft
                decay = jnp.exp(log_decay)
                arg = jnp.maximum(root_argument(log_decay, decay), ROOT_FLOOR)
                root = arg * lax.rsqrt(arg)
                cum = jnp.where(start, 0.0, decay)
                value = jnp.where(start, 1.0, root) * igate * lru
                rate_ref[row, at, :] = rate
                igate_ref[row, at, :] = igate
                for shift in (1, 2, 4):
                    live = place >= shift
                    value = value + cum * jnp.where(live, pltpu.roll(value, shift, 0), 0.0)
                    cum = cum * jnp.where(live, pltpu.roll(cum, shift, 0), 1.0)
                value = value + cum * run_state
                cum = cum * run_cum
                state_ref[row, at, :] = value
                cum_ref[row, at, :] = cum
                run_state = value[SUBLANES - 1 :, :]
                run_cum = cum[SUBLANES - 1 :, :]
            later.append((run_cum, run_state))
        return tuple(later)

    one, zero = (jnp.ones((1, width), jnp.float32), jnp.zeros((1, width), jnp.float32))
    done = lax.fori_loop(0, length // span, scan_step, tuple((one, zero) for _ in range(rows)))
    for row in range(rows):
        for place in range(2):
            last_ref[row, place : place + 1, :] = done[row][place]


def carried(sent_ref, got_ref, out_ref, send_sem, recv_sem, backward):
    seq, count = (lax.axis_index("seq"), lax.axis_size("seq"))

    def other(step):
        return {"seq": lax.rem(seq + step, count)}

    barrier = pltpu.get_barrier_semaphore()
    for step in range(1, count):
        pl.semaphore_signal(barrier, inc=1, device_id=other(step), device_id_type=MESH)
    pl.semaphore_wait(barrier, count - 1)
    copies = [
        pltpu.make_async_remote_copy(
            src_ref=sent_ref,
            dst_ref=got_ref.at[seq],
            send_sem=send_sem.at[step - 1],
            recv_sem=recv_sem.at[step - 1],
            device_id=other(step),
            device_id_type=MESH,
        )
        for step in range(1, count)
    ]
    for copy in copies:
        copy.start()
    got_ref[seq] = sent_ref[...]
    for copy in copies:
        copy.wait()
    for row in range(sent_ref.shape[0]):
        total = jnp.zeros(out_ref.shape[1:], jnp.float32)
        for place in range(count - 1, 0, -1) if backward else range(count - 1):
            longer = got_ref[place, row, 0:1, :] * total + got_ref[place, row, 1:2, :]
            total = jnp.where(place > seq if backward else place < seq, longer, total)
        out_ref[row] = total


def adjoint_kernel(rows, *refs):
    (
        dres_ref,
        weight_ref,
        pre_ref,
        state_ref,
        cum_ref,
        carry_ref,
        rate_ref,
        dist_ref,
        par_ref,
    ), outs = by_rows(refs, rows, (False, False, True, True, True, False, True, False, False))
    dgate_ref, local_ref, back_ref, first_ref, dmix_ref = outs
    _, length, width = dmix_ref.shape
    for row in range(rows):
        dmix_ref[row] = lax.dot_general(
            dres_ref[row * length : (row + 1) * length, :],
            weight_ref[...],
            (((1,), (1,)), ((), ())),
            preferred_element_type=jnp.float32,
        )
    soft = par_ref[7:8, :]
    place = lax.broadcasted_iota(jnp.int32, (SUBLANES, width), 0)
    last = length // STEP - 1

    def step(index, carry):
        base = pl.multiple_of((last - index) * STEP, STEP)
        later = []
        for row in range(rows):
            run_cum, run_back = carry[row]
            entering = carry_ref[row]
            pieces = []
            for half in reversed(range(STEP // SUBLANES)):
                at = pl.ds(base + half * SUBLANES, SUBLANES)
                start = across(dist_ref[row, at, :], width) == 0
                state = state_ref[row, at, :] + cum_ref[row, at, :] * entering
                act, slope = gelu_pair(pre_ref[row, at, :])
                dmix = dmix_ref[row, at, :]
                pieces.append(dmix * state * slope)
                dstate = dmix * act
                coef = jnp.where(start, 0.0, jnp.exp(rate_ref[row, at, :] * soft))
                value = coef * dstate
                for shift in (1, 2, 4):
                    live = place < SUBLANES - shift
                    turn = SUBLANES - shift
                    value = value + coef * jnp.where(live, pltpu.roll(value, turn, 0), 0.0)
                    coef = coef * jnp.where(live, pltpu.roll(coef, turn, 0), 1.0)
                value = value + coef * run_back
                coef = coef * run_cum
                inside = place < SUBLANES - 1
                local_ref[row, at, :] = dstate + jnp.where(
                    inside, pltpu.roll(value, SUBLANES - 1, 0), run_back
                )
                back_ref[row, at, :] = jnp.where(inside, pltpu.roll(coef, SUBLANES - 1, 0), run_cum)
                run_back = value[:1, :]
                run_cum = coef[:1, :]
            dgate_ref[row, pl.ds(base, STEP), :] = jnp.concatenate(pieces[::-1], axis=0).astype(
                jnp.bfloat16
            )
            later.append((run_cum, run_back))
        return tuple(later)

    one, zero = (jnp.ones((1, width), jnp.float32), jnp.zeros((1, width), jnp.float32))
    done = lax.fori_loop(0, last + 1, step, tuple((one, zero) for _ in range(rows)))
    for row in range(rows):
        first_ref[row] = done[row][1]


def backward_kernel(head_size, rows, *refs):
    first_at = 2
    sent_ref, got_ref, send_sem, recv_sem = refs[-4:]
    leaving_ref = refs[-8]
    lasts = Rows(refs[first_at + 1 : first_at + 1 + rows])

    @pl.when(pl.program_id(0) == 0)
    def _():
        for row in range(rows):
            sent_ref[row, 0:1, :] = lasts[row, 0:1, :]
            sent_ref[row, 1:2, :] = refs[first_at][row]
        carried(sent_ref, got_ref, leaving_ref, send_sem, recv_sem, True)

    block_backward(head_size, rows, 0, leaving_ref, *refs[:-8], *refs[-7:-4])


def later_backward_kernel(head_size, rows, first, *refs):
    held = 4
    block_backward(head_size, rows, first, refs[0], *refs[1 + held :])


def block_backward(head_size, rows, first_block, leaving_ref, *refs):
    (
        local_ref,
        back_ref,
        first_ref,
        last_ref,
        state_ref,
        cum_ref,
        in_ref,
        rate_ref,
        igate_ref,
        lru_ref,
        dist_ref,
        branch_ref,
        rim_ref,
        par_ref,
        gates_ref,
    ), others = by_rows(
        refs, rows, (False,) * 3 + (True,) * 3 + (False,) + (True,) * 3 + (False,) + (True,) * 2 + (False,) * 2
    )
    dbranch_ref, tail_ref, head_ref, dgates_ref = others[:4]
    both_ref, dconv_ref, sums_ref = others[-3:]
    _, length, width = local_ref.shape
    here = pl.program_id(0) + first_block
    block = pl.ds(pl.multiple_of(here * width, width), width)
    taps = [par_ref[k : k + 1, :] for k in range(4)]
    soft = par_ref[7:8, :]
    place = lax.broadcasted_iota(jnp.int32, (SUBLANES, width), 0)
    zeros = jnp.zeros((SUBLANES, width), jnp.float32)

    def gate_step(index, carry):
        sums, earlier = carry
        decay_sum, rate_sum, input_sum = sums
        base = pl.multiple_of(index * STEP, STEP)
        later = []
        for row in range(rows):
            before = earlier[row]
            entering = in_ref[row]
            leaving = leaving_ref[row, :, block]
            lru_both = lru_ref[row, pl.ds(base, STEP), :].astype(jnp.float32)
            drates, dinputs = ([], [])
            for half in range(STEP // SUBLANES):
                at = pl.ds(base + half * SUBLANES, SUBLANES)
                lru = lru_both[half * SUBLANES : (half + 1) * SUBLANES]
                start = across(dist_ref[row, at, :], width) == 0
                adjoint = local_ref[row, at, :] + back_ref[row, at, :] * leaving
                state = state_ref[row, at, :] + cum_ref[row, at, :] * entering
                previous = jnp.where(place < 1, before, pltpu.roll(state, 1, 0))
                before = state[SUBLANES - 1 :, :]
                rate = rate_ref[row, at, :]
                igate = igate_ref[row, at, :]
                log_decay = rate * soft
                decay = jnp.exp(log_decay)
                arg = root_argument(log_decay, decay)
                above = arg > ROOT_FLOOR
                arg = jnp.maximum(arg, ROOT_FLOOR)
                inverse = lax.rsqrt(arg)
                scale = jnp.where(start, 1.0, arg * inverse)
                gated = adjoint * igate
                dscale = gated * lru
                pull = jnp.where(above, dscale * decay * decay * inverse, 0.0)
                dlog = jnp.where(start, 0.0, adjoint * previous * decay - pull)
                dig = adjoint * scale * lru
                weighted = dlog * rate
                decay_sum = decay_sum + weighted
                drates.append(weighted * soft * (1.0 - rate))
                dinputs.append(dig * igate * (1.0 - igate))
                dconv_ref[row, at, :] = gated * scale
            drate = jnp.concatenate(drates, axis=0).astype(jnp.bfloat16)
            dinput = jnp.concatenate(dinputs, axis=0).astype(jnp.bfloat16)
            both_ref[row, pl.ds(base, STEP), :width] = drate
            both_ref[row, pl.ds(base, STEP), width:] = dinput
            drate = drate.astype(jnp.float32)
            dinput = dinput.astype(jnp.float32)
            rate_sum = rate_sum + (drate[:SUBLANES] + drate[SUBLANES:])
            input_sum = input_sum + (dinput[:SUBLANES] + dinput[SUBLANES:])
            later.append(before)
        return ((decay_sum, rate_sum, input_sum), tuple(later))

    sums, _ = lax.fori_loop(
        0,
        length // STEP,
        gate_step,
        ((zeros, zeros, zeros), tuple(in_ref[row] for row in range(rows))),
    )
    for slot, total in zip((5, 6, 7), (sums[1], sums[2], sums[0] * par_ref[8:9, :])):
        sums_ref[slot : slot + 1, :] = jnp.sum(total, axis=0, keepdims=True)

    piece = min(length, 256)
    wide = None
    for row in range(rows):

        def dot_step(index, carry, row=row):
            at = pl.ds(pl.multiple_of(index * piece, piece), piece)
            dconv_ref[row, at, :] += lax.dot_general(
                both_ref[row, at, :],
                gates_ref[...],
                (((1,), (1,)), ((), ())),
                preferred_element_type=jnp.float32,
            )
            return carry

        lax.fori_loop(0, length // piece, dot_step, 0)
        part = lax.dot_general(
            lru_ref[row], both_ref[row], (((0,), (0,)), ((), ())), preferred_element_type=jnp.float32
        )
        wide = part if wide is None else wide + part
    row_head = lax.broadcasted_iota(jnp.int32, (width, width), 0) // head_size
    col_head = lax.broadcasted_iota(jnp.int32, (width, width), 1) // head_size
    own = row_head == col_head
    folds = []
    for part in range(2):
        kept = jnp.where(own, wide[:, part * width : (part + 1) * width], 0.0)
        folded = kept
        for other in range(1, width // head_size):
            folded = folded + pltpu.roll(kept, width - other * head_size, 1)
        folds.append(folded[:, :LANES])

    def conv_step(index, carry):
        sums, following = carry
        sums = list(sums)
        base = pl.multiple_of((length // STEP - 1 - index) * STEP, STEP)
        later = []
        for row in range(rows):
            after = following[row]
            pieces = []
            for half in reversed(range(STEP // SUBLANES)):
                at = pl.ds(base + half * SUBLANES, SUBLANES)
                dist = across(dist_ref[row, at, :], width)
                branch = branch_ref[row, at, :]
                here = dconv_ref[row, at, :]
                total = taps[0] * here
                sums[0] = sums[0] + here * branch
                sums[4] = sums[4] + here
                masked = tuple(jnp.where(dist >= k, here, 0.0) for k in range(1, 4))
                for k in range(1, 4):
                    moved = pltpu.roll(
                        jnp.where(place >= k, masked[k - 1], after[k - 1]), SUBLANES - k, 0
                    )
                    total = total + taps[k] * moved
                    sums[k] = sums[k] + branch * moved
                after = masked
                pieces.append(total)
            whole = jnp.concatenate(pieces[::-1], axis=0)
            dbranch_ref[row, pl.ds(base, STEP), :] = whole.astype(jnp.bfloat16)
            later.append(after)

            @pl.when(index == 0)
            def _(row=row, whole=whole):
                tail_ref[row] = whole[STEP - SUBLANES :]

        return (tuple(sums), tuple(later))

    sums, firsts = lax.fori_loop(
        0,
        length // STEP,
        conv_step,
        ((zeros,) * 5, tuple((zeros,) * 3 for _ in range(rows))),
    )
    sums = list(sums)
    for row in range(rows):
        total = zeros
        rim = rim_ref[row]
        for k in range(1, 4):
            moved = pltpu.roll(jnp.where(place >= k, 0.0, firsts[row][k - 1]), SUBLANES - k, 0)
            total = total + taps[k] * moved
            sums[k] = sums[k] + rim * moved
        head_ref[row] = total
    for slot in range(5):
        sums_ref[slot : slot + 1, :] = jnp.sum(sums[slot], axis=0, keepdims=True)
    above = jnp.zeros((head_size, width), jnp.float32)
    below = jnp.zeros((LANES - head_size - SUBLANES, width), jnp.float32)
    turned = jnp.concatenate([above, sums_ref[...], below], axis=0).T
    lane = lax.broadcasted_iota(jnp.int32, (width, LANES), 1)
    dgates_ref[:, :LANES] = jnp.where(lane < head_size, folds[0], turned).astype(dgates_ref.dtype)
    dgates_ref[:, LANES:] = folds[1].astype(dgates_ref.dtype)


def channel_call(
    kernel, name, arrays, specs, outs, out_specs, scratch, blocks, flops, params=()
):
    moved = sum(math.prod(a.shape) * a.dtype.itemsize for a in (*arrays, *outs))
    return pl.pallas_call(
        kernel,
        name=name,
        grid=(blocks,),
        in_specs=specs,
        out_specs=out_specs,
        out_shape=outs,
        scratch_shapes=scratch,
        compiler_params=pltpu.CompilerParams(vmem_limit_bytes=VMEM_BYTES, **dict(params)),
        cost_estimate=pl.CostEstimate(flops=flops, bytes_accessed=moved, transcendentals=0),
    )(*arrays)


class Recurrence:
    def __init__(self, rows, length, channels, head_size):
        self.rows, self.length, self.channels = (rows, length, channels)
        self.head_size = head_size
        self.width = head_size * LANES // math.gcd(head_size, LANES)
        self.blocks = channels // self.width
        self.flops = 2 * rows * length * channels * 2 * self.width

    def tall(self):
        return pl.BlockSpec((self.rows, self.length, self.width), lambda j: (0, 0, j))

    def short(self, size):
        return pl.BlockSpec((self.rows, size, self.width), lambda j: (0, 0, j))

    def apart(self, size):
        return [pl.BlockSpec((1, size, self.width), lambda j: (0, 0, j))] * self.rows

    def whole(self, rows, size):
        return pl.BlockSpec((rows, size, self.channels), lambda j: (0, 0, 0))

    def flat(self, size):
        return pl.BlockSpec((size, self.width), lambda j: (0, j))

    def dist(self):
        return pl.BlockSpec((self.rows, self.length, LANES), lambda j: (0, 0, 0))

    def gates(self, columns):
        return pl.BlockSpec((self.width, columns), lambda j: (j, 0))

    def shape(self, size, dtype):
        return jax.ShapeDtypeStruct((self.rows, size, self.channels), dtype)

    def widen(self, lru_gates):
        size, width = (self.head_size, self.width)
        heads = width // size
        column = jnp.arange(2 * width)
        source = (column // width) * size + column % size
        spread = (jnp.arange(2 * size)[:, None] == source[None, :]).astype(jnp.bfloat16)
        owner = (column % width) // size
        mine = (jnp.arange(self.channels) // size) % heads
        wide = jnp.dot(lru_gates, spread, preferred_element_type=jnp.float32)
        return jnp.where(mine[:, None] == owner[None, :], wide, 0.0).astype(jnp.bfloat16)

    def forward(self, branch, rim, dist, params, gates):
        f32 = jnp.float32
        outs = [self.shape(self.length, d) for d in (jnp.bfloat16, f32, f32, f32, f32)]
        return channel_call(
            forward_kernel,
            "recurrence_forward",
            (branch, rim, dist, params, gates),
            [self.tall(), self.short(SUBLANES), self.dist(), self.flat(16), self.gates(2 * self.width)],
            outs + [self.shape(2, f32)],
            [self.tall()] * 5 + [self.short(2)],
            [pltpu.VMEM((self.rows, self.length, 2 * self.width), f32)],
            self.blocks,
            self.flops,
        )

    def adjoint(self, dres, weight, pre, state, cum, entering, rate, dist, params):
        f32 = jnp.float32
        outs = [self.shape(self.length, d) for d in (jnp.bfloat16, f32, f32)] + [self.shape(1, f32)]
        tall, apart = (self.tall(), self.apart(self.length))
        return channel_call(
            functools.partial(adjoint_kernel, self.rows),
            "recurrence_adjoint",
            (dres, weight, *pre, *state, *cum, entering, *rate, dist, params),
            [
                pl.BlockSpec(dres.shape, lambda j: (0, 0)),
                self.gates(weight.shape[1]),
                *apart * 3,
                self.short(1),
                *apart,
                self.dist(),
                self.flat(16),
            ],
            outs,
            [tall, tall, tall, self.short(1)],
            [pltpu.VMEM((self.rows, self.length, self.width), f32)],
            self.blocks,
            2 * self.rows * self.length * weight.size,
        )

    def backward(
        self, local, back, first, last, state, cum, entering, rate, igate, lru, dist, branch, rim, params, gates, between_calls
    ):
        f32 = jnp.float32
        outs = [
            self.shape(self.length, jnp.bfloat16),
            self.shape(SUBLANES, f32),
            self.shape(SUBLANES, f32),
            jax.ShapeDtypeStruct((self.channels, 2 * LANES), jnp.bfloat16),
        ]
        seqs = lax.axis_size("seq")
        summary = (self.rows, 2, self.channels)
        arrays = (local, back, first, *last, *state, *cum, entering, *rate, *igate, *lru, dist, *branch, *rim)
        arrays += (params, gates)
        early = self.blocks - 1
        scratch = [
            pltpu.VMEM((self.rows, self.length, 2 * self.width), jnp.bfloat16),
            pltpu.VMEM((self.rows, self.length, self.width), f32),
            pltpu.VMEM((SUBLANES, self.width), f32),
        ]

        def specs(offset):
            rows, width = (self.rows, self.width)

            def wide(rows, size):
                return pl.BlockSpec((rows, size, width), lambda j: (0, 0, j + offset))

            def flat(size):
                return pl.BlockSpec((size, width), lambda j: (0, j + offset))

            def tall(columns):
                return pl.BlockSpec((width, columns), lambda j: (j + offset, 0))

            whole, apart = (wide(rows, self.length), [wide(1, self.length)] * rows)
            given = [whole, whole, self.whole(rows, 1), *[self.whole(1, 2)] * rows, *apart * 2]
            given += [wide(rows, 1), *apart * 3, self.dist(), *apart, *[wide(1, SUBLANES)] * rows]
            given += [flat(16), tall(2 * width)]
            made = [whole, wide(rows, SUBLANES), wide(rows, SUBLANES), tall(2 * LANES)]
            return (given, made)

        given, made = specs(0)
        *found, leaving = channel_call(
            functools.partial(backward_kernel, self.head_size, self.rows),
            "recurrence_backward",
            arrays,
            given,
            outs + [self.shape(1, f32)],
            made + [self.whole(self.rows, 1)],
            scratch
            + [
                pltpu.VMEM(summary, f32),
                pltpu.VMEM((seqs,) + summary, f32),
                pltpu.SemaphoreType.DMA((seqs - 1,)),
                pltpu.SemaphoreType.DMA((seqs - 1,)),
            ],
            early,
            2 * self.flops,
            {"collective_id": 5, "has_side_effects": True},
        )
        between, leaving = between_calls(leaving)
        given, made = specs(early)
        done = pl.pallas_call(
            functools.partial(later_backward_kernel, self.head_size, self.rows, early),
            name="recurrence_backward_end",
            grid=(self.blocks - early,),
            in_specs=[self.whole(self.rows, 1)] + [pl.BlockSpec(memory_space=pl.ANY)] * 4 + given,
            out_specs=made,
            out_shape=outs,
            scratch_shapes=scratch,
            input_output_aliases={1 + k: k for k in range(4)},
            compiler_params=pltpu.CompilerParams(vmem_limit_bytes=VMEM_BYTES),
            cost_estimate=pl.CostEstimate(
                flops=self.flops // 2, bytes_accessed=16 * self.flops // self.width, transcendentals=0
            ),
        )(leaving, *found, *arrays)
        return (*done, between)


def gathered(parts_ref, at):
    return jnp.concatenate([parts_ref[k, at, :] for k in range(parts_ref.shape[0])], axis=1)


def front_kernel(
    parts_ref,
    gain_ref,
    input_ref,
    gate_ref,
    x_ref,
    inverse_ref,
    normed_ref,
    branch_ref,
    pre_ref,
    rim_ref,
    edge_ref,
    landed_ref,
    send_sem,
    recv_sem,
):
    tokens = x_ref.shape[0]
    piece, tall = (64, min(tokens, 512))
    step, steps = (pl.program_id(0), edge_ref.shape[0])
    seq, seqs = (lax.axis_index("seq"), lax.axis_size("seq"))
    barrier = pltpu.get_barrier_semaphore()

    @pl.when(step == 0)
    def _():
        before = {"seq": lax.rem(seq + seqs - 1, seqs)}
        pl.semaphore_signal(barrier, inc=1, device_id=before, device_id_type=MESH)

        def norm(index, carry):
            at = pl.ds(pl.multiple_of(index * piece, piece), piece)
            low = gathered(parts_ref, at)
            x_ref[at, :] = low
            value = low.astype(jnp.float32)
            inverse = lax.rsqrt(jnp.mean(value * value, axis=1, keepdims=True) + EPS)
            inverse_ref[at, :] = jnp.broadcast_to(inverse, (piece, LANES))
            normed_ref[at, :] = (value * inverse * gain_ref[...]).astype(jnp.bfloat16)
            return carry

        lax.fori_loop(0, tokens // piece, norm, 0, unroll=2)

    def multiply(index, carry):
        at = pl.ds(pl.multiple_of(index * tall, tall), tall)
        normed = normed_ref[at, :]
        branch_ref[at, :] = jnp.dot(normed, input_ref[...], preferred_element_type=jnp.float32)
        pre_ref[at, :] = jnp.dot(normed, gate_ref[...], preferred_element_type=jnp.float32)
        return carry

    lax.fori_loop(0, tokens // tall, multiply, 0)
    edge_ref[step] = branch_ref[tokens - SUBLANES :, :]

    def rim_copy(place):
        return pltpu.make_async_remote_copy(
            src_ref=edge_ref.at[place],
            dst_ref=landed_ref.at[place],
            send_sem=send_sem.at[place],
            recv_sem=recv_sem.at[place],
            device_id={"seq": lax.rem(seq + 1, seqs)},
            device_id_type=MESH,
        )

    @pl.when(step == 0)
    def _():
        pl.semaphore_wait(barrier, 1)

    rim_copy(step).start()

    @pl.when(step == steps - 1)
    def _():
        columns = edge_ref.shape[2]
        live = jnp.where(seq > 0, 1.0, 0.0)
        for place in range(steps):
            rim_copy(place).wait()
            rim_ref[:, place * columns : (place + 1) * columns] = live * landed_ref[place]


def front(parts, gain, recur_input, recur_gate):
    count, tokens, width = parts.shape
    model, rec = recur_input.shape
    columns = 4 * LANES
    steps = rec // columns
    low, f32 = (jnp.bfloat16, jnp.float32)
    tall = pl.BlockSpec((model, columns), lambda j: (0, j))
    wide = pl.BlockSpec((tokens, columns), lambda j: (0, j))

    def whole(shape):
        return pl.BlockSpec(shape, lambda j: (0,) * len(shape))

    return pl.pallas_call(
        front_kernel,
        name="norm_and_project",
        grid=(steps,),
        in_specs=[whole(parts.shape), whole((1, model)), tall, tall],
        out_specs=[whole((tokens, model)), whole((tokens, LANES)), whole((tokens, model)), wide, wide]
        + [whole((SUBLANES, rec))],
        out_shape=[
            jax.ShapeDtypeStruct((tokens, model), low),
            jax.ShapeDtypeStruct((tokens, LANES), f32),
            jax.ShapeDtypeStruct((tokens, model), low),
            jax.ShapeDtypeStruct((tokens, rec), f32),
            jax.ShapeDtypeStruct((tokens, rec), f32),
            jax.ShapeDtypeStruct((SUBLANES, rec), f32),
        ],
        scratch_shapes=[
            pltpu.VMEM((steps, SUBLANES, columns), f32),
            pltpu.VMEM((steps, SUBLANES, columns), f32),
            pltpu.SemaphoreType.DMA((steps,)),
            pltpu.SemaphoreType.DMA((steps,)),
        ],
        compiler_params=pltpu.CompilerParams(
            collective_id=3, has_side_effects=True, vmem_limit_bytes=VMEM_BYTES
        ),
        cost_estimate=pl.CostEstimate(
            flops=4 * tokens * model * rec, bytes_accessed=20 * tokens * model, transcendentals=0
        ),
    )(parts, gain[None], recur_input, recur_gate)


def middle_kernel(rows, *refs):
    (last_ref, state_hbm, cum_hbm, pre_hbm, x_ref, out_ref, gain_ref), others = by_rows(
        refs, rows, (True,) * 5 + (False,) * 2
    )
    entering_ref, mixed_ref, resid_ref, normed_ref = others[:4]
    sent_ref, got_ref, held_ref, send_sem, recv_sem, load_sem = others[4:]
    tall, model = resid_ref.shape
    step, steps = (pl.program_id(0), pl.num_programs(0))
    tiles = steps // rows
    slab = 16

    def on_row(place, act):
        for row in range(rows):

            @pl.when(lax.div(place, tiles) == row)
            def _(row=row):
                at = pl.ds(pl.multiple_of(lax.rem(place, tiles) * tall, tall), tall)
                slot = lax.rem(place, 2)
                for kind, source in enumerate((state_hbm, cum_hbm, pre_hbm)):
                    act(
                        pltpu.make_async_copy(
                            source.refs[row].at[0, at], held_ref.at[slot, kind], load_sem.at[slot, kind]
                        )
                    )

    @pl.when(step == 0)
    def _():
        on_row(step, lambda copy: copy.start())
        for row in range(rows):
            sent_ref[row] = last_ref[row]
        carried(sent_ref, got_ref, entering_ref, send_sem, recv_sem, False)

    @pl.when(step + 1 < steps)
    def _():
        on_row(step + 1, lambda copy: copy.start())

    on_row(step, lambda copy: copy.wait())
    slot = lax.rem(step, 2)
    mine = lax.div(step, tiles)

    def mix(index, carry):
        at = pl.ds(pl.multiple_of(index * slab, slab), slab)
        state = held_ref[slot, 0, at, :] + held_ref[slot, 1, at, :] * entering_ref[mine]
        pre = held_ref[slot, 2, at, :]
        inner = jnp.tanh(pre * (GELU_C + (GELU_C * GELU_A) * (pre * pre)))
        mixed_ref[at, :] = (state * (pre * (0.5 + 0.5 * inner))).astype(jnp.bfloat16)
        return carry

    lax.fori_loop(0, tall // slab, mix, 0, unroll=2)
    for row in range(rows):

        @pl.when(mine == row)
        def _(row=row):
            tile = 512
            for first in range(0, model, tile):
                at = slice(first, first + tile)
                resid_ref[:, at] = x_ref.refs[row][:, at].astype(jnp.float32) + jnp.dot(
                    mixed_ref[...], out_ref[:, at], preferred_element_type=jnp.float32
                )

    def norm(index, carry):
        at = pl.ds(pl.multiple_of(index * slab, slab), slab)
        resid = resid_ref[at, :]
        inverse = lax.rsqrt(jnp.mean(resid * resid, axis=1, keepdims=True) + EPS)
        normed_ref[at, :] = (resid * inverse * gain_ref[...]).astype(jnp.bfloat16)
        return carry

    lax.fori_loop(0, tall // slab, norm, 0, unroll=4)


def middle(last, state, cum, pre, x, recur_out, gain):
    rows = len(state)
    _, length, rec = state[0].shape
    model = recur_out.shape[1]
    tall = min(length, 256)
    tiles = length // tall
    tokens = rows * length
    seqs = lax.axis_size("seq")
    low, f32 = (jnp.bfloat16, jnp.float32)

    def whole(shape):
        return pl.BlockSpec(shape, lambda s: (0,) * len(shape), pipeline_mode=pl.Buffered(1))

    def flat(row):
        return lambda s: (jnp.clip(s - row * tiles, 0, tiles - 1), 0)

    summary = (rows, 2, rec)
    return pl.pallas_call(
        functools.partial(middle_kernel, rows),
        name="mix_and_norm",
        grid=(rows * tiles,),
        in_specs=[whole((1, 2, rec))] * rows
        + [pl.BlockSpec(memory_space=pl.ANY)] * (3 * rows)
        + [pl.BlockSpec((tall, model), flat(row)) for row in range(rows)]
        + [whole(recur_out.shape), whole((1, model))],
        out_specs=[
            pl.BlockSpec((rows, 1, rec), lambda s: (0, 0, 0)),
            pl.BlockSpec((tall, rec), lambda s: (s, 0)),
            pl.BlockSpec((tall, model), lambda s: (s, 0)),
            pl.BlockSpec((tall, model), lambda s: (s, 0)),
        ],
        out_shape=[
            jax.ShapeDtypeStruct((rows, 1, rec), f32),
            jax.ShapeDtypeStruct((tokens, rec), low),
            jax.ShapeDtypeStruct((tokens, model), f32),
            jax.ShapeDtypeStruct((tokens, model), low),
        ],
        scratch_shapes=[
            pltpu.VMEM(summary, f32),
            pltpu.VMEM((seqs,) + summary, f32),
            pltpu.VMEM((2, 3, tall, rec), f32),
            pltpu.SemaphoreType.DMA((seqs - 1,)),
            pltpu.SemaphoreType.DMA((seqs - 1,)),
            pltpu.SemaphoreType.DMA((2, 3)),
        ],
        compiler_params=pltpu.CompilerParams(
            collective_id=4, has_side_effects=True, vmem_limit_bytes=VMEM_BYTES
        ),
        cost_estimate=pl.CostEstimate(
            flops=2 * tokens * rec * model, bytes_accessed=14 * tokens * rec, transcendentals=0
        ),
    )(*last, *state, *cum, *pre, *x, recur_out, gain[None])


def hidden_kernel(
    left_ref,
    parts_ref,
    normed_ref,
    gate_ref,
    up_ref,
    down_ref,
    gout_ref,
    hidden_ref,
    dgate_ref,
    dup_ref,
):
    tokens, model = normed_ref.shape
    chunk = down_ref.shape[0]
    rows = left_ref.shape[0]
    length = tokens // rows
    slab = 32

    @pl.when(pl.program_id(0) == 0)
    def _():
        for row in range(rows):

            def collect(index, carry, row=row):
                base = pl.multiple_of(index * slab, slab)
                at = pl.ds(row * length + base, slab)
                low = gathered(parts_ref, at)
                place = base + lax.broadcasted_iota(jnp.int32, low.shape, 0)
                value = jnp.where(place < left_ref[row], low.astype(jnp.float32), 0.0)
                gout_ref[at, :] = value.astype(jnp.bfloat16)
                return carry

            lax.fori_loop(0, length // slab, collect, 0)

    tall = min(tokens, 512)
    wide = 256

    def tile(index, carry):
        at = pl.ds(pl.multiple_of(index * tall, tall), tall)
        for column in range(chunk // wide):
            own = slice(column * wide, (column + 1) * wide)
            gate = jnp.dot(normed_ref[at, :], gate_ref[:, own], preferred_element_type=jnp.float32)
            up = jnp.dot(normed_ref[at, :], up_ref[:, own], preferred_element_type=jnp.float32)
            dhid = lax.dot_general(
                gout_ref[at, :],
                down_ref[own, :],
                (((1,), (1,)), ((), ())),
                preferred_element_type=jnp.float32,
            )
            act, slope = gelu_pair(gate)
            hidden_ref[at, own] = (act * up).astype(jnp.bfloat16)
            dgate_ref[at, own] = (dhid * up * slope).astype(jnp.bfloat16)
            dup_ref[at, own] = (dhid * act).astype(jnp.bfloat16)
        return carry

    lax.fori_loop(0, tokens // tall, tile, 0)


def back_kernel(
    hidden_ref,
    dgate_ref,
    dup_ref,
    gout_ref,
    resid_ref,
    gain_ref,
    gate_ref,
    up_ref,
    down_ref,
    result_ref,
    dres_ref,
    total_ref,
    back_ref,
):
    tall, model = hidden_ref.shape[0], gout_ref.shape[1]
    step, tile = (pl.program_id(0), pl.program_id(1))
    wide = 512
    contract = (((1,), (1,)), ((), ()))
    rows = pl.ds(pl.multiple_of(tile * tall, tall), tall)

    def products(own):
        forth = jnp.dot(hidden_ref[...], down_ref[:, own], preferred_element_type=jnp.float32)
        back = lax.dot_general(
            dgate_ref[...], gate_ref[own, :], contract, preferred_element_type=jnp.float32
        ) + lax.dot_general(
            dup_ref[...], up_ref[own, :], contract, preferred_element_type=jnp.float32
        )
        return (forth, back)

    @pl.when(step == 0)
    def _():
        for first in range(0, model, wide):
            own = slice(first, first + wide)
            forth, back = products(own)
            total_ref[rows, own] = resid_ref[rows, own] + forth
            back_ref[rows, own] = back

    @pl.when(step > 0)
    def _():
        for first in range(0, model, wide):
            own = slice(first, first + wide)
            forth, back = products(own)
            total_ref[rows, own] += forth
            back_ref[rows, own] += back

    @pl.when(step == pl.num_programs(0) - 1)
    def _():
        parts, width = (result_ref.shape[0], result_ref.shape[2])
        small = 16

        def finish(index, carry):
            at = pl.ds(pl.multiple_of(tile * tall + index * small, small), small)
            result = total_ref[at, :].astype(jnp.bfloat16)
            for part in range(parts):
                result_ref[part, at, :] = result[:, part * width : (part + 1) * width]
            resid = resid_ref[at, :]
            inverse = lax.rsqrt(jnp.mean(resid * resid, axis=1, keepdims=True) + EPS)
            normed = resid * inverse
            scaled = back_ref[at, :] * gain_ref[...]
            mean = jnp.mean(scaled * normed, axis=1, keepdims=True)
            dres = gout_ref[at, :].astype(jnp.float32) + inverse * (scaled - normed * mean)
            dres_ref[at, :] = dres.astype(jnp.bfloat16)
            return carry

        lax.fori_loop(0, tall // small, finish, 0, unroll=4)


MLP_CHUNK = 768


def resident(shape):
    return pl.BlockSpec(shape, lambda s: (0,) * len(shape), pipeline_mode=pl.Buffered(1))


def mlp_specs(tokens, model):
    columns = pl.BlockSpec((model, MLP_CHUNK), lambda s: (0, s))
    down = pl.BlockSpec((MLP_CHUNK, model), lambda s: (s, 0))
    made = pl.BlockSpec((tokens, MLP_CHUNK), lambda s: (0, s))
    return ([columns, columns, down], [made] * 3)


def mlp_hidden(left, parts, normed, mlp_gate, mlp_up, mlp_down):
    tokens, model = normed.shape
    ffn = mlp_gate.shape[1]
    low = jnp.bfloat16
    weights, made = mlp_specs(tokens, model)
    tall = jax.ShapeDtypeStruct((tokens, ffn), low)
    return pl.pallas_call(
        hidden_kernel,
        name="mlp_hidden",
        grid=(ffn // MLP_CHUNK,),
        in_specs=[
            pl.BlockSpec(memory_space=pltpu.SMEM),
            resident(parts.shape),
            resident(normed.shape),
            *weights,
        ],
        out_specs=[resident((tokens, model)), *made],
        out_shape=[jax.ShapeDtypeStruct((tokens, model), low), tall, tall, tall],
        compiler_params=pltpu.CompilerParams(vmem_limit_bytes=VMEM_BYTES),
        cost_estimate=pl.CostEstimate(
            flops=6 * tokens * model * ffn,
            bytes_accessed=6 * (model + tokens) * ffn + 6 * tokens * model,
            transcendentals=0,
        ),
    )(left, parts, normed, mlp_gate, mlp_up, mlp_down)


def mlp_back(hidden, dgate, dup, gout, resid, gain, mlp_gate, mlp_up, mlp_down, parts_shape):
    tokens, model = resid.shape
    ffn = mlp_gate.shape[1]
    low, f32 = (jnp.bfloat16, jnp.float32)
    chunk, tall = (2 * MLP_CHUNK, min(tokens, 512))

    def resident(shape):
        return pl.BlockSpec(shape, lambda s, t: (0,) * len(shape), pipeline_mode=pl.Buffered(1))

    columns = pl.BlockSpec((model, chunk), lambda s, t: (0, s))
    down = pl.BlockSpec((chunk, model), lambda s, t: (s, 0))
    made = pl.BlockSpec((tall, chunk), lambda s, t: (t, s))
    return pl.pallas_call(
        back_kernel,
        name="mlp_back",
        grid=(ffn // chunk, tokens // tall),
        in_specs=[
            made,
            made,
            made,
            resident((tokens, model)),
            resident((tokens, model)),
            resident((1, model)),
            columns,
            columns,
            down,
        ],
        out_specs=[resident(parts_shape), resident((tokens, model))],
        out_shape=[
            jax.ShapeDtypeStruct(parts_shape, low),
            jax.ShapeDtypeStruct((tokens, model), low),
        ],
        scratch_shapes=[pltpu.VMEM((tokens, model), f32), pltpu.VMEM((tokens, model), f32)],
        compiler_params=pltpu.CompilerParams(vmem_limit_bytes=VMEM_BYTES),
        cost_estimate=pl.CostEstimate(
            flops=6 * tokens * model * ffn,
            bytes_accessed=6 * (model + tokens) * ffn + 10 * tokens * model,
            transcendentals=0,
        ),
    )(hidden, dgate, dup, gout, resid, gain[None], mlp_gate, mlp_up, mlp_down)


def outputs_kernel(
    device_ref,
    own_ref,
    gate_sum,
    in_sum,
    out_sum,
    small_ref,
    input_ref,
    gate_ref,
    mlp_gate_ref,
    mlp_up_ref,
    gain1_ref,
    gain2_ref,
    sum_gain1,
    sum_in,
    sum_gate,
    sum_taps,
    sum_bias,
    sum_lgates,
    sum_lbias,
    sum_decay,
    sum_out,
    sum_gain2,
    sum_mgate,
    sum_mup,
    sum_down,
):
    rows = sum_mgate.shape[0]
    model = own_ref.shape[1]
    parts = sum_mgate.shape[1] // model
    for part in range(parts):
        at = slice(part * model, (part + 1) * model)
        sum_mgate[:, at] = own_ref[part * rows : (part + 1) * rows, :].astype(jnp.float32)
        sum_mup[:, at] = own_ref[(parts + part) * rows : (parts + part + 1) * rows, :].astype(
            jnp.float32
        )
    sum_down[...] = own_ref[2 * parts * rows :, :].astype(jnp.float32)

    def weighed(*pairs):
        return sum(
            jnp.sum(weight[...].astype(jnp.float32) * gradient[...], axis=1, keepdims=True)
            for weight, gradient in pairs
        )

    def as_row(column, gain):
        lane = lax.broadcasted_iota(jnp.int32, (rows, LANES), 1)
        place = lax.broadcasted_iota(jnp.int32, (rows, LANES), 0)
        whole = lax.broadcasted_iota(jnp.int32, (rows, model), 1)
        own = device_ref[0] * rows + lax.broadcasted_iota(jnp.int32, (rows, model), 0)
        own_gain = jnp.sum(jnp.where(whole == own, gain[...], 0.0), axis=1, keepdims=True)
        return jnp.sum(jnp.where(lane == place, column / own_gain, 0.0), axis=0, keepdims=True)

    row1 = as_row(weighed((input_ref, in_sum), (gate_ref, gate_sum)), gain1_ref)
    row2 = as_row(weighed((mlp_gate_ref, sum_mgate), (mlp_up_ref, sum_mup)), gain2_ref)
    sum_gain1[...] = row1[:, :rows]
    sum_gain2[...] = row2[:, :rows]
    sum_in[...] = in_sum[...]
    sum_gate[...] = gate_sum[...]
    sum_out[...] = out_sum[...]
    channels = small_ref.shape[0]
    size = sum_lgates.shape[1] // 2
    first, second = (small_ref[:, :LANES], small_ref[:, LANES:])
    lane = lax.broadcasted_iota(jnp.int32, (channels, LANES), 1)
    moved = pltpu.roll(second, size, 1)
    sum_lgates[:, :LANES] = jnp.where(lane < size, first, moved)
    sum_lgates[:, LANES:] = moved[:, : 2 * size - LANES]
    filled = jnp.concatenate([first, jnp.zeros((LANES - channels, LANES), jnp.float32)], axis=0)
    turned = filled.T
    sum_taps[...] = turned[size : size + 4, :channels]
    sum_bias[...] = turned[size + 4 : size + 5, :channels]
    sum_lbias[...] = turned[size + 5 : size + 7, :channels]
    sum_decay[...] = turned[size + 7 : size + 8, :channels]


def outputs(
    device, own, gate_sum, in_sum, out_sum, small, recur_input, recur_gate, mlp_gate, mlp_up, gain1, gain2, size
):
    rows, rec = in_sum.shape
    model, ffn = mlp_gate.shape
    channels = small.shape[0]
    f32 = jnp.float32

    def whole(shape):
        return pl.BlockSpec(shape, lambda s, device: (0,) * len(shape))

    def mine(shape):
        return pl.BlockSpec(shape, lambda s, device: (device[0], 0))

    given = (own, gate_sum, in_sum, out_sum, small)
    shapes = [(1, rows), (rows, rec), (rows, rec), (4, channels), (1, channels)]
    shapes += [(channels, 2 * size), (2, channels), (1, channels), out_sum.shape, (1, rows)]
    shapes += [(rows, ffn), (rows, ffn), (own.shape[0] - 2 * ffn // model * rows, model)]
    return pl.pallas_call(
        outputs_kernel,
        name="outputs",
        grid_spec=pltpu.PrefetchScalarGridSpec(
            num_scalar_prefetch=1,
            grid=(1,),
            in_specs=[whole(a.shape) for a in given]
            + [mine((rows, rec))] * 2
            + [mine((rows, ffn))] * 2
            + [whole((1, model))] * 2,
            out_specs=[whole(shape) for shape in shapes],
        ),
        out_shape=[jax.ShapeDtypeStruct(shape, f32) for shape in shapes],
        compiler_params=pltpu.CompilerParams(vmem_limit_bytes=VMEM_BYTES),
    )(
        device[None],
        *given,
        recur_input,
        recur_gate,
        mlp_gate,
        mlp_up,
        gain1[None],
        gain2[None],
    )


def spread_kernel(whole_ref, out_ref):
    out_ref[0] = whole_ref[...]


def spread(whole, count):
    tokens, width = (whole.shape[0], whole.shape[1] // count)
    return pl.pallas_call(
        spread_kernel,
        name="spread_features",
        grid=(count,),
        in_specs=[pl.BlockSpec((tokens, width), lambda j: (0, j))],
        out_specs=pl.BlockSpec((1, tokens, width), lambda j: (j, 0, 0)),
        out_shape=jax.ShapeDtypeStruct((count, tokens, width), whole.dtype),
        cost_estimate=pl.CostEstimate(
            flops=0, bytes_accessed=4 * tokens * whole.shape[1], transcendentals=0
        ),
    )(whole)


CHAN = ("zed", "core")


def features_in(local, pick=slice(None)):
    count = lax.axis_size(CHAN)
    rows, length, width = local.shape
    local = local.reshape(count, rows // count, length, width)[:, pick]
    if width % LANES == 0:
        return lax.all_to_all(local, CHAN, 0, 0, tiled=True).reshape(count, -1, width)
    moved = lax.all_to_all(
        local.reshape(-1, length, width), CHAN, split_axis=0, concat_axis=2, tiled=True
    )
    return moved.reshape(1, -1, count * width)


def features_apart(whole):
    count = lax.axis_size(CHAN)
    if (whole.shape[1] // count) % LANES == 0:
        return spread(whole, count)
    return whole[None]


def features_out(parts, rows):
    blocks, tokens, width = parts.shape
    parts = parts.reshape(blocks, rows, tokens // rows, width)
    if blocks > 1:
        moved = lax.all_to_all(parts, CHAN, 0, 0, tiled=True)
        return moved.reshape(-1, *parts.shape[2:])
    return lax.all_to_all(parts[0], CHAN, split_axis=2, concat_axis=0, tiled=True)


class Corners:
    def __init__(self, seq, zed):
        self.seq_bits, self.zed_bits = (seq.bit_length() - 1, zed.bit_length() - 1)
        self.count = self.seq_bits + self.zed_bits
        self.dims = (2,) * self.count
        self.low = tuple(range(self.seq_bits))[::-1] + tuple(range(self.seq_bits, self.count))[::-1]
        self.high = tuple(range(self.seq_bits)) + tuple(range(self.seq_bits, self.count))[::-1]

    def place(self, dim):
        if dim < self.seq_bits:
            return ("seq", 2 ** (self.seq_bits - 1 - dim))
        return ("zed", 2 ** (self.count - 1 - dim))

    def bit(self, dim):
        axis, weight = self.place(dim)
        return lax.rem(lax.div(lax.axis_index(axis), weight), 2)

    def partner(self, dim):
        axis, weight = self.place(dim)
        return {axis: lax.axis_index(axis) + weight * (1 - 2 * self.bit(dim))}


def tail_kernel(
    corners,
    orders,
    dgate_hbm,
    dbranch_hbm,
    ending_ref,
    leading_ref,
    mixed_hbm,
    dres_hbm,
    gain_ref,
    input_hbm,
    gate_hbm,
    small_hbm,
    *refs,
):
    rows = ending_ref.shape[0]
    normed_hbms, x_hbms, inverse_hbms = (refs[k * rows : (k + 1) * rows] for k in range(3))
    tokens_ref, sum_gate, sum_out, sum_in, sum_small = refs[3 * rows : 3 * rows + 5]
    refs = refs[3 * rows + 5 :]
    stages = corners.count + 1
    dgate, dbranch, mixed, dres, normed, x, inverse, weight_in, weight_gate = refs[:9]
    made_in, made_out, own_small, back, parts, rim = refs[9:15]
    slots_in, slots_out, slots_small = (
        refs[15 + k * stages : 15 + (k + 1) * stages] for k in range(3)
    )
    (
        send_sem,
        recv_sem,
        load_sem,
        move_send,
        move_recv,
        keep_sem,
        rim_send,
        rim_recv,
    ) = refs[15 + 3 * stages :]
    seq, zed, core = (lax.axis_index(axis) for axis in ("seq", "zed", "core"))
    seqs, group = (lax.axis_size("seq"), 2 * lax.axis_size("zed"))
    mine = zed * 2 + core
    length = tokens_ref.shape[1]
    model = x.shape[1]

    def member(index):
        return {"zed": lax.div(index, 2), "core": lax.rem(index, 2)}

    def by_row(sources, target):
        return [
            (source, target.at[pl.ds(row * length, length)]) for row, source in enumerate(sources)
        ]

    pairs = [
        (dbranch_hbm, dbranch),
        (input_hbm, weight_in),
        (dgate_hbm, dgate),
        (gate_hbm, weight_gate),
        *by_row(x_hbms, x),
        *by_row(inverse_hbms, inverse),
        (dres_hbm, dres),
        *by_row(normed_hbms, normed),
        (mixed_hbm, mixed),
        (small_hbm.at[(slice(None),) * corners.count + (core,)], own_small),
    ]
    kinds = []
    for name in ('dbranch', 'win', 'dgate', 'wgate', 'x', 'inverse', 'dres', 'normed', 'mixed', 'small'):
        kinds += [name] * (rows if name in ("normed", "x", "inverse") else 1)
    loads = [
        pltpu.make_async_copy(source, target, load_sem.at[place])
        for place, (source, target) in enumerate(pairs)
    ]
    for load in loads:
        load.start()

    barrier = pltpu.get_barrier_semaphore()
    for other in range(1, group):
        pl.semaphore_signal(
            barrier, inc=1, device_id=member(lax.rem(mine + other, group)), device_id_type=MESH
        )
    for other in range(1, seqs):
        pl.semaphore_signal(
            barrier, inc=1, device_id={"seq": lax.rem(seq + other, seqs)}, device_id_type=MESH
        )
    pl.semaphore_wait(barrier, group - 1 + seqs - 1)

    rim_copy = pltpu.make_async_remote_copy(
        src_ref=leading_ref,
        dst_ref=rim,
        send_sem=rim_send,
        recv_sem=rim_recv,
        device_id={"seq": lax.rem(seq + seqs - 1, seqs)},
        device_id_type=MESH,
    )
    rim_copy.start()

    def own(stream, index):
        if stream < 4:
            return made_in.at[(stream,) + index + (core,)]
        if stream < 6:
            return made_out.at[(stream - 4,) + index + (core,)]
        return own_small.at[index]

    def slot(stream, stage):
        if stream < 4:
            return slots_in[stage].at[stream]
        if stream < 6:
            return slots_out[stage].at[stream - 4]
        return slots_small[stage]

    def copy(stream, stage):
        order = orders[stream]
        every = (slice(None),) * corners.count
        if stage == 0:
            if stream < 4:
                source = made_in.at[(stream,) + every + (1 - core,)]
            elif stream < 6:
                source = made_out.at[(stream - 4,) + every + (1 - core,)]
            else:
                source = small_hbm.at[every + (1 - core,)]
            target = {"core": 1 - core}
        else:
            dim = order[stage - 1]
            fixed = {before: corners.bit(before) for before in order[: stage - 1]}
            fixed[dim] = 1 - corners.bit(dim)
            source = own(stream, tuple(fixed.get(d, slice(None)) for d in range(corners.count)))
            target = corners.partner(dim)
        return pltpu.make_async_remote_copy(
            src_ref=source,
            dst_ref=slot(stream, stage),
            send_sem=send_sem.at[stream, stage],
            recv_sem=recv_sem.at[stream, stage],
            device_id=target,
            device_id_type=MESH,
        )

    sums = [
        sum_gate.at[:, : sum_gate.shape[1] // 2],
        sum_gate.at[:, sum_gate.shape[1] // 2 :],
        sum_in.at[:, : sum_in.shape[1] // 2],
        sum_in.at[:, sum_in.shape[1] // 2 :],
        sum_out.at[:, : sum_out.shape[1] // 2],
        sum_out.at[:, sum_out.shape[1] // 2 :],
        sum_small,
    ]

    def advance(stream, stage):
        order = orders[stream]
        copy(stream, stage).wait_recv()
        left = [dim for dim in range(corners.count) if dim not in order[:stage]]
        fixed = {dim: corners.bit(dim) for dim in order[:stage]}
        arrived = slot(stream, stage)
        if not left:
            index = tuple(fixed[dim] for dim in range(corners.count))
            sums[stream][...] = own(stream, index)[...].astype(jnp.float32) + arrived[...].astype(
                jnp.float32
            )
            return

        def add(index, carry):
            part = {
                dim: lax.rem(lax.div(index, 2 ** (len(left) - 1 - place)), 2)
                for place, dim in enumerate(left)
            }
            kept = own(stream, tuple({**fixed, **part}[dim] for dim in range(corners.count)))
            total = kept[...].astype(jnp.float32) + arrived[
                tuple(part[dim] for dim in left)
            ].astype(jnp.float32)
            kept[...] = total.astype(jnp.bfloat16)
            return carry

        lax.fori_loop(0, 2 ** len(left), add, 0)
        copy(stream, stage + 1).start()

    def move(other, row):
        to = lax.rem(mine + other, group)
        return pltpu.make_async_remote_copy(
            src_ref=parts.at[to, pl.ds(row * length, length)],
            dst_ref=tokens_ref.at[mine * rows + row],
            send_sem=move_send.at[other - 1, row],
            recv_sem=move_recv.at[other - 1, row],
            device_id=member(to),
            device_id_type=MESH,
        )

    def keep(row):
        return pltpu.make_async_copy(
            parts.at[mine, pl.ds(row * length, length)],
            tokens_ref.at[mine * rows + row],
            keep_sem.at[row],
        )

    tile = 256
    width = parts.shape[2]

    def back_row(row):
        at_row = slice(row * length, (row + 1) * length)

        def product(index, carry):
            at = pl.ds(pl.multiple_of(index * tile, tile), tile)
            contract = (((1,), (1,)), ((), ()))
            back[:, at] = lax.dot_general(
                dbranch[at_row, :], weight_in[at, :], contract, preferred_element_type=jnp.float32
            ) + lax.dot_general(
                dgate[at_row, :], weight_gate[at, :], contract, preferred_element_type=jnp.float32
            )
            return carry

        lax.fori_loop(0, model // tile, product, 0)
        slab = 16

        def norm(index, carry):
            base = pl.multiple_of(index * slab, slab)
            at = pl.ds(row * length + base, slab)
            inv = inverse[at, :1]
            value = x[at, :].astype(jnp.float32) * inv
            scaled = back[pl.ds(base, slab), :] * gain_ref[...]
            mean = jnp.mean(scaled * value, axis=1, keepdims=True)
            grad = dres[at, :].astype(jnp.float32) + inv * (scaled - value * mean)
            grad = grad.astype(jnp.bfloat16)
            for part in range(parts.shape[0]):
                parts[part, at, :] = grad[:, part * width : (part + 1) * width]
            return carry

        lax.fori_loop(0, length // slab, norm, 0, unroll=4)
        for other in range(1, group):
            move(other, row).start()
        keep(row).start()

    def weight_product(left, right, made, stream, first):
        columns = made.shape[-1]
        shape = made.shape[1:-1]

        def product(index, carry):
            at = pl.ds(pl.multiple_of(index * tile, tile), tile)
            source = pl.ds(pl.multiple_of(first + index * tile, tile), tile)
            part = lax.dot_general(
                left[...],
                right[:, source],
                (((0,), (0,)), ((), ())),
                preferred_element_type=jnp.float32,
            )
            made[(stream,) + (slice(None),) * len(shape) + (at,)] = part.astype(
                jnp.bfloat16
            ).reshape(shape + (tile,))
            return carry

        lax.fori_loop(0, columns // tile, product, 0)

    half, half_out = (made_in.shape[-1], made_out.shape[-1])
    waited, reached = (set(), {})

    def need(*names):
        for place, name in enumerate(kinds):
            if name in names and place not in waited:
                waited.add(place)
                loads[place].wait()

    def fix_rim():
        need("dbranch")
        rim_copy.wait()
        live = jnp.where(seq < seqs - 1, 1.0, 0.0)
        for row in range(rows):
            at = slice((row + 1) * length - STEP, (row + 1) * length)
            inside = dbranch[at, :].astype(jnp.float32)
            last = ending_ref[row] + live * rim[row]
            dbranch[at, :] = jnp.concatenate([inside[: STEP - SUBLANES], last], axis=0).astype(
                jnp.bfloat16
            )

    def begin(stream):
        copy(stream, 0).start()
        reached[stream] = 0

    def progress(streams):
        for stream in streams:
            if stream in reached and reached[stream] < stages:
                if stream == 6:
                    need("small")
                advance(stream, reached[stream])
                reached[stream] += 1

    def compute(item):
        if item == "gate":
            need("normed", "dgate")
            for stream in (0, 1):
                weight_product(normed, dgate, made_in, stream, stream * half)
                begin(stream)
        elif item == "out":
            need("mixed", "dres")
            for stream in (4, 5):
                weight_product(mixed, dres, made_out, stream - 4, (stream - 4) * half_out)
                begin(stream)
        elif item == "in":
            need("normed", "dbranch")
            for stream in (2, 3):
                weight_product(normed, dbranch, made_in, stream, (stream - 2) * half)
                begin(stream)
        else:
            need("dbranch", "dgate", "win", "wgate", "x", "inverse", "dres")
            back_row(item)

    begin(6)
    fix_rim()
    compute(0)
    compute(1)
    compute('gate')
    progress((6,))
    compute('out')
    progress((0, 1))
    compute('in')
    progress((0, 1))
    progress((4, 5))
    progress((6,))
    while any(reached[stream] < stages for stream in range(7)):
        progress((0, 1, 4, 5, 2, 3, 6))
    for stage in range(stages):
        for stream in range(7):
            copy(stream, stage).wait_send()
    for row in range(rows):
        for other in range(1, group):
            move(other, row).wait()
        keep(row).wait()


def tail(dgate, dbranch, ending, leading, mixed, dres, gain, w_in, w_gate, small, normed, x, inverse):
    corners = Corners(lax.axis_size("seq"), lax.axis_size("zed"))
    group, devices = (lax.axis_size(CHAN), 2 ** (corners.count + 1))
    tokens, model = dres.shape
    rec = dgate.shape[1]
    rows = ending.shape[0]
    length, width = (tokens // rows, model // group)
    low, f32 = (jnp.bfloat16, jnp.float32)
    stages = corners.count + 1
    in_rows, out_rows = (model // devices, rec // devices)
    small = small.reshape(corners.dims + (2, out_rows, small.shape[1]))
    orders = [corners.low, corners.high] * 3 + [corners.low]

    def slots(lead, shape):
        return [pltpu.VMEM(lead + (2,) * (corners.count - k) + shape, low) for k in range(stages)]

    in_shape, out_shape = ((in_rows, rec // 2), (out_rows, model // 2))
    loaded = (dgate, dbranch, mixed, dres, dres, dres)
    loaded += (jax.ShapeDtypeStruct((tokens, LANES), f32), w_in, w_gate)
    anyplace = pl.BlockSpec(memory_space=pl.ANY)
    vmem = pl.BlockSpec(memory_space=pltpu.VMEM)
    dma = pltpu.SemaphoreType.DMA
    moved = sum(math.prod(a.shape) * a.dtype.itemsize for a in loaded)
    return pl.pallas_call(
        functools.partial(tail_kernel, corners, orders),
        name="tail",
        in_specs=[anyplace, anyplace, vmem, vmem, anyplace, anyplace, vmem]
        + [anyplace] * (3 + 3 * rows),
        out_specs=[anyplace] + [vmem] * 4,
        out_shape=[
            jax.ShapeDtypeStruct((group * rows, length, width), low),
            jax.ShapeDtypeStruct((in_rows, rec), f32),
            jax.ShapeDtypeStruct((out_rows, model), f32),
            jax.ShapeDtypeStruct((in_rows, rec), f32),
            jax.ShapeDtypeStruct(small.shape[-2:], f32),
        ],
        scratch_shapes=[pltpu.VMEM(a.shape, a.dtype) for a in loaded]
        + [
            pltpu.VMEM((4,) + corners.dims + (2,) + in_shape, low),
            pltpu.VMEM((2,) + corners.dims + (2,) + out_shape, low),
            pltpu.VMEM(corners.dims + small.shape[-2:], low),
            pltpu.VMEM((length, model), f32),
            pltpu.VMEM((group, tokens, width), low),
            pltpu.VMEM(leading.shape, leading.dtype),
        ]
        + slots((4,), in_shape)
        + slots((2,), out_shape)
        + slots((), small.shape[-2:])
        + [
            dma((7, stages)),
            dma((7, stages)),
            dma((7 + 3 * rows,)),
            dma((group - 1, rows)),
            dma((group - 1, rows)),
            dma((rows,)),
            dma,
            dma,
        ],
        compiler_params=pltpu.CompilerParams(
            collective_id=1, has_side_effects=True, vmem_limit_bytes=60 * 1024 * 1024
        ),
        cost_estimate=pl.CostEstimate(
            flops=10 * tokens * model * rec, bytes_accessed=2 * moved, transcendentals=0
        ),
    )(dgate, dbranch, ending, leading, mixed, dres, gain[None], w_in, w_gate, small, *normed, *x, *inverse)


def grads_kernel(
    normed_ref,
    dgate_ref,
    dup_ref,
    hidden_ref,
    gout_ref,
    out_ref,
    turned_ref,
    made_wide,
    made_down,
    come_wide,
    come_down,
    send_sem,
    recv_sem,
    store_sem,
):
    step = pl.program_id(0)
    core = lax.axis_index("core")
    other = {"core": 1 - core}
    wide_rows, down_rows = (made_wide.shape[3], made_down.shape[3])
    wides, downs = (come_wide.shape[0], come_down.shape[0])
    total = wides + downs
    down_at = wides * wide_rows

    def exchange(made, come, index, slot):
        return pltpu.make_async_remote_copy(
            src_ref=made.at[lax.rem(index, 2), 1 - core],
            dst_ref=come.at[index],
            send_sem=send_sem.at[slot],
            recv_sem=recv_sem.at[slot],
            device_id=other,
            device_id_type=MESH,
        )

    def store_wide(index):
        return pltpu.make_async_copy(
            come_wide.at[index],
            out_ref.at[:, pl.ds(pl.multiple_of(index * wide_rows, wide_rows), wide_rows)],
            store_sem.at[index],
        )

    def store_down(index):
        chips = come_down.shape[1]
        return pltpu.make_async_copy(
            come_down.at[index],
            out_ref.at[pl.ds(index * chips, chips), pl.ds(down_at, down_rows)],
            store_sem.at[index + wides],
        )

    @pl.when(step == 0)
    def _():
        barrier = pltpu.get_barrier_semaphore()
        pl.semaphore_signal(barrier, inc=1, device_id=other, device_id_type=MESH)
        pl.semaphore_wait(barrier, 1)
        turned_ref[...] = normed_ref[...].T

    def product_wide(source, index):
        made = made_wide.at[lax.rem(index, 2)]
        chips, rows = (made.shape[1], made.shape[2])
        tile = 512

        def column(place, carry):
            at = pl.ds(pl.multiple_of(place * tile, tile), tile)
            part = jnp.dot(turned_ref[...], source[:, at], preferred_element_type=jnp.float32)
            part = part.astype(jnp.bfloat16).reshape(chips, 2, rows, tile)
            made[0, :, :, at] = part[:, 0]
            made[1, :, :, at] = part[:, 1]
            return carry

        lax.fori_loop(0, source.shape[1] // tile, column, 0)

    def product_tall(left, right, made_all, index):
        made = made_all.at[lax.rem(index, 2)]
        chips, rows = (made.shape[1], made.shape[2])
        tile = 512

        def column(place, carry):
            at = pl.ds(pl.multiple_of(place * tile, tile), tile)
            part = lax.dot_general(
                left[...], right[:, at], (((0,), (0,)), ((), ())), preferred_element_type=jnp.float32
            )
            part = part.astype(jnp.bfloat16).reshape(chips, 2, rows, tile)
            made[0, :, :, at] = part[:, 0]
            made[1, :, :, at] = part[:, 1]
            return carry

        lax.fori_loop(0, right.shape[1] // tile, column, 0)

    half = wides // 2

    @pl.when(step < half)
    def _():
        product_wide(dgate_ref, step)

    @pl.when((step >= half) & (step < wides))
    def _():
        product_wide(dup_ref, step)

    @pl.when(step < wides)
    def _():
        exchange(made_wide, come_wide, step, step).start()

    @pl.when((step >= wides) & (step < total))
    def _():
        product_tall(hidden_ref, gout_ref, made_down, step - wides)
        exchange(made_down, come_down, step - wides, step).start()

    def finish(made, come, index, slot, store):
        exchange(made, come, index, slot).wait()
        mine = made.at[lax.rem(index, 2), core]
        arrived = come.at[index]

        def add(chip, carry):
            both = mine[chip].astype(jnp.float32) + arrived[chip].astype(jnp.float32)
            arrived[chip] = both.astype(jnp.bfloat16)
            return carry

        lax.fori_loop(0, come.shape[1], add, 0)
        store(index).start()

    before = step - 1

    @pl.when((before >= 0) & (before < wides))
    def _():
        finish(made_wide, come_wide, before, before, store_wide)

    @pl.when(before >= wides)
    def _():
        finish(made_down, come_down, before - wides, before, store_down)

    @pl.when(step == total)
    def _():
        for index in range(wides):
            store_wide(index).wait()
        for index in range(downs):
            store_down(index).wait()


def block_gradients(normed, dgate, dup, hidden, gout):
    tokens, model = normed.shape
    ffn = hidden.shape[1]
    chips = lax.axis_size("seq") * lax.axis_size("zed")
    devices = 2 * chips
    wide_rows, down_rows = (model // devices, ffn // devices)
    chunk = 768
    wides, downs = (2 * ffn // model, ffn // chunk)
    half = wides // 2
    down_chips = chunk // (2 * down_rows)
    rows = wides * wide_rows + down_rows
    low = jnp.bfloat16

    def whole(array):
        return pl.BlockSpec(array.shape, lambda s: (0, 0), pipeline_mode=pl.Buffered(1))

    def part(columns, first, count):
        return pl.BlockSpec((tokens, columns), lambda s: (0, jnp.clip(s - first, 0, count - 1)))

    total = wides + downs
    flops = 6 * tokens * model * ffn
    arrays = (normed, dgate, dup, hidden, gout)
    moved = sum(math.prod(a.shape) * 2 for a in arrays) + chips * rows * model * 2
    return pl.pallas_call(
        grads_kernel,
        name="block_gradients",
        grid=(total + 1,),
        in_specs=[
            whole(normed),
            part(model, 0, half),
            part(model, half, half),
            part(chunk, wides, downs),
            whole(gout),
        ],
        out_specs=pl.BlockSpec(memory_space=pl.ANY),
        out_shape=jax.ShapeDtypeStruct((chips, rows, model), low),
        scratch_shapes=[
            pltpu.VMEM((model, tokens), low),
            pltpu.VMEM((2, 2, chips, wide_rows, model), low),
            pltpu.VMEM((2, 2, down_chips, down_rows, model), low),
            pltpu.VMEM((wides, chips, wide_rows, model), low),
            pltpu.VMEM((downs, down_chips, down_rows, model), low),
            pltpu.SemaphoreType.DMA((total,)),
            pltpu.SemaphoreType.DMA((total,)),
            pltpu.SemaphoreType.DMA((total,)),
        ],
        compiler_params=pltpu.CompilerParams(
            collective_id=2, has_side_effects=True, vmem_limit_bytes=VMEM_BYTES
        ),
        cost_estimate=pl.CostEstimate(flops=flops, bytes_accessed=moved, transcendentals=0),
    )(*arrays)


def passed_along(value, axis, steps):
    count = lax.axis_size(axis)
    leading, last = (max(0, -steps), min(count, count - steps))
    return lax.ppermute(value, axis, [(source, source + steps) for source in range(leading, last)])


def weight_grad(left, right):
    return lax.dot_general(
        left, right, (((0,), (0,)), ((), ())), preferred_element_type=jnp.float32
    ).astype(jnp.bfloat16)


def back_dot(left, right):
    return lax.dot_general(
        left, right, (((1,), (1,)), ((), ())), preferred_element_type=jnp.float32
    )


def fwd_dot(left, right):
    return jnp.dot(left, right, preferred_element_type=jnp.float32)


def gelu_fn(value):
    return jax.nn.gelu(value, approximate=True)


def norm_back(grad_norm, normed, inverse, gain):
    scaled = grad_norm * gain
    mean_term = jnp.mean(scaled * normed, axis=1, keepdims=True)
    return inverse * (scaled - normed * mean_term)


def scattered(gradient):
    return lax.psum_scatter(
        gradient, ("seq", "zed", "core"), scatter_dimension=0, tiled=True
    ).astype(jnp.float32)


def body(
    tokens,
    cotangent,
    doc_starts,
    lengths,
    norm1_gain,
    recur_input,
    recur_gate,
    conv_kernel,
    conv_bias,
    lru_gates,
    lru_bias,
    lru_decay,
    recur_out,
    norm2_gain,
    mlp_gate,
    mlp_up,
    mlp_down,
):
    count = lax.axis_size(CHAN)
    row_count, block_len = (tokens.shape[0] // count, tokens.shape[1])
    model_dim = tokens.shape[2] * count
    tok_count = row_count * block_len
    rec_width = recur_input.shape[1]
    ffn_width = mlp_gate.shape[1]
    head_count = H
    head_size = rec_width // head_count
    tap_count = conv_kernel.shape[0]
    rim_size = tap_count - 1
    seq_index = lax.axis_index("seq")
    position = seq_index * block_len + jnp.arange(block_len, dtype=jnp.int32)
    bounds = jnp.concatenate([doc_starts, lengths[:, None]], axis=1)
    is_before = bounds[:, None, :] <= position[None, :, None]
    seg_start = jnp.max(jnp.where(is_before, bounds[:, None, :], 0), axis=2)
    dist = jnp.broadcast_to(
        (position[None, :] - seg_start)[:, :, None], (row_count, block_len, LANES)
    )
    soft_decay = jax.nn.softplus(-lru_decay)
    params = jnp.concatenate(
        [
            conv_kernel,
            conv_bias[None],
            lru_bias,
            (-8.0 * soft_decay)[None],
            (8.0 * jax.nn.sigmoid(-lru_decay))[None],
            jnp.zeros((SUBLANES - 1, rec_width), jnp.float32),
        ],
        axis=0,
    )
    core = Recurrence(row_count, block_len, rec_width, head_size)
    wide_gates = core.widen(lru_gates)
    if tokens.shape[2] % LANES == 0:
        blocks = [features_in(tokens, slice(row, row + 1)) for row in range(row_count)]
    else:
        side = features_in(tokens)
        blocks = [side[:, row * block_len : (row + 1) * block_len] for row in range(row_count)]
    single = Recurrence(1, block_len, rec_width, head_size)
    per_row = []
    for row in range(row_count):
        block = blocks[row]
        if row:
            block, _ = lax.optimization_barrier((block, per_row[-1][-1]))
        else:
            block, wide_gates, params, dist = lax.optimization_barrier(
                (block, wide_gates, params, dist)
            )
        low_x, inverse, normed, branch, pre, rim = front(block, norm1_gain, recur_input, recur_gate)
        branch, rim = (branch[None], rim[None])
        scanned = single.forward(branch, rim, dist[row : row + 1], params, wide_gates)
        per_row.append((low_x, inverse, normed, branch, pre[None], rim, *scanned))
    low_x, inverse, normed_low, branch, gate_pre, rim, lru_in, rate, igate, state, cum, last = zip(
        *per_row
    )
    entering, mixed_low, resid_one, normed_low2 = middle(
        last, state, cum, gate_pre, low_x, recur_out, norm2_gain
    )
    cotangent, _ = lax.optimization_barrier((cotangent, block))
    cotangent, resid_one = lax.optimization_barrier((features_in(cotangent), resid_one))
    grad_low, hidden_low, mgate_low, mup_low = mlp_hidden(
        lengths - seq_index * block_len, cotangent, normed_low2, mlp_gate, mlp_up, mlp_down
    )
    devices = lax.axis_size(("seq", "zed", "core"))
    own_rows = model_dim // devices
    tiled = own_rows % (2 * SUBLANES) == 0 and tokens.shape[2] % LANES == 0
    if tiled:
        merged = block_gradients(normed_low2, mgate_low, mup_low, hidden_low, grad_low)
        merged, hidden_low = lax.optimization_barrier((merged, hidden_low))
        merged = lax.psum_scatter(merged, "seq", scatter_dimension=0, tiled=True)
    result_parts, resid_low = mlp_back(
        hidden_low,
        mgate_low,
        mup_low,
        grad_low,
        resid_one,
        norm2_gain,
        mlp_gate,
        mlp_up,
        mlp_down,
        cotangent.shape,
    )
    output = features_out(result_parts, row_count)
    gate_low, back_local, back_cum, first_term = core.adjoint(
        resid_low,
        recur_out,
        gate_pre,
        state,
        cum,
        entering,
        rate,
        dist,
        params,
    )
    gate_low = gate_low.reshape(tok_count, rec_width)

    def zed_stage(leaving):
        if not tiled:
            return ((), leaving)
        done, leaving = lax.optimization_barrier((merged, leaving))
        return (lax.psum_scatter(done, "zed", scatter_dimension=0, tiled=True), leaving)

    branch_local, ending, leading, small, merged_own = core.backward(
        back_local,
        back_cum,
        first_term,
        last,
        state,
        cum,
        entering,
        rate,
        igate,
        lru_in,
        dist,
        branch,
        rim,
        params,
        wide_gates,
        zed_stage,
    )
    branch_low = branch_local.reshape(tok_count, rec_width)
    if tiled:
        output, branch_low = lax.optimization_barrier((output, branch_low))
        grad_tokens, sum_rgate, sum_rout, sum_rin, own_small = tail(
            gate_low,
            branch_low,
            ending,
            leading,
            mixed_low,
            resid_low,
            norm1_gain,
            recur_input,
            recur_gate,
            small,
            normed_low,
            low_x,
            inverse,
        )
        device = lax.axis_index(("seq", "zed", "core"))
        sums = outputs(
            device,
            merged_own[0],
            sum_rgate,
            sum_rin,
            sum_rout,
            own_small,
            recur_input,
            recur_gate,
            mlp_gate,
            mlp_up,
            norm1_gain,
            norm2_gain,
            head_size,
        )
        flat = (0, 4, 7, 9)
        sums = [part.reshape(-1) if place in flat else part for place, part in enumerate(sums)]
        return (output, grad_tokens, *sums)
    else:
        from_next = passed_along(
            leading[:, SUBLANES - rim_size :, :].astype(jnp.bfloat16), "seq", -1
        )
        ending = ending + jnp.pad(
            from_next.astype(jnp.float32), ((0, 0), (SUBLANES - rim_size, 0), (0, 0))
        )
        branch_low = lax.dynamic_update_slice(
            branch_local, ending.astype(jnp.bfloat16), (0, block_len - SUBLANES, 0)
        ).reshape(tok_count, rec_width)
        grad_norm1 = back_dot(branch_low, recur_input) + back_dot(gate_low, recur_gate)
        inv_one = jnp.concatenate(inverse)[:, :1]
        normed_one = jnp.concatenate(low_x).astype(jnp.float32) * inv_one
        normed_low = jnp.concatenate(normed_low)
        input_part = norm_back(grad_norm1, normed_one, inv_one, norm1_gain)
        grad_x = (resid_low.astype(jnp.float32) + input_part).astype(jnp.bfloat16)
        grad_tokens = features_out(features_apart(grad_x), row_count)
        sum_mgate, sum_mup, sum_down, sum_rout, sum_rgate, sum_rin = (
            scattered(weight_grad(left, right))
            for left, right in (
                (normed_low2, mgate_low),
                (normed_low2, mup_low),
                (hidden_low, grad_low),
                (mixed_low, resid_low),
                (normed_low, gate_low),
                (normed_low, branch_low),
            )
        )
        own_small = scattered(small)
    sum_lgates = jnp.concatenate(
        [own_small[:, :head_size], own_small[:, LANES : LANES + head_size]], axis=1
    )
    own_sums = jnp.swapaxes(own_small[:, head_size : head_size + SUBLANES], 0, 1)
    device = lax.axis_index(("seq", "zed", "core"))

    def mine(array, size, axis=0):
        return lax.dynamic_slice_in_dim(array, device * size, size, axis)

    def weighed(weight, gradient):
        return jnp.sum(mine(weight, own_rows).astype(jnp.float32) * gradient, axis=1)

    sum_gain1 = (weighed(recur_input, sum_rin) + weighed(recur_gate, sum_rgate)) / mine(
        norm1_gain, own_rows
    )
    sum_gain2 = (weighed(mlp_gate, sum_mgate) + weighed(mlp_up, sum_mup)) / mine(
        norm2_gain, own_rows
    )
    sum_decay = own_sums[7]
    return (
        output,
        grad_tokens,
        sum_gain1,
        sum_rin,
        sum_rgate,
        own_sums[:4],
        own_sums[4],
        sum_lgates,
        own_sums[5:7],
        sum_decay,
        sum_rout,
        sum_gain2,
        sum_mgate,
        sum_mup,
        sum_down,
    )


def solution(mesh):
    seq, chan = (mesh.shape["seq"], mesh.shape["chan"])
    chips = jax.sharding.Mesh(mesh.devices.reshape(seq, chan // 2, 2), ("seq", "zed", "core"))
    chan = ("zed", "core")
    every = ("seq", "zed", "core")
    activations = P(None, "seq", chan)
    rows, columns, vector = (P(every, None), P(None, every), P(every))
    return jax.shard_map(
        body,
        mesh=chips,
        in_specs=(activations, activations, P(chan, None), P(chan)) + (P(),) * 13,
        out_specs=(
            activations,
            activations,
            vector,
            rows,
            rows,
            columns,
            vector,
            rows,
            columns,
            vector,
            rows,
            vector,
            rows,
            rows,
            rows,
        ),
        check_vma=False,
    )
```

```python
import functools
import math

import jax
import jax.numpy as jnp
from jax import lax
from jax.experimental import pallas as pl
from jax.experimental.pallas import tpu as pltpu
from jax.sharding import PartitionSpec as P

H = 16


EPS = 1e-06
ROOT_FLOOR = 1e-06
LANES = 128
SUBLANES = 8
STEP = 16
VMEM_BYTES = 56 * 1024 * 1024
MESH = pl.DeviceIdType.MESH


def sigmoid(value):
    return 0.5 * jnp.tanh(0.5 * value) + 0.5


GELU_C = 0.7978845608
GELU_A = 0.044715


def gelu_pair(value):
    square = value * value
    inner = jnp.tanh(value * (GELU_C + (GELU_C * GELU_A) * square))
    half = 0.5 + 0.5 * inner
    slope = GELU_C + (3.0 * GELU_C * GELU_A) * square
    return (value * half, half + 0.5 * value * (1.0 - inner * inner) * slope)


def root_argument(log_decay, decay):
    y = 2.0 * log_decay
    series = 1.0 + y * (0.5 + y * (1.0 / 6.0 + y * (1.0 / 24.0)))
    return jnp.where(y > -0.05, -y * series, 1.0 - decay * decay)


def across(column, width):
    return jnp.concatenate([column] * (width // LANES), axis=1)


class Rows:
    def __init__(self, refs):
        self.refs = refs

    def __getitem__(self, index):
        if not isinstance(index, tuple):
            return self.refs[index][0]
        return self.refs[index[0]][(0,) + index[1:]]


def by_rows(refs, rows, apart):
    found = []
    for split in apart:
        count = rows if split else 1
        found.append(Rows(refs[:count]) if split else refs[0])
        refs = refs[count:]
    return found, refs


def forward_kernel(
    branch_ref,
    rim_ref,
    dist_ref,
    par_ref,
    gates_ref,
    lru_ref,
    rate_ref,
    igate_ref,
    state_ref,
    cum_ref,
    last_ref,
    both_ref,
):
    rows, length, width = branch_ref.shape
    span = 2 * STEP if rows == 1 else STEP
    taps = [par_ref[k : k + 1, :] for k in range(4)]
    conv_bias, rate_bias, input_bias, soft = (par_ref[k : k + 1, :] for k in range(4, 8))
    place = lax.broadcasted_iota(jnp.int32, (SUBLANES, width), 0)

    for row in range(rows):

        def conv_step(index, before, row=row):
            base = pl.multiple_of(index * STEP, STEP)
            pieces = []
            for half in range(STEP // SUBLANES):
                at = pl.ds(base + half * SUBLANES, SUBLANES)
                here = branch_ref[row, at, :]
                dist = across(dist_ref[row, at, :], width)
                total = conv_bias + taps[0] * here
                for k in range(1, 4):
                    shifted = pltpu.roll(jnp.where(place < SUBLANES - k, here, before), k, 0)
                    total = total + taps[k] * jnp.where(dist >= k, shifted, 0.0)
                pieces.append(total)
                before = here
            lru_ref[row, pl.ds(base, STEP), :] = jnp.concatenate(pieces, axis=0).astype(jnp.bfloat16)
            return before

        lax.fori_loop(0, length // STEP, conv_step, rim_ref[row])

        piece = min(length, 256)

        def dot_step(index, carry, row=row):
            at = pl.ds(pl.multiple_of(index * piece, piece), piece)
            both_ref[row, at, :] = jnp.dot(
                lru_ref[row, at, :], gates_ref[...], preferred_element_type=jnp.float32
            )
            return carry

        lax.fori_loop(0, length // piece, dot_step, 0)

    def scan_step(index, carry):
        base = pl.multiple_of(index * span, span)
        later = []
        for row in range(rows):
            run_cum, run_state = carry[row]
            lru_both = lru_ref[row, pl.ds(base, span), :].astype(jnp.float32)
            for half in range(span // SUBLANES):
                at = pl.ds(base + half * SUBLANES, SUBLANES)
                lru = lru_both[half * SUBLANES : (half + 1) * SUBLANES]
                start = across(dist_ref[row, at, :], width) == 0
                rate = sigmoid(both_ref[row, at, :width] + rate_bias)
                igate = sigmoid(both_ref[row, at, width:] + input_bias)
                log_decay = rate * soft
                decay = jnp.exp(log_decay)
                arg = jnp.maximum(root_argument(log_decay, decay), ROOT_FLOOR)
                root = arg * lax.rsqrt(arg)
                cum = jnp.where(start, 0.0, decay)
                value = jnp.where(start, 1.0, root) * igate * lru
                rate_ref[row, at, :] = rate
                igate_ref[row, at, :] = igate
                for shift in (1, 2, 4):
                    live = place >= shift
                    value = value + cum * jnp.where(live, pltpu.roll(value, shift, 0), 0.0)
                    cum = cum * jnp.where(live, pltpu.roll(cum, shift, 0), 1.0)
                value = value + cum * run_state
                cum = cum * run_cum
                state_ref[row, at, :] = value
                cum_ref[row, at, :] = cum
                run_state = value[SUBLANES - 1 :, :]
                run_cum = cum[SUBLANES - 1 :, :]
            later.append((run_cum, run_state))
        return tuple(later)

    one, zero = (jnp.ones((1, width), jnp.float32), jnp.zeros((1, width), jnp.float32))
    done = lax.fori_loop(0, length // span, scan_step, tuple((one, zero) for _ in range(rows)))
    for row in range(rows):
        for place in range(2):
            last_ref[row, place : place + 1, :] = done[row][place]


def carried(sent_ref, got_ref, out_ref, send_sem, recv_sem, backward):
    seq, count = (lax.axis_index("seq"), lax.axis_size("seq"))

    def other(step):
        return {"seq": lax.rem(seq + step, count)}

    barrier = pltpu.get_barrier_semaphore()
    for step in range(1, count):
        pl.semaphore_signal(barrier, inc=1, device_id=other(step), device_id_type=MESH)
    pl.semaphore_wait(barrier, count - 1)
    copies = [
        pltpu.make_async_remote_copy(
            src_ref=sent_ref,
            dst_ref=got_ref.at[seq],
            send_sem=send_sem.at[step - 1],
            recv_sem=recv_sem.at[step - 1],
            device_id=other(step),
            device_id_type=MESH,
        )
        for step in range(1, count)
    ]
    for copy in copies:
        copy.start()
    got_ref[seq] = sent_ref[...]
    for copy in copies:
        copy.wait()
    for row in range(sent_ref.shape[0]):
        total = jnp.zeros(out_ref.shape[1:], jnp.float32)
        for place in range(count - 1, 0, -1) if backward else range(count - 1):
            longer = got_ref[place, row, 0:1, :] * total + got_ref[place, row, 1:2, :]
            total = jnp.where(place > seq if backward else place < seq, longer, total)
        out_ref[row] = total


def adjoint_kernel(rows, *refs):
    (
        dres_ref,
        weight_ref,
        pre_ref,
        state_ref,
        cum_ref,
        carry_ref,
        rate_ref,
        dist_ref,
        par_ref,
    ), outs = by_rows(refs, rows, (False, False, True, True, True, False, True, False, False))
    dgate_ref, local_ref, back_ref, first_ref, dmix_ref = outs
    _, length, width = dmix_ref.shape
    for row in range(rows):
        dmix_ref[row] = lax.dot_general(
            dres_ref[row * length : (row + 1) * length, :],
            weight_ref[...],
            (((1,), (1,)), ((), ())),
            preferred_element_type=jnp.float32,
        )
    soft = par_ref[7:8, :]
    place = lax.broadcasted_iota(jnp.int32, (SUBLANES, width), 0)
    last = length // STEP - 1

    def step(index, carry):
        base = pl.multiple_of((last - index) * STEP, STEP)
        later = []
        for row in range(rows):
            run_cum, run_back = carry[row]
            entering = carry_ref[row]
            pieces = []
            for half in reversed(range(STEP // SUBLANES)):
                at = pl.ds(base + half * SUBLANES, SUBLANES)
                start = across(dist_ref[row, at, :], width) == 0
                state = state_ref[row, at, :] + cum_ref[row, at, :] * entering
                act, slope = gelu_pair(pre_ref[row, at, :])
                dmix = dmix_ref[row, at, :]
                pieces.append(dmix * state * slope)
                dstate = dmix * act
                coef = jnp.where(start, 0.0, jnp.exp(rate_ref[row, at, :] * soft))
                value = coef * dstate
                for shift in (1, 2, 4):
                    live = place < SUBLANES - shift
                    turn = SUBLANES - shift
                    value = value + coef * jnp.where(live, pltpu.roll(value, turn, 0), 0.0)
                    coef = coef * jnp.where(live, pltpu.roll(coef, turn, 0), 1.0)
                value = value + coef * run_back
                coef = coef * run_cum
                inside = place < SUBLANES - 1
                local_ref[row, at, :] = dstate + jnp.where(
                    inside, pltpu.roll(value, SUBLANES - 1, 0), run_back
                )
                back_ref[row, at, :] = jnp.where(inside, pltpu.roll(coef, SUBLANES - 1, 0), run_cum)
                run_back = value[:1, :]
                run_cum = coef[:1, :]
            dgate_ref[row, pl.ds(base, STEP), :] = jnp.concatenate(pieces[::-1], axis=0).astype(
                jnp.bfloat16
            )
            later.append((run_cum, run_back))
        return tuple(later)

    one, zero = (jnp.ones((1, width), jnp.float32), jnp.zeros((1, width), jnp.float32))
    done = lax.fori_loop(0, last + 1, step, tuple((one, zero) for _ in range(rows)))
    for row in range(rows):
        first_ref[row] = done[row][1]


def backward_kernel(head_size, rows, *refs):
    first_at = 2
    sent_ref, got_ref, send_sem, recv_sem = refs[-4:]
    leaving_ref = refs[-8]
    lasts = Rows(refs[first_at + 1 : first_at + 1 + rows])

    @pl.when(pl.program_id(0) == 0)
    def _():
        for row in range(rows):
            sent_ref[row, 0:1, :] = lasts[row, 0:1, :]
            sent_ref[row, 1:2, :] = refs[first_at][row]
        carried(sent_ref, got_ref, leaving_ref, send_sem, recv_sem, True)

    block_backward(head_size, rows, 0, leaving_ref, *refs[:-8], *refs[-7:-4])


def later_backward_kernel(head_size, rows, first, *refs):
    held = 4
    block_backward(head_size, rows, first, refs[0], *refs[1 + held :])


def block_backward(head_size, rows, first_block, leaving_ref, *refs):
    (
        local_ref,
        back_ref,
        first_ref,
        last_ref,
        state_ref,
        cum_ref,
        in_ref,
        rate_ref,
        igate_ref,
        lru_ref,
        dist_ref,
        branch_ref,
        rim_ref,
        par_ref,
        gates_ref,
    ), others = by_rows(
        refs, rows, (False,) * 3 + (True,) * 3 + (False,) + (True,) * 3 + (False,) + (True,) * 2 + (False,) * 2
    )
    dbranch_ref, tail_ref, head_ref, dgates_ref = others[:4]
    both_ref, dconv_ref, sums_ref = others[-3:]
    _, length, width = local_ref.shape
    here = pl.program_id(0) + first_block
    block = pl.ds(pl.multiple_of(here * width, width), width)
    taps = [par_ref[k : k + 1, :] for k in range(4)]
    soft = par_ref[7:8, :]
    place = lax.broadcasted_iota(jnp.int32, (SUBLANES, width), 0)
    zeros = jnp.zeros((SUBLANES, width), jnp.float32)

    def gate_step(index, carry):
        sums, earlier = carry
        decay_sum, rate_sum, input_sum = sums
        base = pl.multiple_of(index * STEP, STEP)
        later = []
        for row in range(rows):
            before = earlier[row]
            entering = in_ref[row]
            leaving = leaving_ref[row, :, block]
            lru_both = lru_ref[row, pl.ds(base, STEP), :].astype(jnp.float32)
            drates, dinputs = ([], [])
            for half in range(STEP // SUBLANES):
                at = pl.ds(base + half * SUBLANES, SUBLANES)
                lru = lru_both[half * SUBLANES : (half + 1) * SUBLANES]
                start = across(dist_ref[row, at, :], width) == 0
                adjoint = local_ref[row, at, :] + back_ref[row, at, :] * leaving
                state = state_ref[row, at, :] + cum_ref[row, at, :] * entering
                previous = jnp.where(place < 1, before, pltpu.roll(state, 1, 0))
                before = state[SUBLANES - 1 :, :]
                rate = rate_ref[row, at, :]
                igate = igate_ref[row, at, :]
                log_decay = rate * soft
                decay = jnp.exp(log_decay)
                arg = root_argument(log_decay, decay)
                above = arg > ROOT_FLOOR
                arg = jnp.maximum(arg, ROOT_FLOOR)
                inverse = lax.rsqrt(arg)
                scale = jnp.where(start, 1.0, arg * inverse)
                gated = adjoint * igate
                dscale = gated * lru
                pull = jnp.where(above, dscale * decay * decay * inverse, 0.0)
                dlog = jnp.where(start, 0.0, adjoint * previous * decay - pull)
                dig = adjoint * scale * lru
                weighted = dlog * rate
                decay_sum = decay_sum + weighted
                drates.append(weighted * soft * (1.0 - rate))
                dinputs.append(dig * igate * (1.0 - igate))
                dconv_ref[row, at, :] = gated * scale
            drate = jnp.concatenate(drates, axis=0).astype(jnp.bfloat16)
            dinput = jnp.concatenate(dinputs, axis=0).astype(jnp.bfloat16)
            both_ref[row, pl.ds(base, STEP), :width] = drate
            both_ref[row, pl.ds(base, STEP), width:] = dinput
            drate = drate.astype(jnp.float32)
            dinput = dinput.astype(jnp.float32)
            rate_sum = rate_sum + (drate[:SUBLANES] + drate[SUBLANES:])
            input_sum = input_sum + (dinput[:SUBLANES] + dinput[SUBLANES:])
            later.append(before)
        return ((decay_sum, rate_sum, input_sum), tuple(later))

    sums, _ = lax.fori_loop(
        0,
        length // STEP,
        gate_step,
        ((zeros, zeros, zeros), tuple(in_ref[row] for row in range(rows))),
    )
    for slot, total in zip((5, 6, 7), (sums[1], sums[2], sums[0] * par_ref[8:9, :])):
        sums_ref[slot : slot + 1, :] = jnp.sum(total, axis=0, keepdims=True)

    piece = min(length, 256)
    wide = None
    for row in range(rows):

        def dot_step(index, carry, row=row):
            at = pl.ds(pl.multiple_of(index * piece, piece), piece)
            dconv_ref[row, at, :] += lax.dot_general(
                both_ref[row, at, :],
                gates_ref[...],
                (((1,), (1,)), ((), ())),
                preferred_element_type=jnp.float32,
            )
            return carry

        lax.fori_loop(0, length // piece, dot_step, 0)
        part = lax.dot_general(
            lru_ref[row], both_ref[row], (((0,), (0,)), ((), ())), preferred_element_type=jnp.float32
        )
        wide = part if wide is None else wide + part
    row_head = lax.broadcasted_iota(jnp.int32, (width, width), 0) // head_size
    col_head = lax.broadcasted_iota(jnp.int32, (width, width), 1) // head_size
    own = row_head == col_head
    folds = []
    for part in range(2):
        kept = jnp.where(own, wide[:, part * width : (part + 1) * width], 0.0)
        folded = kept
        for other in range(1, width // head_size):
            folded = folded + pltpu.roll(kept, width - other * head_size, 1)
        folds.append(folded[:, :LANES])

    def conv_step(index, carry):
        sums, following = carry
        sums = list(sums)
        base = pl.multiple_of((length // STEP - 1 - index) * STEP, STEP)
        later = []
        for row in range(rows):
            after = following[row]
            pieces = []
            for half in reversed(range(STEP // SUBLANES)):
                at = pl.ds(base + half * SUBLANES, SUBLANES)
                dist = across(dist_ref[row, at, :], width)
                branch = branch_ref[row, at, :]
                here = dconv_ref[row, at, :]
                total = taps[0] * here
                sums[0] = sums[0] + here * branch
                sums[4] = sums[4] + here
                masked = tuple(jnp.where(dist >= k, here, 0.0) for k in range(1, 4))
                for k in range(1, 4):
                    moved = pltpu.roll(
                        jnp.where(place >= k, masked[k - 1], after[k - 1]), SUBLANES - k, 0
                    )
                    total = total + taps[k] * moved
                    sums[k] = sums[k] + branch * moved
                after = masked
                pieces.append(total)
            whole = jnp.concatenate(pieces[::-1], axis=0)
            dbranch_ref[row, pl.ds(base, STEP), :] = whole.astype(jnp.bfloat16)
            later.append(after)

            @pl.when(index == 0)
            def _(row=row, whole=whole):
                tail_ref[row] = whole[STEP - SUBLANES :]

        return (tuple(sums), tuple(later))

    sums, firsts = lax.fori_loop(
        0,
        length // STEP,
        conv_step,
        ((zeros,) * 5, tuple((zeros,) * 3 for _ in range(rows))),
    )
    sums = list(sums)
    for row in range(rows):
        total = zeros
        rim = rim_ref[row]
        for k in range(1, 4):
            moved = pltpu.roll(jnp.where(place >= k, 0.0, firsts[row][k - 1]), SUBLANES - k, 0)
            total = total + taps[k] * moved
            sums[k] = sums[k] + rim * moved
        head_ref[row] = total
    for slot in range(5):
        sums_ref[slot : slot + 1, :] = jnp.sum(sums[slot], axis=0, keepdims=True)
    above = jnp.zeros((head_size, width), jnp.float32)
    below = jnp.zeros((LANES - head_size - SUBLANES, width), jnp.float32)
    turned = jnp.concatenate([above, sums_ref[...], below], axis=0).T
    lane = lax.broadcasted_iota(jnp.int32, (width, LANES), 1)
    dgates_ref[:, :LANES] = jnp.where(lane < head_size, folds[0], turned).astype(dgates_ref.dtype)
    dgates_ref[:, LANES:] = folds[1].astype(dgates_ref.dtype)


def channel_call(
    kernel, name, arrays, specs, outs, out_specs, scratch, blocks, flops, params=()
):
    moved = sum(math.prod(a.shape) * a.dtype.itemsize for a in (*arrays, *outs))
    return pl.pallas_call(
        kernel,
        name=name,
        grid=(blocks,),
        in_specs=specs,
        out_specs=out_specs,
        out_shape=outs,
        scratch_shapes=scratch,
        compiler_params=pltpu.CompilerParams(vmem_limit_bytes=VMEM_BYTES, **dict(params)),
        cost_estimate=pl.CostEstimate(flops=flops, bytes_accessed=moved, transcendentals=0),
    )(*arrays)


class Recurrence:
    def __init__(self, rows, length, channels, head_size):
        self.rows, self.length, self.channels = (rows, length, channels)
        self.head_size = head_size
        self.width = head_size * LANES // math.gcd(head_size, LANES)
        self.blocks = channels // self.width
        self.flops = 2 * rows * length * channels * 2 * self.width

    def tall(self):
        return pl.BlockSpec((self.rows, self.length, self.width), lambda j: (0, 0, j))

    def short(self, size):
        return pl.BlockSpec((self.rows, size, self.width), lambda j: (0, 0, j))

    def apart(self, size):
        return [pl.BlockSpec((1, size, self.width), lambda j: (0, 0, j))] * self.rows

    def whole(self, rows, size):
        return pl.BlockSpec((rows, size, self.channels), lambda j: (0, 0, 0))

    def flat(self, size):
        return pl.BlockSpec((size, self.width), lambda j: (0, j))

    def dist(self):
        return pl.BlockSpec((self.rows, self.length, LANES), lambda j: (0, 0, 0))

    def gates(self, columns):
        return pl.BlockSpec((self.width, columns), lambda j: (j, 0))

    def shape(self, size, dtype):
        return jax.ShapeDtypeStruct((self.rows, size, self.channels), dtype)

    def widen(self, lru_gates):
        size, width = (self.head_size, self.width)
        heads = width // size
        column = jnp.arange(2 * width)
        source = (column // width) * size + column % size
        spread = (jnp.arange(2 * size)[:, None] == source[None, :]).astype(jnp.bfloat16)
        owner = (column % width) // size
        mine = (jnp.arange(self.channels) // size) % heads
        wide = jnp.dot(lru_gates, spread, preferred_element_type=jnp.float32)
        return jnp.where(mine[:, None] == owner[None, :], wide, 0.0).astype(jnp.bfloat16)

    def forward(self, branch, rim, dist, params, gates):
        f32 = jnp.float32
        outs = [self.shape(self.length, d) for d in (jnp.bfloat16, f32, f32, f32, f32)]
        return channel_call(
            forward_kernel,
            "recurrence_forward",
            (branch, rim, dist, params, gates),
            [self.tall(), self.short(SUBLANES), self.dist(), self.flat(16), self.gates(2 * self.width)],
            outs + [self.shape(2, f32)],
            [self.tall()] * 5 + [self.short(2)],
            [pltpu.VMEM((self.rows, self.length, 2 * self.width), f32)],
            self.blocks,
            self.flops,
        )

    def adjoint(self, dres, weight, pre, state, cum, entering, rate, dist, params):
        f32 = jnp.float32
        outs = [self.shape(self.length, d) for d in (jnp.bfloat16, f32, f32)] + [self.shape(1, f32)]
        tall, apart = (self.tall(), self.apart(self.length))
        return channel_call(
            functools.partial(adjoint_kernel, self.rows),
            "recurrence_adjoint",
            (dres, weight, *pre, *state, *cum, entering, *rate, dist, params),
            [
                pl.BlockSpec(dres.shape, lambda j: (0, 0)),
                self.gates(weight.shape[1]),
                *apart * 3,
                self.short(1),
                *apart,
                self.dist(),
                self.flat(16),
            ],
            outs,
            [tall, tall, tall, self.short(1)],
            [pltpu.VMEM((self.rows, self.length, self.width), f32)],
            self.blocks,
            2 * self.rows * self.length * weight.size,
        )

    def backward(
        self, local, back, first, last, state, cum, entering, rate, igate, lru, dist, branch, rim, params, gates, between_calls
    ):
        f32 = jnp.float32
        outs = [
            self.shape(self.length, jnp.bfloat16),
            self.shape(SUBLANES, f32),
            self.shape(SUBLANES, f32),
            jax.ShapeDtypeStruct((self.channels, 2 * LANES), jnp.bfloat16),
        ]
        seqs = lax.axis_size("seq")
        summary = (self.rows, 2, self.channels)
        arrays = (local, back, first, *last, *state, *cum, entering, *rate, *igate, *lru, dist, *branch, *rim)
        arrays += (params, gates)
        early = self.blocks - 1
        scratch = [
            pltpu.VMEM((self.rows, self.length, 2 * self.width), jnp.bfloat16),
            pltpu.VMEM((self.rows, self.length, self.width), f32),
            pltpu.VMEM((SUBLANES, self.width), f32),
        ]

        def specs(offset):
            rows, width = (self.rows, self.width)

            def wide(rows, size):
                return pl.BlockSpec((rows, size, width), lambda j: (0, 0, j + offset))

            def flat(size):
                return pl.BlockSpec((size, width), lambda j: (0, j + offset))

            def tall(columns):
                return pl.BlockSpec((width, columns), lambda j: (j + offset, 0))

            whole, apart = (wide(rows, self.length), [wide(1, self.length)] * rows)
            given = [whole, whole, self.whole(rows, 1), *[self.whole(1, 2)] * rows, *apart * 2]
            given += [wide(rows, 1), *apart * 3, self.dist(), *apart, *[wide(1, SUBLANES)] * rows]
            given += [flat(16), tall(2 * width)]
            made = [whole, wide(rows, SUBLANES), wide(rows, SUBLANES), tall(2 * LANES)]
            return (given, made)

        given, made = specs(0)
        *found, leaving = channel_call(
            functools.partial(backward_kernel, self.head_size, self.rows),
            "recurrence_backward",
            arrays,
            given,
            outs + [self.shape(1, f32)],
            made + [self.whole(self.rows, 1)],
            scratch
            + [
                pltpu.VMEM(summary, f32),
                pltpu.VMEM((seqs,) + summary, f32),
                pltpu.SemaphoreType.DMA((seqs - 1,)),
                pltpu.SemaphoreType.DMA((seqs - 1,)),
            ],
            early,
            2 * self.flops,
            {"collective_id": 5, "has_side_effects": True},
        )
        between, leaving = between_calls(leaving)
        given, made = specs(early)
        done = pl.pallas_call(
            functools.partial(later_backward_kernel, self.head_size, self.rows, early),
            name="recurrence_backward_end",
            grid=(self.blocks - early,),
            in_specs=[self.whole(self.rows, 1)] + [pl.BlockSpec(memory_space=pl.ANY)] * 4 + given,
            out_specs=made,
            out_shape=outs,
            scratch_shapes=scratch,
            input_output_aliases={1 + k: k for k in range(4)},
            compiler_params=pltpu.CompilerParams(vmem_limit_bytes=VMEM_BYTES),
            cost_estimate=pl.CostEstimate(
                flops=self.flops // 2, bytes_accessed=16 * self.flops // self.width, transcendentals=0
            ),
        )(leaving, *found, *arrays)
        return (*done, between)


def gathered(parts_ref, at):
    return jnp.concatenate([parts_ref[k, at, :] for k in range(parts_ref.shape[0])], axis=1)


def front_kernel(
    parts_ref,
    gain_ref,
    input_ref,
    gate_ref,
    x_ref,
    inverse_ref,
    normed_ref,
    branch_ref,
    pre_ref,
    rim_ref,
    edge_ref,
    landed_ref,
    send_sem,
    recv_sem,
):
    tokens = x_ref.shape[0]
    piece, tall = (64, min(tokens, 512))
    step, steps = (pl.program_id(0), edge_ref.shape[0])
    seq, seqs = (lax.axis_index("seq"), lax.axis_size("seq"))
    barrier = pltpu.get_barrier_semaphore()

    @pl.when(step == 0)
    def _():
        before = {"seq": lax.rem(seq + seqs - 1, seqs)}
        pl.semaphore_signal(barrier, inc=1, device_id=before, device_id_type=MESH)

        def norm(index, carry):
            at = pl.ds(pl.multiple_of(index * piece, piece), piece)
            low = gathered(parts_ref, at)
            x_ref[at, :] = low
            value = low.astype(jnp.float32)
            inverse = lax.rsqrt(jnp.mean(value * value, axis=1, keepdims=True) + EPS)
            inverse_ref[at, :] = jnp.broadcast_to(inverse, (piece, LANES))
            normed_ref[at, :] = (value * inverse * gain_ref[...]).astype(jnp.bfloat16)
            return carry

        lax.fori_loop(0, tokens // piece, norm, 0, unroll=2)

    ending = jnp.dot(
        normed_ref[tokens - STEP :, :], input_ref[...], preferred_element_type=jnp.float32
    )
    edge_ref[step] = ending[STEP - SUBLANES :, :]

    def rim_copy(place):
        return pltpu.make_async_remote_copy(
            src_ref=edge_ref.at[place],
            dst_ref=landed_ref.at[place],
            send_sem=send_sem.at[place],
            recv_sem=recv_sem.at[place],
            device_id={"seq": lax.rem(seq + 1, seqs)},
            device_id_type=MESH,
        )

    @pl.when(step == 0)
    def _():
        pl.semaphore_wait(barrier, 1)

    rim_copy(step).start()

    def multiply(index, carry):
        at = pl.ds(pl.multiple_of(index * tall, tall), tall)
        normed = normed_ref[at, :]
        branch_ref[at, :] = jnp.dot(normed, input_ref[...], preferred_element_type=jnp.float32)
        pre_ref[at, :] = jnp.dot(normed, gate_ref[...], preferred_element_type=jnp.float32)
        return carry

    lax.fori_loop(0, tokens // tall, multiply, 0)

    @pl.when(step == steps - 1)
    def _():
        columns = edge_ref.shape[2]
        live = jnp.where(seq > 0, 1.0, 0.0)
        for place in range(steps):
            rim_copy(place).wait()
            rim_ref[:, place * columns : (place + 1) * columns] = live * landed_ref[place]


def front(parts, gain, recur_input, recur_gate):
    count, tokens, width = parts.shape
    model, rec = recur_input.shape
    columns = 4 * LANES
    steps = rec // columns
    low, f32 = (jnp.bfloat16, jnp.float32)
    tall = pl.BlockSpec((model, columns), lambda j: (0, j))
    wide = pl.BlockSpec((tokens, columns), lambda j: (0, j))

    def whole(shape):
        return pl.BlockSpec(shape, lambda j: (0,) * len(shape))

    return pl.pallas_call(
        front_kernel,
        name="norm_and_project",
        grid=(steps,),
        in_specs=[whole(parts.shape), whole((1, model)), tall, tall],
        out_specs=[whole((tokens, model)), whole((tokens, LANES)), whole((tokens, model)), wide, wide]
        + [whole((SUBLANES, rec))],
        out_shape=[
            jax.ShapeDtypeStruct((tokens, model), low),
            jax.ShapeDtypeStruct((tokens, LANES), f32),
            jax.ShapeDtypeStruct((tokens, model), low),
            jax.ShapeDtypeStruct((tokens, rec), f32),
            jax.ShapeDtypeStruct((tokens, rec), f32),
            jax.ShapeDtypeStruct((SUBLANES, rec), f32),
        ],
        scratch_shapes=[
            pltpu.VMEM((steps, SUBLANES, columns), f32),
            pltpu.VMEM((steps, SUBLANES, columns), f32),
            pltpu.SemaphoreType.DMA((steps,)),
            pltpu.SemaphoreType.DMA((steps,)),
        ],
        compiler_params=pltpu.CompilerParams(
            collective_id=3, has_side_effects=True, vmem_limit_bytes=VMEM_BYTES
        ),
        cost_estimate=pl.CostEstimate(
            flops=4 * tokens * model * rec, bytes_accessed=20 * tokens * model, transcendentals=0
        ),
    )(parts, gain[None], recur_input, recur_gate)


def middle_kernel(rows, *refs):
    (last_ref, state_hbm, cum_hbm, pre_hbm, x_ref, out_ref, gain_ref), others = by_rows(
        refs, rows, (True,) * 5 + (False,) * 2
    )
    entering_ref, mixed_ref, resid_ref, normed_ref = others[:4]
    sent_ref, got_ref, held_ref, send_sem, recv_sem, load_sem = others[4:]
    tall, model = resid_ref.shape
    step, steps = (pl.program_id(0), pl.num_programs(0))
    tiles = steps // rows
    slab = 16

    def on_row(place, act):
        for row in range(rows):

            @pl.when(lax.div(place, tiles) == row)
            def _(row=row):
                at = pl.ds(pl.multiple_of(lax.rem(place, tiles) * tall, tall), tall)
                slot = lax.rem(place, 2)
                for kind, source in enumerate((state_hbm, cum_hbm, pre_hbm)):
                    act(
                        pltpu.make_async_copy(
                            source.refs[row].at[0, at], held_ref.at[slot, kind], load_sem.at[slot, kind]
                        )
                    )

    @pl.when(step == 0)
    def _():
        on_row(step, lambda copy: copy.start())
        for row in range(rows):
            sent_ref[row] = last_ref[row]
        carried(sent_ref, got_ref, entering_ref, send_sem, recv_sem, False)

    @pl.when(step + 1 < steps)
    def _():
        on_row(step + 1, lambda copy: copy.start())

    on_row(step, lambda copy: copy.wait())
    slot = lax.rem(step, 2)
    mine = lax.div(step, tiles)

    def mix(index, carry):
        at = pl.ds(pl.multiple_of(index * slab, slab), slab)
        state = held_ref[slot, 0, at, :] + held_ref[slot, 1, at, :] * entering_ref[mine]
        pre = held_ref[slot, 2, at, :]
        inner = jnp.tanh(pre * (GELU_C + (GELU_C * GELU_A) * (pre * pre)))
        mixed_ref[at, :] = (state * (pre * (0.5 + 0.5 * inner))).astype(jnp.bfloat16)
        return carry

    lax.fori_loop(0, tall // slab, mix, 0, unroll=2)
    for row in range(rows):

        @pl.when(mine == row)
        def _(row=row):
            tile = 512
            for first in range(0, model, tile):
                at = slice(first, first + tile)
                resid_ref[:, at] = x_ref.refs[row][:, at].astype(jnp.float32) + jnp.dot(
                    mixed_ref[...], out_ref[:, at], preferred_element_type=jnp.float32
                )

    def norm(index, carry):
        at = pl.ds(pl.multiple_of(index * slab, slab), slab)
        resid = resid_ref[at, :]
        inverse = lax.rsqrt(jnp.mean(resid * resid, axis=1, keepdims=True) + EPS)
        normed_ref[at, :] = (resid * inverse * gain_ref[...]).astype(jnp.bfloat16)
        return carry

    lax.fori_loop(0, tall // slab, norm, 0, unroll=4)


def middle(last, state, cum, pre, x, recur_out, gain):
    rows = len(state)
    _, length, rec = state[0].shape
    model = recur_out.shape[1]
    tall = min(length, 256)
    tiles = length // tall
    tokens = rows * length
    seqs = lax.axis_size("seq")
    low, f32 = (jnp.bfloat16, jnp.float32)

    def whole(shape):
        return pl.BlockSpec(shape, lambda s: (0,) * len(shape), pipeline_mode=pl.Buffered(1))

    def flat(row):
        return lambda s: (jnp.clip(s - row * tiles, 0, tiles - 1), 0)

    summary = (rows, 2, rec)
    return pl.pallas_call(
        functools.partial(middle_kernel, rows),
        name="mix_and_norm",
        grid=(rows * tiles,),
        in_specs=[whole((1, 2, rec))] * rows
        + [pl.BlockSpec(memory_space=pl.ANY)] * (3 * rows)
        + [pl.BlockSpec((tall, model), flat(row)) for row in range(rows)]
        + [whole(recur_out.shape), whole((1, model))],
        out_specs=[
            pl.BlockSpec((rows, 1, rec), lambda s: (0, 0, 0)),
            pl.BlockSpec((tall, rec), lambda s: (s, 0)),
            pl.BlockSpec((tall, model), lambda s: (s, 0)),
            pl.BlockSpec((tall, model), lambda s: (s, 0)),
        ],
        out_shape=[
            jax.ShapeDtypeStruct((rows, 1, rec), f32),
            jax.ShapeDtypeStruct((tokens, rec), low),
            jax.ShapeDtypeStruct((tokens, model), f32),
            jax.ShapeDtypeStruct((tokens, model), low),
        ],
        scratch_shapes=[
            pltpu.VMEM(summary, f32),
            pltpu.VMEM((seqs,) + summary, f32),
            pltpu.VMEM((2, 3, tall, rec), f32),
            pltpu.SemaphoreType.DMA((seqs - 1,)),
            pltpu.SemaphoreType.DMA((seqs - 1,)),
            pltpu.SemaphoreType.DMA((2, 3)),
        ],
        compiler_params=pltpu.CompilerParams(
            collective_id=4, has_side_effects=True, vmem_limit_bytes=VMEM_BYTES
        ),
        cost_estimate=pl.CostEstimate(
            flops=2 * tokens * rec * model, bytes_accessed=14 * tokens * rec, transcendentals=0
        ),
    )(*last, *state, *cum, *pre, *x, recur_out, gain[None])


def hidden_kernel(
    left_ref,
    parts_ref,
    normed_ref,
    gate_ref,
    up_ref,
    down_ref,
    gout_ref,
    hidden_ref,
    dgate_ref,
    dup_ref,
):
    tokens, model = normed_ref.shape
    chunk = down_ref.shape[0]
    rows = left_ref.shape[0]
    length = tokens // rows
    slab = 32

    @pl.when(pl.program_id(0) == 0)
    def _():
        for row in range(rows):

            def collect(index, carry, row=row):
                base = pl.multiple_of(index * slab, slab)
                at = pl.ds(row * length + base, slab)
                low = gathered(parts_ref, at)
                place = base + lax.broadcasted_iota(jnp.int32, low.shape, 0)
                value = jnp.where(place < left_ref[row], low.astype(jnp.float32), 0.0)
                gout_ref[at, :] = value.astype(jnp.bfloat16)
                return carry

            lax.fori_loop(0, length // slab, collect, 0)

    tall = min(tokens, 512)
    wide = 256

    def tile(index, carry):
        at = pl.ds(pl.multiple_of(index * tall, tall), tall)
        for column in range(chunk // wide):
            own = slice(column * wide, (column + 1) * wide)
            gate = jnp.dot(normed_ref[at, :], gate_ref[:, own], preferred_element_type=jnp.float32)
            up = jnp.dot(normed_ref[at, :], up_ref[:, own], preferred_element_type=jnp.float32)
            dhid = lax.dot_general(
                gout_ref[at, :],
                down_ref[own, :],
                (((1,), (1,)), ((), ())),
                preferred_element_type=jnp.float32,
            )
            act, slope = gelu_pair(gate)
            hidden_ref[at, own] = (act * up).astype(jnp.bfloat16)
            dgate_ref[at, own] = (dhid * up * slope).astype(jnp.bfloat16)
            dup_ref[at, own] = (dhid * act).astype(jnp.bfloat16)
        return carry

    lax.fori_loop(0, tokens // tall, tile, 0)


def back_kernel(
    hidden_ref,
    dgate_ref,
    dup_ref,
    gout_hbm,
    resid_hbm,
    gain_ref,
    gate_ref,
    up_ref,
    down_ref,
    result_ref,
    dres_ref,
    total_ref,
    back_ref,
    gout_ref,
    resid_ref,
    load_sem,
):
    tall, model = (hidden_ref.shape[0], gout_ref.shape[1])
    step, tile = (pl.program_id(0), pl.program_id(1))
    wide = 512
    contract = (((1,), (1,)), ((), ()))
    rows = pl.ds(pl.multiple_of(tile * tall, tall), tall)

    def loads():
        return (
            pltpu.make_async_copy(gout_hbm, gout_ref, load_sem.at[0]),
            pltpu.make_async_copy(resid_hbm, resid_ref, load_sem.at[1]),
        )

    @pl.when((step == 0) & (tile == 0))
    def _():
        for load in loads():
            load.start()

    def products(own):
        forth = jnp.dot(hidden_ref[...], down_ref[:, own], preferred_element_type=jnp.float32)
        back = lax.dot_general(
            dgate_ref[...], gate_ref[own, :], contract, preferred_element_type=jnp.float32
        ) + lax.dot_general(
            dup_ref[...], up_ref[own, :], contract, preferred_element_type=jnp.float32
        )
        return (forth, back)

    @pl.when(step == 0)
    def _():
        for first in range(0, model, wide):
            own = slice(first, first + wide)
            forth, back = products(own)
            total_ref[rows, own] = forth
            back_ref[rows, own] = back

    @pl.when(step > 0)
    def _():
        for first in range(0, model, wide):
            own = slice(first, first + wide)
            forth, back = products(own)
            total_ref[rows, own] += forth
            back_ref[rows, own] += back

    @pl.when((step == pl.num_programs(0) - 1) & (tile == 0))
    def _():
        for load in loads():
            load.wait()

    @pl.when(step == pl.num_programs(0) - 1)
    def _():
        parts, width = (result_ref.shape[0], result_ref.shape[2])
        small = 16

        def finish(index, carry):
            at = pl.ds(pl.multiple_of(tile * tall + index * small, small), small)
            resid = resid_ref[at, :]
            result = (resid + total_ref[at, :]).astype(jnp.bfloat16)
            for part in range(parts):
                result_ref[part, at, :] = result[:, part * width : (part + 1) * width]
            inverse = lax.rsqrt(jnp.mean(resid * resid, axis=1, keepdims=True) + EPS)
            normed = resid * inverse
            scaled = back_ref[at, :] * gain_ref[...]
            mean = jnp.mean(scaled * normed, axis=1, keepdims=True)
            dres = gout_ref[at, :].astype(jnp.float32) + inverse * (scaled - normed * mean)
            dres_ref[at, :] = dres.astype(jnp.bfloat16)
            return carry

        lax.fori_loop(0, tall // small, finish, 0, unroll=4)


MLP_CHUNK = 768


def resident(shape):
    return pl.BlockSpec(shape, lambda s: (0,) * len(shape), pipeline_mode=pl.Buffered(1))


def mlp_specs(tokens, model):
    columns = pl.BlockSpec((model, MLP_CHUNK), lambda s: (0, s))
    down = pl.BlockSpec((MLP_CHUNK, model), lambda s: (s, 0))
    made = pl.BlockSpec((tokens, MLP_CHUNK), lambda s: (0, s))
    return ([columns, columns, down], [made] * 3)


def mlp_hidden(left, parts, normed, mlp_gate, mlp_up, mlp_down):
    tokens, model = normed.shape
    ffn = mlp_gate.shape[1]
    low = jnp.bfloat16
    weights, made = mlp_specs(tokens, model)
    tall = jax.ShapeDtypeStruct((tokens, ffn), low)
    return pl.pallas_call(
        hidden_kernel,
        name="mlp_hidden",
        grid=(ffn // MLP_CHUNK,),
        in_specs=[
            pl.BlockSpec(memory_space=pltpu.SMEM),
            resident(parts.shape),
            resident(normed.shape),
            *weights,
        ],
        out_specs=[resident((tokens, model)), *made],
        out_shape=[jax.ShapeDtypeStruct((tokens, model), low), tall, tall, tall],
        compiler_params=pltpu.CompilerParams(vmem_limit_bytes=VMEM_BYTES),
        cost_estimate=pl.CostEstimate(
            flops=6 * tokens * model * ffn,
            bytes_accessed=6 * (model + tokens) * ffn + 6 * tokens * model,
            transcendentals=0,
        ),
    )(left, parts, normed, mlp_gate, mlp_up, mlp_down)


def mlp_back(hidden, dgate, dup, gout, resid, gain, mlp_gate, mlp_up, mlp_down, parts_shape):
    tokens, model = resid.shape
    ffn = mlp_gate.shape[1]
    low, f32 = (jnp.bfloat16, jnp.float32)
    chunk, tall = (1024, min(tokens, 512))

    def resident(shape):
        return pl.BlockSpec(shape, lambda s, t: (0,) * len(shape), pipeline_mode=pl.Buffered(1))

    columns = pl.BlockSpec((model, chunk), lambda s, t: (0, s))
    down = pl.BlockSpec((chunk, model), lambda s, t: (s, 0))
    made = pl.BlockSpec((tall, chunk), lambda s, t: (t, s))
    return pl.pallas_call(
        back_kernel,
        name="mlp_back",
        grid=(ffn // chunk, tokens // tall),
        in_specs=[
            made,
            made,
            made,
            pl.BlockSpec(memory_space=pl.ANY),
            pl.BlockSpec(memory_space=pl.ANY),
            resident((1, model)),
            columns,
            columns,
            down,
        ],
        out_specs=[resident(parts_shape), resident((tokens, model))],
        out_shape=[
            jax.ShapeDtypeStruct(parts_shape, low),
            jax.ShapeDtypeStruct((tokens, model), low),
        ],
        scratch_shapes=[
            pltpu.VMEM((tokens, model), f32),
            pltpu.VMEM((tokens, model), f32),
            pltpu.VMEM((tokens, model), low),
            pltpu.VMEM((tokens, model), f32),
            pltpu.SemaphoreType.DMA((2,)),
        ],
        compiler_params=pltpu.CompilerParams(vmem_limit_bytes=VMEM_BYTES),
        cost_estimate=pl.CostEstimate(
            flops=6 * tokens * model * ffn,
            bytes_accessed=6 * (model + tokens) * ffn + 10 * tokens * model,
            transcendentals=0,
        ),
    )(hidden, dgate, dup, gout, resid, gain[None], mlp_gate, mlp_up, mlp_down)


def outputs_kernel(
    device_ref,
    own_ref,
    gate_sum,
    in_sum,
    out_sum,
    small_ref,
    input_ref,
    gate_ref,
    mlp_gate_ref,
    mlp_up_ref,
    gain1_ref,
    gain2_ref,
    sum_gain1,
    sum_in,
    sum_gate,
    sum_taps,
    sum_bias,
    sum_lgates,
    sum_lbias,
    sum_decay,
    sum_out,
    sum_gain2,
    sum_mgate,
    sum_mup,
    sum_down,
):
    rows = sum_mgate.shape[0]
    model = own_ref.shape[1]
    parts = sum_mgate.shape[1] // model
    for part in range(parts):
        at = slice(part * model, (part + 1) * model)
        sum_mgate[:, at] = own_ref[part * rows : (part + 1) * rows, :].astype(jnp.float32)
        sum_mup[:, at] = own_ref[(parts + part) * rows : (parts + part + 1) * rows, :].astype(
            jnp.float32
        )
    sum_down[...] = own_ref[2 * parts * rows :, :].astype(jnp.float32)

    def weighed(*pairs):
        return sum(
            jnp.sum(weight[...].astype(jnp.float32) * gradient[...], axis=1, keepdims=True)
            for weight, gradient in pairs
        )

    def as_row(column, gain):
        lane = lax.broadcasted_iota(jnp.int32, (rows, LANES), 1)
        place = lax.broadcasted_iota(jnp.int32, (rows, LANES), 0)
        whole = lax.broadcasted_iota(jnp.int32, (rows, model), 1)
        own = device_ref[0] * rows + lax.broadcasted_iota(jnp.int32, (rows, model), 0)
        own_gain = jnp.sum(jnp.where(whole == own, gain[...], 0.0), axis=1, keepdims=True)
        return jnp.sum(jnp.where(lane == place, column / own_gain, 0.0), axis=0, keepdims=True)

    row1 = as_row(weighed((input_ref, in_sum), (gate_ref, gate_sum)), gain1_ref)
    row2 = as_row(weighed((mlp_gate_ref, sum_mgate), (mlp_up_ref, sum_mup)), gain2_ref)
    sum_gain1[...] = row1[:, :rows]
    sum_gain2[...] = row2[:, :rows]
    sum_in[...] = in_sum[...]
    sum_gate[...] = gate_sum[...]
    sum_out[...] = out_sum[...]
    channels = small_ref.shape[0]
    size = sum_lgates.shape[1] // 2
    first, second = (small_ref[:, :LANES], small_ref[:, LANES:])
    lane = lax.broadcasted_iota(jnp.int32, (channels, LANES), 1)
    moved = pltpu.roll(second, size, 1)
    sum_lgates[:, :LANES] = jnp.where(lane < size, first, moved)
    sum_lgates[:, LANES:] = moved[:, : 2 * size - LANES]
    filled = jnp.concatenate([first, jnp.zeros((LANES - channels, LANES), jnp.float32)], axis=0)
    turned = filled.T
    sum_taps[...] = turned[size : size + 4, :channels]
    sum_bias[...] = turned[size + 4 : size + 5, :channels]
    sum_lbias[...] = turned[size + 5 : size + 7, :channels]
    sum_decay[...] = turned[size + 7 : size + 8, :channels]


def outputs(
    device, own, gate_sum, in_sum, out_sum, small, recur_input, recur_gate, mlp_gate, mlp_up, gain1, gain2, size
):
    rows, rec = in_sum.shape
    model, ffn = mlp_gate.shape
    channels = small.shape[0]
    f32 = jnp.float32

    def whole(shape):
        return pl.BlockSpec(shape, lambda s, device: (0,) * len(shape))

    def mine(shape):
        return pl.BlockSpec(shape, lambda s, device: (device[0], 0))

    given = (own, gate_sum, in_sum, out_sum, small)
    shapes = [(1, rows), (rows, rec), (rows, rec), (4, channels), (1, channels)]
    shapes += [(channels, 2 * size), (2, channels), (1, channels), out_sum.shape, (1, rows)]
    shapes += [(rows, ffn), (rows, ffn), (own.shape[0] - 2 * ffn // model * rows, model)]
    return pl.pallas_call(
        outputs_kernel,
        name="outputs",
        grid_spec=pltpu.PrefetchScalarGridSpec(
            num_scalar_prefetch=1,
            grid=(1,),
            in_specs=[whole(a.shape) for a in given]
            + [mine((rows, rec))] * 2
            + [mine((rows, ffn))] * 2
            + [whole((1, model))] * 2,
            out_specs=[whole(shape) for shape in shapes],
        ),
        out_shape=[jax.ShapeDtypeStruct(shape, f32) for shape in shapes],
        compiler_params=pltpu.CompilerParams(vmem_limit_bytes=VMEM_BYTES),
    )(
        device[None],
        *given,
        recur_input,
        recur_gate,
        mlp_gate,
        mlp_up,
        gain1[None],
        gain2[None],
    )


def spread_kernel(whole_ref, out_ref):
    out_ref[0] = whole_ref[...]


def spread(whole, count):
    tokens, width = (whole.shape[0], whole.shape[1] // count)
    return pl.pallas_call(
        spread_kernel,
        name="spread_features",
        grid=(count,),
        in_specs=[pl.BlockSpec((tokens, width), lambda j: (0, j))],
        out_specs=pl.BlockSpec((1, tokens, width), lambda j: (j, 0, 0)),
        out_shape=jax.ShapeDtypeStruct((count, tokens, width), whole.dtype),
        cost_estimate=pl.CostEstimate(
            flops=0, bytes_accessed=4 * tokens * whole.shape[1], transcendentals=0
        ),
    )(whole)


CHAN = ("zed", "core")


def features_in(local, pick=slice(None)):
    count = lax.axis_size(CHAN)
    rows, length, width = local.shape
    local = local.reshape(count, rows // count, length, width)[:, pick]
    if width % LANES == 0:
        return lax.all_to_all(local, CHAN, 0, 0, tiled=True).reshape(count, -1, width)
    moved = lax.all_to_all(
        local.reshape(-1, length, width), CHAN, split_axis=0, concat_axis=2, tiled=True
    )
    return moved.reshape(1, -1, count * width)


def features_apart(whole):
    count = lax.axis_size(CHAN)
    if (whole.shape[1] // count) % LANES == 0:
        return spread(whole, count)
    return whole[None]


def features_out(parts, rows):
    blocks, tokens, width = parts.shape
    parts = parts.reshape(blocks, rows, tokens // rows, width)
    if blocks > 1:
        moved = lax.all_to_all(parts, CHAN, 0, 0, tiled=True)
        return moved.reshape(-1, *parts.shape[2:])
    return lax.all_to_all(parts[0], CHAN, split_axis=2, concat_axis=0, tiled=True)


class Corners:
    def __init__(self, seq, zed):
        self.seq_bits, self.zed_bits = (seq.bit_length() - 1, zed.bit_length() - 1)
        self.count = self.seq_bits + self.zed_bits
        self.dims = (2,) * self.count
        self.low = tuple(range(self.seq_bits))[::-1] + tuple(range(self.seq_bits, self.count))[::-1]
        self.high = tuple(range(self.seq_bits)) + tuple(range(self.seq_bits, self.count))[::-1]

    def place(self, dim):
        if dim < self.seq_bits:
            return ("seq", 2 ** (self.seq_bits - 1 - dim))
        return ("zed", 2 ** (self.count - 1 - dim))

    def bit(self, dim):
        axis, weight = self.place(dim)
        return lax.rem(lax.div(lax.axis_index(axis), weight), 2)

    def partner(self, dim):
        axis, weight = self.place(dim)
        return {axis: lax.axis_index(axis) + weight * (1 - 2 * self.bit(dim))}


def tail_kernel(
    corners,
    orders,
    dgate_hbm,
    dbranch_hbm,
    ending_ref,
    leading_ref,
    mixed_hbm,
    dres_hbm,
    gain_ref,
    input_hbm,
    gate_hbm,
    small_hbm,
    *refs,
):
    rows = ending_ref.shape[0]
    normed_hbms, x_hbms, inverse_hbms = (refs[k * rows : (k + 1) * rows] for k in range(3))
    tokens_ref, sum_gate, sum_out, sum_in, sum_small = refs[3 * rows : 3 * rows + 5]
    refs = refs[3 * rows + 5 :]
    stages = corners.count + 1
    dgate, dbranch, mixed, dres, normed, x, inverse, weight_in, weight_gate = refs[:9]
    made_in, made_out, own_small, back, parts, rim = refs[9:15]
    slots_in, slots_out, slots_small = (
        refs[15 + k * stages : 15 + (k + 1) * stages] for k in range(3)
    )
    (
        send_sem,
        recv_sem,
        load_sem,
        move_send,
        move_recv,
        keep_sem,
        rim_send,
        rim_recv,
    ) = refs[15 + 3 * stages :]
    seq, zed, core = (lax.axis_index(axis) for axis in ("seq", "zed", "core"))
    seqs, group = (lax.axis_size("seq"), 2 * lax.axis_size("zed"))
    mine = zed * 2 + core
    length = tokens_ref.shape[1]
    model = x.shape[1]

    def member(index):
        return {"zed": lax.div(index, 2), "core": lax.rem(index, 2)}

    def by_row(sources, target):
        return [
            (source, target.at[pl.ds(row * length, length)]) for row, source in enumerate(sources)
        ]

    pairs = [
        (dbranch_hbm, dbranch),
        (input_hbm, weight_in),
        (dgate_hbm, dgate),
        (gate_hbm, weight_gate),
        *by_row(x_hbms, x),
        *by_row(inverse_hbms, inverse),
        (dres_hbm, dres),
        *by_row(normed_hbms, normed),
        (mixed_hbm, mixed),
        (small_hbm.at[(slice(None),) * corners.count + (core,)], own_small),
    ]
    kinds = []
    for name in ('dbranch', 'win', 'dgate', 'wgate', 'x', 'inverse', 'dres', 'normed', 'mixed', 'small'):
        kinds += [name] * (rows if name in ("normed", "x", "inverse") else 1)
    loads = [
        pltpu.make_async_copy(source, target, load_sem.at[place])
        for place, (source, target) in enumerate(pairs)
    ]
    for load in loads:
        load.start()

    barrier = pltpu.get_barrier_semaphore()
    for other in range(1, group):
        pl.semaphore_signal(
            barrier, inc=1, device_id=member(lax.rem(mine + other, group)), device_id_type=MESH
        )
    for other in range(1, seqs):
        pl.semaphore_signal(
            barrier, inc=1, device_id={"seq": lax.rem(seq + other, seqs)}, device_id_type=MESH
        )
    pl.semaphore_wait(barrier, group - 1 + seqs - 1)

    rim_copy = pltpu.make_async_remote_copy(
        src_ref=leading_ref,
        dst_ref=rim,
        send_sem=rim_send,
        recv_sem=rim_recv,
        device_id={"seq": lax.rem(seq + seqs - 1, seqs)},
        device_id_type=MESH,
    )
    rim_copy.start()

    def own(stream, index):
        if stream < 4:
            return made_in.at[(stream,) + index + (core,)]
        if stream < 6:
            return made_out.at[(stream - 4,) + index + (core,)]
        return own_small.at[index]

    def slot(stream, stage):
        if stream < 4:
            return slots_in[stage].at[stream]
        if stream < 6:
            return slots_out[stage].at[stream - 4]
        return slots_small[stage]

    def copy(stream, stage):
        order = orders[stream]
        every = (slice(None),) * corners.count
        if stage == 0:
            if stream < 4:
                source = made_in.at[(stream,) + every + (1 - core,)]
            elif stream < 6:
                source = made_out.at[(stream - 4,) + every + (1 - core,)]
            else:
                source = small_hbm.at[every + (1 - core,)]
            target = {"core": 1 - core}
        else:
            dim = order[stage - 1]
            fixed = {before: corners.bit(before) for before in order[: stage - 1]}
            fixed[dim] = 1 - corners.bit(dim)
            source = own(stream, tuple(fixed.get(d, slice(None)) for d in range(corners.count)))
            target = corners.partner(dim)
        return pltpu.make_async_remote_copy(
            src_ref=source,
            dst_ref=slot(stream, stage),
            send_sem=send_sem.at[stream, stage],
            recv_sem=recv_sem.at[stream, stage],
            device_id=target,
            device_id_type=MESH,
        )

    sums = [
        sum_gate.at[:, : sum_gate.shape[1] // 2],
        sum_gate.at[:, sum_gate.shape[1] // 2 :],
        sum_in.at[:, : sum_in.shape[1] // 2],
        sum_in.at[:, sum_in.shape[1] // 2 :],
        sum_out.at[:, : sum_out.shape[1] // 2],
        sum_out.at[:, sum_out.shape[1] // 2 :],
        sum_small,
    ]

    def advance(stream, stage):
        order = orders[stream]
        copy(stream, stage).wait_recv()
        left = [dim for dim in range(corners.count) if dim not in order[:stage]]
        fixed = {dim: corners.bit(dim) for dim in order[:stage]}
        arrived = slot(stream, stage)
        if not left:
            index = tuple(fixed[dim] for dim in range(corners.count))
            sums[stream][...] = own(stream, index)[...].astype(jnp.float32) + arrived[...].astype(
                jnp.float32
            )
            return

        def add(index, carry):
            part = {
                dim: lax.rem(lax.div(index, 2 ** (len(left) - 1 - place)), 2)
                for place, dim in enumerate(left)
            }
            kept = own(stream, tuple({**fixed, **part}[dim] for dim in range(corners.count)))
            total = kept[...].astype(jnp.float32) + arrived[
                tuple(part[dim] for dim in left)
            ].astype(jnp.float32)
            kept[...] = total.astype(jnp.bfloat16)
            return carry

        lax.fori_loop(0, 2 ** len(left), add, 0)
        copy(stream, stage + 1).start()

    def move(other, row):
        to = lax.rem(mine + other, group)
        return pltpu.make_async_remote_copy(
            src_ref=parts.at[to, pl.ds(row * length, length)],
            dst_ref=tokens_ref.at[mine * rows + row],
            send_sem=move_send.at[other - 1, row],
            recv_sem=move_recv.at[other - 1, row],
            device_id=member(to),
            device_id_type=MESH,
        )

    def keep(row):
        return pltpu.make_async_copy(
            parts.at[mine, pl.ds(row * length, length)],
            tokens_ref.at[mine * rows + row],
            keep_sem.at[row],
        )

    tile = 256
    width = parts.shape[2]

    def back_row(row):
        at_row = slice(row * length, (row + 1) * length)

        def product(index, carry):
            at = pl.ds(pl.multiple_of(index * tile, tile), tile)
            contract = (((1,), (1,)), ((), ()))
            back[:, at] = lax.dot_general(
                dbranch[at_row, :], weight_in[at, :], contract, preferred_element_type=jnp.float32
            ) + lax.dot_general(
                dgate[at_row, :], weight_gate[at, :], contract, preferred_element_type=jnp.float32
            )
            return carry

        lax.fori_loop(0, model // tile, product, 0)
        slab = 16

        def norm(index, carry):
            base = pl.multiple_of(index * slab, slab)
            at = pl.ds(row * length + base, slab)
            inv = inverse[at, :1]
            value = x[at, :].astype(jnp.float32) * inv
            scaled = back[pl.ds(base, slab), :] * gain_ref[...]
            mean = jnp.mean(scaled * value, axis=1, keepdims=True)
            grad = dres[at, :].astype(jnp.float32) + inv * (scaled - value * mean)
            grad = grad.astype(jnp.bfloat16)
            for part in range(parts.shape[0]):
                parts[part, at, :] = grad[:, part * width : (part + 1) * width]
            return carry

        lax.fori_loop(0, length // slab, norm, 0, unroll=4)
        for other in range(1, group):
            move(other, row).start()
        keep(row).start()

    def weight_product(left, right, made, stream, first):
        columns = made.shape[-1]
        shape = made.shape[1:-1]

        def product(index, carry):
            at = pl.ds(pl.multiple_of(index * tile, tile), tile)
            source = pl.ds(pl.multiple_of(first + index * tile, tile), tile)
            part = lax.dot_general(
                left[...],
                right[:, source],
                (((0,), (0,)), ((), ())),
                preferred_element_type=jnp.float32,
            )
            made[(stream,) + (slice(None),) * len(shape) + (at,)] = part.astype(
                jnp.bfloat16
            ).reshape(shape + (tile,))
            return carry

        lax.fori_loop(0, columns // tile, product, 0)

    half, half_out = (made_in.shape[-1], made_out.shape[-1])
    waited, reached = (set(), {})

    def need(*names):
        for place, name in enumerate(kinds):
            if name in names and place not in waited:
                waited.add(place)
                loads[place].wait()

    def fix_rim():
        need("dbranch")
        rim_copy.wait()
        live = jnp.where(seq < seqs - 1, 1.0, 0.0)
        for row in range(rows):
            at = slice((row + 1) * length - STEP, (row + 1) * length)
            inside = dbranch[at, :].astype(jnp.float32)
            last = ending_ref[row] + live * rim[row]
            dbranch[at, :] = jnp.concatenate([inside[: STEP - SUBLANES], last], axis=0).astype(
                jnp.bfloat16
            )

    def begin(stream):
        copy(stream, 0).start()
        reached[stream] = 0

    def progress(streams):
        for stream in streams:
            if stream in reached and reached[stream] < stages:
                if stream == 6:
                    need("small")
                advance(stream, reached[stream])
                reached[stream] += 1

    def compute(item):
        if item == "gate":
            need("normed", "dgate")
            for stream in (0, 1):
                weight_product(normed, dgate, made_in, stream, stream * half)
                begin(stream)
        elif item == "out":
            need("mixed", "dres")
            for stream in (4, 5):
                weight_product(mixed, dres, made_out, stream - 4, (stream - 4) * half_out)
                begin(stream)
        elif item == "in":
            need("normed", "dbranch")
            for stream in (2, 3):
                weight_product(normed, dbranch, made_in, stream, (stream - 2) * half)
                begin(stream)
        else:
            need("dbranch", "dgate", "win", "wgate", "x", "inverse", "dres")
            back_row(item)

    begin(6)
    fix_rim()
    compute(0)
    compute(1)
    compute('gate')
    progress((6,))
    compute('out')
    progress((0, 1))
    compute('in')
    progress((0, 1))
    progress((4, 5))
    progress((6,))
    while any(reached[stream] < stages for stream in range(7)):
        progress((0, 1, 4, 5, 2, 3, 6))
    for stage in range(stages):
        for stream in range(7):
            copy(stream, stage).wait_send()
    for row in range(rows):
        for other in range(1, group):
            move(other, row).wait()
        keep(row).wait()


def tail(dgate, dbranch, ending, leading, mixed, dres, gain, w_in, w_gate, small, normed, x, inverse):
    corners = Corners(lax.axis_size("seq"), lax.axis_size("zed"))
    group, devices = (lax.axis_size(CHAN), 2 ** (corners.count + 1))
    tokens, model = dres.shape
    rec = dgate.shape[1]
    rows = ending.shape[0]
    length, width = (tokens // rows, model // group)
    low, f32 = (jnp.bfloat16, jnp.float32)
    stages = corners.count + 1
    in_rows, out_rows = (model // devices, rec // devices)
    small = small.reshape(corners.dims + (2, out_rows, small.shape[1]))
    orders = [corners.low, corners.high] * 3 + [corners.low]

    def slots(lead, shape):
        return [pltpu.VMEM(lead + (2,) * (corners.count - k) + shape, low) for k in range(stages)]

    in_shape, out_shape = ((in_rows, rec // 2), (out_rows, model // 2))
    loaded = (dgate, dbranch, mixed, dres, dres, dres)
    loaded += (jax.ShapeDtypeStruct((tokens, LANES), f32), w_in, w_gate)
    anyplace = pl.BlockSpec(memory_space=pl.ANY)
    vmem = pl.BlockSpec(memory_space=pltpu.VMEM)
    dma = pltpu.SemaphoreType.DMA
    moved = sum(math.prod(a.shape) * a.dtype.itemsize for a in loaded)
    return pl.pallas_call(
        functools.partial(tail_kernel, corners, orders),
        name="tail",
        in_specs=[anyplace, anyplace, vmem, vmem, anyplace, anyplace, vmem]
        + [anyplace] * (3 + 3 * rows),
        out_specs=[anyplace] + [vmem] * 4,
        out_shape=[
            jax.ShapeDtypeStruct((group * rows, length, width), low),
            jax.ShapeDtypeStruct((in_rows, rec), f32),
            jax.ShapeDtypeStruct((out_rows, model), f32),
            jax.ShapeDtypeStruct((in_rows, rec), f32),
            jax.ShapeDtypeStruct(small.shape[-2:], f32),
        ],
        scratch_shapes=[pltpu.VMEM(a.shape, a.dtype) for a in loaded]
        + [
            pltpu.VMEM((4,) + corners.dims + (2,) + in_shape, low),
            pltpu.VMEM((2,) + corners.dims + (2,) + out_shape, low),
            pltpu.VMEM(corners.dims + small.shape[-2:], low),
            pltpu.VMEM((length, model), f32),
            pltpu.VMEM((group, tokens, width), low),
            pltpu.VMEM(leading.shape, leading.dtype),
        ]
        + slots((4,), in_shape)
        + slots((2,), out_shape)
        + slots((), small.shape[-2:])
        + [
            dma((7, stages)),
            dma((7, stages)),
            dma((7 + 3 * rows,)),
            dma((group - 1, rows)),
            dma((group - 1, rows)),
            dma((rows,)),
            dma,
            dma,
        ],
        compiler_params=pltpu.CompilerParams(
            collective_id=1, has_side_effects=True, vmem_limit_bytes=60 * 1024 * 1024
        ),
        cost_estimate=pl.CostEstimate(
            flops=10 * tokens * model * rec, bytes_accessed=2 * moved, transcendentals=0
        ),
    )(dgate, dbranch, ending, leading, mixed, dres, gain[None], w_in, w_gate, small, *normed, *x, *inverse)


def grads_kernel(
    normed_ref,
    dgate_ref,
    dup_ref,
    hidden_ref,
    gout_ref,
    out_ref,
    turned_ref,
    made_wide,
    made_down,
    come_wide,
    come_down,
    send_sem,
    recv_sem,
    store_sem,
):
    step = pl.program_id(0)
    core = lax.axis_index("core")
    other = {"core": 1 - core}
    wide_rows, down_rows = (made_wide.shape[3], made_down.shape[3])
    wides, downs = (come_wide.shape[0], come_down.shape[0])
    total = wides + downs
    down_at = wides * wide_rows

    def exchange(made, come, index, slot):
        return pltpu.make_async_remote_copy(
            src_ref=made.at[lax.rem(index, 2), 1 - core],
            dst_ref=come.at[index],
            send_sem=send_sem.at[slot],
            recv_sem=recv_sem.at[slot],
            device_id=other,
            device_id_type=MESH,
        )

    def store_wide(index):
        return pltpu.make_async_copy(
            come_wide.at[index],
            out_ref.at[:, pl.ds(pl.multiple_of(index * wide_rows, wide_rows), wide_rows)],
            store_sem.at[index],
        )

    def store_down(index):
        chips = come_down.shape[1]
        return pltpu.make_async_copy(
            come_down.at[index],
            out_ref.at[pl.ds(index * chips, chips), pl.ds(down_at, down_rows)],
            store_sem.at[index + wides],
        )

    @pl.when(step == 0)
    def _():
        barrier = pltpu.get_barrier_semaphore()
        pl.semaphore_signal(barrier, inc=1, device_id=other, device_id_type=MESH)
        pl.semaphore_wait(barrier, 1)
        turned_ref[...] = normed_ref[...].T

    def product_wide(source, index):
        made = made_wide.at[lax.rem(index, 2)]
        chips, rows = (made.shape[1], made.shape[2])
        tile = 512

        def column(place, carry):
            at = pl.ds(pl.multiple_of(place * tile, tile), tile)
            part = jnp.dot(turned_ref[...], source[:, at], preferred_element_type=jnp.float32)
            part = part.astype(jnp.bfloat16).reshape(chips, 2, rows, tile)
            made[0, :, :, at] = part[:, 0]
            made[1, :, :, at] = part[:, 1]
            return carry

        lax.fori_loop(0, source.shape[1] // tile, column, 0)

    def product_tall(left, right, made_all, index):
        made = made_all.at[lax.rem(index, 2)]
        chips, rows = (made.shape[1], made.shape[2])
        tile = 512

        def column(place, carry):
            at = pl.ds(pl.multiple_of(place * tile, tile), tile)
            part = lax.dot_general(
                left[...], right[:, at], (((0,), (0,)), ((), ())), preferred_element_type=jnp.float32
            )
            part = part.astype(jnp.bfloat16).reshape(chips, 2, rows, tile)
            made[0, :, :, at] = part[:, 0]
            made[1, :, :, at] = part[:, 1]
            return carry

        lax.fori_loop(0, right.shape[1] // tile, column, 0)

    half = wides // 2

    @pl.when(step < half)
    def _():
        product_wide(dgate_ref, step)

    @pl.when((step >= half) & (step < wides))
    def _():
        product_wide(dup_ref, step)

    @pl.when(step < wides)
    def _():
        exchange(made_wide, come_wide, step, step).start()

    @pl.when((step >= wides) & (step < total))
    def _():
        product_tall(hidden_ref, gout_ref, made_down, step - wides)
        exchange(made_down, come_down, step - wides, step).start()

    def finish(made, come, index, slot, store):
        exchange(made, come, index, slot).wait()
        mine = made.at[lax.rem(index, 2), core]
        arrived = come.at[index]

        def add(chip, carry):
            both = mine[chip].astype(jnp.float32) + arrived[chip].astype(jnp.float32)
            arrived[chip] = both.astype(jnp.bfloat16)
            return carry

        lax.fori_loop(0, come.shape[1], add, 0)
        store(index).start()

    before = step - 1

    @pl.when((before >= 0) & (before < wides))
    def _():
        finish(made_wide, come_wide, before, before, store_wide)

    @pl.when(before >= wides)
    def _():
        finish(made_down, come_down, before - wides, before, store_down)

    @pl.when(step == total)
    def _():
        for index in range(wides):
            store_wide(index).wait()
        for index in range(downs):
            store_down(index).wait()


def block_gradients(normed, dgate, dup, hidden, gout):
    tokens, model = normed.shape
    ffn = hidden.shape[1]
    chips = lax.axis_size("seq") * lax.axis_size("zed")
    devices = 2 * chips
    wide_rows, down_rows = (model // devices, ffn // devices)
    chunk = 768
    wides, downs = (2 * ffn // model, ffn // chunk)
    half = wides // 2
    down_chips = chunk // (2 * down_rows)
    rows = wides * wide_rows + down_rows
    low = jnp.bfloat16

    def whole(array):
        return pl.BlockSpec(array.shape, lambda s: (0, 0), pipeline_mode=pl.Buffered(1))

    def part(columns, first, count):
        return pl.BlockSpec((tokens, columns), lambda s: (0, jnp.clip(s - first, 0, count - 1)))

    total = wides + downs
    flops = 6 * tokens * model * ffn
    arrays = (normed, dgate, dup, hidden, gout)
    moved = sum(math.prod(a.shape) * 2 for a in arrays) + chips * rows * model * 2
    return pl.pallas_call(
        grads_kernel,
        name="block_gradients",
        grid=(total + 1,),
        in_specs=[
            whole(normed),
            part(model, 0, half),
            part(model, half, half),
            part(chunk, wides, downs),
            whole(gout),
        ],
        out_specs=pl.BlockSpec(memory_space=pl.ANY),
        out_shape=jax.ShapeDtypeStruct((chips, rows, model), low),
        scratch_shapes=[
            pltpu.VMEM((model, tokens), low),
            pltpu.VMEM((2, 2, chips, wide_rows, model), low),
            pltpu.VMEM((2, 2, down_chips, down_rows, model), low),
            pltpu.VMEM((wides, chips, wide_rows, model), low),
            pltpu.VMEM((downs, down_chips, down_rows, model), low),
            pltpu.SemaphoreType.DMA((total,)),
            pltpu.SemaphoreType.DMA((total,)),
            pltpu.SemaphoreType.DMA((total,)),
        ],
        compiler_params=pltpu.CompilerParams(
            collective_id=2, has_side_effects=True, vmem_limit_bytes=VMEM_BYTES
        ),
        cost_estimate=pl.CostEstimate(flops=flops, bytes_accessed=moved, transcendentals=0),
    )(*arrays)


def passed_along(value, axis, steps):
    count = lax.axis_size(axis)
    leading, last = (max(0, -steps), min(count, count - steps))
    return lax.ppermute(value, axis, [(source, source + steps) for source in range(leading, last)])


def weight_grad(left, right):
    return lax.dot_general(
        left, right, (((0,), (0,)), ((), ())), preferred_element_type=jnp.float32
    ).astype(jnp.bfloat16)


def back_dot(left, right):
    return lax.dot_general(
        left, right, (((1,), (1,)), ((), ())), preferred_element_type=jnp.float32
    )


def fwd_dot(left, right):
    return jnp.dot(left, right, preferred_element_type=jnp.float32)


def gelu_fn(value):
    return jax.nn.gelu(value, approximate=True)


def norm_back(grad_norm, normed, inverse, gain):
    scaled = grad_norm * gain
    mean_term = jnp.mean(scaled * normed, axis=1, keepdims=True)
    return inverse * (scaled - normed * mean_term)


def scattered(gradient):
    return lax.psum_scatter(
        gradient, ("seq", "zed", "core"), scatter_dimension=0, tiled=True
    ).astype(jnp.float32)


def body(
    tokens,
    cotangent,
    doc_starts,
    lengths,
    norm1_gain,
    recur_input,
    recur_gate,
    conv_kernel,
    conv_bias,
    lru_gates,
    lru_bias,
    lru_decay,
    recur_out,
    norm2_gain,
    mlp_gate,
    mlp_up,
    mlp_down,
):
    count = lax.axis_size(CHAN)
    row_count, block_len = (tokens.shape[0] // count, tokens.shape[1])
    model_dim = tokens.shape[2] * count
    tok_count = row_count * block_len
    rec_width = recur_input.shape[1]
    ffn_width = mlp_gate.shape[1]
    head_count = H
    head_size = rec_width // head_count
    tap_count = conv_kernel.shape[0]
    rim_size = tap_count - 1
    seq_index = lax.axis_index("seq")
    position = seq_index * block_len + jnp.arange(block_len, dtype=jnp.int32)
    bounds = jnp.concatenate([doc_starts, lengths[:, None]], axis=1)
    is_before = bounds[:, None, :] <= position[None, :, None]
    seg_start = jnp.max(jnp.where(is_before, bounds[:, None, :], 0), axis=2)
    dist = jnp.broadcast_to(
        (position[None, :] - seg_start)[:, :, None], (row_count, block_len, LANES)
    )
    soft_decay = jax.nn.softplus(-lru_decay)
    params = jnp.concatenate(
        [
            conv_kernel,
            conv_bias[None],
            lru_bias,
            (-8.0 * soft_decay)[None],
            (8.0 * jax.nn.sigmoid(-lru_decay))[None],
            jnp.zeros((SUBLANES - 1, rec_width), jnp.float32),
        ],
        axis=0,
    )
    core = Recurrence(row_count, block_len, rec_width, head_size)
    wide_gates = core.widen(lru_gates)
    if tokens.shape[2] % LANES == 0:
        blocks = [features_in(tokens, slice(0, 1))]
        later, wide_gates, params, dist = lax.optimization_barrier(
            (tokens, wide_gates, params, dist)
        )
        blocks += [features_in(later, slice(row, row + 1)) for row in range(1, row_count)]
    else:
        side = features_in(tokens)
        blocks = [side[:, row * block_len : (row + 1) * block_len] for row in range(row_count)]
    single = Recurrence(1, block_len, rec_width, head_size)
    per_row = []
    for row in range(row_count):
        block = blocks[row]
        if row:
            block, _ = lax.optimization_barrier((block, per_row[-1][-1]))
        low_x, inverse, normed, branch, pre, rim = front(block, norm1_gain, recur_input, recur_gate)
        branch, rim = (branch[None], rim[None])
        scanned = single.forward(branch, rim, dist[row : row + 1], params, wide_gates)
        per_row.append((low_x, inverse, normed, branch, pre[None], rim, *scanned))
    low_x, inverse, normed_low, branch, gate_pre, rim, lru_in, rate, igate, state, cum, last = zip(
        *per_row
    )
    entering, mixed_low, resid_one, normed_low2 = middle(
        last, state, cum, gate_pre, low_x, recur_out, norm2_gain
    )
    cotangent, _ = lax.optimization_barrier((cotangent, block))
    cotangent, resid_one = lax.optimization_barrier((features_in(cotangent), resid_one))
    grad_low, hidden_low, mgate_low, mup_low = mlp_hidden(
        lengths - seq_index * block_len, cotangent, normed_low2, mlp_gate, mlp_up, mlp_down
    )
    devices = lax.axis_size(("seq", "zed", "core"))
    own_rows = model_dim // devices
    tiled = own_rows % (2 * SUBLANES) == 0 and tokens.shape[2] % LANES == 0
    if tiled:
        merged = block_gradients(normed_low2, mgate_low, mup_low, hidden_low, grad_low)
        merged, hidden_low = lax.optimization_barrier((merged, hidden_low))
        merged = lax.psum_scatter(merged, "seq", scatter_dimension=0, tiled=True)
    result_parts, resid_low = mlp_back(
        hidden_low,
        mgate_low,
        mup_low,
        grad_low,
        resid_one,
        norm2_gain,
        mlp_gate,
        mlp_up,
        mlp_down,
        cotangent.shape,
    )
    output = features_out(result_parts, row_count)
    gate_low, back_local, back_cum, first_term = core.adjoint(
        resid_low,
        recur_out,
        gate_pre,
        state,
        cum,
        entering,
        rate,
        dist,
        params,
    )
    gate_low = gate_low.reshape(tok_count, rec_width)

    def zed_stage(leaving):
        if not tiled:
            return ((), leaving)
        done, leaving = lax.optimization_barrier((merged, leaving))
        return (lax.psum_scatter(done, "zed", scatter_dimension=0, tiled=True), leaving)

    branch_local, ending, leading, small, merged_own = core.backward(
        back_local,
        back_cum,
        first_term,
        last,
        state,
        cum,
        entering,
        rate,
        igate,
        lru_in,
        dist,
        branch,
        rim,
        params,
        wide_gates,
        zed_stage,
    )
    branch_low = branch_local.reshape(tok_count, rec_width)
    if tiled:
        output, branch_low = lax.optimization_barrier((output, branch_low))
        grad_tokens, sum_rgate, sum_rout, sum_rin, own_small = tail(
            gate_low,
            branch_low,
            ending,
            leading,
            mixed_low,
            resid_low,
            norm1_gain,
            recur_input,
            recur_gate,
            small,
            normed_low,
            low_x,
            inverse,
        )
        device = lax.axis_index(("seq", "zed", "core"))
        sums = outputs(
            device,
            merged_own[0],
            sum_rgate,
            sum_rin,
            sum_rout,
            own_small,
            recur_input,
            recur_gate,
            mlp_gate,
            mlp_up,
            norm1_gain,
            norm2_gain,
            head_size,
        )
        flat = (0, 4, 7, 9)
        sums = [part.reshape(-1) if place in flat else part for place, part in enumerate(sums)]
        return (output, grad_tokens, *sums)
    else:
        from_next = passed_along(
            leading[:, SUBLANES - rim_size :, :].astype(jnp.bfloat16), "seq", -1
        )
        ending = ending + jnp.pad(
            from_next.astype(jnp.float32), ((0, 0), (SUBLANES - rim_size, 0), (0, 0))
        )
        branch_low = lax.dynamic_update_slice(
            branch_local, ending.astype(jnp.bfloat16), (0, block_len - SUBLANES, 0)
        ).reshape(tok_count, rec_width)
        grad_norm1 = back_dot(branch_low, recur_input) + back_dot(gate_low, recur_gate)
        inv_one = jnp.concatenate(inverse)[:, :1]
        normed_one = jnp.concatenate(low_x).astype(jnp.float32) * inv_one
        normed_low = jnp.concatenate(normed_low)
        input_part = norm_back(grad_norm1, normed_one, inv_one, norm1_gain)
        grad_x = (resid_low.astype(jnp.float32) + input_part).astype(jnp.bfloat16)
        grad_tokens = features_out(features_apart(grad_x), row_count)
        sum_mgate, sum_mup, sum_down, sum_rout, sum_rgate, sum_rin = (
            scattered(weight_grad(left, right))
            for left, right in (
                (normed_low2, mgate_low),
                (normed_low2, mup_low),
                (hidden_low, grad_low),
                (mixed_low, resid_low),
                (normed_low, gate_low),
                (normed_low, branch_low),
            )
        )
        own_small = scattered(small)
    sum_lgates = jnp.concatenate(
        [own_small[:, :head_size], own_small[:, LANES : LANES + head_size]], axis=1
    )
    own_sums = jnp.swapaxes(own_small[:, head_size : head_size + SUBLANES], 0, 1)
    device = lax.axis_index(("seq", "zed", "core"))

    def mine(array, size, axis=0):
        return lax.dynamic_slice_in_dim(array, device * size, size, axis)

    def weighed(weight, gradient):
        return jnp.sum(mine(weight, own_rows).astype(jnp.float32) * gradient, axis=1)

    sum_gain1 = (weighed(recur_input, sum_rin) + weighed(recur_gate, sum_rgate)) / mine(
        norm1_gain, own_rows
    )
    sum_gain2 = (weighed(mlp_gate, sum_mgate) + weighed(mlp_up, sum_mup)) / mine(
        norm2_gain, own_rows
    )
    sum_decay = own_sums[7]
    return (
        output,
        grad_tokens,
        sum_gain1,
        sum_rin,
        sum_rgate,
        own_sums[:4],
        own_sums[4],
        sum_lgates,
        own_sums[5:7],
        sum_decay,
        sum_rout,
        sum_gain2,
        sum_mgate,
        sum_mup,
        sum_down,
    )


def solution(mesh):
    seq, chan = (mesh.shape["seq"], mesh.shape["chan"])
    chips = jax.sharding.Mesh(mesh.devices.reshape(seq, chan // 2, 2), ("seq", "zed", "core"))
    chan = ("zed", "core")
    every = ("seq", "zed", "core")
    activations = P(None, "seq", chan)
    rows, columns, vector = (P(every, None), P(None, every), P(every))
    return jax.shard_map(
        body,
        mesh=chips,
        in_specs=(activations, activations, P(chan, None), P(chan)) + (P(),) * 13,
        out_specs=(
            activations,
            activations,
            vector,
            rows,
            rows,
            columns,
            vector,
            rows,
            columns,
            vector,
            rows,
            vector,
            rows,
            rows,
            rows,
        ),
        check_vma=False,
    )
```

```python
import functools
import math

import jax
import jax.numpy as jnp
from jax import lax
from jax.experimental import pallas as pl
from jax.experimental.pallas import tpu as pltpu
from jax.sharding import PartitionSpec as P

H = 16


EPS = 1e-06
ROOT_FLOOR = 1e-06
LANES = 128
SUBLANES = 8
STEP = 16
VMEM_BYTES = 56 * 1024 * 1024
MESH = pl.DeviceIdType.MESH


def sigmoid(value):
    return 0.5 * jnp.tanh(0.5 * value) + 0.5


GELU_C = 0.7978845608
GELU_A = 0.044715


def gelu_pair(value):
    square = value * value
    inner = jnp.tanh(value * (GELU_C + (GELU_C * GELU_A) * square))
    half = 0.5 + 0.5 * inner
    slope = GELU_C + (3.0 * GELU_C * GELU_A) * square
    return (value * half, half + 0.5 * value * (1.0 - inner * inner) * slope)


def root_argument(log_decay, decay):
    y = 2.0 * log_decay
    series = 1.0 + y * (0.5 + y * (1.0 / 6.0 + y * (1.0 / 24.0)))
    return jnp.where(y > -0.05, -y * series, 1.0 - decay * decay)


def across(column, width):
    return jnp.concatenate([column] * (width // LANES), axis=1)


class Rows:
    def __init__(self, refs):
        self.refs = refs

    def __getitem__(self, index):
        if not isinstance(index, tuple):
            return self.refs[index][0]
        return self.refs[index[0]][(0,) + index[1:]]


def by_rows(refs, rows, apart):
    found = []
    for split in apart:
        count = rows if split else 1
        found.append(Rows(refs[:count]) if split else refs[0])
        refs = refs[count:]
    return found, refs


def scan_block(
    branch_ref,
    rim_ref,
    dist_ref,
    par_ref,
    gates_ref,
    lru_ref,
    rate_ref,
    igate_ref,
    state_ref,
    cum_ref,
    last_ref,
    both_ref,
):
    rows, length, width = branch_ref.shape
    span = 2 * STEP if rows == 1 else STEP
    taps = [par_ref[k : k + 1, :] for k in range(4)]
    conv_bias, rate_bias, input_bias, soft = (par_ref[k : k + 1, :] for k in range(4, 8))
    place = lax.broadcasted_iota(jnp.int32, (SUBLANES, width), 0)

    for row in range(rows):

        def conv_step(index, before, row=row):
            base = pl.multiple_of(index * STEP, STEP)
            pieces = []
            for half in range(STEP // SUBLANES):
                at = pl.ds(base + half * SUBLANES, SUBLANES)
                here = branch_ref[row, at, :]
                dist = across(dist_ref[row, at, :], width)
                total = conv_bias + taps[0] * here
                for k in range(1, 4):
                    shifted = pltpu.roll(jnp.where(place < SUBLANES - k, here, before), k, 0)
                    total = total + taps[k] * jnp.where(dist >= k, shifted, 0.0)
                pieces.append(total)
                before = here
            lru_ref[row, pl.ds(base, STEP), :] = jnp.concatenate(pieces, axis=0).astype(jnp.bfloat16)
            return before

        lax.fori_loop(0, length // STEP, conv_step, rim_ref[row], unroll=2)

        piece = min(length, 256)

        def dot_step(index, carry, row=row):
            at = pl.ds(pl.multiple_of(index * piece, piece), piece)
            both_ref[row, at, :] = jnp.dot(
                lru_ref[row, at, :], gates_ref[...], preferred_element_type=jnp.float32
            )
            return carry

        lax.fori_loop(0, length // piece, dot_step, 0)

    def scan_step(index, carry):
        base = pl.multiple_of(index * span, span)
        later = []
        for row in range(rows):
            run_cum, run_state = carry[row]
            lru_both = lru_ref[row, pl.ds(base, span), :].astype(jnp.float32)
            for half in range(span // SUBLANES):
                at = pl.ds(base + half * SUBLANES, SUBLANES)
                lru = lru_both[half * SUBLANES : (half + 1) * SUBLANES]
                start = across(dist_ref[row, at, :], width) == 0
                rate = sigmoid(both_ref[row, at, :width] + rate_bias)
                igate = sigmoid(both_ref[row, at, width:] + input_bias)
                log_decay = rate * soft
                decay = jnp.exp(log_decay)
                arg = jnp.maximum(root_argument(log_decay, decay), ROOT_FLOOR)
                root = arg * lax.rsqrt(arg)
                cum = jnp.where(start, 0.0, decay)
                value = jnp.where(start, 1.0, root) * igate * lru
                rate_ref[row, at, :] = rate
                igate_ref[row, at, :] = igate
                for shift in (1, 2, 4):
                    live = place >= shift
                    value = value + cum * jnp.where(live, pltpu.roll(value, shift, 0), 0.0)
                    cum = cum * jnp.where(live, pltpu.roll(cum, shift, 0), 1.0)
                value = value + cum * run_state
                cum = cum * run_cum
                state_ref[row, at, :] = value
                cum_ref[row, at, :] = cum
                run_state = value[SUBLANES - 1 :, :]
                run_cum = cum[SUBLANES - 1 :, :]
            later.append((run_cum, run_state))
        return tuple(later)

    one, zero = (jnp.ones((1, width), jnp.float32), jnp.zeros((1, width), jnp.float32))
    done = lax.fori_loop(
        0, length // span, scan_step, tuple((one, zero) for _ in range(rows)), unroll=2
    )
    for row in range(rows):
        for place in range(2):
            last_ref[row, place : place + 1, :] = done[row][place]


def carried(sent_ref, got_ref, out_ref, send_sem, recv_sem, backward):
    seq, count = (lax.axis_index("seq"), lax.axis_size("seq"))

    def other(step):
        return {"seq": lax.rem(seq + step, count)}

    barrier = pltpu.get_barrier_semaphore()
    for step in range(1, count):
        pl.semaphore_signal(barrier, inc=1, device_id=other(step), device_id_type=MESH)
    pl.semaphore_wait(barrier, count - 1)
    copies = [
        pltpu.make_async_remote_copy(
            src_ref=sent_ref,
            dst_ref=got_ref.at[seq],
            send_sem=send_sem.at[step - 1],
            recv_sem=recv_sem.at[step - 1],
            device_id=other(step),
            device_id_type=MESH,
        )
        for step in range(1, count)
    ]
    for copy in copies:
        copy.start()
    got_ref[seq] = sent_ref[...]
    for copy in copies:
        copy.wait()
    for row in range(sent_ref.shape[0]):
        total = jnp.zeros(out_ref.shape[1:], jnp.float32)
        for place in range(count - 1, 0, -1) if backward else range(count - 1):
            longer = got_ref[place, row, 0:1, :] * total + got_ref[place, row, 1:2, :]
            total = jnp.where(place > seq if backward else place < seq, longer, total)
        out_ref[row] = total


def adjoint_kernel(rows, *refs):
    (
        dres_ref,
        weight_ref,
        pre_ref,
        state_ref,
        cum_ref,
        carry_ref,
        rate_ref,
        dist_ref,
        par_ref,
    ), outs = by_rows(refs, rows, (False, False, True, True, True, False, True, False, False))
    dgate_ref, local_ref, back_ref, first_ref, dmix_ref = outs
    _, length, width = dmix_ref.shape
    for row in range(rows):
        dmix_ref[row] = lax.dot_general(
            dres_ref[row * length : (row + 1) * length, :],
            weight_ref[...],
            (((1,), (1,)), ((), ())),
            preferred_element_type=jnp.float32,
        )
    soft = par_ref[7:8, :]
    place = lax.broadcasted_iota(jnp.int32, (SUBLANES, width), 0)
    last = length // STEP - 1

    def step(index, carry):
        base = pl.multiple_of((last - index) * STEP, STEP)
        later = []
        for row in range(rows):
            run_cum, run_back = carry[row]
            entering = carry_ref[row]
            pieces = []
            for half in reversed(range(STEP // SUBLANES)):
                at = pl.ds(base + half * SUBLANES, SUBLANES)
                start = across(dist_ref[row, at, :], width) == 0
                state = state_ref[row, at, :] + cum_ref[row, at, :] * entering
                act, slope = gelu_pair(pre_ref[row, at, :])
                dmix = dmix_ref[row, at, :]
                pieces.append(dmix * state * slope)
                dstate = dmix * act
                coef = jnp.where(start, 0.0, jnp.exp(rate_ref[row, at, :] * soft))
                value = coef * dstate
                for shift in (1, 2, 4):
                    live = place < SUBLANES - shift
                    turn = SUBLANES - shift
                    value = value + coef * jnp.where(live, pltpu.roll(value, turn, 0), 0.0)
                    coef = coef * jnp.where(live, pltpu.roll(coef, turn, 0), 1.0)
                value = value + coef * run_back
                coef = coef * run_cum
                inside = place < SUBLANES - 1
                local_ref[row, at, :] = dstate + jnp.where(
                    inside, pltpu.roll(value, SUBLANES - 1, 0), run_back
                )
                back_ref[row, at, :] = jnp.where(inside, pltpu.roll(coef, SUBLANES - 1, 0), run_cum)
                run_back = value[:1, :]
                run_cum = coef[:1, :]
            dgate_ref[row, pl.ds(base, STEP), :] = jnp.concatenate(pieces[::-1], axis=0).astype(
                jnp.bfloat16
            )
            later.append((run_cum, run_back))
        return tuple(later)

    one, zero = (jnp.ones((1, width), jnp.float32), jnp.zeros((1, width), jnp.float32))
    done = lax.fori_loop(0, last + 1, step, tuple((one, zero) for _ in range(rows)), unroll=2)
    for row in range(rows):
        first_ref[row] = done[row][1]


def backward_kernel(head_size, rows, *refs):
    first_at = 2
    sent_ref, got_ref, send_sem, recv_sem = refs[-4:]
    leaving_ref = refs[-8]
    lasts = Rows(refs[first_at + 1 : first_at + 1 + rows])

    @pl.when(pl.program_id(0) == 0)
    def _():
        for row in range(rows):
            sent_ref[row, 0:1, :] = lasts[row, 0:1, :]
            sent_ref[row, 1:2, :] = refs[first_at][row]
        carried(sent_ref, got_ref, leaving_ref, send_sem, recv_sem, True)

    block_backward(head_size, rows, 0, leaving_ref, *refs[:-8], *refs[-7:-4])


def later_backward_kernel(head_size, rows, first, *refs):
    held = 4
    block_backward(head_size, rows, first, refs[0], *refs[1 + held :])


def block_backward(head_size, rows, first_block, leaving_ref, *refs):
    (
        local_ref,
        back_ref,
        first_ref,
        last_ref,
        state_ref,
        cum_ref,
        in_ref,
        rate_ref,
        igate_ref,
        lru_ref,
        dist_ref,
        branch_ref,
        rim_ref,
        par_ref,
        gates_ref,
    ), others = by_rows(
        refs, rows, (False,) * 3 + (True,) * 3 + (False,) + (True,) * 3 + (False,) + (True,) * 2 + (False,) * 2
    )
    dbranch_ref, tail_ref, head_ref, dgates_ref = others[:4]
    both_ref, dconv_ref, sums_ref = others[-3:]
    _, length, width = local_ref.shape
    here = pl.program_id(0) + first_block
    block = pl.ds(pl.multiple_of(here * width, width), width)
    taps = [par_ref[k : k + 1, :] for k in range(4)]
    soft = par_ref[7:8, :]
    place = lax.broadcasted_iota(jnp.int32, (SUBLANES, width), 0)
    zeros = jnp.zeros((SUBLANES, width), jnp.float32)

    def gate_step(index, carry):
        sums, earlier = carry
        decay_sum, rate_sum, input_sum = sums
        base = pl.multiple_of(index * STEP, STEP)
        later = []
        for row in range(rows):
            before = earlier[row]
            entering = in_ref[row]
            leaving = leaving_ref[row, :, block]
            lru_both = lru_ref[row, pl.ds(base, STEP), :].astype(jnp.float32)
            drates, dinputs = ([], [])
            for half in range(STEP // SUBLANES):
                at = pl.ds(base + half * SUBLANES, SUBLANES)
                lru = lru_both[half * SUBLANES : (half + 1) * SUBLANES]
                start = across(dist_ref[row, at, :], width) == 0
                adjoint = local_ref[row, at, :] + back_ref[row, at, :] * leaving
                state = state_ref[row, at, :] + cum_ref[row, at, :] * entering
                previous = jnp.where(place < 1, before, pltpu.roll(state, 1, 0))
                before = state[SUBLANES - 1 :, :]
                rate = rate_ref[row, at, :]
                igate = igate_ref[row, at, :]
                log_decay = rate * soft
                decay = jnp.exp(log_decay)
                arg = root_argument(log_decay, decay)
                above = arg > ROOT_FLOOR
                arg = jnp.maximum(arg, ROOT_FLOOR)
                inverse = lax.rsqrt(arg)
                scale = jnp.where(start, 1.0, arg * inverse)
                gated = adjoint * igate
                dscale = gated * lru
                pull = jnp.where(above, dscale * decay * decay * inverse, 0.0)
                dlog = jnp.where(start, 0.0, adjoint * previous * decay - pull)
                dig = adjoint * scale * lru
                weighted = dlog * rate
                decay_sum = decay_sum + weighted
                drates.append(weighted * soft * (1.0 - rate))
                dinputs.append(dig * igate * (1.0 - igate))
                dconv_ref[row, at, :] = gated * scale
            drate = jnp.concatenate(drates, axis=0).astype(jnp.bfloat16)
            dinput = jnp.concatenate(dinputs, axis=0).astype(jnp.bfloat16)
            both_ref[row, pl.ds(base, STEP), :width] = drate
            both_ref[row, pl.ds(base, STEP), width:] = dinput
            drate = drate.astype(jnp.float32)
            dinput = dinput.astype(jnp.float32)
            rate_sum = rate_sum + (drate[:SUBLANES] + drate[SUBLANES:])
            input_sum = input_sum + (dinput[:SUBLANES] + dinput[SUBLANES:])
            later.append(before)
        return ((decay_sum, rate_sum, input_sum), tuple(later))

    sums, _ = lax.fori_loop(
        0,
        length // STEP,
        gate_step,
        ((zeros, zeros, zeros), tuple(in_ref[row] for row in range(rows))),
        unroll=2,
    )
    for slot, total in zip((5, 6, 7), (sums[1], sums[2], sums[0] * par_ref[8:9, :])):
        sums_ref[slot : slot + 1, :] = jnp.sum(total, axis=0, keepdims=True)

    piece = min(length, 256)
    wide = None
    for row in range(rows):

        def dot_step(index, carry, row=row):
            at = pl.ds(pl.multiple_of(index * piece, piece), piece)
            dconv_ref[row, at, :] += lax.dot_general(
                both_ref[row, at, :],
                gates_ref[...],
                (((1,), (1,)), ((), ())),
                preferred_element_type=jnp.float32,
            )
            return carry

        lax.fori_loop(0, length // piece, dot_step, 0)
        part = lax.dot_general(
            lru_ref[row], both_ref[row], (((0,), (0,)), ((), ())), preferred_element_type=jnp.float32
        )
        wide = part if wide is None else wide + part
    row_head = lax.broadcasted_iota(jnp.int32, (width, width), 0) // head_size
    col_head = lax.broadcasted_iota(jnp.int32, (width, width), 1) // head_size
    own = row_head == col_head
    folds = []
    for part in range(2):
        kept = jnp.where(own, wide[:, part * width : (part + 1) * width], 0.0)
        folded = kept
        for other in range(1, width // head_size):
            folded = folded + pltpu.roll(kept, width - other * head_size, 1)
        folds.append(folded[:, :LANES])

    def conv_step(index, carry):
        sums, following = carry
        sums = list(sums)
        base = pl.multiple_of((length // STEP - 1 - index) * STEP, STEP)
        later = []
        for row in range(rows):
            after = following[row]
            pieces = []
            for half in reversed(range(STEP // SUBLANES)):
                at = pl.ds(base + half * SUBLANES, SUBLANES)
                dist = across(dist_ref[row, at, :], width)
                branch = branch_ref[row, at, :]
                here = dconv_ref[row, at, :]
                total = taps[0] * here
                sums[0] = sums[0] + here * branch
                sums[4] = sums[4] + here
                masked = tuple(jnp.where(dist >= k, here, 0.0) for k in range(1, 4))
                for k in range(1, 4):
                    moved = pltpu.roll(
                        jnp.where(place >= k, masked[k - 1], after[k - 1]), SUBLANES - k, 0
                    )
                    total = total + taps[k] * moved
                    sums[k] = sums[k] + branch * moved
                after = masked
                pieces.append(total)
            whole = jnp.concatenate(pieces[::-1], axis=0)
            dbranch_ref[row, pl.ds(base, STEP), :] = whole.astype(jnp.bfloat16)
            later.append(after)

            @pl.when(index == 0)
            def _(row=row, whole=whole):
                tail_ref[row] = whole[STEP - SUBLANES :]

        return (tuple(sums), tuple(later))

    sums, firsts = lax.fori_loop(
        0,
        length // STEP,
        conv_step,
        ((zeros,) * 5, tuple((zeros,) * 3 for _ in range(rows))),
        unroll=2,
    )
    sums = list(sums)
    for row in range(rows):
        total = zeros
        rim = rim_ref[row]
        for k in range(1, 4):
            moved = pltpu.roll(jnp.where(place >= k, 0.0, firsts[row][k - 1]), SUBLANES - k, 0)
            total = total + taps[k] * moved
            sums[k] = sums[k] + rim * moved
        head_ref[row] = total
    for slot in range(5):
        sums_ref[slot : slot + 1, :] = jnp.sum(sums[slot], axis=0, keepdims=True)
    above = jnp.zeros((head_size, width), jnp.float32)
    below = jnp.zeros((LANES - head_size - SUBLANES, width), jnp.float32)
    turned = jnp.concatenate([above, sums_ref[...], below], axis=0).T
    lane = lax.broadcasted_iota(jnp.int32, (width, LANES), 1)
    dgates_ref[:, :LANES] = jnp.where(lane < head_size, folds[0], turned).astype(dgates_ref.dtype)
    dgates_ref[:, LANES:] = folds[1].astype(dgates_ref.dtype)


def channel_call(
    kernel, name, arrays, specs, outs, out_specs, scratch, blocks, flops, params=()
):
    moved = sum(math.prod(a.shape) * a.dtype.itemsize for a in (*arrays, *outs))
    return pl.pallas_call(
        kernel,
        name=name,
        grid=(blocks,),
        in_specs=specs,
        out_specs=out_specs,
        out_shape=outs,
        scratch_shapes=scratch,
        compiler_params=pltpu.CompilerParams(vmem_limit_bytes=VMEM_BYTES, **dict(params)),
        cost_estimate=pl.CostEstimate(flops=flops, bytes_accessed=moved, transcendentals=0),
    )(*arrays)


class Recurrence:
    def __init__(self, rows, length, channels, head_size):
        self.rows, self.length, self.channels = (rows, length, channels)
        self.head_size = head_size
        self.width = head_size * LANES // math.gcd(head_size, LANES)
        self.blocks = channels // self.width
        self.flops = 2 * rows * length * channels * 2 * self.width

    def tall(self):
        return pl.BlockSpec((self.rows, self.length, self.width), lambda j: (0, 0, j))

    def short(self, size):
        return pl.BlockSpec((self.rows, size, self.width), lambda j: (0, 0, j))

    def apart(self, size):
        return [pl.BlockSpec((1, size, self.width), lambda j: (0, 0, j))] * self.rows

    def whole(self, rows, size):
        return pl.BlockSpec((rows, size, self.channels), lambda j: (0, 0, 0))

    def flat(self, size):
        return pl.BlockSpec((size, self.width), lambda j: (0, j))

    def dist(self):
        return pl.BlockSpec((self.rows, self.length, LANES), lambda j: (0, 0, 0))

    def gates(self, columns):
        return pl.BlockSpec((self.width, columns), lambda j: (j, 0))

    def shape(self, size, dtype):
        return jax.ShapeDtypeStruct((self.rows, size, self.channels), dtype)

    def widen(self, lru_gates):
        size, width = (self.head_size, self.width)
        heads = width // size
        column = jnp.arange(2 * width)
        source = (column // width) * size + column % size
        spread = (jnp.arange(2 * size)[:, None] == source[None, :]).astype(jnp.bfloat16)
        owner = (column % width) // size
        mine = (jnp.arange(self.channels) // size) % heads
        wide = jnp.dot(lru_gates, spread, preferred_element_type=jnp.float32)
        return jnp.where(mine[:, None] == owner[None, :], wide, 0.0).astype(jnp.bfloat16)

    def adjoint(self, dres, weight, pre, state, cum, entering, rate, dist, params):
        f32 = jnp.float32
        outs = [self.shape(self.length, d) for d in (jnp.bfloat16, f32, f32)] + [self.shape(1, f32)]
        tall, apart = (self.tall(), self.apart(self.length))
        return channel_call(
            functools.partial(adjoint_kernel, self.rows),
            "recurrence_adjoint",
            (dres, weight, *pre, *state, *cum, entering, *rate, dist, params),
            [
                pl.BlockSpec(dres.shape, lambda j: (0, 0)),
                self.gates(weight.shape[1]),
                *apart * 3,
                self.short(1),
                *apart,
                self.dist(),
                self.flat(16),
            ],
            outs,
            [tall, tall, tall, self.short(1)],
            [pltpu.VMEM((self.rows, self.length, self.width), f32)],
            self.blocks,
            2 * self.rows * self.length * weight.size,
        )

    def backward(
        self, local, back, first, last, state, cum, entering, rate, igate, lru, dist, branch, rim, params, gates, between_calls
    ):
        f32 = jnp.float32
        outs = [
            self.shape(self.length, jnp.bfloat16),
            self.shape(SUBLANES, f32),
            self.shape(SUBLANES, f32),
            jax.ShapeDtypeStruct((self.channels, 2 * LANES), jnp.bfloat16),
        ]
        seqs = lax.axis_size("seq")
        summary = (self.rows, 2, self.channels)
        arrays = (local, back, first, *last, *state, *cum, entering, *rate, *igate, *lru, dist, *branch, *rim)
        arrays += (params, gates)
        early = self.blocks - 1
        scratch = [
            pltpu.VMEM((self.rows, self.length, 2 * self.width), jnp.bfloat16),
            pltpu.VMEM((self.rows, self.length, self.width), f32),
            pltpu.VMEM((SUBLANES, self.width), f32),
        ]

        def specs(offset):
            rows, width = (self.rows, self.width)

            def wide(rows, size):
                return pl.BlockSpec((rows, size, width), lambda j: (0, 0, j + offset))

            def flat(size):
                return pl.BlockSpec((size, width), lambda j: (0, j + offset))

            def tall(columns):
                return pl.BlockSpec((width, columns), lambda j: (j + offset, 0))

            whole, apart = (wide(rows, self.length), [wide(1, self.length)] * rows)
            given = [whole, whole, self.whole(rows, 1), *[self.whole(1, 2)] * rows, *apart * 2]
            given += [wide(rows, 1), *apart * 3, self.dist(), *apart, *[wide(1, SUBLANES)] * rows]
            given += [flat(16), tall(2 * width)]
            made = [whole, wide(rows, SUBLANES), wide(rows, SUBLANES), tall(2 * LANES)]
            return (given, made)

        given, made = specs(0)
        *found, leaving = channel_call(
            functools.partial(backward_kernel, self.head_size, self.rows),
            "recurrence_backward",
            arrays,
            given,
            outs + [self.shape(1, f32)],
            made + [self.whole(self.rows, 1)],
            scratch
            + [
                pltpu.VMEM(summary, f32),
                pltpu.VMEM((seqs,) + summary, f32),
                pltpu.SemaphoreType.DMA((seqs - 1,)),
                pltpu.SemaphoreType.DMA((seqs - 1,)),
            ],
            early,
            2 * self.flops,
            {"collective_id": 5, "has_side_effects": True},
        )
        between, leaving = between_calls(leaving)
        given, made = specs(early)
        done = pl.pallas_call(
            functools.partial(later_backward_kernel, self.head_size, self.rows, early),
            name="recurrence_backward_end",
            grid=(self.blocks - early,),
            in_specs=[self.whole(self.rows, 1)] + [pl.BlockSpec(memory_space=pl.ANY)] * 4 + given,
            out_specs=made,
            out_shape=outs,
            scratch_shapes=scratch,
            input_output_aliases={1 + k: k for k in range(4)},
            compiler_params=pltpu.CompilerParams(vmem_limit_bytes=VMEM_BYTES),
            cost_estimate=pl.CostEstimate(
                flops=self.flops // 2, bytes_accessed=16 * self.flops // self.width, transcendentals=0
            ),
        )(leaving, *found, *arrays)
        return (*done, between)


def gathered(parts_ref, at):
    return jnp.concatenate([parts_ref[k, at, :] for k in range(parts_ref.shape[0])], axis=1)


def front_kernel(
    parts_ref,
    gain_ref,
    input_ref,
    gate_ref,
    dist_ref,
    par_ref,
    gates_ref,
    x_ref,
    inverse_ref,
    normed_ref,
    branch_ref,
    pre_ref,
    rim_ref,
    lru_ref,
    rate_ref,
    igate_ref,
    state_ref,
    cum_ref,
    last_ref,
    edge_ref,
    landed_ref,
    both_ref,
    send_sem,
    recv_sem,
):
    tokens = x_ref.shape[0]
    piece, tall = (64, min(tokens, 512))
    step = pl.program_id(0)
    seq, seqs = (lax.axis_index("seq"), lax.axis_size("seq"))
    barrier = pltpu.get_barrier_semaphore()

    @pl.when(step == 0)
    def _():
        before = {"seq": lax.rem(seq + seqs - 1, seqs)}
        pl.semaphore_signal(barrier, inc=1, device_id=before, device_id_type=MESH)

        def norm(index, carry):
            at = pl.ds(pl.multiple_of(index * piece, piece), piece)
            low = gathered(parts_ref, at)
            x_ref[at, :] = low
            value = low.astype(jnp.float32)
            inverse = lax.rsqrt(jnp.mean(value * value, axis=1, keepdims=True) + EPS)
            inverse_ref[at, :] = jnp.broadcast_to(inverse, (piece, LANES))
            normed_ref[at, :] = (value * inverse * gain_ref[...]).astype(jnp.bfloat16)
            return carry

        lax.fori_loop(0, tokens // piece, norm, 0, unroll=2)

    ending = jnp.dot(
        normed_ref[tokens - STEP :, :], input_ref[...], preferred_element_type=jnp.float32
    )
    edge_ref[step] = ending[STEP - SUBLANES :, :]
    rim_copy = pltpu.make_async_remote_copy(
        src_ref=edge_ref.at[step],
        dst_ref=landed_ref.at[step],
        send_sem=send_sem.at[step],
        recv_sem=recv_sem.at[step],
        device_id={"seq": lax.rem(seq + 1, seqs)},
        device_id_type=MESH,
    )

    @pl.when(step == 0)
    def _():
        pl.semaphore_wait(barrier, 1)

    rim_copy.start()

    def multiply(index, carry):
        at = pl.ds(pl.multiple_of(index * tall, tall), tall)
        normed = normed_ref[at, :]
        branch_ref[0, at, :] = jnp.dot(normed, input_ref[...], preferred_element_type=jnp.float32)
        pre_ref[0, at, :] = jnp.dot(normed, gate_ref[...], preferred_element_type=jnp.float32)
        return carry

    lax.fori_loop(0, tokens // tall, multiply, 0)
    rim_copy.wait()
    rim_ref[0] = jnp.where(seq > 0, 1.0, 0.0) * landed_ref[step]
    scan_block(
        branch_ref,
        rim_ref,
        dist_ref,
        par_ref,
        gates_ref,
        lru_ref,
        rate_ref,
        igate_ref,
        state_ref,
        cum_ref,
        last_ref,
        both_ref,
    )


def front(parts, gain, recur_input, recur_gate, dist, params, gates):
    count, tokens, width = parts.shape
    model, rec = recur_input.shape
    columns = gates.shape[1] // 2
    steps = rec // columns
    low, f32 = (jnp.bfloat16, jnp.float32)
    tall = pl.BlockSpec((model, columns), lambda j: (0, j))

    def whole(shape):
        return pl.BlockSpec(shape, lambda j: (0,) * len(shape))

    def wide(size, dtype):
        spec = pl.BlockSpec((1, size, columns), lambda j: (0, 0, j))
        return (spec, jax.ShapeDtypeStruct((1, size, rec), dtype))

    made = [wide(tokens, f32), wide(tokens, f32), wide(SUBLANES, f32), wide(tokens, low)]
    made += [wide(tokens, f32)] * 4 + [wide(2, f32)]
    return pl.pallas_call(
        front_kernel,
        name="project_and_scan",
        grid=(steps,),
        in_specs=[
            whole(parts.shape),
            whole((1, model)),
            tall,
            tall,
            whole(dist.shape),
            pl.BlockSpec((16, columns), lambda j: (0, j)),
            pl.BlockSpec((columns, 2 * columns), lambda j: (j, 0)),
        ],
        out_specs=[whole((tokens, model)), whole((tokens, LANES)), whole((tokens, model))]
        + [spec for spec, _ in made],
        out_shape=[
            jax.ShapeDtypeStruct((tokens, model), low),
            jax.ShapeDtypeStruct((tokens, LANES), f32),
            jax.ShapeDtypeStruct((tokens, model), low),
        ]
        + [shape for _, shape in made],
        scratch_shapes=[
            pltpu.VMEM((steps, SUBLANES, columns), f32),
            pltpu.VMEM((steps, SUBLANES, columns), f32),
            pltpu.VMEM((1, tokens, 2 * columns), f32),
            pltpu.SemaphoreType.DMA((steps,)),
            pltpu.SemaphoreType.DMA((steps,)),
        ],
        compiler_params=pltpu.CompilerParams(
            collective_id=3, has_side_effects=True, vmem_limit_bytes=VMEM_BYTES
        ),
        cost_estimate=pl.CostEstimate(
            flops=5 * tokens * model * rec, bytes_accessed=40 * tokens * model, transcendentals=0
        ),
    )(parts, gain[None], recur_input, recur_gate, dist, params, gates)


def middle_kernel(rows, *refs):
    (last_ref, state_hbm, cum_hbm, pre_hbm, x_ref, out_ref, gain_ref), others = by_rows(
        refs, rows, (True,) * 5 + (False,) * 2
    )
    entering_ref, mixed_ref, resid_ref, normed_ref = others[:4]
    sent_ref, got_ref, held_ref, send_sem, recv_sem, load_sem = others[4:]
    tall, model = resid_ref.shape
    step, steps = (pl.program_id(0), pl.num_programs(0))
    tiles = steps // rows
    slab = 16

    def on_row(place, act):
        for row in range(rows):

            @pl.when(lax.div(place, tiles) == row)
            def _(row=row):
                at = pl.ds(pl.multiple_of(lax.rem(place, tiles) * tall, tall), tall)
                slot = lax.rem(place, 2)
                for kind, source in enumerate((state_hbm, cum_hbm, pre_hbm)):
                    act(
                        pltpu.make_async_copy(
                            source.refs[row].at[0, at], held_ref.at[slot, kind], load_sem.at[slot, kind]
                        )
                    )

    @pl.when(step == 0)
    def _():
        on_row(step, lambda copy: copy.start())
        for row in range(rows):
            sent_ref[row] = last_ref[row]
        carried(sent_ref, got_ref, entering_ref, send_sem, recv_sem, False)

    @pl.when(step + 1 < steps)
    def _():
        on_row(step + 1, lambda copy: copy.start())

    on_row(step, lambda copy: copy.wait())
    slot = lax.rem(step, 2)
    mine = lax.div(step, tiles)

    def mix(index, carry):
        at = pl.ds(pl.multiple_of(index * slab, slab), slab)
        state = held_ref[slot, 0, at, :] + held_ref[slot, 1, at, :] * entering_ref[mine]
        pre = held_ref[slot, 2, at, :]
        inner = jnp.tanh(pre * (GELU_C + (GELU_C * GELU_A) * (pre * pre)))
        mixed_ref[at, :] = (state * (pre * (0.5 + 0.5 * inner))).astype(jnp.bfloat16)
        return carry

    lax.fori_loop(0, tall // slab, mix, 0, unroll=2)
    for row in range(rows):

        @pl.when(mine == row)
        def _(row=row):
            tile = 512
            for first in range(0, model, tile):
                at = slice(first, first + tile)
                resid_ref[:, at] = x_ref.refs[row][:, at].astype(jnp.float32) + jnp.dot(
                    mixed_ref[...], out_ref[:, at], preferred_element_type=jnp.float32
                )

    def norm(index, carry):
        at = pl.ds(pl.multiple_of(index * slab, slab), slab)
        resid = resid_ref[at, :]
        inverse = lax.rsqrt(jnp.mean(resid * resid, axis=1, keepdims=True) + EPS)
        normed_ref[at, :] = (resid * inverse * gain_ref[...]).astype(jnp.bfloat16)
        return carry

    lax.fori_loop(0, tall // slab, norm, 0, unroll=4)


def middle(last, state, cum, pre, x, recur_out, gain):
    rows = len(state)
    _, length, rec = state[0].shape
    model = recur_out.shape[1]
    tall = min(length, 256)
    tiles = length // tall
    tokens = rows * length
    seqs = lax.axis_size("seq")
    low, f32 = (jnp.bfloat16, jnp.float32)

    def whole(shape):
        return pl.BlockSpec(shape, lambda s: (0,) * len(shape), pipeline_mode=pl.Buffered(1))

    def flat(row):
        return lambda s: (jnp.clip(s - row * tiles, 0, tiles - 1), 0)

    summary = (rows, 2, rec)
    return pl.pallas_call(
        functools.partial(middle_kernel, rows),
        name="mix_and_norm",
        grid=(rows * tiles,),
        in_specs=[whole((1, 2, rec))] * rows
        + [pl.BlockSpec(memory_space=pl.ANY)] * (3 * rows)
        + [pl.BlockSpec((tall, model), flat(row)) for row in range(rows)]
        + [whole(recur_out.shape), whole((1, model))],
        out_specs=[
            pl.BlockSpec((rows, 1, rec), lambda s: (0, 0, 0)),
            pl.BlockSpec((tall, rec), lambda s: (s, 0)),
            pl.BlockSpec((tall, model), lambda s: (s, 0)),
            pl.BlockSpec((tall, model), lambda s: (s, 0)),
        ],
        out_shape=[
            jax.ShapeDtypeStruct((rows, 1, rec), f32),
            jax.ShapeDtypeStruct((tokens, rec), low),
            jax.ShapeDtypeStruct((tokens, model), f32),
            jax.ShapeDtypeStruct((tokens, model), low),
        ],
        scratch_shapes=[
            pltpu.VMEM(summary, f32),
            pltpu.VMEM((seqs,) + summary, f32),
            pltpu.VMEM((2, 3, tall, rec), f32),
            pltpu.SemaphoreType.DMA((seqs - 1,)),
            pltpu.SemaphoreType.DMA((seqs - 1,)),
            pltpu.SemaphoreType.DMA((2, 3)),
        ],
        compiler_params=pltpu.CompilerParams(
            collective_id=4, has_side_effects=True, vmem_limit_bytes=VMEM_BYTES
        ),
        cost_estimate=pl.CostEstimate(
            flops=2 * tokens * rec * model, bytes_accessed=14 * tokens * rec, transcendentals=0
        ),
    )(*last, *state, *cum, *pre, *x, recur_out, gain[None])


def hidden_kernel(
    left_ref,
    parts_ref,
    normed_ref,
    gate_ref,
    up_ref,
    down_ref,
    gout_ref,
    hidden_ref,
    dgate_ref,
    dup_ref,
):
    tokens, model = normed_ref.shape
    chunk = down_ref.shape[0]
    rows = left_ref.shape[0]
    length = tokens // rows
    slab = 32

    @pl.when(pl.program_id(0) == 0)
    def _():
        for row in range(rows):

            def collect(index, carry, row=row):
                base = pl.multiple_of(index * slab, slab)
                at = pl.ds(row * length + base, slab)
                low = gathered(parts_ref, at)
                place = base + lax.broadcasted_iota(jnp.int32, low.shape, 0)
                value = jnp.where(place < left_ref[row], low.astype(jnp.float32), 0.0)
                gout_ref[at, :] = value.astype(jnp.bfloat16)
                return carry

            lax.fori_loop(0, length // slab, collect, 0)

    tall = min(tokens, 512)
    wide = 256

    def tile(index, carry):
        at = pl.ds(pl.multiple_of(index * tall, tall), tall)
        for column in range(chunk // wide):
            own = slice(column * wide, (column + 1) * wide)
            gate = jnp.dot(normed_ref[at, :], gate_ref[:, own], preferred_element_type=jnp.float32)
            up = jnp.dot(normed_ref[at, :], up_ref[:, own], preferred_element_type=jnp.float32)
            dhid = lax.dot_general(
                gout_ref[at, :],
                down_ref[own, :],
                (((1,), (1,)), ((), ())),
                preferred_element_type=jnp.float32,
            )
            act, slope = gelu_pair(gate)
            hidden_ref[at, own] = (act * up).astype(jnp.bfloat16)
            dgate_ref[at, own] = (dhid * up * slope).astype(jnp.bfloat16)
            dup_ref[at, own] = (dhid * act).astype(jnp.bfloat16)
        return carry

    lax.fori_loop(0, tokens // tall, tile, 0)


def back_kernel(
    hidden_ref,
    dgate_ref,
    dup_ref,
    gout_hbm,
    resid_hbm,
    gain_ref,
    gate_ref,
    up_ref,
    down_ref,
    result_ref,
    dres_ref,
    total_ref,
    back_ref,
    gout_ref,
    resid_ref,
    load_sem,
):
    tall, model = (hidden_ref.shape[0], gout_ref.shape[1])
    step, tile = (pl.program_id(0), pl.program_id(1))
    wide = 512
    contract = (((1,), (1,)), ((), ()))
    rows = pl.ds(pl.multiple_of(tile * tall, tall), tall)

    def loads():
        return (
            pltpu.make_async_copy(gout_hbm, gout_ref, load_sem.at[0]),
            pltpu.make_async_copy(resid_hbm, resid_ref, load_sem.at[1]),
        )

    @pl.when((step == 0) & (tile == 0))
    def _():
        for load in loads():
            load.start()

    def products(own):
        forth = jnp.dot(hidden_ref[...], down_ref[:, own], preferred_element_type=jnp.float32)
        back = lax.dot_general(
            dgate_ref[...], gate_ref[own, :], contract, preferred_element_type=jnp.float32
        ) + lax.dot_general(
            dup_ref[...], up_ref[own, :], contract, preferred_element_type=jnp.float32
        )
        return (forth, back)

    @pl.when(step == 0)
    def _():
        for first in range(0, model, wide):
            own = slice(first, first + wide)
            forth, back = products(own)
            total_ref[rows, own] = forth
            back_ref[rows, own] = back

    @pl.when(step > 0)
    def _():
        for first in range(0, model, wide):
            own = slice(first, first + wide)
            forth, back = products(own)
            total_ref[rows, own] += forth
            back_ref[rows, own] += back

    @pl.when((step == pl.num_programs(0) - 1) & (tile == 0))
    def _():
        for load in loads():
            load.wait()

    @pl.when(step == pl.num_programs(0) - 1)
    def _():
        parts, width = (result_ref.shape[0], result_ref.shape[2])
        small = 16

        def finish(index, carry):
            at = pl.ds(pl.multiple_of(tile * tall + index * small, small), small)
            resid = resid_ref[at, :]
            result = (resid + total_ref[at, :]).astype(jnp.bfloat16)
            for part in range(parts):
                result_ref[part, at, :] = result[:, part * width : (part + 1) * width]
            inverse = lax.rsqrt(jnp.mean(resid * resid, axis=1, keepdims=True) + EPS)
            normed = resid * inverse
            scaled = back_ref[at, :] * gain_ref[...]
            mean = jnp.mean(scaled * normed, axis=1, keepdims=True)
            dres = gout_ref[at, :].astype(jnp.float32) + inverse * (scaled - normed * mean)
            dres_ref[at, :] = dres.astype(jnp.bfloat16)
            return carry

        lax.fori_loop(0, tall // small, finish, 0, unroll=4)


MLP_CHUNK = 768


def resident(shape):
    return pl.BlockSpec(shape, lambda s: (0,) * len(shape), pipeline_mode=pl.Buffered(1))


def mlp_specs(tokens, model):
    columns = pl.BlockSpec((model, MLP_CHUNK), lambda s: (0, s))
    down = pl.BlockSpec((MLP_CHUNK, model), lambda s: (s, 0))
    made = pl.BlockSpec((tokens, MLP_CHUNK), lambda s: (0, s))
    return ([columns, columns, down], [made] * 3)


def mlp_hidden(left, parts, normed, mlp_gate, mlp_up, mlp_down):
    tokens, model = normed.shape
    ffn = mlp_gate.shape[1]
    low = jnp.bfloat16
    weights, made = mlp_specs(tokens, model)
    tall = jax.ShapeDtypeStruct((tokens, ffn), low)
    return pl.pallas_call(
        hidden_kernel,
        name="mlp_hidden",
        grid=(ffn // MLP_CHUNK,),
        in_specs=[
            pl.BlockSpec(memory_space=pltpu.SMEM),
            resident(parts.shape),
            resident(normed.shape),
            *weights,
        ],
        out_specs=[resident((tokens, model)), *made],
        out_shape=[jax.ShapeDtypeStruct((tokens, model), low), tall, tall, tall],
        compiler_params=pltpu.CompilerParams(vmem_limit_bytes=VMEM_BYTES),
        cost_estimate=pl.CostEstimate(
            flops=6 * tokens * model * ffn,
            bytes_accessed=6 * (model + tokens) * ffn + 6 * tokens * model,
            transcendentals=0,
        ),
    )(left, parts, normed, mlp_gate, mlp_up, mlp_down)


def mlp_back(hidden, dgate, dup, gout, resid, gain, mlp_gate, mlp_up, mlp_down, parts_shape):
    tokens, model = resid.shape
    ffn = mlp_gate.shape[1]
    low, f32 = (jnp.bfloat16, jnp.float32)
    chunk, tall = (1024, min(tokens, 512))

    def resident(shape):
        return pl.BlockSpec(shape, lambda s, t: (0,) * len(shape), pipeline_mode=pl.Buffered(1))

    columns = pl.BlockSpec((model, chunk), lambda s, t: (0, s))
    down = pl.BlockSpec((chunk, model), lambda s, t: (s, 0))
    made = pl.BlockSpec((tall, chunk), lambda s, t: (t, s))
    return pl.pallas_call(
        back_kernel,
        name="mlp_back",
        grid=(ffn // chunk, tokens // tall),
        in_specs=[
            made,
            made,
            made,
            pl.BlockSpec(memory_space=pl.ANY),
            pl.BlockSpec(memory_space=pl.ANY),
            resident((1, model)),
            columns,
            columns,
            down,
        ],
        out_specs=[resident(parts_shape), resident((tokens, model))],
        out_shape=[
            jax.ShapeDtypeStruct(parts_shape, low),
            jax.ShapeDtypeStruct((tokens, model), low),
        ],
        scratch_shapes=[
            pltpu.VMEM((tokens, model), f32),
            pltpu.VMEM((tokens, model), f32),
            pltpu.VMEM((tokens, model), low),
            pltpu.VMEM((tokens, model), f32),
            pltpu.SemaphoreType.DMA((2,)),
        ],
        compiler_params=pltpu.CompilerParams(vmem_limit_bytes=VMEM_BYTES),
        cost_estimate=pl.CostEstimate(
            flops=6 * tokens * model * ffn,
            bytes_accessed=6 * (model + tokens) * ffn + 10 * tokens * model,
            transcendentals=0,
        ),
    )(hidden, dgate, dup, gout, resid, gain[None], mlp_gate, mlp_up, mlp_down)


def outputs_kernel(
    device_ref,
    own_ref,
    gate_sum,
    in_sum,
    out_sum,
    small_ref,
    input_ref,
    gate_ref,
    mlp_gate_ref,
    mlp_up_ref,
    gain1_ref,
    gain2_ref,
    sum_gain1,
    sum_in,
    sum_gate,
    sum_taps,
    sum_bias,
    sum_lgates,
    sum_lbias,
    sum_decay,
    sum_out,
    sum_gain2,
    sum_mgate,
    sum_mup,
    sum_down,
):
    rows = sum_mgate.shape[0]
    model = own_ref.shape[1]
    parts = sum_mgate.shape[1] // model
    for part in range(parts):
        at = slice(part * model, (part + 1) * model)
        sum_mgate[:, at] = own_ref[part * rows : (part + 1) * rows, :].astype(jnp.float32)
        sum_mup[:, at] = own_ref[(parts + part) * rows : (parts + part + 1) * rows, :].astype(
            jnp.float32
        )
    sum_down[...] = own_ref[2 * parts * rows :, :].astype(jnp.float32)

    def weighed(*pairs):
        return sum(
            jnp.sum(weight[...].astype(jnp.float32) * gradient[...], axis=1, keepdims=True)
            for weight, gradient in pairs
        )

    def as_row(column, gain):
        lane = lax.broadcasted_iota(jnp.int32, (rows, LANES), 1)
        place = lax.broadcasted_iota(jnp.int32, (rows, LANES), 0)
        whole = lax.broadcasted_iota(jnp.int32, (rows, model), 1)
        own = device_ref[0] * rows + lax.broadcasted_iota(jnp.int32, (rows, model), 0)
        own_gain = jnp.sum(jnp.where(whole == own, gain[...], 0.0), axis=1, keepdims=True)
        return jnp.sum(jnp.where(lane == place, column / own_gain, 0.0), axis=0, keepdims=True)

    row1 = as_row(weighed((input_ref, in_sum), (gate_ref, gate_sum)), gain1_ref)
    row2 = as_row(weighed((mlp_gate_ref, sum_mgate), (mlp_up_ref, sum_mup)), gain2_ref)
    sum_gain1[...] = row1[:, :rows]
    sum_gain2[...] = row2[:, :rows]
    sum_in[...] = in_sum[...]
    sum_gate[...] = gate_sum[...]
    sum_out[...] = out_sum[...]
    channels = small_ref.shape[0]
    size = sum_lgates.shape[1] // 2
    first, second = (small_ref[:, :LANES], small_ref[:, LANES:])
    lane = lax.broadcasted_iota(jnp.int32, (channels, LANES), 1)
    moved = pltpu.roll(second, size, 1)
    sum_lgates[:, :LANES] = jnp.where(lane < size, first, moved)
    sum_lgates[:, LANES:] = moved[:, : 2 * size - LANES]
    filled = jnp.concatenate([first, jnp.zeros((LANES - channels, LANES), jnp.float32)], axis=0)
    turned = filled.T
    sum_taps[...] = turned[size : size + 4, :channels]
    sum_bias[...] = turned[size + 4 : size + 5, :channels]
    sum_lbias[...] = turned[size + 5 : size + 7, :channels]
    sum_decay[...] = turned[size + 7 : size + 8, :channels]


def outputs(
    device, own, gate_sum, in_sum, out_sum, small, recur_input, recur_gate, mlp_gate, mlp_up, gain1, gain2, size
):
    rows, rec = in_sum.shape
    model, ffn = mlp_gate.shape
    channels = small.shape[0]
    f32 = jnp.float32

    def whole(shape):
        return pl.BlockSpec(shape, lambda s, device: (0,) * len(shape))

    def mine(shape):
        return pl.BlockSpec(shape, lambda s, device: (device[0], 0))

    given = (own, gate_sum, in_sum, out_sum, small)
    shapes = [(1, rows), (rows, rec), (rows, rec), (4, channels), (1, channels)]
    shapes += [(channels, 2 * size), (2, channels), (1, channels), out_sum.shape, (1, rows)]
    shapes += [(rows, ffn), (rows, ffn), (own.shape[0] - 2 * ffn // model * rows, model)]
    return pl.pallas_call(
        outputs_kernel,
        name="outputs",
        grid_spec=pltpu.PrefetchScalarGridSpec(
            num_scalar_prefetch=1,
            grid=(1,),
            in_specs=[whole(a.shape) for a in given]
            + [mine((rows, rec))] * 2
            + [mine((rows, ffn))] * 2
            + [whole((1, model))] * 2,
            out_specs=[whole(shape) for shape in shapes],
        ),
        out_shape=[jax.ShapeDtypeStruct(shape, f32) for shape in shapes],
        compiler_params=pltpu.CompilerParams(vmem_limit_bytes=VMEM_BYTES),
    )(
        device[None],
        *given,
        recur_input,
        recur_gate,
        mlp_gate,
        mlp_up,
        gain1[None],
        gain2[None],
    )


def spread_kernel(whole_ref, out_ref):
    out_ref[0] = whole_ref[...]


def spread(whole, count):
    tokens, width = (whole.shape[0], whole.shape[1] // count)
    return pl.pallas_call(
        spread_kernel,
        name="spread_features",
        grid=(count,),
        in_specs=[pl.BlockSpec((tokens, width), lambda j: (0, j))],
        out_specs=pl.BlockSpec((1, tokens, width), lambda j: (j, 0, 0)),
        out_shape=jax.ShapeDtypeStruct((count, tokens, width), whole.dtype),
        cost_estimate=pl.CostEstimate(
            flops=0, bytes_accessed=4 * tokens * whole.shape[1], transcendentals=0
        ),
    )(whole)


CHAN = ("zed", "core")


def features_in(local, pick=slice(None)):
    count = lax.axis_size(CHAN)
    rows, length, width = local.shape
    local = local.reshape(count, rows // count, length, width)[:, pick]
    if width % LANES == 0:
        return lax.all_to_all(local, CHAN, 0, 0, tiled=True).reshape(count, -1, width)
    moved = lax.all_to_all(
        local.reshape(-1, length, width), CHAN, split_axis=0, concat_axis=2, tiled=True
    )
    return moved.reshape(1, -1, count * width)


def features_apart(whole):
    count = lax.axis_size(CHAN)
    if (whole.shape[1] // count) % LANES == 0:
        return spread(whole, count)
    return whole[None]


def features_out(parts, rows):
    blocks, tokens, width = parts.shape
    parts = parts.reshape(blocks, rows, tokens // rows, width)
    if blocks > 1:
        moved = lax.all_to_all(parts, CHAN, 0, 0, tiled=True)
        return moved.reshape(-1, *parts.shape[2:])
    return lax.all_to_all(parts[0], CHAN, split_axis=2, concat_axis=0, tiled=True)


class Corners:
    def __init__(self, seq, zed):
        self.seq_bits, self.zed_bits = (seq.bit_length() - 1, zed.bit_length() - 1)
        self.count = self.seq_bits + self.zed_bits
        self.dims = (2,) * self.count
        self.low = tuple(range(self.seq_bits))[::-1] + tuple(range(self.seq_bits, self.count))[::-1]
        self.high = tuple(range(self.seq_bits)) + tuple(range(self.seq_bits, self.count))[::-1]

    def place(self, dim):
        if dim < self.seq_bits:
            return ("seq", 2 ** (self.seq_bits - 1 - dim))
        return ("zed", 2 ** (self.count - 1 - dim))

    def bit(self, dim):
        axis, weight = self.place(dim)
        return lax.rem(lax.div(lax.axis_index(axis), weight), 2)

    def partner(self, dim):
        axis, weight = self.place(dim)
        return {axis: lax.axis_index(axis) + weight * (1 - 2 * self.bit(dim))}


def tail_kernel(
    corners,
    orders,
    dgate_hbm,
    dbranch_hbm,
    ending_ref,
    leading_ref,
    mixed_hbm,
    dres_hbm,
    gain_ref,
    input_hbm,
    gate_hbm,
    small_hbm,
    *refs,
):
    rows = ending_ref.shape[0]
    normed_hbms, x_hbms, inverse_hbms = (refs[k * rows : (k + 1) * rows] for k in range(3))
    tokens_ref, sum_gate, sum_out, sum_in, sum_small = refs[3 * rows : 3 * rows + 5]
    refs = refs[3 * rows + 5 :]
    stages = corners.count + 1
    dgate, dbranch, mixed, dres, normed, x, inverse, weight_in, weight_gate = refs[:9]
    made_in, made_out, own_small, back, parts, rim = refs[9:15]
    slots_in, slots_out, slots_small = (
        refs[15 + k * stages : 15 + (k + 1) * stages] for k in range(3)
    )
    (
        send_sem,
        recv_sem,
        load_sem,
        move_send,
        move_recv,
        keep_sem,
        rim_send,
        rim_recv,
    ) = refs[15 + 3 * stages :]
    seq, zed, core = (lax.axis_index(axis) for axis in ("seq", "zed", "core"))
    seqs, group = (lax.axis_size("seq"), 2 * lax.axis_size("zed"))
    mine = zed * 2 + core
    length = tokens_ref.shape[1]
    model = x.shape[1]

    def member(index):
        return {"zed": lax.div(index, 2), "core": lax.rem(index, 2)}

    def by_row(sources, target):
        return [
            (source, target.at[pl.ds(row * length, length)]) for row, source in enumerate(sources)
        ]

    pairs = [
        (dbranch_hbm, dbranch),
        (input_hbm, weight_in),
        (dgate_hbm, dgate),
        (gate_hbm, weight_gate),
        *by_row(x_hbms, x),
        *by_row(inverse_hbms, inverse),
        (dres_hbm, dres),
        *by_row(normed_hbms, normed),
        (mixed_hbm, mixed),
        (small_hbm.at[(slice(None),) * corners.count + (core,)], own_small),
    ]
    kinds = []
    for name in ('dbranch', 'win', 'dgate', 'wgate', 'x', 'inverse', 'dres', 'normed', 'mixed', 'small'):
        kinds += [name] * (rows if name in ("normed", "x", "inverse") else 1)
    loads = [
        pltpu.make_async_copy(source, target, load_sem.at[place])
        for place, (source, target) in enumerate(pairs)
    ]
    for load in loads:
        load.start()

    barrier = pltpu.get_barrier_semaphore()
    for other in range(1, group):
        pl.semaphore_signal(
            barrier, inc=1, device_id=member(lax.rem(mine + other, group)), device_id_type=MESH
        )
    for other in range(1, seqs):
        pl.semaphore_signal(
            barrier, inc=1, device_id={"seq": lax.rem(seq + other, seqs)}, device_id_type=MESH
        )
    pl.semaphore_wait(barrier, group - 1 + seqs - 1)

    rim_copy = pltpu.make_async_remote_copy(
        src_ref=leading_ref,
        dst_ref=rim,
        send_sem=rim_send,
        recv_sem=rim_recv,
        device_id={"seq": lax.rem(seq + seqs - 1, seqs)},
        device_id_type=MESH,
    )
    rim_copy.start()

    def own(stream, index):
        if stream < 4:
            return made_in.at[(stream,) + index + (core,)]
        if stream < 6:
            return made_out.at[(stream - 4,) + index + (core,)]
        return own_small.at[index]

    def slot(stream, stage):
        if stream < 4:
            return slots_in[stage].at[stream]
        if stream < 6:
            return slots_out[stage].at[stream - 4]
        return slots_small[stage]

    def copy(stream, stage):
        order = orders[stream]
        every = (slice(None),) * corners.count
        if stage == 0:
            if stream < 4:
                source = made_in.at[(stream,) + every + (1 - core,)]
            elif stream < 6:
                source = made_out.at[(stream - 4,) + every + (1 - core,)]
            else:
                source = small_hbm.at[every + (1 - core,)]
            target = {"core": 1 - core}
        else:
            dim = order[stage - 1]
            fixed = {before: corners.bit(before) for before in order[: stage - 1]}
            fixed[dim] = 1 - corners.bit(dim)
            source = own(stream, tuple(fixed.get(d, slice(None)) for d in range(corners.count)))
            target = corners.partner(dim)
        return pltpu.make_async_remote_copy(
            src_ref=source,
            dst_ref=slot(stream, stage),
            send_sem=send_sem.at[stream, stage],
            recv_sem=recv_sem.at[stream, stage],
            device_id=target,
            device_id_type=MESH,
        )

    sums = [
        sum_gate.at[:, : sum_gate.shape[1] // 2],
        sum_gate.at[:, sum_gate.shape[1] // 2 :],
        sum_in.at[:, : sum_in.shape[1] // 2],
        sum_in.at[:, sum_in.shape[1] // 2 :],
        sum_out.at[:, : sum_out.shape[1] // 2],
        sum_out.at[:, sum_out.shape[1] // 2 :],
        sum_small,
    ]

    def advance(stream, stage):
        order = orders[stream]
        copy(stream, stage).wait_recv()
        left = [dim for dim in range(corners.count) if dim not in order[:stage]]
        fixed = {dim: corners.bit(dim) for dim in order[:stage]}
        arrived = slot(stream, stage)
        if not left:
            index = tuple(fixed[dim] for dim in range(corners.count))
            sums[stream][...] = own(stream, index)[...].astype(jnp.float32) + arrived[...].astype(
                jnp.float32
            )
            return

        def add(index, carry):
            part = {
                dim: lax.rem(lax.div(index, 2 ** (len(left) - 1 - place)), 2)
                for place, dim in enumerate(left)
            }
            kept = own(stream, tuple({**fixed, **part}[dim] for dim in range(corners.count)))
            total = kept[...].astype(jnp.float32) + arrived[
                tuple(part[dim] for dim in left)
            ].astype(jnp.float32)
            kept[...] = total.astype(jnp.bfloat16)
            return carry

        lax.fori_loop(0, 2 ** len(left), add, 0)
        copy(stream, stage + 1).start()

    def move(other, row):
        to = lax.rem(mine + other, group)
        return pltpu.make_async_remote_copy(
            src_ref=parts.at[to, pl.ds(row * length, length)],
            dst_ref=tokens_ref.at[mine * rows + row],
            send_sem=move_send.at[other - 1, row],
            recv_sem=move_recv.at[other - 1, row],
            device_id=member(to),
            device_id_type=MESH,
        )

    def keep(row):
        return pltpu.make_async_copy(
            parts.at[mine, pl.ds(row * length, length)],
            tokens_ref.at[mine * rows + row],
            keep_sem.at[row],
        )

    tile = 256
    width = parts.shape[2]

    def back_row(row):
        at_row = slice(row * length, (row + 1) * length)

        def product(index, carry):
            at = pl.ds(pl.multiple_of(index * tile, tile), tile)
            contract = (((1,), (1,)), ((), ()))
            back[:, at] = lax.dot_general(
                dbranch[at_row, :], weight_in[at, :], contract, preferred_element_type=jnp.float32
            ) + lax.dot_general(
                dgate[at_row, :], weight_gate[at, :], contract, preferred_element_type=jnp.float32
            )
            return carry

        lax.fori_loop(0, model // tile, product, 0)
        slab = 16

        def norm(index, carry):
            base = pl.multiple_of(index * slab, slab)
            at = pl.ds(row * length + base, slab)
            inv = inverse[at, :1]
            value = x[at, :].astype(jnp.float32) * inv
            scaled = back[pl.ds(base, slab), :] * gain_ref[...]
            mean = jnp.mean(scaled * value, axis=1, keepdims=True)
            grad = dres[at, :].astype(jnp.float32) + inv * (scaled - value * mean)
            grad = grad.astype(jnp.bfloat16)
            for part in range(parts.shape[0]):
                parts[part, at, :] = grad[:, part * width : (part + 1) * width]
            return carry

        lax.fori_loop(0, length // slab, norm, 0, unroll=4)
        for other in range(1, group):
            move(other, row).start()
        keep(row).start()

    def weight_product(left, right, made, stream, first):
        columns = made.shape[-1]
        shape = made.shape[1:-1]

        def product(index, carry):
            at = pl.ds(pl.multiple_of(index * tile, tile), tile)
            source = pl.ds(pl.multiple_of(first + index * tile, tile), tile)
            part = lax.dot_general(
                left[...],
                right[:, source],
                (((0,), (0,)), ((), ())),
                preferred_element_type=jnp.float32,
            )
            made[(stream,) + (slice(None),) * len(shape) + (at,)] = part.astype(
                jnp.bfloat16
            ).reshape(shape + (tile,))
            return carry

        lax.fori_loop(0, columns // tile, product, 0)

    half, half_out = (made_in.shape[-1], made_out.shape[-1])
    waited, reached = (set(), {})

    def need(*names):
        for place, name in enumerate(kinds):
            if name in names and place not in waited:
                waited.add(place)
                loads[place].wait()

    def fix_rim():
        need("dbranch")
        rim_copy.wait()
        live = jnp.where(seq < seqs - 1, 1.0, 0.0)
        for row in range(rows):
            at = slice((row + 1) * length - STEP, (row + 1) * length)
            inside = dbranch[at, :].astype(jnp.float32)
            last = ending_ref[row] + live * rim[row]
            dbranch[at, :] = jnp.concatenate([inside[: STEP - SUBLANES], last], axis=0).astype(
                jnp.bfloat16
            )

    def begin(stream):
        copy(stream, 0).start()
        reached[stream] = 0

    def progress(streams):
        for stream in streams:
            if stream in reached and reached[stream] < stages:
                if stream == 6:
                    need("small")
                advance(stream, reached[stream])
                reached[stream] += 1

    def compute(item):
        if item == "gate":
            need("normed", "dgate")
            for stream in (0, 1):
                weight_product(normed, dgate, made_in, stream, stream * half)
                begin(stream)
        elif item == "out":
            need("mixed", "dres")
            for stream in (4, 5):
                weight_product(mixed, dres, made_out, stream - 4, (stream - 4) * half_out)
                begin(stream)
        elif item == "in":
            need("normed", "dbranch")
            for stream in (2, 3):
                weight_product(normed, dbranch, made_in, stream, (stream - 2) * half)
                begin(stream)
        else:
            need("dbranch", "dgate", "win", "wgate", "x", "inverse", "dres")
            back_row(item)

    begin(6)
    fix_rim()
    compute(0)
    compute(1)
    compute('gate')
    progress((6,))
    compute('out')
    progress((0, 1))
    compute('in')
    progress((0, 1))
    progress((4, 5))
    progress((6,))
    while any(reached[stream] < stages for stream in range(7)):
        progress((0, 1, 4, 5, 2, 3, 6))
    for stage in range(stages):
        for stream in range(7):
            copy(stream, stage).wait_send()
    for row in range(rows):
        for other in range(1, group):
            move(other, row).wait()
        keep(row).wait()


def tail(dgate, dbranch, ending, leading, mixed, dres, gain, w_in, w_gate, small, normed, x, inverse):
    corners = Corners(lax.axis_size("seq"), lax.axis_size("zed"))
    group, devices = (lax.axis_size(CHAN), 2 ** (corners.count + 1))
    tokens, model = dres.shape
    rec = dgate.shape[1]
    rows = ending.shape[0]
    length, width = (tokens // rows, model // group)
    low, f32 = (jnp.bfloat16, jnp.float32)
    stages = corners.count + 1
    in_rows, out_rows = (model // devices, rec // devices)
    small = small.reshape(corners.dims + (2, out_rows, small.shape[1]))
    orders = [corners.low, corners.high] * 3 + [corners.low]

    def slots(lead, shape):
        return [pltpu.VMEM(lead + (2,) * (corners.count - k) + shape, low) for k in range(stages)]

    in_shape, out_shape = ((in_rows, rec // 2), (out_rows, model // 2))
    loaded = (dgate, dbranch, mixed, dres, dres, dres)
    loaded += (jax.ShapeDtypeStruct((tokens, LANES), f32), w_in, w_gate)
    anyplace = pl.BlockSpec(memory_space=pl.ANY)
    vmem = pl.BlockSpec(memory_space=pltpu.VMEM)
    dma = pltpu.SemaphoreType.DMA
    moved = sum(math.prod(a.shape) * a.dtype.itemsize for a in loaded)
    return pl.pallas_call(
        functools.partial(tail_kernel, corners, orders),
        name="tail",
        in_specs=[anyplace, anyplace, vmem, vmem, anyplace, anyplace, vmem]
        + [anyplace] * (3 + 3 * rows),
        out_specs=[anyplace] + [vmem] * 4,
        out_shape=[
            jax.ShapeDtypeStruct((group * rows, length, width), low),
            jax.ShapeDtypeStruct((in_rows, rec), f32),
            jax.ShapeDtypeStruct((out_rows, model), f32),
            jax.ShapeDtypeStruct((in_rows, rec), f32),
            jax.ShapeDtypeStruct(small.shape[-2:], f32),
        ],
        scratch_shapes=[pltpu.VMEM(a.shape, a.dtype) for a in loaded]
        + [
            pltpu.VMEM((4,) + corners.dims + (2,) + in_shape, low),
            pltpu.VMEM((2,) + corners.dims + (2,) + out_shape, low),
            pltpu.VMEM(corners.dims + small.shape[-2:], low),
            pltpu.VMEM((length, model), f32),
            pltpu.VMEM((group, tokens, width), low),
            pltpu.VMEM(leading.shape, leading.dtype),
        ]
        + slots((4,), in_shape)
        + slots((2,), out_shape)
        + slots((), small.shape[-2:])
        + [
            dma((7, stages)),
            dma((7, stages)),
            dma((7 + 3 * rows,)),
            dma((group - 1, rows)),
            dma((group - 1, rows)),
            dma((rows,)),
            dma,
            dma,
        ],
        compiler_params=pltpu.CompilerParams(
            collective_id=1, has_side_effects=True, vmem_limit_bytes=60 * 1024 * 1024
        ),
        cost_estimate=pl.CostEstimate(
            flops=10 * tokens * model * rec, bytes_accessed=2 * moved, transcendentals=0
        ),
    )(dgate, dbranch, ending, leading, mixed, dres, gain[None], w_in, w_gate, small, *normed, *x, *inverse)


def grads_kernel(
    normed_ref,
    dgate_ref,
    dup_ref,
    hidden_ref,
    gout_ref,
    out_ref,
    turned_ref,
    made_wide,
    made_down,
    come_wide,
    come_down,
    send_sem,
    recv_sem,
    store_sem,
):
    step = pl.program_id(0)
    core = lax.axis_index("core")
    other = {"core": 1 - core}
    wide_rows, down_rows = (made_wide.shape[3], made_down.shape[3])
    wides, downs = (come_wide.shape[0], come_down.shape[0])
    total = wides + downs
    down_at = wides * wide_rows

    def exchange(made, come, index, slot):
        return pltpu.make_async_remote_copy(
            src_ref=made.at[lax.rem(index, 2), 1 - core],
            dst_ref=come.at[index],
            send_sem=send_sem.at[slot],
            recv_sem=recv_sem.at[slot],
            device_id=other,
            device_id_type=MESH,
        )

    def store_wide(index):
        return pltpu.make_async_copy(
            come_wide.at[index],
            out_ref.at[:, pl.ds(pl.multiple_of(index * wide_rows, wide_rows), wide_rows)],
            store_sem.at[index],
        )

    def store_down(index):
        chips = come_down.shape[1]
        return pltpu.make_async_copy(
            come_down.at[index],
            out_ref.at[pl.ds(index * chips, chips), pl.ds(down_at, down_rows)],
            store_sem.at[index + wides],
        )

    @pl.when(step == 0)
    def _():
        barrier = pltpu.get_barrier_semaphore()
        pl.semaphore_signal(barrier, inc=1, device_id=other, device_id_type=MESH)
        pl.semaphore_wait(barrier, 1)
        turned_ref[...] = normed_ref[...].T

    def product_wide(source, index):
        made = made_wide.at[lax.rem(index, 2)]
        chips, rows = (made.shape[1], made.shape[2])
        tile = 512

        def column(place, carry):
            at = pl.ds(pl.multiple_of(place * tile, tile), tile)
            part = jnp.dot(turned_ref[...], source[:, at], preferred_element_type=jnp.float32)
            part = part.astype(jnp.bfloat16).reshape(chips, 2, rows, tile)
            made[0, :, :, at] = part[:, 0]
            made[1, :, :, at] = part[:, 1]
            return carry

        lax.fori_loop(0, source.shape[1] // tile, column, 0)

    def product_tall(left, right, made_all, index):
        made = made_all.at[lax.rem(index, 2)]
        chips, rows = (made.shape[1], made.shape[2])
        tile = 512

        def column(place, carry):
            at = pl.ds(pl.multiple_of(place * tile, tile), tile)
            part = lax.dot_general(
                left[...], right[:, at], (((0,), (0,)), ((), ())), preferred_element_type=jnp.float32
            )
            part = part.astype(jnp.bfloat16).reshape(chips, 2, rows, tile)
            made[0, :, :, at] = part[:, 0]
            made[1, :, :, at] = part[:, 1]
            return carry

        lax.fori_loop(0, right.shape[1] // tile, column, 0)

    half = wides // 2

    @pl.when(step < half)
    def _():
        product_wide(dgate_ref, step)

    @pl.when((step >= half) & (step < wides))
    def _():
        product_wide(dup_ref, step)

    @pl.when(step < wides)
    def _():
        exchange(made_wide, come_wide, step, step).start()

    @pl.when((step >= wides) & (step < total))
    def _():
        product_tall(hidden_ref, gout_ref, made_down, step - wides)
        exchange(made_down, come_down, step - wides, step).start()

    def finish(made, come, index, slot, store):
        exchange(made, come, index, slot).wait()
        mine = made.at[lax.rem(index, 2), core]
        arrived = come.at[index]

        def add(chip, carry):
            both = mine[chip].astype(jnp.float32) + arrived[chip].astype(jnp.float32)
            arrived[chip] = both.astype(jnp.bfloat16)
            return carry

        lax.fori_loop(0, come.shape[1], add, 0)
        store(index).start()

    before = step - 1

    @pl.when((before >= 0) & (before < wides))
    def _():
        finish(made_wide, come_wide, before, before, store_wide)

    @pl.when(before >= wides)
    def _():
        finish(made_down, come_down, before - wides, before, store_down)

    @pl.when(step == total)
    def _():
        for index in range(wides):
            store_wide(index).wait()
        for index in range(downs):
            store_down(index).wait()


def block_gradients(normed, dgate, dup, hidden, gout):
    tokens, model = normed.shape
    ffn = hidden.shape[1]
    chips = lax.axis_size("seq") * lax.axis_size("zed")
    devices = 2 * chips
    wide_rows, down_rows = (model // devices, ffn // devices)
    chunk = 768
    wides, downs = (2 * ffn // model, ffn // chunk)
    half = wides // 2
    down_chips = chunk // (2 * down_rows)
    rows = wides * wide_rows + down_rows
    low = jnp.bfloat16

    def whole(array):
        return pl.BlockSpec(array.shape, lambda s: (0, 0), pipeline_mode=pl.Buffered(1))

    def part(columns, first, count):
        return pl.BlockSpec((tokens, columns), lambda s: (0, jnp.clip(s - first, 0, count - 1)))

    total = wides + downs
    flops = 6 * tokens * model * ffn
    arrays = (normed, dgate, dup, hidden, gout)
    moved = sum(math.prod(a.shape) * 2 for a in arrays) + chips * rows * model * 2
    return pl.pallas_call(
        grads_kernel,
        name="block_gradients",
        grid=(total + 1,),
        in_specs=[
            whole(normed),
            part(model, 0, half),
            part(model, half, half),
            part(chunk, wides, downs),
            whole(gout),
        ],
        out_specs=pl.BlockSpec(memory_space=pl.ANY),
        out_shape=jax.ShapeDtypeStruct((chips, rows, model), low),
        scratch_shapes=[
            pltpu.VMEM((model, tokens), low),
            pltpu.VMEM((2, 2, chips, wide_rows, model), low),
            pltpu.VMEM((2, 2, down_chips, down_rows, model), low),
            pltpu.VMEM((wides, chips, wide_rows, model), low),
            pltpu.VMEM((downs, down_chips, down_rows, model), low),
            pltpu.SemaphoreType.DMA((total,)),
            pltpu.SemaphoreType.DMA((total,)),
            pltpu.SemaphoreType.DMA((total,)),
        ],
        compiler_params=pltpu.CompilerParams(
            collective_id=2, has_side_effects=True, vmem_limit_bytes=VMEM_BYTES
        ),
        cost_estimate=pl.CostEstimate(flops=flops, bytes_accessed=moved, transcendentals=0),
    )(*arrays)


def passed_along(value, axis, steps):
    count = lax.axis_size(axis)
    leading, last = (max(0, -steps), min(count, count - steps))
    return lax.ppermute(value, axis, [(source, source + steps) for source in range(leading, last)])


def weight_grad(left, right):
    return lax.dot_general(
        left, right, (((0,), (0,)), ((), ())), preferred_element_type=jnp.float32
    ).astype(jnp.bfloat16)


def back_dot(left, right):
    return lax.dot_general(
        left, right, (((1,), (1,)), ((), ())), preferred_element_type=jnp.float32
    )


def fwd_dot(left, right):
    return jnp.dot(left, right, preferred_element_type=jnp.float32)


def gelu_fn(value):
    return jax.nn.gelu(value, approximate=True)


def norm_back(grad_norm, normed, inverse, gain):
    scaled = grad_norm * gain
    mean_term = jnp.mean(scaled * normed, axis=1, keepdims=True)
    return inverse * (scaled - normed * mean_term)


def scattered(gradient):
    return lax.psum_scatter(
        gradient, ("seq", "zed", "core"), scatter_dimension=0, tiled=True
    ).astype(jnp.float32)


def body(
    tokens,
    cotangent,
    doc_starts,
    lengths,
    norm1_gain,
    recur_input,
    recur_gate,
    conv_kernel,
    conv_bias,
    lru_gates,
    lru_bias,
    lru_decay,
    recur_out,
    norm2_gain,
    mlp_gate,
    mlp_up,
    mlp_down,
):
    count = lax.axis_size(CHAN)
    row_count, block_len = (tokens.shape[0] // count, tokens.shape[1])
    model_dim = tokens.shape[2] * count
    tok_count = row_count * block_len
    rec_width = recur_input.shape[1]
    ffn_width = mlp_gate.shape[1]
    head_count = H
    head_size = rec_width // head_count
    tap_count = conv_kernel.shape[0]
    rim_size = tap_count - 1
    seq_index = lax.axis_index("seq")
    position = seq_index * block_len + jnp.arange(block_len, dtype=jnp.int32)
    bounds = jnp.concatenate([doc_starts, lengths[:, None]], axis=1)
    is_before = bounds[:, None, :] <= position[None, :, None]
    seg_start = jnp.max(jnp.where(is_before, bounds[:, None, :], 0), axis=2)
    dist = jnp.broadcast_to(
        (position[None, :] - seg_start)[:, :, None], (row_count, block_len, LANES)
    )
    soft_decay = jax.nn.softplus(-lru_decay)
    params = jnp.concatenate(
        [
            conv_kernel,
            conv_bias[None],
            lru_bias,
            (-8.0 * soft_decay)[None],
            (8.0 * jax.nn.sigmoid(-lru_decay))[None],
            jnp.zeros((SUBLANES - 1, rec_width), jnp.float32),
        ],
        axis=0,
    )
    core = Recurrence(row_count, block_len, rec_width, head_size)
    wide_gates = core.widen(lru_gates)
    if tokens.shape[2] % LANES == 0:
        blocks = [features_in(tokens, slice(0, 1))]
        later, wide_gates, params, dist = lax.optimization_barrier(
            (tokens, wide_gates, params, dist)
        )
        blocks += [features_in(later, slice(row, row + 1)) for row in range(1, row_count)]
    else:
        side = features_in(tokens)
        blocks = [side[:, row * block_len : (row + 1) * block_len] for row in range(row_count)]
    per_row = []
    for row in range(row_count):
        block = blocks[row]
        if row:
            block, _ = lax.optimization_barrier((block, per_row[-1][-1]))
        per_row.append(
            front(
                block,
                norm1_gain,
                recur_input,
                recur_gate,
                dist[row : row + 1],
                params,
                wide_gates,
            )
        )
    low_x, inverse, normed_low, branch, gate_pre, rim, lru_in, rate, igate, state, cum, last = zip(
        *per_row
    )
    entering, mixed_low, resid_one, normed_low2 = middle(
        last, state, cum, gate_pre, low_x, recur_out, norm2_gain
    )
    cotangent, _ = lax.optimization_barrier((cotangent, block))
    cotangent, resid_one = lax.optimization_barrier((features_in(cotangent), resid_one))
    grad_low, hidden_low, mgate_low, mup_low = mlp_hidden(
        lengths - seq_index * block_len, cotangent, normed_low2, mlp_gate, mlp_up, mlp_down
    )
    devices = lax.axis_size(("seq", "zed", "core"))
    own_rows = model_dim // devices
    tiled = own_rows % (2 * SUBLANES) == 0 and tokens.shape[2] % LANES == 0
    if tiled:
        merged = block_gradients(normed_low2, mgate_low, mup_low, hidden_low, grad_low)
        merged, hidden_low = lax.optimization_barrier((merged, hidden_low))
        merged = lax.psum_scatter(merged, "seq", scatter_dimension=0, tiled=True)
    result_parts, resid_low = mlp_back(
        hidden_low,
        mgate_low,
        mup_low,
        grad_low,
        resid_one,
        norm2_gain,
        mlp_gate,
        mlp_up,
        mlp_down,
        cotangent.shape,
    )
    output = features_out(result_parts, row_count)
    gate_low, back_local, back_cum, first_term = core.adjoint(
        resid_low,
        recur_out,
        gate_pre,
        state,
        cum,
        entering,
        rate,
        dist,
        params,
    )
    gate_low = gate_low.reshape(tok_count, rec_width)

    def zed_stage(leaving):
        if not tiled:
            return ((), leaving)
        done, leaving = lax.optimization_barrier((merged, leaving))
        return (lax.psum_scatter(done, "zed", scatter_dimension=0, tiled=True), leaving)

    branch_local, ending, leading, small, merged_own = core.backward(
        back_local,
        back_cum,
        first_term,
        last,
        state,
        cum,
        entering,
        rate,
        igate,
        lru_in,
        dist,
        branch,
        rim,
        params,
        wide_gates,
        zed_stage,
    )
    branch_low = branch_local.reshape(tok_count, rec_width)
    if tiled:
        output, branch_low = lax.optimization_barrier((output, branch_low))
        grad_tokens, sum_rgate, sum_rout, sum_rin, own_small = tail(
            gate_low,
            branch_low,
            ending,
            leading,
            mixed_low,
            resid_low,
            norm1_gain,
            recur_input,
            recur_gate,
            small,
            normed_low,
            low_x,
            inverse,
        )
        device = lax.axis_index(("seq", "zed", "core"))
        sums = outputs(
            device,
            merged_own[0],
            sum_rgate,
            sum_rin,
            sum_rout,
            own_small,
            recur_input,
            recur_gate,
            mlp_gate,
            mlp_up,
            norm1_gain,
            norm2_gain,
            head_size,
        )
        flat = (0, 4, 7, 9)
        sums = [part.reshape(-1) if place in flat else part for place, part in enumerate(sums)]
        return (output, grad_tokens, *sums)
    else:
        from_next = passed_along(
            leading[:, SUBLANES - rim_size :, :].astype(jnp.bfloat16), "seq", -1
        )
        ending = ending + jnp.pad(
            from_next.astype(jnp.float32), ((0, 0), (SUBLANES - rim_size, 0), (0, 0))
        )
        branch_low = lax.dynamic_update_slice(
            branch_local, ending.astype(jnp.bfloat16), (0, block_len - SUBLANES, 0)
        ).reshape(tok_count, rec_width)
        grad_norm1 = back_dot(branch_low, recur_input) + back_dot(gate_low, recur_gate)
        inv_one = jnp.concatenate(inverse)[:, :1]
        normed_one = jnp.concatenate(low_x).astype(jnp.float32) * inv_one
        normed_low = jnp.concatenate(normed_low)
        input_part = norm_back(grad_norm1, normed_one, inv_one, norm1_gain)
        grad_x = (resid_low.astype(jnp.float32) + input_part).astype(jnp.bfloat16)
        grad_tokens = features_out(features_apart(grad_x), row_count)
        sum_mgate, sum_mup, sum_down, sum_rout, sum_rgate, sum_rin = (
            scattered(weight_grad(left, right))
            for left, right in (
                (normed_low2, mgate_low),
                (normed_low2, mup_low),
                (hidden_low, grad_low),
                (mixed_low, resid_low),
                (normed_low, gate_low),
                (normed_low, branch_low),
            )
        )
        own_small = scattered(small)
    sum_lgates = jnp.concatenate(
        [own_small[:, :head_size], own_small[:, LANES : LANES + head_size]], axis=1
    )
    own_sums = jnp.swapaxes(own_small[:, head_size : head_size + SUBLANES], 0, 1)
    device = lax.axis_index(("seq", "zed", "core"))

    def mine(array, size, axis=0):
        return lax.dynamic_slice_in_dim(array, device * size, size, axis)

    def weighed(weight, gradient):
        return jnp.sum(mine(weight, own_rows).astype(jnp.float32) * gradient, axis=1)

    sum_gain1 = (weighed(recur_input, sum_rin) + weighed(recur_gate, sum_rgate)) / mine(
        norm1_gain, own_rows
    )
    sum_gain2 = (weighed(mlp_gate, sum_mgate) + weighed(mlp_up, sum_mup)) / mine(
        norm2_gain, own_rows
    )
    sum_decay = own_sums[7]
    return (
        output,
        grad_tokens,
        sum_gain1,
        sum_rin,
        sum_rgate,
        own_sums[:4],
        own_sums[4],
        sum_lgates,
        own_sums[5:7],
        sum_decay,
        sum_rout,
        sum_gain2,
        sum_mgate,
        sum_mup,
        sum_down,
    )


def solution(mesh):
    seq, chan = (mesh.shape["seq"], mesh.shape["chan"])
    chips = jax.sharding.Mesh(mesh.devices.reshape(seq, chan // 2, 2), ("seq", "zed", "core"))
    chan = ("zed", "core")
    every = ("seq", "zed", "core")
    activations = P(None, "seq", chan)
    rows, columns, vector = (P(every, None), P(None, every), P(every))
    return jax.shard_map(
        body,
        mesh=chips,
        in_specs=(activations, activations, P(chan, None), P(chan)) + (P(),) * 13,
        out_specs=(
            activations,
            activations,
            vector,
            rows,
            rows,
            columns,
            vector,
            rows,
            columns,
            vector,
            rows,
            vector,
            rows,
            rows,
            rows,
        ),
        check_vma=False,
    )
```

```python
import functools
import math

import jax
import jax.numpy as jnp
from jax import lax
from jax.experimental import pallas as pl
from jax.experimental.pallas import tpu as pltpu
from jax.sharding import PartitionSpec as P

H = 16


EPS = 1e-06
ROOT_FLOOR = 1e-06
LANES = 128
SUBLANES = 8
STEP = 16
VMEM_BYTES = 56 * 1024 * 1024
MESH = pl.DeviceIdType.MESH


def sigmoid(value):
    return 0.5 * jnp.tanh(0.5 * value) + 0.5


GELU_C = 0.7978845608
GELU_A = 0.044715


def gelu_pair(value):
    square = value * value
    inner = jnp.tanh(value * (GELU_C + (GELU_C * GELU_A) * square))
    half = 0.5 + 0.5 * inner
    slope = GELU_C + (3.0 * GELU_C * GELU_A) * square
    return (value * half, half + 0.5 * value * (1.0 - inner * inner) * slope)


def root_argument(log_decay, decay):
    y = 2.0 * log_decay
    series = 1.0 + y * (0.5 + y * (1.0 / 6.0 + y * (1.0 / 24.0)))
    return jnp.where(y > -0.05, -y * series, 1.0 - decay * decay)


def across(column, width):
    return jnp.concatenate([column] * (width // LANES), axis=1)


class Rows:
    def __init__(self, refs):
        self.refs = refs

    def __getitem__(self, index):
        if not isinstance(index, tuple):
            return self.refs[index][0]
        return self.refs[index[0]][(0,) + index[1:]]


def by_rows(refs, rows, apart):
    found = []
    for split in apart:
        count = rows if split else 1
        found.append(Rows(refs[:count]) if split else refs[0])
        refs = refs[count:]
    return found, refs


def scan_block(
    branch_ref,
    rim_ref,
    dist_ref,
    par_ref,
    gates_ref,
    lru_ref,
    rate_ref,
    igate_ref,
    state_ref,
    cum_ref,
    last_ref,
    both_ref,
):
    rows, length, width = branch_ref.shape
    span = 2 * STEP if rows == 1 else STEP
    taps = [par_ref[k : k + 1, :] for k in range(4)]
    conv_bias, rate_bias, input_bias, soft = (par_ref[k : k + 1, :] for k in range(4, 8))
    place = lax.broadcasted_iota(jnp.int32, (SUBLANES, width), 0)

    for row in range(rows):

        def conv_step(index, before, row=row):
            base = pl.multiple_of(index * STEP, STEP)
            pieces = []
            for half in range(STEP // SUBLANES):
                at = pl.ds(base + half * SUBLANES, SUBLANES)
                here = branch_ref[row, at, :]
                dist = across(dist_ref[row, at, :], width)
                total = conv_bias + taps[0] * here
                for k in range(1, 4):
                    shifted = pltpu.roll(jnp.where(place < SUBLANES - k, here, before), k, 0)
                    total = total + taps[k] * jnp.where(dist >= k, shifted, 0.0)
                pieces.append(total)
                before = here
            lru_ref[row, pl.ds(base, STEP), :] = jnp.concatenate(pieces, axis=0).astype(jnp.bfloat16)
            return before

        lax.fori_loop(0, length // STEP, conv_step, rim_ref[row], unroll=2)

        piece = min(length, 256)

        def dot_step(index, carry, row=row):
            at = pl.ds(pl.multiple_of(index * piece, piece), piece)
            both_ref[row, at, :] = jnp.dot(
                lru_ref[row, at, :], gates_ref[...], preferred_element_type=jnp.float32
            )
            return carry

        lax.fori_loop(0, length // piece, dot_step, 0)

    def scan_step(index, carry):
        base = pl.multiple_of(index * span, span)
        later = []
        for row in range(rows):
            run_cum, run_state = carry[row]
            lru_both = lru_ref[row, pl.ds(base, span), :].astype(jnp.float32)
            for half in range(span // SUBLANES):
                at = pl.ds(base + half * SUBLANES, SUBLANES)
                lru = lru_both[half * SUBLANES : (half + 1) * SUBLANES]
                start = across(dist_ref[row, at, :], width) == 0
                rate = sigmoid(both_ref[row, at, :width] + rate_bias)
                igate = sigmoid(both_ref[row, at, width:] + input_bias)
                log_decay = rate * soft
                decay = jnp.exp(log_decay)
                arg = jnp.maximum(root_argument(log_decay, decay), ROOT_FLOOR)
                root = arg * lax.rsqrt(arg)
                cum = jnp.where(start, 0.0, decay)
                value = jnp.where(start, 1.0, root) * igate * lru
                rate_ref[row, at, :] = rate
                igate_ref[row, at, :] = igate
                for shift in (1, 2, 4):
                    live = place >= shift
                    value = value + cum * jnp.where(live, pltpu.roll(value, shift, 0), 0.0)
                    cum = cum * jnp.where(live, pltpu.roll(cum, shift, 0), 1.0)
                value = value + cum * run_state
                cum = cum * run_cum
                state_ref[row, at, :] = value
                cum_ref[row, at, :] = cum
                run_state = value[SUBLANES - 1 :, :]
                run_cum = cum[SUBLANES - 1 :, :]
            later.append((run_cum, run_state))
        return tuple(later)

    one, zero = (jnp.ones((1, width), jnp.float32), jnp.zeros((1, width), jnp.float32))
    done = lax.fori_loop(
        0, length // span, scan_step, tuple((one, zero) for _ in range(rows)), unroll=2
    )
    for row in range(rows):
        for place in range(2):
            last_ref[row, place : place + 1, :] = done[row][place]


def carried(sent_ref, got_ref, out_ref, send_sem, recv_sem, backward):
    seq, count = (lax.axis_index("seq"), lax.axis_size("seq"))

    def other(step):
        return {"seq": lax.rem(seq + step, count)}

    barrier = pltpu.get_barrier_semaphore()
    for step in range(1, count):
        pl.semaphore_signal(barrier, inc=1, device_id=other(step), device_id_type=MESH)
    pl.semaphore_wait(barrier, count - 1)
    copies = [
        pltpu.make_async_remote_copy(
            src_ref=sent_ref,
            dst_ref=got_ref.at[seq],
            send_sem=send_sem.at[step - 1],
            recv_sem=recv_sem.at[step - 1],
            device_id=other(step),
            device_id_type=MESH,
        )
        for step in range(1, count)
    ]
    for copy in copies:
        copy.start()
    got_ref[seq] = sent_ref[...]
    for copy in copies:
        copy.wait()
    for row in range(sent_ref.shape[0]):
        total = jnp.zeros(out_ref.shape[1:], jnp.float32)
        for place in range(count - 1, 0, -1) if backward else range(count - 1):
            longer = got_ref[place, row, 0:1, :] * total + got_ref[place, row, 1:2, :]
            total = jnp.where(place > seq if backward else place < seq, longer, total)
        out_ref[row] = total


def adjoint_kernel(rows, *refs):
    (
        dres_ref,
        weight_ref,
        pre_ref,
        state_ref,
        cum_ref,
        carry_ref,
        rate_ref,
        dist_ref,
        par_ref,
    ), outs = by_rows(refs, rows, (False, False, True, True, True, False, True, False, False))
    dgate_ref, local_ref, back_ref, first_ref, dmix_ref = outs
    _, length, width = dmix_ref.shape
    for row in range(rows):
        dmix_ref[row] = lax.dot_general(
            dres_ref[row * length : (row + 1) * length, :],
            weight_ref[...],
            (((1,), (1,)), ((), ())),
            preferred_element_type=jnp.float32,
        )
    soft = par_ref[7:8, :]
    place = lax.broadcasted_iota(jnp.int32, (SUBLANES, width), 0)
    last = length // STEP - 1

    def step(index, carry):
        base = pl.multiple_of((last - index) * STEP, STEP)
        later = []
        for row in range(rows):
            run_cum, run_back = carry[row]
            entering = carry_ref[row]
            pieces = []
            for half in reversed(range(STEP // SUBLANES)):
                at = pl.ds(base + half * SUBLANES, SUBLANES)
                start = across(dist_ref[row, at, :], width) == 0
                state = state_ref[row, at, :] + cum_ref[row, at, :] * entering
                act, slope = gelu_pair(pre_ref[row, at, :])
                dmix = dmix_ref[row, at, :]
                pieces.append(dmix * state * slope)
                dstate = dmix * act
                coef = jnp.where(start, 0.0, jnp.exp(rate_ref[row, at, :] * soft))
                value = coef * dstate
                for shift in (1, 2, 4):
                    live = place < SUBLANES - shift
                    turn = SUBLANES - shift
                    value = value + coef * jnp.where(live, pltpu.roll(value, turn, 0), 0.0)
                    coef = coef * jnp.where(live, pltpu.roll(coef, turn, 0), 1.0)
                value = value + coef * run_back
                coef = coef * run_cum
                inside = place < SUBLANES - 1
                local_ref[row, at, :] = dstate + jnp.where(
                    inside, pltpu.roll(value, SUBLANES - 1, 0), run_back
                )
                back_ref[row, at, :] = jnp.where(inside, pltpu.roll(coef, SUBLANES - 1, 0), run_cum)
                run_back = value[:1, :]
                run_cum = coef[:1, :]
            dgate_ref[row, pl.ds(base, STEP), :] = jnp.concatenate(pieces[::-1], axis=0).astype(
                jnp.bfloat16
            )
            later.append((run_cum, run_back))
        return tuple(later)

    one, zero = (jnp.ones((1, width), jnp.float32), jnp.zeros((1, width), jnp.float32))
    done = lax.fori_loop(0, last + 1, step, tuple((one, zero) for _ in range(rows)), unroll=2)
    for row in range(rows):
        first_ref[row] = done[row][1]


def backward_kernel(head_size, rows, *refs):
    first_at = 2
    sent_ref, got_ref, send_sem, recv_sem = refs[-4:]
    leaving_ref = refs[-8]
    lasts = Rows(refs[first_at + 1 : first_at + 1 + rows])

    @pl.when(pl.program_id(0) == 0)
    def _():
        for row in range(rows):
            sent_ref[row, 0:1, :] = lasts[row, 0:1, :]
            sent_ref[row, 1:2, :] = refs[first_at][row]
        carried(sent_ref, got_ref, leaving_ref, send_sem, recv_sem, True)

    block_backward(head_size, rows, 0, leaving_ref, *refs[:-8], *refs[-7:-4])


def later_backward_kernel(head_size, rows, first, *refs):
    held = 4
    block_backward(head_size, rows, first, refs[0], *refs[1 + held :])


def block_backward(head_size, rows, first_block, leaving_ref, *refs):
    (
        local_ref,
        back_ref,
        first_ref,
        last_ref,
        state_ref,
        cum_ref,
        in_ref,
        rate_ref,
        igate_ref,
        lru_ref,
        dist_ref,
        branch_ref,
        rim_ref,
        par_ref,
        gates_ref,
    ), others = by_rows(
        refs, rows, (False,) * 3 + (True,) * 3 + (False,) + (True,) * 3 + (False,) + (True,) * 2 + (False,) * 2
    )
    dbranch_ref, tail_ref, head_ref, dgates_ref = others[:4]
    both_ref, dconv_ref, sums_ref = others[-3:]
    _, length, width = local_ref.shape
    here = pl.program_id(0) + first_block
    block = pl.ds(pl.multiple_of(here * width, width), width)
    taps = [par_ref[k : k + 1, :] for k in range(4)]
    soft = par_ref[7:8, :]
    place = lax.broadcasted_iota(jnp.int32, (SUBLANES, width), 0)
    zeros = jnp.zeros((SUBLANES, width), jnp.float32)

    def gate_step(index, carry):
        sums, earlier = carry
        decay_sum, rate_sum, input_sum = sums
        base = pl.multiple_of(index * STEP, STEP)
        later = []
        for row in range(rows):
            before = earlier[row]
            entering = in_ref[row]
            leaving = leaving_ref[row, :, block]
            lru_both = lru_ref[row, pl.ds(base, STEP), :].astype(jnp.float32)
            drates, dinputs = ([], [])
            for half in range(STEP // SUBLANES):
                at = pl.ds(base + half * SUBLANES, SUBLANES)
                lru = lru_both[half * SUBLANES : (half + 1) * SUBLANES]
                start = across(dist_ref[row, at, :], width) == 0
                adjoint = local_ref[row, at, :] + back_ref[row, at, :] * leaving
                state = state_ref[row, at, :] + cum_ref[row, at, :] * entering
                previous = jnp.where(place < 1, before, pltpu.roll(state, 1, 0))
                before = state[SUBLANES - 1 :, :]
                rate = rate_ref[row, at, :]
                igate = igate_ref[row, at, :]
                log_decay = rate * soft
                decay = jnp.exp(log_decay)
                arg = root_argument(log_decay, decay)
                above = arg > ROOT_FLOOR
                arg = jnp.maximum(arg, ROOT_FLOOR)
                inverse = lax.rsqrt(arg)
                scale = jnp.where(start, 1.0, arg * inverse)
                gated = adjoint * igate
                dscale = gated * lru
                pull = jnp.where(above, dscale * decay * decay * inverse, 0.0)
                dlog = jnp.where(start, 0.0, adjoint * previous * decay - pull)
                dig = adjoint * scale * lru
                weighted = dlog * rate
                decay_sum = decay_sum + weighted
                drates.append(weighted * soft * (1.0 - rate))
                dinputs.append(dig * igate * (1.0 - igate))
                dconv_ref[row, at, :] = gated * scale
            drate = jnp.concatenate(drates, axis=0).astype(jnp.bfloat16)
            dinput = jnp.concatenate(dinputs, axis=0).astype(jnp.bfloat16)
            both_ref[row, pl.ds(base, STEP), :width] = drate
            both_ref[row, pl.ds(base, STEP), width:] = dinput
            drate = drate.astype(jnp.float32)
            dinput = dinput.astype(jnp.float32)
            rate_sum = rate_sum + (drate[:SUBLANES] + drate[SUBLANES:])
            input_sum = input_sum + (dinput[:SUBLANES] + dinput[SUBLANES:])
            later.append(before)
        return ((decay_sum, rate_sum, input_sum), tuple(later))

    sums, _ = lax.fori_loop(
        0,
        length // STEP,
        gate_step,
        ((zeros, zeros, zeros), tuple(in_ref[row] for row in range(rows))),
        unroll=2,
    )
    for slot, total in zip((5, 6, 7), (sums[1], sums[2], sums[0] * par_ref[8:9, :])):
        sums_ref[slot : slot + 1, :] = jnp.sum(total, axis=0, keepdims=True)

    piece = min(length, 256)
    wide = None
    for row in range(rows):

        def dot_step(index, carry, row=row):
            at = pl.ds(pl.multiple_of(index * piece, piece), piece)
            dconv_ref[row, at, :] += lax.dot_general(
                both_ref[row, at, :],
                gates_ref[...],
                (((1,), (1,)), ((), ())),
                preferred_element_type=jnp.float32,
            )
            return carry

        lax.fori_loop(0, length // piece, dot_step, 0)
        part = lax.dot_general(
            lru_ref[row], both_ref[row], (((0,), (0,)), ((), ())), preferred_element_type=jnp.float32
        )
        wide = part if wide is None else wide + part
    row_head = lax.broadcasted_iota(jnp.int32, (width, width), 0) // head_size
    col_head = lax.broadcasted_iota(jnp.int32, (width, width), 1) // head_size
    own = row_head == col_head
    folds = []
    for part in range(2):
        kept = jnp.where(own, wide[:, part * width : (part + 1) * width], 0.0)
        folded = kept
        for other in range(1, width // head_size):
            folded = folded + pltpu.roll(kept, width - other * head_size, 1)
        folds.append(folded[:, :LANES])

    def conv_step(index, carry):
        sums, following = carry
        sums = list(sums)
        base = pl.multiple_of((length // STEP - 1 - index) * STEP, STEP)
        later = []
        for row in range(rows):
            after = following[row]
            pieces = []
            for half in reversed(range(STEP // SUBLANES)):
                at = pl.ds(base + half * SUBLANES, SUBLANES)
                dist = across(dist_ref[row, at, :], width)
                branch = branch_ref[row, at, :]
                here = dconv_ref[row, at, :]
                total = taps[0] * here
                sums[0] = sums[0] + here * branch
                sums[4] = sums[4] + here
                masked = tuple(jnp.where(dist >= k, here, 0.0) for k in range(1, 4))
                for k in range(1, 4):
                    moved = pltpu.roll(
                        jnp.where(place >= k, masked[k - 1], after[k - 1]), SUBLANES - k, 0
                    )
                    total = total + taps[k] * moved
                    sums[k] = sums[k] + branch * moved
                after = masked
                pieces.append(total)
            whole = jnp.concatenate(pieces[::-1], axis=0)
            dbranch_ref[row, pl.ds(base, STEP), :] = whole.astype(jnp.bfloat16)
            later.append(after)

            @pl.when(index == 0)
            def _(row=row, whole=whole):
                tail_ref[row] = whole[STEP - SUBLANES :]

        return (tuple(sums), tuple(later))

    sums, firsts = lax.fori_loop(
        0,
        length // STEP,
        conv_step,
        ((zeros,) * 5, tuple((zeros,) * 3 for _ in range(rows))),
        unroll=2,
    )
    sums = list(sums)
    for row in range(rows):
        total = zeros
        rim = rim_ref[row]
        for k in range(1, 4):
            moved = pltpu.roll(jnp.where(place >= k, 0.0, firsts[row][k - 1]), SUBLANES - k, 0)
            total = total + taps[k] * moved
            sums[k] = sums[k] + rim * moved
        head_ref[row] = total
    for slot in range(5):
        sums_ref[slot : slot + 1, :] = jnp.sum(sums[slot], axis=0, keepdims=True)
    above = jnp.zeros((head_size, width), jnp.float32)
    below = jnp.zeros((LANES - head_size - SUBLANES, width), jnp.float32)
    turned = jnp.concatenate([above, sums_ref[...], below], axis=0).T
    lane = lax.broadcasted_iota(jnp.int32, (width, LANES), 1)
    dgates_ref[:, :LANES] = jnp.where(lane < head_size, folds[0], turned).astype(dgates_ref.dtype)
    dgates_ref[:, LANES:] = folds[1].astype(dgates_ref.dtype)


def channel_call(
    kernel, name, arrays, specs, outs, out_specs, scratch, blocks, flops, params=()
):
    moved = sum(math.prod(a.shape) * a.dtype.itemsize for a in (*arrays, *outs))
    return pl.pallas_call(
        kernel,
        name=name,
        grid=(blocks,),
        in_specs=specs,
        out_specs=out_specs,
        out_shape=outs,
        scratch_shapes=scratch,
        compiler_params=pltpu.CompilerParams(vmem_limit_bytes=VMEM_BYTES, **dict(params)),
        cost_estimate=pl.CostEstimate(flops=flops, bytes_accessed=moved, transcendentals=0),
    )(*arrays)


class Recurrence:
    def __init__(self, rows, length, channels, head_size):
        self.rows, self.length, self.channels = (rows, length, channels)
        self.head_size = head_size
        self.width = head_size * LANES // math.gcd(head_size, LANES)
        self.blocks = channels // self.width
        self.flops = 2 * rows * length * channels * 2 * self.width

    def tall(self):
        return pl.BlockSpec((self.rows, self.length, self.width), lambda j: (0, 0, j))

    def short(self, size):
        return pl.BlockSpec((self.rows, size, self.width), lambda j: (0, 0, j))

    def apart(self, size):
        return [pl.BlockSpec((1, size, self.width), lambda j: (0, 0, j))] * self.rows

    def whole(self, rows, size):
        return pl.BlockSpec((rows, size, self.channels), lambda j: (0, 0, 0))

    def flat(self, size):
        return pl.BlockSpec((size, self.width), lambda j: (0, j))

    def dist(self):
        return pl.BlockSpec((self.rows, self.length, LANES), lambda j: (0, 0, 0))

    def gates(self, columns):
        return pl.BlockSpec((self.width, columns), lambda j: (j, 0))

    def shape(self, size, dtype):
        return jax.ShapeDtypeStruct((self.rows, size, self.channels), dtype)

    def widen(self, lru_gates):
        size, width = (self.head_size, self.width)
        heads = width // size
        column = jnp.arange(2 * width)
        source = (column // width) * size + column % size
        spread = (jnp.arange(2 * size)[:, None] == source[None, :]).astype(jnp.bfloat16)
        owner = (column % width) // size
        mine = (jnp.arange(self.channels) // size) % heads
        wide = jnp.dot(lru_gates, spread, preferred_element_type=jnp.float32)
        return jnp.where(mine[:, None] == owner[None, :], wide, 0.0).astype(jnp.bfloat16)

    def adjoint(self, dres, weight, pre, state, cum, entering, rate, dist, params):
        f32 = jnp.float32
        outs = [self.shape(self.length, d) for d in (jnp.bfloat16, f32, f32)] + [self.shape(1, f32)]
        tall, apart = (self.tall(), self.apart(self.length))
        return channel_call(
            functools.partial(adjoint_kernel, self.rows),
            "recurrence_adjoint",
            (dres, weight, *pre, *state, *cum, entering, *rate, dist, params),
            [
                pl.BlockSpec(dres.shape, lambda j: (0, 0)),
                self.gates(weight.shape[1]),
                *apart * 3,
                self.short(1),
                *apart,
                self.dist(),
                self.flat(16),
            ],
            outs,
            [tall, tall, tall, self.short(1)],
            [pltpu.VMEM((self.rows, self.length, self.width), f32)],
            self.blocks,
            2 * self.rows * self.length * weight.size,
        )

    def backward(
        self, local, back, first, last, state, cum, entering, rate, igate, lru, dist, branch, rim, params, gates, between_calls
    ):
        f32 = jnp.float32
        outs = [
            self.shape(self.length, jnp.bfloat16),
            self.shape(SUBLANES, f32),
            self.shape(SUBLANES, f32),
            jax.ShapeDtypeStruct((self.channels, 2 * LANES), jnp.bfloat16),
        ]
        seqs = lax.axis_size("seq")
        summary = (self.rows, 2, self.channels)
        arrays = (local, back, first, *last, *state, *cum, entering, *rate, *igate, *lru, dist, *branch, *rim)
        arrays += (params, gates)
        early = self.blocks - 1
        scratch = [
            pltpu.VMEM((self.rows, self.length, 2 * self.width), jnp.bfloat16),
            pltpu.VMEM((self.rows, self.length, self.width), f32),
            pltpu.VMEM((SUBLANES, self.width), f32),
        ]

        def specs(offset):
            rows, width = (self.rows, self.width)

            def wide(rows, size):
                return pl.BlockSpec((rows, size, width), lambda j: (0, 0, j + offset))

            def flat(size):
                return pl.BlockSpec((size, width), lambda j: (0, j + offset))

            def tall(columns):
                return pl.BlockSpec((width, columns), lambda j: (j + offset, 0))

            whole, apart = (wide(rows, self.length), [wide(1, self.length)] * rows)
            given = [whole, whole, self.whole(rows, 1), *[self.whole(1, 2)] * rows, *apart * 2]
            given += [wide(rows, 1), *apart * 3, self.dist(), *apart, *[wide(1, SUBLANES)] * rows]
            given += [flat(16), tall(2 * width)]
            made = [whole, wide(rows, SUBLANES), wide(rows, SUBLANES), tall(2 * LANES)]
            return (given, made)

        given, made = specs(0)
        *found, leaving = channel_call(
            functools.partial(backward_kernel, self.head_size, self.rows),
            "recurrence_backward",
            arrays,
            given,
            outs + [self.shape(1, f32)],
            made + [self.whole(self.rows, 1)],
            scratch
            + [
                pltpu.VMEM(summary, f32),
                pltpu.VMEM((seqs,) + summary, f32),
                pltpu.SemaphoreType.DMA((seqs - 1,)),
                pltpu.SemaphoreType.DMA((seqs - 1,)),
            ],
            early,
            2 * self.flops,
            {"collective_id": 5, "has_side_effects": True},
        )
        between, leaving = between_calls(leaving)
        given, made = specs(early)
        done = pl.pallas_call(
            functools.partial(later_backward_kernel, self.head_size, self.rows, early),
            name="recurrence_backward_end",
            grid=(self.blocks - early,),
            in_specs=[self.whole(self.rows, 1)] + [pl.BlockSpec(memory_space=pl.ANY)] * 4 + given,
            out_specs=made,
            out_shape=outs,
            scratch_shapes=scratch,
            input_output_aliases={1 + k: k for k in range(4)},
            compiler_params=pltpu.CompilerParams(vmem_limit_bytes=VMEM_BYTES),
            cost_estimate=pl.CostEstimate(
                flops=self.flops // 2, bytes_accessed=16 * self.flops // self.width, transcendentals=0
            ),
        )(leaving, *found, *arrays)
        return (*done, between)


def gathered(parts_ref, at):
    return jnp.concatenate([parts_ref[k, at, :] for k in range(parts_ref.shape[0])], axis=1)


def front_kernel(
    parts_ref,
    gain_ref,
    input_ref,
    gate_ref,
    dist_ref,
    par_ref,
    gates_ref,
    x_ref,
    inverse_ref,
    normed_ref,
    branch_ref,
    pre_ref,
    rim_ref,
    lru_ref,
    rate_ref,
    igate_ref,
    state_ref,
    cum_ref,
    last_ref,
    landed_ref,
    both_ref,
    send_sem,
    recv_sem,
):
    tokens = x_ref.shape[0]
    piece, tall = (64, min(tokens, 512))
    step = pl.program_id(0)
    seq, seqs = (lax.axis_index("seq"), lax.axis_size("seq"))
    barrier = pltpu.get_barrier_semaphore()

    @pl.when(step == 0)
    def _():
        before = {"seq": lax.rem(seq + seqs - 1, seqs)}
        pl.semaphore_signal(barrier, inc=1, device_id=before, device_id_type=MESH)

        def norm(index, carry):
            at = pl.ds(pl.multiple_of(index * piece, piece), piece)
            low = gathered(parts_ref, at)
            x_ref[at, :] = low
            value = low.astype(jnp.float32)
            inverse = lax.rsqrt(jnp.mean(value * value, axis=1, keepdims=True) + EPS)
            inverse_ref[at, :] = jnp.broadcast_to(inverse, (piece, LANES))
            normed_ref[at, :] = (value * inverse * gain_ref[...]).astype(jnp.bfloat16)
            return carry

        lax.fori_loop(0, tokens // piece, norm, 0, unroll=2)

    rim_copy = pltpu.make_async_remote_copy(
        src_ref=normed_ref.at[tokens - STEP :],
        dst_ref=landed_ref,
        send_sem=send_sem,
        recv_sem=recv_sem,
        device_id={"seq": lax.rem(seq + 1, seqs)},
        device_id_type=MESH,
    )

    @pl.when(step == 0)
    def _():
        pl.semaphore_wait(barrier, 1)
        rim_copy.start()

    def multiply(index, carry):
        at = pl.ds(pl.multiple_of(index * tall, tall), tall)
        normed = normed_ref[at, :]
        branch_ref[0, at, :] = jnp.dot(normed, input_ref[...], preferred_element_type=jnp.float32)
        pre_ref[0, at, :] = jnp.dot(normed, gate_ref[...], preferred_element_type=jnp.float32)
        return carry

    lax.fori_loop(0, tokens // tall, multiply, 0)

    @pl.when(step == 0)
    def _():
        rim_copy.wait()

    before = jnp.dot(landed_ref[...], input_ref[...], preferred_element_type=jnp.float32)
    rim_ref[0] = jnp.where(seq > 0, 1.0, 0.0) * before[STEP - SUBLANES :]
    scan_block(
        branch_ref,
        rim_ref,
        dist_ref,
        par_ref,
        gates_ref,
        lru_ref,
        rate_ref,
        igate_ref,
        state_ref,
        cum_ref,
        last_ref,
        both_ref,
    )


def front(parts, gain, recur_input, recur_gate, dist, params, gates):
    count, tokens, width = parts.shape
    model, rec = recur_input.shape
    columns = gates.shape[1] // 2
    steps = rec // columns
    low, f32 = (jnp.bfloat16, jnp.float32)
    tall = pl.BlockSpec((model, columns), lambda j: (0, j))

    def whole(shape):
        return pl.BlockSpec(shape, lambda j: (0,) * len(shape))

    def wide(size, dtype):
        spec = pl.BlockSpec((1, size, columns), lambda j: (0, 0, j))
        return (spec, jax.ShapeDtypeStruct((1, size, rec), dtype))

    made = [wide(tokens, f32), wide(tokens, f32), wide(SUBLANES, f32), wide(tokens, low)]
    made += [wide(tokens, f32)] * 4 + [wide(2, f32)]
    return pl.pallas_call(
        front_kernel,
        name="project_and_scan",
        grid=(steps,),
        in_specs=[
            whole(parts.shape),
            whole((1, model)),
            tall,
            tall,
            whole(dist.shape),
            pl.BlockSpec((16, columns), lambda j: (0, j)),
            pl.BlockSpec((columns, 2 * columns), lambda j: (j, 0)),
        ],
        out_specs=[whole((tokens, model)), whole((tokens, LANES)), whole((tokens, model))]
        + [spec for spec, _ in made],
        out_shape=[
            jax.ShapeDtypeStruct((tokens, model), low),
            jax.ShapeDtypeStruct((tokens, LANES), f32),
            jax.ShapeDtypeStruct((tokens, model), low),
        ]
        + [shape for _, shape in made],
        scratch_shapes=[
            pltpu.VMEM((STEP, model), low),
            pltpu.VMEM((1, tokens, 2 * columns), f32),
            pltpu.SemaphoreType.DMA,
            pltpu.SemaphoreType.DMA,
        ],
        compiler_params=pltpu.CompilerParams(
            collective_id=3, has_side_effects=True, vmem_limit_bytes=VMEM_BYTES
        ),
        cost_estimate=pl.CostEstimate(
            flops=5 * tokens * model * rec, bytes_accessed=40 * tokens * model, transcendentals=0
        ),
    )(parts, gain[None], recur_input, recur_gate, dist, params, gates)


def middle_kernel(rows, *refs):
    (last_ref, state_hbm, cum_hbm, pre_hbm, x_ref, out_ref, gain_ref), others = by_rows(
        refs, rows, (True,) * 5 + (False,) * 2
    )
    entering_ref, mixed_ref, resid_ref, normed_ref = others[:4]
    sent_ref, got_ref, held_ref, send_sem, recv_sem, load_sem = others[4:]
    tall, model = resid_ref.shape
    step, steps = (pl.program_id(0), pl.num_programs(0))
    tiles = steps // rows
    slab = 16

    def on_row(place, act):
        for row in range(rows):

            @pl.when(lax.div(place, tiles) == row)
            def _(row=row):
                at = pl.ds(pl.multiple_of(lax.rem(place, tiles) * tall, tall), tall)
                slot = lax.rem(place, 2)
                for kind, source in enumerate((state_hbm, cum_hbm, pre_hbm)):
                    act(
                        pltpu.make_async_copy(
                            source.refs[row].at[0, at], held_ref.at[slot, kind], load_sem.at[slot, kind]
                        )
                    )

    @pl.when(step == 0)
    def _():
        on_row(step, lambda copy: copy.start())
        for row in range(rows):
            sent_ref[row] = last_ref[row]
        carried(sent_ref, got_ref, entering_ref, send_sem, recv_sem, False)

    @pl.when(step + 1 < steps)
    def _():
        on_row(step + 1, lambda copy: copy.start())

    on_row(step, lambda copy: copy.wait())
    slot = lax.rem(step, 2)
    mine = lax.div(step, tiles)

    def mix(index, carry):
        at = pl.ds(pl.multiple_of(index * slab, slab), slab)
        state = held_ref[slot, 0, at, :] + held_ref[slot, 1, at, :] * entering_ref[mine]
        pre = held_ref[slot, 2, at, :]
        inner = jnp.tanh(pre * (GELU_C + (GELU_C * GELU_A) * (pre * pre)))
        mixed_ref[at, :] = (state * (pre * (0.5 + 0.5 * inner))).astype(jnp.bfloat16)
        return carry

    lax.fori_loop(0, tall // slab, mix, 0, unroll=2)
    for row in range(rows):

        @pl.when(mine == row)
        def _(row=row):
            tile = 512
            for first in range(0, model, tile):
                at = slice(first, first + tile)
                resid_ref[:, at] = x_ref.refs[row][:, at].astype(jnp.float32) + jnp.dot(
                    mixed_ref[...], out_ref[:, at], preferred_element_type=jnp.float32
                )

    def norm(index, carry):
        at = pl.ds(pl.multiple_of(index * slab, slab), slab)
        resid = resid_ref[at, :]
        inverse = lax.rsqrt(jnp.mean(resid * resid, axis=1, keepdims=True) + EPS)
        normed_ref[at, :] = (resid * inverse * gain_ref[...]).astype(jnp.bfloat16)
        return carry

    lax.fori_loop(0, tall // slab, norm, 0, unroll=4)


def middle(last, state, cum, pre, x, recur_out, gain):
    rows = len(state)
    _, length, rec = state[0].shape
    model = recur_out.shape[1]
    tall = min(length, 256)
    tiles = length // tall
    tokens = rows * length
    seqs = lax.axis_size("seq")
    low, f32 = (jnp.bfloat16, jnp.float32)

    def whole(shape):
        return pl.BlockSpec(shape, lambda s: (0,) * len(shape), pipeline_mode=pl.Buffered(1))

    def flat(row):
        return lambda s: (jnp.clip(s - row * tiles, 0, tiles - 1), 0)

    summary = (rows, 2, rec)
    return pl.pallas_call(
        functools.partial(middle_kernel, rows),
        name="mix_and_norm",
        grid=(rows * tiles,),
        in_specs=[whole((1, 2, rec))] * rows
        + [pl.BlockSpec(memory_space=pl.ANY)] * (3 * rows)
        + [pl.BlockSpec((tall, model), flat(row)) for row in range(rows)]
        + [whole(recur_out.shape), whole((1, model))],
        out_specs=[
            pl.BlockSpec((rows, 1, rec), lambda s: (0, 0, 0)),
            pl.BlockSpec((tall, rec), lambda s: (s, 0)),
            pl.BlockSpec((tall, model), lambda s: (s, 0)),
            pl.BlockSpec((tall, model), lambda s: (s, 0)),
        ],
        out_shape=[
            jax.ShapeDtypeStruct((rows, 1, rec), f32),
            jax.ShapeDtypeStruct((tokens, rec), low),
            jax.ShapeDtypeStruct((tokens, model), f32),
            jax.ShapeDtypeStruct((tokens, model), low),
        ],
        scratch_shapes=[
            pltpu.VMEM(summary, f32),
            pltpu.VMEM((seqs,) + summary, f32),
            pltpu.VMEM((2, 3, tall, rec), f32),
            pltpu.SemaphoreType.DMA((seqs - 1,)),
            pltpu.SemaphoreType.DMA((seqs - 1,)),
            pltpu.SemaphoreType.DMA((2, 3)),
        ],
        compiler_params=pltpu.CompilerParams(
            collective_id=4, has_side_effects=True, vmem_limit_bytes=VMEM_BYTES
        ),
        cost_estimate=pl.CostEstimate(
            flops=2 * tokens * rec * model, bytes_accessed=14 * tokens * rec, transcendentals=0
        ),
    )(*last, *state, *cum, *pre, *x, recur_out, gain[None])


def hidden_kernel(
    left_ref,
    parts_ref,
    normed_ref,
    gate_ref,
    up_ref,
    down_ref,
    gout_ref,
    hidden_ref,
    dgate_ref,
    dup_ref,
):
    tokens, model = normed_ref.shape
    chunk = down_ref.shape[0]
    rows = left_ref.shape[0]
    length = tokens // rows
    slab = 32

    @pl.when(pl.program_id(0) == 0)
    def _():
        for row in range(rows):

            def collect(index, carry, row=row):
                base = pl.multiple_of(index * slab, slab)
                at = pl.ds(row * length + base, slab)
                low = gathered(parts_ref, at)
                place = base + lax.broadcasted_iota(jnp.int32, low.shape, 0)
                value = jnp.where(place < left_ref[row], low.astype(jnp.float32), 0.0)
                gout_ref[at, :] = value.astype(jnp.bfloat16)
                return carry

            lax.fori_loop(0, length // slab, collect, 0)

    tall = min(tokens, 512)
    wide = 256

    def tile(index, carry):
        at = pl.ds(pl.multiple_of(index * tall, tall), tall)
        for column in range(chunk // wide):
            own = slice(column * wide, (column + 1) * wide)
            gate = jnp.dot(normed_ref[at, :], gate_ref[:, own], preferred_element_type=jnp.float32)
            up = jnp.dot(normed_ref[at, :], up_ref[:, own], preferred_element_type=jnp.float32)
            dhid = lax.dot_general(
                gout_ref[at, :],
                down_ref[own, :],
                (((1,), (1,)), ((), ())),
                preferred_element_type=jnp.float32,
            )
            act, slope = gelu_pair(gate)
            hidden_ref[at, own] = (act * up).astype(jnp.bfloat16)
            dgate_ref[at, own] = (dhid * up * slope).astype(jnp.bfloat16)
            dup_ref[at, own] = (dhid * act).astype(jnp.bfloat16)
        return carry

    lax.fori_loop(0, tokens // tall, tile, 0)


def back_kernel(
    hidden_ref,
    dgate_ref,
    dup_ref,
    gout_hbm,
    resid_hbm,
    gain_ref,
    gate_ref,
    up_ref,
    down_ref,
    result_ref,
    dres_ref,
    total_ref,
    back_ref,
    gout_ref,
    resid_ref,
    load_sem,
):
    tall, model = (hidden_ref.shape[0], gout_ref.shape[1])
    step, tile = (pl.program_id(0), pl.program_id(1))
    wide = 512
    contract = (((1,), (1,)), ((), ()))
    rows = pl.ds(pl.multiple_of(tile * tall, tall), tall)

    def loads():
        return (
            pltpu.make_async_copy(gout_hbm, gout_ref, load_sem.at[0]),
            pltpu.make_async_copy(resid_hbm, resid_ref, load_sem.at[1]),
        )

    @pl.when((step == 0) & (tile == 0))
    def _():
        for load in loads():
            load.start()

    def products(own):
        forth = jnp.dot(hidden_ref[...], down_ref[:, own], preferred_element_type=jnp.float32)
        back = lax.dot_general(
            dgate_ref[...], gate_ref[own, :], contract, preferred_element_type=jnp.float32
        ) + lax.dot_general(
            dup_ref[...], up_ref[own, :], contract, preferred_element_type=jnp.float32
        )
        return (forth, back)

    @pl.when(step == 0)
    def _():
        for first in range(0, model, wide):
            own = slice(first, first + wide)
            forth, back = products(own)
            total_ref[rows, own] = forth
            back_ref[rows, own] = back

    @pl.when(step > 0)
    def _():
        for first in range(0, model, wide):
            own = slice(first, first + wide)
            forth, back = products(own)
            total_ref[rows, own] += forth
            back_ref[rows, own] += back

    @pl.when((step == pl.num_programs(0) - 1) & (tile == 0))
    def _():
        for load in loads():
            load.wait()

    @pl.when(step == pl.num_programs(0) - 1)
    def _():
        parts, width = (result_ref.shape[0], result_ref.shape[2])
        small = 16

        def finish(index, carry):
            at = pl.ds(pl.multiple_of(tile * tall + index * small, small), small)
            resid = resid_ref[at, :]
            result = (resid + total_ref[at, :]).astype(jnp.bfloat16)
            for part in range(parts):
                result_ref[part, at, :] = result[:, part * width : (part + 1) * width]
            inverse = lax.rsqrt(jnp.mean(resid * resid, axis=1, keepdims=True) + EPS)
            normed = resid * inverse
            scaled = back_ref[at, :] * gain_ref[...]
            mean = jnp.mean(scaled * normed, axis=1, keepdims=True)
            dres = gout_ref[at, :].astype(jnp.float32) + inverse * (scaled - normed * mean)
            dres_ref[at, :] = dres.astype(jnp.bfloat16)
            return carry

        lax.fori_loop(0, tall // small, finish, 0, unroll=4)


MLP_CHUNK = 768


def resident(shape):
    return pl.BlockSpec(shape, lambda s: (0,) * len(shape), pipeline_mode=pl.Buffered(1))


def mlp_specs(tokens, model):
    columns = pl.BlockSpec((model, MLP_CHUNK), lambda s: (0, s))
    down = pl.BlockSpec((MLP_CHUNK, model), lambda s: (s, 0))
    made = pl.BlockSpec((tokens, MLP_CHUNK), lambda s: (0, s))
    return ([columns, columns, down], [made] * 3)


def mlp_hidden(left, parts, normed, mlp_gate, mlp_up, mlp_down):
    tokens, model = normed.shape
    ffn = mlp_gate.shape[1]
    low = jnp.bfloat16
    weights, made = mlp_specs(tokens, model)
    tall = jax.ShapeDtypeStruct((tokens, ffn), low)
    return pl.pallas_call(
        hidden_kernel,
        name="mlp_hidden",
        grid=(ffn // MLP_CHUNK,),
        in_specs=[
            pl.BlockSpec(memory_space=pltpu.SMEM),
            resident(parts.shape),
            resident(normed.shape),
            *weights,
        ],
        out_specs=[resident((tokens, model)), *made],
        out_shape=[jax.ShapeDtypeStruct((tokens, model), low), tall, tall, tall],
        compiler_params=pltpu.CompilerParams(vmem_limit_bytes=VMEM_BYTES),
        cost_estimate=pl.CostEstimate(
            flops=6 * tokens * model * ffn,
            bytes_accessed=6 * (model + tokens) * ffn + 6 * tokens * model,
            transcendentals=0,
        ),
    )(left, parts, normed, mlp_gate, mlp_up, mlp_down)


def mlp_back(hidden, dgate, dup, gout, resid, gain, mlp_gate, mlp_up, mlp_down, parts_shape):
    tokens, model = resid.shape
    ffn = mlp_gate.shape[1]
    low, f32 = (jnp.bfloat16, jnp.float32)
    chunk, tall = (1024, min(tokens, 512))

    def resident(shape):
        return pl.BlockSpec(shape, lambda s, t: (0,) * len(shape), pipeline_mode=pl.Buffered(1))

    columns = pl.BlockSpec((model, chunk), lambda s, t: (0, s))
    down = pl.BlockSpec((chunk, model), lambda s, t: (s, 0))
    made = pl.BlockSpec((tall, chunk), lambda s, t: (t, s))
    return pl.pallas_call(
        back_kernel,
        name="mlp_back",
        grid=(ffn // chunk, tokens // tall),
        in_specs=[
            made,
            made,
            made,
            pl.BlockSpec(memory_space=pl.ANY),
            pl.BlockSpec(memory_space=pl.ANY),
            resident((1, model)),
            columns,
            columns,
            down,
        ],
        out_specs=[resident(parts_shape), resident((tokens, model))],
        out_shape=[
            jax.ShapeDtypeStruct(parts_shape, low),
            jax.ShapeDtypeStruct((tokens, model), low),
        ],
        scratch_shapes=[
            pltpu.VMEM((tokens, model), f32),
            pltpu.VMEM((tokens, model), f32),
            pltpu.VMEM((tokens, model), low),
            pltpu.VMEM((tokens, model), f32),
            pltpu.SemaphoreType.DMA((2,)),
        ],
        compiler_params=pltpu.CompilerParams(vmem_limit_bytes=VMEM_BYTES),
        cost_estimate=pl.CostEstimate(
            flops=6 * tokens * model * ffn,
            bytes_accessed=6 * (model + tokens) * ffn + 10 * tokens * model,
            transcendentals=0,
        ),
    )(hidden, dgate, dup, gout, resid, gain[None], mlp_gate, mlp_up, mlp_down)


def outputs_kernel(
    device_ref,
    own_ref,
    gate_sum,
    in_sum,
    out_sum,
    small_ref,
    input_ref,
    gate_ref,
    mlp_gate_ref,
    mlp_up_ref,
    gain1_ref,
    gain2_ref,
    sum_gain1,
    sum_in,
    sum_gate,
    sum_taps,
    sum_bias,
    sum_lgates,
    sum_lbias,
    sum_decay,
    sum_out,
    sum_gain2,
    sum_mgate,
    sum_mup,
    sum_down,
):
    rows = sum_mgate.shape[0]
    model = own_ref.shape[1]
    parts = sum_mgate.shape[1] // model
    for part in range(parts):
        at = slice(part * model, (part + 1) * model)
        sum_mgate[:, at] = own_ref[part * rows : (part + 1) * rows, :].astype(jnp.float32)
        sum_mup[:, at] = own_ref[(parts + part) * rows : (parts + part + 1) * rows, :].astype(
            jnp.float32
        )
    sum_down[...] = own_ref[2 * parts * rows :, :].astype(jnp.float32)

    def weighed(*pairs):
        return sum(
            jnp.sum(weight[...].astype(jnp.float32) * gradient[...], axis=1, keepdims=True)
            for weight, gradient in pairs
        )

    def as_row(column, gain):
        lane = lax.broadcasted_iota(jnp.int32, (rows, LANES), 1)
        place = lax.broadcasted_iota(jnp.int32, (rows, LANES), 0)
        whole = lax.broadcasted_iota(jnp.int32, (rows, model), 1)
        own = device_ref[0] * rows + lax.broadcasted_iota(jnp.int32, (rows, model), 0)
        own_gain = jnp.sum(jnp.where(whole == own, gain[...], 0.0), axis=1, keepdims=True)
        return jnp.sum(jnp.where(lane == place, column / own_gain, 0.0), axis=0, keepdims=True)

    row1 = as_row(weighed((input_ref, in_sum), (gate_ref, gate_sum)), gain1_ref)
    row2 = as_row(weighed((mlp_gate_ref, sum_mgate), (mlp_up_ref, sum_mup)), gain2_ref)
    sum_gain1[...] = row1[:, :rows]
    sum_gain2[...] = row2[:, :rows]
    sum_in[...] = in_sum[...]
    sum_gate[...] = gate_sum[...]
    sum_out[...] = out_sum[...]
    channels = small_ref.shape[0]
    size = sum_lgates.shape[1] // 2
    first, second = (small_ref[:, :LANES], small_ref[:, LANES:])
    lane = lax.broadcasted_iota(jnp.int32, (channels, LANES), 1)
    moved = pltpu.roll(second, size, 1)
    sum_lgates[:, :LANES] = jnp.where(lane < size, first, moved)
    sum_lgates[:, LANES:] = moved[:, : 2 * size - LANES]
    filled = jnp.concatenate([first, jnp.zeros((LANES - channels, LANES), jnp.float32)], axis=0)
    turned = filled.T
    sum_taps[...] = turned[size : size + 4, :channels]
    sum_bias[...] = turned[size + 4 : size + 5, :channels]
    sum_lbias[...] = turned[size + 5 : size + 7, :channels]
    sum_decay[...] = turned[size + 7 : size + 8, :channels]


def outputs(
    device, own, gate_sum, in_sum, out_sum, small, recur_input, recur_gate, mlp_gate, mlp_up, gain1, gain2, size
):
    rows, rec = in_sum.shape
    model, ffn = mlp_gate.shape
    channels = small.shape[0]
    f32 = jnp.float32

    def whole(shape):
        return pl.BlockSpec(shape, lambda s, device: (0,) * len(shape))

    def mine(shape):
        return pl.BlockSpec(shape, lambda s, device: (device[0], 0))

    given = (own, gate_sum, in_sum, out_sum, small)
    shapes = [(1, rows), (rows, rec), (rows, rec), (4, channels), (1, channels)]
    shapes += [(channels, 2 * size), (2, channels), (1, channels), out_sum.shape, (1, rows)]
    shapes += [(rows, ffn), (rows, ffn), (own.shape[0] - 2 * ffn // model * rows, model)]
    return pl.pallas_call(
        outputs_kernel,
        name="outputs",
        grid_spec=pltpu.PrefetchScalarGridSpec(
            num_scalar_prefetch=1,
            grid=(1,),
            in_specs=[whole(a.shape) for a in given]
            + [mine((rows, rec))] * 2
            + [mine((rows, ffn))] * 2
            + [whole((1, model))] * 2,
            out_specs=[whole(shape) for shape in shapes],
        ),
        out_shape=[jax.ShapeDtypeStruct(shape, f32) for shape in shapes],
        compiler_params=pltpu.CompilerParams(vmem_limit_bytes=VMEM_BYTES),
    )(
        device[None],
        *given,
        recur_input,
        recur_gate,
        mlp_gate,
        mlp_up,
        gain1[None],
        gain2[None],
    )


def spread_kernel(whole_ref, out_ref):
    out_ref[0] = whole_ref[...]


def spread(whole, count):
    tokens, width = (whole.shape[0], whole.shape[1] // count)
    return pl.pallas_call(
        spread_kernel,
        name="spread_features",
        grid=(count,),
        in_specs=[pl.BlockSpec((tokens, width), lambda j: (0, j))],
        out_specs=pl.BlockSpec((1, tokens, width), lambda j: (j, 0, 0)),
        out_shape=jax.ShapeDtypeStruct((count, tokens, width), whole.dtype),
        cost_estimate=pl.CostEstimate(
            flops=0, bytes_accessed=4 * tokens * whole.shape[1], transcendentals=0
        ),
    )(whole)


CHAN = ("zed", "core")


def features_in(local, pick=slice(None)):
    count = lax.axis_size(CHAN)
    rows, length, width = local.shape
    local = local.reshape(count, rows // count, length, width)[:, pick]
    if width % LANES == 0:
        return lax.all_to_all(local, CHAN, 0, 0, tiled=True).reshape(count, -1, width)
    moved = lax.all_to_all(
        local.reshape(-1, length, width), CHAN, split_axis=0, concat_axis=2, tiled=True
    )
    return moved.reshape(1, -1, count * width)


def features_apart(whole):
    count = lax.axis_size(CHAN)
    if (whole.shape[1] // count) % LANES == 0:
        return spread(whole, count)
    return whole[None]


def features_out(parts, rows):
    blocks, tokens, width = parts.shape
    parts = parts.reshape(blocks, rows, tokens // rows, width)
    if blocks > 1:
        moved = lax.all_to_all(parts, CHAN, 0, 0, tiled=True)
        return moved.reshape(-1, *parts.shape[2:])
    return lax.all_to_all(parts[0], CHAN, split_axis=2, concat_axis=0, tiled=True)


class Corners:
    def __init__(self, seq, zed):
        self.seq_bits, self.zed_bits = (seq.bit_length() - 1, zed.bit_length() - 1)
        self.count = self.seq_bits + self.zed_bits
        self.dims = (2,) * self.count
        self.low = tuple(range(self.seq_bits))[::-1] + tuple(range(self.seq_bits, self.count))[::-1]
        self.high = tuple(range(self.seq_bits)) + tuple(range(self.seq_bits, self.count))[::-1]

    def place(self, dim):
        if dim < self.seq_bits:
            return ("seq", 2 ** (self.seq_bits - 1 - dim))
        return ("zed", 2 ** (self.count - 1 - dim))

    def bit(self, dim):
        axis, weight = self.place(dim)
        return lax.rem(lax.div(lax.axis_index(axis), weight), 2)

    def partner(self, dim):
        axis, weight = self.place(dim)
        return {axis: lax.axis_index(axis) + weight * (1 - 2 * self.bit(dim))}


def tail_kernel(
    corners,
    orders,
    dgate_hbm,
    dbranch_hbm,
    ending_ref,
    leading_ref,
    mixed_hbm,
    dres_hbm,
    gain_ref,
    input_hbm,
    gate_hbm,
    small_hbm,
    *refs,
):
    rows = ending_ref.shape[0]
    normed_hbms, x_hbms, inverse_hbms = (refs[k * rows : (k + 1) * rows] for k in range(3))
    tokens_ref, sum_gate, sum_out, sum_in, sum_small = refs[3 * rows : 3 * rows + 5]
    refs = refs[3 * rows + 5 :]
    stages = corners.count + 1
    dgate, dbranch, mixed, dres, normed, x, inverse, weight_in, weight_gate = refs[:9]
    made_in, made_out, own_small, back, parts, rim = refs[9:15]
    slots_in, slots_out, slots_small = (
        refs[15 + k * stages : 15 + (k + 1) * stages] for k in range(3)
    )
    (
        send_sem,
        recv_sem,
        load_sem,
        move_send,
        move_recv,
        keep_sem,
        rim_send,
        rim_recv,
    ) = refs[15 + 3 * stages :]
    seq, zed, core = (lax.axis_index(axis) for axis in ("seq", "zed", "core"))
    seqs, group = (lax.axis_size("seq"), 2 * lax.axis_size("zed"))
    mine = zed * 2 + core
    length = tokens_ref.shape[1]
    model = x.shape[1]

    def member(index):
        return {"zed": lax.div(index, 2), "core": lax.rem(index, 2)}

    def by_row(sources, target):
        return [
            (source, target.at[pl.ds(row * length, length)]) for row, source in enumerate(sources)
        ]

    pairs = [
        (dbranch_hbm, dbranch),
        (input_hbm, weight_in),
        (dgate_hbm, dgate),
        (gate_hbm, weight_gate),
        *by_row(x_hbms, x),
        *by_row(inverse_hbms, inverse),
        (dres_hbm, dres),
        *by_row(normed_hbms, normed),
        (mixed_hbm, mixed),
        (small_hbm.at[(slice(None),) * corners.count + (core,)], own_small),
    ]
    kinds = []
    for name in ('dbranch', 'win', 'dgate', 'wgate', 'x', 'inverse', 'dres', 'normed', 'mixed', 'small'):
        kinds += [name] * (rows if name in ("normed", "x", "inverse") else 1)
    loads = [
        pltpu.make_async_copy(source, target, load_sem.at[place])
        for place, (source, target) in enumerate(pairs)
    ]
    for load in loads:
        load.start()

    barrier = pltpu.get_barrier_semaphore()
    for other in range(1, group):
        pl.semaphore_signal(
            barrier, inc=1, device_id=member(lax.rem(mine + other, group)), device_id_type=MESH
        )
    for other in range(1, seqs):
        pl.semaphore_signal(
            barrier, inc=1, device_id={"seq": lax.rem(seq + other, seqs)}, device_id_type=MESH
        )
    pl.semaphore_wait(barrier, group - 1 + seqs - 1)

    rim_copy = pltpu.make_async_remote_copy(
        src_ref=leading_ref,
        dst_ref=rim,
        send_sem=rim_send,
        recv_sem=rim_recv,
        device_id={"seq": lax.rem(seq + seqs - 1, seqs)},
        device_id_type=MESH,
    )
    rim_copy.start()

    def own(stream, index):
        if stream < 4:
            return made_in.at[(stream,) + index + (core,)]
        if stream < 6:
            return made_out.at[(stream - 4,) + index + (core,)]
        return own_small.at[index]

    def slot(stream, stage):
        if stream < 4:
            return slots_in[stage].at[stream]
        if stream < 6:
            return slots_out[stage].at[stream - 4]
        return slots_small[stage]

    def copy(stream, stage):
        order = orders[stream]
        every = (slice(None),) * corners.count
        if stage == 0:
            if stream < 4:
                source = made_in.at[(stream,) + every + (1 - core,)]
            elif stream < 6:
                source = made_out.at[(stream - 4,) + every + (1 - core,)]
            else:
                source = small_hbm.at[every + (1 - core,)]
            target = {"core": 1 - core}
        else:
            dim = order[stage - 1]
            fixed = {before: corners.bit(before) for before in order[: stage - 1]}
            fixed[dim] = 1 - corners.bit(dim)
            source = own(stream, tuple(fixed.get(d, slice(None)) for d in range(corners.count)))
            target = corners.partner(dim)
        return pltpu.make_async_remote_copy(
            src_ref=source,
            dst_ref=slot(stream, stage),
            send_sem=send_sem.at[stream, stage],
            recv_sem=recv_sem.at[stream, stage],
            device_id=target,
            device_id_type=MESH,
        )

    sums = [
        sum_gate.at[:, : sum_gate.shape[1] // 2],
        sum_gate.at[:, sum_gate.shape[1] // 2 :],
        sum_in.at[:, : sum_in.shape[1] // 2],
        sum_in.at[:, sum_in.shape[1] // 2 :],
        sum_out.at[:, : sum_out.shape[1] // 2],
        sum_out.at[:, sum_out.shape[1] // 2 :],
        sum_small,
    ]

    def advance(stream, stage):
        order = orders[stream]
        copy(stream, stage).wait_recv()
        left = [dim for dim in range(corners.count) if dim not in order[:stage]]
        fixed = {dim: corners.bit(dim) for dim in order[:stage]}
        arrived = slot(stream, stage)
        if not left:
            index = tuple(fixed[dim] for dim in range(corners.count))
            sums[stream][...] = own(stream, index)[...].astype(jnp.float32) + arrived[...].astype(
                jnp.float32
            )
            return

        def add(index, carry):
            part = {
                dim: lax.rem(lax.div(index, 2 ** (len(left) - 1 - place)), 2)
                for place, dim in enumerate(left)
            }
            kept = own(stream, tuple({**fixed, **part}[dim] for dim in range(corners.count)))
            total = kept[...].astype(jnp.float32) + arrived[
                tuple(part[dim] for dim in left)
            ].astype(jnp.float32)
            kept[...] = total.astype(jnp.bfloat16)
            return carry

        lax.fori_loop(0, 2 ** len(left), add, 0)
        copy(stream, stage + 1).start()

    def move(other, row):
        to = lax.rem(mine + other, group)
        return pltpu.make_async_remote_copy(
            src_ref=parts.at[to, pl.ds(row * length, length)],
            dst_ref=tokens_ref.at[mine * rows + row],
            send_sem=move_send.at[other - 1, row],
            recv_sem=move_recv.at[other - 1, row],
            device_id=member(to),
            device_id_type=MESH,
        )

    def keep(row):
        return pltpu.make_async_copy(
            parts.at[mine, pl.ds(row * length, length)],
            tokens_ref.at[mine * rows + row],
            keep_sem.at[row],
        )

    tile = 256
    width = parts.shape[2]

    def back_row(row):
        at_row = slice(row * length, (row + 1) * length)

        def product(index, carry):
            at = pl.ds(pl.multiple_of(index * tile, tile), tile)
            contract = (((1,), (1,)), ((), ()))
            back[:, at] = lax.dot_general(
                dbranch[at_row, :], weight_in[at, :], contract, preferred_element_type=jnp.float32
            ) + lax.dot_general(
                dgate[at_row, :], weight_gate[at, :], contract, preferred_element_type=jnp.float32
            )
            return carry

        lax.fori_loop(0, model // tile, product, 0)
        slab = 16

        def norm(index, carry):
            base = pl.multiple_of(index * slab, slab)
            at = pl.ds(row * length + base, slab)
            inv = inverse[at, :1]
            value = x[at, :].astype(jnp.float32) * inv
            scaled = back[pl.ds(base, slab), :] * gain_ref[...]
            mean = jnp.mean(scaled * value, axis=1, keepdims=True)
            grad = dres[at, :].astype(jnp.float32) + inv * (scaled - value * mean)
            grad = grad.astype(jnp.bfloat16)
            for part in range(parts.shape[0]):
                parts[part, at, :] = grad[:, part * width : (part + 1) * width]
            return carry

        lax.fori_loop(0, length // slab, norm, 0, unroll=4)
        for other in range(1, group):
            move(other, row).start()
        keep(row).start()

    def weight_product(left, right, made, stream, first):
        columns = made.shape[-1]
        shape = made.shape[1:-1]

        def product(index, carry):
            at = pl.ds(pl.multiple_of(index * tile, tile), tile)
            source = pl.ds(pl.multiple_of(first + index * tile, tile), tile)
            part = lax.dot_general(
                left[...],
                right[:, source],
                (((0,), (0,)), ((), ())),
                preferred_element_type=jnp.float32,
            )
            made[(stream,) + (slice(None),) * len(shape) + (at,)] = part.astype(
                jnp.bfloat16
            ).reshape(shape + (tile,))
            return carry

        lax.fori_loop(0, columns // tile, product, 0)

    half, half_out = (made_in.shape[-1], made_out.shape[-1])
    waited, reached = (set(), {})

    def need(*names):
        for place, name in enumerate(kinds):
            if name in names and place not in waited:
                waited.add(place)
                loads[place].wait()

    def fix_rim():
        need("dbranch")
        rim_copy.wait()
        live = jnp.where(seq < seqs - 1, 1.0, 0.0)
        for row in range(rows):
            at = slice((row + 1) * length - STEP, (row + 1) * length)
            inside = dbranch[at, :].astype(jnp.float32)
            last = ending_ref[row] + live * rim[row]
            dbranch[at, :] = jnp.concatenate([inside[: STEP - SUBLANES], last], axis=0).astype(
                jnp.bfloat16
            )

    def begin(stream):
        copy(stream, 0).start()
        reached[stream] = 0

    def progress(streams):
        for stream in streams:
            if stream in reached and reached[stream] < stages:
                if stream == 6:
                    need("small")
                advance(stream, reached[stream])
                reached[stream] += 1

    def compute(item):
        if item == "gate":
            need("normed", "dgate")
            for stream in (0, 1):
                weight_product(normed, dgate, made_in, stream, stream * half)
                begin(stream)
        elif item == "out":
            need("mixed", "dres")
            for stream in (4, 5):
                weight_product(mixed, dres, made_out, stream - 4, (stream - 4) * half_out)
                begin(stream)
        elif item == "in":
            need("normed", "dbranch")
            for stream in (2, 3):
                weight_product(normed, dbranch, made_in, stream, (stream - 2) * half)
                begin(stream)
        else:
            need("dbranch", "dgate", "win", "wgate", "x", "inverse", "dres")
            back_row(item)

    begin(6)
    fix_rim()
    compute(0)
    compute(1)
    compute('gate')
    progress((6,))
    compute('out')
    progress((0, 1))
    compute('in')
    progress((0, 1))
    progress((4, 5))
    progress((6,))
    while any(reached[stream] < stages for stream in range(7)):
        progress((0, 1, 4, 5, 2, 3, 6))
    for stage in range(stages):
        for stream in range(7):
            copy(stream, stage).wait_send()
    for row in range(rows):
        for other in range(1, group):
            move(other, row).wait()
        keep(row).wait()


def tail(dgate, dbranch, ending, leading, mixed, dres, gain, w_in, w_gate, small, normed, x, inverse):
    corners = Corners(lax.axis_size("seq"), lax.axis_size("zed"))
    group, devices = (lax.axis_size(CHAN), 2 ** (corners.count + 1))
    tokens, model = dres.shape
    rec = dgate.shape[1]
    rows = ending.shape[0]
    length, width = (tokens // rows, model // group)
    low, f32 = (jnp.bfloat16, jnp.float32)
    stages = corners.count + 1
    in_rows, out_rows = (model // devices, rec // devices)
    small = small.reshape(corners.dims + (2, out_rows, small.shape[1]))
    orders = [corners.low, corners.high] * 3 + [corners.low]

    def slots(lead, shape):
        return [pltpu.VMEM(lead + (2,) * (corners.count - k) + shape, low) for k in range(stages)]

    in_shape, out_shape = ((in_rows, rec // 2), (out_rows, model // 2))
    loaded = (dgate, dbranch, mixed, dres, dres, dres)
    loaded += (jax.ShapeDtypeStruct((tokens, LANES), f32), w_in, w_gate)
    anyplace = pl.BlockSpec(memory_space=pl.ANY)
    vmem = pl.BlockSpec(memory_space=pltpu.VMEM)
    dma = pltpu.SemaphoreType.DMA
    moved = sum(math.prod(a.shape) * a.dtype.itemsize for a in loaded)
    return pl.pallas_call(
        functools.partial(tail_kernel, corners, orders),
        name="tail",
        in_specs=[anyplace, anyplace, vmem, vmem, anyplace, anyplace, vmem]
        + [anyplace] * (3 + 3 * rows),
        out_specs=[anyplace] + [vmem] * 4,
        out_shape=[
            jax.ShapeDtypeStruct((group * rows, length, width), low),
            jax.ShapeDtypeStruct((in_rows, rec), f32),
            jax.ShapeDtypeStruct((out_rows, model), f32),
            jax.ShapeDtypeStruct((in_rows, rec), f32),
            jax.ShapeDtypeStruct(small.shape[-2:], f32),
        ],
        scratch_shapes=[pltpu.VMEM(a.shape, a.dtype) for a in loaded]
        + [
            pltpu.VMEM((4,) + corners.dims + (2,) + in_shape, low),
            pltpu.VMEM((2,) + corners.dims + (2,) + out_shape, low),
            pltpu.VMEM(corners.dims + small.shape[-2:], low),
            pltpu.VMEM((length, model), f32),
            pltpu.VMEM((group, tokens, width), low),
            pltpu.VMEM(leading.shape, leading.dtype),
        ]
        + slots((4,), in_shape)
        + slots((2,), out_shape)
        + slots((), small.shape[-2:])
        + [
            dma((7, stages)),
            dma((7, stages)),
            dma((7 + 3 * rows,)),
            dma((group - 1, rows)),
            dma((group - 1, rows)),
            dma((rows,)),
            dma,
            dma,
        ],
        compiler_params=pltpu.CompilerParams(
            collective_id=1, has_side_effects=True, vmem_limit_bytes=60 * 1024 * 1024
        ),
        cost_estimate=pl.CostEstimate(
            flops=10 * tokens * model * rec, bytes_accessed=2 * moved, transcendentals=0
        ),
    )(dgate, dbranch, ending, leading, mixed, dres, gain[None], w_in, w_gate, small, *normed, *x, *inverse)


def grads_kernel(
    normed_ref,
    dgate_ref,
    dup_ref,
    hidden_ref,
    gout_ref,
    out_ref,
    turned_ref,
    made_wide,
    made_down,
    come_wide,
    come_down,
    send_sem,
    recv_sem,
    store_sem,
):
    step = pl.program_id(0)
    core = lax.axis_index("core")
    other = {"core": 1 - core}
    wide_rows, down_rows = (made_wide.shape[3], made_down.shape[3])
    wides, downs = (come_wide.shape[0], come_down.shape[0])
    total = wides + downs
    down_at = wides * wide_rows

    def exchange(made, come, index, slot):
        return pltpu.make_async_remote_copy(
            src_ref=made.at[lax.rem(index, 2), 1 - core],
            dst_ref=come.at[index],
            send_sem=send_sem.at[slot],
            recv_sem=recv_sem.at[slot],
            device_id=other,
            device_id_type=MESH,
        )

    def store_wide(index):
        return pltpu.make_async_copy(
            come_wide.at[index],
            out_ref.at[:, pl.ds(pl.multiple_of(index * wide_rows, wide_rows), wide_rows)],
            store_sem.at[index],
        )

    def store_down(index):
        chips = come_down.shape[1]
        return pltpu.make_async_copy(
            come_down.at[index],
            out_ref.at[pl.ds(index * chips, chips), pl.ds(down_at, down_rows)],
            store_sem.at[index + wides],
        )

    @pl.when(step == 0)
    def _():
        barrier = pltpu.get_barrier_semaphore()
        pl.semaphore_signal(barrier, inc=1, device_id=other, device_id_type=MESH)
        pl.semaphore_wait(barrier, 1)
        turned_ref[...] = normed_ref[...].T

    def product_wide(source, index):
        made = made_wide.at[lax.rem(index, 2)]
        chips, rows = (made.shape[1], made.shape[2])
        tile = 512

        def column(place, carry):
            at = pl.ds(pl.multiple_of(place * tile, tile), tile)
            part = jnp.dot(turned_ref[...], source[:, at], preferred_element_type=jnp.float32)
            part = part.astype(jnp.bfloat16).reshape(chips, 2, rows, tile)
            made[0, :, :, at] = part[:, 0]
            made[1, :, :, at] = part[:, 1]
            return carry

        lax.fori_loop(0, source.shape[1] // tile, column, 0)

    def product_tall(left, right, made_all, index):
        made = made_all.at[lax.rem(index, 2)]
        chips, rows = (made.shape[1], made.shape[2])
        tile = 512

        def column(place, carry):
            at = pl.ds(pl.multiple_of(place * tile, tile), tile)
            part = lax.dot_general(
                left[...], right[:, at], (((0,), (0,)), ((), ())), preferred_element_type=jnp.float32
            )
            part = part.astype(jnp.bfloat16).reshape(chips, 2, rows, tile)
            made[0, :, :, at] = part[:, 0]
            made[1, :, :, at] = part[:, 1]
            return carry

        lax.fori_loop(0, right.shape[1] // tile, column, 0)

    half = wides // 2

    @pl.when(step < half)
    def _():
        product_wide(dgate_ref, step)

    @pl.when((step >= half) & (step < wides))
    def _():
        product_wide(dup_ref, step)

    @pl.when(step < wides)
    def _():
        exchange(made_wide, come_wide, step, step).start()

    @pl.when((step >= wides) & (step < total))
    def _():
        product_tall(hidden_ref, gout_ref, made_down, step - wides)
        exchange(made_down, come_down, step - wides, step).start()

    def finish(made, come, index, slot, store):
        exchange(made, come, index, slot).wait()
        mine = made.at[lax.rem(index, 2), core]
        arrived = come.at[index]

        def add(chip, carry):
            both = mine[chip].astype(jnp.float32) + arrived[chip].astype(jnp.float32)
            arrived[chip] = both.astype(jnp.bfloat16)
            return carry

        lax.fori_loop(0, come.shape[1], add, 0)
        store(index).start()

    before = step - 1

    @pl.when((before >= 0) & (before < wides))
    def _():
        finish(made_wide, come_wide, before, before, store_wide)

    @pl.when(before >= wides)
    def _():
        finish(made_down, come_down, before - wides, before, store_down)

    @pl.when(step == total)
    def _():
        for index in range(wides):
            store_wide(index).wait()
        for index in range(downs):
            store_down(index).wait()


def block_gradients(normed, dgate, dup, hidden, gout):
    tokens, model = normed.shape
    ffn = hidden.shape[1]
    chips = lax.axis_size("seq") * lax.axis_size("zed")
    devices = 2 * chips
    wide_rows, down_rows = (model // devices, ffn // devices)
    chunk = 768
    wides, downs = (2 * ffn // model, ffn // chunk)
    half = wides // 2
    down_chips = chunk // (2 * down_rows)
    rows = wides * wide_rows + down_rows
    low = jnp.bfloat16

    def whole(array):
        return pl.BlockSpec(array.shape, lambda s: (0, 0), pipeline_mode=pl.Buffered(1))

    def part(columns, first, count):
        return pl.BlockSpec((tokens, columns), lambda s: (0, jnp.clip(s - first, 0, count - 1)))

    total = wides + downs
    flops = 6 * tokens * model * ffn
    arrays = (normed, dgate, dup, hidden, gout)
    moved = sum(math.prod(a.shape) * 2 for a in arrays) + chips * rows * model * 2
    return pl.pallas_call(
        grads_kernel,
        name="block_gradients",
        grid=(total + 1,),
        in_specs=[
            whole(normed),
            part(model, 0, half),
            part(model, half, half),
            part(chunk, wides, downs),
            whole(gout),
        ],
        out_specs=pl.BlockSpec(memory_space=pl.ANY),
        out_shape=jax.ShapeDtypeStruct((chips, rows, model), low),
        scratch_shapes=[
            pltpu.VMEM((model, tokens), low),
            pltpu.VMEM((2, 2, chips, wide_rows, model), low),
            pltpu.VMEM((2, 2, down_chips, down_rows, model), low),
            pltpu.VMEM((wides, chips, wide_rows, model), low),
            pltpu.VMEM((downs, down_chips, down_rows, model), low),
            pltpu.SemaphoreType.DMA((total,)),
            pltpu.SemaphoreType.DMA((total,)),
            pltpu.SemaphoreType.DMA((total,)),
        ],
        compiler_params=pltpu.CompilerParams(
            collective_id=2, has_side_effects=True, vmem_limit_bytes=VMEM_BYTES
        ),
        cost_estimate=pl.CostEstimate(flops=flops, bytes_accessed=moved, transcendentals=0),
    )(*arrays)


def passed_along(value, axis, steps):
    count = lax.axis_size(axis)
    leading, last = (max(0, -steps), min(count, count - steps))
    return lax.ppermute(value, axis, [(source, source + steps) for source in range(leading, last)])


def weight_grad(left, right):
    return lax.dot_general(
        left, right, (((0,), (0,)), ((), ())), preferred_element_type=jnp.float32
    ).astype(jnp.bfloat16)


def back_dot(left, right):
    return lax.dot_general(
        left, right, (((1,), (1,)), ((), ())), preferred_element_type=jnp.float32
    )


def fwd_dot(left, right):
    return jnp.dot(left, right, preferred_element_type=jnp.float32)


def gelu_fn(value):
    return jax.nn.gelu(value, approximate=True)


def norm_back(grad_norm, normed, inverse, gain):
    scaled = grad_norm * gain
    mean_term = jnp.mean(scaled * normed, axis=1, keepdims=True)
    return inverse * (scaled - normed * mean_term)


def scattered(gradient):
    return lax.psum_scatter(
        gradient, ("seq", "zed", "core"), scatter_dimension=0, tiled=True
    ).astype(jnp.float32)


def body(
    tokens,
    cotangent,
    doc_starts,
    lengths,
    norm1_gain,
    recur_input,
    recur_gate,
    conv_kernel,
    conv_bias,
    lru_gates,
    lru_bias,
    lru_decay,
    recur_out,
    norm2_gain,
    mlp_gate,
    mlp_up,
    mlp_down,
):
    count = lax.axis_size(CHAN)
    row_count, block_len = (tokens.shape[0] // count, tokens.shape[1])
    model_dim = tokens.shape[2] * count
    tok_count = row_count * block_len
    rec_width = recur_input.shape[1]
    ffn_width = mlp_gate.shape[1]
    head_count = H
    head_size = rec_width // head_count
    tap_count = conv_kernel.shape[0]
    rim_size = tap_count - 1
    seq_index = lax.axis_index("seq")
    position = seq_index * block_len + jnp.arange(block_len, dtype=jnp.int32)
    bounds = jnp.concatenate([doc_starts, lengths[:, None]], axis=1)
    is_before = bounds[:, None, :] <= position[None, :, None]
    seg_start = jnp.max(jnp.where(is_before, bounds[:, None, :], 0), axis=2)
    dist = jnp.broadcast_to(
        (position[None, :] - seg_start)[:, :, None], (row_count, block_len, LANES)
    )
    soft_decay = jax.nn.softplus(-lru_decay)
    params = jnp.concatenate(
        [
            conv_kernel,
            conv_bias[None],
            lru_bias,
            (-8.0 * soft_decay)[None],
            (8.0 * jax.nn.sigmoid(-lru_decay))[None],
            jnp.zeros((SUBLANES - 1, rec_width), jnp.float32),
        ],
        axis=0,
    )
    core = Recurrence(row_count, block_len, rec_width, head_size)
    wide_gates = core.widen(lru_gates)
    if tokens.shape[2] % LANES == 0:
        blocks = [features_in(tokens, slice(0, 1))]
        later, wide_gates, params, dist = lax.optimization_barrier(
            (tokens, wide_gates, params, dist)
        )
        blocks += [features_in(later, slice(row, row + 1)) for row in range(1, row_count)]
    else:
        side = features_in(tokens)
        blocks = [side[:, row * block_len : (row + 1) * block_len] for row in range(row_count)]
    per_row = []
    for row in range(row_count):
        block = blocks[row]
        if row:
            block, _ = lax.optimization_barrier((block, per_row[-1][-1]))
        per_row.append(
            front(
                block,
                norm1_gain,
                recur_input,
                recur_gate,
                dist[row : row + 1],
                params,
                wide_gates,
            )
        )
    low_x, inverse, normed_low, branch, gate_pre, rim, lru_in, rate, igate, state, cum, last = zip(
        *per_row
    )
    entering, mixed_low, resid_one, normed_low2 = middle(
        last, state, cum, gate_pre, low_x, recur_out, norm2_gain
    )
    cotangent, _ = lax.optimization_barrier((cotangent, block))
    cotangent, resid_one = lax.optimization_barrier((features_in(cotangent), resid_one))
    grad_low, hidden_low, mgate_low, mup_low = mlp_hidden(
        lengths - seq_index * block_len, cotangent, normed_low2, mlp_gate, mlp_up, mlp_down
    )
    devices = lax.axis_size(("seq", "zed", "core"))
    own_rows = model_dim // devices
    tiled = own_rows % (2 * SUBLANES) == 0 and tokens.shape[2] % LANES == 0
    if tiled:
        merged = block_gradients(normed_low2, mgate_low, mup_low, hidden_low, grad_low)
        merged, hidden_low = lax.optimization_barrier((merged, hidden_low))
        merged = lax.psum_scatter(merged, "seq", scatter_dimension=0, tiled=True)
    result_parts, resid_low = mlp_back(
        hidden_low,
        mgate_low,
        mup_low,
        grad_low,
        resid_one,
        norm2_gain,
        mlp_gate,
        mlp_up,
        mlp_down,
        cotangent.shape,
    )
    output = features_out(result_parts, row_count)
    gate_low, back_local, back_cum, first_term = core.adjoint(
        resid_low,
        recur_out,
        gate_pre,
        state,
        cum,
        entering,
        rate,
        dist,
        params,
    )
    gate_low = gate_low.reshape(tok_count, rec_width)

    def zed_stage(leaving):
        if not tiled:
            return ((), leaving)
        done, leaving = lax.optimization_barrier((merged, leaving))
        return (lax.psum_scatter(done, "zed", scatter_dimension=0, tiled=True), leaving)

    branch_local, ending, leading, small, merged_own = core.backward(
        back_local,
        back_cum,
        first_term,
        last,
        state,
        cum,
        entering,
        rate,
        igate,
        lru_in,
        dist,
        branch,
        rim,
        params,
        wide_gates,
        zed_stage,
    )
    branch_low = branch_local.reshape(tok_count, rec_width)
    if tiled:
        output, branch_low = lax.optimization_barrier((output, branch_low))
        grad_tokens, sum_rgate, sum_rout, sum_rin, own_small = tail(
            gate_low,
            branch_low,
            ending,
            leading,
            mixed_low,
            resid_low,
            norm1_gain,
            recur_input,
            recur_gate,
            small,
            normed_low,
            low_x,
            inverse,
        )
        device = lax.axis_index(("seq", "zed", "core"))
        sums = outputs(
            device,
            merged_own[0],
            sum_rgate,
            sum_rin,
            sum_rout,
            own_small,
            recur_input,
            recur_gate,
            mlp_gate,
            mlp_up,
            norm1_gain,
            norm2_gain,
            head_size,
        )
        flat = (0, 4, 7, 9)
        sums = [part.reshape(-1) if place in flat else part for place, part in enumerate(sums)]
        return (output, grad_tokens, *sums)
    else:
        from_next = passed_along(
            leading[:, SUBLANES - rim_size :, :].astype(jnp.bfloat16), "seq", -1
        )
        ending = ending + jnp.pad(
            from_next.astype(jnp.float32), ((0, 0), (SUBLANES - rim_size, 0), (0, 0))
        )
        branch_low = lax.dynamic_update_slice(
            branch_local, ending.astype(jnp.bfloat16), (0, block_len - SUBLANES, 0)
        ).reshape(tok_count, rec_width)
        grad_norm1 = back_dot(branch_low, recur_input) + back_dot(gate_low, recur_gate)
        inv_one = jnp.concatenate(inverse)[:, :1]
        normed_one = jnp.concatenate(low_x).astype(jnp.float32) * inv_one
        normed_low = jnp.concatenate(normed_low)
        input_part = norm_back(grad_norm1, normed_one, inv_one, norm1_gain)
        grad_x = (resid_low.astype(jnp.float32) + input_part).astype(jnp.bfloat16)
        grad_tokens = features_out(features_apart(grad_x), row_count)
        sum_mgate, sum_mup, sum_down, sum_rout, sum_rgate, sum_rin = (
            scattered(weight_grad(left, right))
            for left, right in (
                (normed_low2, mgate_low),
                (normed_low2, mup_low),
                (hidden_low, grad_low),
                (mixed_low, resid_low),
                (normed_low, gate_low),
                (normed_low, branch_low),
            )
        )
        own_small = scattered(small)
    sum_lgates = jnp.concatenate(
        [own_small[:, :head_size], own_small[:, LANES : LANES + head_size]], axis=1
    )
    own_sums = jnp.swapaxes(own_small[:, head_size : head_size + SUBLANES], 0, 1)
    device = lax.axis_index(("seq", "zed", "core"))

    def mine(array, size, axis=0):
        return lax.dynamic_slice_in_dim(array, device * size, size, axis)

    def weighed(weight, gradient):
        return jnp.sum(mine(weight, own_rows).astype(jnp.float32) * gradient, axis=1)

    sum_gain1 = (weighed(recur_input, sum_rin) + weighed(recur_gate, sum_rgate)) / mine(
        norm1_gain, own_rows
    )
    sum_gain2 = (weighed(mlp_gate, sum_mgate) + weighed(mlp_up, sum_mup)) / mine(
        norm2_gain, own_rows
    )
    sum_decay = own_sums[7]
    return (
        output,
        grad_tokens,
        sum_gain1,
        sum_rin,
        sum_rgate,
        own_sums[:4],
        own_sums[4],
        sum_lgates,
        own_sums[5:7],
        sum_decay,
        sum_rout,
        sum_gain2,
        sum_mgate,
        sum_mup,
        sum_down,
    )


def solution(mesh):
    seq, chan = (mesh.shape["seq"], mesh.shape["chan"])
    chips = jax.sharding.Mesh(mesh.devices.reshape(seq, chan // 2, 2), ("seq", "zed", "core"))
    chan = ("zed", "core")
    every = ("seq", "zed", "core")
    activations = P(None, "seq", chan)
    rows, columns, vector = (P(every, None), P(None, every), P(every))
    return jax.shard_map(
        body,
        mesh=chips,
        in_specs=(activations, activations, P(chan, None), P(chan)) + (P(),) * 13,
        out_specs=(
            activations,
            activations,
            vector,
            rows,
            rows,
            columns,
            vector,
            rows,
            columns,
            vector,
            rows,
            vector,
            rows,
            rows,
            rows,
        ),
        check_vma=False,
    )
```

```python
import functools
import math

import jax
import jax.numpy as jnp
from jax import lax
from jax.experimental import pallas as pl
from jax.experimental.pallas import tpu as pltpu
from jax.sharding import PartitionSpec as P

H = 16


EPS = 1e-06
ROOT_FLOOR = 1e-06
LANES = 128
SUBLANES = 8
STEP = 16
VMEM_BYTES = 56 * 1024 * 1024
MESH = pl.DeviceIdType.MESH


def sigmoid(value):
    return 0.5 * jnp.tanh(0.5 * value) + 0.5


GELU_C = 0.7978845608
GELU_A = 0.044715


def gelu_pair(value):
    square = value * value
    inner = jnp.tanh(value * (GELU_C + (GELU_C * GELU_A) * square))
    half = 0.5 + 0.5 * inner
    slope = GELU_C + (3.0 * GELU_C * GELU_A) * square
    return (value * half, half + 0.5 * value * (1.0 - inner * inner) * slope)


def root_argument(log_decay, decay):
    y = 2.0 * log_decay
    series = 1.0 + y * (0.5 + y * (1.0 / 6.0 + y * (1.0 / 24.0)))
    return jnp.where(y > -0.05, -y * series, 1.0 - decay * decay)


def across(column, width):
    return jnp.concatenate([column] * (width // LANES), axis=1)


class Rows:
    def __init__(self, refs):
        self.refs = refs

    def __getitem__(self, index):
        if not isinstance(index, tuple):
            return self.refs[index][0]
        return self.refs[index[0]][(0,) + index[1:]]


def by_rows(refs, rows, apart):
    found = []
    for split in apart:
        count = rows if split else 1
        found.append(Rows(refs[:count]) if split else refs[0])
        refs = refs[count:]
    return found, refs


def scan_block(
    branch_ref,
    rim_ref,
    dist_ref,
    par_ref,
    gates_ref,
    lru_ref,
    rate_ref,
    igate_ref,
    state_ref,
    cum_ref,
    last_ref,
    both_ref,
):
    rows, length, width = branch_ref.shape
    span = 2 * STEP if rows == 1 else STEP
    taps = [par_ref[k : k + 1, :] for k in range(4)]
    conv_bias, rate_bias, input_bias, soft = (par_ref[k : k + 1, :] for k in range(4, 8))
    place = lax.broadcasted_iota(jnp.int32, (SUBLANES, width), 0)

    for row in range(rows):

        def conv_step(index, before, row=row):
            base = pl.multiple_of(index * STEP, STEP)
            pieces = []
            for half in range(STEP // SUBLANES):
                at = pl.ds(base + half * SUBLANES, SUBLANES)
                here = branch_ref[row, at, :]
                dist = across(dist_ref[row, at, :], width)
                total = conv_bias + taps[0] * here
                for k in range(1, 4):
                    shifted = pltpu.roll(jnp.where(place < SUBLANES - k, here, before), k, 0)
                    total = total + taps[k] * jnp.where(dist >= k, shifted, 0.0)
                pieces.append(total)
                before = here
            lru_ref[row, pl.ds(base, STEP), :] = jnp.concatenate(pieces, axis=0).astype(jnp.bfloat16)
            return before

        lax.fori_loop(0, length // STEP, conv_step, rim_ref[row], unroll=2)

        piece = min(length, 256)

        def dot_step(index, carry, row=row):
            at = pl.ds(pl.multiple_of(index * piece, piece), piece)
            both_ref[row, at, :] = jnp.dot(
                lru_ref[row, at, :], gates_ref[...], preferred_element_type=jnp.float32
            )
            return carry

        lax.fori_loop(0, length // piece, dot_step, 0)

    def scan_step(index, carry):
        base = pl.multiple_of(index * span, span)
        later = []
        for row in range(rows):
            run_cum, run_state = carry[row]
            lru_both = lru_ref[row, pl.ds(base, span), :].astype(jnp.float32)
            for half in range(span // SUBLANES):
                at = pl.ds(base + half * SUBLANES, SUBLANES)
                lru = lru_both[half * SUBLANES : (half + 1) * SUBLANES]
                start = across(dist_ref[row, at, :], width) == 0
                rate = sigmoid(both_ref[row, at, :width] + rate_bias)
                igate = sigmoid(both_ref[row, at, width:] + input_bias)
                log_decay = rate * soft
                decay = jnp.exp(log_decay)
                arg = jnp.maximum(root_argument(log_decay, decay), ROOT_FLOOR)
                root = arg * lax.rsqrt(arg)
                cum = jnp.where(start, 0.0, decay)
                value = jnp.where(start, 1.0, root) * igate * lru
                rate_ref[row, at, :] = rate
                igate_ref[row, at, :] = igate
                for shift in (1, 2, 4):
                    live = place >= shift
                    value = value + cum * jnp.where(live, pltpu.roll(value, shift, 0), 0.0)
                    cum = cum * jnp.where(live, pltpu.roll(cum, shift, 0), 1.0)
                value = value + cum * run_state
                cum = cum * run_cum
                state_ref[row, at, :] = value
                cum_ref[row, at, :] = cum
                run_state = value[SUBLANES - 1 :, :]
                run_cum = cum[SUBLANES - 1 :, :]
            later.append((run_cum, run_state))
        return tuple(later)

    one, zero = (jnp.ones((1, width), jnp.float32), jnp.zeros((1, width), jnp.float32))
    done = lax.fori_loop(
        0, length // span, scan_step, tuple((one, zero) for _ in range(rows)), unroll=2
    )
    for row in range(rows):
        for place in range(2):
            last_ref[row, place : place + 1, :] = done[row][place]


def carried(sent_ref, got_ref, out_ref, send_sem, recv_sem, backward):
    seq, count = (lax.axis_index("seq"), lax.axis_size("seq"))

    def other(step):
        return {"seq": lax.rem(seq + step, count)}

    barrier = pltpu.get_barrier_semaphore()
    for step in range(1, count):
        pl.semaphore_signal(barrier, inc=1, device_id=other(step), device_id_type=MESH)
    pl.semaphore_wait(barrier, count - 1)
    copies = [
        pltpu.make_async_remote_copy(
            src_ref=sent_ref,
            dst_ref=got_ref.at[seq],
            send_sem=send_sem.at[step - 1],
            recv_sem=recv_sem.at[step - 1],
            device_id=other(step),
            device_id_type=MESH,
        )
        for step in range(1, count)
    ]
    for copy in copies:
        copy.start()
    got_ref[seq] = sent_ref[...]
    for copy in copies:
        copy.wait()
    for row in range(sent_ref.shape[0]):
        total = jnp.zeros(out_ref.shape[1:], jnp.float32)
        for place in range(count - 1, 0, -1) if backward else range(count - 1):
            longer = got_ref[place, row, 0:1, :] * total + got_ref[place, row, 1:2, :]
            total = jnp.where(place > seq if backward else place < seq, longer, total)
        out_ref[row] = total


def adjoint_kernel(rows, *refs):
    (
        dres_ref,
        weight_ref,
        pre_ref,
        state_ref,
        cum_ref,
        carry_ref,
        rate_ref,
        dist_ref,
        par_ref,
    ), outs = by_rows(refs, rows, (False, False, True, True, True, False, True, False, False))
    dgate_ref, local_ref, back_ref, first_ref, dmix_ref = outs
    _, length, width = dmix_ref.shape
    for row in range(rows):
        dmix_ref[row] = lax.dot_general(
            dres_ref[row * length : (row + 1) * length, :],
            weight_ref[...],
            (((1,), (1,)), ((), ())),
            preferred_element_type=jnp.float32,
        )
    soft = par_ref[7:8, :]
    place = lax.broadcasted_iota(jnp.int32, (SUBLANES, width), 0)
    last = length // STEP - 1

    def step(index, carry):
        base = pl.multiple_of((last - index) * STEP, STEP)
        later = []
        for row in range(rows):
            run_cum, run_back = carry[row]
            entering = carry_ref[row]
            pieces = []
            for half in reversed(range(STEP // SUBLANES)):
                at = pl.ds(base + half * SUBLANES, SUBLANES)
                start = across(dist_ref[row, at, :], width) == 0
                state = state_ref[row, at, :] + cum_ref[row, at, :] * entering
                act, slope = gelu_pair(pre_ref[row, at, :])
                dmix = dmix_ref[row, at, :]
                pieces.append(dmix * state * slope)
                dstate = dmix * act
                coef = jnp.where(start, 0.0, jnp.exp(rate_ref[row, at, :] * soft))
                value = coef * dstate
                for shift in (1, 2, 4):
                    live = place < SUBLANES - shift
                    turn = SUBLANES - shift
                    value = value + coef * jnp.where(live, pltpu.roll(value, turn, 0), 0.0)
                    coef = coef * jnp.where(live, pltpu.roll(coef, turn, 0), 1.0)
                value = value + coef * run_back
                coef = coef * run_cum
                inside = place < SUBLANES - 1
                local_ref[row, at, :] = dstate + jnp.where(
                    inside, pltpu.roll(value, SUBLANES - 1, 0), run_back
                )
                back_ref[row, at, :] = jnp.where(inside, pltpu.roll(coef, SUBLANES - 1, 0), run_cum)
                run_back = value[:1, :]
                run_cum = coef[:1, :]
            dgate_ref[row, pl.ds(base, STEP), :] = jnp.concatenate(pieces[::-1], axis=0).astype(
                jnp.bfloat16
            )
            later.append((run_cum, run_back))
        return tuple(later)

    one, zero = (jnp.ones((1, width), jnp.float32), jnp.zeros((1, width), jnp.float32))
    done = lax.fori_loop(0, last + 1, step, tuple((one, zero) for _ in range(rows)), unroll=2)
    for row in range(rows):
        first_ref[row] = done[row][1]


def backward_kernel(head_size, rows, *refs):
    first_at = 2
    sent_ref, got_ref, send_sem, recv_sem = refs[-4:]
    leaving_ref = refs[-8]
    lasts = Rows(refs[first_at + 1 : first_at + 1 + rows])

    @pl.when(pl.program_id(0) == 0)
    def _():
        for row in range(rows):
            sent_ref[row, 0:1, :] = lasts[row, 0:1, :]
            sent_ref[row, 1:2, :] = refs[first_at][row]
        carried(sent_ref, got_ref, leaving_ref, send_sem, recv_sem, True)

    block_backward(head_size, rows, 0, leaving_ref, *refs[:-8], *refs[-7:-4])


def later_backward_kernel(head_size, rows, first, *refs):
    held = 4
    block_backward(head_size, rows, first, refs[0], *refs[1 + held :])


def block_backward(head_size, rows, first_block, leaving_ref, *refs):
    (
        local_ref,
        back_ref,
        first_ref,
        last_ref,
        state_ref,
        cum_ref,
        in_ref,
        rate_ref,
        igate_ref,
        lru_ref,
        dist_ref,
        branch_ref,
        rim_ref,
        par_ref,
        gates_ref,
    ), others = by_rows(
        refs, rows, (False,) * 3 + (True,) * 3 + (False,) + (True,) * 3 + (False,) + (True,) * 2 + (False,) * 2
    )
    dbranch_ref, tail_ref, head_ref, dgates_ref = others[:4]
    both_ref, dconv_ref, sums_ref = others[-3:]
    _, length, width = local_ref.shape
    here = pl.program_id(0) + first_block
    block = pl.ds(pl.multiple_of(here * width, width), width)
    taps = [par_ref[k : k + 1, :] for k in range(4)]
    soft = par_ref[7:8, :]
    place = lax.broadcasted_iota(jnp.int32, (SUBLANES, width), 0)
    zeros = jnp.zeros((SUBLANES, width), jnp.float32)

    def gate_step(index, carry):
        sums, earlier = carry
        decay_sum, rate_sum, input_sum = sums
        base = pl.multiple_of(index * STEP, STEP)
        later = []
        for row in range(rows):
            before = earlier[row]
            entering = in_ref[row]
            leaving = leaving_ref[row, :, block]
            lru_both = lru_ref[row, pl.ds(base, STEP), :].astype(jnp.float32)
            drates, dinputs = ([], [])
            for half in range(STEP // SUBLANES):
                at = pl.ds(base + half * SUBLANES, SUBLANES)
                lru = lru_both[half * SUBLANES : (half + 1) * SUBLANES]
                start = across(dist_ref[row, at, :], width) == 0
                adjoint = local_ref[row, at, :] + back_ref[row, at, :] * leaving
                state = state_ref[row, at, :] + cum_ref[row, at, :] * entering
                previous = jnp.where(place < 1, before, pltpu.roll(state, 1, 0))
                before = state[SUBLANES - 1 :, :]
                rate = rate_ref[row, at, :]
                igate = igate_ref[row, at, :]
                log_decay = rate * soft
                decay = jnp.exp(log_decay)
                arg = root_argument(log_decay, decay)
                above = arg > ROOT_FLOOR
                arg = jnp.maximum(arg, ROOT_FLOOR)
                inverse = lax.rsqrt(arg)
                scale = jnp.where(start, 1.0, arg * inverse)
                gated = adjoint * igate
                dscale = gated * lru
                pull = jnp.where(above, dscale * decay * decay * inverse, 0.0)
                dlog = jnp.where(start, 0.0, adjoint * previous * decay - pull)
                dig = adjoint * scale * lru
                weighted = dlog * rate
                decay_sum = decay_sum + weighted
                drates.append(weighted * soft * (1.0 - rate))
                dinputs.append(dig * igate * (1.0 - igate))
                dconv_ref[row, at, :] = gated * scale
            drate = jnp.concatenate(drates, axis=0).astype(jnp.bfloat16)
            dinput = jnp.concatenate(dinputs, axis=0).astype(jnp.bfloat16)
            both_ref[row, pl.ds(base, STEP), :width] = drate
            both_ref[row, pl.ds(base, STEP), width:] = dinput
            drate = drate.astype(jnp.float32)
            dinput = dinput.astype(jnp.float32)
            rate_sum = rate_sum + (drate[:SUBLANES] + drate[SUBLANES:])
            input_sum = input_sum + (dinput[:SUBLANES] + dinput[SUBLANES:])
            later.append(before)
        return ((decay_sum, rate_sum, input_sum), tuple(later))

    sums, _ = lax.fori_loop(
        0,
        length // STEP,
        gate_step,
        ((zeros, zeros, zeros), tuple(in_ref[row] for row in range(rows))),
        unroll=2,
    )
    for slot, total in zip((5, 6, 7), (sums[1], sums[2], sums[0] * par_ref[8:9, :])):
        sums_ref[slot : slot + 1, :] = jnp.sum(total, axis=0, keepdims=True)

    piece = min(length, 256)
    wide = None
    for row in range(rows):

        def dot_step(index, carry, row=row):
            at = pl.ds(pl.multiple_of(index * piece, piece), piece)
            dconv_ref[row, at, :] += lax.dot_general(
                both_ref[row, at, :],
                gates_ref[...],
                (((1,), (1,)), ((), ())),
                preferred_element_type=jnp.float32,
            )
            return carry

        lax.fori_loop(0, length // piece, dot_step, 0)
        part = lax.dot_general(
            lru_ref[row], both_ref[row], (((0,), (0,)), ((), ())), preferred_element_type=jnp.float32
        )
        wide = part if wide is None else wide + part
    row_head = lax.broadcasted_iota(jnp.int32, (width, width), 0) // head_size
    col_head = lax.broadcasted_iota(jnp.int32, (width, width), 1) // head_size
    own = row_head == col_head
    folds = []
    for part in range(2):
        kept = jnp.where(own, wide[:, part * width : (part + 1) * width], 0.0)
        folded = kept
        for other in range(1, width // head_size):
            folded = folded + pltpu.roll(kept, width - other * head_size, 1)
        folds.append(folded[:, :LANES])

    def conv_step(index, carry):
        sums, following = carry
        sums = list(sums)
        base = pl.multiple_of((length // STEP - 1 - index) * STEP, STEP)
        later = []
        for row in range(rows):
            after = following[row]
            pieces = []
            for half in reversed(range(STEP // SUBLANES)):
                at = pl.ds(base + half * SUBLANES, SUBLANES)
                dist = across(dist_ref[row, at, :], width)
                branch = branch_ref[row, at, :]
                here = dconv_ref[row, at, :]
                total = taps[0] * here
                sums[0] = sums[0] + here * branch
                sums[4] = sums[4] + here
                masked = tuple(jnp.where(dist >= k, here, 0.0) for k in range(1, 4))
                for k in range(1, 4):
                    moved = pltpu.roll(
                        jnp.where(place >= k, masked[k - 1], after[k - 1]), SUBLANES - k, 0
                    )
                    total = total + taps[k] * moved
                    sums[k] = sums[k] + branch * moved
                after = masked
                pieces.append(total)
            whole = jnp.concatenate(pieces[::-1], axis=0)
            dbranch_ref[row, pl.ds(base, STEP), :] = whole.astype(jnp.bfloat16)
            later.append(after)

            @pl.when(index == 0)
            def _(row=row, whole=whole):
                tail_ref[row] = whole[STEP - SUBLANES :]

        return (tuple(sums), tuple(later))

    sums, firsts = lax.fori_loop(
        0,
        length // STEP,
        conv_step,
        ((zeros,) * 5, tuple((zeros,) * 3 for _ in range(rows))),
        unroll=2,
    )
    sums = list(sums)
    for row in range(rows):
        total = zeros
        rim = rim_ref[row]
        for k in range(1, 4):
            moved = pltpu.roll(jnp.where(place >= k, 0.0, firsts[row][k - 1]), SUBLANES - k, 0)
            total = total + taps[k] * moved
            sums[k] = sums[k] + rim * moved
        head_ref[row] = total
    for slot in range(5):
        sums_ref[slot : slot + 1, :] = jnp.sum(sums[slot], axis=0, keepdims=True)
    above = jnp.zeros((head_size, width), jnp.float32)
    below = jnp.zeros((LANES - head_size - SUBLANES, width), jnp.float32)
    turned = jnp.concatenate([above, sums_ref[...], below], axis=0).T
    lane = lax.broadcasted_iota(jnp.int32, (width, LANES), 1)
    dgates_ref[:, :LANES] = jnp.where(lane < head_size, folds[0], turned).astype(dgates_ref.dtype)
    dgates_ref[:, LANES:] = folds[1].astype(dgates_ref.dtype)


def channel_call(
    kernel, name, arrays, specs, outs, out_specs, scratch, blocks, flops, params=()
):
    moved = sum(math.prod(a.shape) * a.dtype.itemsize for a in (*arrays, *outs))
    return pl.pallas_call(
        kernel,
        name=name,
        grid=(blocks,),
        in_specs=specs,
        out_specs=out_specs,
        out_shape=outs,
        scratch_shapes=scratch,
        compiler_params=pltpu.CompilerParams(vmem_limit_bytes=VMEM_BYTES, **dict(params)),
        cost_estimate=pl.CostEstimate(flops=flops, bytes_accessed=moved, transcendentals=0),
    )(*arrays)


class Recurrence:
    def __init__(self, rows, length, channels, head_size):
        self.rows, self.length, self.channels = (rows, length, channels)
        self.head_size = head_size
        self.width = head_size * LANES // math.gcd(head_size, LANES)
        self.blocks = channels // self.width
        self.flops = 2 * rows * length * channels * 2 * self.width

    def tall(self):
        return pl.BlockSpec((self.rows, self.length, self.width), lambda j: (0, 0, j))

    def short(self, size):
        return pl.BlockSpec((self.rows, size, self.width), lambda j: (0, 0, j))

    def apart(self, size):
        return [pl.BlockSpec((1, size, self.width), lambda j: (0, 0, j))] * self.rows

    def whole(self, rows, size):
        return pl.BlockSpec((rows, size, self.channels), lambda j: (0, 0, 0))

    def flat(self, size):
        return pl.BlockSpec((size, self.width), lambda j: (0, j))

    def dist(self):
        return pl.BlockSpec((self.rows, self.length, LANES), lambda j: (0, 0, 0))

    def gates(self, columns):
        return pl.BlockSpec((self.width, columns), lambda j: (j, 0))

    def shape(self, size, dtype):
        return jax.ShapeDtypeStruct((self.rows, size, self.channels), dtype)

    def widen(self, lru_gates):
        size, width = (self.head_size, self.width)
        heads = width // size
        column = jnp.arange(2 * width)
        source = (column // width) * size + column % size
        spread = (jnp.arange(2 * size)[:, None] == source[None, :]).astype(jnp.bfloat16)
        owner = (column % width) // size
        mine = (jnp.arange(self.channels) // size) % heads
        wide = jnp.dot(lru_gates, spread, preferred_element_type=jnp.float32)
        return jnp.where(mine[:, None] == owner[None, :], wide, 0.0).astype(jnp.bfloat16)

    def adjoint(self, dres, weight, pre, state, cum, entering, rate, dist, params):
        f32 = jnp.float32
        outs = [self.shape(self.length, d) for d in (jnp.bfloat16, f32, f32)] + [self.shape(1, f32)]
        tall, apart = (self.tall(), self.apart(self.length))
        return channel_call(
            functools.partial(adjoint_kernel, self.rows),
            "recurrence_adjoint",
            (dres, weight, *pre, *state, *cum, entering, *rate, dist, params),
            [
                pl.BlockSpec(dres.shape, lambda j: (0, 0)),
                self.gates(weight.shape[1]),
                *apart * 3,
                self.short(1),
                *apart,
                self.dist(),
                self.flat(16),
            ],
            outs,
            [tall, tall, tall, self.short(1)],
            [pltpu.VMEM((self.rows, self.length, self.width), f32)],
            self.blocks,
            2 * self.rows * self.length * weight.size,
        )

    def backward(
        self, local, back, first, last, state, cum, entering, rate, igate, lru, dist, branch, rim, params, gates, between_calls
    ):
        f32 = jnp.float32
        outs = [
            self.shape(self.length, jnp.bfloat16),
            self.shape(SUBLANES, f32),
            self.shape(SUBLANES, f32),
            jax.ShapeDtypeStruct((self.channels, 2 * LANES), jnp.bfloat16),
        ]
        seqs = lax.axis_size("seq")
        summary = (self.rows, 2, self.channels)
        arrays = (local, back, first, *last, *state, *cum, entering, *rate, *igate, *lru, dist, *branch, *rim)
        arrays += (params, gates)
        early = self.blocks - 1
        scratch = [
            pltpu.VMEM((self.rows, self.length, 2 * self.width), jnp.bfloat16),
            pltpu.VMEM((self.rows, self.length, self.width), f32),
            pltpu.VMEM((SUBLANES, self.width), f32),
        ]

        def specs(offset):
            rows, width = (self.rows, self.width)

            def wide(rows, size):
                return pl.BlockSpec((rows, size, width), lambda j: (0, 0, j + offset))

            def flat(size):
                return pl.BlockSpec((size, width), lambda j: (0, j + offset))

            def tall(columns):
                return pl.BlockSpec((width, columns), lambda j: (j + offset, 0))

            whole, apart = (wide(rows, self.length), [wide(1, self.length)] * rows)
            given = [whole, whole, self.whole(rows, 1), *[self.whole(1, 2)] * rows, *apart * 2]
            given += [wide(rows, 1), *apart * 3, self.dist(), *apart, *[wide(1, SUBLANES)] * rows]
            given += [flat(16), tall(2 * width)]
            made = [whole, wide(rows, SUBLANES), wide(rows, SUBLANES), tall(2 * LANES)]
            return (given, made)

        given, made = specs(0)
        *found, leaving = channel_call(
            functools.partial(backward_kernel, self.head_size, self.rows),
            "recurrence_backward",
            arrays,
            given,
            outs + [self.shape(1, f32)],
            made + [self.whole(self.rows, 1)],
            scratch
            + [
                pltpu.VMEM(summary, f32),
                pltpu.VMEM((seqs,) + summary, f32),
                pltpu.SemaphoreType.DMA((seqs - 1,)),
                pltpu.SemaphoreType.DMA((seqs - 1,)),
            ],
            early,
            2 * self.flops,
            {"collective_id": 5, "has_side_effects": True},
        )
        between, leaving = between_calls(leaving)
        given, made = specs(early)
        done = pl.pallas_call(
            functools.partial(later_backward_kernel, self.head_size, self.rows, early),
            name="recurrence_backward_end",
            grid=(self.blocks - early,),
            in_specs=[self.whole(self.rows, 1)] + [pl.BlockSpec(memory_space=pl.ANY)] * 4 + given,
            out_specs=made,
            out_shape=outs,
            scratch_shapes=scratch,
            input_output_aliases={1 + k: k for k in range(4)},
            compiler_params=pltpu.CompilerParams(vmem_limit_bytes=VMEM_BYTES),
            cost_estimate=pl.CostEstimate(
                flops=self.flops // 2, bytes_accessed=16 * self.flops // self.width, transcendentals=0
            ),
        )(leaving, *found, *arrays)
        return (*done, between)


def gathered(parts_ref, at):
    return jnp.concatenate([parts_ref[k, at, :] for k in range(parts_ref.shape[0])], axis=1)


def front_kernel(
    parts_ref,
    gain_ref,
    input_ref,
    gate_ref,
    dist_ref,
    par_ref,
    gates_ref,
    x_ref,
    inverse_ref,
    normed_ref,
    branch_ref,
    pre_ref,
    rim_ref,
    lru_ref,
    rate_ref,
    igate_ref,
    state_ref,
    cum_ref,
    last_ref,
    landed_ref,
    both_ref,
    send_sem,
    recv_sem,
):
    tokens = x_ref.shape[0]
    piece, tall = (64, min(tokens, 512))
    step = pl.program_id(0)
    seq, seqs = (lax.axis_index("seq"), lax.axis_size("seq"))
    barrier = pltpu.get_barrier_semaphore()

    @pl.when(step == 0)
    def _():
        before = {"seq": lax.rem(seq + seqs - 1, seqs)}
        pl.semaphore_signal(barrier, inc=1, device_id=before, device_id_type=MESH)

        def norm(index, carry):
            at = pl.ds(pl.multiple_of(index * piece, piece), piece)
            low = gathered(parts_ref, at)
            x_ref[at, :] = low
            value = low.astype(jnp.float32)
            inverse = lax.rsqrt(jnp.mean(value * value, axis=1, keepdims=True) + EPS)
            inverse_ref[at, :] = jnp.broadcast_to(inverse, (piece, LANES))
            normed_ref[at, :] = (value * inverse * gain_ref[...]).astype(jnp.bfloat16)
            return carry

        lax.fori_loop(0, tokens // piece, norm, 0, unroll=2)

    rim_copy = pltpu.make_async_remote_copy(
        src_ref=normed_ref.at[tokens - STEP :],
        dst_ref=landed_ref,
        send_sem=send_sem,
        recv_sem=recv_sem,
        device_id={"seq": lax.rem(seq + 1, seqs)},
        device_id_type=MESH,
    )

    @pl.when(step == 0)
    def _():
        pl.semaphore_wait(barrier, 1)
        rim_copy.start()

    def multiply(index, carry):
        at = pl.ds(pl.multiple_of(index * tall, tall), tall)
        normed = normed_ref[at, :]
        branch_ref[0, at, :] = jnp.dot(normed, input_ref[...], preferred_element_type=jnp.float32)
        pre_ref[0, at, :] = jnp.dot(normed, gate_ref[...], preferred_element_type=jnp.float32)
        return carry

    lax.fori_loop(0, tokens // tall, multiply, 0)

    @pl.when(step == 0)
    def _():
        rim_copy.wait()

    before = jnp.dot(landed_ref[...], input_ref[...], preferred_element_type=jnp.float32)
    rim_ref[0] = jnp.where(seq > 0, 1.0, 0.0) * before[STEP - SUBLANES :]
    scan_block(
        branch_ref,
        rim_ref,
        dist_ref,
        par_ref,
        gates_ref,
        lru_ref,
        rate_ref,
        igate_ref,
        state_ref,
        cum_ref,
        last_ref,
        both_ref,
    )


def front(parts, gain, recur_input, recur_gate, dist, params, gates):
    count, tokens, width = parts.shape
    model, rec = recur_input.shape
    columns = gates.shape[1] // 2
    steps = rec // columns
    low, f32 = (jnp.bfloat16, jnp.float32)
    tall = pl.BlockSpec((model, columns), lambda j: (0, j))

    def whole(shape):
        return pl.BlockSpec(shape, lambda j: (0,) * len(shape))

    def wide(size, dtype):
        spec = pl.BlockSpec((1, size, columns), lambda j: (0, 0, j))
        return (spec, jax.ShapeDtypeStruct((1, size, rec), dtype))

    made = [wide(tokens, f32), wide(tokens, f32), wide(SUBLANES, f32), wide(tokens, low)]
    made += [wide(tokens, f32)] * 4 + [wide(2, f32)]
    return pl.pallas_call(
        front_kernel,
        name="project_and_scan",
        grid=(steps,),
        in_specs=[
            whole(parts.shape),
            whole((1, model)),
            tall,
            tall,
            whole(dist.shape),
            pl.BlockSpec((16, columns), lambda j: (0, j)),
            pl.BlockSpec((columns, 2 * columns), lambda j: (j, 0)),
        ],
        out_specs=[whole((tokens, model)), whole((tokens, LANES)), whole((tokens, model))]
        + [spec for spec, _ in made],
        out_shape=[
            jax.ShapeDtypeStruct((tokens, model), low),
            jax.ShapeDtypeStruct((tokens, LANES), f32),
            jax.ShapeDtypeStruct((tokens, model), low),
        ]
        + [shape for _, shape in made],
        scratch_shapes=[
            pltpu.VMEM((STEP, model), low),
            pltpu.VMEM((1, tokens, 2 * columns), f32),
            pltpu.SemaphoreType.DMA,
            pltpu.SemaphoreType.DMA,
        ],
        compiler_params=pltpu.CompilerParams(
            collective_id=3, has_side_effects=True, vmem_limit_bytes=VMEM_BYTES
        ),
        cost_estimate=pl.CostEstimate(
            flops=5 * tokens * model * rec, bytes_accessed=40 * tokens * model, transcendentals=0
        ),
    )(parts, gain[None], recur_input, recur_gate, dist, params, gates)


def middle_kernel(rows, *refs):
    (last_ref, state_hbm, cum_hbm, pre_hbm, x_ref, out_ref, gain_ref), others = by_rows(
        refs, rows, (True,) * 5 + (False,) * 2
    )
    entering_ref, mixed_ref, resid_ref, normed_ref = others[:4]
    sent_ref, got_ref, held_ref, send_sem, recv_sem, load_sem = others[4:]
    tall, model = resid_ref.shape
    step, steps = (pl.program_id(0), pl.num_programs(0))
    tiles = steps // rows
    slab = 16

    def on_row(place, act):
        for row in range(rows):

            @pl.when(lax.div(place, tiles) == row)
            def _(row=row):
                at = pl.ds(pl.multiple_of(lax.rem(place, tiles) * tall, tall), tall)
                slot = lax.rem(place, 2)
                for kind, source in enumerate((state_hbm, cum_hbm, pre_hbm)):
                    act(
                        pltpu.make_async_copy(
                            source.refs[row].at[0, at], held_ref.at[slot, kind], load_sem.at[slot, kind]
                        )
                    )

    @pl.when(step == 0)
    def _():
        on_row(step, lambda copy: copy.start())
        for row in range(rows):
            sent_ref[row] = last_ref[row]
        carried(sent_ref, got_ref, entering_ref, send_sem, recv_sem, False)

    @pl.when(step + 1 < steps)
    def _():
        on_row(step + 1, lambda copy: copy.start())

    on_row(step, lambda copy: copy.wait())
    slot = lax.rem(step, 2)
    mine = lax.div(step, tiles)

    def mix(index, carry):
        at = pl.ds(pl.multiple_of(index * slab, slab), slab)
        state = held_ref[slot, 0, at, :] + held_ref[slot, 1, at, :] * entering_ref[mine]
        pre = held_ref[slot, 2, at, :]
        inner = jnp.tanh(pre * (GELU_C + (GELU_C * GELU_A) * (pre * pre)))
        mixed_ref[at, :] = (state * (pre * (0.5 + 0.5 * inner))).astype(jnp.bfloat16)
        return carry

    lax.fori_loop(0, tall // slab, mix, 0, unroll=2)
    for row in range(rows):

        @pl.when(mine == row)
        def _(row=row):
            tile = 512
            for first in range(0, model, tile):
                at = slice(first, first + tile)
                resid_ref[:, at] = x_ref.refs[row][:, at].astype(jnp.float32) + jnp.dot(
                    mixed_ref[...], out_ref[:, at], preferred_element_type=jnp.float32
                )

    def norm(index, carry):
        at = pl.ds(pl.multiple_of(index * slab, slab), slab)
        resid = resid_ref[at, :]
        inverse = lax.rsqrt(jnp.mean(resid * resid, axis=1, keepdims=True) + EPS)
        normed_ref[at, :] = (resid * inverse * gain_ref[...]).astype(jnp.bfloat16)
        return carry

    lax.fori_loop(0, tall // slab, norm, 0, unroll=4)


def middle(last, state, cum, pre, x, recur_out, gain):
    rows = len(state)
    _, length, rec = state[0].shape
    model = recur_out.shape[1]
    tall = min(length, 256)
    tiles = length // tall
    tokens = rows * length
    seqs = lax.axis_size("seq")
    low, f32 = (jnp.bfloat16, jnp.float32)

    def whole(shape):
        return pl.BlockSpec(shape, lambda s: (0,) * len(shape), pipeline_mode=pl.Buffered(1))

    def flat(row):
        return lambda s: (jnp.clip(s - row * tiles, 0, tiles - 1), 0)

    summary = (rows, 2, rec)
    return pl.pallas_call(
        functools.partial(middle_kernel, rows),
        name="mix_and_norm",
        grid=(rows * tiles,),
        in_specs=[whole((1, 2, rec))] * rows
        + [pl.BlockSpec(memory_space=pl.ANY)] * (3 * rows)
        + [pl.BlockSpec((tall, model), flat(row)) for row in range(rows)]
        + [whole(recur_out.shape), whole((1, model))],
        out_specs=[
            pl.BlockSpec((rows, 1, rec), lambda s: (0, 0, 0)),
            pl.BlockSpec((tall, rec), lambda s: (s, 0)),
            pl.BlockSpec((tall, model), lambda s: (s, 0)),
            pl.BlockSpec((tall, model), lambda s: (s, 0)),
        ],
        out_shape=[
            jax.ShapeDtypeStruct((rows, 1, rec), f32),
            jax.ShapeDtypeStruct((tokens, rec), low),
            jax.ShapeDtypeStruct((tokens, model), f32),
            jax.ShapeDtypeStruct((tokens, model), low),
        ],
        scratch_shapes=[
            pltpu.VMEM(summary, f32),
            pltpu.VMEM((seqs,) + summary, f32),
            pltpu.VMEM((2, 3, tall, rec), f32),
            pltpu.SemaphoreType.DMA((seqs - 1,)),
            pltpu.SemaphoreType.DMA((seqs - 1,)),
            pltpu.SemaphoreType.DMA((2, 3)),
        ],
        compiler_params=pltpu.CompilerParams(
            collective_id=4, has_side_effects=True, vmem_limit_bytes=VMEM_BYTES
        ),
        cost_estimate=pl.CostEstimate(
            flops=2 * tokens * rec * model, bytes_accessed=14 * tokens * rec, transcendentals=0
        ),
    )(*last, *state, *cum, *pre, *x, recur_out, gain[None])


def hidden_kernel(
    left_ref,
    parts_ref,
    normed_ref,
    gate_ref,
    up_ref,
    down_ref,
    gout_ref,
    hidden_ref,
    dgate_ref,
    dup_ref,
):
    tokens, model = normed_ref.shape
    chunk = down_ref.shape[0]
    rows = left_ref.shape[0]
    length = tokens // rows
    slab = 32

    @pl.when(pl.program_id(0) == 0)
    def _():
        for row in range(rows):

            def collect(index, carry, row=row):
                base = pl.multiple_of(index * slab, slab)
                at = pl.ds(row * length + base, slab)
                low = gathered(parts_ref, at)
                place = base + lax.broadcasted_iota(jnp.int32, low.shape, 0)
                value = jnp.where(place < left_ref[row], low.astype(jnp.float32), 0.0)
                gout_ref[at, :] = value.astype(jnp.bfloat16)
                return carry

            lax.fori_loop(0, length // slab, collect, 0)

    tall = min(tokens, 512)
    wide = 256

    def tile(index, carry):
        at = pl.ds(pl.multiple_of(index * tall, tall), tall)
        for column in range(chunk // wide):
            own = slice(column * wide, (column + 1) * wide)
            gate = jnp.dot(normed_ref[at, :], gate_ref[:, own], preferred_element_type=jnp.float32)
            up = jnp.dot(normed_ref[at, :], up_ref[:, own], preferred_element_type=jnp.float32)
            dhid = lax.dot_general(
                gout_ref[at, :],
                down_ref[own, :],
                (((1,), (1,)), ((), ())),
                preferred_element_type=jnp.float32,
            )
            act, slope = gelu_pair(gate)
            hidden_ref[at, own] = (act * up).astype(jnp.bfloat16)
            dgate_ref[at, own] = (dhid * up * slope).astype(jnp.bfloat16)
            dup_ref[at, own] = (dhid * act).astype(jnp.bfloat16)
        return carry

    lax.fori_loop(0, tokens // tall, tile, 0, unroll=True)


def back_kernel(
    hidden_ref,
    dgate_ref,
    dup_ref,
    gout_hbm,
    resid_hbm,
    gain_ref,
    gate_ref,
    up_ref,
    down_ref,
    result_ref,
    dres_ref,
    total_ref,
    back_ref,
    gout_ref,
    resid_ref,
    load_sem,
):
    tall, model = (hidden_ref.shape[0], gout_ref.shape[1])
    step, tile = (pl.program_id(0), pl.program_id(1))
    wide = 512
    contract = (((1,), (1,)), ((), ()))
    rows = pl.ds(pl.multiple_of(tile * tall, tall), tall)

    def loads():
        return (
            pltpu.make_async_copy(gout_hbm, gout_ref, load_sem.at[0]),
            pltpu.make_async_copy(resid_hbm, resid_ref, load_sem.at[1]),
        )

    @pl.when((step == 0) & (tile == 0))
    def _():
        for load in loads():
            load.start()

    def products(own):
        forth = jnp.dot(hidden_ref[...], down_ref[:, own], preferred_element_type=jnp.float32)
        back = lax.dot_general(
            dgate_ref[...], gate_ref[own, :], contract, preferred_element_type=jnp.float32
        ) + lax.dot_general(
            dup_ref[...], up_ref[own, :], contract, preferred_element_type=jnp.float32
        )
        return (forth, back)

    @pl.when(step == 0)
    def _():
        for first in range(0, model, wide):
            own = slice(first, first + wide)
            forth, back = products(own)
            total_ref[rows, own] = forth
            back_ref[rows, own] = back

    @pl.when(step > 0)
    def _():
        for first in range(0, model, wide):
            own = slice(first, first + wide)
            forth, back = products(own)
            total_ref[rows, own] += forth
            back_ref[rows, own] += back

    @pl.when((step == pl.num_programs(0) - 1) & (tile == 0))
    def _():
        for load in loads():
            load.wait()

    @pl.when(step == pl.num_programs(0) - 1)
    def _():
        parts, width = (result_ref.shape[0], result_ref.shape[2])
        small = 16

        def finish(index, carry):
            at = pl.ds(pl.multiple_of(tile * tall + index * small, small), small)
            resid = resid_ref[at, :]
            result = (resid + total_ref[at, :]).astype(jnp.bfloat16)
            for part in range(parts):
                result_ref[part, at, :] = result[:, part * width : (part + 1) * width]
            inverse = lax.rsqrt(jnp.mean(resid * resid, axis=1, keepdims=True) + EPS)
            normed = resid * inverse
            scaled = back_ref[at, :] * gain_ref[...]
            mean = jnp.mean(scaled * normed, axis=1, keepdims=True)
            dres = gout_ref[at, :].astype(jnp.float32) + inverse * (scaled - normed * mean)
            dres_ref[at, :] = dres.astype(jnp.bfloat16)
            return carry

        lax.fori_loop(0, tall // small, finish, 0, unroll=4)


MLP_CHUNK = 768


def resident(shape):
    return pl.BlockSpec(shape, lambda s: (0,) * len(shape), pipeline_mode=pl.Buffered(1))


def mlp_specs(tokens, model):
    columns = pl.BlockSpec((model, MLP_CHUNK), lambda s: (0, s))
    down = pl.BlockSpec((MLP_CHUNK, model), lambda s: (s, 0))
    made = pl.BlockSpec((tokens, MLP_CHUNK), lambda s: (0, s))
    return ([columns, columns, down], [made] * 3)


def mlp_hidden(left, parts, normed, mlp_gate, mlp_up, mlp_down):
    tokens, model = normed.shape
    ffn = mlp_gate.shape[1]
    low = jnp.bfloat16
    weights, made = mlp_specs(tokens, model)
    tall = jax.ShapeDtypeStruct((tokens, ffn), low)
    return pl.pallas_call(
        hidden_kernel,
        name="mlp_hidden",
        grid=(ffn // MLP_CHUNK,),
        in_specs=[
            pl.BlockSpec(memory_space=pltpu.SMEM),
            resident(parts.shape),
            resident(normed.shape),
            *weights,
        ],
        out_specs=[resident((tokens, model)), *made],
        out_shape=[jax.ShapeDtypeStruct((tokens, model), low), tall, tall, tall],
        compiler_params=pltpu.CompilerParams(vmem_limit_bytes=VMEM_BYTES),
        cost_estimate=pl.CostEstimate(
            flops=6 * tokens * model * ffn,
            bytes_accessed=6 * (model + tokens) * ffn + 6 * tokens * model,
            transcendentals=0,
        ),
    )(left, parts, normed, mlp_gate, mlp_up, mlp_down)


def mlp_back(hidden, dgate, dup, gout, resid, gain, mlp_gate, mlp_up, mlp_down, parts_shape):
    tokens, model = resid.shape
    ffn = mlp_gate.shape[1]
    low, f32 = (jnp.bfloat16, jnp.float32)
    chunk, tall = (1024, min(tokens, 512))

    def resident(shape):
        return pl.BlockSpec(shape, lambda s, t: (0,) * len(shape), pipeline_mode=pl.Buffered(1))

    columns = pl.BlockSpec((model, chunk), lambda s, t: (0, s))
    down = pl.BlockSpec((chunk, model), lambda s, t: (s, 0))
    made = pl.BlockSpec((tall, chunk), lambda s, t: (t, s))
    return pl.pallas_call(
        back_kernel,
        name="mlp_back",
        grid=(ffn // chunk, tokens // tall),
        in_specs=[
            made,
            made,
            made,
            pl.BlockSpec(memory_space=pl.ANY),
            pl.BlockSpec(memory_space=pl.ANY),
            resident((1, model)),
            columns,
            columns,
            down,
        ],
        out_specs=[resident(parts_shape), resident((tokens, model))],
        out_shape=[
            jax.ShapeDtypeStruct(parts_shape, low),
            jax.ShapeDtypeStruct((tokens, model), low),
        ],
        scratch_shapes=[
            pltpu.VMEM((tokens, model), f32),
            pltpu.VMEM((tokens, model), f32),
            pltpu.VMEM((tokens, model), low),
            pltpu.VMEM((tokens, model), f32),
            pltpu.SemaphoreType.DMA((2,)),
        ],
        compiler_params=pltpu.CompilerParams(vmem_limit_bytes=VMEM_BYTES),
        cost_estimate=pl.CostEstimate(
            flops=6 * tokens * model * ffn,
            bytes_accessed=6 * (model + tokens) * ffn + 10 * tokens * model,
            transcendentals=0,
        ),
    )(hidden, dgate, dup, gout, resid, gain[None], mlp_gate, mlp_up, mlp_down)


def outputs_kernel(
    device_ref,
    own_ref,
    gate_sum,
    in_sum,
    out_sum,
    small_ref,
    input_ref,
    gate_ref,
    mlp_gate_ref,
    mlp_up_ref,
    gain1_ref,
    gain2_ref,
    sum_gain1,
    sum_in,
    sum_gate,
    sum_taps,
    sum_bias,
    sum_lgates,
    sum_lbias,
    sum_decay,
    sum_out,
    sum_gain2,
    sum_mgate,
    sum_mup,
    sum_down,
):
    rows = sum_mgate.shape[0]
    model = own_ref.shape[1]
    parts = sum_mgate.shape[1] // model
    for part in range(parts):
        at = slice(part * model, (part + 1) * model)
        sum_mgate[:, at] = own_ref[part * rows : (part + 1) * rows, :].astype(jnp.float32)
        sum_mup[:, at] = own_ref[(parts + part) * rows : (parts + part + 1) * rows, :].astype(
            jnp.float32
        )
    sum_down[...] = own_ref[2 * parts * rows :, :].astype(jnp.float32)

    def weighed(*pairs):
        return sum(
            jnp.sum(weight[...].astype(jnp.float32) * gradient[...], axis=1, keepdims=True)
            for weight, gradient in pairs
        )

    def as_row(column, gain):
        lane = lax.broadcasted_iota(jnp.int32, (rows, LANES), 1)
        place = lax.broadcasted_iota(jnp.int32, (rows, LANES), 0)
        whole = lax.broadcasted_iota(jnp.int32, (rows, model), 1)
        own = device_ref[0] * rows + lax.broadcasted_iota(jnp.int32, (rows, model), 0)
        own_gain = jnp.sum(jnp.where(whole == own, gain[...], 0.0), axis=1, keepdims=True)
        return jnp.sum(jnp.where(lane == place, column / own_gain, 0.0), axis=0, keepdims=True)

    row1 = as_row(weighed((input_ref, in_sum), (gate_ref, gate_sum)), gain1_ref)
    row2 = as_row(weighed((mlp_gate_ref, sum_mgate), (mlp_up_ref, sum_mup)), gain2_ref)
    sum_gain1[...] = row1[:, :rows]
    sum_gain2[...] = row2[:, :rows]
    sum_in[...] = in_sum[...]
    sum_gate[...] = gate_sum[...]
    sum_out[...] = out_sum[...]
    channels = small_ref.shape[0]
    size = sum_lgates.shape[1] // 2
    first, second = (small_ref[:, :LANES], small_ref[:, LANES:])
    lane = lax.broadcasted_iota(jnp.int32, (channels, LANES), 1)
    moved = pltpu.roll(second, size, 1)
    sum_lgates[:, :LANES] = jnp.where(lane < size, first, moved)
    sum_lgates[:, LANES:] = moved[:, : 2 * size - LANES]
    filled = jnp.concatenate([first, jnp.zeros((LANES - channels, LANES), jnp.float32)], axis=0)
    turned = filled.T
    sum_taps[...] = turned[size : size + 4, :channels]
    sum_bias[...] = turned[size + 4 : size + 5, :channels]
    sum_lbias[...] = turned[size + 5 : size + 7, :channels]
    sum_decay[...] = turned[size + 7 : size + 8, :channels]


def outputs(
    device, own, gate_sum, in_sum, out_sum, small, recur_input, recur_gate, mlp_gate, mlp_up, gain1, gain2, size
):
    rows, rec = in_sum.shape
    model, ffn = mlp_gate.shape
    channels = small.shape[0]
    f32 = jnp.float32

    def whole(shape):
        return pl.BlockSpec(shape, lambda s, device: (0,) * len(shape))

    def mine(shape):
        return pl.BlockSpec(shape, lambda s, device: (device[0], 0))

    given = (own, gate_sum, in_sum, out_sum, small)
    shapes = [(1, rows), (rows, rec), (rows, rec), (4, channels), (1, channels)]
    shapes += [(channels, 2 * size), (2, channels), (1, channels), out_sum.shape, (1, rows)]
    shapes += [(rows, ffn), (rows, ffn), (own.shape[0] - 2 * ffn // model * rows, model)]
    return pl.pallas_call(
        outputs_kernel,
        name="outputs",
        grid_spec=pltpu.PrefetchScalarGridSpec(
            num_scalar_prefetch=1,
            grid=(1,),
            in_specs=[whole(a.shape) for a in given]
            + [mine((rows, rec))] * 2
            + [mine((rows, ffn))] * 2
            + [whole((1, model))] * 2,
            out_specs=[whole(shape) for shape in shapes],
        ),
        out_shape=[jax.ShapeDtypeStruct(shape, f32) for shape in shapes],
        compiler_params=pltpu.CompilerParams(vmem_limit_bytes=VMEM_BYTES),
    )(
        device[None],
        *given,
        recur_input,
        recur_gate,
        mlp_gate,
        mlp_up,
        gain1[None],
        gain2[None],
    )


def spread_kernel(whole_ref, out_ref):
    out_ref[0] = whole_ref[...]


def spread(whole, count):
    tokens, width = (whole.shape[0], whole.shape[1] // count)
    return pl.pallas_call(
        spread_kernel,
        name="spread_features",
        grid=(count,),
        in_specs=[pl.BlockSpec((tokens, width), lambda j: (0, j))],
        out_specs=pl.BlockSpec((1, tokens, width), lambda j: (j, 0, 0)),
        out_shape=jax.ShapeDtypeStruct((count, tokens, width), whole.dtype),
        cost_estimate=pl.CostEstimate(
            flops=0, bytes_accessed=4 * tokens * whole.shape[1], transcendentals=0
        ),
    )(whole)


CHAN = ("zed", "core")


def features_in(local, pick=slice(None)):
    count = lax.axis_size(CHAN)
    rows, length, width = local.shape
    local = local.reshape(count, rows // count, length, width)[:, pick]
    if width % LANES == 0:
        return lax.all_to_all(local, CHAN, 0, 0, tiled=True).reshape(count, -1, width)
    moved = lax.all_to_all(
        local.reshape(-1, length, width), CHAN, split_axis=0, concat_axis=2, tiled=True
    )
    return moved.reshape(1, -1, count * width)


def features_apart(whole):
    count = lax.axis_size(CHAN)
    if (whole.shape[1] // count) % LANES == 0:
        return spread(whole, count)
    return whole[None]


def features_out(parts, rows):
    blocks, tokens, width = parts.shape
    parts = parts.reshape(blocks, rows, tokens // rows, width)
    if blocks > 1:
        moved = lax.all_to_all(parts, CHAN, 0, 0, tiled=True)
        return moved.reshape(-1, *parts.shape[2:])
    return lax.all_to_all(parts[0], CHAN, split_axis=2, concat_axis=0, tiled=True)


class Corners:
    def __init__(self, seq, zed):
        self.seq_bits, self.zed_bits = (seq.bit_length() - 1, zed.bit_length() - 1)
        self.count = self.seq_bits + self.zed_bits
        self.dims = (2,) * self.count
        self.low = tuple(range(self.seq_bits))[::-1] + tuple(range(self.seq_bits, self.count))[::-1]
        self.high = tuple(range(self.seq_bits)) + tuple(range(self.seq_bits, self.count))[::-1]

    def place(self, dim):
        if dim < self.seq_bits:
            return ("seq", 2 ** (self.seq_bits - 1 - dim))
        return ("zed", 2 ** (self.count - 1 - dim))

    def bit(self, dim):
        axis, weight = self.place(dim)
        return lax.rem(lax.div(lax.axis_index(axis), weight), 2)

    def partner(self, dim):
        axis, weight = self.place(dim)
        return {axis: lax.axis_index(axis) + weight * (1 - 2 * self.bit(dim))}


def tail_kernel(
    corners,
    orders,
    dgate_hbm,
    dbranch_hbm,
    ending_ref,
    leading_ref,
    mixed_hbm,
    dres_hbm,
    gain_ref,
    input_hbm,
    gate_hbm,
    small_hbm,
    *refs,
):
    rows = ending_ref.shape[0]
    normed_hbms, x_hbms, inverse_hbms = (refs[k * rows : (k + 1) * rows] for k in range(3))
    tokens_ref, sum_gate, sum_out, sum_in, sum_small = refs[3 * rows : 3 * rows + 5]
    refs = refs[3 * rows + 5 :]
    stages = corners.count + 1
    dgate, dbranch, mixed, dres, normed, x, inverse, weight_in, weight_gate = refs[:9]
    made_in, made_out, own_small, back, parts, rim = refs[9:15]
    slots_in, slots_out, slots_small = (
        refs[15 + k * stages : 15 + (k + 1) * stages] for k in range(3)
    )
    (
        send_sem,
        recv_sem,
        load_sem,
        move_send,
        move_recv,
        keep_sem,
        rim_send,
        rim_recv,
    ) = refs[15 + 3 * stages :]
    seq, zed, core = (lax.axis_index(axis) for axis in ("seq", "zed", "core"))
    seqs, group = (lax.axis_size("seq"), 2 * lax.axis_size("zed"))
    mine = zed * 2 + core
    length = tokens_ref.shape[1]
    model = x.shape[1]

    def member(index):
        return {"zed": lax.div(index, 2), "core": lax.rem(index, 2)}

    def by_row(sources, target):
        return [
            (source, target.at[pl.ds(row * length, length)]) for row, source in enumerate(sources)
        ]

    pairs = [
        (dbranch_hbm, dbranch),
        (input_hbm, weight_in),
        (dgate_hbm, dgate),
        (gate_hbm, weight_gate),
        *by_row(x_hbms, x),
        *by_row(inverse_hbms, inverse),
        (dres_hbm, dres),
        *by_row(normed_hbms, normed),
        (mixed_hbm, mixed),
        (small_hbm.at[(slice(None),) * corners.count + (core,)], own_small),
    ]
    kinds = []
    for name in ('dbranch', 'win', 'dgate', 'wgate', 'x', 'inverse', 'dres', 'normed', 'mixed', 'small'):
        kinds += [name] * (rows if name in ("normed", "x", "inverse") else 1)
    loads = [
        pltpu.make_async_copy(source, target, load_sem.at[place])
        for place, (source, target) in enumerate(pairs)
    ]
    for load in loads:
        load.start()

    barrier = pltpu.get_barrier_semaphore()
    for other in range(1, group):
        pl.semaphore_signal(
            barrier, inc=1, device_id=member(lax.rem(mine + other, group)), device_id_type=MESH
        )
    for other in range(1, seqs):
        pl.semaphore_signal(
            barrier, inc=1, device_id={"seq": lax.rem(seq + other, seqs)}, device_id_type=MESH
        )
    pl.semaphore_wait(barrier, group - 1 + seqs - 1)

    rim_copy = pltpu.make_async_remote_copy(
        src_ref=leading_ref,
        dst_ref=rim,
        send_sem=rim_send,
        recv_sem=rim_recv,
        device_id={"seq": lax.rem(seq + seqs - 1, seqs)},
        device_id_type=MESH,
    )
    rim_copy.start()

    def own(stream, index):
        if stream < 4:
            return made_in.at[(stream,) + index + (core,)]
        if stream < 6:
            return made_out.at[(stream - 4,) + index + (core,)]
        return own_small.at[index]

    def slot(stream, stage):
        if stream < 4:
            return slots_in[stage].at[stream]
        if stream < 6:
            return slots_out[stage].at[stream - 4]
        return slots_small[stage]

    def copy(stream, stage):
        order = orders[stream]
        every = (slice(None),) * corners.count
        if stage == 0:
            if stream < 4:
                source = made_in.at[(stream,) + every + (1 - core,)]
            elif stream < 6:
                source = made_out.at[(stream - 4,) + every + (1 - core,)]
            else:
                source = small_hbm.at[every + (1 - core,)]
            target = {"core": 1 - core}
        else:
            dim = order[stage - 1]
            fixed = {before: corners.bit(before) for before in order[: stage - 1]}
            fixed[dim] = 1 - corners.bit(dim)
            source = own(stream, tuple(fixed.get(d, slice(None)) for d in range(corners.count)))
            target = corners.partner(dim)
        return pltpu.make_async_remote_copy(
            src_ref=source,
            dst_ref=slot(stream, stage),
            send_sem=send_sem.at[stream, stage],
            recv_sem=recv_sem.at[stream, stage],
            device_id=target,
            device_id_type=MESH,
        )

    sums = [
        sum_gate.at[:, : sum_gate.shape[1] // 2],
        sum_gate.at[:, sum_gate.shape[1] // 2 :],
        sum_in.at[:, : sum_in.shape[1] // 2],
        sum_in.at[:, sum_in.shape[1] // 2 :],
        sum_out.at[:, : sum_out.shape[1] // 2],
        sum_out.at[:, sum_out.shape[1] // 2 :],
        sum_small,
    ]

    def advance(stream, stage):
        order = orders[stream]
        copy(stream, stage).wait_recv()
        left = [dim for dim in range(corners.count) if dim not in order[:stage]]
        fixed = {dim: corners.bit(dim) for dim in order[:stage]}
        arrived = slot(stream, stage)
        if not left:
            index = tuple(fixed[dim] for dim in range(corners.count))
            sums[stream][...] = own(stream, index)[...].astype(jnp.float32) + arrived[...].astype(
                jnp.float32
            )
            return

        def add(index, carry):
            part = {
                dim: lax.rem(lax.div(index, 2 ** (len(left) - 1 - place)), 2)
                for place, dim in enumerate(left)
            }
            kept = own(stream, tuple({**fixed, **part}[dim] for dim in range(corners.count)))
            total = kept[...].astype(jnp.float32) + arrived[
                tuple(part[dim] for dim in left)
            ].astype(jnp.float32)
            kept[...] = total.astype(jnp.bfloat16)
            return carry

        lax.fori_loop(0, 2 ** len(left), add, 0)
        copy(stream, stage + 1).start()

    def move(other, row):
        to = lax.rem(mine + other, group)
        return pltpu.make_async_remote_copy(
            src_ref=parts.at[to, pl.ds(row * length, length)],
            dst_ref=tokens_ref.at[mine * rows + row],
            send_sem=move_send.at[other - 1, row],
            recv_sem=move_recv.at[other - 1, row],
            device_id=member(to),
            device_id_type=MESH,
        )

    def keep(row):
        return pltpu.make_async_copy(
            parts.at[mine, pl.ds(row * length, length)],
            tokens_ref.at[mine * rows + row],
            keep_sem.at[row],
        )

    tile = 256
    width = parts.shape[2]

    def back_row(row):
        tile = 512
        at_row = slice(row * length, (row + 1) * length)

        def product(index, carry):
            at = pl.ds(pl.multiple_of(index * tile, tile), tile)
            contract = (((1,), (1,)), ((), ()))
            back[:, at] = lax.dot_general(
                dbranch[at_row, :], weight_in[at, :], contract, preferred_element_type=jnp.float32
            ) + lax.dot_general(
                dgate[at_row, :], weight_gate[at, :], contract, preferred_element_type=jnp.float32
            )
            return carry

        lax.fori_loop(0, model // tile, product, 0, unroll=True)
        slab = 16

        def norm(index, carry):
            base = pl.multiple_of(index * slab, slab)
            at = pl.ds(row * length + base, slab)
            inv = inverse[at, :1]
            value = x[at, :].astype(jnp.float32) * inv
            scaled = back[pl.ds(base, slab), :] * gain_ref[...]
            mean = jnp.mean(scaled * value, axis=1, keepdims=True)
            grad = dres[at, :].astype(jnp.float32) + inv * (scaled - value * mean)
            grad = grad.astype(jnp.bfloat16)
            for part in range(parts.shape[0]):
                parts[part, at, :] = grad[:, part * width : (part + 1) * width]
            return carry

        lax.fori_loop(0, length // slab, norm, 0, unroll=4)
        for other in range(1, group):
            move(other, row).start()
        keep(row).start()

    def weight_product(left, right, made, stream, first):
        columns = made.shape[-1]
        shape = made.shape[1:-1]

        tile = columns

        def product(index, carry):
            at = pl.ds(pl.multiple_of(index * tile, tile), tile)
            source = pl.ds(pl.multiple_of(first + index * tile, tile), tile)
            part = lax.dot_general(
                left[...],
                right[:, source],
                (((0,), (0,)), ((), ())),
                preferred_element_type=jnp.float32,
            )
            made[(stream,) + (slice(None),) * len(shape) + (at,)] = part.astype(
                jnp.bfloat16
            ).reshape(shape + (tile,))
            return carry

        lax.fori_loop(0, columns // tile, product, 0)

    half, half_out = (made_in.shape[-1], made_out.shape[-1])
    waited, reached = (set(), {})

    def need(*names):
        for place, name in enumerate(kinds):
            if name in names and place not in waited:
                waited.add(place)
                loads[place].wait()

    def fix_rim():
        need("dbranch")
        rim_copy.wait()
        live = jnp.where(seq < seqs - 1, 1.0, 0.0)
        for row in range(rows):
            at = slice((row + 1) * length - STEP, (row + 1) * length)
            inside = dbranch[at, :].astype(jnp.float32)
            last = ending_ref[row] + live * rim[row]
            dbranch[at, :] = jnp.concatenate([inside[: STEP - SUBLANES], last], axis=0).astype(
                jnp.bfloat16
            )

    def begin(stream):
        copy(stream, 0).start()
        reached[stream] = 0

    def progress(streams):
        for stream in streams:
            if stream in reached and reached[stream] < stages:
                if stream == 6:
                    need("small")
                advance(stream, reached[stream])
                reached[stream] += 1

    def compute(item):
        if item == "gate":
            need("normed", "dgate")
            for stream in (0, 1):
                weight_product(normed, dgate, made_in, stream, stream * half)
                begin(stream)
        elif item == "out":
            need("mixed", "dres")
            for stream in (4, 5):
                weight_product(mixed, dres, made_out, stream - 4, (stream - 4) * half_out)
                begin(stream)
        elif item == "in":
            need("normed", "dbranch")
            for stream in (2, 3):
                weight_product(normed, dbranch, made_in, stream, (stream - 2) * half)
                begin(stream)
        else:
            need("dbranch", "dgate", "win", "wgate", "x", "inverse", "dres")
            back_row(item)

    begin(6)
    fix_rim()
    compute(0)
    compute(1)
    compute('gate')
    progress((6,))
    compute('out')
    progress((0, 1))
    compute('in')
    progress((0, 1))
    progress((4, 5))
    progress((6,))
    while any(reached[stream] < stages for stream in range(7)):
        progress((0, 1, 4, 5, 2, 3, 6))
    for stage in range(stages):
        for stream in range(7):
            copy(stream, stage).wait_send()
    for row in range(rows):
        for other in range(1, group):
            move(other, row).wait()
        keep(row).wait()


def tail(dgate, dbranch, ending, leading, mixed, dres, gain, w_in, w_gate, small, normed, x, inverse):
    corners = Corners(lax.axis_size("seq"), lax.axis_size("zed"))
    group, devices = (lax.axis_size(CHAN), 2 ** (corners.count + 1))
    tokens, model = dres.shape
    rec = dgate.shape[1]
    rows = ending.shape[0]
    length, width = (tokens // rows, model // group)
    low, f32 = (jnp.bfloat16, jnp.float32)
    stages = corners.count + 1
    in_rows, out_rows = (model // devices, rec // devices)
    small = small.reshape(corners.dims + (2, out_rows, small.shape[1]))
    orders = [corners.low, corners.high] * 3 + [corners.low]

    def slots(lead, shape):
        return [pltpu.VMEM(lead + (2,) * (corners.count - k) + shape, low) for k in range(stages)]

    in_shape, out_shape = ((in_rows, rec // 2), (out_rows, model // 2))
    loaded = (dgate, dbranch, mixed, dres, dres, dres)
    loaded += (jax.ShapeDtypeStruct((tokens, LANES), f32), w_in, w_gate)
    anyplace = pl.BlockSpec(memory_space=pl.ANY)
    vmem = pl.BlockSpec(memory_space=pltpu.VMEM)
    dma = pltpu.SemaphoreType.DMA
    moved = sum(math.prod(a.shape) * a.dtype.itemsize for a in loaded)
    return pl.pallas_call(
        functools.partial(tail_kernel, corners, orders),
        name="tail",
        in_specs=[anyplace, anyplace, vmem, vmem, anyplace, anyplace, vmem]
        + [anyplace] * (3 + 3 * rows),
        out_specs=[anyplace] + [vmem] * 4,
        out_shape=[
            jax.ShapeDtypeStruct((group * rows, length, width), low),
            jax.ShapeDtypeStruct((in_rows, rec), f32),
            jax.ShapeDtypeStruct((out_rows, model), f32),
            jax.ShapeDtypeStruct((in_rows, rec), f32),
            jax.ShapeDtypeStruct(small.shape[-2:], f32),
        ],
        scratch_shapes=[pltpu.VMEM(a.shape, a.dtype) for a in loaded]
        + [
            pltpu.VMEM((4,) + corners.dims + (2,) + in_shape, low),
            pltpu.VMEM((2,) + corners.dims + (2,) + out_shape, low),
            pltpu.VMEM(corners.dims + small.shape[-2:], low),
            pltpu.VMEM((length, model), f32),
            pltpu.VMEM((group, tokens, width), low),
            pltpu.VMEM(leading.shape, leading.dtype),
        ]
        + slots((4,), in_shape)
        + slots((2,), out_shape)
        + slots((), small.shape[-2:])
        + [
            dma((7, stages)),
            dma((7, stages)),
            dma((7 + 3 * rows,)),
            dma((group - 1, rows)),
            dma((group - 1, rows)),
            dma((rows,)),
            dma,
            dma,
        ],
        compiler_params=pltpu.CompilerParams(
            collective_id=1, has_side_effects=True, vmem_limit_bytes=60 * 1024 * 1024
        ),
        cost_estimate=pl.CostEstimate(
            flops=10 * tokens * model * rec, bytes_accessed=2 * moved, transcendentals=0
        ),
    )(dgate, dbranch, ending, leading, mixed, dres, gain[None], w_in, w_gate, small, *normed, *x, *inverse)


def grads_kernel(
    normed_ref,
    dgate_ref,
    dup_ref,
    hidden_ref,
    gout_ref,
    out_ref,
    made_wide,
    made_down,
    come_wide,
    come_down,
    send_sem,
    recv_sem,
    store_sem,
):
    step = pl.program_id(0)
    core = lax.axis_index("core")
    other = {"core": 1 - core}
    wide_rows, down_rows = (made_wide.shape[3], made_down.shape[3])
    wides, downs = (come_wide.shape[0], come_down.shape[0])
    total = wides + downs
    down_at = wides * wide_rows

    def exchange(made, come, index, slot):
        return pltpu.make_async_remote_copy(
            src_ref=made.at[lax.rem(index, 3), 1 - core],
            dst_ref=come.at[index],
            send_sem=send_sem.at[slot],
            recv_sem=recv_sem.at[slot],
            device_id=other,
            device_id_type=MESH,
        )

    def store_wide(index):
        return pltpu.make_async_copy(
            come_wide.at[index],
            out_ref.at[:, pl.ds(pl.multiple_of(index * wide_rows, wide_rows), wide_rows)],
            store_sem.at[index],
        )

    def store_down(index):
        chips = come_down.shape[1]
        return pltpu.make_async_copy(
            come_down.at[index],
            out_ref.at[pl.ds(index * chips, chips), pl.ds(down_at, down_rows)],
            store_sem.at[index + wides],
        )

    @pl.when(step == 0)
    def _():
        barrier = pltpu.get_barrier_semaphore()
        pl.semaphore_signal(barrier, inc=1, device_id=other, device_id_type=MESH)
        pl.semaphore_wait(barrier, 1)

    def product_wide(source, index):
        made = made_wide.at[lax.rem(index, 3)]
        chips, rows = (made.shape[1], made.shape[2])
        tile = 512

        def column(place, carry):
            at = pl.ds(pl.multiple_of(place * tile, tile), tile)
            part = lax.dot_general(
                normed_ref[...], source[:, at], (((0,), (0,)), ((), ())), preferred_element_type=jnp.float32
            )
            part = part.astype(jnp.bfloat16).reshape(chips, 2, rows, tile)
            made[0, :, :, at] = part[:, 0]
            made[1, :, :, at] = part[:, 1]
            return carry

        lax.fori_loop(0, source.shape[1] // tile, column, 0, unroll=True)

    def product_tall(left, right, made_all, index):
        made = made_all.at[lax.rem(index, 3)]
        chips, rows = (made.shape[1], made.shape[2])
        tile = 512

        def column(place, carry):
            at = pl.ds(pl.multiple_of(place * tile, tile), tile)
            part = lax.dot_general(
                left[...], right[:, at], (((0,), (0,)), ((), ())), preferred_element_type=jnp.float32
            )
            part = part.astype(jnp.bfloat16).reshape(chips, 2, rows, tile)
            made[0, :, :, at] = part[:, 0]
            made[1, :, :, at] = part[:, 1]
            return carry

        lax.fori_loop(0, right.shape[1] // tile, column, 0, unroll=True)

    half = wides // 2

    @pl.when(step < half)
    def _():
        product_wide(dgate_ref, step)

    @pl.when((step >= half) & (step < wides))
    def _():
        product_wide(dup_ref, step)

    @pl.when(step < wides)
    def _():
        exchange(made_wide, come_wide, step, step).start()

    @pl.when((step >= wides) & (step < total))
    def _():
        product_tall(hidden_ref, gout_ref, made_down, step - wides)
        exchange(made_down, come_down, step - wides, step).start()

    def finish(made, come, index, slot, store):
        exchange(made, come, index, slot).wait()
        mine = made.at[lax.rem(index, 3), core]
        arrived = come.at[index]

        def add(chip, carry):
            both = mine[chip].astype(jnp.float32) + arrived[chip].astype(jnp.float32)
            arrived[chip] = both.astype(jnp.bfloat16)
            return carry

        lax.fori_loop(0, come.shape[1], add, 0, unroll=4)
        store(index).start()

    before = step - 2

    @pl.when((before >= 0) & (before < wides))
    def _():
        finish(made_wide, come_wide, before, before, store_wide)

    @pl.when(before >= wides)
    def _():
        finish(made_down, come_down, before - wides, before, store_down)

    @pl.when(step == total + 1)
    def _():
        for index in range(wides):
            store_wide(index).wait()
        for index in range(downs):
            store_down(index).wait()


def block_gradients(normed, dgate, dup, hidden, gout):
    tokens, model = normed.shape
    ffn = hidden.shape[1]
    chips = lax.axis_size("seq") * lax.axis_size("zed")
    devices = 2 * chips
    wide_rows, down_rows = (model // devices, ffn // devices)
    chunk = 768
    wides, downs = (2 * ffn // model, ffn // chunk)
    half = wides // 2
    down_chips = chunk // (2 * down_rows)
    rows = wides * wide_rows + down_rows
    low = jnp.bfloat16

    def whole(array):
        return pl.BlockSpec(array.shape, lambda s: (0, 0), pipeline_mode=pl.Buffered(1))

    def part(columns, first, count):
        return pl.BlockSpec((tokens, columns), lambda s: (0, jnp.clip(s - first, 0, count - 1)))

    total = wides + downs
    flops = 6 * tokens * model * ffn
    arrays = (normed, dgate, dup, hidden, gout)
    moved = sum(math.prod(a.shape) * 2 for a in arrays) + chips * rows * model * 2
    return pl.pallas_call(
        grads_kernel,
        name="block_gradients",
        grid=(total + 2,),
        in_specs=[
            whole(normed),
            part(model, 0, half),
            part(model, half, half),
            part(chunk, wides, downs),
            whole(gout),
        ],
        out_specs=pl.BlockSpec(memory_space=pl.ANY),
        out_shape=jax.ShapeDtypeStruct((chips, rows, model), low),
        scratch_shapes=[
            pltpu.VMEM((3, 2, chips, wide_rows, model), low),
            pltpu.VMEM((3, 2, down_chips, down_rows, model), low),
            pltpu.VMEM((wides, chips, wide_rows, model), low),
            pltpu.VMEM((downs, down_chips, down_rows, model), low),
            pltpu.SemaphoreType.DMA((total,)),
            pltpu.SemaphoreType.DMA((total,)),
            pltpu.SemaphoreType.DMA((total,)),
        ],
        compiler_params=pltpu.CompilerParams(
            collective_id=2, has_side_effects=True, vmem_limit_bytes=VMEM_BYTES
        ),
        cost_estimate=pl.CostEstimate(flops=flops, bytes_accessed=moved, transcendentals=0),
    )(*arrays)


def passed_along(value, axis, steps):
    count = lax.axis_size(axis)
    leading, last = (max(0, -steps), min(count, count - steps))
    return lax.ppermute(value, axis, [(source, source + steps) for source in range(leading, last)])


def weight_grad(left, right):
    return lax.dot_general(
        left, right, (((0,), (0,)), ((), ())), preferred_element_type=jnp.float32
    ).astype(jnp.bfloat16)


def back_dot(left, right):
    return lax.dot_general(
        left, right, (((1,), (1,)), ((), ())), preferred_element_type=jnp.float32
    )


def fwd_dot(left, right):
    return jnp.dot(left, right, preferred_element_type=jnp.float32)


def gelu_fn(value):
    return jax.nn.gelu(value, approximate=True)


def norm_back(grad_norm, normed, inverse, gain):
    scaled = grad_norm * gain
    mean_term = jnp.mean(scaled * normed, axis=1, keepdims=True)
    return inverse * (scaled - normed * mean_term)


def scattered(gradient):
    return lax.psum_scatter(
        gradient, ("seq", "zed", "core"), scatter_dimension=0, tiled=True
    ).astype(jnp.float32)


def body(
    tokens,
    cotangent,
    doc_starts,
    lengths,
    norm1_gain,
    recur_input,
    recur_gate,
    conv_kernel,
    conv_bias,
    lru_gates,
    lru_bias,
    lru_decay,
    recur_out,
    norm2_gain,
    mlp_gate,
    mlp_up,
    mlp_down,
):
    count = lax.axis_size(CHAN)
    row_count, block_len = (tokens.shape[0] // count, tokens.shape[1])
    model_dim = tokens.shape[2] * count
    tok_count = row_count * block_len
    rec_width = recur_input.shape[1]
    ffn_width = mlp_gate.shape[1]
    head_count = H
    head_size = rec_width // head_count
    tap_count = conv_kernel.shape[0]
    rim_size = tap_count - 1
    seq_index = lax.axis_index("seq")
    position = seq_index * block_len + jnp.arange(block_len, dtype=jnp.int32)
    bounds = jnp.concatenate([doc_starts, lengths[:, None]], axis=1)
    is_before = bounds[:, None, :] <= position[None, :, None]
    seg_start = jnp.max(jnp.where(is_before, bounds[:, None, :], 0), axis=2)
    dist = jnp.broadcast_to(
        (position[None, :] - seg_start)[:, :, None], (row_count, block_len, LANES)
    )
    soft_decay = jax.nn.softplus(-lru_decay)
    params = jnp.concatenate(
        [
            conv_kernel,
            conv_bias[None],
            lru_bias,
            (-8.0 * soft_decay)[None],
            (8.0 * jax.nn.sigmoid(-lru_decay))[None],
            jnp.zeros((SUBLANES - 1, rec_width), jnp.float32),
        ],
        axis=0,
    )
    core = Recurrence(row_count, block_len, rec_width, head_size)
    wide_gates = core.widen(lru_gates)
    if tokens.shape[2] % LANES == 0:
        blocks = [features_in(tokens, slice(0, 1))]
        later, wide_gates, params, dist = lax.optimization_barrier(
            (tokens, wide_gates, params, dist)
        )
        blocks += [features_in(later, slice(row, row + 1)) for row in range(1, row_count)]
    else:
        side = features_in(tokens)
        blocks = [side[:, row * block_len : (row + 1) * block_len] for row in range(row_count)]
    per_row = []
    for row in range(row_count):
        block = blocks[row]
        if row:
            block, _ = lax.optimization_barrier((block, per_row[-1][-1]))
        per_row.append(
            front(
                block,
                norm1_gain,
                recur_input,
                recur_gate,
                dist[row : row + 1],
                params,
                wide_gates,
            )
        )
    low_x, inverse, normed_low, branch, gate_pre, rim, lru_in, rate, igate, state, cum, last = zip(
        *per_row
    )
    entering, mixed_low, resid_one, normed_low2 = middle(
        last, state, cum, gate_pre, low_x, recur_out, norm2_gain
    )
    cotangent, _ = lax.optimization_barrier((cotangent, block))
    cotangent, resid_one = lax.optimization_barrier((features_in(cotangent), resid_one))
    grad_low, hidden_low, mgate_low, mup_low = mlp_hidden(
        lengths - seq_index * block_len, cotangent, normed_low2, mlp_gate, mlp_up, mlp_down
    )
    devices = lax.axis_size(("seq", "zed", "core"))
    own_rows = model_dim // devices
    tiled = own_rows % (2 * SUBLANES) == 0 and tokens.shape[2] % LANES == 0
    if tiled:
        merged = block_gradients(normed_low2, mgate_low, mup_low, hidden_low, grad_low)
        merged, hidden_low = lax.optimization_barrier((merged, hidden_low))
        merged = lax.psum_scatter(merged, "seq", scatter_dimension=0, tiled=True)
    result_parts, resid_low = mlp_back(
        hidden_low,
        mgate_low,
        mup_low,
        grad_low,
        resid_one,
        norm2_gain,
        mlp_gate,
        mlp_up,
        mlp_down,
        cotangent.shape,
    )
    output = features_out(result_parts, row_count)
    gate_low, back_local, back_cum, first_term = core.adjoint(
        resid_low,
        recur_out,
        gate_pre,
        state,
        cum,
        entering,
        rate,
        dist,
        params,
    )
    gate_low = gate_low.reshape(tok_count, rec_width)

    def zed_stage(leaving):
        if not tiled:
            return ((), leaving)
        done, leaving = lax.optimization_barrier((merged, leaving))
        return (lax.psum_scatter(done, "zed", scatter_dimension=0, tiled=True), leaving)

    branch_local, ending, leading, small, merged_own = core.backward(
        back_local,
        back_cum,
        first_term,
        last,
        state,
        cum,
        entering,
        rate,
        igate,
        lru_in,
        dist,
        branch,
        rim,
        params,
        wide_gates,
        zed_stage,
    )
    branch_low = branch_local.reshape(tok_count, rec_width)
    if tiled:
        output, branch_low = lax.optimization_barrier((output, branch_low))
        grad_tokens, sum_rgate, sum_rout, sum_rin, own_small = tail(
            gate_low,
            branch_low,
            ending,
            leading,
            mixed_low,
            resid_low,
            norm1_gain,
            recur_input,
            recur_gate,
            small,
            normed_low,
            low_x,
            inverse,
        )
        device = lax.axis_index(("seq", "zed", "core"))
        sums = outputs(
            device,
            merged_own[0],
            sum_rgate,
            sum_rin,
            sum_rout,
            own_small,
            recur_input,
            recur_gate,
            mlp_gate,
            mlp_up,
            norm1_gain,
            norm2_gain,
            head_size,
        )
        flat = (0, 4, 7, 9)
        sums = [part.reshape(-1) if place in flat else part for place, part in enumerate(sums)]
        return (output, grad_tokens, *sums)
    else:
        from_next = passed_along(
            leading[:, SUBLANES - rim_size :, :].astype(jnp.bfloat16), "seq", -1
        )
        ending = ending + jnp.pad(
            from_next.astype(jnp.float32), ((0, 0), (SUBLANES - rim_size, 0), (0, 0))
        )
        branch_low = lax.dynamic_update_slice(
            branch_local, ending.astype(jnp.bfloat16), (0, block_len - SUBLANES, 0)
        ).reshape(tok_count, rec_width)
        grad_norm1 = back_dot(branch_low, recur_input) + back_dot(gate_low, recur_gate)
        inv_one = jnp.concatenate(inverse)[:, :1]
        normed_one = jnp.concatenate(low_x).astype(jnp.float32) * inv_one
        normed_low = jnp.concatenate(normed_low)
        input_part = norm_back(grad_norm1, normed_one, inv_one, norm1_gain)
        grad_x = (resid_low.astype(jnp.float32) + input_part).astype(jnp.bfloat16)
        grad_tokens = features_out(features_apart(grad_x), row_count)
        sum_mgate, sum_mup, sum_down, sum_rout, sum_rgate, sum_rin = (
            scattered(weight_grad(left, right))
            for left, right in (
                (normed_low2, mgate_low),
                (normed_low2, mup_low),
                (hidden_low, grad_low),
                (mixed_low, resid_low),
                (normed_low, gate_low),
                (normed_low, branch_low),
            )
        )
        own_small = scattered(small)
    sum_lgates = jnp.concatenate(
        [own_small[:, :head_size], own_small[:, LANES : LANES + head_size]], axis=1
    )
    own_sums = jnp.swapaxes(own_small[:, head_size : head_size + SUBLANES], 0, 1)
    device = lax.axis_index(("seq", "zed", "core"))

    def mine(array, size, axis=0):
        return lax.dynamic_slice_in_dim(array, device * size, size, axis)

    def weighed(weight, gradient):
        return jnp.sum(mine(weight, own_rows).astype(jnp.float32) * gradient, axis=1)

    sum_gain1 = (weighed(recur_input, sum_rin) + weighed(recur_gate, sum_rgate)) / mine(
        norm1_gain, own_rows
    )
    sum_gain2 = (weighed(mlp_gate, sum_mgate) + weighed(mlp_up, sum_mup)) / mine(
        norm2_gain, own_rows
    )
    sum_decay = own_sums[7]
    return (
        output,
        grad_tokens,
        sum_gain1,
        sum_rin,
        sum_rgate,
        own_sums[:4],
        own_sums[4],
        sum_lgates,
        own_sums[5:7],
        sum_decay,
        sum_rout,
        sum_gain2,
        sum_mgate,
        sum_mup,
        sum_down,
    )


def solution(mesh):
    seq, chan = (mesh.shape["seq"], mesh.shape["chan"])
    chips = jax.sharding.Mesh(mesh.devices.reshape(seq, chan // 2, 2), ("seq", "zed", "core"))
    chan = ("zed", "core")
    every = ("seq", "zed", "core")
    activations = P(None, "seq", chan)
    rows, columns, vector = (P(every, None), P(None, every), P(every))
    return jax.shard_map(
        body,
        mesh=chips,
        in_specs=(activations, activations, P(chan, None), P(chan)) + (P(),) * 13,
        out_specs=(
            activations,
            activations,
            vector,
            rows,
            rows,
            columns,
            vector,
            rows,
            columns,
            vector,
            rows,
            vector,
            rows,
            rows,
            rows,
        ),
        check_vma=False,
    )
```

```python
import functools
import math

import jax
import jax.numpy as jnp
from jax import lax
from jax.experimental import pallas as pl
from jax.experimental.pallas import tpu as pltpu
from jax.sharding import PartitionSpec as P

H = 16


EPS = 1e-06
ROOT_FLOOR = 1e-06
LANES = 128
SUBLANES = 8
STEP = 16
VMEM_BYTES = 56 * 1024 * 1024
MESH = pl.DeviceIdType.MESH


def sigmoid(value):
    return 0.5 * jnp.tanh(0.5 * value) + 0.5


GELU_C = 0.7978845608
GELU_A = 0.044715


def gelu_pair(value):
    square = value * value
    inner = jnp.tanh(value * (GELU_C + (GELU_C * GELU_A) * square))
    half = 0.5 + 0.5 * inner
    slope = GELU_C + (3.0 * GELU_C * GELU_A) * square
    return (value * half, half + 0.5 * value * (1.0 - inner * inner) * slope)


def root_argument(log_decay, decay):
    y = 2.0 * log_decay
    series = 1.0 + y * (0.5 + y * (1.0 / 6.0 + y * (1.0 / 24.0)))
    return jnp.where(y > -0.05, -y * series, 1.0 - decay * decay)


def across(column, width):
    return jnp.concatenate([column] * (width // LANES), axis=1)


class Rows:
    def __init__(self, refs):
        self.refs = refs

    def __getitem__(self, index):
        if not isinstance(index, tuple):
            return self.refs[index][0]
        return self.refs[index[0]][(0,) + index[1:]]


def by_rows(refs, rows, apart):
    found = []
    for split in apart:
        count = rows if split else 1
        found.append(Rows(refs[:count]) if split else refs[0])
        refs = refs[count:]
    return found, refs


def scan_block(
    branch_ref,
    rim_ref,
    dist_ref,
    par_ref,
    gates_ref,
    lru_ref,
    rate_ref,
    igate_ref,
    state_ref,
    cum_ref,
    last_ref,
    both_ref,
):
    rows, length, width = branch_ref.shape
    span = 2 * STEP if rows == 1 else STEP
    taps = [par_ref[k : k + 1, :] for k in range(4)]
    conv_bias, rate_bias, input_bias, soft = (par_ref[k : k + 1, :] for k in range(4, 8))
    place = lax.broadcasted_iota(jnp.int32, (SUBLANES, width), 0)

    for row in range(rows):

        def conv_step(index, before, row=row):
            base = pl.multiple_of(index * STEP, STEP)
            pieces = []
            for half in range(STEP // SUBLANES):
                at = pl.ds(base + half * SUBLANES, SUBLANES)
                here = branch_ref[row, at, :]
                dist = across(dist_ref[row, at, :], width)
                total = conv_bias + taps[0] * here
                for k in range(1, 4):
                    shifted = pltpu.roll(jnp.where(place < SUBLANES - k, here, before), k, 0)
                    total = total + taps[k] * jnp.where(dist >= k, shifted, 0.0)
                pieces.append(total)
                before = here
            lru_ref[row, pl.ds(base, STEP), :] = jnp.concatenate(pieces, axis=0).astype(jnp.bfloat16)
            return before

        lax.fori_loop(0, length // STEP, conv_step, rim_ref[row], unroll=2)

        piece = min(length, 256)

        def dot_step(index, carry, row=row):
            at = pl.ds(pl.multiple_of(index * piece, piece), piece)
            both_ref[row, at, :] = jnp.dot(
                lru_ref[row, at, :], gates_ref[...], preferred_element_type=jnp.float32
            )
            return carry

        lax.fori_loop(0, length // piece, dot_step, 0)

    def scan_step(index, carry):
        base = pl.multiple_of(index * span, span)
        later = []
        for row in range(rows):
            run_cum, run_state = carry[row]
            lru_both = lru_ref[row, pl.ds(base, span), :].astype(jnp.float32)
            for half in range(span // SUBLANES):
                at = pl.ds(base + half * SUBLANES, SUBLANES)
                lru = lru_both[half * SUBLANES : (half + 1) * SUBLANES]
                start = across(dist_ref[row, at, :], width) == 0
                rate = sigmoid(both_ref[row, at, :width] + rate_bias)
                igate = sigmoid(both_ref[row, at, width:] + input_bias)
                log_decay = rate * soft
                decay = jnp.exp(log_decay)
                arg = jnp.maximum(root_argument(log_decay, decay), ROOT_FLOOR)
                root = arg * lax.rsqrt(arg)
                cum = jnp.where(start, 0.0, decay)
                value = jnp.where(start, 1.0, root) * igate * lru
                rate_ref[row, at, :] = rate
                igate_ref[row, at, :] = igate
                for shift in (1, 2, 4):
                    live = place >= shift
                    value = value + cum * jnp.where(live, pltpu.roll(value, shift, 0), 0.0)
                    cum = cum * jnp.where(live, pltpu.roll(cum, shift, 0), 1.0)
                value = value + cum * run_state
                cum = cum * run_cum
                state_ref[row, at, :] = value
                cum_ref[row, at, :] = cum
                run_state = value[SUBLANES - 1 :, :]
                run_cum = cum[SUBLANES - 1 :, :]
            later.append((run_cum, run_state))
        return tuple(later)

    one, zero = (jnp.ones((1, width), jnp.float32), jnp.zeros((1, width), jnp.float32))
    done = lax.fori_loop(
        0, length // span, scan_step, tuple((one, zero) for _ in range(rows)), unroll=2
    )
    for row in range(rows):
        for place in range(2):
            last_ref[row, place : place + 1, :] = done[row][place]


def carried(sent_ref, got_ref, out_ref, send_sem, recv_sem, backward):
    seq, count = (lax.axis_index("seq"), lax.axis_size("seq"))

    def other(step):
        return {"seq": lax.rem(seq + step, count)}

    barrier = pltpu.get_barrier_semaphore()
    for step in range(1, count):
        pl.semaphore_signal(barrier, inc=1, device_id=other(step), device_id_type=MESH)
    pl.semaphore_wait(barrier, count - 1)
    copies = [
        pltpu.make_async_remote_copy(
            src_ref=sent_ref,
            dst_ref=got_ref.at[seq],
            send_sem=send_sem.at[step - 1],
            recv_sem=recv_sem.at[step - 1],
            device_id=other(step),
            device_id_type=MESH,
        )
        for step in range(1, count)
    ]
    for copy in copies:
        copy.start()
    got_ref[seq] = sent_ref[...]
    for copy in copies:
        copy.wait()
    for row in range(sent_ref.shape[0]):
        total = jnp.zeros(out_ref.shape[1:], jnp.float32)
        for place in range(count - 1, 0, -1) if backward else range(count - 1):
            longer = got_ref[place, row, 0:1, :] * total + got_ref[place, row, 1:2, :]
            total = jnp.where(place > seq if backward else place < seq, longer, total)
        out_ref[row] = total


def adjoint_kernel(rows, *refs):
    (
        dres_ref,
        weight_ref,
        pre_ref,
        state_ref,
        cum_ref,
        carry_ref,
        rate_ref,
        dist_ref,
        par_ref,
    ), outs = by_rows(refs, rows, (False, False, True, True, True, False, True, False, False))
    dgate_ref, local_ref, back_ref, first_ref, dmix_ref = outs
    _, length, width = dmix_ref.shape
    for row in range(rows):
        dmix_ref[row] = lax.dot_general(
            dres_ref[row * length : (row + 1) * length, :],
            weight_ref[...],
            (((1,), (1,)), ((), ())),
            preferred_element_type=jnp.float32,
        )
    soft = par_ref[7:8, :]
    place = lax.broadcasted_iota(jnp.int32, (SUBLANES, width), 0)
    last = length // STEP - 1

    def step(index, carry):
        base = pl.multiple_of((last - index) * STEP, STEP)
        later = []
        for row in range(rows):
            run_cum, run_back = carry[row]
            entering = carry_ref[row]
            pieces = []
            for half in reversed(range(STEP // SUBLANES)):
                at = pl.ds(base + half * SUBLANES, SUBLANES)
                start = across(dist_ref[row, at, :], width) == 0
                state = state_ref[row, at, :] + cum_ref[row, at, :] * entering
                act, slope = gelu_pair(pre_ref[row, at, :])
                dmix = dmix_ref[row, at, :]
                pieces.append(dmix * state * slope)
                dstate = dmix * act
                coef = jnp.where(start, 0.0, jnp.exp(rate_ref[row, at, :] * soft))
                value = coef * dstate
                for shift in (1, 2, 4):
                    live = place < SUBLANES - shift
                    turn = SUBLANES - shift
                    value = value + coef * jnp.where(live, pltpu.roll(value, turn, 0), 0.0)
                    coef = coef * jnp.where(live, pltpu.roll(coef, turn, 0), 1.0)
                value = value + coef * run_back
                coef = coef * run_cum
                inside = place < SUBLANES - 1
                local_ref[row, at, :] = dstate + jnp.where(
                    inside, pltpu.roll(value, SUBLANES - 1, 0), run_back
                )
                back_ref[row, at, :] = jnp.where(inside, pltpu.roll(coef, SUBLANES - 1, 0), run_cum)
                run_back = value[:1, :]
                run_cum = coef[:1, :]
            dgate_ref[row, pl.ds(base, STEP), :] = jnp.concatenate(pieces[::-1], axis=0).astype(
                jnp.bfloat16
            )
            later.append((run_cum, run_back))
        return tuple(later)

    one, zero = (jnp.ones((1, width), jnp.float32), jnp.zeros((1, width), jnp.float32))
    done = lax.fori_loop(0, last + 1, step, tuple((one, zero) for _ in range(rows)), unroll=2)
    for row in range(rows):
        first_ref[row] = done[row][1]


def backward_kernel(head_size, rows, *refs):
    first_at = 2
    sent_ref, got_ref, send_sem, recv_sem = refs[-4:]
    leaving_ref = refs[-8]
    lasts = Rows(refs[first_at + 1 : first_at + 1 + rows])

    @pl.when(pl.program_id(0) == 0)
    def _():
        for row in range(rows):
            sent_ref[row, 0:1, :] = lasts[row, 0:1, :]
            sent_ref[row, 1:2, :] = refs[first_at][row]
        carried(sent_ref, got_ref, leaving_ref, send_sem, recv_sem, True)

    block_backward(head_size, rows, 0, leaving_ref, *refs[:-8], *refs[-7:-4])


def later_backward_kernel(head_size, rows, first, *refs):
    held = 4
    block_backward(head_size, rows, first, refs[0], *refs[1 + held :])


def block_backward(head_size, rows, first_block, leaving_ref, *refs):
    (
        local_ref,
        back_ref,
        first_ref,
        last_ref,
        state_ref,
        cum_ref,
        in_ref,
        rate_ref,
        igate_ref,
        lru_ref,
        dist_ref,
        branch_ref,
        rim_ref,
        par_ref,
        gates_ref,
    ), others = by_rows(
        refs, rows, (False,) * 3 + (True,) * 3 + (False,) + (True,) * 3 + (False,) + (True,) * 2 + (False,) * 2
    )
    dbranch_ref, tail_ref, head_ref, dgates_ref = others[:4]
    both_ref, dconv_ref, sums_ref = others[-3:]
    _, length, width = local_ref.shape
    here = pl.program_id(0) + first_block
    block = pl.ds(pl.multiple_of(here * width, width), width)
    taps = [par_ref[k : k + 1, :] for k in range(4)]
    soft = par_ref[7:8, :]
    place = lax.broadcasted_iota(jnp.int32, (SUBLANES, width), 0)
    zeros = jnp.zeros((SUBLANES, width), jnp.float32)

    def gate_step(index, carry):
        sums, earlier = carry
        decay_sum, rate_sum, input_sum = sums
        base = pl.multiple_of(index * STEP, STEP)
        later = []
        for row in range(rows):
            before = earlier[row]
            entering = in_ref[row]
            leaving = leaving_ref[row, :, block]
            lru_both = lru_ref[row, pl.ds(base, STEP), :].astype(jnp.float32)
            drates, dinputs = ([], [])
            for half in range(STEP // SUBLANES):
                at = pl.ds(base + half * SUBLANES, SUBLANES)
                lru = lru_both[half * SUBLANES : (half + 1) * SUBLANES]
                start = across(dist_ref[row, at, :], width) == 0
                adjoint = local_ref[row, at, :] + back_ref[row, at, :] * leaving
                state = state_ref[row, at, :] + cum_ref[row, at, :] * entering
                previous = jnp.where(place < 1, before, pltpu.roll(state, 1, 0))
                before = state[SUBLANES - 1 :, :]
                rate = rate_ref[row, at, :]
                igate = igate_ref[row, at, :]
                log_decay = rate * soft
                decay = jnp.exp(log_decay)
                arg = root_argument(log_decay, decay)
                above = arg > ROOT_FLOOR
                arg = jnp.maximum(arg, ROOT_FLOOR)
                inverse = lax.rsqrt(arg)
                scale = jnp.where(start, 1.0, arg * inverse)
                gated = adjoint * igate
                dscale = gated * lru
                pull = jnp.where(above, dscale * decay * decay * inverse, 0.0)
                dlog = jnp.where(start, 0.0, adjoint * previous * decay - pull)
                dig = adjoint * scale * lru
                weighted = dlog * rate
                decay_sum = decay_sum + weighted
                drates.append(weighted * soft * (1.0 - rate))
                dinputs.append(dig * igate * (1.0 - igate))
                dconv_ref[row, at, :] = gated * scale
            drate = jnp.concatenate(drates, axis=0).astype(jnp.bfloat16)
            dinput = jnp.concatenate(dinputs, axis=0).astype(jnp.bfloat16)
            both_ref[row, pl.ds(base, STEP), :width] = drate
            both_ref[row, pl.ds(base, STEP), width:] = dinput
            drate = drate.astype(jnp.float32)
            dinput = dinput.astype(jnp.float32)
            rate_sum = rate_sum + (drate[:SUBLANES] + drate[SUBLANES:])
            input_sum = input_sum + (dinput[:SUBLANES] + dinput[SUBLANES:])
            later.append(before)
        return ((decay_sum, rate_sum, input_sum), tuple(later))

    sums, _ = lax.fori_loop(
        0,
        length // STEP,
        gate_step,
        ((zeros, zeros, zeros), tuple(in_ref[row] for row in range(rows))),
        unroll=2,
    )
    for slot, total in zip((5, 6, 7), (sums[1], sums[2], sums[0] * par_ref[8:9, :])):
        sums_ref[slot : slot + 1, :] = jnp.sum(total, axis=0, keepdims=True)

    piece = min(length, 256)
    wide = None
    for row in range(rows):

        def dot_step(index, carry, row=row):
            at = pl.ds(pl.multiple_of(index * piece, piece), piece)
            dconv_ref[row, at, :] += lax.dot_general(
                both_ref[row, at, :],
                gates_ref[...],
                (((1,), (1,)), ((), ())),
                preferred_element_type=jnp.float32,
            )
            return carry

        lax.fori_loop(0, length // piece, dot_step, 0)
        part = lax.dot_general(
            lru_ref[row], both_ref[row], (((0,), (0,)), ((), ())), preferred_element_type=jnp.float32
        )
        wide = part if wide is None else wide + part
    row_head = lax.broadcasted_iota(jnp.int32, (width, width), 0) // head_size
    col_head = lax.broadcasted_iota(jnp.int32, (width, width), 1) // head_size
    own = row_head == col_head
    folds = []
    for part in range(2):
        kept = jnp.where(own, wide[:, part * width : (part + 1) * width], 0.0)
        folded = kept
        for other in range(1, width // head_size):
            folded = folded + pltpu.roll(kept, width - other * head_size, 1)
        folds.append(folded[:, :LANES])

    def conv_step(index, carry):
        sums, following = carry
        sums = list(sums)
        base = pl.multiple_of((length // STEP - 1 - index) * STEP, STEP)
        later = []
        for row in range(rows):
            after = following[row]
            pieces = []
            for half in reversed(range(STEP // SUBLANES)):
                at = pl.ds(base + half * SUBLANES, SUBLANES)
                dist = across(dist_ref[row, at, :], width)
                branch = branch_ref[row, at, :]
                here = dconv_ref[row, at, :]
                total = taps[0] * here
                sums[0] = sums[0] + here * branch
                sums[4] = sums[4] + here
                masked = tuple(jnp.where(dist >= k, here, 0.0) for k in range(1, 4))
                for k in range(1, 4):
                    moved = pltpu.roll(
                        jnp.where(place >= k, masked[k - 1], after[k - 1]), SUBLANES - k, 0
                    )
                    total = total + taps[k] * moved
                    sums[k] = sums[k] + branch * moved
                after = masked
                pieces.append(total)
            whole = jnp.concatenate(pieces[::-1], axis=0)
            dbranch_ref[row, pl.ds(base, STEP), :] = whole.astype(jnp.bfloat16)
            later.append(after)

            @pl.when(index == 0)
            def _(row=row, whole=whole):
                tail_ref[row] = whole[STEP - SUBLANES :]

        return (tuple(sums), tuple(later))

    sums, firsts = lax.fori_loop(
        0,
        length // STEP,
        conv_step,
        ((zeros,) * 5, tuple((zeros,) * 3 for _ in range(rows))),
        unroll=2,
    )
    sums = list(sums)
    for row in range(rows):
        total = zeros
        rim = rim_ref[row]
        for k in range(1, 4):
            moved = pltpu.roll(jnp.where(place >= k, 0.0, firsts[row][k - 1]), SUBLANES - k, 0)
            total = total + taps[k] * moved
            sums[k] = sums[k] + rim * moved
        head_ref[row] = total
    for slot in range(5):
        sums_ref[slot : slot + 1, :] = jnp.sum(sums[slot], axis=0, keepdims=True)
    above = jnp.zeros((head_size, width), jnp.float32)
    below = jnp.zeros((LANES - head_size - SUBLANES, width), jnp.float32)
    turned = jnp.concatenate([above, sums_ref[...], below], axis=0).T
    lane = lax.broadcasted_iota(jnp.int32, (width, LANES), 1)
    dgates_ref[:, :LANES] = jnp.where(lane < head_size, folds[0], turned).astype(dgates_ref.dtype)
    dgates_ref[:, LANES:] = folds[1].astype(dgates_ref.dtype)


def channel_call(
    kernel, name, arrays, specs, outs, out_specs, scratch, blocks, flops, params=()
):
    moved = sum(math.prod(a.shape) * a.dtype.itemsize for a in (*arrays, *outs))
    return pl.pallas_call(
        kernel,
        name=name,
        grid=(blocks,),
        in_specs=specs,
        out_specs=out_specs,
        out_shape=outs,
        scratch_shapes=scratch,
        compiler_params=pltpu.CompilerParams(vmem_limit_bytes=VMEM_BYTES, **dict(params)),
        cost_estimate=pl.CostEstimate(flops=flops, bytes_accessed=moved, transcendentals=0),
    )(*arrays)


class Recurrence:
    def __init__(self, rows, length, channels, head_size):
        self.rows, self.length, self.channels = (rows, length, channels)
        self.head_size = head_size
        self.width = head_size * LANES // math.gcd(head_size, LANES)
        self.blocks = channels // self.width
        self.flops = 2 * rows * length * channels * 2 * self.width

    def tall(self):
        return pl.BlockSpec((self.rows, self.length, self.width), lambda j: (0, 0, j))

    def short(self, size):
        return pl.BlockSpec((self.rows, size, self.width), lambda j: (0, 0, j))

    def apart(self, size):
        return [pl.BlockSpec((1, size, self.width), lambda j: (0, 0, j))] * self.rows

    def whole(self, rows, size):
        return pl.BlockSpec((rows, size, self.channels), lambda j: (0, 0, 0))

    def flat(self, size):
        return pl.BlockSpec((size, self.width), lambda j: (0, j))

    def dist(self):
        return pl.BlockSpec((self.rows, self.length, LANES), lambda j: (0, 0, 0))

    def gates(self, columns):
        return pl.BlockSpec((self.width, columns), lambda j: (j, 0))

    def shape(self, size, dtype):
        return jax.ShapeDtypeStruct((self.rows, size, self.channels), dtype)

    def widen(self, lru_gates):
        size, width = (self.head_size, self.width)
        heads = width // size
        column = jnp.arange(2 * width)
        source = (column // width) * size + column % size
        spread = (jnp.arange(2 * size)[:, None] == source[None, :]).astype(jnp.bfloat16)
        owner = (column % width) // size
        mine = (jnp.arange(self.channels) // size) % heads
        wide = jnp.dot(lru_gates, spread, preferred_element_type=jnp.float32)
        return jnp.where(mine[:, None] == owner[None, :], wide, 0.0).astype(jnp.bfloat16)

    def adjoint(self, dres, weight, pre, state, cum, entering, rate, dist, params):
        f32 = jnp.float32
        outs = [self.shape(self.length, d) for d in (jnp.bfloat16, f32, f32)] + [self.shape(1, f32)]
        tall, apart = (self.tall(), self.apart(self.length))
        return channel_call(
            functools.partial(adjoint_kernel, self.rows),
            "recurrence_adjoint",
            (dres, weight, *pre, *state, *cum, entering, *rate, dist, params),
            [
                pl.BlockSpec(dres.shape, lambda j: (0, 0)),
                self.gates(weight.shape[1]),
                *apart * 3,
                self.short(1),
                *apart,
                self.dist(),
                self.flat(16),
            ],
            outs,
            [tall, tall, tall, self.short(1)],
            [pltpu.VMEM((self.rows, self.length, self.width), f32)],
            self.blocks,
            2 * self.rows * self.length * weight.size,
        )

    def backward(
        self, local, back, first, last, state, cum, entering, rate, igate, lru, dist, branch, rim, params, gates, between_calls
    ):
        f32 = jnp.float32
        outs = [
            self.shape(self.length, jnp.bfloat16),
            self.shape(SUBLANES, f32),
            self.shape(SUBLANES, f32),
            jax.ShapeDtypeStruct((self.channels, 2 * LANES), jnp.bfloat16),
        ]
        seqs = lax.axis_size("seq")
        summary = (self.rows, 2, self.channels)
        arrays = (local, back, first, *last, *state, *cum, entering, *rate, *igate, *lru, dist, *branch, *rim)
        arrays += (params, gates)
        early = self.blocks - 1
        scratch = [
            pltpu.VMEM((self.rows, self.length, 2 * self.width), jnp.bfloat16),
            pltpu.VMEM((self.rows, self.length, self.width), f32),
            pltpu.VMEM((SUBLANES, self.width), f32),
        ]

        def specs(offset):
            rows, width = (self.rows, self.width)

            def wide(rows, size):
                return pl.BlockSpec((rows, size, width), lambda j: (0, 0, j + offset))

            def flat(size):
                return pl.BlockSpec((size, width), lambda j: (0, j + offset))

            def tall(columns):
                return pl.BlockSpec((width, columns), lambda j: (j + offset, 0))

            whole, apart = (wide(rows, self.length), [wide(1, self.length)] * rows)
            given = [whole, whole, self.whole(rows, 1), *[self.whole(1, 2)] * rows, *apart * 2]
            given += [wide(rows, 1), *apart * 3, self.dist(), *apart, *[wide(1, SUBLANES)] * rows]
            given += [flat(16), tall(2 * width)]
            made = [whole, wide(rows, SUBLANES), wide(rows, SUBLANES), tall(2 * LANES)]
            return (given, made)

        given, made = specs(0)
        *found, leaving = channel_call(
            functools.partial(backward_kernel, self.head_size, self.rows),
            "recurrence_backward",
            arrays,
            given,
            outs + [self.shape(1, f32)],
            made + [self.whole(self.rows, 1)],
            scratch
            + [
                pltpu.VMEM(summary, f32),
                pltpu.VMEM((seqs,) + summary, f32),
                pltpu.SemaphoreType.DMA((seqs - 1,)),
                pltpu.SemaphoreType.DMA((seqs - 1,)),
            ],
            early,
            2 * self.flops,
            {"collective_id": 5, "has_side_effects": True},
        )
        between, leaving = between_calls(leaving)
        given, made = specs(early)
        done = pl.pallas_call(
            functools.partial(later_backward_kernel, self.head_size, self.rows, early),
            name="recurrence_backward_end",
            grid=(self.blocks - early,),
            in_specs=[self.whole(self.rows, 1)] + [pl.BlockSpec(memory_space=pl.ANY)] * 4 + given,
            out_specs=made,
            out_shape=outs,
            scratch_shapes=scratch,
            input_output_aliases={1 + k: k for k in range(4)},
            compiler_params=pltpu.CompilerParams(vmem_limit_bytes=VMEM_BYTES),
            cost_estimate=pl.CostEstimate(
                flops=self.flops // 2, bytes_accessed=16 * self.flops // self.width, transcendentals=0
            ),
        )(leaving, *found, *arrays)
        return (*done, between)


def gathered(parts_ref, at):
    return jnp.concatenate([parts_ref[k, at, :] for k in range(parts_ref.shape[0])], axis=1)


def front_kernel(
    parts_ref,
    gain_ref,
    input_ref,
    gate_ref,
    dist_ref,
    par_ref,
    gates_ref,
    x_ref,
    inverse_ref,
    normed_ref,
    branch_ref,
    pre_ref,
    rim_ref,
    lru_ref,
    rate_ref,
    igate_ref,
    state_ref,
    cum_ref,
    last_ref,
    landed_ref,
    both_ref,
    send_sem,
    recv_sem,
):
    tokens = x_ref.shape[0]
    piece, tall = (64, min(tokens, 512))
    step = pl.program_id(0)
    seq, seqs = (lax.axis_index("seq"), lax.axis_size("seq"))
    barrier = pltpu.get_barrier_semaphore()

    @pl.when(step == 0)
    def _():
        before = {"seq": lax.rem(seq + seqs - 1, seqs)}
        pl.semaphore_signal(barrier, inc=1, device_id=before, device_id_type=MESH)

        def norm(index, carry):
            at = pl.ds(pl.multiple_of(index * piece, piece), piece)
            low = gathered(parts_ref, at)
            x_ref[at, :] = low
            value = low.astype(jnp.float32)
            inverse = lax.rsqrt(jnp.mean(value * value, axis=1, keepdims=True) + EPS)
            inverse_ref[at, :] = jnp.broadcast_to(inverse, (piece, LANES))
            normed_ref[at, :] = (value * inverse * gain_ref[...]).astype(jnp.bfloat16)
            return carry

        lax.fori_loop(0, tokens // piece, norm, 0, unroll=2)

    rim_copy = pltpu.make_async_remote_copy(
        src_ref=normed_ref.at[tokens - STEP :],
        dst_ref=landed_ref,
        send_sem=send_sem,
        recv_sem=recv_sem,
        device_id={"seq": lax.rem(seq + 1, seqs)},
        device_id_type=MESH,
    )

    @pl.when(step == 0)
    def _():
        pl.semaphore_wait(barrier, 1)
        rim_copy.start()

    def multiply(index, carry):
        at = pl.ds(pl.multiple_of(index * tall, tall), tall)
        normed = normed_ref[at, :]
        branch_ref[0, at, :] = jnp.dot(normed, input_ref[...], preferred_element_type=jnp.float32)
        pre_ref[0, at, :] = jnp.dot(normed, gate_ref[...], preferred_element_type=jnp.float32)
        return carry

    lax.fori_loop(0, tokens // tall, multiply, 0)

    @pl.when(step == 0)
    def _():
        rim_copy.wait()

    before = jnp.dot(landed_ref[...], input_ref[...], preferred_element_type=jnp.float32)
    rim_ref[0] = jnp.where(seq > 0, 1.0, 0.0) * before[STEP - SUBLANES :]
    scan_block(
        branch_ref,
        rim_ref,
        dist_ref,
        par_ref,
        gates_ref,
        lru_ref,
        rate_ref,
        igate_ref,
        state_ref,
        cum_ref,
        last_ref,
        both_ref,
    )


def front(parts, gain, recur_input, recur_gate, dist, params, gates):
    count, tokens, width = parts.shape
    model, rec = recur_input.shape
    columns = gates.shape[1] // 2
    steps = rec // columns
    low, f32 = (jnp.bfloat16, jnp.float32)
    tall = pl.BlockSpec((model, columns), lambda j: (0, j))

    def whole(shape):
        return pl.BlockSpec(shape, lambda j: (0,) * len(shape))

    def wide(size, dtype):
        spec = pl.BlockSpec((1, size, columns), lambda j: (0, 0, j))
        return (spec, jax.ShapeDtypeStruct((1, size, rec), dtype))

    made = [wide(tokens, f32), wide(tokens, f32), wide(SUBLANES, f32), wide(tokens, low)]
    made += [wide(tokens, f32)] * 4 + [wide(2, f32)]
    return pl.pallas_call(
        front_kernel,
        name="project_and_scan",
        grid=(steps,),
        in_specs=[
            whole(parts.shape),
            whole((1, model)),
            tall,
            tall,
            whole(dist.shape),
            pl.BlockSpec((16, columns), lambda j: (0, j)),
            pl.BlockSpec((columns, 2 * columns), lambda j: (j, 0)),
        ],
        out_specs=[whole((tokens, model)), whole((tokens, LANES)), whole((tokens, model))]
        + [spec for spec, _ in made],
        out_shape=[
            jax.ShapeDtypeStruct((tokens, model), low),
            jax.ShapeDtypeStruct((tokens, LANES), f32),
            jax.ShapeDtypeStruct((tokens, model), low),
        ]
        + [shape for _, shape in made],
        scratch_shapes=[
            pltpu.VMEM((STEP, model), low),
            pltpu.VMEM((1, tokens, 2 * columns), f32),
            pltpu.SemaphoreType.DMA,
            pltpu.SemaphoreType.DMA,
        ],
        compiler_params=pltpu.CompilerParams(
            collective_id=3, has_side_effects=True, vmem_limit_bytes=VMEM_BYTES
        ),
        cost_estimate=pl.CostEstimate(
            flops=5 * tokens * model * rec, bytes_accessed=40 * tokens * model, transcendentals=0
        ),
    )(parts, gain[None], recur_input, recur_gate, dist, params, gates)


def middle_kernel(rows, *refs):
    (last_ref, state_hbm, cum_hbm, pre_hbm, x_ref, out_ref, gain_ref), others = by_rows(
        refs, rows, (True,) * 5 + (False,) * 2
    )
    entering_ref, mixed_ref, resid_ref, normed_ref = others[:4]
    sent_ref, got_ref, held_ref, send_sem, recv_sem, load_sem = others[4:]
    tall, model = resid_ref.shape
    step, steps = (pl.program_id(0), pl.num_programs(0))
    tiles = steps // rows
    slab = 16

    def on_row(place, act):
        for row in range(rows):

            @pl.when(lax.div(place, tiles) == row)
            def _(row=row):
                at = pl.ds(pl.multiple_of(lax.rem(place, tiles) * tall, tall), tall)
                slot = lax.rem(place, 2)
                for kind, source in enumerate((state_hbm, cum_hbm, pre_hbm)):
                    act(
                        pltpu.make_async_copy(
                            source.refs[row].at[0, at], held_ref.at[slot, kind], load_sem.at[slot, kind]
                        )
                    )

    @pl.when(step == 0)
    def _():
        on_row(step, lambda copy: copy.start())
        for row in range(rows):
            sent_ref[row] = last_ref[row]
        carried(sent_ref, got_ref, entering_ref, send_sem, recv_sem, False)

    @pl.when(step + 1 < steps)
    def _():
        on_row(step + 1, lambda copy: copy.start())

    on_row(step, lambda copy: copy.wait())
    slot = lax.rem(step, 2)
    mine = lax.div(step, tiles)

    def mix(index, carry):
        at = pl.ds(pl.multiple_of(index * slab, slab), slab)
        state = held_ref[slot, 0, at, :] + held_ref[slot, 1, at, :] * entering_ref[mine]
        pre = held_ref[slot, 2, at, :]
        inner = jnp.tanh(pre * (GELU_C + (GELU_C * GELU_A) * (pre * pre)))
        mixed_ref[at, :] = (state * (pre * (0.5 + 0.5 * inner))).astype(jnp.bfloat16)
        return carry

    lax.fori_loop(0, tall // slab, mix, 0, unroll=2)
    for row in range(rows):

        @pl.when(mine == row)
        def _(row=row):
            tile = 512
            for first in range(0, model, tile):
                at = slice(first, first + tile)
                resid_ref[:, at] = x_ref.refs[row][:, at].astype(jnp.float32) + jnp.dot(
                    mixed_ref[...], out_ref[:, at], preferred_element_type=jnp.float32
                )

    def norm(index, carry):
        at = pl.ds(pl.multiple_of(index * slab, slab), slab)
        resid = resid_ref[at, :]
        inverse = lax.rsqrt(jnp.mean(resid * resid, axis=1, keepdims=True) + EPS)
        normed_ref[at, :] = (resid * inverse * gain_ref[...]).astype(jnp.bfloat16)
        return carry

    lax.fori_loop(0, tall // slab, norm, 0, unroll=4)


def middle(last, state, cum, pre, x, recur_out, gain):
    rows = len(state)
    _, length, rec = state[0].shape
    model = recur_out.shape[1]
    tall = min(length, 256)
    tiles = length // tall
    tokens = rows * length
    seqs = lax.axis_size("seq")
    low, f32 = (jnp.bfloat16, jnp.float32)

    def whole(shape):
        return pl.BlockSpec(shape, lambda s: (0,) * len(shape), pipeline_mode=pl.Buffered(1))

    def flat(row):
        return lambda s: (jnp.clip(s - row * tiles, 0, tiles - 1), 0)

    summary = (rows, 2, rec)
    return pl.pallas_call(
        functools.partial(middle_kernel, rows),
        name="mix_and_norm",
        grid=(rows * tiles,),
        in_specs=[whole((1, 2, rec))] * rows
        + [pl.BlockSpec(memory_space=pl.ANY)] * (3 * rows)
        + [pl.BlockSpec((tall, model), flat(row)) for row in range(rows)]
        + [whole(recur_out.shape), whole((1, model))],
        out_specs=[
            pl.BlockSpec((rows, 1, rec), lambda s: (0, 0, 0)),
            pl.BlockSpec((tall, rec), lambda s: (s, 0)),
            pl.BlockSpec((tall, model), lambda s: (s, 0)),
            pl.BlockSpec((tall, model), lambda s: (s, 0)),
        ],
        out_shape=[
            jax.ShapeDtypeStruct((rows, 1, rec), f32),
            jax.ShapeDtypeStruct((tokens, rec), low),
            jax.ShapeDtypeStruct((tokens, model), f32),
            jax.ShapeDtypeStruct((tokens, model), low),
        ],
        scratch_shapes=[
            pltpu.VMEM(summary, f32),
            pltpu.VMEM((seqs,) + summary, f32),
            pltpu.VMEM((2, 3, tall, rec), f32),
            pltpu.SemaphoreType.DMA((seqs - 1,)),
            pltpu.SemaphoreType.DMA((seqs - 1,)),
            pltpu.SemaphoreType.DMA((2, 3)),
        ],
        compiler_params=pltpu.CompilerParams(
            collective_id=4, has_side_effects=True, vmem_limit_bytes=VMEM_BYTES
        ),
        cost_estimate=pl.CostEstimate(
            flops=2 * tokens * rec * model, bytes_accessed=14 * tokens * rec, transcendentals=0
        ),
    )(*last, *state, *cum, *pre, *x, recur_out, gain[None])


def hidden_kernel(
    left_ref,
    parts_ref,
    normed_ref,
    gate_ref,
    up_ref,
    down_ref,
    gout_ref,
    hidden_ref,
    dgate_ref,
    dup_ref,
):
    tokens, model = normed_ref.shape
    chunk = down_ref.shape[0]
    rows = left_ref.shape[0]
    length = tokens // rows
    slab = 32

    @pl.when(pl.program_id(0) == 0)
    def _():
        for row in range(rows):

            def collect(index, carry, row=row):
                base = pl.multiple_of(index * slab, slab)
                at = pl.ds(row * length + base, slab)
                low = gathered(parts_ref, at)
                place = base + lax.broadcasted_iota(jnp.int32, low.shape, 0)
                value = jnp.where(place < left_ref[row], low.astype(jnp.float32), 0.0)
                gout_ref[at, :] = value.astype(jnp.bfloat16)
                return carry

            lax.fori_loop(0, length // slab, collect, 0)

    tall = min(tokens, 512)
    wide = 256

    def tile(index, carry):
        at = pl.ds(pl.multiple_of(index * tall, tall), tall)
        for column in range(chunk // wide):
            own = slice(column * wide, (column + 1) * wide)
            gate = jnp.dot(normed_ref[at, :], gate_ref[:, own], preferred_element_type=jnp.float32)
            up = jnp.dot(normed_ref[at, :], up_ref[:, own], preferred_element_type=jnp.float32)
            dhid = lax.dot_general(
                gout_ref[at, :],
                down_ref[own, :],
                (((1,), (1,)), ((), ())),
                preferred_element_type=jnp.float32,
            )
            act, slope = gelu_pair(gate)
            hidden_ref[at, own] = (act * up).astype(jnp.bfloat16)
            dgate_ref[at, own] = (dhid * up * slope).astype(jnp.bfloat16)
            dup_ref[at, own] = (dhid * act).astype(jnp.bfloat16)
        return carry

    lax.fori_loop(0, tokens // tall, tile, 0, unroll=True)


def back_kernel(
    hidden_ref,
    dgate_ref,
    dup_ref,
    gout_hbm,
    resid_hbm,
    gain_ref,
    gate_ref,
    up_ref,
    down_ref,
    result_ref,
    dres_ref,
    total_ref,
    back_ref,
    gout_ref,
    resid_ref,
    load_sem,
):
    tall, model = (hidden_ref.shape[0], gout_ref.shape[1])
    step, tile = (pl.program_id(0), pl.program_id(1))
    wide = 512
    contract = (((1,), (1,)), ((), ()))
    rows = pl.ds(pl.multiple_of(tile * tall, tall), tall)

    def loads():
        return (
            pltpu.make_async_copy(gout_hbm, gout_ref, load_sem.at[0]),
            pltpu.make_async_copy(resid_hbm, resid_ref, load_sem.at[1]),
        )

    @pl.when((step == 0) & (tile == 0))
    def _():
        for load in loads():
            load.start()

    def products(own):
        forth = jnp.dot(hidden_ref[...], down_ref[:, own], preferred_element_type=jnp.float32)
        back = lax.dot_general(
            dgate_ref[...], gate_ref[own, :], contract, preferred_element_type=jnp.float32
        ) + lax.dot_general(
            dup_ref[...], up_ref[own, :], contract, preferred_element_type=jnp.float32
        )
        return (forth, back)

    @pl.when(step == 0)
    def _():
        for first in range(0, model, wide):
            own = slice(first, first + wide)
            forth, back = products(own)
            total_ref[rows, own] = forth
            back_ref[rows, own] = back

    @pl.when(step > 0)
    def _():
        for first in range(0, model, wide):
            own = slice(first, first + wide)
            forth, back = products(own)
            total_ref[rows, own] += forth
            back_ref[rows, own] += back

    @pl.when((step == pl.num_programs(0) - 1) & (tile == 0))
    def _():
        for load in loads():
            load.wait()

    @pl.when(step == pl.num_programs(0) - 1)
    def _():
        parts, width = (result_ref.shape[0], result_ref.shape[2])
        small = 16

        def finish(index, carry):
            at = pl.ds(pl.multiple_of(tile * tall + index * small, small), small)
            resid = resid_ref[at, :]
            result = (resid + total_ref[at, :]).astype(jnp.bfloat16)
            for part in range(parts):
                result_ref[part, at, :] = result[:, part * width : (part + 1) * width]
            inverse = lax.rsqrt(jnp.mean(resid * resid, axis=1, keepdims=True) + EPS)
            normed = resid * inverse
            scaled = back_ref[at, :] * gain_ref[...]
            mean = jnp.mean(scaled * normed, axis=1, keepdims=True)
            dres = gout_ref[at, :].astype(jnp.float32) + inverse * (scaled - normed * mean)
            dres_ref[at, :] = dres.astype(jnp.bfloat16)
            return carry

        lax.fori_loop(0, tall // small, finish, 0, unroll=4)


MLP_CHUNK = 768


def resident(shape):
    return pl.BlockSpec(shape, lambda s: (0,) * len(shape), pipeline_mode=pl.Buffered(1))


def mlp_specs(tokens, model):
    columns = pl.BlockSpec((model, MLP_CHUNK), lambda s: (0, s))
    down = pl.BlockSpec((MLP_CHUNK, model), lambda s: (s, 0))
    made = pl.BlockSpec((tokens, MLP_CHUNK), lambda s: (0, s))
    return ([columns, columns, down], [made] * 3)


def mlp_hidden(left, parts, normed, mlp_gate, mlp_up, mlp_down):
    tokens, model = normed.shape
    ffn = mlp_gate.shape[1]
    low = jnp.bfloat16
    weights, made = mlp_specs(tokens, model)
    tall = jax.ShapeDtypeStruct((tokens, ffn), low)
    return pl.pallas_call(
        hidden_kernel,
        name="mlp_hidden",
        grid=(ffn // MLP_CHUNK,),
        in_specs=[
            pl.BlockSpec(memory_space=pltpu.SMEM),
            resident(parts.shape),
            resident(normed.shape),
            *weights,
        ],
        out_specs=[resident((tokens, model)), *made],
        out_shape=[jax.ShapeDtypeStruct((tokens, model), low), tall, tall, tall],
        compiler_params=pltpu.CompilerParams(vmem_limit_bytes=VMEM_BYTES),
        cost_estimate=pl.CostEstimate(
            flops=6 * tokens * model * ffn,
            bytes_accessed=6 * (model + tokens) * ffn + 6 * tokens * model,
            transcendentals=0,
        ),
    )(left, parts, normed, mlp_gate, mlp_up, mlp_down)


def mlp_back(hidden, dgate, dup, gout, resid, gain, mlp_gate, mlp_up, mlp_down, parts_shape):
    tokens, model = resid.shape
    ffn = mlp_gate.shape[1]
    low, f32 = (jnp.bfloat16, jnp.float32)
    chunk, tall = (1024, min(tokens, 512))

    def resident(shape):
        return pl.BlockSpec(shape, lambda s, t: (0,) * len(shape), pipeline_mode=pl.Buffered(1))

    columns = pl.BlockSpec((model, chunk), lambda s, t: (0, s))
    down = pl.BlockSpec((chunk, model), lambda s, t: (s, 0))
    made = pl.BlockSpec((tall, chunk), lambda s, t: (t, s))
    return pl.pallas_call(
        back_kernel,
        name="mlp_back",
        grid=(ffn // chunk, tokens // tall),
        in_specs=[
            made,
            made,
            made,
            pl.BlockSpec(memory_space=pl.ANY),
            pl.BlockSpec(memory_space=pl.ANY),
            resident((1, model)),
            columns,
            columns,
            down,
        ],
        out_specs=[resident(parts_shape), resident((tokens, model))],
        out_shape=[
            jax.ShapeDtypeStruct(parts_shape, low),
            jax.ShapeDtypeStruct((tokens, model), low),
        ],
        scratch_shapes=[
            pltpu.VMEM((tokens, model), f32),
            pltpu.VMEM((tokens, model), f32),
            pltpu.VMEM((tokens, model), low),
            pltpu.VMEM((tokens, model), f32),
            pltpu.SemaphoreType.DMA((2,)),
        ],
        compiler_params=pltpu.CompilerParams(vmem_limit_bytes=VMEM_BYTES),
        cost_estimate=pl.CostEstimate(
            flops=6 * tokens * model * ffn,
            bytes_accessed=6 * (model + tokens) * ffn + 10 * tokens * model,
            transcendentals=0,
        ),
    )(hidden, dgate, dup, gout, resid, gain[None], mlp_gate, mlp_up, mlp_down)


def outputs_kernel(
    device_ref,
    own_ref,
    gate_sum,
    in_sum,
    out_sum,
    small_ref,
    input_ref,
    gate_ref,
    mlp_gate_ref,
    mlp_up_ref,
    gain1_ref,
    gain2_ref,
    sum_gain1,
    sum_in,
    sum_gate,
    sum_taps,
    sum_bias,
    sum_lgates,
    sum_lbias,
    sum_decay,
    sum_out,
    sum_gain2,
    sum_mgate,
    sum_mup,
    sum_down,
):
    rows = sum_mgate.shape[0]
    model = own_ref.shape[1]
    parts = sum_mgate.shape[1] // model
    for part in range(parts):
        at = slice(part * model, (part + 1) * model)
        sum_mgate[:, at] = own_ref[part * rows : (part + 1) * rows, :].astype(jnp.float32)
        sum_mup[:, at] = own_ref[(parts + part) * rows : (parts + part + 1) * rows, :].astype(
            jnp.float32
        )
    sum_down[...] = own_ref[2 * parts * rows :, :].astype(jnp.float32)

    def weighed(*pairs):
        return sum(
            jnp.sum(weight[...].astype(jnp.float32) * gradient[...], axis=1, keepdims=True)
            for weight, gradient in pairs
        )

    def as_row(column, gain):
        lane = lax.broadcasted_iota(jnp.int32, (rows, LANES), 1)
        place = lax.broadcasted_iota(jnp.int32, (rows, LANES), 0)
        whole = lax.broadcasted_iota(jnp.int32, (rows, model), 1)
        own = device_ref[0] * rows + lax.broadcasted_iota(jnp.int32, (rows, model), 0)
        own_gain = jnp.sum(jnp.where(whole == own, gain[...], 0.0), axis=1, keepdims=True)
        return jnp.sum(jnp.where(lane == place, column / own_gain, 0.0), axis=0, keepdims=True)

    row1 = as_row(weighed((input_ref, in_sum), (gate_ref, gate_sum)), gain1_ref)
    row2 = as_row(weighed((mlp_gate_ref, sum_mgate), (mlp_up_ref, sum_mup)), gain2_ref)
    sum_gain1[...] = row1[:, :rows]
    sum_gain2[...] = row2[:, :rows]
    sum_in[...] = in_sum[...]
    sum_gate[...] = gate_sum[...]
    sum_out[...] = out_sum[...]
    channels = small_ref.shape[0]
    size = sum_lgates.shape[1] // 2
    first, second = (small_ref[:, :LANES], small_ref[:, LANES:])
    lane = lax.broadcasted_iota(jnp.int32, (channels, LANES), 1)
    moved = pltpu.roll(second, size, 1)
    sum_lgates[:, :LANES] = jnp.where(lane < size, first, moved)
    sum_lgates[:, LANES:] = moved[:, : 2 * size - LANES]
    filled = jnp.concatenate([first, jnp.zeros((LANES - channels, LANES), jnp.float32)], axis=0)
    turned = filled.T
    sum_taps[...] = turned[size : size + 4, :channels]
    sum_bias[...] = turned[size + 4 : size + 5, :channels]
    sum_lbias[...] = turned[size + 5 : size + 7, :channels]
    sum_decay[...] = turned[size + 7 : size + 8, :channels]


def outputs(
    device, own, gate_sum, in_sum, out_sum, small, recur_input, recur_gate, mlp_gate, mlp_up, gain1, gain2, size
):
    rows, rec = in_sum.shape
    model, ffn = mlp_gate.shape
    channels = small.shape[0]
    f32 = jnp.float32

    def whole(shape):
        return pl.BlockSpec(shape, lambda s, device: (0,) * len(shape))

    def mine(shape):
        return pl.BlockSpec(shape, lambda s, device: (device[0], 0))

    given = (own, gate_sum, in_sum, out_sum, small)
    shapes = [(1, rows), (rows, rec), (rows, rec), (4, channels), (1, channels)]
    shapes += [(channels, 2 * size), (2, channels), (1, channels), out_sum.shape, (1, rows)]
    shapes += [(rows, ffn), (rows, ffn), (own.shape[0] - 2 * ffn // model * rows, model)]
    return pl.pallas_call(
        outputs_kernel,
        name="outputs",
        grid_spec=pltpu.PrefetchScalarGridSpec(
            num_scalar_prefetch=1,
            grid=(1,),
            in_specs=[whole(a.shape) for a in given]
            + [mine((rows, rec))] * 2
            + [mine((rows, ffn))] * 2
            + [whole((1, model))] * 2,
            out_specs=[whole(shape) for shape in shapes],
        ),
        out_shape=[jax.ShapeDtypeStruct(shape, f32) for shape in shapes],
        compiler_params=pltpu.CompilerParams(vmem_limit_bytes=VMEM_BYTES),
    )(
        device[None],
        *given,
        recur_input,
        recur_gate,
        mlp_gate,
        mlp_up,
        gain1[None],
        gain2[None],
    )


def spread_kernel(whole_ref, out_ref):
    out_ref[0] = whole_ref[...]


def spread(whole, count):
    tokens, width = (whole.shape[0], whole.shape[1] // count)
    return pl.pallas_call(
        spread_kernel,
        name="spread_features",
        grid=(count,),
        in_specs=[pl.BlockSpec((tokens, width), lambda j: (0, j))],
        out_specs=pl.BlockSpec((1, tokens, width), lambda j: (j, 0, 0)),
        out_shape=jax.ShapeDtypeStruct((count, tokens, width), whole.dtype),
        cost_estimate=pl.CostEstimate(
            flops=0, bytes_accessed=4 * tokens * whole.shape[1], transcendentals=0
        ),
    )(whole)


CHAN = ("zed", "core")


def features_in(local, pick=slice(None)):
    count = lax.axis_size(CHAN)
    rows, length, width = local.shape
    local = local.reshape(count, rows // count, length, width)[:, pick]
    if width % LANES == 0:
        return lax.all_to_all(local, CHAN, 0, 0, tiled=True).reshape(count, -1, width)
    moved = lax.all_to_all(
        local.reshape(-1, length, width), CHAN, split_axis=0, concat_axis=2, tiled=True
    )
    return moved.reshape(1, -1, count * width)


def features_apart(whole):
    count = lax.axis_size(CHAN)
    if (whole.shape[1] // count) % LANES == 0:
        return spread(whole, count)
    return whole[None]


def features_out(parts, rows):
    blocks, tokens, width = parts.shape
    parts = parts.reshape(blocks, rows, tokens // rows, width)
    if blocks > 1:
        moved = lax.all_to_all(parts, CHAN, 0, 0, tiled=True)
        return moved.reshape(-1, *parts.shape[2:])
    return lax.all_to_all(parts[0], CHAN, split_axis=2, concat_axis=0, tiled=True)


class Corners:
    def __init__(self, seq, zed):
        self.seq_bits, self.zed_bits = (seq.bit_length() - 1, zed.bit_length() - 1)
        self.count = self.seq_bits + self.zed_bits
        self.dims = (2,) * self.count
        self.low = tuple(range(self.seq_bits))[::-1] + tuple(range(self.seq_bits, self.count))[::-1]
        self.high = tuple(range(self.seq_bits)) + tuple(range(self.seq_bits, self.count))[::-1]

    def place(self, dim):
        if dim < self.seq_bits:
            return ("seq", 2 ** (self.seq_bits - 1 - dim))
        return ("zed", 2 ** (self.count - 1 - dim))

    def bit(self, dim):
        axis, weight = self.place(dim)
        return lax.rem(lax.div(lax.axis_index(axis), weight), 2)

    def partner(self, dim):
        axis, weight = self.place(dim)
        return {axis: lax.axis_index(axis) + weight * (1 - 2 * self.bit(dim))}


def tail_kernel(
    corners,
    orders,
    dgate_hbm,
    dbranch_hbm,
    ending_ref,
    leading_ref,
    mixed_hbm,
    dres_hbm,
    gain_ref,
    input_hbm,
    gate_hbm,
    small_hbm,
    *refs,
):
    rows = ending_ref.shape[0]
    normed_hbms, x_hbms, inverse_hbms = (refs[k * rows : (k + 1) * rows] for k in range(3))
    tokens_ref, sum_gate, sum_out, sum_in, sum_small = refs[3 * rows : 3 * rows + 5]
    refs = refs[3 * rows + 5 :]
    stages = corners.count + 1
    dgate, dbranch, mixed, dres, normed, x, inverse, weight_in, weight_gate = refs[:9]
    made_in, made_out, own_small, back, parts, rim = refs[9:15]
    slots_in, slots_out, slots_small = (
        refs[15 + k * stages : 15 + (k + 1) * stages] for k in range(3)
    )
    (
        send_sem,
        recv_sem,
        load_sem,
        move_send,
        move_recv,
        keep_sem,
        rim_send,
        rim_recv,
    ) = refs[15 + 3 * stages :]
    seq, zed, core = (lax.axis_index(axis) for axis in ("seq", "zed", "core"))
    seqs, group = (lax.axis_size("seq"), 2 * lax.axis_size("zed"))
    mine = zed * 2 + core
    length = tokens_ref.shape[1]
    model = x.shape[1]

    def member(index):
        return {"zed": lax.div(index, 2), "core": lax.rem(index, 2)}

    def by_row(sources, target):
        return [
            (source, target.at[pl.ds(row * length, length)]) for row, source in enumerate(sources)
        ]

    pairs = [
        (dbranch_hbm, dbranch),
        (input_hbm, weight_in),
        (dgate_hbm, dgate),
        (gate_hbm, weight_gate),
        *by_row(x_hbms, x),
        *by_row(inverse_hbms, inverse),
        (dres_hbm, dres),
        *by_row(normed_hbms, normed),
        (mixed_hbm, mixed),
        (small_hbm.at[(slice(None),) * corners.count + (core,)], own_small),
    ]
    kinds = []
    for name in ('dbranch', 'win', 'dgate', 'wgate', 'x', 'inverse', 'dres', 'normed', 'mixed', 'small'):
        kinds += [name] * (rows if name in ("normed", "x", "inverse") else 1)
    loads = [
        pltpu.make_async_copy(source, target, load_sem.at[place])
        for place, (source, target) in enumerate(pairs)
    ]
    for load in loads:
        load.start()

    barrier = pltpu.get_barrier_semaphore()
    for other in range(1, group):
        pl.semaphore_signal(
            barrier, inc=1, device_id=member(lax.rem(mine + other, group)), device_id_type=MESH
        )
    for other in range(1, seqs):
        pl.semaphore_signal(
            barrier, inc=1, device_id={"seq": lax.rem(seq + other, seqs)}, device_id_type=MESH
        )
    pl.semaphore_wait(barrier, group - 1 + seqs - 1)

    rim_copy = pltpu.make_async_remote_copy(
        src_ref=leading_ref,
        dst_ref=rim,
        send_sem=rim_send,
        recv_sem=rim_recv,
        device_id={"seq": lax.rem(seq + seqs - 1, seqs)},
        device_id_type=MESH,
    )
    rim_copy.start()

    def own(stream, index):
        if stream < 4:
            return made_in.at[(stream,) + index + (core,)]
        if stream < 6:
            return made_out.at[(stream - 4,) + index + (core,)]
        return own_small.at[index]

    def slot(stream, stage):
        if stream < 4:
            return slots_in[stage].at[stream]
        if stream < 6:
            return slots_out[stage].at[stream - 4]
        return slots_small[stage]

    def copy(stream, stage):
        order = orders[stream]
        every = (slice(None),) * corners.count
        if stage == 0:
            if stream < 4:
                source = made_in.at[(stream,) + every + (1 - core,)]
            elif stream < 6:
                source = made_out.at[(stream - 4,) + every + (1 - core,)]
            else:
                source = small_hbm.at[every + (1 - core,)]
            target = {"core": 1 - core}
        else:
            dim = order[stage - 1]
            fixed = {before: corners.bit(before) for before in order[: stage - 1]}
            fixed[dim] = 1 - corners.bit(dim)
            source = own(stream, tuple(fixed.get(d, slice(None)) for d in range(corners.count)))
            target = corners.partner(dim)
        return pltpu.make_async_remote_copy(
            src_ref=source,
            dst_ref=slot(stream, stage),
            send_sem=send_sem.at[stream, stage],
            recv_sem=recv_sem.at[stream, stage],
            device_id=target,
            device_id_type=MESH,
        )

    sums = [
        sum_gate.at[:, : sum_gate.shape[1] // 2],
        sum_gate.at[:, sum_gate.shape[1] // 2 :],
        sum_in.at[:, : sum_in.shape[1] // 2],
        sum_in.at[:, sum_in.shape[1] // 2 :],
        sum_out.at[:, : sum_out.shape[1] // 2],
        sum_out.at[:, sum_out.shape[1] // 2 :],
        sum_small,
    ]

    def advance(stream, stage):
        order = orders[stream]
        copy(stream, stage).wait_recv()
        left = [dim for dim in range(corners.count) if dim not in order[:stage]]
        fixed = {dim: corners.bit(dim) for dim in order[:stage]}
        arrived = slot(stream, stage)
        if not left:
            index = tuple(fixed[dim] for dim in range(corners.count))
            sums[stream][...] = own(stream, index)[...].astype(jnp.float32) + arrived[...].astype(
                jnp.float32
            )
            return

        def add(index, carry):
            part = {
                dim: lax.rem(lax.div(index, 2 ** (len(left) - 1 - place)), 2)
                for place, dim in enumerate(left)
            }
            kept = own(stream, tuple({**fixed, **part}[dim] for dim in range(corners.count)))
            total = kept[...].astype(jnp.float32) + arrived[
                tuple(part[dim] for dim in left)
            ].astype(jnp.float32)
            kept[...] = total.astype(jnp.bfloat16)
            return carry

        lax.fori_loop(0, 2 ** len(left), add, 0)
        copy(stream, stage + 1).start()

    def move(other, row):
        to = lax.rem(mine + other, group)
        return pltpu.make_async_remote_copy(
            src_ref=parts.at[to, pl.ds(row * length, length)],
            dst_ref=tokens_ref.at[mine * rows + row],
            send_sem=move_send.at[other - 1, row],
            recv_sem=move_recv.at[other - 1, row],
            device_id=member(to),
            device_id_type=MESH,
        )

    def keep(row):
        return pltpu.make_async_copy(
            parts.at[mine, pl.ds(row * length, length)],
            tokens_ref.at[mine * rows + row],
            keep_sem.at[row],
        )

    tile = 256
    width = parts.shape[2]

    def back_row(row):
        at_row = slice(row * length, (row + 1) * length)

        def product(index, carry):
            at = pl.ds(pl.multiple_of(index * tile, tile), tile)
            contract = (((1,), (1,)), ((), ()))
            back[:, at] = lax.dot_general(
                dbranch[at_row, :], weight_in[at, :], contract, preferred_element_type=jnp.float32
            ) + lax.dot_general(
                dgate[at_row, :], weight_gate[at, :], contract, preferred_element_type=jnp.float32
            )
            return carry

        lax.fori_loop(0, model // tile, product, 0)
        slab = 16

        def norm(index, carry):
            base = pl.multiple_of(index * slab, slab)
            at = pl.ds(row * length + base, slab)
            inv = inverse[at, :1]
            value = x[at, :].astype(jnp.float32) * inv
            scaled = back[pl.ds(base, slab), :] * gain_ref[...]
            mean = jnp.mean(scaled * value, axis=1, keepdims=True)
            grad = dres[at, :].astype(jnp.float32) + inv * (scaled - value * mean)
            grad = grad.astype(jnp.bfloat16)
            for part in range(parts.shape[0]):
                parts[part, at, :] = grad[:, part * width : (part + 1) * width]
            return carry

        lax.fori_loop(0, length // slab, norm, 0, unroll=4)
        for other in range(1, group):
            move(other, row).start()
        keep(row).start()

    def weight_product(left, right, made, stream, first):
        columns = made.shape[-1]
        shape = made.shape[1:-1]

        def product(index, carry):
            at = pl.ds(pl.multiple_of(index * tile, tile), tile)
            source = pl.ds(pl.multiple_of(first + index * tile, tile), tile)
            part = lax.dot_general(
                left[...],
                right[:, source],
                (((0,), (0,)), ((), ())),
                preferred_element_type=jnp.float32,
            )
            made[(stream,) + (slice(None),) * len(shape) + (at,)] = part.astype(
                jnp.bfloat16
            ).reshape(shape + (tile,))
            return carry

        lax.fori_loop(0, columns // tile, product, 0)

    half, half_out = (made_in.shape[-1], made_out.shape[-1])
    waited, reached = (set(), {})

    def need(*names):
        for place, name in enumerate(kinds):
            if name in names and place not in waited:
                waited.add(place)
                loads[place].wait()

    def fix_rim():
        need("dbranch")
        rim_copy.wait()
        live = jnp.where(seq < seqs - 1, 1.0, 0.0)
        for row in range(rows):
            at = slice((row + 1) * length - STEP, (row + 1) * length)
            inside = dbranch[at, :].astype(jnp.float32)
            last = ending_ref[row] + live * rim[row]
            dbranch[at, :] = jnp.concatenate([inside[: STEP - SUBLANES], last], axis=0).astype(
                jnp.bfloat16
            )

    def begin(stream):
        copy(stream, 0).start()
        reached[stream] = 0

    def progress(streams):
        for stream in streams:
            if stream in reached and reached[stream] < stages:
                if stream == 6:
                    need("small")
                advance(stream, reached[stream])
                reached[stream] += 1

    def compute(item):
        if item == "gate":
            need("normed", "dgate")
            for stream in (0, 1):
                weight_product(normed, dgate, made_in, stream, stream * half)
                begin(stream)
        elif item == "out":
            need("mixed", "dres")
            for stream in (4, 5):
                weight_product(mixed, dres, made_out, stream - 4, (stream - 4) * half_out)
                begin(stream)
        elif item == "in":
            need("normed", "dbranch")
            for stream in (2, 3):
                weight_product(normed, dbranch, made_in, stream, (stream - 2) * half)
                begin(stream)
        else:
            need("dbranch", "dgate", "win", "wgate", "x", "inverse", "dres")
            back_row(item)

    begin(6)
    fix_rim()
    compute(0)
    compute(1)
    compute('gate')
    progress((6,))
    compute('out')
    progress((0, 1))
    compute('in')
    progress((0, 1))
    progress((4, 5))
    progress((6,))
    while any(reached[stream] < stages for stream in range(7)):
        progress((0, 1, 4, 5, 2, 3, 6))
    for stage in range(stages):
        for stream in range(7):
            copy(stream, stage).wait_send()
    for row in range(rows):
        for other in range(1, group):
            move(other, row).wait()
        keep(row).wait()


def tail(dgate, dbranch, ending, leading, mixed, dres, gain, w_in, w_gate, small, normed, x, inverse):
    corners = Corners(lax.axis_size("seq"), lax.axis_size("zed"))
    group, devices = (lax.axis_size(CHAN), 2 ** (corners.count + 1))
    tokens, model = dres.shape
    rec = dgate.shape[1]
    rows = ending.shape[0]
    length, width = (tokens // rows, model // group)
    low, f32 = (jnp.bfloat16, jnp.float32)
    stages = corners.count + 1
    in_rows, out_rows = (model // devices, rec // devices)
    small = small.reshape(corners.dims + (2, out_rows, small.shape[1]))
    orders = [corners.low, corners.high] * 3 + [corners.low]

    def slots(lead, shape):
        return [pltpu.VMEM(lead + (2,) * (corners.count - k) + shape, low) for k in range(stages)]

    in_shape, out_shape = ((in_rows, rec // 2), (out_rows, model // 2))
    loaded = (dgate, dbranch, mixed, dres, dres, dres)
    loaded += (jax.ShapeDtypeStruct((tokens, LANES), f32), w_in, w_gate)
    anyplace = pl.BlockSpec(memory_space=pl.ANY)
    vmem = pl.BlockSpec(memory_space=pltpu.VMEM)
    dma = pltpu.SemaphoreType.DMA
    moved = sum(math.prod(a.shape) * a.dtype.itemsize for a in loaded)
    return pl.pallas_call(
        functools.partial(tail_kernel, corners, orders),
        name="tail",
        in_specs=[anyplace, anyplace, vmem, vmem, anyplace, anyplace, vmem]
        + [anyplace] * (3 + 3 * rows),
        out_specs=[anyplace] + [vmem] * 4,
        out_shape=[
            jax.ShapeDtypeStruct((group * rows, length, width), low),
            jax.ShapeDtypeStruct((in_rows, rec), f32),
            jax.ShapeDtypeStruct((out_rows, model), f32),
            jax.ShapeDtypeStruct((in_rows, rec), f32),
            jax.ShapeDtypeStruct(small.shape[-2:], f32),
        ],
        scratch_shapes=[pltpu.VMEM(a.shape, a.dtype) for a in loaded]
        + [
            pltpu.VMEM((4,) + corners.dims + (2,) + in_shape, low),
            pltpu.VMEM((2,) + corners.dims + (2,) + out_shape, low),
            pltpu.VMEM(corners.dims + small.shape[-2:], low),
            pltpu.VMEM((length, model), f32),
            pltpu.VMEM((group, tokens, width), low),
            pltpu.VMEM(leading.shape, leading.dtype),
        ]
        + slots((4,), in_shape)
        + slots((2,), out_shape)
        + slots((), small.shape[-2:])
        + [
            dma((7, stages)),
            dma((7, stages)),
            dma((7 + 3 * rows,)),
            dma((group - 1, rows)),
            dma((group - 1, rows)),
            dma((rows,)),
            dma,
            dma,
        ],
        compiler_params=pltpu.CompilerParams(
            collective_id=1, has_side_effects=True, vmem_limit_bytes=60 * 1024 * 1024
        ),
        cost_estimate=pl.CostEstimate(
            flops=10 * tokens * model * rec, bytes_accessed=2 * moved, transcendentals=0
        ),
    )(dgate, dbranch, ending, leading, mixed, dres, gain[None], w_in, w_gate, small, *normed, *x, *inverse)


def grads_kernel(
    normed_ref,
    dgate_ref,
    dup_ref,
    hidden_ref,
    gout_ref,
    out_ref,
    made_wide,
    made_down,
    come_wide,
    come_down,
    send_sem,
    recv_sem,
    store_sem,
):
    step = pl.program_id(0)
    core = lax.axis_index("core")
    other = {"core": 1 - core}
    wide_rows, down_rows = (made_wide.shape[3], made_down.shape[3])
    wides, downs = (come_wide.shape[0], come_down.shape[0])
    total = wides + downs
    down_at = wides * wide_rows

    def exchange(made, come, index, slot):
        return pltpu.make_async_remote_copy(
            src_ref=made.at[lax.rem(index, 3), 1 - core],
            dst_ref=come.at[index],
            send_sem=send_sem.at[slot],
            recv_sem=recv_sem.at[slot],
            device_id=other,
            device_id_type=MESH,
        )

    def store_wide(index):
        return pltpu.make_async_copy(
            come_wide.at[index],
            out_ref.at[:, pl.ds(pl.multiple_of(index * wide_rows, wide_rows), wide_rows)],
            store_sem.at[index],
        )

    def store_down(index):
        chips = come_down.shape[1]
        return pltpu.make_async_copy(
            come_down.at[index],
            out_ref.at[pl.ds(index * chips, chips), pl.ds(down_at, down_rows)],
            store_sem.at[index + wides],
        )

    @pl.when(step == 0)
    def _():
        barrier = pltpu.get_barrier_semaphore()
        pl.semaphore_signal(barrier, inc=1, device_id=other, device_id_type=MESH)
        pl.semaphore_wait(barrier, 1)

    def product_wide(source, index):
        made = made_wide.at[lax.rem(index, 3)]
        chips, rows = (made.shape[1], made.shape[2])
        tile = 512

        def column(place, carry):
            at = pl.ds(pl.multiple_of(place * tile, tile), tile)
            part = lax.dot_general(
                normed_ref[...], source[:, at], (((0,), (0,)), ((), ())), preferred_element_type=jnp.float32
            )
            part = part.astype(jnp.bfloat16).reshape(chips, 2, rows, tile)
            made[0, :, :, at] = part[:, 0]
            made[1, :, :, at] = part[:, 1]
            return carry

        lax.fori_loop(0, source.shape[1] // tile, column, 0, unroll=True)

    def product_tall(left, right, made_all, index):
        made = made_all.at[lax.rem(index, 3)]
        chips, rows = (made.shape[1], made.shape[2])
        tile = 512

        def column(place, carry):
            at = pl.ds(pl.multiple_of(place * tile, tile), tile)
            part = lax.dot_general(
                left[...], right[:, at], (((0,), (0,)), ((), ())), preferred_element_type=jnp.float32
            )
            part = part.astype(jnp.bfloat16).reshape(chips, 2, rows, tile)
            made[0, :, :, at] = part[:, 0]
            made[1, :, :, at] = part[:, 1]
            return carry

        lax.fori_loop(0, right.shape[1] // tile, column, 0, unroll=True)

    half = wides // 2

    @pl.when(step < half)
    def _():
        product_wide(dgate_ref, step)

    @pl.when((step >= half) & (step < wides))
    def _():
        product_wide(dup_ref, step)

    @pl.when(step < wides)
    def _():
        exchange(made_wide, come_wide, step, step).start()

    @pl.when((step >= wides) & (step < total))
    def _():
        product_tall(hidden_ref, gout_ref, made_down, step - wides)
        exchange(made_down, come_down, step - wides, step).start()

    def finish(made, come, index, slot, store):
        exchange(made, come, index, slot).wait()
        mine = made.at[lax.rem(index, 3), core]
        arrived = come.at[index]

        def add(chip, carry):
            both = mine[chip].astype(jnp.float32) + arrived[chip].astype(jnp.float32)
            arrived[chip] = both.astype(jnp.bfloat16)
            return carry

        lax.fori_loop(0, come.shape[1], add, 0, unroll=4)
        store(index).start()

    before = step - 2

    @pl.when((before >= 0) & (before < wides))
    def _():
        finish(made_wide, come_wide, before, before, store_wide)

    @pl.when(before >= wides)
    def _():
        finish(made_down, come_down, before - wides, before, store_down)

    @pl.when(step == total + 1)
    def _():
        for index in range(wides):
            store_wide(index).wait()
        for index in range(downs):
            store_down(index).wait()


def block_gradients(normed, dgate, dup, hidden, gout):
    tokens, model = normed.shape
    ffn = hidden.shape[1]
    chips = lax.axis_size("seq") * lax.axis_size("zed")
    devices = 2 * chips
    wide_rows, down_rows = (model // devices, ffn // devices)
    chunk = 768
    wides, downs = (2 * ffn // model, ffn // chunk)
    half = wides // 2
    down_chips = chunk // (2 * down_rows)
    rows = wides * wide_rows + down_rows
    low = jnp.bfloat16

    def whole(array):
        return pl.BlockSpec(array.shape, lambda s: (0, 0), pipeline_mode=pl.Buffered(1))

    def part(columns, first, count):
        return pl.BlockSpec((tokens, columns), lambda s: (0, jnp.clip(s - first, 0, count - 1)))

    total = wides + downs
    flops = 6 * tokens * model * ffn
    arrays = (normed, dgate, dup, hidden, gout)
    moved = sum(math.prod(a.shape) * 2 for a in arrays) + chips * rows * model * 2
    return pl.pallas_call(
        grads_kernel,
        name="block_gradients",
        grid=(total + 2,),
        in_specs=[
            whole(normed),
            part(model, 0, half),
            part(model, half, half),
            part(chunk, wides, downs),
            whole(gout),
        ],
        out_specs=pl.BlockSpec(memory_space=pl.ANY),
        out_shape=jax.ShapeDtypeStruct((chips, rows, model), low),
        scratch_shapes=[
            pltpu.VMEM((3, 2, chips, wide_rows, model), low),
            pltpu.VMEM((3, 2, down_chips, down_rows, model), low),
            pltpu.VMEM((wides, chips, wide_rows, model), low),
            pltpu.VMEM((downs, down_chips, down_rows, model), low),
            pltpu.SemaphoreType.DMA((total,)),
            pltpu.SemaphoreType.DMA((total,)),
            pltpu.SemaphoreType.DMA((total,)),
        ],
        compiler_params=pltpu.CompilerParams(
            collective_id=2, has_side_effects=True, vmem_limit_bytes=VMEM_BYTES
        ),
        cost_estimate=pl.CostEstimate(flops=flops, bytes_accessed=moved, transcendentals=0),
    )(*arrays)


def passed_along(value, axis, steps):
    count = lax.axis_size(axis)
    leading, last = (max(0, -steps), min(count, count - steps))
    return lax.ppermute(value, axis, [(source, source + steps) for source in range(leading, last)])


def weight_grad(left, right):
    return lax.dot_general(
        left, right, (((0,), (0,)), ((), ())), preferred_element_type=jnp.float32
    ).astype(jnp.bfloat16)


def back_dot(left, right):
    return lax.dot_general(
        left, right, (((1,), (1,)), ((), ())), preferred_element_type=jnp.float32
    )


def fwd_dot(left, right):
    return jnp.dot(left, right, preferred_element_type=jnp.float32)


def gelu_fn(value):
    return jax.nn.gelu(value, approximate=True)


def norm_back(grad_norm, normed, inverse, gain):
    scaled = grad_norm * gain
    mean_term = jnp.mean(scaled * normed, axis=1, keepdims=True)
    return inverse * (scaled - normed * mean_term)


def scattered(gradient):
    return lax.psum_scatter(
        gradient, ("seq", "zed", "core"), scatter_dimension=0, tiled=True
    ).astype(jnp.float32)


def body(
    tokens,
    cotangent,
    doc_starts,
    lengths,
    norm1_gain,
    recur_input,
    recur_gate,
    conv_kernel,
    conv_bias,
    lru_gates,
    lru_bias,
    lru_decay,
    recur_out,
    norm2_gain,
    mlp_gate,
    mlp_up,
    mlp_down,
):
    count = lax.axis_size(CHAN)
    row_count, block_len = (tokens.shape[0] // count, tokens.shape[1])
    model_dim = tokens.shape[2] * count
    tok_count = row_count * block_len
    rec_width = recur_input.shape[1]
    ffn_width = mlp_gate.shape[1]
    head_count = H
    head_size = rec_width // head_count
    tap_count = conv_kernel.shape[0]
    rim_size = tap_count - 1
    seq_index = lax.axis_index("seq")
    position = seq_index * block_len + jnp.arange(block_len, dtype=jnp.int32)
    bounds = jnp.concatenate([doc_starts, lengths[:, None]], axis=1)
    is_before = bounds[:, None, :] <= position[None, :, None]
    seg_start = jnp.max(jnp.where(is_before, bounds[:, None, :], 0), axis=2)
    dist = jnp.broadcast_to(
        (position[None, :] - seg_start)[:, :, None], (row_count, block_len, LANES)
    )
    soft_decay = jax.nn.softplus(-lru_decay)
    params = jnp.concatenate(
        [
            conv_kernel,
            conv_bias[None],
            lru_bias,
            (-8.0 * soft_decay)[None],
            (8.0 * jax.nn.sigmoid(-lru_decay))[None],
            jnp.zeros((SUBLANES - 1, rec_width), jnp.float32),
        ],
        axis=0,
    )
    core = Recurrence(row_count, block_len, rec_width, head_size)
    wide_gates = core.widen(lru_gates)
    if tokens.shape[2] % LANES == 0:
        blocks = [features_in(tokens, slice(0, 1))]
        later, wide_gates, params, dist = lax.optimization_barrier(
            (tokens, wide_gates, params, dist)
        )
        blocks += [features_in(later, slice(row, row + 1)) for row in range(1, row_count)]
    else:
        side = features_in(tokens)
        blocks = [side[:, row * block_len : (row + 1) * block_len] for row in range(row_count)]
    per_row = []
    for row in range(row_count):
        block = blocks[row]
        if row:
            block, _ = lax.optimization_barrier((block, per_row[-1][-1]))
        per_row.append(
            front(
                block,
                norm1_gain,
                recur_input,
                recur_gate,
                dist[row : row + 1],
                params,
                wide_gates,
            )
        )
    low_x, inverse, normed_low, branch, gate_pre, rim, lru_in, rate, igate, state, cum, last = zip(
        *per_row
    )
    entering, mixed_low, resid_one, normed_low2 = middle(
        last, state, cum, gate_pre, low_x, recur_out, norm2_gain
    )
    cotangent, _ = lax.optimization_barrier((cotangent, block))
    cotangent, resid_one = lax.optimization_barrier((features_in(cotangent), resid_one))
    grad_low, hidden_low, mgate_low, mup_low = mlp_hidden(
        lengths - seq_index * block_len, cotangent, normed_low2, mlp_gate, mlp_up, mlp_down
    )
    devices = lax.axis_size(("seq", "zed", "core"))
    own_rows = model_dim // devices
    tiled = own_rows % (2 * SUBLANES) == 0 and tokens.shape[2] % LANES == 0
    if tiled:
        merged = block_gradients(normed_low2, mgate_low, mup_low, hidden_low, grad_low)
        merged, hidden_low = lax.optimization_barrier((merged, hidden_low))
        merged = lax.psum_scatter(merged, "seq", scatter_dimension=0, tiled=True)
    result_parts, resid_low = mlp_back(
        hidden_low,
        mgate_low,
        mup_low,
        grad_low,
        resid_one,
        norm2_gain,
        mlp_gate,
        mlp_up,
        mlp_down,
        cotangent.shape,
    )
    output = features_out(result_parts, row_count)
    gate_low, back_local, back_cum, first_term = core.adjoint(
        resid_low,
        recur_out,
        gate_pre,
        state,
        cum,
        entering,
        rate,
        dist,
        params,
    )
    gate_low = gate_low.reshape(tok_count, rec_width)

    def zed_stage(leaving):
        if not tiled:
            return ((), leaving)
        done, leaving = lax.optimization_barrier((merged, leaving))
        return (lax.psum_scatter(done, "zed", scatter_dimension=0, tiled=True), leaving)

    branch_local, ending, leading, small, merged_own = core.backward(
        back_local,
        back_cum,
        first_term,
        last,
        state,
        cum,
        entering,
        rate,
        igate,
        lru_in,
        dist,
        branch,
        rim,
        params,
        wide_gates,
        zed_stage,
    )
    branch_low = branch_local.reshape(tok_count, rec_width)
    if tiled:
        output, branch_low = lax.optimization_barrier((output, branch_low))
        grad_tokens, sum_rgate, sum_rout, sum_rin, own_small = tail(
            gate_low,
            branch_low,
            ending,
            leading,
            mixed_low,
            resid_low,
            norm1_gain,
            recur_input,
            recur_gate,
            small,
            normed_low,
            low_x,
            inverse,
        )
        device = lax.axis_index(("seq", "zed", "core"))
        sums = outputs(
            device,
            merged_own[0],
            sum_rgate,
            sum_rin,
            sum_rout,
            own_small,
            recur_input,
            recur_gate,
            mlp_gate,
            mlp_up,
            norm1_gain,
            norm2_gain,
            head_size,
        )
        flat = (0, 4, 7, 9)
        sums = [part.reshape(-1) if place in flat else part for place, part in enumerate(sums)]
        return (output, grad_tokens, *sums)
    else:
        from_next = passed_along(
            leading[:, SUBLANES - rim_size :, :].astype(jnp.bfloat16), "seq", -1
        )
        ending = ending + jnp.pad(
            from_next.astype(jnp.float32), ((0, 0), (SUBLANES - rim_size, 0), (0, 0))
        )
        branch_low = lax.dynamic_update_slice(
            branch_local, ending.astype(jnp.bfloat16), (0, block_len - SUBLANES, 0)
        ).reshape(tok_count, rec_width)
        grad_norm1 = back_dot(branch_low, recur_input) + back_dot(gate_low, recur_gate)
        inv_one = jnp.concatenate(inverse)[:, :1]
        normed_one = jnp.concatenate(low_x).astype(jnp.float32) * inv_one
        normed_low = jnp.concatenate(normed_low)
        input_part = norm_back(grad_norm1, normed_one, inv_one, norm1_gain)
        grad_x = (resid_low.astype(jnp.float32) + input_part).astype(jnp.bfloat16)
        grad_tokens = features_out(features_apart(grad_x), row_count)
        sum_mgate, sum_mup, sum_down, sum_rout, sum_rgate, sum_rin = (
            scattered(weight_grad(left, right))
            for left, right in (
                (normed_low2, mgate_low),
                (normed_low2, mup_low),
                (hidden_low, grad_low),
                (mixed_low, resid_low),
                (normed_low, gate_low),
                (normed_low, branch_low),
            )
        )
        own_small = scattered(small)
    sum_lgates = jnp.concatenate(
        [own_small[:, :head_size], own_small[:, LANES : LANES + head_size]], axis=1
    )
    own_sums = jnp.swapaxes(own_small[:, head_size : head_size + SUBLANES], 0, 1)
    device = lax.axis_index(("seq", "zed", "core"))

    def mine(array, size, axis=0):
        return lax.dynamic_slice_in_dim(array, device * size, size, axis)

    def weighed(weight, gradient):
        return jnp.sum(mine(weight, own_rows).astype(jnp.float32) * gradient, axis=1)

    sum_gain1 = (weighed(recur_input, sum_rin) + weighed(recur_gate, sum_rgate)) / mine(
        norm1_gain, own_rows
    )
    sum_gain2 = (weighed(mlp_gate, sum_mgate) + weighed(mlp_up, sum_mup)) / mine(
        norm2_gain, own_rows
    )
    sum_decay = own_sums[7]
    return (
        output,
        grad_tokens,
        sum_gain1,
        sum_rin,
        sum_rgate,
        own_sums[:4],
        own_sums[4],
        sum_lgates,
        own_sums[5:7],
        sum_decay,
        sum_rout,
        sum_gain2,
        sum_mgate,
        sum_mup,
        sum_down,
    )


def solution(mesh):
    seq, chan = (mesh.shape["seq"], mesh.shape["chan"])
    chips = jax.sharding.Mesh(mesh.devices.reshape(seq, chan // 2, 2), ("seq", "zed", "core"))
    chan = ("zed", "core")
    every = ("seq", "zed", "core")
    activations = P(None, "seq", chan)
    rows, columns, vector = (P(every, None), P(None, every), P(every))
    return jax.shard_map(
        body,
        mesh=chips,
        in_specs=(activations, activations, P(chan, None), P(chan)) + (P(),) * 13,
        out_specs=(
            activations,
            activations,
            vector,
            rows,
            rows,
            columns,
            vector,
            rows,
            columns,
            vector,
            rows,
            vector,
            rows,
            rows,
            rows,
        ),
        check_vma=False,
    )
```

```python
import functools
import math

import jax
import jax.numpy as jnp
from jax import lax
from jax.experimental import pallas as pl
from jax.experimental.pallas import tpu as pltpu
from jax.sharding import PartitionSpec as P

H = 16


EPS = 1e-06
ROOT_FLOOR = 1e-06
LANES = 128
SUBLANES = 8
STEP = 16
VMEM_BYTES = 56 * 1024 * 1024
MESH = pl.DeviceIdType.MESH


def sigmoid(value):
    return 0.5 * jnp.tanh(0.5 * value) + 0.5


GELU_C = 0.7978845608
GELU_A = 0.044715


def gelu_pair(value):
    square = value * value
    inner = jnp.tanh(value * (GELU_C + (GELU_C * GELU_A) * square))
    half = 0.5 + 0.5 * inner
    slope = GELU_C + (3.0 * GELU_C * GELU_A) * square
    return (value * half, half + 0.5 * value * (1.0 - inner * inner) * slope)


def root_argument(log_decay, decay):
    y = 2.0 * log_decay
    series = 1.0 + y * (0.5 + y * (1.0 / 6.0 + y * (1.0 / 24.0)))
    return jnp.where(y > -0.05, -y * series, 1.0 - decay * decay)


def across(column, width):
    return jnp.concatenate([column] * (width // LANES), axis=1)


class Rows:
    def __init__(self, refs):
        self.refs = refs

    def __getitem__(self, index):
        if not isinstance(index, tuple):
            return self.refs[index][0]
        return self.refs[index[0]][(0,) + index[1:]]


def by_rows(refs, rows, apart):
    found = []
    for split in apart:
        count = rows if split else 1
        found.append(Rows(refs[:count]) if split else refs[0])
        refs = refs[count:]
    return found, refs


def scan_block(
    branch_ref,
    rim_ref,
    dist_ref,
    par_ref,
    gates_ref,
    lru_ref,
    rate_ref,
    igate_ref,
    state_ref,
    cum_ref,
    last_ref,
    both_ref,
):
    rows, length, width = branch_ref.shape
    span = 2 * STEP if rows == 1 else STEP
    taps = [par_ref[k : k + 1, :] for k in range(4)]
    conv_bias, rate_bias, input_bias, soft = (par_ref[k : k + 1, :] for k in range(4, 8))
    place = lax.broadcasted_iota(jnp.int32, (SUBLANES, width), 0)

    for row in range(rows):

        def conv_step(index, before, row=row):
            base = pl.multiple_of(index * STEP, STEP)
            pieces = []
            for half in range(STEP // SUBLANES):
                at = pl.ds(base + half * SUBLANES, SUBLANES)
                here = branch_ref[row, at, :]
                dist = across(dist_ref[row, at, :], width)
                total = conv_bias + taps[0] * here
                for k in range(1, 4):
                    shifted = pltpu.roll(jnp.where(place < SUBLANES - k, here, before), k, 0)
                    total = total + taps[k] * jnp.where(dist >= k, shifted, 0.0)
                pieces.append(total)
                before = here
            lru_ref[row, pl.ds(base, STEP), :] = jnp.concatenate(pieces, axis=0).astype(jnp.bfloat16)
            return before

        lax.fori_loop(0, length // STEP, conv_step, rim_ref[row], unroll=2)

        piece = min(length, 256)

        def dot_step(index, carry, row=row):
            at = pl.ds(pl.multiple_of(index * piece, piece), piece)
            both_ref[row, at, :] = jnp.dot(
                lru_ref[row, at, :], gates_ref[...], preferred_element_type=jnp.float32
            )
            return carry

        lax.fori_loop(0, length // piece, dot_step, 0)

    def scan_step(index, carry):
        base = pl.multiple_of(index * span, span)
        later = []
        for row in range(rows):
            run_cum, run_state = carry[row]
            lru_both = lru_ref[row, pl.ds(base, span), :].astype(jnp.float32)
            for half in range(span // SUBLANES):
                at = pl.ds(base + half * SUBLANES, SUBLANES)
                lru = lru_both[half * SUBLANES : (half + 1) * SUBLANES]
                start = across(dist_ref[row, at, :], width) == 0
                rate = sigmoid(both_ref[row, at, :width] + rate_bias)
                igate = sigmoid(both_ref[row, at, width:] + input_bias)
                log_decay = rate * soft
                decay = jnp.exp(log_decay)
                arg = jnp.maximum(root_argument(log_decay, decay), ROOT_FLOOR)
                root = arg * lax.rsqrt(arg)
                cum = jnp.where(start, 0.0, decay)
                value = jnp.where(start, 1.0, root) * igate * lru
                rate_ref[row, at, :] = rate
                igate_ref[row, at, :] = igate
                for shift in (1, 2, 4):
                    live = place >= shift
                    value = value + cum * jnp.where(live, pltpu.roll(value, shift, 0), 0.0)
                    cum = cum * jnp.where(live, pltpu.roll(cum, shift, 0), 1.0)
                value = value + cum * run_state
                cum = cum * run_cum
                state_ref[row, at, :] = value
                cum_ref[row, at, :] = cum
                run_state = value[SUBLANES - 1 :, :]
                run_cum = cum[SUBLANES - 1 :, :]
            later.append((run_cum, run_state))
        return tuple(later)

    one, zero = (jnp.ones((1, width), jnp.float32), jnp.zeros((1, width), jnp.float32))
    done = lax.fori_loop(
        0, length // span, scan_step, tuple((one, zero) for _ in range(rows)), unroll=2
    )
    for row in range(rows):
        for place in range(2):
            last_ref[row, place : place + 1, :] = done[row][place]


def carried(sent_ref, got_ref, out_ref, send_sem, recv_sem, backward):
    seq, count = (lax.axis_index("seq"), lax.axis_size("seq"))

    def other(step):
        return {"seq": lax.rem(seq + step, count)}

    barrier = pltpu.get_barrier_semaphore()
    for step in range(1, count):
        pl.semaphore_signal(barrier, inc=1, device_id=other(step), device_id_type=MESH)
    pl.semaphore_wait(barrier, count - 1)
    copies = [
        pltpu.make_async_remote_copy(
            src_ref=sent_ref,
            dst_ref=got_ref.at[seq],
            send_sem=send_sem.at[step - 1],
            recv_sem=recv_sem.at[step - 1],
            device_id=other(step),
            device_id_type=MESH,
        )
        for step in range(1, count)
    ]
    for copy in copies:
        copy.start()
    got_ref[seq] = sent_ref[...]
    for copy in copies:
        copy.wait()
    for row in range(sent_ref.shape[0]):
        total = jnp.zeros(out_ref.shape[1:], jnp.float32)
        for place in range(count - 1, 0, -1) if backward else range(count - 1):
            longer = got_ref[place, row, 0:1, :] * total + got_ref[place, row, 1:2, :]
            total = jnp.where(place > seq if backward else place < seq, longer, total)
        out_ref[row] = total


def adjoint_kernel(rows, *refs):
    (
        dres_ref,
        weight_ref,
        pre_ref,
        state_ref,
        cum_ref,
        carry_ref,
        rate_ref,
        dist_ref,
        par_ref,
    ), outs = by_rows(refs, rows, (False, False, True, True, True, False, True, False, False))
    dgate_ref, local_ref, back_ref, first_ref, dmix_ref = outs
    _, length, width = dmix_ref.shape
    for row in range(rows):
        dmix_ref[row] = lax.dot_general(
            dres_ref[row * length : (row + 1) * length, :],
            weight_ref[...],
            (((1,), (1,)), ((), ())),
            preferred_element_type=jnp.float32,
        )
    soft = par_ref[7:8, :]
    place = lax.broadcasted_iota(jnp.int32, (SUBLANES, width), 0)
    last = length // STEP - 1

    def step(index, carry):
        base = pl.multiple_of((last - index) * STEP, STEP)
        later = []
        for row in range(rows):
            run_cum, run_back = carry[row]
            entering = carry_ref[row]
            pieces = []
            for half in reversed(range(STEP // SUBLANES)):
                at = pl.ds(base + half * SUBLANES, SUBLANES)
                start = across(dist_ref[row, at, :], width) == 0
                state = state_ref[row, at, :] + cum_ref[row, at, :] * entering
                act, slope = gelu_pair(pre_ref[row, at, :])
                dmix = dmix_ref[row, at, :]
                pieces.append(dmix * state * slope)
                dstate = dmix * act
                coef = jnp.where(start, 0.0, jnp.exp(rate_ref[row, at, :] * soft))
                value = coef * dstate
                for shift in (1, 2, 4):
                    live = place < SUBLANES - shift
                    turn = SUBLANES - shift
                    value = value + coef * jnp.where(live, pltpu.roll(value, turn, 0), 0.0)
                    coef = coef * jnp.where(live, pltpu.roll(coef, turn, 0), 1.0)
                value = value + coef * run_back
                coef = coef * run_cum
                inside = place < SUBLANES - 1
                local_ref[row, at, :] = dstate + jnp.where(
                    inside, pltpu.roll(value, SUBLANES - 1, 0), run_back
                )
                back_ref[row, at, :] = jnp.where(inside, pltpu.roll(coef, SUBLANES - 1, 0), run_cum)
                run_back = value[:1, :]
                run_cum = coef[:1, :]
            dgate_ref[row, pl.ds(base, STEP), :] = jnp.concatenate(pieces[::-1], axis=0).astype(
                jnp.bfloat16
            )
            later.append((run_cum, run_back))
        return tuple(later)

    one, zero = (jnp.ones((1, width), jnp.float32), jnp.zeros((1, width), jnp.float32))
    done = lax.fori_loop(0, last + 1, step, tuple((one, zero) for _ in range(rows)), unroll=2)
    for row in range(rows):
        first_ref[row] = done[row][1]


def backward_kernel(head_size, rows, *refs):
    first_at = 2
    sent_ref, got_ref, send_sem, recv_sem = refs[-4:]
    leaving_ref = refs[-8]
    lasts = Rows(refs[first_at + 1 : first_at + 1 + rows])

    @pl.when(pl.program_id(0) == 0)
    def _():
        for row in range(rows):
            sent_ref[row, 0:1, :] = lasts[row, 0:1, :]
            sent_ref[row, 1:2, :] = refs[first_at][row]
        carried(sent_ref, got_ref, leaving_ref, send_sem, recv_sem, True)

    block_backward(head_size, rows, 0, leaving_ref, *refs[:-8], *refs[-7:-4])


def later_backward_kernel(head_size, rows, first, *refs):
    held = 4
    block_backward(head_size, rows, first, refs[0], *refs[1 + held :])


def block_backward(head_size, rows, first_block, leaving_ref, *refs):
    (
        local_ref,
        back_ref,
        first_ref,
        last_ref,
        state_ref,
        cum_ref,
        in_ref,
        rate_ref,
        igate_ref,
        lru_ref,
        dist_ref,
        branch_ref,
        rim_ref,
        par_ref,
        gates_ref,
    ), others = by_rows(
        refs, rows, (False,) * 3 + (True,) * 3 + (False,) + (True,) * 3 + (False,) + (True,) * 2 + (False,) * 2
    )
    dbranch_ref, tail_ref, head_ref, dgates_ref = others[:4]
    both_ref, dconv_ref, sums_ref = others[-3:]
    _, length, width = local_ref.shape
    here = pl.program_id(0) + first_block
    block = pl.ds(pl.multiple_of(here * width, width), width)
    taps = [par_ref[k : k + 1, :] for k in range(4)]
    soft = par_ref[7:8, :]
    place = lax.broadcasted_iota(jnp.int32, (SUBLANES, width), 0)
    zeros = jnp.zeros((SUBLANES, width), jnp.float32)

    def gate_step(index, carry):
        sums, earlier = carry
        decay_sum, rate_sum, input_sum = sums
        base = pl.multiple_of(index * STEP, STEP)
        later = []
        for row in range(rows):
            before = earlier[row]
            entering = in_ref[row]
            leaving = leaving_ref[row, :, block]
            lru_both = lru_ref[row, pl.ds(base, STEP), :].astype(jnp.float32)
            drates, dinputs = ([], [])
            for half in range(STEP // SUBLANES):
                at = pl.ds(base + half * SUBLANES, SUBLANES)
                lru = lru_both[half * SUBLANES : (half + 1) * SUBLANES]
                start = across(dist_ref[row, at, :], width) == 0
                adjoint = local_ref[row, at, :] + back_ref[row, at, :] * leaving
                state = state_ref[row, at, :] + cum_ref[row, at, :] * entering
                previous = jnp.where(place < 1, before, pltpu.roll(state, 1, 0))
                before = state[SUBLANES - 1 :, :]
                rate = rate_ref[row, at, :]
                igate = igate_ref[row, at, :]
                log_decay = rate * soft
                decay = jnp.exp(log_decay)
                arg = root_argument(log_decay, decay)
                above = arg > ROOT_FLOOR
                arg = jnp.maximum(arg, ROOT_FLOOR)
                inverse = lax.rsqrt(arg)
                scale = jnp.where(start, 1.0, arg * inverse)
                gated = adjoint * igate
                dscale = gated * lru
                pull = jnp.where(above, dscale * decay * decay * inverse, 0.0)
                dlog = jnp.where(start, 0.0, adjoint * previous * decay - pull)
                dig = adjoint * scale * lru
                weighted = dlog * rate
                decay_sum = decay_sum + weighted
                drates.append(weighted * soft * (1.0 - rate))
                dinputs.append(dig * igate * (1.0 - igate))
                dconv_ref[row, at, :] = gated * scale
            drate = jnp.concatenate(drates, axis=0).astype(jnp.bfloat16)
            dinput = jnp.concatenate(dinputs, axis=0).astype(jnp.bfloat16)
            both_ref[row, pl.ds(base, STEP), :width] = drate
            both_ref[row, pl.ds(base, STEP), width:] = dinput
            drate = drate.astype(jnp.float32)
            dinput = dinput.astype(jnp.float32)
            rate_sum = rate_sum + (drate[:SUBLANES] + drate[SUBLANES:])
            input_sum = input_sum + (dinput[:SUBLANES] + dinput[SUBLANES:])
            later.append(before)
        return ((decay_sum, rate_sum, input_sum), tuple(later))

    sums, _ = lax.fori_loop(
        0,
        length // STEP,
        gate_step,
        ((zeros, zeros, zeros), tuple(in_ref[row] for row in range(rows))),
        unroll=2,
    )
    for slot, total in zip((5, 6, 7), (sums[1], sums[2], sums[0] * par_ref[8:9, :])):
        sums_ref[slot : slot + 1, :] = jnp.sum(total, axis=0, keepdims=True)

    piece = min(length, 256)
    wide = None
    for row in range(rows):

        def dot_step(index, carry, row=row):
            at = pl.ds(pl.multiple_of(index * piece, piece), piece)
            dconv_ref[row, at, :] += lax.dot_general(
                both_ref[row, at, :],
                gates_ref[...],
                (((1,), (1,)), ((), ())),
                preferred_element_type=jnp.float32,
            )
            return carry

        lax.fori_loop(0, length // piece, dot_step, 0)
        part = lax.dot_general(
            lru_ref[row], both_ref[row], (((0,), (0,)), ((), ())), preferred_element_type=jnp.float32
        )
        wide = part if wide is None else wide + part
    row_head = lax.broadcasted_iota(jnp.int32, (width, width), 0) // head_size
    col_head = lax.broadcasted_iota(jnp.int32, (width, width), 1) // head_size
    own = row_head == col_head
    folds = []
    for part in range(2):
        kept = jnp.where(own, wide[:, part * width : (part + 1) * width], 0.0)
        folded = kept
        for other in range(1, width // head_size):
            folded = folded + pltpu.roll(kept, width - other * head_size, 1)
        folds.append(folded[:, :LANES])

    def conv_step(index, carry):
        sums, following = carry
        sums = list(sums)
        base = pl.multiple_of((length // STEP - 1 - index) * STEP, STEP)
        later = []
        for row in range(rows):
            after = following[row]
            pieces = []
            for half in reversed(range(STEP // SUBLANES)):
                at = pl.ds(base + half * SUBLANES, SUBLANES)
                dist = across(dist_ref[row, at, :], width)
                branch = branch_ref[row, at, :]
                here = dconv_ref[row, at, :]
                total = taps[0] * here
                sums[0] = sums[0] + here * branch
                sums[4] = sums[4] + here
                masked = tuple(jnp.where(dist >= k, here, 0.0) for k in range(1, 4))
                for k in range(1, 4):
                    moved = pltpu.roll(
                        jnp.where(place >= k, masked[k - 1], after[k - 1]), SUBLANES - k, 0
                    )
                    total = total + taps[k] * moved
                    sums[k] = sums[k] + branch * moved
                after = masked
                pieces.append(total)
            whole = jnp.concatenate(pieces[::-1], axis=0)
            dbranch_ref[row, pl.ds(base, STEP), :] = whole.astype(jnp.bfloat16)
            later.append(after)

            @pl.when(index == 0)
            def _(row=row, whole=whole):
                tail_ref[row] = whole[STEP - SUBLANES :]

        return (tuple(sums), tuple(later))

    sums, firsts = lax.fori_loop(
        0,
        length // STEP,
        conv_step,
        ((zeros,) * 5, tuple((zeros,) * 3 for _ in range(rows))),
        unroll=2,
    )
    sums = list(sums)
    for row in range(rows):
        total = zeros
        rim = rim_ref[row]
        for k in range(1, 4):
            moved = pltpu.roll(jnp.where(place >= k, 0.0, firsts[row][k - 1]), SUBLANES - k, 0)
            total = total + taps[k] * moved
            sums[k] = sums[k] + rim * moved
        head_ref[row] = total
    for slot in range(5):
        sums_ref[slot : slot + 1, :] = jnp.sum(sums[slot], axis=0, keepdims=True)
    above = jnp.zeros((head_size, width), jnp.float32)
    below = jnp.zeros((LANES - head_size - SUBLANES, width), jnp.float32)
    turned = jnp.concatenate([above, sums_ref[...], below], axis=0).T
    lane = lax.broadcasted_iota(jnp.int32, (width, LANES), 1)
    dgates_ref[:, :LANES] = jnp.where(lane < head_size, folds[0], turned).astype(dgates_ref.dtype)
    dgates_ref[:, LANES:] = folds[1].astype(dgates_ref.dtype)


def channel_call(
    kernel, name, arrays, specs, outs, out_specs, scratch, blocks, flops, params=()
):
    moved = sum(math.prod(a.shape) * a.dtype.itemsize for a in (*arrays, *outs))
    return pl.pallas_call(
        kernel,
        name=name,
        grid=(blocks,),
        in_specs=specs,
        out_specs=out_specs,
        out_shape=outs,
        scratch_shapes=scratch,
        compiler_params=pltpu.CompilerParams(vmem_limit_bytes=VMEM_BYTES, **dict(params)),
        cost_estimate=pl.CostEstimate(flops=flops, bytes_accessed=moved, transcendentals=0),
    )(*arrays)


class Recurrence:
    def __init__(self, rows, length, channels, head_size):
        self.rows, self.length, self.channels = (rows, length, channels)
        self.head_size = head_size
        self.width = head_size * LANES // math.gcd(head_size, LANES)
        self.blocks = channels // self.width
        self.flops = 2 * rows * length * channels * 2 * self.width

    def tall(self):
        return pl.BlockSpec((self.rows, self.length, self.width), lambda j: (0, 0, j))

    def short(self, size):
        return pl.BlockSpec((self.rows, size, self.width), lambda j: (0, 0, j))

    def apart(self, size):
        return [pl.BlockSpec((1, size, self.width), lambda j: (0, 0, j))] * self.rows

    def whole(self, rows, size):
        return pl.BlockSpec((rows, size, self.channels), lambda j: (0, 0, 0))

    def flat(self, size):
        return pl.BlockSpec((size, self.width), lambda j: (0, j))

    def dist(self):
        return pl.BlockSpec((self.rows, self.length, LANES), lambda j: (0, 0, 0))

    def gates(self, columns):
        return pl.BlockSpec((self.width, columns), lambda j: (j, 0))

    def shape(self, size, dtype):
        return jax.ShapeDtypeStruct((self.rows, size, self.channels), dtype)

    def widen(self, lru_gates):
        size, width = (self.head_size, self.width)
        heads = width // size
        column = jnp.arange(2 * width)
        source = (column // width) * size + column % size
        spread = (jnp.arange(2 * size)[:, None] == source[None, :]).astype(jnp.bfloat16)
        owner = (column % width) // size
        mine = (jnp.arange(self.channels) // size) % heads
        wide = jnp.dot(lru_gates, spread, preferred_element_type=jnp.float32)
        return jnp.where(mine[:, None] == owner[None, :], wide, 0.0).astype(jnp.bfloat16)

    def adjoint(self, dres, weight, pre, state, cum, entering, rate, dist, params):
        f32 = jnp.float32
        outs = [self.shape(self.length, d) for d in (jnp.bfloat16, f32, f32)] + [self.shape(1, f32)]
        tall, apart = (self.tall(), self.apart(self.length))
        return channel_call(
            functools.partial(adjoint_kernel, self.rows),
            "recurrence_adjoint",
            (dres, weight, *pre, *state, *cum, entering, *rate, dist, params),
            [
                pl.BlockSpec(dres.shape, lambda j: (0, 0)),
                self.gates(weight.shape[1]),
                *apart * 3,
                self.short(1),
                *apart,
                self.dist(),
                self.flat(16),
            ],
            outs,
            [tall, tall, tall, self.short(1)],
            [pltpu.VMEM((self.rows, self.length, self.width), f32)],
            self.blocks,
            2 * self.rows * self.length * weight.size,
        )

    def backward(
        self, local, back, first, last, state, cum, entering, rate, igate, lru, dist, branch, rim, params, gates, between_calls
    ):
        f32 = jnp.float32
        outs = [
            self.shape(self.length, jnp.bfloat16),
            self.shape(SUBLANES, f32),
            self.shape(SUBLANES, f32),
            jax.ShapeDtypeStruct((self.channels, 2 * LANES), jnp.bfloat16),
        ]
        seqs = lax.axis_size("seq")
        summary = (self.rows, 2, self.channels)
        arrays = (local, back, first, *last, *state, *cum, entering, *rate, *igate, *lru, dist, *branch, *rim)
        arrays += (params, gates)
        early = self.blocks - 1
        scratch = [
            pltpu.VMEM((self.rows, self.length, 2 * self.width), jnp.bfloat16),
            pltpu.VMEM((self.rows, self.length, self.width), f32),
            pltpu.VMEM((SUBLANES, self.width), f32),
        ]

        def specs(offset):
            rows, width = (self.rows, self.width)

            def wide(rows, size):
                return pl.BlockSpec((rows, size, width), lambda j: (0, 0, j + offset))

            def flat(size):
                return pl.BlockSpec((size, width), lambda j: (0, j + offset))

            def tall(columns):
                return pl.BlockSpec((width, columns), lambda j: (j + offset, 0))

            whole, apart = (wide(rows, self.length), [wide(1, self.length)] * rows)
            given = [whole, whole, self.whole(rows, 1), *[self.whole(1, 2)] * rows, *apart * 2]
            given += [wide(rows, 1), *apart * 3, self.dist(), *apart, *[wide(1, SUBLANES)] * rows]
            given += [flat(16), tall(2 * width)]
            made = [whole, wide(rows, SUBLANES), wide(rows, SUBLANES), tall(2 * LANES)]
            return (given, made)

        given, made = specs(0)
        *found, leaving = channel_call(
            functools.partial(backward_kernel, self.head_size, self.rows),
            "recurrence_backward",
            arrays,
            given,
            outs + [self.shape(1, f32)],
            made + [self.whole(self.rows, 1)],
            scratch
            + [
                pltpu.VMEM(summary, f32),
                pltpu.VMEM((seqs,) + summary, f32),
                pltpu.SemaphoreType.DMA((seqs - 1,)),
                pltpu.SemaphoreType.DMA((seqs - 1,)),
            ],
            early,
            2 * self.flops,
            {"collective_id": 5, "has_side_effects": True},
        )
        between, leaving = between_calls(leaving)
        given, made = specs(early)
        done = pl.pallas_call(
            functools.partial(later_backward_kernel, self.head_size, self.rows, early),
            name="recurrence_backward_end",
            grid=(self.blocks - early,),
            in_specs=[self.whole(self.rows, 1)] + [pl.BlockSpec(memory_space=pl.ANY)] * 4 + given,
            out_specs=made,
            out_shape=outs,
            scratch_shapes=scratch,
            input_output_aliases={1 + k: k for k in range(4)},
            compiler_params=pltpu.CompilerParams(vmem_limit_bytes=VMEM_BYTES),
            cost_estimate=pl.CostEstimate(
                flops=self.flops // 2, bytes_accessed=16 * self.flops // self.width, transcendentals=0
            ),
        )(leaving, *found, *arrays)
        return (*done, between)


def gathered(parts_ref, at):
    return jnp.concatenate([parts_ref[k, at, :] for k in range(parts_ref.shape[0])], axis=1)


def front_kernel(
    parts_ref,
    gain_ref,
    input_ref,
    gate_ref,
    dist_ref,
    par_ref,
    gates_ref,
    x_ref,
    inverse_ref,
    normed_ref,
    branch_ref,
    pre_ref,
    rim_ref,
    lru_ref,
    rate_ref,
    igate_ref,
    state_ref,
    cum_ref,
    last_ref,
    landed_ref,
    both_ref,
    send_sem,
    recv_sem,
):
    tokens = x_ref.shape[0]
    piece, tall = (64, min(tokens, 512))
    step = pl.program_id(0)
    seq, seqs = (lax.axis_index("seq"), lax.axis_size("seq"))
    barrier = pltpu.get_barrier_semaphore()

    @pl.when(step == 0)
    def _():
        before = {"seq": lax.rem(seq + seqs - 1, seqs)}
        pl.semaphore_signal(barrier, inc=1, device_id=before, device_id_type=MESH)

        def norm(index, carry):
            at = pl.ds(pl.multiple_of(index * piece, piece), piece)
            low = gathered(parts_ref, at)
            x_ref[at, :] = low
            value = low.astype(jnp.float32)
            inverse = lax.rsqrt(jnp.mean(value * value, axis=1, keepdims=True) + EPS)
            inverse_ref[at, :] = jnp.broadcast_to(inverse, (piece, LANES))
            normed_ref[at, :] = (value * inverse * gain_ref[...]).astype(jnp.bfloat16)
            return carry

        lax.fori_loop(0, tokens // piece, norm, 0, unroll=2)

    rim_copy = pltpu.make_async_remote_copy(
        src_ref=normed_ref.at[tokens - STEP :],
        dst_ref=landed_ref,
        send_sem=send_sem,
        recv_sem=recv_sem,
        device_id={"seq": lax.rem(seq + 1, seqs)},
        device_id_type=MESH,
    )

    @pl.when(step == 0)
    def _():
        pl.semaphore_wait(barrier, 1)
        rim_copy.start()

    def multiply(index, carry):
        at = pl.ds(pl.multiple_of(index * tall, tall), tall)
        normed = normed_ref[at, :]
        branch_ref[0, at, :] = jnp.dot(normed, input_ref[...], preferred_element_type=jnp.float32)
        pre_ref[0, at, :] = jnp.dot(normed, gate_ref[...], preferred_element_type=jnp.float32)
        return carry

    lax.fori_loop(0, tokens // tall, multiply, 0)

    @pl.when(step == 0)
    def _():
        rim_copy.wait()

    before = jnp.dot(landed_ref[...], input_ref[...], preferred_element_type=jnp.float32)
    rim_ref[0] = jnp.where(seq > 0, 1.0, 0.0) * before[STEP - SUBLANES :]
    scan_block(
        branch_ref,
        rim_ref,
        dist_ref,
        par_ref,
        gates_ref,
        lru_ref,
        rate_ref,
        igate_ref,
        state_ref,
        cum_ref,
        last_ref,
        both_ref,
    )


def front(parts, gain, recur_input, recur_gate, dist, params, gates):
    count, tokens, width = parts.shape
    model, rec = recur_input.shape
    columns = gates.shape[1] // 2
    steps = rec // columns
    low, f32 = (jnp.bfloat16, jnp.float32)
    tall = pl.BlockSpec((model, columns), lambda j: (0, j))

    def whole(shape):
        return pl.BlockSpec(shape, lambda j: (0,) * len(shape))

    def wide(size, dtype):
        spec = pl.BlockSpec((1, size, columns), lambda j: (0, 0, j))
        return (spec, jax.ShapeDtypeStruct((1, size, rec), dtype))

    made = [wide(tokens, f32), wide(tokens, f32), wide(SUBLANES, f32), wide(tokens, low)]
    made += [wide(tokens, f32)] * 4 + [wide(2, f32)]
    return pl.pallas_call(
        front_kernel,
        name="project_and_scan",
        grid=(steps,),
        in_specs=[
            whole(parts.shape),
            whole((1, model)),
            tall,
            tall,
            whole(dist.shape),
            pl.BlockSpec((16, columns), lambda j: (0, j)),
            pl.BlockSpec((columns, 2 * columns), lambda j: (j, 0)),
        ],
        out_specs=[whole((tokens, model)), whole((tokens, LANES)), whole((tokens, model))]
        + [spec for spec, _ in made],
        out_shape=[
            jax.ShapeDtypeStruct((tokens, model), low),
            jax.ShapeDtypeStruct((tokens, LANES), f32),
            jax.ShapeDtypeStruct((tokens, model), low),
        ]
        + [shape for _, shape in made],
        scratch_shapes=[
            pltpu.VMEM((STEP, model), low),
            pltpu.VMEM((1, tokens, 2 * columns), f32),
            pltpu.SemaphoreType.DMA,
            pltpu.SemaphoreType.DMA,
        ],
        compiler_params=pltpu.CompilerParams(
            collective_id=3, has_side_effects=True, vmem_limit_bytes=VMEM_BYTES
        ),
        cost_estimate=pl.CostEstimate(
            flops=5 * tokens * model * rec, bytes_accessed=40 * tokens * model, transcendentals=0
        ),
    )(parts, gain[None], recur_input, recur_gate, dist, params, gates)


def middle_kernel(rows, *refs):
    (last_ref, state_hbm, cum_hbm, pre_hbm, x_ref, out_ref, gain_ref), others = by_rows(
        refs, rows, (True,) * 5 + (False,) * 2
    )
    entering_ref, mixed_ref, resid_ref, normed_ref = others[:4]
    sent_ref, got_ref, held_ref, send_sem, recv_sem, load_sem = others[4:]
    tall, model = resid_ref.shape
    step, steps = (pl.program_id(0), pl.num_programs(0))
    tiles = steps // rows
    slab = 16

    def on_row(place, act):
        for row in range(rows):

            @pl.when(lax.div(place, tiles) == row)
            def _(row=row):
                at = pl.ds(pl.multiple_of(lax.rem(place, tiles) * tall, tall), tall)
                slot = lax.rem(place, 2)
                for kind, source in enumerate((state_hbm, cum_hbm, pre_hbm)):
                    act(
                        pltpu.make_async_copy(
                            source.refs[row].at[0, at], held_ref.at[slot, kind], load_sem.at[slot, kind]
                        )
                    )

    @pl.when(step == 0)
    def _():
        on_row(step, lambda copy: copy.start())
        for row in range(rows):
            sent_ref[row] = last_ref[row]
        carried(sent_ref, got_ref, entering_ref, send_sem, recv_sem, False)

    @pl.when(step + 1 < steps)
    def _():
        on_row(step + 1, lambda copy: copy.start())

    on_row(step, lambda copy: copy.wait())
    slot = lax.rem(step, 2)
    mine = lax.div(step, tiles)

    def mix(index, carry):
        at = pl.ds(pl.multiple_of(index * slab, slab), slab)
        state = held_ref[slot, 0, at, :] + held_ref[slot, 1, at, :] * entering_ref[mine]
        pre = held_ref[slot, 2, at, :]
        inner = jnp.tanh(pre * (GELU_C + (GELU_C * GELU_A) * (pre * pre)))
        mixed_ref[at, :] = (state * (pre * (0.5 + 0.5 * inner))).astype(jnp.bfloat16)
        return carry

    lax.fori_loop(0, tall // slab, mix, 0, unroll=2)
    for row in range(rows):

        @pl.when(mine == row)
        def _(row=row):
            tile = 512
            for first in range(0, model, tile):
                at = slice(first, first + tile)
                resid_ref[:, at] = x_ref.refs[row][:, at].astype(jnp.float32) + jnp.dot(
                    mixed_ref[...], out_ref[:, at], preferred_element_type=jnp.float32
                )

    def norm(index, carry):
        at = pl.ds(pl.multiple_of(index * slab, slab), slab)
        resid = resid_ref[at, :]
        inverse = lax.rsqrt(jnp.mean(resid * resid, axis=1, keepdims=True) + EPS)
        normed_ref[at, :] = (resid * inverse * gain_ref[...]).astype(jnp.bfloat16)
        return carry

    lax.fori_loop(0, tall // slab, norm, 0, unroll=4)


def middle(last, state, cum, pre, x, recur_out, gain):
    rows = len(state)
    _, length, rec = state[0].shape
    model = recur_out.shape[1]
    tall = min(length, 256)
    tiles = length // tall
    tokens = rows * length
    seqs = lax.axis_size("seq")
    low, f32 = (jnp.bfloat16, jnp.float32)

    def whole(shape):
        return pl.BlockSpec(shape, lambda s: (0,) * len(shape), pipeline_mode=pl.Buffered(1))

    def flat(row):
        return lambda s: (jnp.clip(s - row * tiles, 0, tiles - 1), 0)

    summary = (rows, 2, rec)
    return pl.pallas_call(
        functools.partial(middle_kernel, rows),
        name="mix_and_norm",
        grid=(rows * tiles,),
        in_specs=[whole((1, 2, rec))] * rows
        + [pl.BlockSpec(memory_space=pl.ANY)] * (3 * rows)
        + [pl.BlockSpec((tall, model), flat(row)) for row in range(rows)]
        + [whole(recur_out.shape), whole((1, model))],
        out_specs=[
            pl.BlockSpec((rows, 1, rec), lambda s: (0, 0, 0)),
            pl.BlockSpec((tall, rec), lambda s: (s, 0)),
            pl.BlockSpec((tall, model), lambda s: (s, 0)),
            pl.BlockSpec((tall, model), lambda s: (s, 0)),
        ],
        out_shape=[
            jax.ShapeDtypeStruct((rows, 1, rec), f32),
            jax.ShapeDtypeStruct((tokens, rec), low),
            jax.ShapeDtypeStruct((tokens, model), f32),
            jax.ShapeDtypeStruct((tokens, model), low),
        ],
        scratch_shapes=[
            pltpu.VMEM(summary, f32),
            pltpu.VMEM((seqs,) + summary, f32),
            pltpu.VMEM((2, 3, tall, rec), f32),
            pltpu.SemaphoreType.DMA((seqs - 1,)),
            pltpu.SemaphoreType.DMA((seqs - 1,)),
            pltpu.SemaphoreType.DMA((2, 3)),
        ],
        compiler_params=pltpu.CompilerParams(
            collective_id=4, has_side_effects=True, vmem_limit_bytes=VMEM_BYTES
        ),
        cost_estimate=pl.CostEstimate(
            flops=2 * tokens * rec * model, bytes_accessed=14 * tokens * rec, transcendentals=0
        ),
    )(*last, *state, *cum, *pre, *x, recur_out, gain[None])


def hidden_kernel(
    left_ref,
    parts_ref,
    normed_ref,
    gate_ref,
    up_ref,
    down_ref,
    gout_ref,
    hidden_ref,
    dgate_ref,
    dup_ref,
):
    tokens, model = normed_ref.shape
    chunk = down_ref.shape[0]
    rows = left_ref.shape[0]
    length = tokens // rows
    slab = 32

    @pl.when(pl.program_id(0) == 0)
    def _():
        for row in range(rows):

            def collect(index, carry, row=row):
                base = pl.multiple_of(index * slab, slab)
                at = pl.ds(row * length + base, slab)
                low = gathered(parts_ref, at)
                place = base + lax.broadcasted_iota(jnp.int32, low.shape, 0)
                value = jnp.where(place < left_ref[row], low.astype(jnp.float32), 0.0)
                gout_ref[at, :] = value.astype(jnp.bfloat16)
                return carry

            lax.fori_loop(0, length // slab, collect, 0)

    tall = min(tokens, 512)
    wide = 256

    def tile(index, carry):
        at = pl.ds(pl.multiple_of(index * tall, tall), tall)
        for column in range(chunk // wide):
            own = slice(column * wide, (column + 1) * wide)
            gate = jnp.dot(normed_ref[at, :], gate_ref[:, own], preferred_element_type=jnp.float32)
            up = jnp.dot(normed_ref[at, :], up_ref[:, own], preferred_element_type=jnp.float32)
            dhid = lax.dot_general(
                gout_ref[at, :],
                down_ref[own, :],
                (((1,), (1,)), ((), ())),
                preferred_element_type=jnp.float32,
            )
            act, slope = gelu_pair(gate)
            hidden_ref[at, own] = (act * up).astype(jnp.bfloat16)
            dgate_ref[at, own] = (dhid * up * slope).astype(jnp.bfloat16)
            dup_ref[at, own] = (dhid * act).astype(jnp.bfloat16)
        return carry

    lax.fori_loop(0, tokens // tall, tile, 0, unroll=True)


def back_kernel(
    hidden_ref,
    dgate_ref,
    dup_ref,
    gout_hbm,
    resid_hbm,
    gain_ref,
    gate_ref,
    up_ref,
    down_ref,
    result_ref,
    dres_ref,
    total_ref,
    back_ref,
    gout_ref,
    resid_ref,
    load_sem,
):
    tall, model = (hidden_ref.shape[0], gout_ref.shape[1])
    step, tile = (pl.program_id(0), pl.program_id(1))
    wide = 512
    contract = (((1,), (1,)), ((), ()))
    rows = pl.ds(pl.multiple_of(tile * tall, tall), tall)

    def loads():
        return (
            pltpu.make_async_copy(gout_hbm, gout_ref, load_sem.at[0]),
            pltpu.make_async_copy(resid_hbm, resid_ref, load_sem.at[1]),
        )

    @pl.when((step == 0) & (tile == 0))
    def _():
        for load in loads():
            load.start()

    def products(own):
        forth = jnp.dot(hidden_ref[...], down_ref[:, own], preferred_element_type=jnp.float32)
        back = lax.dot_general(
            dgate_ref[...], gate_ref[own, :], contract, preferred_element_type=jnp.float32
        ) + lax.dot_general(
            dup_ref[...], up_ref[own, :], contract, preferred_element_type=jnp.float32
        )
        return (forth, back)

    @pl.when(step == 0)
    def _():
        for first in range(0, model, wide):
            own = slice(first, first + wide)
            forth, back = products(own)
            total_ref[rows, own] = forth
            back_ref[rows, own] = back

    @pl.when(step > 0)
    def _():
        for first in range(0, model, wide):
            own = slice(first, first + wide)
            forth, back = products(own)
            total_ref[rows, own] += forth
            back_ref[rows, own] += back

    @pl.when((step == pl.num_programs(0) - 1) & (tile == 0))
    def _():
        for load in loads():
            load.wait()

    @pl.when(step == pl.num_programs(0) - 1)
    def _():
        parts, width = (result_ref.shape[0], result_ref.shape[2])
        small = 16

        def finish(index, carry):
            at = pl.ds(pl.multiple_of(tile * tall + index * small, small), small)
            resid = resid_ref[at, :]
            result = (resid + total_ref[at, :]).astype(jnp.bfloat16)
            for part in range(parts):
                result_ref[part, at, :] = result[:, part * width : (part + 1) * width]
            inverse = lax.rsqrt(jnp.mean(resid * resid, axis=1, keepdims=True) + EPS)
            normed = resid * inverse
            scaled = back_ref[at, :] * gain_ref[...]
            mean = jnp.mean(scaled * normed, axis=1, keepdims=True)
            dres = gout_ref[at, :].astype(jnp.float32) + inverse * (scaled - normed * mean)
            dres_ref[at, :] = dres.astype(jnp.bfloat16)
            return carry

        lax.fori_loop(0, tall // small, finish, 0, unroll=4)


MLP_CHUNK = 768


def resident(shape):
    return pl.BlockSpec(shape, lambda s: (0,) * len(shape), pipeline_mode=pl.Buffered(1))


def mlp_specs(tokens, model):
    columns = pl.BlockSpec((model, MLP_CHUNK), lambda s: (0, s))
    down = pl.BlockSpec((MLP_CHUNK, model), lambda s: (s, 0))
    made = pl.BlockSpec((tokens, MLP_CHUNK), lambda s: (0, s))
    return ([columns, columns, down], [made] * 3)


def mlp_hidden(left, parts, normed, mlp_gate, mlp_up, mlp_down):
    tokens, model = normed.shape
    ffn = mlp_gate.shape[1]
    low = jnp.bfloat16
    weights, made = mlp_specs(tokens, model)
    tall = jax.ShapeDtypeStruct((tokens, ffn), low)
    return pl.pallas_call(
        hidden_kernel,
        name="mlp_hidden",
        grid=(ffn // MLP_CHUNK,),
        in_specs=[
            pl.BlockSpec(memory_space=pltpu.SMEM),
            resident(parts.shape),
            resident(normed.shape),
            *weights,
        ],
        out_specs=[resident((tokens, model)), *made],
        out_shape=[jax.ShapeDtypeStruct((tokens, model), low), tall, tall, tall],
        compiler_params=pltpu.CompilerParams(vmem_limit_bytes=VMEM_BYTES),
        cost_estimate=pl.CostEstimate(
            flops=6 * tokens * model * ffn,
            bytes_accessed=6 * (model + tokens) * ffn + 6 * tokens * model,
            transcendentals=0,
        ),
    )(left, parts, normed, mlp_gate, mlp_up, mlp_down)


def mlp_back(hidden, dgate, dup, gout, resid, gain, mlp_gate, mlp_up, mlp_down, parts_shape):
    tokens, model = resid.shape
    ffn = mlp_gate.shape[1]
    low, f32 = (jnp.bfloat16, jnp.float32)
    chunk, tall = (1024, min(tokens, 512))

    def resident(shape):
        return pl.BlockSpec(shape, lambda s, t: (0,) * len(shape), pipeline_mode=pl.Buffered(1))

    columns = pl.BlockSpec((model, chunk), lambda s, t: (0, s))
    down = pl.BlockSpec((chunk, model), lambda s, t: (s, 0))
    made = pl.BlockSpec((tall, chunk), lambda s, t: (t, s))
    return pl.pallas_call(
        back_kernel,
        name="mlp_back",
        grid=(ffn // chunk, tokens // tall),
        in_specs=[
            made,
            made,
            made,
            pl.BlockSpec(memory_space=pl.ANY),
            pl.BlockSpec(memory_space=pl.ANY),
            resident((1, model)),
            columns,
            columns,
            down,
        ],
        out_specs=[resident(parts_shape), resident((tokens, model))],
        out_shape=[
            jax.ShapeDtypeStruct(parts_shape, low),
            jax.ShapeDtypeStruct((tokens, model), low),
        ],
        scratch_shapes=[
            pltpu.VMEM((tokens, model), f32),
            pltpu.VMEM((tokens, model), f32),
            pltpu.VMEM((tokens, model), low),
            pltpu.VMEM((tokens, model), f32),
            pltpu.SemaphoreType.DMA((2,)),
        ],
        compiler_params=pltpu.CompilerParams(vmem_limit_bytes=VMEM_BYTES),
        cost_estimate=pl.CostEstimate(
            flops=6 * tokens * model * ffn,
            bytes_accessed=6 * (model + tokens) * ffn + 10 * tokens * model,
            transcendentals=0,
        ),
    )(hidden, dgate, dup, gout, resid, gain[None], mlp_gate, mlp_up, mlp_down)


def outputs_kernel(
    device_ref,
    own_ref,
    gate_sum,
    in_sum,
    out_sum,
    small_ref,
    input_ref,
    gate_ref,
    mlp_gate_ref,
    mlp_up_ref,
    gain1_ref,
    gain2_ref,
    sum_gain1,
    sum_in,
    sum_gate,
    sum_taps,
    sum_bias,
    sum_lgates,
    sum_lbias,
    sum_decay,
    sum_out,
    sum_gain2,
    sum_mgate,
    sum_mup,
    sum_down,
):
    rows = sum_mgate.shape[0]
    model = own_ref.shape[1]
    parts = sum_mgate.shape[1] // model
    for part in range(parts):
        at = slice(part * model, (part + 1) * model)
        sum_mgate[:, at] = own_ref[part * rows : (part + 1) * rows, :].astype(jnp.float32)
        sum_mup[:, at] = own_ref[(parts + part) * rows : (parts + part + 1) * rows, :].astype(
            jnp.float32
        )
    sum_down[...] = own_ref[2 * parts * rows :, :].astype(jnp.float32)

    def weighed(*pairs):
        return sum(
            jnp.sum(weight[...].astype(jnp.float32) * gradient[...], axis=1, keepdims=True)
            for weight, gradient in pairs
        )

    def as_row(column, gain):
        lane = lax.broadcasted_iota(jnp.int32, (rows, LANES), 1)
        place = lax.broadcasted_iota(jnp.int32, (rows, LANES), 0)
        whole = lax.broadcasted_iota(jnp.int32, (rows, model), 1)
        own = device_ref[0] * rows + lax.broadcasted_iota(jnp.int32, (rows, model), 0)
        own_gain = jnp.sum(jnp.where(whole == own, gain[...], 0.0), axis=1, keepdims=True)
        return jnp.sum(jnp.where(lane == place, column / own_gain, 0.0), axis=0, keepdims=True)

    row1 = as_row(weighed((input_ref, in_sum), (gate_ref, gate_sum)), gain1_ref)
    row2 = as_row(weighed((mlp_gate_ref, sum_mgate), (mlp_up_ref, sum_mup)), gain2_ref)
    sum_gain1[...] = row1[:, :rows]
    sum_gain2[...] = row2[:, :rows]
    sum_in[...] = in_sum[...]
    sum_gate[...] = gate_sum[...]
    sum_out[...] = out_sum[...]
    channels = small_ref.shape[0]
    size = sum_lgates.shape[1] // 2
    first, second = (small_ref[:, :LANES], small_ref[:, LANES:])
    lane = lax.broadcasted_iota(jnp.int32, (channels, LANES), 1)
    moved = pltpu.roll(second, size, 1)
    sum_lgates[:, :LANES] = jnp.where(lane < size, first, moved)
    sum_lgates[:, LANES:] = moved[:, : 2 * size - LANES]
    filled = jnp.concatenate([first, jnp.zeros((LANES - channels, LANES), jnp.float32)], axis=0)
    turned = filled.T
    sum_taps[...] = turned[size : size + 4, :channels]
    sum_bias[...] = turned[size + 4 : size + 5, :channels]
    sum_lbias[...] = turned[size + 5 : size + 7, :channels]
    sum_decay[...] = turned[size + 7 : size + 8, :channels]


def outputs(
    device, own, gate_sum, in_sum, out_sum, small, recur_input, recur_gate, mlp_gate, mlp_up, gain1, gain2, size
):
    rows, rec = in_sum.shape
    model, ffn = mlp_gate.shape
    channels = small.shape[0]
    f32 = jnp.float32

    def whole(shape):
        return pl.BlockSpec(shape, lambda s, device: (0,) * len(shape))

    def mine(shape):
        return pl.BlockSpec(shape, lambda s, device: (device[0], 0))

    given = (own, gate_sum, in_sum, out_sum, small)
    shapes = [(1, rows), (rows, rec), (rows, rec), (4, channels), (1, channels)]
    shapes += [(channels, 2 * size), (2, channels), (1, channels), out_sum.shape, (1, rows)]
    shapes += [(rows, ffn), (rows, ffn), (own.shape[0] - 2 * ffn // model * rows, model)]
    return pl.pallas_call(
        outputs_kernel,
        name="outputs",
        grid_spec=pltpu.PrefetchScalarGridSpec(
            num_scalar_prefetch=1,
            grid=(1,),
            in_specs=[whole(a.shape) for a in given]
            + [mine((rows, rec))] * 2
            + [mine((rows, ffn))] * 2
            + [whole((1, model))] * 2,
            out_specs=[whole(shape) for shape in shapes],
        ),
        out_shape=[jax.ShapeDtypeStruct(shape, f32) for shape in shapes],
        compiler_params=pltpu.CompilerParams(vmem_limit_bytes=VMEM_BYTES),
    )(
        device[None],
        *given,
        recur_input,
        recur_gate,
        mlp_gate,
        mlp_up,
        gain1[None],
        gain2[None],
    )


def spread_kernel(whole_ref, out_ref):
    out_ref[0] = whole_ref[...]


def spread(whole, count):
    tokens, width = (whole.shape[0], whole.shape[1] // count)
    return pl.pallas_call(
        spread_kernel,
        name="spread_features",
        grid=(count,),
        in_specs=[pl.BlockSpec((tokens, width), lambda j: (0, j))],
        out_specs=pl.BlockSpec((1, tokens, width), lambda j: (j, 0, 0)),
        out_shape=jax.ShapeDtypeStruct((count, tokens, width), whole.dtype),
        cost_estimate=pl.CostEstimate(
            flops=0, bytes_accessed=4 * tokens * whole.shape[1], transcendentals=0
        ),
    )(whole)


CHAN = ("zed", "core")


def features_in(local, pick=slice(None)):
    count = lax.axis_size(CHAN)
    rows, length, width = local.shape
    local = local.reshape(count, rows // count, length, width)[:, pick]
    if width % LANES == 0:
        return lax.all_to_all(local, CHAN, 0, 0, tiled=True).reshape(count, -1, width)
    moved = lax.all_to_all(
        local.reshape(-1, length, width), CHAN, split_axis=0, concat_axis=2, tiled=True
    )
    return moved.reshape(1, -1, count * width)


def features_apart(whole):
    count = lax.axis_size(CHAN)
    if (whole.shape[1] // count) % LANES == 0:
        return spread(whole, count)
    return whole[None]


def features_out(parts, rows):
    blocks, tokens, width = parts.shape
    parts = parts.reshape(blocks, rows, tokens // rows, width)
    if blocks > 1:
        moved = lax.all_to_all(parts, CHAN, 0, 0, tiled=True)
        return moved.reshape(-1, *parts.shape[2:])
    return lax.all_to_all(parts[0], CHAN, split_axis=2, concat_axis=0, tiled=True)


class Corners:
    def __init__(self, seq, zed):
        self.seq_bits, self.zed_bits = (seq.bit_length() - 1, zed.bit_length() - 1)
        self.count = self.seq_bits + self.zed_bits
        self.dims = (2,) * self.count
        self.low = tuple(range(self.seq_bits))[::-1] + tuple(range(self.seq_bits, self.count))[::-1]
        self.high = tuple(range(self.seq_bits)) + tuple(range(self.seq_bits, self.count))[::-1]

    def place(self, dim):
        if dim < self.seq_bits:
            return ("seq", 2 ** (self.seq_bits - 1 - dim))
        return ("zed", 2 ** (self.count - 1 - dim))

    def bit(self, dim):
        axis, weight = self.place(dim)
        return lax.rem(lax.div(lax.axis_index(axis), weight), 2)

    def partner(self, dim):
        axis, weight = self.place(dim)
        return {axis: lax.axis_index(axis) + weight * (1 - 2 * self.bit(dim))}


def tail_kernel(
    corners,
    orders,
    dgate_hbm,
    dbranch_hbm,
    ending_ref,
    leading_ref,
    mixed_hbm,
    dres_hbm,
    gain_ref,
    input_hbm,
    gate_hbm,
    small_hbm,
    *refs,
):
    rows = ending_ref.shape[0]
    normed_hbms, x_hbms, inverse_hbms = (refs[k * rows : (k + 1) * rows] for k in range(3))
    tokens_ref, sum_gate, sum_out, sum_in, sum_small = refs[3 * rows : 3 * rows + 5]
    refs = refs[3 * rows + 5 :]
    stages = corners.count + 1
    dgate, dbranch, mixed, dres, normed, x, inverse, weight_in, weight_gate = refs[:9]
    made_in, made_out, own_small, back, parts, rim = refs[9:15]
    slots_in, slots_out, slots_small = (
        refs[15 + k * stages : 15 + (k + 1) * stages] for k in range(3)
    )
    (
        send_sem,
        recv_sem,
        load_sem,
        move_send,
        move_recv,
        keep_sem,
        rim_send,
        rim_recv,
    ) = refs[15 + 3 * stages :]
    seq, zed, core = (lax.axis_index(axis) for axis in ("seq", "zed", "core"))
    seqs, group = (lax.axis_size("seq"), 2 * lax.axis_size("zed"))
    mine = zed * 2 + core
    length = tokens_ref.shape[1]
    model = x.shape[1]

    def member(index):
        return {"zed": lax.div(index, 2), "core": lax.rem(index, 2)}

    def by_row(sources, target):
        return [
            (source, target.at[pl.ds(row * length, length)]) for row, source in enumerate(sources)
        ]

    pairs = [
        (dbranch_hbm, dbranch),
        (input_hbm, weight_in),
        (dgate_hbm, dgate),
        (gate_hbm, weight_gate),
        *by_row(x_hbms, x),
        *by_row(inverse_hbms, inverse),
        (dres_hbm, dres),
        *by_row(normed_hbms, normed),
        (mixed_hbm, mixed),
        (small_hbm.at[(slice(None),) * corners.count + (core,)], own_small),
    ]
    kinds = []
    for name in ('dbranch', 'win', 'dgate', 'wgate', 'x', 'inverse', 'dres', 'normed', 'mixed', 'small'):
        kinds += [name] * (rows if name in ("normed", "x", "inverse") else 1)
    loads = [
        pltpu.make_async_copy(source, target, load_sem.at[place])
        for place, (source, target) in enumerate(pairs)
    ]
    for load in loads:
        load.start()

    barrier = pltpu.get_barrier_semaphore()
    for other in range(1, group):
        pl.semaphore_signal(
            barrier, inc=1, device_id=member(lax.rem(mine + other, group)), device_id_type=MESH
        )
    for other in range(1, seqs):
        pl.semaphore_signal(
            barrier, inc=1, device_id={"seq": lax.rem(seq + other, seqs)}, device_id_type=MESH
        )
    pl.semaphore_wait(barrier, group - 1 + seqs - 1)

    rim_copy = pltpu.make_async_remote_copy(
        src_ref=leading_ref,
        dst_ref=rim,
        send_sem=rim_send,
        recv_sem=rim_recv,
        device_id={"seq": lax.rem(seq + seqs - 1, seqs)},
        device_id_type=MESH,
    )
    rim_copy.start()

    def own(stream, index):
        if stream < 4:
            return made_in.at[(stream,) + index + (core,)]
        if stream < 6:
            return made_out.at[(stream - 4,) + index + (core,)]
        return own_small.at[index]

    def slot(stream, stage):
        if stream < 4:
            return slots_in[stage].at[stream]
        if stream < 6:
            return slots_out[stage].at[stream - 4]
        return slots_small[stage]

    def copy(stream, stage):
        order = orders[stream]
        every = (slice(None),) * corners.count
        if stage == 0:
            if stream < 4:
                source = made_in.at[(stream,) + every + (1 - core,)]
            elif stream < 6:
                source = made_out.at[(stream - 4,) + every + (1 - core,)]
            else:
                source = small_hbm.at[every + (1 - core,)]
            target = {"core": 1 - core}
        else:
            dim = order[stage - 1]
            fixed = {before: corners.bit(before) for before in order[: stage - 1]}
            fixed[dim] = 1 - corners.bit(dim)
            source = own(stream, tuple(fixed.get(d, slice(None)) for d in range(corners.count)))
            target = corners.partner(dim)
        return pltpu.make_async_remote_copy(
            src_ref=source,
            dst_ref=slot(stream, stage),
            send_sem=send_sem.at[stream, stage],
            recv_sem=recv_sem.at[stream, stage],
            device_id=target,
            device_id_type=MESH,
        )

    sums = [
        sum_gate.at[:, : sum_gate.shape[1] // 2],
        sum_gate.at[:, sum_gate.shape[1] // 2 :],
        sum_in.at[:, : sum_in.shape[1] // 2],
        sum_in.at[:, sum_in.shape[1] // 2 :],
        sum_out.at[:, : sum_out.shape[1] // 2],
        sum_out.at[:, sum_out.shape[1] // 2 :],
        sum_small,
    ]

    def advance(stream, stage):
        order = orders[stream]
        copy(stream, stage).wait_recv()
        left = [dim for dim in range(corners.count) if dim not in order[:stage]]
        fixed = {dim: corners.bit(dim) for dim in order[:stage]}
        arrived = slot(stream, stage)
        if not left:
            index = tuple(fixed[dim] for dim in range(corners.count))
            sums[stream][...] = own(stream, index)[...].astype(jnp.float32) + arrived[...].astype(
                jnp.float32
            )
            return

        def add(index, carry):
            part = {
                dim: lax.rem(lax.div(index, 2 ** (len(left) - 1 - place)), 2)
                for place, dim in enumerate(left)
            }
            kept = own(stream, tuple({**fixed, **part}[dim] for dim in range(corners.count)))
            total = kept[...].astype(jnp.float32) + arrived[
                tuple(part[dim] for dim in left)
            ].astype(jnp.float32)
            kept[...] = total.astype(jnp.bfloat16)
            return carry

        lax.fori_loop(0, 2 ** len(left), add, 0)
        copy(stream, stage + 1).start()

    def move(other, row):
        to = lax.rem(mine + other, group)
        return pltpu.make_async_remote_copy(
            src_ref=parts.at[to, pl.ds(row * length, length)],
            dst_ref=tokens_ref.at[mine * rows + row],
            send_sem=move_send.at[other - 1, row],
            recv_sem=move_recv.at[other - 1, row],
            device_id=member(to),
            device_id_type=MESH,
        )

    def keep(row):
        return pltpu.make_async_copy(
            parts.at[mine, pl.ds(row * length, length)],
            tokens_ref.at[mine * rows + row],
            keep_sem.at[row],
        )

    tile = 256
    width = parts.shape[2]

    def back_row(row):
        at_row = pl.ds(pl.multiple_of(row * length, length), length)

        def product(index, carry):
            at = pl.ds(pl.multiple_of(index * tile, tile), tile)
            contract = (((1,), (1,)), ((), ()))
            back[:, at] = lax.dot_general(
                dbranch[at_row, :], weight_in[at, :], contract, preferred_element_type=jnp.float32
            ) + lax.dot_general(
                dgate[at_row, :], weight_gate[at, :], contract, preferred_element_type=jnp.float32
            )
            return carry

        lax.fori_loop(0, model // tile, product, 0)
        slab = 16

        def norm(index, carry):
            base = pl.multiple_of(index * slab, slab)
            at = pl.ds(row * length + base, slab)
            inv = inverse[at, :1]
            value = x[at, :].astype(jnp.float32) * inv
            scaled = back[pl.ds(base, slab), :] * gain_ref[...]
            mean = jnp.mean(scaled * value, axis=1, keepdims=True)
            grad = dres[at, :].astype(jnp.float32) + inv * (scaled - value * mean)
            grad = grad.astype(jnp.bfloat16)
            for part in range(parts.shape[0]):
                parts[part, at, :] = grad[:, part * width : (part + 1) * width]
            return carry

        lax.fori_loop(0, length // slab, norm, 0, unroll=4)
        for other in range(1, group):
            move(other, row).start()
        keep(row).start()

    def weight_product(left, right, made, stream, first):
        columns = made.shape[-1]
        shape = made.shape[1:-1]

        def product(index, carry):
            at = pl.ds(pl.multiple_of(index * tile, tile), tile)
            source = pl.ds(pl.multiple_of(first + index * tile, tile), tile)
            part = lax.dot_general(
                left[...],
                right[:, source],
                (((0,), (0,)), ((), ())),
                preferred_element_type=jnp.float32,
            )
            made[(stream,) + (slice(None),) * len(shape) + (at,)] = part.astype(
                jnp.bfloat16
            ).reshape(shape + (tile,))
            return carry

        lax.fori_loop(0, columns // tile, product, 0)

    half, half_out = (made_in.shape[-1], made_out.shape[-1])
    waited, reached = (set(), {})

    def need(*names):
        for place, name in enumerate(kinds):
            if name in names and place not in waited:
                waited.add(place)
                loads[place].wait()

    def fix_rim():
        need("dbranch")
        rim_copy.wait()
        live = jnp.where(seq < seqs - 1, 1.0, 0.0)
        for row in range(rows):
            at = slice((row + 1) * length - STEP, (row + 1) * length)
            inside = dbranch[at, :].astype(jnp.float32)
            last = ending_ref[row] + live * rim[row]
            dbranch[at, :] = jnp.concatenate([inside[: STEP - SUBLANES], last], axis=0).astype(
                jnp.bfloat16
            )

    def begin(stream):
        copy(stream, 0).start()
        reached[stream] = 0

    def progress(streams):
        for stream in streams:
            if stream in reached and reached[stream] < stages:
                if stream == 6:
                    need("small")
                advance(stream, reached[stream])
                reached[stream] += 1

    def pair(stream):
        if stream == 4:
            need("mixed", "dres")
            left, right, made, slots, first = (mixed, dres, made_out, slots_out[0], 4)
        elif stream == 0:
            need("normed", "dgate")
            left, right, made, slots, first = (normed, dgate, made_in, slots_in[0], 0)
        else:
            need("normed", "dbranch")
            left, right, made, slots, first = (normed, dbranch, made_in, slots_in[0], 0)
        columns = made.shape[-1]
        every = (slice(None),) * corners.count

        def one(place, carry):
            held = stream - first + place
            weight_product(left, right, made, held, place * columns)
            pltpu.make_async_remote_copy(
                src_ref=made.at[(held,) + every + (1 - core,)],
                dst_ref=slots.at[held],
                send_sem=send_sem.at[stream + place, 0],
                recv_sem=recv_sem.at[stream + place, 0],
                device_id={"core": 1 - core},
                device_id_type=MESH,
            ).start()
            return carry

        lax.fori_loop(0, 2, one, 0)
        reached[stream] = reached[stream + 1] = 0

    def back_rows():
        need("dbranch", "dgate", "win", "wgate", "x", "inverse", "dres")

        def one(row, carry):
            back_row(row)
            return carry

        lax.fori_loop(0, rows, one, 0)

    begin(6)
    fix_rim()
    back_rows()
    pair(0)
    progress((6,))
    pair(4)
    progress((0, 1))
    pair(2)
    progress((0, 1))
    progress((4, 5))
    progress((6,))
    while any(reached[stream] < stages for stream in range(7)):
        progress((0, 1, 4, 5, 2, 3, 6))
    for stage in range(stages):
        for stream in range(7):
            copy(stream, stage).wait_send()
    for row in range(rows):
        for other in range(1, group):
            move(other, row).wait()
        keep(row).wait()


def tail(dgate, dbranch, ending, leading, mixed, dres, gain, w_in, w_gate, small, normed, x, inverse):
    corners = Corners(lax.axis_size("seq"), lax.axis_size("zed"))
    group, devices = (lax.axis_size(CHAN), 2 ** (corners.count + 1))
    tokens, model = dres.shape
    rec = dgate.shape[1]
    rows = ending.shape[0]
    length, width = (tokens // rows, model // group)
    low, f32 = (jnp.bfloat16, jnp.float32)
    stages = corners.count + 1
    in_rows, out_rows = (model // devices, rec // devices)
    small = small.reshape(corners.dims + (2, out_rows, small.shape[1]))
    orders = [corners.low, corners.high] * 3 + [corners.low]

    def slots(lead, shape):
        return [pltpu.VMEM(lead + (2,) * (corners.count - k) + shape, low) for k in range(stages)]

    in_shape, out_shape = ((in_rows, rec // 2), (out_rows, model // 2))
    loaded = (dgate, dbranch, mixed, dres, dres, dres)
    loaded += (jax.ShapeDtypeStruct((tokens, LANES), f32), w_in, w_gate)
    anyplace = pl.BlockSpec(memory_space=pl.ANY)
    vmem = pl.BlockSpec(memory_space=pltpu.VMEM)
    dma = pltpu.SemaphoreType.DMA
    moved = sum(math.prod(a.shape) * a.dtype.itemsize for a in loaded)
    return pl.pallas_call(
        functools.partial(tail_kernel, corners, orders),
        name="tail",
        in_specs=[anyplace, anyplace, vmem, vmem, anyplace, anyplace, vmem]
        + [anyplace] * (3 + 3 * rows),
        out_specs=[anyplace] + [vmem] * 4,
        out_shape=[
            jax.ShapeDtypeStruct((group * rows, length, width), low),
            jax.ShapeDtypeStruct((in_rows, rec), f32),
            jax.ShapeDtypeStruct((out_rows, model), f32),
            jax.ShapeDtypeStruct((in_rows, rec), f32),
            jax.ShapeDtypeStruct(small.shape[-2:], f32),
        ],
        scratch_shapes=[pltpu.VMEM(a.shape, a.dtype) for a in loaded]
        + [
            pltpu.VMEM((4,) + corners.dims + (2,) + in_shape, low),
            pltpu.VMEM((2,) + corners.dims + (2,) + out_shape, low),
            pltpu.VMEM(corners.dims + small.shape[-2:], low),
            pltpu.VMEM((length, model), f32),
            pltpu.VMEM((group, tokens, width), low),
            pltpu.VMEM(leading.shape, leading.dtype),
        ]
        + slots((4,), in_shape)
        + slots((2,), out_shape)
        + slots((), small.shape[-2:])
        + [
            dma((7, stages)),
            dma((7, stages)),
            dma((7 + 3 * rows,)),
            dma((group - 1, rows)),
            dma((group - 1, rows)),
            dma((rows,)),
            dma,
            dma,
        ],
        compiler_params=pltpu.CompilerParams(
            collective_id=1, has_side_effects=True, vmem_limit_bytes=60 * 1024 * 1024
        ),
        cost_estimate=pl.CostEstimate(
            flops=10 * tokens * model * rec, bytes_accessed=2 * moved, transcendentals=0
        ),
    )(dgate, dbranch, ending, leading, mixed, dres, gain[None], w_in, w_gate, small, *normed, *x, *inverse)


def grads_kernel(
    normed_ref,
    dgate_ref,
    dup_ref,
    hidden_ref,
    gout_ref,
    out_ref,
    made_wide,
    made_down,
    come_wide,
    come_down,
    send_sem,
    recv_sem,
    store_sem,
):
    step = pl.program_id(0)
    core = lax.axis_index("core")
    other = {"core": 1 - core}
    wide_rows, down_rows = (made_wide.shape[3], made_down.shape[3])
    wides, downs = (come_wide.shape[0], come_down.shape[0])
    total = wides + downs
    down_at = wides * wide_rows

    def exchange(made, come, index, slot):
        return pltpu.make_async_remote_copy(
            src_ref=made.at[lax.rem(index, 3), 1 - core],
            dst_ref=come.at[index],
            send_sem=send_sem.at[slot],
            recv_sem=recv_sem.at[slot],
            device_id=other,
            device_id_type=MESH,
        )

    def store_wide(index):
        return pltpu.make_async_copy(
            come_wide.at[index],
            out_ref.at[:, pl.ds(pl.multiple_of(index * wide_rows, wide_rows), wide_rows)],
            store_sem.at[index],
        )

    def store_down(index):
        chips = come_down.shape[1]
        return pltpu.make_async_copy(
            come_down.at[index],
            out_ref.at[pl.ds(index * chips, chips), pl.ds(down_at, down_rows)],
            store_sem.at[index + wides],
        )

    @pl.when(step == 0)
    def _():
        barrier = pltpu.get_barrier_semaphore()
        pl.semaphore_signal(barrier, inc=1, device_id=other, device_id_type=MESH)
        pl.semaphore_wait(barrier, 1)

    def product_wide(source, index):
        made = made_wide.at[lax.rem(index, 3)]
        chips, rows = (made.shape[1], made.shape[2])
        tile = 512

        def column(place, carry):
            at = pl.ds(pl.multiple_of(place * tile, tile), tile)
            part = lax.dot_general(
                normed_ref[...], source[:, at], (((0,), (0,)), ((), ())), preferred_element_type=jnp.float32
            )
            part = part.astype(jnp.bfloat16).reshape(chips, 2, rows, tile)
            made[0, :, :, at] = part[:, 0]
            made[1, :, :, at] = part[:, 1]
            return carry

        lax.fori_loop(0, source.shape[1] // tile, column, 0, unroll=True)

    def product_tall(left, right, made_all, index):
        made = made_all.at[lax.rem(index, 3)]
        chips, rows = (made.shape[1], made.shape[2])
        tile = 512

        def column(place, carry):
            at = pl.ds(pl.multiple_of(place * tile, tile), tile)
            part = lax.dot_general(
                left[...], right[:, at], (((0,), (0,)), ((), ())), preferred_element_type=jnp.float32
            )
            part = part.astype(jnp.bfloat16).reshape(chips, 2, rows, tile)
            made[0, :, :, at] = part[:, 0]
            made[1, :, :, at] = part[:, 1]
            return carry

        lax.fori_loop(0, right.shape[1] // tile, column, 0, unroll=True)

    half = wides // 2

    @pl.when(step < half)
    def _():
        product_wide(dgate_ref, step)

    @pl.when((step >= half) & (step < wides))
    def _():
        product_wide(dup_ref, step)

    @pl.when(step < wides)
    def _():
        exchange(made_wide, come_wide, step, step).start()

    @pl.when((step >= wides) & (step < total))
    def _():
        product_tall(hidden_ref, gout_ref, made_down, step - wides)
        exchange(made_down, come_down, step - wides, step).start()

    def finish(made, come, index, slot, store):
        exchange(made, come, index, slot).wait()
        mine = made.at[lax.rem(index, 3), core]
        arrived = come.at[index]

        def add(chip, carry):
            both = mine[chip].astype(jnp.float32) + arrived[chip].astype(jnp.float32)
            arrived[chip] = both.astype(jnp.bfloat16)
            return carry

        lax.fori_loop(0, come.shape[1], add, 0, unroll=4)
        store(index).start()

    before = step - 2

    @pl.when((before >= 0) & (before < wides))
    def _():
        finish(made_wide, come_wide, before, before, store_wide)

    @pl.when(before >= wides)
    def _():
        finish(made_down, come_down, before - wides, before, store_down)

    @pl.when(step == total + 1)
    def _():
        for index in range(wides):
            store_wide(index).wait()
        for index in range(downs):
            store_down(index).wait()


def block_gradients(normed, dgate, dup, hidden, gout):
    tokens, model = normed.shape
    ffn = hidden.shape[1]
    chips = lax.axis_size("seq") * lax.axis_size("zed")
    devices = 2 * chips
    wide_rows, down_rows = (model // devices, ffn // devices)
    chunk = 768
    wides, downs = (2 * ffn // model, ffn // chunk)
    half = wides // 2
    down_chips = chunk // (2 * down_rows)
    rows = wides * wide_rows + down_rows
    low = jnp.bfloat16

    def whole(array):
        return pl.BlockSpec(array.shape, lambda s: (0, 0), pipeline_mode=pl.Buffered(1))

    def part(columns, first, count):
        return pl.BlockSpec((tokens, columns), lambda s: (0, jnp.clip(s - first, 0, count - 1)))

    total = wides + downs
    flops = 6 * tokens * model * ffn
    arrays = (normed, dgate, dup, hidden, gout)
    moved = sum(math.prod(a.shape) * 2 for a in arrays) + chips * rows * model * 2
    return pl.pallas_call(
        grads_kernel,
        name="block_gradients",
        grid=(total + 2,),
        in_specs=[
            whole(normed),
            part(model, 0, half),
            part(model, half, half),
            part(chunk, wides, downs),
            whole(gout),
        ],
        out_specs=pl.BlockSpec(memory_space=pl.ANY),
        out_shape=jax.ShapeDtypeStruct((chips, rows, model), low),
        scratch_shapes=[
            pltpu.VMEM((3, 2, chips, wide_rows, model), low),
            pltpu.VMEM((3, 2, down_chips, down_rows, model), low),
            pltpu.VMEM((wides, chips, wide_rows, model), low),
            pltpu.VMEM((downs, down_chips, down_rows, model), low),
            pltpu.SemaphoreType.DMA((total,)),
            pltpu.SemaphoreType.DMA((total,)),
            pltpu.SemaphoreType.DMA((total,)),
        ],
        compiler_params=pltpu.CompilerParams(
            collective_id=2, has_side_effects=True, vmem_limit_bytes=VMEM_BYTES
        ),
        cost_estimate=pl.CostEstimate(flops=flops, bytes_accessed=moved, transcendentals=0),
    )(*arrays)


def passed_along(value, axis, steps):
    count = lax.axis_size(axis)
    leading, last = (max(0, -steps), min(count, count - steps))
    return lax.ppermute(value, axis, [(source, source + steps) for source in range(leading, last)])


def weight_grad(left, right):
    return lax.dot_general(
        left, right, (((0,), (0,)), ((), ())), preferred_element_type=jnp.float32
    ).astype(jnp.bfloat16)


def back_dot(left, right):
    return lax.dot_general(
        left, right, (((1,), (1,)), ((), ())), preferred_element_type=jnp.float32
    )


def fwd_dot(left, right):
    return jnp.dot(left, right, preferred_element_type=jnp.float32)


def gelu_fn(value):
    return jax.nn.gelu(value, approximate=True)


def norm_back(grad_norm, normed, inverse, gain):
    scaled = grad_norm * gain
    mean_term = jnp.mean(scaled * normed, axis=1, keepdims=True)
    return inverse * (scaled - normed * mean_term)


def scattered(gradient):
    return lax.psum_scatter(
        gradient, ("seq", "zed", "core"), scatter_dimension=0, tiled=True
    ).astype(jnp.float32)


def body(
    tokens,
    cotangent,
    doc_starts,
    lengths,
    norm1_gain,
    recur_input,
    recur_gate,
    conv_kernel,
    conv_bias,
    lru_gates,
    lru_bias,
    lru_decay,
    recur_out,
    norm2_gain,
    mlp_gate,
    mlp_up,
    mlp_down,
):
    count = lax.axis_size(CHAN)
    row_count, block_len = (tokens.shape[0] // count, tokens.shape[1])
    model_dim = tokens.shape[2] * count
    tok_count = row_count * block_len
    rec_width = recur_input.shape[1]
    ffn_width = mlp_gate.shape[1]
    head_count = H
    head_size = rec_width // head_count
    tap_count = conv_kernel.shape[0]
    rim_size = tap_count - 1
    seq_index = lax.axis_index("seq")
    position = seq_index * block_len + jnp.arange(block_len, dtype=jnp.int32)
    bounds = jnp.concatenate([doc_starts, lengths[:, None]], axis=1)
    is_before = bounds[:, None, :] <= position[None, :, None]
    seg_start = jnp.max(jnp.where(is_before, bounds[:, None, :], 0), axis=2)
    dist = jnp.broadcast_to(
        (position[None, :] - seg_start)[:, :, None], (row_count, block_len, LANES)
    )
    soft_decay = jax.nn.softplus(-lru_decay)
    params = jnp.concatenate(
        [
            conv_kernel,
            conv_bias[None],
            lru_bias,
            (-8.0 * soft_decay)[None],
            (8.0 * jax.nn.sigmoid(-lru_decay))[None],
            jnp.zeros((SUBLANES - 1, rec_width), jnp.float32),
        ],
        axis=0,
    )
    core = Recurrence(row_count, block_len, rec_width, head_size)
    wide_gates = core.widen(lru_gates)
    if tokens.shape[2] % LANES == 0:
        blocks = [features_in(tokens, slice(0, 1))]
        later, wide_gates, params, dist = lax.optimization_barrier(
            (tokens, wide_gates, params, dist)
        )
        blocks += [features_in(later, slice(row, row + 1)) for row in range(1, row_count)]
    else:
        side = features_in(tokens)
        blocks = [side[:, row * block_len : (row + 1) * block_len] for row in range(row_count)]
    per_row = []
    for row in range(row_count):
        block = blocks[row]
        if row:
            block, _ = lax.optimization_barrier((block, per_row[-1][-1]))
        per_row.append(
            front(
                block,
                norm1_gain,
                recur_input,
                recur_gate,
                dist[row : row + 1],
                params,
                wide_gates,
            )
        )
    low_x, inverse, normed_low, branch, gate_pre, rim, lru_in, rate, igate, state, cum, last = zip(
        *per_row
    )
    entering, mixed_low, resid_one, normed_low2 = middle(
        last, state, cum, gate_pre, low_x, recur_out, norm2_gain
    )
    cotangent, _ = lax.optimization_barrier((cotangent, block))
    cotangent, resid_one = lax.optimization_barrier((features_in(cotangent), resid_one))
    grad_low, hidden_low, mgate_low, mup_low = mlp_hidden(
        lengths - seq_index * block_len, cotangent, normed_low2, mlp_gate, mlp_up, mlp_down
    )
    devices = lax.axis_size(("seq", "zed", "core"))
    own_rows = model_dim // devices
    tiled = own_rows % (2 * SUBLANES) == 0 and tokens.shape[2] % LANES == 0
    if tiled:
        merged = block_gradients(normed_low2, mgate_low, mup_low, hidden_low, grad_low)
        merged, hidden_low = lax.optimization_barrier((merged, hidden_low))
        merged = lax.psum_scatter(merged, "seq", scatter_dimension=0, tiled=True)
    result_parts, resid_low = mlp_back(
        hidden_low,
        mgate_low,
        mup_low,
        grad_low,
        resid_one,
        norm2_gain,
        mlp_gate,
        mlp_up,
        mlp_down,
        cotangent.shape,
    )
    output = features_out(result_parts, row_count)
    gate_low, back_local, back_cum, first_term = core.adjoint(
        resid_low,
        recur_out,
        gate_pre,
        state,
        cum,
        entering,
        rate,
        dist,
        params,
    )
    gate_low = gate_low.reshape(tok_count, rec_width)

    def zed_stage(leaving):
        if not tiled:
            return ((), leaving)
        done, leaving = lax.optimization_barrier((merged, leaving))
        return (lax.psum_scatter(done, "zed", scatter_dimension=0, tiled=True), leaving)

    branch_local, ending, leading, small, merged_own = core.backward(
        back_local,
        back_cum,
        first_term,
        last,
        state,
        cum,
        entering,
        rate,
        igate,
        lru_in,
        dist,
        branch,
        rim,
        params,
        wide_gates,
        zed_stage,
    )
    branch_low = branch_local.reshape(tok_count, rec_width)
    if tiled:
        output, branch_low = lax.optimization_barrier((output, branch_low))
        grad_tokens, sum_rgate, sum_rout, sum_rin, own_small = tail(
            gate_low,
            branch_low,
            ending,
            leading,
            mixed_low,
            resid_low,
            norm1_gain,
            recur_input,
            recur_gate,
            small,
            normed_low,
            low_x,
            inverse,
        )
        device = lax.axis_index(("seq", "zed", "core"))
        sums = outputs(
            device,
            merged_own[0],
            sum_rgate,
            sum_rin,
            sum_rout,
            own_small,
            recur_input,
            recur_gate,
            mlp_gate,
            mlp_up,
            norm1_gain,
            norm2_gain,
            head_size,
        )
        flat = (0, 4, 7, 9)
        sums = [part.reshape(-1) if place in flat else part for place, part in enumerate(sums)]
        return (output, grad_tokens, *sums)
    else:
        from_next = passed_along(
            leading[:, SUBLANES - rim_size :, :].astype(jnp.bfloat16), "seq", -1
        )
        ending = ending + jnp.pad(
            from_next.astype(jnp.float32), ((0, 0), (SUBLANES - rim_size, 0), (0, 0))
        )
        branch_low = lax.dynamic_update_slice(
            branch_local, ending.astype(jnp.bfloat16), (0, block_len - SUBLANES, 0)
        ).reshape(tok_count, rec_width)
        grad_norm1 = back_dot(branch_low, recur_input) + back_dot(gate_low, recur_gate)
        inv_one = jnp.concatenate(inverse)[:, :1]
        normed_one = jnp.concatenate(low_x).astype(jnp.float32) * inv_one
        normed_low = jnp.concatenate(normed_low)
        input_part = norm_back(grad_norm1, normed_one, inv_one, norm1_gain)
        grad_x = (resid_low.astype(jnp.float32) + input_part).astype(jnp.bfloat16)
        grad_tokens = features_out(features_apart(grad_x), row_count)
        sum_mgate, sum_mup, sum_down, sum_rout, sum_rgate, sum_rin = (
            scattered(weight_grad(left, right))
            for left, right in (
                (normed_low2, mgate_low),
                (normed_low2, mup_low),
                (hidden_low, grad_low),
                (mixed_low, resid_low),
                (normed_low, gate_low),
                (normed_low, branch_low),
            )
        )
        own_small = scattered(small)
    sum_lgates = jnp.concatenate(
        [own_small[:, :head_size], own_small[:, LANES : LANES + head_size]], axis=1
    )
    own_sums = jnp.swapaxes(own_small[:, head_size : head_size + SUBLANES], 0, 1)
    device = lax.axis_index(("seq", "zed", "core"))

    def mine(array, size, axis=0):
        return lax.dynamic_slice_in_dim(array, device * size, size, axis)

    def weighed(weight, gradient):
        return jnp.sum(mine(weight, own_rows).astype(jnp.float32) * gradient, axis=1)

    sum_gain1 = (weighed(recur_input, sum_rin) + weighed(recur_gate, sum_rgate)) / mine(
        norm1_gain, own_rows
    )
    sum_gain2 = (weighed(mlp_gate, sum_mgate) + weighed(mlp_up, sum_mup)) / mine(
        norm2_gain, own_rows
    )
    sum_decay = own_sums[7]
    return (
        output,
        grad_tokens,
        sum_gain1,
        sum_rin,
        sum_rgate,
        own_sums[:4],
        own_sums[4],
        sum_lgates,
        own_sums[5:7],
        sum_decay,
        sum_rout,
        sum_gain2,
        sum_mgate,
        sum_mup,
        sum_down,
    )


def solution(mesh):
    seq, chan = (mesh.shape["seq"], mesh.shape["chan"])
    chips = jax.sharding.Mesh(mesh.devices.reshape(seq, chan // 2, 2), ("seq", "zed", "core"))
    chan = ("zed", "core")
    every = ("seq", "zed", "core")
    activations = P(None, "seq", chan)
    rows, columns, vector = (P(every, None), P(None, every), P(every))
    return jax.shard_map(
        body,
        mesh=chips,
        in_specs=(activations, activations, P(chan, None), P(chan)) + (P(),) * 13,
        out_specs=(
            activations,
            activations,
            vector,
            rows,
            rows,
            columns,
            vector,
            rows,
            columns,
            vector,
            rows,
            vector,
            rows,
            rows,
            rows,
        ),
        check_vma=False,
    )
```
